32 devices in a mesh: shard: 4 (over z), ctx: 4 (over y, x), tp: 2 (over core).
Axes of the slice: x: 2, y: 2, z: 4, core: 2. Of those that a mesh axis runs over, the one named last changes fastest.
Arguments:
- inputs: float32 [16, 2048, 768], P(('shard', 'tp'), 'ctx'), may hold values from -6 to 6
- cotangent: float32 [16, 2048, 768], P(('shard', 'tp'), 'ctx'), may hold values from -6 to 6
- rand_blocks: int32 [12, 30, 3], replicated, may hold values from 1 to 30, as said below
- slot_of: int32 [12], replicated, may hold values from 0 to 11, as said below
- master: float32 [12, 768, 768], P('shard', ('ctx', 'tp'))
- moment_one: float32 [12, 768, 768], P('shard', ('ctx', 'tp'))
- moment_two: float32 [12, 768, 768], P('shard', ('ctx', 'tp')), as said below
- small_params: float32 [9216], P(('shard', 'ctx', 'tp'))
- small_one: float32 [9216], P(('shard', 'ctx', 'tp'))
- small_two: float32 [9216], P(('shard', 'ctx', 'tp')), as said below
Outputs:
- layer_out: float32 [16, 2048, 768], P(('shard', 'tp'), 'ctx')
- input_grad: float32 [16, 2048, 768], P(('shard', 'tp'), 'ctx')
- master_new: float32 [12, 768, 768], P('shard', ('ctx', 'tp'))
- moment_one_new: float32 [12, 768, 768], P('shard', ('ctx', 'tp'))
- moment_two_new: float32 [12, 768, 768], P('shard', ('ctx', 'tp'))
- small_new: float32 [9216], P(('shard', 'ctx', 'tp'))
- small_one_new: float32 [9216], P(('shard', 'ctx', 'tp'))
- small_two_new: float32 [9216], P(('shard', 'ctx', 'tp'))
The draws below stay inside these ranges and needn't reach their ends.
Inputs may be any that keep to these rules, and one draw needn't show every extreme that they name: For head h and middle query block i (1 to 30), rand_blocks[h, i - 1] names three different key blocks, none of them 0, 31, i - 1, i or i + 1. `slot_of`: the 12 entries name different slots; slot s belongs to index s // 3 of the shard axis; some index holds exactly 3 matrices, the others as many as the draw gives. `moment_two`: every entry is positive. `small_two`: every entry is positive.
All inputs are finite; a program needn't handle non-finite values.
Results may differ from the reference program's by a relative error of at most 0.023.
Values may be sent and summed in bfloat16 or wider, within the bound.
A program may use at most 256 MiB of HBM per device.

```python
import math
import jax
import jax.numpy as jnp
from jax import lax

D = 768
FF = 3072
H = 12
BLOCK = 64
NR = 3
SLOTS = 3
STEP = 5
LEN = 2048
SEQS = 16
TOKENS = 32768
NB = 32
FB = 4
NMAT = 12
OWNERS = 4
SLOTS_ALL = 12
NSMALL = 9216


def owner_table(key):
    base = jax.random.fold_in(key, 17)
    key_owner, key_rest, key_order = jax.random.split(base, 3)
    full_owner = jax.random.randint(key_owner, (), 0, OWNERS)
    others = jax.random.permutation(key_rest, SLOTS_ALL - SLOTS)
    others = others + SLOTS * (others >= full_owner * SLOTS).astype(jnp.int32)
    slot_table = jnp.concatenate([full_owner * SLOTS + jnp.arange(SLOTS, dtype=jnp.int32), others[:NMAT - SLOTS].astype(jnp.int32)])
    matrix_order = jax.random.permutation(key_order, NMAT)
    return slot_table[matrix_order].astype(jnp.int32)


def per_slot(slot_table, matrix_values, empty_value):
    matches = (slot_table[:, None] == jnp.arange(SLOTS_ALL)[None, :]).astype(jnp.float32)
    return jnp.sum(matches * matrix_values[:, None], axis=0) + (1.0 - jnp.sum(matches, axis=0)) * empty_value


def weight_spreads():
    listed = [math.sqrt(2.0 / D)] * 2 + [math.sqrt(1.0 / D), math.sqrt(8.0 / D)] + [math.sqrt(1.0 / D)] * FB + [math.sqrt(1.0 / FF)] * FB
    return jnp.array(listed, dtype=jnp.float32)


def grad_sizes():
    listed = [0.3, 0.3, 0.5, 0.2] + [0.2] * FB + [0.45] * FB
    return jnp.array(listed, dtype=jnp.float32) * math.sqrt(TOKENS)


def small_sizes():
    front = [jnp.full((D,), level, jnp.float32) for level in [0.3, 0.5, 0.57, 0.8, 0.8]]
    middle = [jnp.full((FF,), 0.2, jnp.float32)]
    back = [jnp.full((D,), level, jnp.float32) for level in [0.7, 1.0, 1.0]]
    return jnp.concatenate(front + middle + back) * math.sqrt(TOKENS)


def draw_slot_of(key, part):
    return owner_table(key)


def draw_rand_blocks(key, part):
    scores = jax.random.randint(key, (H, NB - 2, NB), 0, 1 << 20) * NB + jnp.arange(NB, dtype=jnp.int32)[None, None, :]
    row_ids = jnp.arange(1, NB - 1)[:, None]
    column_ids = jnp.arange(NB)[None, :]
    banned = (column_ids == 0) | (column_ids == NB - 1) | (jnp.abs(column_ids - row_ids) <= 1)
    scores = jnp.where(banned[None, :, :], -1, scores)
    ignored, picks = lax.top_k(scores, NR)
    return picks.astype(jnp.int32)


def draw_master(key, part):
    spread = per_slot(owner_table(key), weight_spreads(), math.sqrt(1.0 / D))
    gauss_draw = jax.random.truncated_normal(jax.random.fold_in(key, 1), -4.0, 4.0, (SLOTS_ALL, D, D), jnp.float32)
    return gauss_draw * spread[:, None, None]


def draw_moment_one(key, part):
    sizes = per_slot(owner_table(key), grad_sizes(), 0.3 * math.sqrt(TOKENS))
    gauss_draw = jax.random.truncated_normal(jax.random.fold_in(key, 2), -4.0, 4.0, (SLOTS_ALL, D, D), jnp.float32)
    return 0.111 * gauss_draw * sizes[:, None, None]


def draw_moment_two(key, part):
    sizes = per_slot(owner_table(key), grad_sizes(), 0.3 * math.sqrt(TOKENS))
    multiple = jax.random.uniform(jax.random.fold_in(key, 3), (SLOTS_ALL, 1, 1), jnp.float32, 1.0, 4.0)
    factor = jnp.exp(jax.random.uniform(jax.random.fold_in(key, 4), (SLOTS_ALL, D, D), jnp.float32, math.log(0.5), math.log(2.0)))
    return 0.001 * multiple * factor * (sizes * sizes)[:, None, None]


def draw_small_params(key, part):
    gauss_draw = jax.random.truncated_normal(jax.random.fold_in(key, 5), -4.0, 4.0, (NSMALL,), jnp.float32)
    positions = jnp.arange(NSMALL)
    gain_one = (positions >= 3 * D) & (positions < 4 * D)
    gain_two = (positions >= 6 * D + FF) & (positions < 7 * D + FF)
    is_gain = gain_one | gain_two
    return jnp.where(is_gain, 1.0 + 0.1 * gauss_draw, 0.2 * gauss_draw)


def draw_small_one(key, part):
    gauss_draw = jax.random.truncated_normal(jax.random.fold_in(key, 6), -4.0, 4.0, (NSMALL,), jnp.float32)
    return 0.111 * gauss_draw * small_sizes()


def draw_small_two(key, part):
    multiple = jax.random.uniform(jax.random.fold_in(key, 7), (), jnp.float32, 1.0, 4.0)
    factor = jnp.exp(jax.random.uniform(jax.random.fold_in(key, 8), (NSMALL,), jnp.float32, math.log(0.5), math.log(2.0)))
    sizes = small_sizes()
    return 0.001 * multiple * factor * sizes * sizes


def level_of(rng, shape, cuts, least, largest):
    factor_of = 1.0
    for dim, blocks in cuts:
        heights = jax.random.uniform(jax.random.fold_in(jax.random.fold_in(rng, 6), dim), (blocks,), jnp.float32, least / len(cuts), largest / len(cuts))
        factor_of = factor_of * jnp.repeat(jnp.exp(heights), shape[dim] // blocks).reshape((-1,) + (1,) * (len(shape) - 1 - dim))
    return factor_of


def normal_values(rng, dims, scale, most, shards=(), kind=jnp.bfloat16):
    values = scale * jax.random.normal(rng, dims, jnp.float32)
    if shards:
        values = values * level_of(rng, dims, shards, -0.22, 0.18)
    return jnp.clip(values, -most, most).astype(kind)


def setup_inputs(seed: int = 0) -> dict:
    keys = jax.random.split(jax.random.key(seed), 11)
    inputs = normal_values(keys[0], (SEQS, LEN, D), 1.0, 6.0, ((0, 8), (1, 4)), jnp.float32)
    cotangent = normal_values(keys[1], (SEQS, LEN, D), 1.0, 6.0, ((0, 8), (1, 4)), jnp.float32)
    rand_blocks = draw_rand_blocks(jax.random.fold_in(keys[10], 71), 0)
    slot_of = draw_slot_of(jax.random.fold_in(keys[10], 71), 0)
    master = draw_master(jax.random.fold_in(keys[10], 71), 0)
    moment_one = draw_moment_one(jax.random.fold_in(keys[10], 71), 0)
    moment_two = draw_moment_two(jax.random.fold_in(keys[10], 71), 0)
    small_params = draw_small_params(jax.random.fold_in(keys[10], 71), 0)
    small_one = draw_small_one(jax.random.fold_in(keys[10], 71), 0)
    small_two = draw_small_two(jax.random.fold_in(keys[10], 71), 0)
    return dict(inputs=inputs, cotangent=cotangent, rand_blocks=rand_blocks, slot_of=slot_of, master=master, moment_one=moment_one, moment_two=moment_two, small_params=small_params, small_one=small_one, small_two=small_two)


@jax.custom_vjp
def low(v):
    return lax.optimization_barrier(v.astype(jnp.bfloat16)).astype(jnp.float32)

@jax.custom_vjp
def low_back(v):
    return v

def low_keep(v):
    return (low(v), None)

def low_pass(kept, grad):
    return (grad,)

def back_keep(v):
    return (v, None)

def back_low(kept, grad):
    return (low(grad),)
low.defvjp(low_keep, low_pass)
low_back.defvjp(back_keep, back_low)
highest = lax.Precision.HIGHEST
norm_eps = 1e-12
beta_one = 0.9
beta_two = 0.999
adam_eps = 1e-08
rate_value = 0.04
small_rate = 0.25

def layer_norm(field, gain, shift):
    centred = field - lax.optimization_barrier(jnp.mean(field, axis=-1, keepdims=True))
    spread = lax.optimization_barrier(jnp.mean(centred * centred, axis=-1, keepdims=True))
    return centred * lax.rsqrt(spread + norm_eps) * gain + shift

def gelu_tanh(field):
    return jax.nn.gelu(field, approximate=True)

def split_small(params, model_width):
    ffn_width = params.shape[0] - 8 * model_width
    pieces = [params[index * model_width:(index + 1) * model_width] for index in range(5)]
    up_start = 5 * model_width
    pieces.append(params[up_start:up_start + ffn_width])
    tail_start = up_start + ffn_width
    for index in range(3):
        pieces.append(params[tail_start + index * model_width:tail_start + (index + 1) * model_width])
    return tuple(pieces)

def adam_update(weight, first, second, grad, decay, rate):
    count = float(STEP)
    first_new = beta_one * first + (1.0 - beta_one) * grad
    second_new = beta_two * second + (1.0 - beta_two) * grad * grad
    first_hat = first_new / (1.0 - beta_one ** count)
    second_hat = second_new / (1.0 - beta_two ** count)
    weight_new = weight - rate * (first_hat / (jnp.sqrt(second_hat) + adam_eps) + decay * weight)
    return (weight_new, first_new, second_new)

def token_mask(rand_blocks, nblocks, block):
    row_ids = jnp.arange(nblocks)[:, None]
    column_ids = jnp.arange(nblocks)[None, :]
    fixed = (row_ids == 0) | (row_ids == nblocks - 1) | (column_ids == 0) | (column_ids == nblocks - 1) | (jnp.abs(row_ids - column_ids) <= 1)
    picked = jnp.any(rand_blocks[:, :, :, None] == jnp.arange(nblocks)[None, None, None, :], axis=2)
    border = jnp.zeros((rand_blocks.shape[0], 1, nblocks), dtype=bool)
    picked = jnp.concatenate([border, picked, border], axis=1)
    blocks_on = fixed[None, :, :] | picked
    return jnp.repeat(jnp.repeat(blocks_on, block, axis=1), block, axis=2)

def forward(batch_in, matrices, smalls, allowed):
    model_width = batch_in.shape[-1]
    seq_len = batch_in.shape[1]
    head_count = allowed.shape[0]
    head_dim = model_width // head_count
    ffn_blocks = (matrices.shape[0] - 4) // 2
    weights = low(matrices)
    params = low(smalls)
    q_bias, v_bias, o_bias, gain_one, shift_one, up_bias, down_bias, gain_two, shift_two = split_small(params, model_width)
    x_low = low(batch_in)

    def project(weight):
        return jnp.einsum('gld,de->gle', x_low, weight, precision=highest)
    queries = low_back(low(project(weights[0]) + q_bias))
    key_proj = low_back(low(project(weights[1])))
    value_proj = low_back(low(project(weights[2]) + v_bias))

    def attend(parts):
        query_one, key_one, value_one = parts
        shaped = (seq_len, head_count, head_dim)
        scores = jnp.einsum('qhd,khd->hqk', query_one.reshape(shaped), key_one.reshape(shaped), precision=highest) * 0.125
        scores = jnp.where(allowed, low_back(scores), -1e+30)
        probs = low(jax.nn.softmax(scores, axis=-1))
        mixed = jnp.einsum('hqk,khd->qhd', probs, value_one.reshape(shaped), precision=highest)
        return mixed.reshape(seq_len, model_width)
    context = lax.map(jax.checkpoint(attend), (queries, key_proj, value_proj))
    context = low_back(low(context))
    attn_out = low_back(jnp.einsum('gld,de->gle', context, weights[3], precision=highest) + o_bias)
    after_attn = layer_norm(batch_in + attn_out, gain_one, shift_one)
    ffn_in = low(after_attn)
    up_proj = low_back(jnp.einsum('gld,bdh->glbh', ffn_in, weights[4:4 + ffn_blocks], precision=highest) + up_bias.reshape(ffn_blocks, model_width))
    hidden = low(gelu_tanh(up_proj))
    ffn_out = low_back(jnp.einsum('glbh,beh->gle', hidden, weights[4 + ffn_blocks:4 + 2 * ffn_blocks], precision=highest) + down_bias)
    return layer_norm(after_attn + ffn_out, gain_two, shift_two)

def reference(inputs, cotangent, rand_blocks, slot_of, master, moment_one, moment_two, small_params, small_one, small_two):
    allowed = token_mask(rand_blocks, LEN // BLOCK, BLOCK)
    matrices = master[slot_of]
    group_size = math.gcd(SEQS, max(1, 4096 // LEN))
    group_count = SEQS // group_size
    grouped_in = inputs.reshape(group_count, group_size, LEN, D)
    grouped_cot = cotangent.reshape(group_count, group_size, LEN, D)

    def one_group(totals, items):
        batch_in, batch_cot = items

        def layer(field, mats, smalls):
            return forward(field, mats, smalls, allowed)
        outputs, pull = jax.vjp(layer, batch_in, matrices, small_params)
        grad_in, grad_mats, grad_small = pull(batch_cot)
        return ((totals[0] + grad_mats, totals[1] + grad_small), (outputs, grad_in))
    start = (jnp.zeros(matrices.shape, jnp.float32), jnp.zeros(small_params.shape, jnp.float32))
    (mat_grads, small_grads), (outputs, grad_in) = lax.scan(one_group, start, (grouped_in, grouped_cot))
    slot_grads = jnp.zeros(master.shape, jnp.float32).at[slot_of].add(mat_grads)
    master_new, first_new, second_new = adam_update(master, moment_one, moment_two, slot_grads, 0.01, rate_value)
    small_new, small_first, small_second = adam_update(small_params, small_one, small_two, small_grads, 0.0, small_rate)
    return (outputs.reshape(SEQS, LEN, D), grad_in.reshape(SEQS, LEN, D), master_new, first_new, second_new, small_new, small_first, small_second)
```

```python
import functools

import jax
import jax.numpy as jnp
from jax import lax
from jax.experimental import pallas as pl
from jax.experimental.pallas import tpu as pltpu
from jax.sharding import PartitionSpec as P

STEP = 5
norm_eps = 1e-12
beta_one = 0.9
beta_two = 0.999
adam_eps = 1e-08
rate_value = 0.04
small_rate = 0.25
score_scale = 0.125
gelu_root = 0.7978845608
gelu_cube = 0.044715

BLOCK = 64
HEAD = 64
PACK = 4
masked_score = -1e30


def wide_dot(a, b, dims):
    return lax.dot_general(a, b, (dims, ((), ())), preferred_element_type=jnp.float32)


def head_masks(rows):
    lane = lax.broadcasted_iota(jnp.int32, (rows, PACK * HEAD), 1) // HEAD
    return [lane == h for h in range(PACK)]


def spread_heads(block, masks):
    zero = jnp.zeros_like(block)
    return jnp.concatenate([jnp.where(m, block, zero) for m in masks], axis=0)


def own_heads(full, masks):
    total = None
    for h, m in enumerate(masks):
        piece = jnp.where(m, full[h * BLOCK : (h + 1) * BLOCK], 0.0)
        total = piece if total is None else total + piece
    return total


def rows_of(ref, index, count=1):
    return ref[pl.ds(pl.multiple_of(index * BLOCK, BLOCK), count * BLOCK), :]


def picked_rows(ref, picks, low_half):
    halves = []
    for pair in range(PACK // 2):
        cols = pl.ds(pair * 2 * HEAD, 2 * HEAD)
        first = ref[pl.ds(pl.multiple_of(picks[2 * pair] * BLOCK, BLOCK), BLOCK), cols]
        second = ref[pl.ds(pl.multiple_of(picks[2 * pair + 1] * BLOCK, BLOCK), BLOCK), cols]
        halves.append(jnp.where(low_half, first, second))
    return jnp.concatenate(halves, axis=1)


def gathered(ref, block, last, picks, low_half):
    pieces = [rows_of(ref, 0), rows_of(ref, last), rows_of(ref, block - 1, 3)]
    pieces += [picked_rows(ref, p, low_half) for p in picks]
    return jnp.concatenate(pieces, axis=0)


def middle_scores(keys, spread, block, last):
    scores = wide_dot(keys, spread, ((1,), (1,)))
    first_off = jnp.where(block == 1, masked_score, 0.0)
    last_off = jnp.where(block == last - 1, masked_score, 0.0)
    b = BLOCK
    return jnp.concatenate(
        [
            scores[: 2 * b],
            scores[2 * b : 3 * b] + first_off,
            scores[3 * b : 4 * b],
            scores[4 * b : 5 * b] + last_off,
            scores[5 * b :],
        ],
        axis=0,
    )


def attend_kernel(unroll, half_ref, table_ref, q_ref, k_ref, v_ref, out_ref, lse_ref, kept):
    half = half_ref[0]
    group = pl.program_id(0)
    nblocks = k_ref.shape[0] // BLOCK
    local = q_ref.shape[0] // BLOCK
    last = nblocks - 1
    picks_each = table_ref.shape[2]
    masks = head_masks(BLOCK)
    low_half = lax.broadcasted_iota(jnp.int32, (BLOCK, 2 * HEAD), 1) < HEAD

    def middle(step, carry):
        mine = step + 1 - half
        block = mine + local * half
        picks = [
            [table_ref[group * PACK + h, block - 1, r] for h in range(PACK)]
            for r in range(picks_each)
        ]
        spread = spread_heads(rows_of(q_ref, mine), masks)
        keys = gathered(k_ref, block, last, picks, low_half)
        values = gathered(v_ref, block, last, picks, low_half)
        scores = middle_scores(keys, spread, block, last)
        top = jnp.max(scores, axis=0, keepdims=True)
        probs = jnp.exp(scores - top)
        total = jnp.sum(probs, axis=0, keepdims=True)
        low = (probs * (1.0 / total)).astype(jnp.bfloat16)
        full = wide_dot(low, values, ((0,), (0,)))
        out_ref[pl.ds(pl.multiple_of(mine * BLOCK, BLOCK), BLOCK), :] = own_heads(
            full, masks
        ).astype(jnp.bfloat16)
        lse_ref[0, pl.ds(mine, 1), :] = top + jnp.log(total)
        return carry

    lax.fori_loop(0, local - 1, middle, 0, unroll=unroll)

    edge = (local - 1) * half
    spread = spread_heads(rows_of(q_ref, edge), masks)
    span = 8 * BLOCK
    chunks = nblocks // 8
    top = None
    for c in range(chunks):
        scores = wide_dot(k_ref[c * span : (c + 1) * span, :], spread, ((1,), (1,)))
        kept[c * span : (c + 1) * span, :] = scores
        high = jnp.max(scores, axis=0, keepdims=True)
        top = high if top is None else jnp.maximum(top, high)
    total = None
    for c in range(chunks):
        probs = jnp.exp(kept[c * span : (c + 1) * span, :] - top)
        kept[c * span : (c + 1) * span, :] = probs
        part = jnp.sum(probs, axis=0, keepdims=True)
        total = part if total is None else total + part
    scale = 1.0 / total
    full = None
    for c in range(chunks):
        low = (kept[c * span : (c + 1) * span, :] * scale).astype(jnp.bfloat16)
        part = wide_dot(low, v_ref[c * span : (c + 1) * span, :], ((0,), (0,)))
        full = part if full is None else full + part
    out_ref[pl.ds(pl.multiple_of(edge * BLOCK, BLOCK), BLOCK), :] = own_heads(
        full, masks
    ).astype(jnp.bfloat16)
    lse_ref[0, pl.ds(edge, 1), :] = top + jnp.log(total)


def attend(half, table, q, k, v, unroll=3):
    tokens, width = q.shape
    seq = k.shape[0]
    lanes = PACK * HEAD
    groups = width // lanes
    blocks = tokens // BLOCK
    spec = pltpu.PrefetchScalarGridSpec(
        num_scalar_prefetch=2,
        grid=(groups,),
        in_specs=[
            pl.BlockSpec((tokens, lanes), lambda g, *_: (0, g)),
            pl.BlockSpec((seq, lanes), lambda g, *_: (0, g)),
            pl.BlockSpec((seq, lanes), lambda g, *_: (0, g)),
        ],
        out_specs=[
            pl.BlockSpec((tokens, lanes), lambda g, *_: (0, g)),
            pl.BlockSpec((1, blocks, lanes), lambda g, *_: (g, 0, 0)),
        ],
        scratch_shapes=[pltpu.VMEM((seq, lanes), jnp.float32)],
    )
    return pl.pallas_call(
        functools.partial(attend_kernel, unroll),
        grid_spec=spec,
        out_shape=[
            jax.ShapeDtypeStruct((tokens, width), jnp.bfloat16),
            jax.ShapeDtypeStruct((groups, blocks, lanes), jnp.float32),
        ],
        name="attend",
        compiler_params=pltpu.CompilerParams(vmem_limit_bytes=56 << 20),
        cost_estimate=pl.CostEstimate(
            flops=60_000_000_000, bytes_accessed=12 << 20, transcendentals=16_000_000
        ),
    )(half, table, q, k, v)


def attend_back_kernel(
    unroll,
    half_ref,
    table_ref,
    q_ref,
    k_ref,
    v_ref,
    lse_ref,
    do_ref,
    dq_ref,
    dk_ref,
    dv_ref,
    dk_acc,
    dv_acc,
    kept_p,
    kept_g,
):
    half = half_ref[0]
    group = pl.program_id(0)
    nblocks = k_ref.shape[0] // BLOCK
    local = q_ref.shape[0] // BLOCK
    last = nblocks - 1
    picks_each = table_ref.shape[2]
    masks = head_masks(BLOCK)
    low_half = lax.broadcasted_iota(jnp.int32, (BLOCK, 2 * HEAD), 1) < HEAD
    span = 8 * BLOCK
    chunks = nblocks // 8

    edge = (local - 1) * half
    spread = spread_heads(rows_of(q_ref, edge), masks)
    spread_do = spread_heads(rows_of(do_ref, edge), masks)
    lse = lse_ref[0, pl.ds(edge, 1), :]
    delta = None
    for c in range(chunks):
        rows = slice(c * span, (c + 1) * span)
        probs = jnp.exp(wide_dot(k_ref[rows, :], spread, ((1,), (1,))) - lse)
        gp = wide_dot(v_ref[rows, :], spread_do, ((1,), (1,)))
        kept_p[rows, :] = probs
        kept_g[rows, :] = gp
        part = jnp.sum(probs * gp, axis=0, keepdims=True)
        delta = part if delta is None else delta + part
    full = None
    for c in range(chunks):
        rows = slice(c * span, (c + 1) * span)
        probs = kept_p[rows, :]
        ds = (probs * (kept_g[rows, :] - delta)).astype(jnp.bfloat16)
        dv_acc[rows, :] = wide_dot(probs.astype(jnp.bfloat16), spread_do, ((1,), (0,)))
        dk_acc[rows, :] = wide_dot(ds, spread, ((1,), (0,)))
        part = wide_dot(ds, k_ref[rows, :], ((0,), (0,)))
        full = part if full is None else full + part
    dq_ref[pl.ds(pl.multiple_of(edge * BLOCK, BLOCK), BLOCK), :] = (
        own_heads(full, masks) * 0.125
    ).astype(jnp.bfloat16)

    def scatter(acc, piece, block, picks):
        b = BLOCK
        acc[0:b, :] += piece[:b]
        acc[last * b : (last + 1) * b, :] += piece[b : 2 * b]
        window = pl.ds(pl.multiple_of((block - 1) * b, b), 3 * b)
        acc[window, :] += piece[2 * b : 5 * b]
        for r, p in enumerate(picks):
            part = piece[(5 + r) * b : (6 + r) * b]
            for pair in range(PACK // 2):
                lanes = slice(pair * 2 * HEAD, (pair + 1) * 2 * HEAD)
                cols = pl.ds(pair * 2 * HEAD, 2 * HEAD)
                sub = part[:, lanes]
                acc[pl.ds(pl.multiple_of(p[2 * pair] * b, b), b), cols] += jnp.where(
                    low_half, sub, 0.0
                )
                acc[pl.ds(pl.multiple_of(p[2 * pair + 1] * b, b), b), cols] += jnp.where(
                    low_half, 0.0, sub
                )

    def middle(step, carry):
        mine = step + 1 - half
        block = mine + local * half
        picks = [
            [table_ref[group * PACK + h, block - 1, r] for h in range(PACK)]
            for r in range(picks_each)
        ]
        spread = spread_heads(rows_of(q_ref, mine), masks)
        spread_do = spread_heads(rows_of(do_ref, mine), masks)
        keys = gathered(k_ref, block, last, picks, low_half)
        values = gathered(v_ref, block, last, picks, low_half)
        scores = middle_scores(keys, spread, block, last)
        probs = jnp.exp(scores - lse_ref[0, pl.ds(mine, 1), :])
        gp = wide_dot(values, spread_do, ((1,), (1,)))
        delta = jnp.sum(probs * gp, axis=0, keepdims=True)
        ds = (probs * (gp - delta)).astype(jnp.bfloat16)
        low = probs.astype(jnp.bfloat16)
        scatter(dv_acc, wide_dot(low, spread_do, ((1,), (0,))), block, picks)
        scatter(dk_acc, wide_dot(ds, spread, ((1,), (0,))), block, picks)
        full = wide_dot(ds, keys, ((0,), (0,)))
        dq_ref[pl.ds(pl.multiple_of(mine * BLOCK, BLOCK), BLOCK), :] = (
            own_heads(full, masks) * 0.125
        ).astype(jnp.bfloat16)
        return carry

    lax.fori_loop(0, local - 1, middle, 0, unroll=unroll)
    dk_ref[...] = dk_acc[...].astype(jnp.bfloat16)
    dv_ref[...] = dv_acc[...].astype(jnp.bfloat16)


def attend_back(half, table, q, k, v, lse, do, unroll=3):
    tokens, width = q.shape
    seq = k.shape[0]
    lanes = PACK * HEAD
    groups = width // lanes
    blocks = tokens // BLOCK
    mine = pl.BlockSpec((tokens, lanes), lambda g, *_: (0, g))
    whole = pl.BlockSpec((seq, lanes), lambda g, *_: (0, g))
    spec = pltpu.PrefetchScalarGridSpec(
        num_scalar_prefetch=2,
        grid=(groups,),
        in_specs=[
            mine,
            whole,
            whole,
            pl.BlockSpec((1, blocks, lanes), lambda g, *_: (g, 0, 0)),
            mine,
        ],
        out_specs=[mine, whole, whole],
        scratch_shapes=[pltpu.VMEM((seq, lanes), jnp.float32)] * 4,
    )
    return pl.pallas_call(
        functools.partial(attend_back_kernel, unroll),
        grid_spec=spec,
        out_shape=[
            jax.ShapeDtypeStruct((tokens, width), jnp.bfloat16),
            jax.ShapeDtypeStruct((seq, width), jnp.bfloat16),
            jax.ShapeDtypeStruct((seq, width), jnp.bfloat16),
        ],
        name="attend_back",
        compiler_params=pltpu.CompilerParams(vmem_limit_bytes=56 << 20),
        cost_estimate=pl.CostEstimate(
            flops=120_000_000_000, bytes_accessed=24 << 20, transcendentals=16_000_000
        ),
    )(half, table, q, k, v, lse, do)


TILE = 256
MID = 512


def cols_mean(value):
    return jnp.mean(value, axis=-1, keepdims=True)


def normed(field):
    centred = field - cols_mean(field)
    rate = lax.rsqrt(cols_mean(centred * centred) + norm_eps)
    return centred * rate, rate


def norm_back(cot, normal, rate, gain):
    dn = cot * gain
    return rate * (dn - cols_mean(dn) - normal * cols_mean(dn * normal))


def matrix(ref):
    value = ref[...]
    return value.reshape(value.shape[1] * value.shape[3], value.shape[4])


def add_row(ref, row, value):
    ref[row : row + 1, :] += jnp.sum(value, axis=0, keepdims=True)


SLOT_AT = 5


def weight_spec(weights, which, single=True):
    shards, groups, held, rows, width = weights.shape

    def place(step, info):
        slot = info[SLOT_AT + which(step)]
        return (slot // held, 0, slot % held, 0, 0)

    mode = pl.Buffered(1) if single else None
    return pl.BlockSpec((1, groups, 1, rows, width), place, pipeline_mode=mode)


def fixed(shape):
    return pl.BlockSpec(shape, lambda step, info: (0,) * len(shape), pipeline_mode=pl.Buffered(1))


def resident(shape):
    return pl.BlockSpec(shape, lambda step, info: (0,) * len(shape))


def call(kernel, name, info, grid, in_specs, out_specs, out_shape, scratch, args, flops, moved):
    return pl.pallas_call(
        kernel,
        name=name,
        grid_spec=pltpu.PrefetchScalarGridSpec(
            num_scalar_prefetch=1,
            grid=(grid,),
            in_specs=in_specs,
            out_specs=out_specs,
            scratch_shapes=scratch,
        ),
        out_shape=out_shape,
        compiler_params=pltpu.CompilerParams(vmem_limit_bytes=60 << 20),
        cost_estimate=pl.CostEstimate(
            flops=flops, bytes_accessed=moved, transcendentals=0
        ),
    )(info, *args)


def bf16_of(*shape):
    return jax.ShapeDtypeStruct(shape, jnp.bfloat16)


def f32_of(*shape):
    return jax.ShapeDtypeStruct(shape, jnp.float32)


NN = ((1,), (0,))
NT = ((1,), (1,))
TN = ((0,), (0,))


def project_kernel(info, x_ref, small, wq, wk, wv, q_ref, k_ref, v_ref):
    x = x_ref[0]

    @pl.when(pl.program_id(0) < 2)
    def own():
        q = wide_dot(x, matrix(wq), NN) + small[0:1, :]
        q_ref[...] = q.astype(jnp.bfloat16) * jnp.bfloat16(score_scale)

    k_ref[...] = wide_dot(x, matrix(wk), NN).astype(jnp.bfloat16)
    v_ref[...] = (wide_dot(x, matrix(wv), NN) + small[1:2, :]).astype(jnp.bfloat16)


def project(info, x_all, small, weights):
    _, mid, width = x_all.shape

    def chunk(step, info):
        return lax.rem(step + 2 * info[0], 4)

    return call(
        project_kernel,
        "project",
        info,
        4,
        [
            pl.BlockSpec((1, mid, width), lambda g, info: (info[1 + chunk(g, info)], 0, 0)),
            fixed(small.shape),
            weight_spec(weights, lambda g: 0),
            weight_spec(weights, lambda g: 1),
            weight_spec(weights, lambda g: 2),
        ],
        [
            pl.BlockSpec((mid, width), lambda g, info: (jnp.minimum(g, 1), 0)),
            pl.BlockSpec((mid, width), lambda g, info: (chunk(g, info), 0)),
            pl.BlockSpec((mid, width), lambda g, info: (chunk(g, info), 0)),
        ],
        [bf16_of(2 * mid, width), bf16_of(4 * mid, width), bf16_of(4 * mid, width)],
        [],
        (x_all, small, weights, weights, weights),
        6_000_000_000,
        16 << 20,
    )


def front_kernel(
    info,
    ctx_ref,
    x_ref,
    cot_ref,
    small,
    wo,
    u0,
    u1,
    u2,
    u3,
    v0,
    v1,
    v2,
    v3,
    out_ref,
    n1_ref,
    r1_ref,
    fi_ref,
    fit_ref,
    hid_ref,
    gel_ref,
    gh2_ref,
    gmt_ref,
    sums_ref,
):
    attn_out = wide_dot(ctx_ref[...], matrix(wo), NN) + small[2:3, :]
    n1, r1 = normed(x_ref[0].astype(jnp.float32) + attn_out)
    n1_ref[...] = n1
    r1_ref[...] = jnp.broadcast_to(r1, r1_ref.shape)
    after = n1 * small[3:4, :] + small[4:5, :]
    ffn_in = after.astype(jnp.bfloat16)
    fi_ref[...] = ffn_in
    fit_ref[...] = ffn_in.T
    total = after + small[9:10, :]
    for b, (up_w, down_w) in enumerate(((u0, v0), (u1, v1), (u2, v2), (u3, v3))):
        up = wide_dot(ffn_in, matrix(up_w), NN) + small[5 + b : 6 + b, :]
        square = up * up
        bent = jnp.tanh(gelu_root * up * (1.0 + gelu_cube * square))
        rise = 0.5 * (1.0 + bent)
        hidden = (up * rise).astype(jnp.bfloat16)
        hid_ref[b] = hidden
        slope = rise + (0.5 * gelu_root) * up * (1.0 - bent * bent) * (
            1.0 + (3.0 * gelu_cube) * square
        )
        gel_ref[b] = slope.astype(jnp.bfloat16)
        total = total + wide_dot(hidden, matrix(down_w), NT)
    n2, r2 = normed(total)
    out_ref[0] = (n2 * small[10:11, :] + small[11:12, :]).astype(jnp.bfloat16)
    cot = cot_ref[0].astype(jnp.float32)
    gh2 = norm_back(cot, n2, r2, small[10:11, :])
    gh2_ref[...] = gh2
    mixed = gh2.astype(jnp.bfloat16)
    gmt_ref[...] = mixed.T

    @pl.when(pl.program_id(0) == 0)
    def clear():
        sums_ref[...] = jnp.zeros_like(sums_ref)

    add_row(sums_ref, 0, mixed.astype(jnp.float32))
    add_row(sums_ref, 1, cot * n2)
    add_row(sums_ref, 2, cot)


def front(info, ctx, x_all, cot, small, weights):
    tokens, width = ctx.shape
    mid = x_all.shape[1]
    per = mid // TILE
    steps = tokens // TILE

    def arrived(t, info):
        return (info[1 + 2 * info[0] + t // per], t % per, 0)

    def rows(dtype_shape):
        return pl.BlockSpec(dtype_shape, lambda t, info: (t, 0))

    specs = [weight_spec(weights, lambda t, m=m: m) for m in range(3, 12)]
    wide4 = pl.BlockSpec((4, TILE, width), lambda t, info: (0, t, 0))
    flipped = pl.BlockSpec((width, TILE), lambda t, info: (0, t))
    return call(
        front_kernel,
        "front",
        info,
        steps,
        [
            rows((TILE, width)),
            pl.BlockSpec((1, TILE, width), arrived),
            pl.BlockSpec((1, TILE, width), arrived),
            fixed(small.shape),
            *specs,
        ],
        [
            pl.BlockSpec((1, TILE, width), arrived),
            rows((TILE, width)),
            rows((TILE, 128)),
            rows((TILE, width)),
            flipped,
            wide4,
            wide4,
            rows((TILE, width)),
            flipped,
            resident((8, width)),
        ],
        [
            bf16_of(2, mid, width),
            f32_of(tokens, width),
            f32_of(tokens, 128),
            bf16_of(tokens, width),
            bf16_of(width, tokens),
            bf16_of(4, tokens, width),
            bf16_of(4, tokens, width),
            f32_of(tokens, width),
            bf16_of(width, tokens),
            f32_of(8, width),
        ],
        [],
        (ctx, x_all, cot, small, *([weights] * 9)),
        11_000_000_000,
        40 << 20,
    )


def back_kernel(
    info,
    gh2_ref,
    hid_ref,
    gel_ref,
    fit_ref,
    gmt_ref,
    n1_ref,
    r1_ref,
    ctx_ref,
    small,
    up_w,
    down_w,
    wo,
    pair_ref,
    dwo_ref,
    gh1_ref,
    dctx_ref,
    sums_ref,
    gy,
    gu,
):
    step = pl.program_id(0)
    tokens, width = gh2_ref.shape
    tiles = tokens // TILE
    groups, _, rows, _ = pair_ref.shape

    @pl.when(step == 0)
    def clear():
        sums_ref[...] = jnp.zeros_like(sums_ref)
        gy[...] = gh2_ref[...]

    @pl.when(step < 4)
    def ffn():
        up_block = matrix(up_w)
        down_block = matrix(down_w)

        def one(t, carry):
            at = pl.ds(pl.multiple_of(t * TILE, TILE), TILE)
            mixed = gh2_ref[at, :].astype(jnp.bfloat16)
            grad = wide_dot(mixed, down_block, NN) * gel_ref[0, at, :].astype(jnp.float32)
            low = grad.astype(jnp.bfloat16)
            gu[at, :] = low
            gy[at, :] += wide_dot(low, up_block, NT)
            sums_ref[pl.ds(step, 1), :] += jnp.sum(
                low.astype(jnp.float32), axis=0, keepdims=True
            )
            return carry

        lax.fori_loop(0, tiles, one, 0)
        grad_up = wide_dot(fit_ref[...], gu[...], NN).astype(jnp.bfloat16)
        pair_ref[:, 0:1] = grad_up.reshape(groups, 1, rows, width)
        grad_down = wide_dot(gmt_ref[...], hid_ref[0], NN).astype(jnp.bfloat16)
        pair_ref[:, 1:2] = grad_down.reshape(groups, 1, rows, width)

    @pl.when(step == 4)
    def first_norm():
        out_w = matrix(wo)

        def one(t, carry):
            at = pl.ds(pl.multiple_of(t * TILE, TILE), TILE)
            grad = gy[at, :]
            n1 = n1_ref[at, :]
            gh1 = norm_back(grad, n1, r1_ref[at, 0:1], small[3:4, :])
            gh1_ref[at, :] = gh1
            low = gh1.astype(jnp.bfloat16)
            gu[at, :] = low
            dctx_ref[at, :] = wide_dot(low, out_w, NT).astype(jnp.bfloat16)
            add_row(sums_ref, 4, low.astype(jnp.float32))
            add_row(sums_ref, 5, grad * n1)
            add_row(sums_ref, 6, grad)
            return carry

        lax.fori_loop(0, tiles, one, 0)
        grad_out = wide_dot(ctx_ref[...].T, gu[...], NN).astype(jnp.bfloat16)
        dwo_ref[...] = grad_out.reshape(dwo_ref.shape)


def back(info, gh2, hid, gel, fit, gmt, n1, r1, ctx, small, weights):
    tokens, width = gh2.shape
    _, groups, _, rows, _ = weights.shape

    def block(b, info):
        return (jnp.minimum(b, 3), 0, 0)

    return call(
        back_kernel,
        "back",
        info,
        5,
        [
            fixed((tokens, width)),
            pl.BlockSpec((1, tokens, width), block),
            pl.BlockSpec((1, tokens, width), block),
            fixed((width, tokens)),
            fixed((width, tokens)),
            fixed((tokens, width)),
            fixed((tokens, 128)),
            fixed((tokens, width)),
            fixed(small.shape),
            weight_spec(weights, lambda b: 4 + jnp.minimum(b, 3), False),
            weight_spec(weights, lambda b: 8 + jnp.minimum(b, 3), False),
            weight_spec(weights, lambda b: 3),
        ],
        [
            pl.BlockSpec((groups, 2, rows, width), lambda b, info: (0, jnp.minimum(b, 3), 0, 0)),
            resident((groups, rows, width)),
            resident((tokens, width)),
            resident((tokens, width)),
            resident((8, width)),
        ],
        [
            bf16_of(groups, 8, rows, width),
            bf16_of(groups, rows, width),
            f32_of(tokens, width),
            bf16_of(tokens, width),
            f32_of(8, width),
        ],
        [pltpu.VMEM((tokens, width), jnp.float32), pltpu.VMEM((tokens, width), jnp.bfloat16)],
        (gh2, hid, gel, fit, gmt, n1, r1, ctx, small, weights, weights, weights),
        22_000_000_000,
        40 << 20,
    )


def spill_kernel(info, dk_ref, dv_ref, wk, wv, out_ref):
    total = wide_dot(dk_ref[...], matrix(wk), NT) + wide_dot(dv_ref[...], matrix(wv), NT)
    out_ref[...] = total.astype(jnp.bfloat16)


def spill(info, dk, dv, weights):
    seq, width = dk.shape
    mid = seq // 4

    def other(b, info):
        return (2 * (1 - info[0]) + b, 0)

    return call(
        spill_kernel,
        "spill",
        info,
        2,
        [
            pl.BlockSpec((mid, width), other),
            pl.BlockSpec((mid, width), other),
            weight_spec(weights, lambda b: 1),
            weight_spec(weights, lambda b: 2),
        ],
        [pl.BlockSpec((mid, width), lambda b, info: (b, 0))],
        [bf16_of(2 * mid, width)],
        [],
        (dk, dv, weights, weights),
        2_400_000_000,
        8 << 20,
    )[0]


def weight_grads_kernel(
    info, x_ref, dq_ref, dk_ref, dv_ref, out_ref, sums_ref, q_acc, k_acc, v_acc
):
    step = pl.program_id(0)

    @pl.when(step == 0)
    def clear():
        sums_ref[...] = jnp.zeros_like(sums_ref)
        k_acc[...] = jnp.zeros_like(k_acc)
        v_acc[...] = jnp.zeros_like(v_acc)
        q_acc[...] = jnp.zeros_like(q_acc)

    flipped = x_ref[0].T
    k_acc[...] += wide_dot(flipped, dk_ref[...], NN)
    v_acc[...] += wide_dot(flipped, dv_ref[...], NN)
    add_row(sums_ref, 1, dv_ref[...].astype(jnp.float32))

    @pl.when(step < 2)
    def own():
        q_acc[...] += wide_dot(flipped, dq_ref[...], NN)
        add_row(sums_ref, 0, dq_ref[...].astype(jnp.float32))

    @pl.when(step == 3)
    def finish():
        groups, _, rows, width = out_ref.shape
        for m, acc in enumerate((q_acc, k_acc, v_acc)):
            out_ref[:, m : m + 1] = (
                acc[...].astype(jnp.bfloat16).reshape(groups, 1, rows, width)
            )


def weight_grads(info, x_all, dq, dk, dv, groups):
    _, mid, width = x_all.shape
    rows = width // groups

    def chunk(step, info):
        return lax.rem(step + 2 * info[0], 4)

    return call(
        weight_grads_kernel,
        "weight_grads",
        info,
        4,
        [
            pl.BlockSpec((1, mid, width), lambda g, info: (info[1 + chunk(g, info)], 0, 0)),
            pl.BlockSpec((mid, width), lambda g, info: (jnp.minimum(g, 1), 0)),
            pl.BlockSpec((mid, width), lambda g, info: (chunk(g, info), 0)),
            pl.BlockSpec((mid, width), lambda g, info: (chunk(g, info), 0)),
        ],
        [resident((groups, 3, rows, width)), resident((8, width))],
        [bf16_of(groups, 3, rows, width), f32_of(8, width)],
        [pltpu.VMEM((width, width), jnp.float32)] * 3,
        (x_all, dq, dk, dv),
        6_000_000_000,
        14 << 20,
    )


def input_grads_kernel(info, gh1_ref, dq_ref, dk_ref, dv_ref, more_ref, wq, wk, wv, out_ref):
    total = gh1_ref[...] + more_ref[...].astype(jnp.float32)
    total = total + wide_dot(dq_ref[...], matrix(wq), NT)
    total = total + wide_dot(dk_ref[...], matrix(wk), NT)
    total = total + wide_dot(dv_ref[...], matrix(wv), NT)
    out_ref[0] = total.astype(jnp.bfloat16)


def input_grads(info, gh1, dq, dk, dv, more, weights):
    tokens, width = gh1.shape
    steps = tokens // TILE
    mid = tokens // 2
    per = mid // TILE
    mine = pl.BlockSpec((TILE, width), lambda t, info: (t, 0))
    place = pl.BlockSpec((TILE, width), lambda t, info: (info[0] * steps + t, 0))

    return call(
        input_grads_kernel,
        "input_grads",
        info,
        steps,
        [
            mine,
            mine,
            place,
            place,
            mine,
            weight_spec(weights, lambda t: 0),
            weight_spec(weights, lambda t: 1),
            weight_spec(weights, lambda t: 2),
        ],
        [
            pl.BlockSpec(
                (1, TILE, width),
                lambda t, info: (info[1 + 2 * info[0] + t // per], t % per, 0),
            )
        ],
        [bf16_of(2, mid, width)],
        [],
        (gh1, dq, dk, dv, more, weights, weights, weights),
        3_700_000_000,
        14 << 20,
    )[0]


def adam_update(weight, first, second, grad, decay, rate):
    count = float(STEP)
    first_new = beta_one * first + (1.0 - beta_one) * grad
    second_new = beta_two * second + (1.0 - beta_two) * grad * grad
    first_hat = first_new / (1.0 - beta_one**count)
    second_hat = second_new / (1.0 - beta_two**count)
    weight_new = weight - rate * (first_hat / (jnp.sqrt(second_hat) + adam_eps) + decay * weight)
    return (weight_new, first_new, second_new)


def moves(n_ctx, n_tp, pick):
    pairs = []
    for c in range(n_ctx):
        for t in range(n_tp):
            side, core = t // 2, t % 2
            to_ctx = 2 * core + (pick ^ (c & 1))
            to_tp = 2 * side + c // 2
            pairs.append((c * n_tp + t, to_ctx * n_tp + to_tp))
    return pairs


def shards(
    inputs,
    cotangent,
    rand_blocks,
    slot_of,
    master,
    moment_one,
    moment_two,
    small_params,
    small_one,
    small_two,
):
    n_shard = lax.axis_size("shard")
    n_ctx = lax.axis_size("ctx")
    n_tp = lax.axis_size("tp")
    groups = n_ctx * n_tp
    held, rows, width = master.shape
    span = small_params.shape[0]
    my_ctx = lax.axis_index("ctx")
    my_tp = lax.axis_index("tp")
    parity = lax.rem(my_ctx, 2)
    half = lax.rem(my_tp, 2)
    plane = ("ctx", "tp")
    forth = [moves(n_ctx, n_tp, pick) for pick in range(2)]
    home = [[(b, a) for a, b in pairs] for pairs in forth]
    swap = [(t, t ^ 1) for t in range(n_tp)]

    arrival = [(b ^ parity) + 2 * (half ^ (j // 2)) for j, b in enumerate((0, 1, 0, 1))]
    info = jnp.concatenate([jnp.stack([half, *arrival]).astype(jnp.int32), slot_of])
    half_one = info[:1]

    def sent(field, pick):
        low = field.astype(jnp.bfloat16)
        return jnp.where(parity == 0, low[pick], low[1 - pick])

    def brought(field):
        pieces = [lax.ppermute(sent(field, pick), plane, forth[pick]) for pick in range(2)]
        return jnp.stack(pieces)

    def returned(field):
        first, second = [lax.ppermute(field[pick], plane, home[pick]) for pick in range(2)]
        swapped = parity == 1
        out = jnp.stack(
            [jnp.where(swapped, second, first), jnp.where(swapped, first, second)]
        )
        return out.astype(jnp.float32)

    x_own = brought(inputs)
    x_other = lax.ppermute(x_own, "tp", swap)
    x_all = jnp.concatenate([x_own, x_other])
    low = master.astype(jnp.bfloat16)
    weights = lax.all_gather(low, ("shard", "ctx", "tp"), axis=0)
    weights = weights.reshape(n_shard, groups, held, rows, width)
    small_low = small_params.astype(jnp.bfloat16)
    small = lax.all_gather(small_low, ("shard", "ctx", "tp"), axis=0, tiled=True)
    small = small.reshape(-1, width).astype(jnp.float32)

    q, k, v = project(info, x_all, small, weights)
    context, lse = attend(half_one, rand_blocks, q, k, v, 5)
    cot = brought(cotangent)
    out_low, n1, r1, fi, fit, hid, gel, gh2, gmt, sums_two = front(
        info, context, x_all, cot, small, weights
    )
    layer_out = returned(out_low)
    ffn_grads, out_grad, gh1, dctx, sums_one = back(
        info, gh2, hid, gel, fit, gmt, n1, r1, context, small, weights
    )
    ffn_rows = lax.psum_scatter(ffn_grads, plane, scatter_dimension=0, tiled=False)
    dq, dk, dv = attend_back(half_one, rand_blocks, q, k, v, lse, dctx, 5)
    more = lax.ppermute(spill(info, dk, dv, weights), "tp", swap)
    qkv_grads, sums_qkv = weight_grads(info, x_all, dq, dk, dv, groups)
    small_grad = jnp.concatenate(
        [
            sums_qkv[0],
            sums_qkv[1],
            sums_one[4],
            sums_one[5],
            sums_one[6],
            sums_one[0:4].reshape(-1),
            sums_two[0],
            sums_two[1],
            sums_two[2],
        ]
    )
    extra = -(-n_shard * span // width)
    small_rows = small_grad.reshape(n_shard, groups, span).transpose(1, 0, 2)
    small_rows = jnp.pad(
        small_rows.reshape(groups, n_shard * span), ((0, 0), (0, extra * width - n_shard * span))
    ).reshape(groups, extra, width)
    late = jnp.concatenate(
        [
            qkv_grads.reshape(groups, 3 * rows, width),
            out_grad,
            small_rows.astype(jnp.bfloat16),
        ],
        axis=1,
    )
    late_rows = lax.psum_scatter(late, plane, scatter_dimension=0, tiled=False)
    input_low = input_grads(info, gh1, dq, dk, dv, more, weights)
    input_grad = returned(input_low)

    own_rows = jnp.concatenate(
        [
            late_rows[: 4 * rows].reshape(4, rows, width),
            ffn_rows[0::2],
            ffn_rows[1::2],
        ]
    )
    picker = slot_of[None, :] == jnp.arange(n_shard * held, dtype=jnp.int32)[:, None]
    packed = jnp.einsum(
        "sm,mrd->srd", picker.astype(jnp.bfloat16), own_rows, preferred_element_type=jnp.float32
    ).astype(jnp.bfloat16)
    small_sum = late_rows[4 * rows :].reshape(-1)[: n_shard * span].reshape(n_shard, span)
    small_sum = jnp.pad(small_sum, ((0, 0), (0, width - span)))[:, None, :]
    final = jnp.concatenate([packed.reshape(n_shard, held * rows, width), small_sum], axis=1)
    final = lax.psum_scatter(final, "shard", scatter_dimension=0, tiled=False).astype(jnp.float32)
    slot_grads = final[: held * rows].reshape(held, rows, width)
    small_owned = final[held * rows, :span]
    master_new, first_new, second_new = adam_update(
        master, moment_one, moment_two, slot_grads, 0.01, rate_value
    )
    small_new, small_first, small_second = adam_update(
        small_params, small_one, small_two, small_owned, 0.0, small_rate
    )
    return (
        layer_out,
        input_grad,
        master_new,
        first_new,
        second_new,
        small_new,
        small_first,
        small_second,
    )


def solution(mesh):
    tokens = P(("shard", "tp"), "ctx", None)
    stored = P("shard", ("ctx", "tp"), None)
    spread = P(("shard", "ctx", "tp"))
    return jax.shard_map(
        shards,
        mesh=mesh,
        in_specs=(tokens, tokens, P(), P(), stored, stored, stored, spread, spread, spread),
        out_specs=(tokens, tokens, stored, stored, stored, spread, spread, spread),
        check_vma=False,
    )
```

```python
import functools

import jax
import jax.numpy as jnp
from jax import lax
from jax.experimental import pallas as pl
from jax.experimental.pallas import tpu as pltpu
from jax.sharding import PartitionSpec as P

STEP = 5
norm_eps = 1e-12
beta_one = 0.9
beta_two = 0.999
adam_eps = 1e-08
rate_value = 0.04
small_rate = 0.25
score_scale = 0.125
gelu_root = 0.7978845608
gelu_cube = 0.044715

BLOCK = 64
HEAD = 64
PACK = 4
masked_score = -1e30


def wide_dot(a, b, dims):
    return lax.dot_general(a, b, (dims, ((), ())), preferred_element_type=jnp.float32)


def head_masks(rows):
    lane = lax.broadcasted_iota(jnp.int32, (rows, PACK * HEAD), 1) // HEAD
    return [lane == h for h in range(PACK)]


def spread_heads(block, masks):
    zero = jnp.zeros_like(block)
    return jnp.concatenate([jnp.where(m, block, zero) for m in masks], axis=0)


def own_heads(full, masks):
    total = None
    for h, m in enumerate(masks):
        piece = jnp.where(m, full[h * BLOCK : (h + 1) * BLOCK], 0.0)
        total = piece if total is None else total + piece
    return total


def rows_of(ref, index, count=1):
    return ref[pl.ds(pl.multiple_of(index * BLOCK, BLOCK), count * BLOCK), :]


def picked_rows(ref, picks, low_half):
    halves = []
    for pair in range(PACK // 2):
        cols = pl.ds(pair * 2 * HEAD, 2 * HEAD)
        first = ref[pl.ds(pl.multiple_of(picks[2 * pair] * BLOCK, BLOCK), BLOCK), cols]
        second = ref[pl.ds(pl.multiple_of(picks[2 * pair + 1] * BLOCK, BLOCK), BLOCK), cols]
        halves.append(jnp.where(low_half, first, second))
    return jnp.concatenate(halves, axis=1)


def gathered(ref, block, last, picks, low_half):
    pieces = [rows_of(ref, 0), rows_of(ref, last), rows_of(ref, block - 1, 3)]
    pieces += [picked_rows(ref, p, low_half) for p in picks]
    return jnp.concatenate(pieces, axis=0)


def middle_scores(keys, spread, block, last):
    scores = wide_dot(keys, spread, ((1,), (1,)))
    first_off = jnp.where(block == 1, masked_score, 0.0)
    last_off = jnp.where(block == last - 1, masked_score, 0.0)
    b = BLOCK
    return jnp.concatenate(
        [
            scores[: 2 * b],
            scores[2 * b : 3 * b] + first_off,
            scores[3 * b : 4 * b],
            scores[4 * b : 5 * b] + last_off,
            scores[5 * b :],
        ],
        axis=0,
    )


def attend_kernel(unroll, half_ref, table_ref, q_ref, k_ref, v_ref, out_ref, lse_ref, kept):
    half = half_ref[0]
    group = pl.program_id(0)
    nblocks = k_ref.shape[0] // BLOCK
    local = q_ref.shape[0] // BLOCK
    last = nblocks - 1
    picks_each = table_ref.shape[2]
    masks = head_masks(BLOCK)
    low_half = lax.broadcasted_iota(jnp.int32, (BLOCK, 2 * HEAD), 1) < HEAD

    def middle(step, carry):
        mine = step + 1 - half
        block = mine + local * half
        picks = [
            [table_ref[group * PACK + h, block - 1, r] for h in range(PACK)]
            for r in range(picks_each)
        ]
        spread = spread_heads(rows_of(q_ref, mine), masks)
        keys = gathered(k_ref, block, last, picks, low_half)
        values = gathered(v_ref, block, last, picks, low_half)
        scores = middle_scores(keys, spread, block, last)
        top = jnp.max(scores, axis=0, keepdims=True)
        probs = jnp.exp(scores - top)
        total = jnp.sum(probs, axis=0, keepdims=True)
        low = (probs * (1.0 / total)).astype(jnp.bfloat16)
        full = wide_dot(low, values, ((0,), (0,)))
        out_ref[pl.ds(pl.multiple_of(mine * BLOCK, BLOCK), BLOCK), :] = own_heads(
            full, masks
        ).astype(jnp.bfloat16)
        lse_ref[0, pl.ds(mine, 1), :] = top + jnp.log(total)
        return carry

    lax.fori_loop(0, local - 1, middle, 0, unroll=unroll)

    edge = (local - 1) * half
    spread = spread_heads(rows_of(q_ref, edge), masks)
    span = 8 * BLOCK
    chunks = nblocks // 8
    top = None
    for c in range(chunks):
        scores = wide_dot(k_ref[c * span : (c + 1) * span, :], spread, ((1,), (1,)))
        kept[c * span : (c + 1) * span, :] = scores
        high = jnp.max(scores, axis=0, keepdims=True)
        top = high if top is None else jnp.maximum(top, high)
    total = None
    for c in range(chunks):
        probs = jnp.exp(kept[c * span : (c + 1) * span, :] - top)
        kept[c * span : (c + 1) * span, :] = probs
        part = jnp.sum(probs, axis=0, keepdims=True)
        total = part if total is None else total + part
    scale = 1.0 / total
    full = None
    for c in range(chunks):
        low = (kept[c * span : (c + 1) * span, :] * scale).astype(jnp.bfloat16)
        part = wide_dot(low, v_ref[c * span : (c + 1) * span, :], ((0,), (0,)))
        full = part if full is None else full + part
    out_ref[pl.ds(pl.multiple_of(edge * BLOCK, BLOCK), BLOCK), :] = own_heads(
        full, masks
    ).astype(jnp.bfloat16)
    lse_ref[0, pl.ds(edge, 1), :] = top + jnp.log(total)


def attend(half, table, q, k, v, unroll=3):
    tokens, width = q.shape
    seq = k.shape[0]
    lanes = PACK * HEAD
    groups = width // lanes
    blocks = tokens // BLOCK
    spec = pltpu.PrefetchScalarGridSpec(
        num_scalar_prefetch=2,
        grid=(groups,),
        in_specs=[
            pl.BlockSpec((tokens, lanes), lambda g, *_: (0, g)),
            pl.BlockSpec((seq, lanes), lambda g, *_: (0, g)),
            pl.BlockSpec((seq, lanes), lambda g, *_: (0, g)),
        ],
        out_specs=[
            pl.BlockSpec((tokens, lanes), lambda g, *_: (0, g)),
            pl.BlockSpec((1, blocks, lanes), lambda g, *_: (g, 0, 0)),
        ],
        scratch_shapes=[pltpu.VMEM((seq, lanes), jnp.float32)],
    )
    return pl.pallas_call(
        functools.partial(attend_kernel, unroll),
        grid_spec=spec,
        out_shape=[
            jax.ShapeDtypeStruct((tokens, width), jnp.bfloat16),
            jax.ShapeDtypeStruct((groups, blocks, lanes), jnp.float32),
        ],
        name="attend",
        compiler_params=pltpu.CompilerParams(vmem_limit_bytes=56 << 20),
        cost_estimate=pl.CostEstimate(
            flops=60_000_000_000, bytes_accessed=12 << 20, transcendentals=16_000_000
        ),
    )(half, table, q, k, v)


def attend_back_kernel(
    unroll,
    half_ref,
    table_ref,
    q_ref,
    k_ref,
    v_ref,
    lse_ref,
    do_ref,
    dq_ref,
    dk_ref,
    dv_ref,
    dk_acc,
    dv_acc,
    kept_p,
    kept_g,
):
    half = half_ref[0]
    group = pl.program_id(0)
    nblocks = k_ref.shape[0] // BLOCK
    local = q_ref.shape[0] // BLOCK
    last = nblocks - 1
    picks_each = table_ref.shape[2]
    masks = head_masks(BLOCK)
    low_half = lax.broadcasted_iota(jnp.int32, (BLOCK, 2 * HEAD), 1) < HEAD
    span = 8 * BLOCK
    chunks = nblocks // 8

    edge = (local - 1) * half
    spread = spread_heads(rows_of(q_ref, edge), masks)
    spread_do = spread_heads(rows_of(do_ref, edge), masks)
    lse = lse_ref[0, pl.ds(edge, 1), :]
    delta = None
    for c in range(chunks):
        rows = slice(c * span, (c + 1) * span)
        probs = jnp.exp(wide_dot(k_ref[rows, :], spread, ((1,), (1,))) - lse)
        gp = wide_dot(v_ref[rows, :], spread_do, ((1,), (1,)))
        kept_p[rows, :] = probs
        kept_g[rows, :] = gp
        part = jnp.sum(probs * gp, axis=0, keepdims=True)
        delta = part if delta is None else delta + part
    full = None
    for c in range(chunks):
        rows = slice(c * span, (c + 1) * span)
        probs = kept_p[rows, :]
        ds = (probs * (kept_g[rows, :] - delta)).astype(jnp.bfloat16)
        dv_acc[rows, :] = wide_dot(probs.astype(jnp.bfloat16), spread_do, ((1,), (0,)))
        dk_acc[rows, :] = wide_dot(ds, spread, ((1,), (0,)))
        part = wide_dot(ds, k_ref[rows, :], ((0,), (0,)))
        full = part if full is None else full + part
    dq_ref[pl.ds(pl.multiple_of(edge * BLOCK, BLOCK), BLOCK), :] = (
        own_heads(full, masks) * 0.125
    ).astype(jnp.bfloat16)

    def scatter(acc, piece, block, picks):
        b = BLOCK
        acc[0:b, :] += piece[:b]
        acc[last * b : (last + 1) * b, :] += piece[b : 2 * b]
        window = pl.ds(pl.multiple_of((block - 1) * b, b), 3 * b)
        acc[window, :] += piece[2 * b : 5 * b]
        for r, p in enumerate(picks):
            part = piece[(5 + r) * b : (6 + r) * b]
            for pair in range(PACK // 2):
                lanes = slice(pair * 2 * HEAD, (pair + 1) * 2 * HEAD)
                cols = pl.ds(pair * 2 * HEAD, 2 * HEAD)
                sub = part[:, lanes]
                acc[pl.ds(pl.multiple_of(p[2 * pair] * b, b), b), cols] += jnp.where(
                    low_half, sub, 0.0
                )
                acc[pl.ds(pl.multiple_of(p[2 * pair + 1] * b, b), b), cols] += jnp.where(
                    low_half, 0.0, sub
                )

    def middle(step, carry):
        mine = step + 1 - half
        block = mine + local * half
        picks = [
            [table_ref[group * PACK + h, block - 1, r] for h in range(PACK)]
            for r in range(picks_each)
        ]
        spread = spread_heads(rows_of(q_ref, mine), masks)
        spread_do = spread_heads(rows_of(do_ref, mine), masks)
        keys = gathered(k_ref, block, last, picks, low_half)
        values = gathered(v_ref, block, last, picks, low_half)
        scores = middle_scores(keys, spread, block, last)
        probs = jnp.exp(scores - lse_ref[0, pl.ds(mine, 1), :])
        gp = wide_dot(values, spread_do, ((1,), (1,)))
        delta = jnp.sum(probs * gp, axis=0, keepdims=True)
        ds = (probs * (gp - delta)).astype(jnp.bfloat16)
        low = probs.astype(jnp.bfloat16)
        scatter(dv_acc, wide_dot(low, spread_do, ((1,), (0,))), block, picks)
        scatter(dk_acc, wide_dot(ds, spread, ((1,), (0,))), block, picks)
        full = wide_dot(ds, keys, ((0,), (0,)))
        dq_ref[pl.ds(pl.multiple_of(mine * BLOCK, BLOCK), BLOCK), :] = (
            own_heads(full, masks) * 0.125
        ).astype(jnp.bfloat16)
        return carry

    lax.fori_loop(0, local - 1, middle, 0, unroll=unroll)
    dk_ref[...] = dk_acc[...].astype(jnp.bfloat16)
    dv_ref[...] = dv_acc[...].astype(jnp.bfloat16)


def attend_back(half, table, q, k, v, lse, do, unroll=3):
    tokens, width = q.shape
    seq = k.shape[0]
    lanes = PACK * HEAD
    groups = width // lanes
    blocks = tokens // BLOCK
    mine = pl.BlockSpec((tokens, lanes), lambda g, *_: (0, g))
    whole = pl.BlockSpec((seq, lanes), lambda g, *_: (0, g))
    spec = pltpu.PrefetchScalarGridSpec(
        num_scalar_prefetch=2,
        grid=(groups,),
        in_specs=[
            mine,
            whole,
            whole,
            pl.BlockSpec((1, blocks, lanes), lambda g, *_: (g, 0, 0)),
            mine,
        ],
        out_specs=[mine, whole, whole],
        scratch_shapes=[pltpu.VMEM((seq, lanes), jnp.float32)] * 4,
    )
    return pl.pallas_call(
        functools.partial(attend_back_kernel, unroll),
        grid_spec=spec,
        out_shape=[
            jax.ShapeDtypeStruct((tokens, width), jnp.bfloat16),
            jax.ShapeDtypeStruct((seq, width), jnp.bfloat16),
            jax.ShapeDtypeStruct((seq, width), jnp.bfloat16),
        ],
        name="attend_back",
        compiler_params=pltpu.CompilerParams(vmem_limit_bytes=56 << 20),
        cost_estimate=pl.CostEstimate(
            flops=120_000_000_000, bytes_accessed=24 << 20, transcendentals=16_000_000
        ),
    )(half, table, q, k, v, lse, do)


TILE = 256
MID = 512


def cols_mean(value):
    return jnp.mean(value, axis=-1, keepdims=True)


def normed(field):
    centred = field - cols_mean(field)
    rate = lax.rsqrt(cols_mean(centred * centred) + norm_eps)
    return centred * rate, rate


def norm_back(cot, normal, rate, gain):
    dn = cot * gain
    return rate * (dn - cols_mean(dn) - normal * cols_mean(dn * normal))


def matrix(ref):
    value = ref[...]
    return value.reshape(value.shape[1] * value.shape[3], value.shape[4])


def add_row(ref, row, value):
    ref[row : row + 1, :] += jnp.sum(value, axis=0, keepdims=True)


SLOT_AT = 5


def weight_spec(weights, which, single=True):
    shards, groups, held, rows, width = weights.shape

    def place(step, info):
        slot = info[SLOT_AT + which(step)]
        return (slot // held, 0, slot % held, 0, 0)

    mode = pl.Buffered(1) if single else None
    return pl.BlockSpec((1, groups, 1, rows, width), place, pipeline_mode=mode)


def fixed(shape):
    return pl.BlockSpec(shape, lambda step, info: (0,) * len(shape), pipeline_mode=pl.Buffered(1))


def resident(shape):
    return pl.BlockSpec(shape, lambda step, info: (0,) * len(shape))


def call(kernel, name, info, grid, in_specs, out_specs, out_shape, scratch, args, flops, moved):
    return pl.pallas_call(
        kernel,
        name=name,
        grid_spec=pltpu.PrefetchScalarGridSpec(
            num_scalar_prefetch=1,
            grid=(grid,),
            in_specs=in_specs,
            out_specs=out_specs,
            scratch_shapes=scratch,
        ),
        out_shape=out_shape,
        compiler_params=pltpu.CompilerParams(vmem_limit_bytes=60 << 20),
        cost_estimate=pl.CostEstimate(
            flops=flops, bytes_accessed=moved, transcendentals=0
        ),
    )(info, *args)


def bf16_of(*shape):
    return jax.ShapeDtypeStruct(shape, jnp.bfloat16)


def f32_of(*shape):
    return jax.ShapeDtypeStruct(shape, jnp.float32)


NN = ((1,), (0,))
NT = ((1,), (1,))
TN = ((0,), (0,))


def project_kernel(info, x_ref, small, wq, wk, wv, q_ref, k_ref, v_ref):
    x = x_ref[0]

    @pl.when(pl.program_id(0) < 2)
    def own():
        q = wide_dot(x, matrix(wq), NN) + small[0:1, :]
        q_ref[...] = q.astype(jnp.bfloat16) * jnp.bfloat16(score_scale)

    k_ref[...] = wide_dot(x, matrix(wk), NN).astype(jnp.bfloat16)
    v_ref[...] = (wide_dot(x, matrix(wv), NN) + small[1:2, :]).astype(jnp.bfloat16)


def project(info, x_all, small, weights):
    _, mid, width = x_all.shape

    def chunk(step, info):
        return lax.rem(step + 2 * info[0], 4)

    return call(
        project_kernel,
        "project",
        info,
        4,
        [
            pl.BlockSpec((1, mid, width), lambda g, info: (info[1 + chunk(g, info)], 0, 0)),
            fixed(small.shape),
            weight_spec(weights, lambda g: 0),
            weight_spec(weights, lambda g: 1),
            weight_spec(weights, lambda g: 2),
        ],
        [
            pl.BlockSpec((mid, width), lambda g, info: (jnp.minimum(g, 1), 0)),
            pl.BlockSpec((mid, width), lambda g, info: (chunk(g, info), 0)),
            pl.BlockSpec((mid, width), lambda g, info: (chunk(g, info), 0)),
        ],
        [bf16_of(2 * mid, width), bf16_of(4 * mid, width), bf16_of(4 * mid, width)],
        [],
        (x_all, small, weights, weights, weights),
        6_000_000_000,
        16 << 20,
    )


def front_kernel(
    info,
    ctx_ref,
    x_ref,
    cot_ref,
    small,
    wo,
    u0,
    u1,
    u2,
    u3,
    v0,
    v1,
    v2,
    v3,
    out_ref,
    n1_ref,
    r1_ref,
    fi_ref,
    fit_ref,
    hid_ref,
    gel_ref,
    gh2_ref,
    gmt_ref,
    sums_ref,
):
    attn_out = wide_dot(ctx_ref[...], matrix(wo), NN) + small[2:3, :]
    n1, r1 = normed(x_ref[0].astype(jnp.float32) + attn_out)
    n1_ref[...] = n1
    r1_ref[...] = jnp.broadcast_to(r1, r1_ref.shape)
    after = n1 * small[3:4, :] + small[4:5, :]
    ffn_in = after.astype(jnp.bfloat16)
    fi_ref[...] = ffn_in
    fit_ref[...] = ffn_in.T
    total = after + small[9:10, :]
    for b, (up_w, down_w) in enumerate(((u0, v0), (u1, v1), (u2, v2), (u3, v3))):
        up = wide_dot(ffn_in, matrix(up_w), NN) + small[5 + b : 6 + b, :]
        square = up * up
        bent = jnp.tanh(gelu_root * up * (1.0 + gelu_cube * square))
        rise = 0.5 * (1.0 + bent)
        hidden = (up * rise).astype(jnp.bfloat16)
        hid_ref[b] = hidden
        slope = rise + (0.5 * gelu_root) * up * (1.0 - bent * bent) * (
            1.0 + (3.0 * gelu_cube) * square
        )
        gel_ref[b] = slope.astype(jnp.bfloat16)
        total = total + wide_dot(hidden, matrix(down_w), NT)
    n2, r2 = normed(total)
    out_ref[0] = (n2 * small[10:11, :] + small[11:12, :]).astype(jnp.bfloat16)
    cot = cot_ref[0].astype(jnp.float32)
    gh2 = norm_back(cot, n2, r2, small[10:11, :])
    gh2_ref[...] = gh2
    mixed = gh2.astype(jnp.bfloat16)
    gmt_ref[...] = mixed.T

    @pl.when(pl.program_id(0) == 0)
    def clear():
        sums_ref[...] = jnp.zeros_like(sums_ref)

    add_row(sums_ref, 0, mixed.astype(jnp.float32))
    add_row(sums_ref, 1, cot * n2)
    add_row(sums_ref, 2, cot)


def front(info, ctx, x_all, cot, small, weights):
    tokens, width = ctx.shape
    mid = x_all.shape[1]
    per = mid // TILE
    steps = tokens // TILE

    def arrived(t, info):
        return (info[1 + 2 * info[0] + t // per], t % per, 0)

    def rows(dtype_shape):
        return pl.BlockSpec(dtype_shape, lambda t, info: (t, 0))

    specs = [weight_spec(weights, lambda t, m=m: m) for m in range(3, 12)]
    wide4 = pl.BlockSpec((4, TILE, width), lambda t, info: (0, t, 0))
    flipped = pl.BlockSpec((width, TILE), lambda t, info: (0, t))
    return call(
        front_kernel,
        "front",
        info,
        steps,
        [
            rows((TILE, width)),
            pl.BlockSpec((1, TILE, width), arrived),
            pl.BlockSpec((1, TILE, width), arrived),
            fixed(small.shape),
            *specs,
        ],
        [
            pl.BlockSpec((1, TILE, width), arrived),
            rows((TILE, width)),
            rows((TILE, 128)),
            rows((TILE, width)),
            flipped,
            wide4,
            wide4,
            rows((TILE, width)),
            flipped,
            resident((8, width)),
        ],
        [
            bf16_of(2, mid, width),
            f32_of(tokens, width),
            f32_of(tokens, 128),
            bf16_of(tokens, width),
            bf16_of(width, tokens),
            bf16_of(4, tokens, width),
            bf16_of(4, tokens, width),
            f32_of(tokens, width),
            bf16_of(width, tokens),
            f32_of(8, width),
        ],
        [],
        (ctx, x_all, cot, small, *([weights] * 9)),
        11_000_000_000,
        40 << 20,
    )


def back_kernel(
    info,
    gh2_ref,
    hid_ref,
    gel_ref,
    fit_ref,
    gmt_ref,
    n1_ref,
    r1_ref,
    ctx_ref,
    small,
    up_w,
    down_w,
    wo,
    pair_ref,
    dwo_ref,
    gh1_ref,
    dctx_ref,
    sums_ref,
    gy,
    gu,
):
    step = pl.program_id(0)
    tokens, width = gh2_ref.shape
    tiles = tokens // TILE
    groups, _, rows, _ = pair_ref.shape

    @pl.when(step == 0)
    def clear():
        sums_ref[...] = jnp.zeros_like(sums_ref)
        gy[...] = gh2_ref[...]

    @pl.when(step < 4)
    def ffn():
        up_block = matrix(up_w)
        down_block = matrix(down_w)

        def one(t, carry):
            at = pl.ds(pl.multiple_of(t * TILE, TILE), TILE)
            mixed = gh2_ref[at, :].astype(jnp.bfloat16)
            grad = wide_dot(mixed, down_block, NN) * gel_ref[0, at, :].astype(jnp.float32)
            low = grad.astype(jnp.bfloat16)
            gu[at, :] = low
            gy[at, :] += wide_dot(low, up_block, NT)
            sums_ref[pl.ds(step, 1), :] += jnp.sum(
                low.astype(jnp.float32), axis=0, keepdims=True
            )
            return carry

        lax.fori_loop(0, tiles, one, 0)
        grad_up = wide_dot(fit_ref[...], gu[...], NN).astype(jnp.bfloat16)
        pair_ref[:, 0:1] = grad_up.reshape(groups, 1, rows, width)
        grad_down = wide_dot(gmt_ref[...], hid_ref[0], NN).astype(jnp.bfloat16)
        pair_ref[:, 1:2] = grad_down.reshape(groups, 1, rows, width)

    @pl.when(step == 4)
    def first_norm():
        out_w = matrix(wo)

        def one(t, carry):
            at = pl.ds(pl.multiple_of(t * TILE, TILE), TILE)
            grad = gy[at, :]
            n1 = n1_ref[at, :]
            gh1 = norm_back(grad, n1, r1_ref[at, 0:1], small[3:4, :])
            gh1_ref[at, :] = gh1
            low = gh1.astype(jnp.bfloat16)
            gu[at, :] = low
            dctx_ref[at, :] = wide_dot(low, out_w, NT).astype(jnp.bfloat16)
            add_row(sums_ref, 4, low.astype(jnp.float32))
            add_row(sums_ref, 5, grad * n1)
            add_row(sums_ref, 6, grad)
            return carry

        lax.fori_loop(0, tiles, one, 0)
        grad_out = wide_dot(ctx_ref[...].T, gu[...], NN).astype(jnp.bfloat16)
        dwo_ref[...] = grad_out.reshape(dwo_ref.shape)


def back(info, gh2, hid, gel, fit, gmt, n1, r1, ctx, small, weights):
    tokens, width = gh2.shape
    _, groups, _, rows, _ = weights.shape

    def block(b, info):
        return (jnp.minimum(b, 3), 0, 0)

    return call(
        back_kernel,
        "back",
        info,
        5,
        [
            fixed((tokens, width)),
            pl.BlockSpec((1, tokens, width), block),
            pl.BlockSpec((1, tokens, width), block),
            fixed((width, tokens)),
            fixed((width, tokens)),
            fixed((tokens, width)),
            fixed((tokens, 128)),
            fixed((tokens, width)),
            fixed(small.shape),
            weight_spec(weights, lambda b: 4 + jnp.minimum(b, 3), False),
            weight_spec(weights, lambda b: 8 + jnp.minimum(b, 3), False),
            weight_spec(weights, lambda b: 3),
        ],
        [
            pl.BlockSpec((groups, 2, rows, width), lambda b, info: (0, jnp.minimum(b, 3), 0, 0)),
            resident((groups, rows, width)),
            resident((tokens, width)),
            resident((tokens, width)),
            resident((8, width)),
        ],
        [
            bf16_of(groups, 8, rows, width),
            bf16_of(groups, rows, width),
            f32_of(tokens, width),
            bf16_of(tokens, width),
            f32_of(8, width),
        ],
        [pltpu.VMEM((tokens, width), jnp.float32), pltpu.VMEM((tokens, width), jnp.bfloat16)],
        (gh2, hid, gel, fit, gmt, n1, r1, ctx, small, weights, weights, weights),
        22_000_000_000,
        40 << 20,
    )


def spill_kernel(info, dk_ref, dv_ref, wk, wv, out_ref):
    total = wide_dot(dk_ref[...], matrix(wk), NT) + wide_dot(dv_ref[...], matrix(wv), NT)
    out_ref[...] = total.astype(jnp.bfloat16)


def spill(info, dk, dv, weights):
    seq, width = dk.shape
    mid = seq // 4

    def other(b, info):
        return (2 * (1 - info[0]) + b, 0)

    return call(
        spill_kernel,
        "spill",
        info,
        2,
        [
            pl.BlockSpec((mid, width), other),
            pl.BlockSpec((mid, width), other),
            weight_spec(weights, lambda b: 1),
            weight_spec(weights, lambda b: 2),
        ],
        [pl.BlockSpec((mid, width), lambda b, info: (b, 0))],
        [bf16_of(2 * mid, width)],
        [],
        (dk, dv, weights, weights),
        2_400_000_000,
        8 << 20,
    )[0]


def weight_grads_kernel(
    info, x_ref, dq_ref, dk_ref, dv_ref, out_ref, sums_ref, q_acc, k_acc, v_acc
):
    step = pl.program_id(0)

    @pl.when(step == 0)
    def clear():
        sums_ref[...] = jnp.zeros_like(sums_ref)
        k_acc[...] = jnp.zeros_like(k_acc)
        v_acc[...] = jnp.zeros_like(v_acc)
        q_acc[...] = jnp.zeros_like(q_acc)

    flipped = x_ref[0].T
    k_acc[...] += wide_dot(flipped, dk_ref[...], NN)
    v_acc[...] += wide_dot(flipped, dv_ref[...], NN)
    add_row(sums_ref, 1, dv_ref[...].astype(jnp.float32))

    @pl.when(step < 2)
    def own():
        q_acc[...] += wide_dot(flipped, dq_ref[...], NN)
        add_row(sums_ref, 0, dq_ref[...].astype(jnp.float32))

    @pl.when(step == 3)
    def finish():
        groups, _, rows, width = out_ref.shape
        for m, acc in enumerate((q_acc, k_acc, v_acc)):
            out_ref[:, m : m + 1] = (
                acc[...].astype(jnp.bfloat16).reshape(groups, 1, rows, width)
            )


def weight_grads(info, x_all, dq, dk, dv, groups):
    _, mid, width = x_all.shape
    rows = width // groups

    def chunk(step, info):
        return lax.rem(step + 2 * info[0], 4)

    return call(
        weight_grads_kernel,
        "weight_grads",
        info,
        4,
        [
            pl.BlockSpec((1, mid, width), lambda g, info: (info[1 + chunk(g, info)], 0, 0)),
            pl.BlockSpec((mid, width), lambda g, info: (jnp.minimum(g, 1), 0)),
            pl.BlockSpec((mid, width), lambda g, info: (chunk(g, info), 0)),
            pl.BlockSpec((mid, width), lambda g, info: (chunk(g, info), 0)),
        ],
        [resident((groups, 3, rows, width)), resident((8, width))],
        [bf16_of(groups, 3, rows, width), f32_of(8, width)],
        [pltpu.VMEM((width, width), jnp.float32)] * 3,
        (x_all, dq, dk, dv),
        6_000_000_000,
        14 << 20,
    )


def input_grads_kernel(info, gh1_ref, dq_ref, dk_ref, dv_ref, more_ref, wq, wk, wv, out_ref):
    total = gh1_ref[...] + more_ref[...].astype(jnp.float32)
    total = total + wide_dot(dq_ref[...], matrix(wq), NT)
    total = total + wide_dot(dk_ref[...], matrix(wk), NT)
    total = total + wide_dot(dv_ref[...], matrix(wv), NT)
    out_ref[0] = total.astype(jnp.bfloat16)


def input_grads(info, gh1, dq, dk, dv, more, weights):
    tokens, width = gh1.shape
    steps = tokens // TILE
    mid = tokens // 2
    per = mid // TILE
    mine = pl.BlockSpec((TILE, width), lambda t, info: (t, 0))
    place = pl.BlockSpec((TILE, width), lambda t, info: (info[0] * steps + t, 0))

    return call(
        input_grads_kernel,
        "input_grads",
        info,
        steps,
        [
            mine,
            mine,
            place,
            place,
            mine,
            weight_spec(weights, lambda t: 0),
            weight_spec(weights, lambda t: 1),
            weight_spec(weights, lambda t: 2),
        ],
        [
            pl.BlockSpec(
                (1, TILE, width),
                lambda t, info: (info[1 + 2 * info[0] + t // per], t % per, 0),
            )
        ],
        [bf16_of(2, mid, width)],
        [],
        (gh1, dq, dk, dv, more, weights, weights, weights),
        3_700_000_000,
        14 << 20,
    )[0]


def adam_update(weight, first, second, grad, decay, rate):
    count = float(STEP)
    first_new = beta_one * first + (1.0 - beta_one) * grad
    second_new = beta_two * second + (1.0 - beta_two) * grad * grad
    first_hat = first_new / (1.0 - beta_one**count)
    second_hat = second_new / (1.0 - beta_two**count)
    weight_new = weight - rate * (first_hat / (jnp.sqrt(second_hat) + adam_eps) + decay * weight)
    return (weight_new, first_new, second_new)


def moves(n_ctx, n_tp, pick):
    pairs = []
    for c in range(n_ctx):
        for t in range(n_tp):
            side, core = t // 2, t % 2
            to_ctx = 2 * core + (pick ^ (c & 1))
            to_tp = 2 * side + c // 2
            pairs.append((c * n_tp + t, to_ctx * n_tp + to_tp))
    return pairs


def shards(
    inputs,
    cotangent,
    rand_blocks,
    slot_of,
    master,
    moment_one,
    moment_two,
    small_params,
    small_one,
    small_two,
):
    n_shard = lax.axis_size("shard")
    n_ctx = lax.axis_size("ctx")
    n_tp = lax.axis_size("tp")
    groups = n_ctx * n_tp
    held, rows, width = master.shape
    span = small_params.shape[0]
    my_ctx = lax.axis_index("ctx")
    my_tp = lax.axis_index("tp")
    parity = lax.rem(my_ctx, 2)
    half = lax.rem(my_tp, 2)
    plane = ("ctx", "tp")
    forth = [moves(n_ctx, n_tp, pick) for pick in range(2)]
    home = [[(b, a) for a, b in pairs] for pairs in forth]
    swap = [(t, t ^ 1) for t in range(n_tp)]

    arrival = [(b ^ parity) + 2 * (half ^ (j // 2)) for j, b in enumerate((0, 1, 0, 1))]
    info = jnp.concatenate([jnp.stack([half, *arrival]).astype(jnp.int32), slot_of])
    half_one = info[:1]

    def sent(field, pick):
        low = field.astype(jnp.bfloat16)
        return jnp.where(parity == 0, low[pick], low[1 - pick])

    def brought(field):
        pieces = [lax.ppermute(sent(field, pick), plane, forth[pick]) for pick in range(2)]
        return jnp.stack(pieces)

    def returned(field):
        first, second = [lax.ppermute(field[pick], plane, home[pick]) for pick in range(2)]
        swapped = parity == 1
        out = jnp.stack(
            [jnp.where(swapped, second, first), jnp.where(swapped, first, second)]
        )
        return out.astype(jnp.float32)

    x_own = brought(inputs)
    x_other = lax.ppermute(x_own, "tp", swap)
    x_all = jnp.concatenate([x_own, x_other])
    low = master.astype(jnp.bfloat16)
    weights = lax.all_gather(low, ("shard", "ctx", "tp"), axis=0)
    weights = weights.reshape(n_shard, groups, held, rows, width)
    small_low = small_params.astype(jnp.bfloat16)
    small = lax.all_gather(small_low, ("shard", "ctx", "tp"), axis=0, tiled=True)
    small = small.reshape(-1, width).astype(jnp.float32)

    q, k, v = project(info, x_all, small, weights)
    context, lse = attend(half_one, rand_blocks, q, k, v, 5)
    cot = brought(cotangent)
    out_low, n1, r1, fi, fit, hid, gel, gh2, gmt, sums_two = front(
        info, context, x_all, cot, small, weights
    )
    layer_out = returned(out_low)
    ffn_grads, out_grad, gh1, dctx, sums_one = back(
        info, gh2, hid, gel, fit, gmt, n1, r1, context, small, weights
    )
    ffn_rows = lax.psum_scatter(ffn_grads, plane, scatter_dimension=0, tiled=False)
    dq, dk, dv = attend_back(half_one, rand_blocks, q, k, v, lse, dctx, 5)
    more = lax.ppermute(spill(info, dk, dv, weights), "tp", swap)
    qkv_grads, sums_qkv = weight_grads(info, x_all, dq, dk, dv, groups)
    small_grad = jnp.concatenate(
        [
            sums_qkv[0],
            sums_qkv[1],
            sums_one[4],
            sums_one[5],
            sums_one[6],
            sums_one[0:4].reshape(-1),
            sums_two[0],
            sums_two[1],
            sums_two[2],
        ]
    )
    extra = -(-n_shard * span // width)
    small_rows = small_grad.reshape(n_shard, groups, span).transpose(1, 0, 2)
    small_rows = jnp.pad(
        small_rows.reshape(groups, n_shard * span), ((0, 0), (0, extra * width - n_shard * span))
    ).reshape(groups, extra, width)
    late = jnp.concatenate(
        [
            qkv_grads.reshape(groups, 3 * rows, width),
            out_grad,
            small_rows.astype(jnp.bfloat16),
        ],
        axis=1,
    )
    late, ffn_rows = lax.optimization_barrier((late, ffn_rows))
    late_rows = lax.psum_scatter(late, plane, scatter_dimension=0, tiled=False)
    input_low = input_grads(info, gh1, dq, dk, dv, more, weights)
    input_grad = returned(input_low)

    own_rows = jnp.concatenate(
        [
            late_rows[: 4 * rows].reshape(4, rows, width),
            ffn_rows[0::2],
            ffn_rows[1::2],
        ]
    )
    picker = slot_of[None, :] == jnp.arange(n_shard * held, dtype=jnp.int32)[:, None]
    packed = jnp.einsum(
        "sm,mrd->srd", picker.astype(jnp.bfloat16), own_rows, preferred_element_type=jnp.float32
    ).astype(jnp.bfloat16)
    small_sum = late_rows[4 * rows :].reshape(-1)[: n_shard * span].reshape(n_shard, span)
    small_sum = jnp.pad(small_sum, ((0, 0), (0, width - span)))[:, None, :]
    final = jnp.concatenate([packed.reshape(n_shard, held * rows, width), small_sum], axis=1)
    final = lax.psum_scatter(final, "shard", scatter_dimension=0, tiled=False).astype(jnp.float32)
    slot_grads = final[: held * rows].reshape(held, rows, width)
    small_owned = final[held * rows, :span]
    master_new, first_new, second_new = adam_update(
        master, moment_one, moment_two, slot_grads, 0.01, rate_value
    )
    small_new, small_first, small_second = adam_update(
        small_params, small_one, small_two, small_owned, 0.0, small_rate
    )
    return (
        layer_out,
        input_grad,
        master_new,
        first_new,
        second_new,
        small_new,
        small_first,
        small_second,
    )


def solution(mesh):
    tokens = P(("shard", "tp"), "ctx", None)
    stored = P("shard", ("ctx", "tp"), None)
    spread = P(("shard", "ctx", "tp"))
    return jax.shard_map(
        shards,
        mesh=mesh,
        in_specs=(tokens, tokens, P(), P(), stored, stored, stored, spread, spread, spread),
        out_specs=(tokens, tokens, stored, stored, stored, spread, spread, spread),
        check_vma=False,
    )
```

```python
import functools

import jax
import jax.numpy as jnp
from jax import lax
from jax.experimental import pallas as pl
from jax.experimental.pallas import tpu as pltpu
from jax.sharding import PartitionSpec as P

STEP = 5
norm_eps = 1e-12
beta_one = 0.9
beta_two = 0.999
adam_eps = 1e-08
rate_value = 0.04
small_rate = 0.25
score_scale = 0.125
gelu_root = 0.7978845608
gelu_cube = 0.044715

BLOCK = 64
HEAD = 64
PACK = 4
masked_score = -1e30


def wide_dot(a, b, dims):
    return lax.dot_general(a, b, (dims, ((), ())), preferred_element_type=jnp.float32)


def head_masks(rows):
    lane = lax.broadcasted_iota(jnp.int32, (rows, PACK * HEAD), 1) // HEAD
    return [lane == h for h in range(PACK)]


def spread_heads(block, masks):
    zero = jnp.zeros_like(block)
    return jnp.concatenate([jnp.where(m, block, zero) for m in masks], axis=0)


def own_heads(full, masks):
    total = None
    for h, m in enumerate(masks):
        piece = jnp.where(m, full[h * BLOCK : (h + 1) * BLOCK], 0.0)
        total = piece if total is None else total + piece
    return total


def rows_of(ref, index, count=1):
    return ref[pl.ds(pl.multiple_of(index * BLOCK, BLOCK), count * BLOCK), :]


def picked_rows(ref, picks, low_half):
    halves = []
    for pair in range(PACK // 2):
        cols = pl.ds(pair * 2 * HEAD, 2 * HEAD)
        first = ref[pl.ds(pl.multiple_of(picks[2 * pair] * BLOCK, BLOCK), BLOCK), cols]
        second = ref[pl.ds(pl.multiple_of(picks[2 * pair + 1] * BLOCK, BLOCK), BLOCK), cols]
        halves.append(jnp.where(low_half, first, second))
    return jnp.concatenate(halves, axis=1)


def gathered(ref, block, last, picks, low_half):
    pieces = [rows_of(ref, 0), rows_of(ref, last), rows_of(ref, block - 1, 3)]
    pieces += [picked_rows(ref, p, low_half) for p in picks]
    return jnp.concatenate(pieces, axis=0)


def middle_scores(keys, spread, block, last):
    scores = wide_dot(keys, spread, ((1,), (1,)))
    first_off = jnp.where(block == 1, masked_score, 0.0)
    last_off = jnp.where(block == last - 1, masked_score, 0.0)
    b = BLOCK
    return jnp.concatenate(
        [
            scores[: 2 * b],
            scores[2 * b : 3 * b] + first_off,
            scores[3 * b : 4 * b],
            scores[4 * b : 5 * b] + last_off,
            scores[5 * b :],
        ],
        axis=0,
    )


def attend_kernel(unroll, half_ref, table_ref, q_ref, k_ref, v_ref, out_ref, lse_ref, kept):
    half = half_ref[0]
    group = pl.program_id(0)
    nblocks = k_ref.shape[0] // BLOCK
    local = q_ref.shape[0] // BLOCK
    last = nblocks - 1
    picks_each = table_ref.shape[2]
    masks = head_masks(BLOCK)
    low_half = lax.broadcasted_iota(jnp.int32, (BLOCK, 2 * HEAD), 1) < HEAD

    def middle(step, carry):
        mine = step + 1 - half
        block = mine + local * half
        picks = [
            [table_ref[group * PACK + h, block - 1, r] for h in range(PACK)]
            for r in range(picks_each)
        ]
        spread = spread_heads(rows_of(q_ref, mine), masks)
        keys = gathered(k_ref, block, last, picks, low_half)
        values = gathered(v_ref, block, last, picks, low_half)
        scores = middle_scores(keys, spread, block, last)
        top = jnp.max(scores, axis=0, keepdims=True)
        probs = jnp.exp(scores - top)
        total = jnp.sum(probs, axis=0, keepdims=True)
        low = (probs * (1.0 / total)).astype(jnp.bfloat16)
        full = wide_dot(low, values, ((0,), (0,)))
        out_ref[pl.ds(pl.multiple_of(mine * BLOCK, BLOCK), BLOCK), :] = own_heads(
            full, masks
        ).astype(jnp.bfloat16)
        lse_ref[0, pl.ds(mine, 1), :] = top + jnp.log(total)
        return carry

    lax.fori_loop(0, local - 1, middle, 0, unroll=unroll)

    edge = (local - 1) * half
    spread = spread_heads(rows_of(q_ref, edge), masks)
    span = 8 * BLOCK
    chunks = nblocks // 8
    top = None
    for c in range(chunks):
        scores = wide_dot(k_ref[c * span : (c + 1) * span, :], spread, ((1,), (1,)))
        kept[c * span : (c + 1) * span, :] = scores
        high = jnp.max(scores, axis=0, keepdims=True)
        top = high if top is None else jnp.maximum(top, high)
    total = None
    for c in range(chunks):
        probs = jnp.exp(kept[c * span : (c + 1) * span, :] - top)
        kept[c * span : (c + 1) * span, :] = probs
        part = jnp.sum(probs, axis=0, keepdims=True)
        total = part if total is None else total + part
    scale = 1.0 / total
    full = None
    for c in range(chunks):
        low = (kept[c * span : (c + 1) * span, :] * scale).astype(jnp.bfloat16)
        part = wide_dot(low, v_ref[c * span : (c + 1) * span, :], ((0,), (0,)))
        full = part if full is None else full + part
    out_ref[pl.ds(pl.multiple_of(edge * BLOCK, BLOCK), BLOCK), :] = own_heads(
        full, masks
    ).astype(jnp.bfloat16)
    lse_ref[0, pl.ds(edge, 1), :] = top + jnp.log(total)


def attend(half, table, q, k, v, unroll=3):
    tokens, width = q.shape
    seq = k.shape[0]
    lanes = PACK * HEAD
    groups = width // lanes
    blocks = tokens // BLOCK
    spec = pltpu.PrefetchScalarGridSpec(
        num_scalar_prefetch=2,
        grid=(groups,),
        in_specs=[
            pl.BlockSpec((tokens, lanes), lambda g, *_: (0, g)),
            pl.BlockSpec((seq, lanes), lambda g, *_: (0, g)),
            pl.BlockSpec((seq, lanes), lambda g, *_: (0, g)),
        ],
        out_specs=[
            pl.BlockSpec((tokens, lanes), lambda g, *_: (0, g)),
            pl.BlockSpec((1, blocks, lanes), lambda g, *_: (g, 0, 0)),
        ],
        scratch_shapes=[pltpu.VMEM((seq, lanes), jnp.float32)],
    )
    return pl.pallas_call(
        functools.partial(attend_kernel, unroll),
        grid_spec=spec,
        out_shape=[
            jax.ShapeDtypeStruct((tokens, width), jnp.bfloat16),
            jax.ShapeDtypeStruct((groups, blocks, lanes), jnp.float32),
        ],
        name="attend",
        compiler_params=pltpu.CompilerParams(vmem_limit_bytes=56 << 20),
        cost_estimate=pl.CostEstimate(
            flops=60_000_000_000, bytes_accessed=12 << 20, transcendentals=16_000_000
        ),
    )(half, table, q, k, v)


def attend_back_kernel(
    unroll,
    half_ref,
    table_ref,
    q_ref,
    k_ref,
    v_ref,
    lse_ref,
    do_ref,
    dq_ref,
    dk_ref,
    dv_ref,
    dk_acc,
    dv_acc,
    kept_p,
    kept_g,
):
    half = half_ref[0]
    group = pl.program_id(0)
    nblocks = k_ref.shape[0] // BLOCK
    local = q_ref.shape[0] // BLOCK
    last = nblocks - 1
    picks_each = table_ref.shape[2]
    masks = head_masks(BLOCK)
    low_half = lax.broadcasted_iota(jnp.int32, (BLOCK, 2 * HEAD), 1) < HEAD
    span = 8 * BLOCK
    chunks = nblocks // 8

    edge = (local - 1) * half
    spread = spread_heads(rows_of(q_ref, edge), masks)
    spread_do = spread_heads(rows_of(do_ref, edge), masks)
    lse = lse_ref[0, pl.ds(edge, 1), :]
    delta = None
    for c in range(chunks):
        rows = slice(c * span, (c + 1) * span)
        probs = jnp.exp(wide_dot(k_ref[rows, :], spread, ((1,), (1,))) - lse)
        gp = wide_dot(v_ref[rows, :], spread_do, ((1,), (1,)))
        kept_p[rows, :] = probs
        kept_g[rows, :] = gp
        part = jnp.sum(probs * gp, axis=0, keepdims=True)
        delta = part if delta is None else delta + part
    full = None
    for c in range(chunks):
        rows = slice(c * span, (c + 1) * span)
        probs = kept_p[rows, :]
        ds = (probs * (kept_g[rows, :] - delta)).astype(jnp.bfloat16)
        dv_acc[rows, :] = wide_dot(probs.astype(jnp.bfloat16), spread_do, ((1,), (0,)))
        dk_acc[rows, :] = wide_dot(ds, spread, ((1,), (0,)))
        part = wide_dot(ds, k_ref[rows, :], ((0,), (0,)))
        full = part if full is None else full + part
    dq_ref[pl.ds(pl.multiple_of(edge * BLOCK, BLOCK), BLOCK), :] = (
        own_heads(full, masks) * 0.125
    ).astype(jnp.bfloat16)

    def scatter(acc, piece, block, picks):
        b = BLOCK
        acc[0:b, :] += piece[:b]
        acc[last * b : (last + 1) * b, :] += piece[b : 2 * b]
        window = pl.ds(pl.multiple_of((block - 1) * b, b), 3 * b)
        acc[window, :] += piece[2 * b : 5 * b]
        for r, p in enumerate(picks):
            part = piece[(5 + r) * b : (6 + r) * b]
            for pair in range(PACK // 2):
                lanes = slice(pair * 2 * HEAD, (pair + 1) * 2 * HEAD)
                cols = pl.ds(pair * 2 * HEAD, 2 * HEAD)
                sub = part[:, lanes]
                acc[pl.ds(pl.multiple_of(p[2 * pair] * b, b), b), cols] += jnp.where(
                    low_half, sub, 0.0
                )
                acc[pl.ds(pl.multiple_of(p[2 * pair + 1] * b, b), b), cols] += jnp.where(
                    low_half, 0.0, sub
                )

    def middle(step, carry):
        mine = step + 1 - half
        block = mine + local * half
        picks = [
            [table_ref[group * PACK + h, block - 1, r] for h in range(PACK)]
            for r in range(picks_each)
        ]
        spread = spread_heads(rows_of(q_ref, mine), masks)
        spread_do = spread_heads(rows_of(do_ref, mine), masks)
        keys = gathered(k_ref, block, last, picks, low_half)
        values = gathered(v_ref, block, last, picks, low_half)
        scores = middle_scores(keys, spread, block, last)
        probs = jnp.exp(scores - lse_ref[0, pl.ds(mine, 1), :])
        gp = wide_dot(values, spread_do, ((1,), (1,)))
        delta = jnp.sum(probs * gp, axis=0, keepdims=True)
        ds = (probs * (gp - delta)).astype(jnp.bfloat16)
        low = probs.astype(jnp.bfloat16)
        scatter(dv_acc, wide_dot(low, spread_do, ((1,), (0,))), block, picks)
        scatter(dk_acc, wide_dot(ds, spread, ((1,), (0,))), block, picks)
        full = wide_dot(ds, keys, ((0,), (0,)))
        dq_ref[pl.ds(pl.multiple_of(mine * BLOCK, BLOCK), BLOCK), :] = (
            own_heads(full, masks) * 0.125
        ).astype(jnp.bfloat16)
        return carry

    lax.fori_loop(0, local - 1, middle, 0, unroll=unroll)
    dk_ref[...] = dk_acc[...].astype(jnp.bfloat16)
    dv_ref[...] = dv_acc[...].astype(jnp.bfloat16)


def attend_back(half, table, q, k, v, lse, do, unroll=3):
    tokens, width = q.shape
    seq = k.shape[0]
    lanes = PACK * HEAD
    groups = width // lanes
    blocks = tokens // BLOCK
    mine = pl.BlockSpec((tokens, lanes), lambda g, *_: (0, g))
    whole = pl.BlockSpec((seq, lanes), lambda g, *_: (0, g))
    spec = pltpu.PrefetchScalarGridSpec(
        num_scalar_prefetch=2,
        grid=(groups,),
        in_specs=[
            mine,
            whole,
            whole,
            pl.BlockSpec((1, blocks, lanes), lambda g, *_: (g, 0, 0)),
            mine,
        ],
        out_specs=[mine, whole, whole],
        scratch_shapes=[pltpu.VMEM((seq, lanes), jnp.float32)] * 4,
    )
    return pl.pallas_call(
        functools.partial(attend_back_kernel, unroll),
        grid_spec=spec,
        out_shape=[
            jax.ShapeDtypeStruct((tokens, width), jnp.bfloat16),
            jax.ShapeDtypeStruct((seq, width), jnp.bfloat16),
            jax.ShapeDtypeStruct((seq, width), jnp.bfloat16),
        ],
        name="attend_back",
        compiler_params=pltpu.CompilerParams(vmem_limit_bytes=56 << 20),
        cost_estimate=pl.CostEstimate(
            flops=120_000_000_000, bytes_accessed=24 << 20, transcendentals=16_000_000
        ),
    )(half, table, q, k, v, lse, do)


TILE = 256
MID = 512


def cols_mean(value):
    return jnp.mean(value, axis=-1, keepdims=True)


def normed(field):
    centred = field - cols_mean(field)
    rate = lax.rsqrt(cols_mean(centred * centred) + norm_eps)
    return centred * rate, rate


def norm_back(cot, normal, rate, gain):
    dn = cot * gain
    return rate * (dn - cols_mean(dn) - normal * cols_mean(dn * normal))


def matrix(ref):
    value = ref[...]
    return value.reshape(-1, value.shape[-1])


def add_row(ref, row, value):
    ref[row : row + 1, :] += jnp.sum(value, axis=0, keepdims=True)


def first_spec(first, rows, which):
    groups, _, width = first.shape
    return pl.BlockSpec(
        (groups, rows, width), lambda step, info: (0, which, 0), pipeline_mode=pl.Buffered(1)
    )


def rest_spec(rest, which, single=True):
    groups, _, rows, width = rest.shape
    mode = pl.Buffered(1) if single else None
    return pl.BlockSpec(
        (groups, 1, rows, width), lambda step, info: (0, which(step) - 3, 0, 0), pipeline_mode=mode
    )


def fixed(shape):
    return pl.BlockSpec(shape, lambda step, info: (0,) * len(shape), pipeline_mode=pl.Buffered(1))


def resident(shape):
    return pl.BlockSpec(shape, lambda step, info: (0,) * len(shape))


def call(kernel, name, info, grid, in_specs, out_specs, out_shape, scratch, args, flops, moved):
    return pl.pallas_call(
        kernel,
        name=name,
        grid_spec=pltpu.PrefetchScalarGridSpec(
            num_scalar_prefetch=1,
            grid=(grid,),
            in_specs=in_specs,
            out_specs=out_specs,
            scratch_shapes=scratch,
        ),
        out_shape=out_shape,
        compiler_params=pltpu.CompilerParams(vmem_limit_bytes=60 << 20),
        cost_estimate=pl.CostEstimate(
            flops=flops, bytes_accessed=moved, transcendentals=0
        ),
    )(info, *args)


def bf16_of(*shape):
    return jax.ShapeDtypeStruct(shape, jnp.bfloat16)


def f32_of(*shape):
    return jax.ShapeDtypeStruct(shape, jnp.float32)


NN = ((1,), (0,))
NT = ((1,), (1,))
TN = ((0,), (0,))


def project_kernel(info, x_ref, small, wq, wk, wv, q_ref, k_ref, v_ref):
    x = x_ref[0]

    @pl.when(pl.program_id(0) < 2)
    def own():
        q = wide_dot(x, matrix(wq), NN) + small[0:1, :]
        q_ref[...] = q.astype(jnp.bfloat16) * jnp.bfloat16(score_scale)

    k_ref[...] = wide_dot(x, matrix(wk), NN).astype(jnp.bfloat16)
    v_ref[...] = (wide_dot(x, matrix(wv), NN) + small[1:2, :]).astype(jnp.bfloat16)


def project(info, x_all, small, first, rows):
    _, mid, width = x_all.shape

    def chunk(step, info):
        return lax.rem(step + 2 * info[0], 4)

    return call(
        project_kernel,
        "project",
        info,
        4,
        [
            pl.BlockSpec((1, mid, width), lambda g, info: (info[1 + chunk(g, info)], 0, 0)),
            fixed(small.shape),
            *[first_spec(first, rows, m) for m in range(3)],
        ],
        [
            pl.BlockSpec((mid, width), lambda g, info: (jnp.minimum(g, 1), 0)),
            pl.BlockSpec((mid, width), lambda g, info: (chunk(g, info), 0)),
            pl.BlockSpec((mid, width), lambda g, info: (chunk(g, info), 0)),
        ],
        [bf16_of(2 * mid, width), bf16_of(4 * mid, width), bf16_of(4 * mid, width)],
        [],
        (x_all, small, first, first, first),
        6_000_000_000,
        16 << 20,
    )


def front_kernel(
    info,
    ctx_ref,
    x_ref,
    cot_ref,
    small,
    wo,
    u0,
    u1,
    u2,
    u3,
    v0,
    v1,
    v2,
    v3,
    out_ref,
    n1_ref,
    r1_ref,
    fi_ref,
    fit_ref,
    hid_ref,
    gel_ref,
    gh2_ref,
    gmt_ref,
    sums_ref,
):
    attn_out = wide_dot(ctx_ref[...], matrix(wo), NN) + small[2:3, :]
    n1, r1 = normed(x_ref[0].astype(jnp.float32) + attn_out)
    n1_ref[...] = n1
    r1_ref[...] = jnp.broadcast_to(r1, r1_ref.shape)
    after = n1 * small[3:4, :] + small[4:5, :]
    ffn_in = after.astype(jnp.bfloat16)
    fi_ref[...] = ffn_in
    fit_ref[...] = ffn_in.T
    total = after + small[9:10, :]
    for b, (up_w, down_w) in enumerate(((u0, v0), (u1, v1), (u2, v2), (u3, v3))):
        up = wide_dot(ffn_in, matrix(up_w), NN) + small[5 + b : 6 + b, :]
        square = up * up
        bent = jnp.tanh(gelu_root * up * (1.0 + gelu_cube * square))
        rise = 0.5 * (1.0 + bent)
        hidden = (up * rise).astype(jnp.bfloat16)
        hid_ref[b] = hidden
        slope = rise + (0.5 * gelu_root) * up * (1.0 - bent * bent) * (
            1.0 + (3.0 * gelu_cube) * square
        )
        gel_ref[b] = slope.astype(jnp.bfloat16)
        total = total + wide_dot(hidden, matrix(down_w), NT)
    n2, r2 = normed(total)
    out_ref[0] = (n2 * small[10:11, :] + small[11:12, :]).astype(jnp.bfloat16)
    cot = cot_ref[0].astype(jnp.float32)
    gh2 = norm_back(cot, n2, r2, small[10:11, :])
    gh2_ref[...] = gh2
    mixed = gh2.astype(jnp.bfloat16)
    gmt_ref[...] = mixed.T

    @pl.when(pl.program_id(0) == 0)
    def clear():
        sums_ref[...] = jnp.zeros_like(sums_ref)

    add_row(sums_ref, 0, mixed.astype(jnp.float32))
    add_row(sums_ref, 1, cot * n2)
    add_row(sums_ref, 2, cot)


def front(info, ctx, x_all, cot, small, rest):
    tokens, width = ctx.shape
    mid = x_all.shape[1]
    per = mid // TILE
    steps = tokens // TILE

    def arrived(t, info):
        return (info[1 + 2 * info[0] + t // per], t % per, 0)

    def rows(dtype_shape):
        return pl.BlockSpec(dtype_shape, lambda t, info: (t, 0))

    specs = [rest_spec(rest, lambda t, m=m: m) for m in range(3, 12)]
    wide4 = pl.BlockSpec((4, TILE, width), lambda t, info: (0, t, 0))
    flipped = pl.BlockSpec((width, TILE), lambda t, info: (0, t))
    return call(
        front_kernel,
        "front",
        info,
        steps,
        [
            rows((TILE, width)),
            pl.BlockSpec((1, TILE, width), arrived),
            pl.BlockSpec((1, TILE, width), arrived),
            fixed(small.shape),
            *specs,
        ],
        [
            pl.BlockSpec((1, TILE, width), arrived),
            rows((TILE, width)),
            rows((TILE, 128)),
            rows((TILE, width)),
            flipped,
            wide4,
            wide4,
            rows((TILE, width)),
            flipped,
            resident((8, width)),
        ],
        [
            bf16_of(2, mid, width),
            f32_of(tokens, width),
            f32_of(tokens, 128),
            bf16_of(tokens, width),
            bf16_of(width, tokens),
            bf16_of(4, tokens, width),
            bf16_of(4, tokens, width),
            f32_of(tokens, width),
            bf16_of(width, tokens),
            f32_of(8, width),
        ],
        [],
        (ctx, x_all, cot, small, *([rest] * 9)),
        11_000_000_000,
        40 << 20,
    )


def back_kernel(
    info,
    gh2_ref,
    hid_ref,
    gel_ref,
    fit_ref,
    gmt_ref,
    n1_ref,
    r1_ref,
    ctx_ref,
    small,
    up_w,
    down_w,
    wo,
    pair_ref,
    dwo_ref,
    gh1_ref,
    dctx_ref,
    sums_ref,
    gy,
    gu,
):
    step = pl.program_id(0)
    tokens, width = gh2_ref.shape
    tiles = tokens // TILE
    groups, _, rows, _ = pair_ref.shape

    @pl.when(step == 0)
    def clear():
        sums_ref[...] = jnp.zeros_like(sums_ref)
        gy[...] = gh2_ref[...]

    @pl.when(step < 4)
    def ffn():
        up_block = matrix(up_w)
        down_block = matrix(down_w)

        def one(t, carry):
            at = pl.ds(pl.multiple_of(t * TILE, TILE), TILE)
            mixed = gh2_ref[at, :].astype(jnp.bfloat16)
            grad = wide_dot(mixed, down_block, NN) * gel_ref[0, at, :].astype(jnp.float32)
            low = grad.astype(jnp.bfloat16)
            gu[at, :] = low
            gy[at, :] += wide_dot(low, up_block, NT)
            sums_ref[pl.ds(step, 1), :] += jnp.sum(
                low.astype(jnp.float32), axis=0, keepdims=True
            )
            return carry

        lax.fori_loop(0, tiles, one, 0)
        grad_up = wide_dot(fit_ref[...], gu[...], NN).astype(jnp.bfloat16)
        pair_ref[:, 0:1] = grad_up.reshape(groups, 1, rows, width)
        grad_down = wide_dot(gmt_ref[...], hid_ref[0], NN).astype(jnp.bfloat16)
        pair_ref[:, 1:2] = grad_down.reshape(groups, 1, rows, width)

    @pl.when(step == 4)
    def first_norm():
        out_w = matrix(wo)

        def one(t, carry):
            at = pl.ds(pl.multiple_of(t * TILE, TILE), TILE)
            grad = gy[at, :]
            n1 = n1_ref[at, :]
            gh1 = norm_back(grad, n1, r1_ref[at, 0:1], small[3:4, :])
            gh1_ref[at, :] = gh1
            low = gh1.astype(jnp.bfloat16)
            gu[at, :] = low
            dctx_ref[at, :] = wide_dot(low, out_w, NT).astype(jnp.bfloat16)
            add_row(sums_ref, 4, low.astype(jnp.float32))
            add_row(sums_ref, 5, grad * n1)
            add_row(sums_ref, 6, grad)
            return carry

        lax.fori_loop(0, tiles, one, 0)
        grad_out = wide_dot(ctx_ref[...].T, gu[...], NN).astype(jnp.bfloat16)
        dwo_ref[...] = grad_out.reshape(dwo_ref.shape)


def back(info, gh2, hid, gel, fit, gmt, n1, r1, ctx, small, rest):
    tokens, width = gh2.shape
    groups, _, rows, _ = rest.shape

    def block(b, info):
        return (jnp.minimum(b, 3), 0, 0)

    return call(
        back_kernel,
        "back",
        info,
        5,
        [
            fixed((tokens, width)),
            pl.BlockSpec((1, tokens, width), block),
            pl.BlockSpec((1, tokens, width), block),
            fixed((width, tokens)),
            fixed((width, tokens)),
            fixed((tokens, width)),
            fixed((tokens, 128)),
            fixed((tokens, width)),
            fixed(small.shape),
            rest_spec(rest, lambda b: 4 + jnp.minimum(b, 3), False),
            rest_spec(rest, lambda b: 8 + jnp.minimum(b, 3), False),
            rest_spec(rest, lambda b: 3),
        ],
        [
            pl.BlockSpec((groups, 2, rows, width), lambda b, info: (0, jnp.minimum(b, 3), 0, 0)),
            resident((groups, rows, width)),
            resident((tokens, width)),
            resident((tokens, width)),
            resident((8, width)),
        ],
        [
            bf16_of(groups, 8, rows, width),
            bf16_of(groups, rows, width),
            f32_of(tokens, width),
            bf16_of(tokens, width),
            f32_of(8, width),
        ],
        [pltpu.VMEM((tokens, width), jnp.float32), pltpu.VMEM((tokens, width), jnp.bfloat16)],
        (gh2, hid, gel, fit, gmt, n1, r1, ctx, small, rest, rest, rest),
        22_000_000_000,
        40 << 20,
    )


def spill_kernel(info, dk_ref, dv_ref, wk, wv, out_ref):
    total = wide_dot(dk_ref[...], matrix(wk), NT) + wide_dot(dv_ref[...], matrix(wv), NT)
    out_ref[...] = total.astype(jnp.bfloat16)


def spill(info, dk, dv, first, rows):
    seq, width = dk.shape
    mid = seq // 4

    def other(b, info):
        return (2 * (1 - info[0]) + b, 0)

    return call(
        spill_kernel,
        "spill",
        info,
        2,
        [
            pl.BlockSpec((mid, width), other),
            pl.BlockSpec((mid, width), other),
            first_spec(first, rows, 1),
            first_spec(first, rows, 2),
        ],
        [pl.BlockSpec((mid, width), lambda b, info: (b, 0))],
        [bf16_of(2 * mid, width)],
        [],
        (dk, dv, first, first),
        2_400_000_000,
        8 << 20,
    )[0]


def weight_grads_kernel(
    info, x_ref, dq_ref, dk_ref, dv_ref, out_ref, sums_ref, q_acc, k_acc, v_acc
):
    step = pl.program_id(0)

    @pl.when(step == 0)
    def clear():
        sums_ref[...] = jnp.zeros_like(sums_ref)
        k_acc[...] = jnp.zeros_like(k_acc)
        v_acc[...] = jnp.zeros_like(v_acc)
        q_acc[...] = jnp.zeros_like(q_acc)

    flipped = x_ref[0].T
    k_acc[...] += wide_dot(flipped, dk_ref[...], NN)
    v_acc[...] += wide_dot(flipped, dv_ref[...], NN)
    add_row(sums_ref, 1, dv_ref[...].astype(jnp.float32))

    @pl.when(step < 2)
    def own():
        q_acc[...] += wide_dot(flipped, dq_ref[...], NN)
        add_row(sums_ref, 0, dq_ref[...].astype(jnp.float32))

    @pl.when(step == 3)
    def finish():
        groups, _, rows, width = out_ref.shape
        for m, acc in enumerate((q_acc, k_acc, v_acc)):
            out_ref[:, m : m + 1] = (
                acc[...].astype(jnp.bfloat16).reshape(groups, 1, rows, width)
            )


def weight_grads(info, x_all, dq, dk, dv, groups):
    _, mid, width = x_all.shape
    rows = width // groups

    def chunk(step, info):
        return lax.rem(step + 2 * info[0], 4)

    return call(
        weight_grads_kernel,
        "weight_grads",
        info,
        4,
        [
            pl.BlockSpec((1, mid, width), lambda g, info: (info[1 + chunk(g, info)], 0, 0)),
            pl.BlockSpec((mid, width), lambda g, info: (jnp.minimum(g, 1), 0)),
            pl.BlockSpec((mid, width), lambda g, info: (chunk(g, info), 0)),
            pl.BlockSpec((mid, width), lambda g, info: (chunk(g, info), 0)),
        ],
        [resident((groups, 3, rows, width)), resident((8, width))],
        [bf16_of(groups, 3, rows, width), f32_of(8, width)],
        [pltpu.VMEM((width, width), jnp.float32)] * 3,
        (x_all, dq, dk, dv),
        6_000_000_000,
        14 << 20,
    )


def input_grads_kernel(info, gh1_ref, dq_ref, dk_ref, dv_ref, more_ref, wq, wk, wv, out_ref):
    total = gh1_ref[...] + more_ref[...].astype(jnp.float32)
    total = total + wide_dot(dq_ref[...], matrix(wq), NT)
    total = total + wide_dot(dk_ref[...], matrix(wk), NT)
    total = total + wide_dot(dv_ref[...], matrix(wv), NT)
    out_ref[0] = total.astype(jnp.bfloat16)


def input_grads(info, gh1, dq, dk, dv, more, first, rows):
    tokens, width = gh1.shape
    steps = tokens // TILE
    mid = tokens // 2
    per = mid // TILE
    mine = pl.BlockSpec((TILE, width), lambda t, info: (t, 0))
    place = pl.BlockSpec((TILE, width), lambda t, info: (info[0] * steps + t, 0))

    return call(
        input_grads_kernel,
        "input_grads",
        info,
        steps,
        [
            mine,
            mine,
            place,
            place,
            mine,
            *[first_spec(first, rows, m) for m in range(3)],
        ],
        [
            pl.BlockSpec(
                (1, TILE, width),
                lambda t, info: (info[1 + 2 * info[0] + t // per], t % per, 0),
            )
        ],
        [bf16_of(2, mid, width)],
        [],
        (gh1, dq, dk, dv, more, first, first, first),
        3_700_000_000,
        14 << 20,
    )[0]


MESH = pl.DeviceIdType.MESH
KINDS = 3


def place_of():
    c, t = lax.axis_index("ctx"), lax.axis_index("tp")
    return lax.axis_index("shard"), c, t


def send(src, dst, sems, index, target):
    send_sems, recv_sems = sems
    return pltpu.make_async_remote_copy(
        src_ref=src,
        dst_ref=dst,
        send_sem=send_sems.at[index],
        recv_sem=recv_sems.at[index],
        device_id=target,
        device_id_type=MESH,
    )


def bring_kernel(
    n_shard,
    n_ctx,
    n_tp,
    slots,
    part_ref,
    low_ref,
    xs_ref,
    x_ref,
    first_ref,
    rest_ref,
    got,
    mine,
    total,
    pool,
    sel,
    x_s,
    x_r,
    xt_s,
    xt_r,
    za_s,
    za_r,
    zb_s,
    zb_r,
    zc_s,
    zc_r,
    q_s,
    q_r,
    qt_s,
    qt_r,
    r_s,
    r_r,
    rt_s,
    rt_r,
    own_sem,
):
    z, c, t = place_of()
    side, core, bit = t // 2, lax.rem(t, 2), lax.rem(c, 2)
    held = low_ref.shape[0]
    piece = mine.shape[0]
    chunks, per = 3, 3
    me = c * n_tp + t

    def far(dz):
        return (lax.rem(z + dz, n_shard), c, t)

    def across(mask):
        return (z, c ^ mask, t)

    def beside(dt):
        return (z, c, lax.rem(t + dt, n_tp))

    barrier = pltpu.get_barrier_semaphore()
    friends = [far(dz) for dz in range(1, n_shard)]
    friends += [(z, c ^ m, t) for m in range(1, n_ctx)]
    friends += [beside(dt) for dt in range(1, n_tp)]
    friends += [(z, c ^ m, t ^ 1) for m in range(1, n_ctx)]
    for friend in friends:
        pl.semaphore_signal(barrier, inc=1, device_id=friend, device_id_type=MESH)
    pl.semaphore_wait(barrier, len(friends))

    stays = c // 2 == core
    goes = [(z, 2 * core + (p ^ bit), 2 * side + c // 2) for p in range(2)]
    x_moves = [send(xs_ref.at[p], x_ref.at[p], (x_s, x_r), p, goes[p]) for p in range(2)]
    x_keep = pltpu.make_async_copy(xs_ref.at[0], x_ref.at[0], x_r.at[0])

    za = [
        send(
            part_ref.at[pl.ds(pl.multiple_of(far(dz)[0] * piece, piece), piece)],
            got.at[dz - 1],
            (za_s, za_r),
            dz - 1,
            far(dz),
        )
        for dz in range(1, n_shard)
    ]
    for copy in za:
        copy.start()

    @pl.when(stays)
    def keep():
        x_keep.start()

    @pl.when(jnp.logical_not(stays))
    def leave():
        x_moves[0].start()

    x_moves[1].start()
    summed = part_ref[pl.ds(pl.multiple_of(z * piece, piece), piece), :]
    for dz, copy in enumerate(za):
        copy.wait_recv()
        summed = summed + got[dz]
    mine[...] = summed
    here = pl.ds(pl.multiple_of(z * piece, piece), piece)
    zb = [
        send(mine, total.at[here], (zb_s, zb_r), dz - 1, far(dz)) for dz in range(1, n_shard)
    ]
    for copy in zb:
        copy.start()
    total[here, :] = summed
    pool_here = pl.ds(z * held, held)
    zc = [
        send(low_ref, pool.at[pool_here], (zc_s, zc_r), dz - 1, far(dz))
        for dz in range(1, n_shard)
    ]
    for copy in zc:
        copy.start()
    pool_own = pltpu.make_async_copy(low_ref, pool.at[pool_here], own_sem.at[0])
    pool_own.start()
    for copy in zb:
        copy.wait_recv()

    q_moves = [
        send(total, first_ref.at[me], (q_s, q_r), k, across(m)) for k, m in enumerate((1, 2, 3))
    ]
    for copy in q_moves:
        copy.start()
    first_own = pltpu.make_async_copy(total, first_ref.at[me], own_sem.at[1])
    first_own.start()
    qt_own = [
        send(total, first_ref.at[me], (qt_s, qt_r), dt - 1, beside(dt)) for dt in range(1, n_tp)
    ]
    for copy in qt_own:
        copy.start()

    x_over = [
        send(x_ref.at[p], x_ref.at[2 + p], (xt_s, xt_r), p, (z, c, t ^ 1)) for p in range(2)
    ]

    @pl.when(stays)
    def kept():
        x_keep.wait()

    @pl.when(jnp.logical_not(stays))
    def came():
        x_moves[0].wait_recv()

    x_over[0].start()
    x_moves[1].wait_recv()
    x_over[1].start()

    qt_on = []
    for k, m in enumerate((1, 2, 3)):
        q_moves[k].wait_recv()
        place = (c ^ m) * n_tp + t
        for dt in range(1, n_tp):
            copy = send(
                first_ref.at[place],
                first_ref.at[place],
                (qt_s, qt_r),
                (k + 1) * (n_tp - 1) + dt - 1,
                beside(dt),
            )
            copy.start()
            qt_on.append(copy)

    for copy in zc:
        copy.wait_recv()
    pool_own.wait()
    for m in range(chunks * per):
        sel[m] = pool[slots[KINDS + m]]
    rest_own = pltpu.make_async_copy(sel, rest_ref.at[me], own_sem.at[2])
    rest_own.start()
    r_moves = []
    rt_moves = []
    for k in range(chunks):
        span = pl.ds(k * per, per)
        pair = [
            send(
                sel.at[span],
                rest_ref.at[me, span],
                (r_s, r_r),
                k * 3 + j,
                across(m),
            )
            for j, m in enumerate((1, 2))
        ]
        for copy in pair:
            copy.start()
        r_moves.append(pair)
        for dt in range(1, n_tp):
            copy = send(
                sel.at[span],
                rest_ref.at[me, span],
                (rt_s, rt_r),
                (k * 4) * (n_tp - 1) + dt - 1,
                beside(dt),
            )
            copy.start()
            rt_moves.append(copy)

    def pass_on(k, which, place):
        span = pl.ds(k * per, per)
        for dt in range(1, n_tp):
            copy = send(
                rest_ref.at[place, span],
                rest_ref.at[place, span],
                (rt_s, rt_r),
                (k * 4 + which) * (n_tp - 1) + dt - 1,
                beside(dt),
            )
            copy.start()
            rt_moves.append(copy)

    onward = []
    for k in range(chunks):
        span = pl.ds(k * per, per)
        for j in range(2):
            r_moves[k][j].wait_recv()
        odd = lax.rem(core + k, 2)
        source = jnp.where(odd == 0, c ^ 1, c ^ 2) * n_tp + t
        target = (z, jnp.where(odd == 0, c ^ 2, c ^ 1), t)
        copy = send(
            rest_ref.at[source, span], rest_ref.at[source, span], (r_s, r_r), k * 3 + 2, target
        )
        copy.start()
        onward.append(copy)
        pass_on(k, 1, (c ^ 1) * n_tp + t)
        pass_on(k, 2, (c ^ 2) * n_tp + t)
    for k in range(chunks):
        onward[k].wait_recv()
        pass_on(k, 3, (c ^ 3) * n_tp + t)

    for copy in x_over:
        copy.wait()

    @pl.when(jnp.logical_not(stays))
    def left():
        x_moves[0].wait_send()

    x_moves[1].wait_send()
    for copy in (*za, *zb, *zc, *q_moves, *onward):
        copy.wait_send()
    for pair in r_moves:
        for copy in pair:
            copy.wait_send()
    for copy in (*qt_own, *qt_on, *rt_moves):
        copy.wait()
    first_own.wait()
    rest_own.wait()


def bring(slots, part, low, xs, n_shard, n_ctx, n_tp):
    held, rows, width = low.shape
    total_rows = part.shape[0]
    groups = n_ctx * n_tp
    mid = xs.shape[1]
    anywhere = pl.BlockSpec(memory_space=pl.ANY)
    dma = pltpu.SemaphoreType.DMA
    pairs = [2, 2, n_shard - 1, n_shard - 1, n_shard - 1, 3]
    pairs += [4 * (n_tp - 1), 9, 12 * (n_tp - 1)]
    sems = [dma((n,)) for n in pairs for _ in range(2)]
    return pl.pallas_call(
        functools.partial(bring_kernel, n_shard, n_ctx, n_tp),
        name="bring",
        in_specs=[
            pl.BlockSpec(memory_space=pltpu.SMEM),
            pl.BlockSpec(memory_space=pltpu.VMEM),
            anywhere,
            anywhere,
        ],
        out_specs=[anywhere, anywhere, anywhere],
        out_shape=[
            jax.ShapeDtypeStruct((4, mid, width), jnp.bfloat16),
            jax.ShapeDtypeStruct((groups, total_rows, width), jnp.bfloat16),
            jax.ShapeDtypeStruct((groups, 9, rows, width), jnp.bfloat16),
        ],
        scratch_shapes=[
            pltpu.VMEM((n_shard - 1, total_rows // n_shard, width), jnp.bfloat16),
            pltpu.VMEM((total_rows // n_shard, width), jnp.bfloat16),
            pltpu.VMEM((total_rows, width), jnp.bfloat16),
            pltpu.VMEM((n_shard * held, rows, width), jnp.bfloat16),
            pltpu.VMEM((9, rows, width), jnp.bfloat16),
            *sems,
            dma((3,)),
        ],
        compiler_params=pltpu.CompilerParams(
            collective_id=0, has_side_effects=True, vmem_limit_bytes=40 << 20
        ),
        cost_estimate=pl.CostEstimate(flops=0, bytes_accessed=40 << 20, transcendentals=0),
    )(slots, part, low, xs)


def adam_update(weight, first, second, grad, decay, rate):
    count = float(STEP)
    first_new = beta_one * first + (1.0 - beta_one) * grad
    second_new = beta_two * second + (1.0 - beta_two) * grad * grad
    first_hat = first_new / (1.0 - beta_one**count)
    second_hat = second_new / (1.0 - beta_two**count)
    weight_new = weight - rate * (first_hat / (jnp.sqrt(second_hat) + adam_eps) + decay * weight)
    return (weight_new, first_new, second_new)


def moves(n_ctx, n_tp, pick):
    pairs = []
    for c in range(n_ctx):
        for t in range(n_tp):
            side, core = t // 2, t % 2
            to_ctx = 2 * core + (pick ^ (c & 1))
            to_tp = 2 * side + c // 2
            pairs.append((c * n_tp + t, to_ctx * n_tp + to_tp))
    return pairs


def shards(
    inputs,
    cotangent,
    rand_blocks,
    slot_of,
    master,
    moment_one,
    moment_two,
    small_params,
    small_one,
    small_two,
):
    n_shard = lax.axis_size("shard")
    n_ctx = lax.axis_size("ctx")
    n_tp = lax.axis_size("tp")
    groups = n_ctx * n_tp
    held, rows, width = master.shape
    span = small_params.shape[0]
    my_ctx = lax.axis_index("ctx")
    my_tp = lax.axis_index("tp")
    parity = lax.rem(my_ctx, 2)
    half = lax.rem(my_tp, 2)
    plane = ("ctx", "tp")
    forth = [moves(n_ctx, n_tp, pick) for pick in range(2)]
    home = [[(b, a) for a, b in pairs] for pairs in forth]
    swap = [(t, t ^ 1) for t in range(n_tp)]

    arrival = [(b ^ parity) + 2 * (half ^ (j // 2)) for j, b in enumerate((0, 1, 0, 1))]
    info = jnp.stack([half, *arrival]).astype(jnp.int32)
    half_one = info[:1]

    def sent(field, pick):
        low = field.astype(jnp.bfloat16)
        return jnp.where(parity == 0, low[pick], low[1 - pick])

    def returned(field):
        first, second = [lax.ppermute(field[pick], plane, home[pick]) for pick in range(2)]
        swapped = parity == 1
        out = jnp.stack(
            [jnp.where(swapped, second, first), jnp.where(swapped, first, second)]
        )
        return out.astype(jnp.float32)

    low = master.astype(jnp.bfloat16)
    my_shard = lax.axis_index("shard")
    mine = my_shard * held + jnp.arange(held, dtype=jnp.int32)
    zero = jnp.zeros_like(low)
    parts = [
        jnp.sum(jnp.where((slot_of[m] == mine)[:, None, None], low, zero), axis=0, dtype=jnp.float32)
        for m in range(3)
    ]
    spread = (jnp.arange(n_shard) == my_shard)[:, None]
    small_part = jnp.where(spread, small_params[None, :], 0.0).reshape(-1)
    used = 3 * rows * width + n_shard * span
    total_rows = -(-used // (width * 16 * n_shard)) * 16 * n_shard
    small_part = jnp.pad(small_part, (0, total_rows * width - used)).reshape(-1, width)
    part = jnp.concatenate([*parts, small_part]).astype(jnp.bfloat16)
    xs = jnp.stack([sent(inputs, pick) for pick in range(2)])
    x_all, first, rest = bring(slot_of, part, low, xs, n_shard, n_ctx, n_tp)
    small = first[:, 3 * rows :, :].reshape(groups, -1)[:, : n_shard * span]
    small = small.reshape(groups, n_shard, span).transpose(1, 0, 2)
    small = small.reshape(-1, width).astype(jnp.float32)

    cots, x_all = lax.optimization_barrier(
        ([sent(cotangent, pick) for pick in range(2)], x_all)
    )
    cot = jnp.stack([lax.ppermute(cots[pick], plane, forth[pick]) for pick in range(2)])

    q, k, v = project(info, x_all, small, first, rows)
    context, lse = attend(half_one, rand_blocks, q, k, v, 5)
    out_low, n1, r1, fi, fit, hid, gel, gh2, gmt, sums_two = front(
        info, context, x_all, cot, small, rest
    )
    layer_out = returned(out_low)
    ffn_grads, out_grad, gh1, dctx, sums_one = back(
        info, gh2, hid, gel, fit, gmt, n1, r1, context, small, rest
    )
    ffn_rows = lax.psum_scatter(ffn_grads, plane, scatter_dimension=0, tiled=False)
    dq, dk, dv = attend_back(half_one, rand_blocks, q, k, v, lse, dctx, 5)
    more = lax.ppermute(spill(info, dk, dv, first, rows), "tp", swap)
    qkv_grads, sums_qkv = weight_grads(info, x_all, dq, dk, dv, groups)
    small_grad = jnp.concatenate(
        [
            sums_qkv[0],
            sums_qkv[1],
            sums_one[4],
            sums_one[5],
            sums_one[6],
            sums_one[0:4].reshape(-1),
            sums_two[0],
            sums_two[1],
            sums_two[2],
        ]
    )
    extra = -(-n_shard * span // width)
    small_rows = small_grad.reshape(n_shard, groups, span).transpose(1, 0, 2)
    small_rows = jnp.pad(
        small_rows.reshape(groups, n_shard * span), ((0, 0), (0, extra * width - n_shard * span))
    ).reshape(groups, extra, width)
    late = jnp.concatenate(
        [
            qkv_grads.reshape(groups, 3 * rows, width),
            out_grad,
            small_rows.astype(jnp.bfloat16),
        ],
        axis=1,
    )
    late, ffn_rows = lax.optimization_barrier((late, ffn_rows))
    late_rows = lax.psum_scatter(late, plane, scatter_dimension=0, tiled=False)
    input_low = input_grads(info, gh1, dq, dk, dv, more, first, rows)
    input_grad = returned(input_low)

    own_rows = jnp.concatenate(
        [
            late_rows[: 4 * rows].reshape(4, rows, width),
            ffn_rows[0::2],
            ffn_rows[1::2],
        ]
    )
    picker = slot_of[None, :] == jnp.arange(n_shard * held, dtype=jnp.int32)[:, None]
    packed = jnp.einsum(
        "sm,mrd->srd", picker.astype(jnp.bfloat16), own_rows, preferred_element_type=jnp.float32
    ).astype(jnp.bfloat16)
    small_sum = late_rows[4 * rows :].reshape(-1)[: n_shard * span].reshape(n_shard, span)
    small_sum = jnp.pad(small_sum, ((0, 0), (0, width - span)))[:, None, :]
    final = jnp.concatenate([packed.reshape(n_shard, held * rows, width), small_sum], axis=1)
    final = lax.psum_scatter(final, "shard", scatter_dimension=0, tiled=False).astype(jnp.float32)
    slot_grads = final[: held * rows].reshape(held, rows, width)
    small_owned = final[held * rows, :span]
    master_new, first_new, second_new = adam_update(
        master, moment_one, moment_two, slot_grads, 0.01, rate_value
    )
    small_new, small_first, small_second = adam_update(
        small_params, small_one, small_two, small_owned, 0.0, small_rate
    )
    return (
        layer_out,
        input_grad,
        master_new,
        first_new,
        second_new,
        small_new,
        small_first,
        small_second,
    )


def solution(mesh):
    tokens = P(("shard", "tp"), "ctx", None)
    stored = P("shard", ("ctx", "tp"), None)
    spread = P(("shard", "ctx", "tp"))
    return jax.shard_map(
        shards,
        mesh=mesh,
        in_specs=(tokens, tokens, P(), P(), stored, stored, stored, spread, spread, spread),
        out_specs=(tokens, tokens, stored, stored, stored, spread, spread, spread),
        check_vma=False,
    )
```

```python
import functools

import jax
import jax.numpy as jnp
from jax import lax
from jax.experimental import pallas as pl
from jax.experimental.pallas import tpu as pltpu
from jax.sharding import PartitionSpec as P

STEP = 5
norm_eps = 1e-12
beta_one = 0.9
beta_two = 0.999
adam_eps = 1e-08
rate_value = 0.04
small_rate = 0.25
score_scale = 0.125
gelu_root = 0.7978845608
gelu_cube = 0.044715

BLOCK = 64
HEAD = 64
PACK = 4
masked_score = -1e30


def wide_dot(a, b, dims):
    return lax.dot_general(a, b, (dims, ((), ())), preferred_element_type=jnp.float32)


def head_masks(rows):
    lane = lax.broadcasted_iota(jnp.int32, (rows, PACK * HEAD), 1) // HEAD
    return [lane == h for h in range(PACK)]


def spread_heads(block, masks):
    zero = jnp.zeros_like(block)
    return jnp.concatenate([jnp.where(m, block, zero) for m in masks], axis=0)


def own_heads(full, masks):
    total = None
    for h, m in enumerate(masks):
        piece = jnp.where(m, full[h * BLOCK : (h + 1) * BLOCK], 0.0)
        total = piece if total is None else total + piece
    return total


def rows_of(ref, index, count=1):
    return ref[pl.ds(pl.multiple_of(index * BLOCK, BLOCK), count * BLOCK), :]


def picked_rows(ref, picks, low_half):
    halves = []
    for pair in range(PACK // 2):
        cols = pl.ds(pair * 2 * HEAD, 2 * HEAD)
        first = ref[pl.ds(pl.multiple_of(picks[2 * pair] * BLOCK, BLOCK), BLOCK), cols]
        second = ref[pl.ds(pl.multiple_of(picks[2 * pair + 1] * BLOCK, BLOCK), BLOCK), cols]
        halves.append(jnp.where(low_half, first, second))
    return jnp.concatenate(halves, axis=1)


def gathered(ref, block, last, picks, low_half):
    pieces = [rows_of(ref, 0), rows_of(ref, last), rows_of(ref, block - 1, 3)]
    pieces += [picked_rows(ref, p, low_half) for p in picks]
    return jnp.concatenate(pieces, axis=0)


def middle_scores(keys, spread, block, last):
    scores = wide_dot(keys, spread, ((1,), (1,)))
    first_off = jnp.where(block == 1, masked_score, 0.0)
    last_off = jnp.where(block == last - 1, masked_score, 0.0)
    b = BLOCK
    return jnp.concatenate(
        [
            scores[: 2 * b],
            scores[2 * b : 3 * b] + first_off,
            scores[3 * b : 4 * b],
            scores[4 * b : 5 * b] + last_off,
            scores[5 * b :],
        ],
        axis=0,
    )


def attend_kernel(unroll, half_ref, table_ref, q_ref, k_ref, v_ref, out_ref, lse_ref, kept):
    half = half_ref[0]
    group = pl.program_id(0)
    nblocks = k_ref.shape[0] // BLOCK
    local = q_ref.shape[0] // BLOCK
    last = nblocks - 1
    picks_each = table_ref.shape[2]
    masks = head_masks(BLOCK)
    low_half = lax.broadcasted_iota(jnp.int32, (BLOCK, 2 * HEAD), 1) < HEAD

    def middle(step, carry):
        mine = step + 1 - half
        block = mine + local * half
        picks = [
            [table_ref[group * PACK + h, block - 1, r] for h in range(PACK)]
            for r in range(picks_each)
        ]
        spread = spread_heads(rows_of(q_ref, mine), masks)
        keys = gathered(k_ref, block, last, picks, low_half)
        values = gathered(v_ref, block, last, picks, low_half)
        scores = middle_scores(keys, spread, block, last)
        top = jnp.max(scores, axis=0, keepdims=True)
        probs = jnp.exp(scores - top)
        total = jnp.sum(probs, axis=0, keepdims=True)
        low = (probs * (1.0 / total)).astype(jnp.bfloat16)
        full = wide_dot(low, values, ((0,), (0,)))
        out_ref[pl.ds(pl.multiple_of(mine * BLOCK, BLOCK), BLOCK), :] = own_heads(
            full, masks
        ).astype(jnp.bfloat16)
        lse_ref[0, pl.ds(mine, 1), :] = top + jnp.log(total)
        return carry

    lax.fori_loop(0, local - 1, middle, 0, unroll=unroll)

    edge = (local - 1) * half
    spread = spread_heads(rows_of(q_ref, edge), masks)
    span = 8 * BLOCK
    chunks = nblocks // 8
    top = None
    for c in range(chunks):
        scores = wide_dot(k_ref[c * span : (c + 1) * span, :], spread, ((1,), (1,)))
        kept[c * span : (c + 1) * span, :] = scores
        high = jnp.max(scores, axis=0, keepdims=True)
        top = high if top is None else jnp.maximum(top, high)
    total = None
    for c in range(chunks):
        probs = jnp.exp(kept[c * span : (c + 1) * span, :] - top)
        kept[c * span : (c + 1) * span, :] = probs
        part = jnp.sum(probs, axis=0, keepdims=True)
        total = part if total is None else total + part
    scale = 1.0 / total
    full = None
    for c in range(chunks):
        low = (kept[c * span : (c + 1) * span, :] * scale).astype(jnp.bfloat16)
        part = wide_dot(low, v_ref[c * span : (c + 1) * span, :], ((0,), (0,)))
        full = part if full is None else full + part
    out_ref[pl.ds(pl.multiple_of(edge * BLOCK, BLOCK), BLOCK), :] = own_heads(
        full, masks
    ).astype(jnp.bfloat16)
    lse_ref[0, pl.ds(edge, 1), :] = top + jnp.log(total)


def attend(half, table, q, k, v, unroll=3):
    tokens, width = q.shape
    seq = k.shape[0]
    lanes = PACK * HEAD
    groups = width // lanes
    blocks = tokens // BLOCK
    spec = pltpu.PrefetchScalarGridSpec(
        num_scalar_prefetch=2,
        grid=(groups,),
        in_specs=[
            pl.BlockSpec((tokens, lanes), lambda g, *_: (0, g)),
            pl.BlockSpec((seq, lanes), lambda g, *_: (0, g)),
            pl.BlockSpec((seq, lanes), lambda g, *_: (0, g)),
        ],
        out_specs=[
            pl.BlockSpec((tokens, lanes), lambda g, *_: (0, g)),
            pl.BlockSpec((1, blocks, lanes), lambda g, *_: (g, 0, 0)),
        ],
        scratch_shapes=[pltpu.VMEM((seq, lanes), jnp.float32)],
    )
    return pl.pallas_call(
        functools.partial(attend_kernel, unroll),
        grid_spec=spec,
        out_shape=[
            jax.ShapeDtypeStruct((tokens, width), jnp.bfloat16),
            jax.ShapeDtypeStruct((groups, blocks, lanes), jnp.float32),
        ],
        name="attend",
        compiler_params=pltpu.CompilerParams(vmem_limit_bytes=56 << 20),
        cost_estimate=pl.CostEstimate(
            flops=60_000_000_000, bytes_accessed=12 << 20, transcendentals=16_000_000
        ),
    )(half, table, q, k, v)


def attend_back_kernel(
    unroll,
    half_ref,
    table_ref,
    q_ref,
    k_ref,
    v_ref,
    lse_ref,
    do_ref,
    dq_ref,
    dk_ref,
    dv_ref,
    dk_acc,
    dv_acc,
    kept_p,
    kept_g,
):
    half = half_ref[0]
    group = pl.program_id(0)
    nblocks = k_ref.shape[0] // BLOCK
    local = q_ref.shape[0] // BLOCK
    last = nblocks - 1
    picks_each = table_ref.shape[2]
    masks = head_masks(BLOCK)
    low_half = lax.broadcasted_iota(jnp.int32, (BLOCK, 2 * HEAD), 1) < HEAD
    span = 8 * BLOCK
    chunks = nblocks // 8

    edge = (local - 1) * half
    spread = spread_heads(rows_of(q_ref, edge), masks)
    spread_do = spread_heads(rows_of(do_ref, edge), masks)
    lse = lse_ref[0, pl.ds(edge, 1), :]
    delta = None
    for c in range(chunks):
        rows = slice(c * span, (c + 1) * span)
        probs = jnp.exp(wide_dot(k_ref[rows, :], spread, ((1,), (1,))) - lse)
        gp = wide_dot(v_ref[rows, :], spread_do, ((1,), (1,)))
        kept_p[rows, :] = probs
        kept_g[rows, :] = gp
        part = jnp.sum(probs * gp, axis=0, keepdims=True)
        delta = part if delta is None else delta + part
    full = None
    for c in range(chunks):
        rows = slice(c * span, (c + 1) * span)
        probs = kept_p[rows, :]
        ds = (probs * (kept_g[rows, :] - delta)).astype(jnp.bfloat16)
        dv_acc[rows, :] = wide_dot(probs.astype(jnp.bfloat16), spread_do, ((1,), (0,)))
        dk_acc[rows, :] = wide_dot(ds, spread, ((1,), (0,)))
        part = wide_dot(ds, k_ref[rows, :], ((0,), (0,)))
        full = part if full is None else full + part
    dq_ref[pl.ds(pl.multiple_of(edge * BLOCK, BLOCK), BLOCK), :] = (
        own_heads(full, masks) * 0.125
    ).astype(jnp.bfloat16)

    def scatter(acc, piece, block, picks):
        b = BLOCK
        acc[0:b, :] += piece[:b]
        acc[last * b : (last + 1) * b, :] += piece[b : 2 * b]
        window = pl.ds(pl.multiple_of((block - 1) * b, b), 3 * b)
        acc[window, :] += piece[2 * b : 5 * b]
        for r, p in enumerate(picks):
            part = piece[(5 + r) * b : (6 + r) * b]
            for pair in range(PACK // 2):
                lanes = slice(pair * 2 * HEAD, (pair + 1) * 2 * HEAD)
                cols = pl.ds(pair * 2 * HEAD, 2 * HEAD)
                sub = part[:, lanes]
                acc[pl.ds(pl.multiple_of(p[2 * pair] * b, b), b), cols] += jnp.where(
                    low_half, sub, 0.0
                )
                acc[pl.ds(pl.multiple_of(p[2 * pair + 1] * b, b), b), cols] += jnp.where(
                    low_half, 0.0, sub
                )

    def middle(step, carry):
        mine = step + 1 - half
        block = mine + local * half
        picks = [
            [table_ref[group * PACK + h, block - 1, r] for h in range(PACK)]
            for r in range(picks_each)
        ]
        spread = spread_heads(rows_of(q_ref, mine), masks)
        spread_do = spread_heads(rows_of(do_ref, mine), masks)
        keys = gathered(k_ref, block, last, picks, low_half)
        values = gathered(v_ref, block, last, picks, low_half)
        scores = middle_scores(keys, spread, block, last)
        probs = jnp.exp(scores - lse_ref[0, pl.ds(mine, 1), :])
        gp = wide_dot(values, spread_do, ((1,), (1,)))
        delta = jnp.sum(probs * gp, axis=0, keepdims=True)
        ds = (probs * (gp - delta)).astype(jnp.bfloat16)
        low = probs.astype(jnp.bfloat16)
        scatter(dv_acc, wide_dot(low, spread_do, ((1,), (0,))), block, picks)
        scatter(dk_acc, wide_dot(ds, spread, ((1,), (0,))), block, picks)
        full = wide_dot(ds, keys, ((0,), (0,)))
        dq_ref[pl.ds(pl.multiple_of(mine * BLOCK, BLOCK), BLOCK), :] = (
            own_heads(full, masks) * 0.125
        ).astype(jnp.bfloat16)
        return carry

    lax.fori_loop(0, local - 1, middle, 0, unroll=unroll)
    dk_ref[...] = dk_acc[...].astype(jnp.bfloat16)
    dv_ref[...] = dv_acc[...].astype(jnp.bfloat16)


def attend_back(half, table, q, k, v, lse, do, unroll=3):
    tokens, width = q.shape
    seq = k.shape[0]
    lanes = PACK * HEAD
    groups = width // lanes
    blocks = tokens // BLOCK
    mine = pl.BlockSpec((tokens, lanes), lambda g, *_: (0, g))
    whole = pl.BlockSpec((seq, lanes), lambda g, *_: (0, g))
    spec = pltpu.PrefetchScalarGridSpec(
        num_scalar_prefetch=2,
        grid=(groups,),
        in_specs=[
            mine,
            whole,
            whole,
            pl.BlockSpec((1, blocks, lanes), lambda g, *_: (g, 0, 0)),
            mine,
        ],
        out_specs=[mine, whole, whole],
        scratch_shapes=[pltpu.VMEM((seq, lanes), jnp.float32)] * 4,
    )
    return pl.pallas_call(
        functools.partial(attend_back_kernel, unroll),
        grid_spec=spec,
        out_shape=[
            jax.ShapeDtypeStruct((tokens, width), jnp.bfloat16),
            jax.ShapeDtypeStruct((seq, width), jnp.bfloat16),
            jax.ShapeDtypeStruct((seq, width), jnp.bfloat16),
        ],
        name="attend_back",
        compiler_params=pltpu.CompilerParams(vmem_limit_bytes=56 << 20),
        cost_estimate=pl.CostEstimate(
            flops=120_000_000_000, bytes_accessed=24 << 20, transcendentals=16_000_000
        ),
    )(half, table, q, k, v, lse, do)


TILE = 256
MID = 512


def cols_mean(value):
    return jnp.mean(value, axis=-1, keepdims=True)


def normed(field):
    centred = field - cols_mean(field)
    rate = lax.rsqrt(cols_mean(centred * centred) + norm_eps)
    return centred * rate, rate


def norm_back(cot, normal, rate, gain):
    dn = cot * gain
    return rate * (dn - cols_mean(dn) - normal * cols_mean(dn * normal))


def matrix(ref):
    value = ref[...]
    return value.reshape(-1, value.shape[-1])


def add_row(ref, row, value):
    ref[row : row + 1, :] += jnp.sum(value, axis=0, keepdims=True)


def first_spec(first, rows, which):
    groups, _, width = first.shape
    return pl.BlockSpec(
        (groups, rows, width), lambda step, info: (0, which, 0), pipeline_mode=pl.Buffered(1)
    )


def rest_spec(rest, which, single=True):
    groups, _, rows, width = rest.shape
    mode = pl.Buffered(1) if single else None
    return pl.BlockSpec(
        (groups, 1, rows, width), lambda step, info: (0, which(step) - 3, 0, 0), pipeline_mode=mode
    )


def fixed(shape):
    return pl.BlockSpec(shape, lambda step, info: (0,) * len(shape), pipeline_mode=pl.Buffered(1))


def resident(shape):
    return pl.BlockSpec(shape, lambda step, info: (0,) * len(shape))


def call(kernel, name, info, grid, in_specs, out_specs, out_shape, scratch, args, flops, moved):
    return pl.pallas_call(
        kernel,
        name=name,
        grid_spec=pltpu.PrefetchScalarGridSpec(
            num_scalar_prefetch=1,
            grid=(grid,),
            in_specs=in_specs,
            out_specs=out_specs,
            scratch_shapes=scratch,
        ),
        out_shape=out_shape,
        compiler_params=pltpu.CompilerParams(vmem_limit_bytes=60 << 20),
        cost_estimate=pl.CostEstimate(
            flops=flops, bytes_accessed=moved, transcendentals=0
        ),
    )(info, *args)


def bf16_of(*shape):
    return jax.ShapeDtypeStruct(shape, jnp.bfloat16)


def f32_of(*shape):
    return jax.ShapeDtypeStruct(shape, jnp.float32)


NN = ((1,), (0,))
NT = ((1,), (1,))
TN = ((0,), (0,))


def project_kernel(info, x_ref, small, wq, wk, wv, q_ref, k_ref, v_ref):
    x = x_ref[0]

    @pl.when(pl.program_id(0) < 2)
    def own():
        q = wide_dot(x, matrix(wq), NN) + small[0:1, :]
        q_ref[...] = q.astype(jnp.bfloat16) * jnp.bfloat16(score_scale)

    k_ref[...] = wide_dot(x, matrix(wk), NN).astype(jnp.bfloat16)
    v_ref[...] = (wide_dot(x, matrix(wv), NN) + small[1:2, :]).astype(jnp.bfloat16)


def project(info, x_all, small, first, rows):
    _, mid, width = x_all.shape

    def chunk(step, info):
        return lax.rem(step + 2 * info[0], 4)

    return call(
        project_kernel,
        "project",
        info,
        4,
        [
            pl.BlockSpec((1, mid, width), lambda g, info: (info[1 + chunk(g, info)], 0, 0)),
            fixed(small.shape),
            *[first_spec(first, rows, m) for m in range(3)],
        ],
        [
            pl.BlockSpec((mid, width), lambda g, info: (jnp.minimum(g, 1), 0)),
            pl.BlockSpec((mid, width), lambda g, info: (chunk(g, info), 0)),
            pl.BlockSpec((mid, width), lambda g, info: (chunk(g, info), 0)),
        ],
        [bf16_of(2 * mid, width), bf16_of(4 * mid, width), bf16_of(4 * mid, width)],
        [],
        (x_all, small, first, first, first),
        6_000_000_000,
        16 << 20,
    )


def front_kernel(
    info,
    ctx_ref,
    x_ref,
    cot_ref,
    small,
    wo,
    u0,
    u1,
    u2,
    u3,
    v0,
    v1,
    v2,
    v3,
    out_ref,
    n1_ref,
    r1_ref,
    fi_ref,
    fit_ref,
    hid_ref,
    gel_ref,
    gh2_ref,
    gmt_ref,
    sums_ref,
):
    attn_out = wide_dot(ctx_ref[...], matrix(wo), NN) + small[2:3, :]
    n1, r1 = normed(x_ref[0].astype(jnp.float32) + attn_out)
    n1_ref[...] = n1
    r1_ref[...] = jnp.broadcast_to(r1, r1_ref.shape)
    after = n1 * small[3:4, :] + small[4:5, :]
    ffn_in = after.astype(jnp.bfloat16)
    fi_ref[...] = ffn_in
    fit_ref[...] = ffn_in.T
    total = after + small[9:10, :]
    for b, (up_w, down_w) in enumerate(((u0, v0), (u1, v1), (u2, v2), (u3, v3))):
        up = wide_dot(ffn_in, matrix(up_w), NN) + small[5 + b : 6 + b, :]
        square = up * up
        bent = jnp.tanh(gelu_root * up * (1.0 + gelu_cube * square))
        rise = 0.5 * (1.0 + bent)
        hidden = (up * rise).astype(jnp.bfloat16)
        hid_ref[b] = hidden
        slope = rise + (0.5 * gelu_root) * up * (1.0 - bent * bent) * (
            1.0 + (3.0 * gelu_cube) * square
        )
        gel_ref[b] = slope.astype(jnp.bfloat16)
        total = total + wide_dot(hidden, matrix(down_w), NT)
    n2, r2 = normed(total)
    out_ref[0] = (n2 * small[10:11, :] + small[11:12, :]).astype(jnp.bfloat16)
    cot = cot_ref[0].astype(jnp.float32)
    gh2 = norm_back(cot, n2, r2, small[10:11, :])
    gh2_ref[...] = gh2
    mixed = gh2.astype(jnp.bfloat16)
    gmt_ref[...] = mixed.T

    @pl.when(pl.program_id(0) == 0)
    def clear():
        sums_ref[...] = jnp.zeros_like(sums_ref)

    add_row(sums_ref, 0, mixed.astype(jnp.float32))
    add_row(sums_ref, 1, cot * n2)
    add_row(sums_ref, 2, cot)


def front(info, ctx, x_all, cot, small, rest):
    tokens, width = ctx.shape
    mid = x_all.shape[1]
    per = mid // TILE
    steps = tokens // TILE

    def arrived(t, info):
        return (info[1 + 2 * info[0] + t // per], t % per, 0)

    def rows(dtype_shape):
        return pl.BlockSpec(dtype_shape, lambda t, info: (t, 0))

    specs = [rest_spec(rest, lambda t, m=m: m) for m in range(3, 12)]
    wide4 = pl.BlockSpec((4, TILE, width), lambda t, info: (0, t, 0))
    flipped = pl.BlockSpec((width, TILE), lambda t, info: (0, t))
    return call(
        front_kernel,
        "front",
        info,
        steps,
        [
            rows((TILE, width)),
            pl.BlockSpec((1, TILE, width), arrived),
            pl.BlockSpec((1, TILE, width), arrived),
            fixed(small.shape),
            *specs,
        ],
        [
            pl.BlockSpec((1, TILE, width), arrived),
            rows((TILE, width)),
            rows((TILE, 128)),
            rows((TILE, width)),
            flipped,
            wide4,
            wide4,
            rows((TILE, width)),
            flipped,
            resident((8, width)),
        ],
        [
            bf16_of(2, mid, width),
            f32_of(tokens, width),
            f32_of(tokens, 128),
            bf16_of(tokens, width),
            bf16_of(width, tokens),
            bf16_of(4, tokens, width),
            bf16_of(4, tokens, width),
            f32_of(tokens, width),
            bf16_of(width, tokens),
            f32_of(8, width),
        ],
        [],
        (ctx, x_all, cot, small, *([rest] * 9)),
        11_000_000_000,
        40 << 20,
    )


def back_kernel(
    info,
    gh2_ref,
    hid_ref,
    gel_ref,
    fit_ref,
    gmt_ref,
    n1_ref,
    r1_ref,
    ctx_ref,
    small,
    up_w,
    down_w,
    wo,
    pair_ref,
    dwo_ref,
    gh1_ref,
    dctx_ref,
    sums_ref,
    gy,
    gu,
):
    step = pl.program_id(0)
    tokens, width = gh2_ref.shape
    tiles = tokens // TILE
    groups, _, rows, _ = pair_ref.shape

    @pl.when(step == 0)
    def clear():
        sums_ref[...] = jnp.zeros_like(sums_ref)
        gy[...] = gh2_ref[...]

    @pl.when(step < 4)
    def ffn():
        up_block = matrix(up_w)
        down_block = matrix(down_w)

        def one(t, carry):
            at = pl.ds(pl.multiple_of(t * TILE, TILE), TILE)
            mixed = gh2_ref[at, :].astype(jnp.bfloat16)
            grad = wide_dot(mixed, down_block, NN) * gel_ref[0, at, :].astype(jnp.float32)
            low = grad.astype(jnp.bfloat16)
            gu[at, :] = low
            gy[at, :] += wide_dot(low, up_block, NT)
            sums_ref[pl.ds(step, 1), :] += jnp.sum(
                low.astype(jnp.float32), axis=0, keepdims=True
            )
            return carry

        lax.fori_loop(0, tiles, one, 0)
        grad_up = wide_dot(fit_ref[...], gu[...], NN).astype(jnp.bfloat16)
        pair_ref[:, 0:1] = grad_up.reshape(groups, 1, rows, width)
        grad_down = wide_dot(gmt_ref[...], hid_ref[0], NN).astype(jnp.bfloat16)
        pair_ref[:, 1:2] = grad_down.reshape(groups, 1, rows, width)

    @pl.when(step == 4)
    def first_norm():
        out_w = matrix(wo)

        def one(t, carry):
            at = pl.ds(pl.multiple_of(t * TILE, TILE), TILE)
            grad = gy[at, :]
            n1 = n1_ref[at, :]
            gh1 = norm_back(grad, n1, r1_ref[at, 0:1], small[3:4, :])
            gh1_ref[at, :] = gh1
            low = gh1.astype(jnp.bfloat16)
            gu[at, :] = low
            dctx_ref[at, :] = wide_dot(low, out_w, NT).astype(jnp.bfloat16)
            add_row(sums_ref, 4, low.astype(jnp.float32))
            add_row(sums_ref, 5, grad * n1)
            add_row(sums_ref, 6, grad)
            return carry

        lax.fori_loop(0, tiles, one, 0)
        grad_out = wide_dot(ctx_ref[...].T, gu[...], NN).astype(jnp.bfloat16)
        dwo_ref[...] = grad_out.reshape(dwo_ref.shape)


def back(info, gh2, hid, gel, fit, gmt, n1, r1, ctx, small, rest):
    tokens, width = gh2.shape
    groups, _, rows, _ = rest.shape

    def block(b, info):
        return (jnp.minimum(b, 3), 0, 0)

    return call(
        back_kernel,
        "back",
        info,
        5,
        [
            fixed((tokens, width)),
            pl.BlockSpec((1, tokens, width), block),
            pl.BlockSpec((1, tokens, width), block),
            fixed((width, tokens)),
            fixed((width, tokens)),
            fixed((tokens, width)),
            fixed((tokens, 128)),
            fixed((tokens, width)),
            fixed(small.shape),
            rest_spec(rest, lambda b: 4 + jnp.minimum(b, 3), False),
            rest_spec(rest, lambda b: 8 + jnp.minimum(b, 3), False),
            rest_spec(rest, lambda b: 3),
        ],
        [
            pl.BlockSpec((groups, 2, rows, width), lambda b, info: (0, jnp.minimum(b, 3), 0, 0)),
            resident((groups, rows, width)),
            resident((tokens, width)),
            resident((tokens, width)),
            resident((8, width)),
        ],
        [
            bf16_of(groups, 8, rows, width),
            bf16_of(groups, rows, width),
            f32_of(tokens, width),
            bf16_of(tokens, width),
            f32_of(8, width),
        ],
        [pltpu.VMEM((tokens, width), jnp.float32), pltpu.VMEM((tokens, width), jnp.bfloat16)],
        (gh2, hid, gel, fit, gmt, n1, r1, ctx, small, rest, rest, rest),
        22_000_000_000,
        40 << 20,
    )


MESH = pl.DeviceIdType.MESH
KINDS = 3


def place_of():
    c, t = lax.axis_index("ctx"), lax.axis_index("tp")
    return lax.axis_index("shard"), c, t


def send(src, dst, sems, index, target):
    send_sems, recv_sems = sems
    return pltpu.make_async_remote_copy(
        src_ref=src,
        dst_ref=dst,
        send_sem=send_sems.at[index],
        recv_sem=recv_sems.at[index],
        device_id=target,
        device_id_type=MESH,
    )


def bring_kernel(
    n_shard,
    n_ctx,
    n_tp,
    slots,
    part_ref,
    low_ref,
    xs_ref,
    x_ref,
    first_ref,
    rest_ref,
    got,
    mine,
    total,
    pool,
    sel,
    x_s,
    x_r,
    xt_s,
    xt_r,
    za_s,
    za_r,
    zb_s,
    zb_r,
    zc_s,
    zc_r,
    q_s,
    q_r,
    qt_s,
    qt_r,
    r_s,
    r_r,
    rt_s,
    rt_r,
    own_sem,
):
    z, c, t = place_of()
    side, core, bit = t // 2, lax.rem(t, 2), lax.rem(c, 2)
    held = low_ref.shape[0]
    piece = mine.shape[0]
    chunks, per = 3, 3
    me = c * n_tp + t

    def far(dz):
        return (lax.rem(z + dz, n_shard), c, t)

    def across(mask):
        return (z, c ^ mask, t)

    def beside(dt):
        return (z, c, lax.rem(t + dt, n_tp))

    barrier = pltpu.get_barrier_semaphore()
    friends = [far(dz) for dz in range(1, n_shard)]
    friends += [(z, c ^ m, t) for m in range(1, n_ctx)]
    friends += [beside(dt) for dt in range(1, n_tp)]
    friends += [(z, c ^ m, t ^ 1) for m in range(1, n_ctx)]
    for friend in friends:
        pl.semaphore_signal(barrier, inc=1, device_id=friend, device_id_type=MESH)
    pl.semaphore_wait(barrier, len(friends))

    stays = c // 2 == core
    goes = [(z, 2 * core + (p ^ bit), 2 * side + c // 2) for p in range(2)]
    x_moves = [send(xs_ref.at[p], x_ref.at[p], (x_s, x_r), p, goes[p]) for p in range(2)]
    x_keep = pltpu.make_async_copy(xs_ref.at[0], x_ref.at[0], x_r.at[0])

    za = [
        send(
            part_ref.at[pl.ds(pl.multiple_of(far(dz)[0] * piece, piece), piece)],
            got.at[dz - 1],
            (za_s, za_r),
            dz - 1,
            far(dz),
        )
        for dz in range(1, n_shard)
    ]
    for copy in za:
        copy.start()

    @pl.when(stays)
    def keep():
        x_keep.start()

    @pl.when(jnp.logical_not(stays))
    def leave():
        x_moves[0].start()

    x_moves[1].start()
    summed = part_ref[pl.ds(pl.multiple_of(z * piece, piece), piece), :]
    for dz, copy in enumerate(za):
        copy.wait_recv()
        summed = summed + got[dz]
    mine[...] = summed
    here = pl.ds(pl.multiple_of(z * piece, piece), piece)
    zb = [
        send(mine, total.at[here], (zb_s, zb_r), dz - 1, far(dz)) for dz in range(1, n_shard)
    ]
    for copy in zb:
        copy.start()
    total[here, :] = summed
    pool_here = pl.ds(z * held, held)
    zc = [
        send(low_ref, pool.at[pool_here], (zc_s, zc_r), dz - 1, far(dz))
        for dz in range(1, n_shard)
    ]
    for copy in zc:
        copy.start()
    pool_own = pltpu.make_async_copy(low_ref, pool.at[pool_here], own_sem.at[0])
    pool_own.start()
    for copy in zb:
        copy.wait_recv()

    q_moves = [
        send(total, first_ref.at[me], (q_s, q_r), k, across(m)) for k, m in enumerate((1, 2, 3))
    ]
    for copy in q_moves:
        copy.start()
    first_own = pltpu.make_async_copy(total, first_ref.at[me], own_sem.at[1])
    first_own.start()
    qt_own = [
        send(total, first_ref.at[me], (qt_s, qt_r), dt - 1, beside(dt)) for dt in range(1, n_tp)
    ]
    for copy in qt_own:
        copy.start()

    x_over = [
        send(x_ref.at[p], x_ref.at[2 + p], (xt_s, xt_r), p, (z, c, t ^ 1)) for p in range(2)
    ]

    @pl.when(stays)
    def kept():
        x_keep.wait()

    @pl.when(jnp.logical_not(stays))
    def came():
        x_moves[0].wait_recv()

    x_over[0].start()
    x_moves[1].wait_recv()
    x_over[1].start()

    qt_on = []
    for k, m in enumerate((1, 2, 3)):
        q_moves[k].wait_recv()
        place = (c ^ m) * n_tp + t
        for dt in range(1, n_tp):
            copy = send(
                first_ref.at[place],
                first_ref.at[place],
                (qt_s, qt_r),
                (k + 1) * (n_tp - 1) + dt - 1,
                beside(dt),
            )
            copy.start()
            qt_on.append(copy)

    for copy in zc:
        copy.wait_recv()
    pool_own.wait()
    for m in range(chunks * per):
        sel[m] = pool[slots[KINDS + m]]
    rest_own = pltpu.make_async_copy(sel, rest_ref.at[me], own_sem.at[2])
    rest_own.start()
    r_moves = []
    rt_moves = []
    for k in range(chunks):
        span = pl.ds(k * per, per)
        pair = [
            send(
                sel.at[span],
                rest_ref.at[me, span],
                (r_s, r_r),
                k * 3 + j,
                across(m),
            )
            for j, m in enumerate((1, 2))
        ]
        for copy in pair:
            copy.start()
        r_moves.append(pair)
        for dt in range(1, n_tp):
            copy = send(
                sel.at[span],
                rest_ref.at[me, span],
                (rt_s, rt_r),
                (k * 4) * (n_tp - 1) + dt - 1,
                beside(dt),
            )
            copy.start()
            rt_moves.append(copy)

    def pass_on(k, which, place):
        span = pl.ds(k * per, per)
        for dt in range(1, n_tp):
            copy = send(
                rest_ref.at[place, span],
                rest_ref.at[place, span],
                (rt_s, rt_r),
                (k * 4 + which) * (n_tp - 1) + dt - 1,
                beside(dt),
            )
            copy.start()
            rt_moves.append(copy)

    onward = []
    for k in range(chunks):
        span = pl.ds(k * per, per)
        for j in range(2):
            r_moves[k][j].wait_recv()
        odd = lax.rem(core + k, 2)
        source = jnp.where(odd == 0, c ^ 1, c ^ 2) * n_tp + t
        target = (z, jnp.where(odd == 0, c ^ 2, c ^ 1), t)
        copy = send(
            rest_ref.at[source, span], rest_ref.at[source, span], (r_s, r_r), k * 3 + 2, target
        )
        copy.start()
        onward.append(copy)
        pass_on(k, 1, (c ^ 1) * n_tp + t)
        pass_on(k, 2, (c ^ 2) * n_tp + t)
    for k in range(chunks):
        onward[k].wait_recv()
        pass_on(k, 3, (c ^ 3) * n_tp + t)

    for copy in x_over:
        copy.wait()

    @pl.when(jnp.logical_not(stays))
    def left():
        x_moves[0].wait_send()

    x_moves[1].wait_send()
    for copy in (*za, *zb, *zc, *q_moves, *onward):
        copy.wait_send()
    for pair in r_moves:
        for copy in pair:
            copy.wait_send()
    for copy in (*qt_own, *qt_on, *rt_moves):
        copy.wait()
    first_own.wait()
    rest_own.wait()


def bring(slots, part, low, xs, n_shard, n_ctx, n_tp):
    held, rows, width = low.shape
    total_rows = part.shape[0]
    groups = n_ctx * n_tp
    mid = xs.shape[1]
    anywhere = pl.BlockSpec(memory_space=pl.ANY)
    dma = pltpu.SemaphoreType.DMA
    pairs = [2, 2, n_shard - 1, n_shard - 1, n_shard - 1, 3]
    pairs += [4 * (n_tp - 1), 9, 12 * (n_tp - 1)]
    sems = [dma((n,)) for n in pairs for _ in range(2)]
    return pl.pallas_call(
        functools.partial(bring_kernel, n_shard, n_ctx, n_tp),
        name="bring",
        in_specs=[
            pl.BlockSpec(memory_space=pltpu.SMEM),
            pl.BlockSpec(memory_space=pltpu.VMEM),
            anywhere,
            anywhere,
        ],
        out_specs=[anywhere, anywhere, anywhere],
        out_shape=[
            jax.ShapeDtypeStruct((4, mid, width), jnp.bfloat16),
            jax.ShapeDtypeStruct((groups, total_rows, width), jnp.bfloat16),
            jax.ShapeDtypeStruct((groups, 9, rows, width), jnp.bfloat16),
        ],
        scratch_shapes=[
            pltpu.VMEM((n_shard - 1, total_rows // n_shard, width), jnp.bfloat16),
            pltpu.VMEM((total_rows // n_shard, width), jnp.bfloat16),
            pltpu.VMEM((total_rows, width), jnp.bfloat16),
            pltpu.VMEM((n_shard * held, rows, width), jnp.bfloat16),
            pltpu.VMEM((9, rows, width), jnp.bfloat16),
            *sems,
            dma((3,)),
        ],
        compiler_params=pltpu.CompilerParams(
            collective_id=0, has_side_effects=True, vmem_limit_bytes=40 << 20
        ),
        cost_estimate=pl.CostEstimate(flops=0, bytes_accessed=40 << 20, transcendentals=0),
    )(slots, part, low, xs)


def late_kernel(
    n_ctx,
    n_tp,
    x_hbm,
    dq_hbm,
    dk_hbm,
    dv_hbm,
    gh1_hbm,
    first_hbm,
    wo_hbm,
    small_ref,
    home_ref,
    rows_ref,
    total_ref,
    x_s,
    dq_s,
    dk_s,
    dv_s,
    gh1_s,
    first_s,
    flipped,
    grads,
    arrived,
    partial,
    met,
    over,
    more,
    back_s,
    small_s,
    small_t,
    small_p,
    in_sem,
    c_s,
    c_r,
    p_s,
    p_r,
    o_s,
    o_r,
    h_s,
    h_r,
    sc_s,
    sc_r,
    sp_s,
    sp_r,
    keep_sem,
):
    z, c, t = place_of()
    side, core, bit = t // 2, lax.rem(t, 2), lax.rem(c, 2)
    _, mid, width = x_s.shape
    tokens = 2 * mid
    rows = rows_ref.shape[1]
    groups = n_ctx * n_tp
    per = groups // 2
    band = width // 2
    tile = mid // 2

    loads = [
        pltpu.make_async_copy(src, dst, in_sem.at[i])
        for i, (src, dst) in enumerate(
            (
                (x_hbm, x_s),
                (dk_hbm, dk_s),
                (dv_hbm, dv_s),
                (dq_hbm, dq_s),
                (first_hbm, first_s),
                (gh1_hbm, gh1_s),
                (wo_hbm, grads.at[:, 3]),
            )
        )
    ]
    for load in loads:
        load.start()

    def across(mask):
        return (z, c ^ mask, t)

    def beside(dt):
        return (z, c, lax.rem(t + dt, n_tp))

    barrier = pltpu.get_barrier_semaphore()
    friends = [(z, c ^ m, t) for m in range(1, n_ctx)]
    friends += [beside(dt) for dt in range(1, n_tp)]
    friends += [(z, c ^ m, t ^ 1) for m in range(1, n_ctx)]
    for friend in friends:
        pl.semaphore_signal(barrier, inc=1, device_id=friend, device_id_type=MESH)
    pl.semaphore_wait(barrier, len(friends))

    core_moves = []

    def exchange(m):
        for dt in range(1, n_tp):
            other = lax.rem(t + dt, n_tp)
            for k in range(n_ctx):
                copy = send(
                    grads.at[k * n_tp + other, m],
                    arrived.at[dt - 1, k, m],
                    (c_s, c_r),
                    ((dt - 1) * n_ctx + k) * 4 + m,
                    beside(dt),
                )
                copy.start()
                core_moves.append((m, copy))

    plane_moves = []

    def meet(m):
        for which, copy in core_moves:
            if which == m:
                copy.wait_recv()
        for k in range(n_ctx):
            value = grads[k * n_tp + t, m]
            for dt in range(1, n_tp):
                value = value + arrived[dt - 1, k, m]
            partial[k, m] = value
        for j in range(1, n_ctx):
            copy = send(
                partial.at[c ^ j, m], met.at[j - 1, m], (p_s, p_r), (j - 1) * 4 + m, across(j)
            )
            copy.start()
            plane_moves.append(copy)

    loads[6].wait()
    exchange(3)
    loads[0].wait()
    for a in range(4):
        own = 1 if a < 2 else 0
        chunk = 2 * (core if own else 1 - core) + ((a % 2) ^ bit)
        flipped[:, pl.ds(pl.multiple_of(chunk * mid, mid), mid)] = x_s[a].T

    mine = pl.ds(pl.multiple_of(core * tokens, tokens), tokens)
    def weight_grad(m, left_at, right):
        def one(i, carry):
            left = flipped[pl.ds(pl.multiple_of(i * band, band), band), left_at]
            value = wide_dot(left, right[...], NN).astype(jnp.bfloat16)
            grads[pl.ds(i * per, per), m] = value.reshape(per, rows, width)
            return carry

        lax.fori_loop(0, 2, one, 0)

    loads[1].wait()
    weight_grad(1, slice(None), dk_s)
    exchange(1)
    meet(3)
    loads[2].wait()
    weight_grad(2, slice(None), dv_s)
    exchange(2)
    meet(1)
    loads[3].wait()
    weight_grad(0, mine, dq_s)
    exchange(0)
    meet(2)

    row = lax.broadcasted_iota(jnp.int32, small_ref.shape, 0)
    q_sum = jnp.sum(dq_s[...].astype(jnp.float32), axis=0, keepdims=True)
    v_sum = jnp.sum(dv_s[...].astype(jnp.float32), axis=0, keepdims=True)
    sums = jnp.where(row == 0, q_sum, jnp.where(row == 1, v_sum, small_ref[...]))
    small_s[...] = sums.astype(jnp.bfloat16)
    small_core = [
        send(small_s, small_t.at[dt - 1], (sc_s, sc_r), dt - 1, beside(dt)) for dt in range(1, n_tp)
    ]
    for copy in small_core:
        copy.start()

    loads[4].wait()

    def weight(m):
        return first_s[:, m * rows : (m + 1) * rows, :].reshape(width, width)

    wq, wk, wv = weight(0), weight(1), weight(2)
    over_moves = []
    for b in range(2):
        at = pl.ds(pl.multiple_of((1 - core) * tokens + b * mid, mid), mid)
        value = wide_dot(dk_s[at, :], wk, NT) + wide_dot(dv_s[at, :], wv, NT)
        over[b] = value.astype(jnp.bfloat16)
        copy = send(over.at[b], more.at[b], (o_s, o_r), b, (z, c, t ^ 1))
        copy.start()
        over_moves.append(copy)

    meet(0)
    value = small_s[...]
    for dt, copy in enumerate(small_core):
        copy.wait_recv()
        value = value + small_t[dt]
    total_ref[...] = value
    small_plane = [
        send(total_ref, small_p.at[j - 1], (sp_s, sp_r), j - 1, across(j)) for j in range(1, n_ctx)
    ]
    for copy in small_plane:
        copy.start()

    loads[5].wait()
    stays = c // 2 == core
    home_moves = []
    for copy in over_moves:
        copy.wait_recv()
    for move in range(2):
        chunk = move ^ bit
        for i in range(2):
            at = pl.ds(pl.multiple_of(core * tokens + chunk * mid + i * tile, tile), tile)
            here = pl.ds(pl.multiple_of(chunk * mid + i * tile, tile), tile)
            value = gh1_s[here, :]
            value = value + more[chunk, i * tile : (i + 1) * tile, :].astype(jnp.float32)
            value = value + wide_dot(dq_s[here, :], wq, NT)
            value = value + wide_dot(dk_s[at, :], wk, NT)
            value = value + wide_dot(dv_s[at, :], wv, NT)
            back_s[move, i * tile : (i + 1) * tile, :] = value.astype(jnp.bfloat16)
        target = (z, 2 * core + chunk, 2 * side + c // 2)
        home_moves.append(send(back_s.at[move], home_ref.at[move], (h_s, h_r), move, target))
        if move == 0:
            keep = pltpu.make_async_copy(back_s.at[0], home_ref.at[0], keep_sem.at[0])

            @pl.when(stays)
            def kept():
                keep.start()

            @pl.when(jnp.logical_not(stays))
            def left():
                home_moves[0].start()

        else:
            home_moves[1].start()

    for copy in plane_moves:
        copy.wait_recv()
    for m in range(4):
        value = partial[c, m]
        for j in range(n_ctx - 1):
            value = value + met[j, m]
        rows_ref[m] = value
    value = total_ref[...]
    for j, copy in enumerate(small_plane):
        copy.wait()
        value = value + small_p[j]
    total_ref[...] = value

    @pl.when(stays)
    def done():
        keep.wait()

    @pl.when(jnp.logical_not(stays))
    def gone():
        home_moves[0].wait()

    home_moves[1].wait()
    for _, copy in core_moves:
        copy.wait_send()
    for copy in (*plane_moves, *over_moves, *small_core):
        copy.wait_send()


def late(x_all, dq, dk, dv, gh1, first, out_grad, small, rows, n_ctx, n_tp):
    _, mid, width = x_all.shape
    groups = n_ctx * n_tp
    anywhere = pl.BlockSpec(memory_space=pl.ANY)
    vmem = pl.BlockSpec(memory_space=pltpu.VMEM)
    dma = pltpu.SemaphoreType.DMA
    low = jnp.bfloat16
    pairs = [4 * n_ctx * (n_tp - 1), 4 * (n_ctx - 1), 2, 2, n_tp - 1, n_ctx - 1]
    return pl.pallas_call(
        functools.partial(late_kernel, n_ctx, n_tp),
        name="late",
        in_specs=[anywhere] * 7 + [vmem],
        out_specs=[anywhere, vmem, vmem],
        out_shape=[
            bf16_of(2, mid, width),
            bf16_of(4, rows, width),
            bf16_of(*small.shape),
        ],
        scratch_shapes=[
            pltpu.VMEM(x_all.shape, low),
            pltpu.VMEM(dq.shape, low),
            pltpu.VMEM(dk.shape, low),
            pltpu.VMEM(dv.shape, low),
            pltpu.VMEM(gh1.shape, jnp.float32),
            pltpu.VMEM(first.shape, low),
            pltpu.VMEM((width, 4 * mid), low),
            pltpu.VMEM((groups, 4, rows, width), low),
            pltpu.VMEM((n_tp - 1, n_ctx, 4, rows, width), low),
            pltpu.VMEM((n_ctx, 4, rows, width), low),
            pltpu.VMEM((n_ctx - 1, 4, rows, width), low),
            pltpu.VMEM((2, mid, width), low),
            pltpu.VMEM((2, mid, width), low),
            pltpu.VMEM((2, mid, width), low),
            pltpu.VMEM(small.shape, low),
            pltpu.VMEM((n_tp - 1, *small.shape), low),
            pltpu.VMEM((n_ctx - 1, *small.shape), low),
            dma((7,)),
            *[dma((n,)) for n in pairs for _ in range(2)],
            dma((1,)),
        ],
        compiler_params=pltpu.CompilerParams(
            collective_id=1, has_side_effects=True, vmem_limit_bytes=60 << 20
        ),
        cost_estimate=pl.CostEstimate(
            flops=12_000_000_000, bytes_accessed=30 << 20, transcendentals=0
        ),
    )(x_all, dq, dk, dv, gh1, first, out_grad, small)


def adam_update(weight, first, second, grad, decay, rate):
    count = float(STEP)
    first_new = beta_one * first + (1.0 - beta_one) * grad
    second_new = beta_two * second + (1.0 - beta_two) * grad * grad
    first_hat = first_new / (1.0 - beta_one**count)
    second_hat = second_new / (1.0 - beta_two**count)
    weight_new = weight - rate * (first_hat / (jnp.sqrt(second_hat) + adam_eps) + decay * weight)
    return (weight_new, first_new, second_new)


def owner_kernel(
    n_shard,
    holder,
    early_ref,
    late_ref,
    small_ref,
    w_ref,
    one_ref,
    two_ref,
    w_out,
    one_out,
    two_out,
    small_out,
    every,
    packed,
    met,
    small_met,
    z_s,
    z_r,
    s_s,
    s_r,
):
    z, c, t = place_of()
    held = w_ref.shape[0]

    def far(dz):
        return (lax.rem(z + dz, n_shard), c, t)

    barrier = pltpu.get_barrier_semaphore()
    for dz in range(1, n_shard):
        pl.semaphore_signal(barrier, inc=1, device_id=far(dz), device_id_type=MESH)
    every[0:4] = late_ref[...]
    every[4:12] = early_ref[...]
    every[12] = jnp.zeros_like(every[12])
    for s in range(n_shard * held):
        packed[s // held, s % held] = every[holder[s]]
    pl.semaphore_wait(barrier, n_shard - 1)
    moves = [
        send(packed.at[far(dz)[0]], met.at[dz - 1], (z_s, z_r), dz - 1, far(dz))
        for dz in range(1, n_shard)
    ]
    moves += [
        send(small_ref, small_met.at[dz - 1], (s_s, s_r), dz - 1, far(dz))
        for dz in range(1, n_shard)
    ]
    for copy in moves:
        copy.start()
    for copy in moves:
        copy.wait()
    for j in range(held):
        grad = packed[z, j].astype(jnp.float32)
        for dz in range(n_shard - 1):
            grad = grad + met[dz, j].astype(jnp.float32)
        w, one, two = adam_update(w_ref[j], one_ref[j], two_ref[j], grad, 0.01, rate_value)
        w_out[j] = w
        one_out[j] = one
        two_out[j] = two
    total = small_ref[...].astype(jnp.float32)
    for dz in range(n_shard - 1):
        total = total + small_met[dz].astype(jnp.float32)
    small_out[...] = total


def owner(holder, early, late_rows, small, master, one, two, n_shard):
    held, rows, width = master.shape
    vmem = pl.BlockSpec(memory_space=pltpu.VMEM)
    dma = pltpu.SemaphoreType.DMA
    return pl.pallas_call(
        functools.partial(owner_kernel, n_shard),
        name="owner",
        in_specs=[pl.BlockSpec(memory_space=pltpu.SMEM)] + [vmem] * 6,
        out_specs=[vmem] * 4,
        out_shape=[f32_of(held, rows, width)] * 3 + [f32_of(*small.shape)],
        scratch_shapes=[
            pltpu.VMEM((13, rows, width), jnp.bfloat16),
            pltpu.VMEM((n_shard, held, rows, width), jnp.bfloat16),
            pltpu.VMEM((n_shard - 1, held, rows, width), jnp.bfloat16),
            pltpu.VMEM((n_shard - 1, *small.shape), jnp.bfloat16),
            *[dma((n_shard - 1,)) for _ in range(4)],
        ],
        compiler_params=pltpu.CompilerParams(
            collective_id=2, has_side_effects=True, vmem_limit_bytes=40 << 20
        ),
        cost_estimate=pl.CostEstimate(flops=0, bytes_accessed=12 << 20, transcendentals=0),
    )(holder, early, late_rows, small, master, one, two)


def moves(n_ctx, n_tp, pick):
    pairs = []
    for c in range(n_ctx):
        for t in range(n_tp):
            side, core = t // 2, t % 2
            to_ctx = 2 * core + (pick ^ (c & 1))
            to_tp = 2 * side + c // 2
            pairs.append((c * n_tp + t, to_ctx * n_tp + to_tp))
    return pairs


def shards(
    inputs,
    cotangent,
    rand_blocks,
    slot_of,
    master,
    moment_one,
    moment_two,
    small_params,
    small_one,
    small_two,
):
    n_shard = lax.axis_size("shard")
    n_ctx = lax.axis_size("ctx")
    n_tp = lax.axis_size("tp")
    groups = n_ctx * n_tp
    held, rows, width = master.shape
    span = small_params.shape[0]
    my_ctx = lax.axis_index("ctx")
    my_tp = lax.axis_index("tp")
    parity = lax.rem(my_ctx, 2)
    half = lax.rem(my_tp, 2)
    plane = ("ctx", "tp")
    forth = [moves(n_ctx, n_tp, pick) for pick in range(2)]
    home = [[(b, a) for a, b in pairs] for pairs in forth]
    swap = [(t, t ^ 1) for t in range(n_tp)]

    arrival = [(b ^ parity) + 2 * (half ^ (j // 2)) for j, b in enumerate((0, 1, 0, 1))]
    info = jnp.stack([half, *arrival]).astype(jnp.int32)
    half_one = info[:1]

    def sent(field, pick):
        low = field.astype(jnp.bfloat16)
        return jnp.where(parity == 0, low[pick], low[1 - pick])

    def returned(first, second):
        swapped = parity == 1
        out = jnp.stack(
            [jnp.where(swapped, second, first), jnp.where(swapped, first, second)]
        )
        return out.astype(jnp.float32)

    low = master.astype(jnp.bfloat16)
    my_shard = lax.axis_index("shard")
    mine = my_shard * held + jnp.arange(held, dtype=jnp.int32)
    zero = jnp.zeros_like(low)
    parts = [
        jnp.sum(jnp.where((slot_of[m] == mine)[:, None, None], low, zero), axis=0, dtype=jnp.float32)
        for m in range(3)
    ]
    spread = (jnp.arange(n_shard) == my_shard)[:, None]
    small_part = jnp.where(spread, small_params[None, :], 0.0).reshape(-1)
    used = 3 * rows * width + n_shard * span
    total_rows = -(-used // (width * 16 * n_shard)) * 16 * n_shard
    small_part = jnp.pad(small_part, (0, total_rows * width - used)).reshape(-1, width)
    part = jnp.concatenate([*parts, small_part]).astype(jnp.bfloat16)
    xs = jnp.stack([sent(inputs, pick) for pick in range(2)])
    x_all, first, rest = bring(slot_of, part, low, xs, n_shard, n_ctx, n_tp)
    small = first[:, 3 * rows :, :].reshape(groups, -1)[:, : n_shard * span]
    small = small.reshape(groups, n_shard, span).transpose(1, 0, 2)
    small = small.reshape(-1, width).astype(jnp.float32)

    cots, x_all = lax.optimization_barrier(
        ([sent(cotangent, pick) for pick in range(2)], x_all)
    )
    cot = jnp.stack([lax.ppermute(cots[pick], plane, forth[pick]) for pick in range(2)])

    q, k, v = project(info, x_all, small, first, rows)
    context, lse = attend(half_one, rand_blocks, q, k, v, 5)
    out_low, n1, r1, fi, fit, hid, gel, gh2, gmt, sums_two = front(
        info, context, x_all, cot, small, rest
    )
    layer_out = returned(*[lax.ppermute(out_low[p], plane, home[p]) for p in range(2)])
    ffn_grads, out_grad, gh1, dctx, sums_one = back(
        info, gh2, hid, gel, fit, gmt, n1, r1, context, small, rest
    )
    ffn_rows = lax.psum_scatter(ffn_grads, plane, scatter_dimension=0, tiled=False)
    dq, dk, dv = attend_back(half_one, rand_blocks, q, k, v, lse, dctx, 5)
    small_rows = jnp.pad(
        jnp.concatenate([sums_one[4:7], sums_one[0:4], sums_two[0:3]]), ((2, 4), (0, 0))
    )
    came, late_rows, small_late = late(
        x_all, dq, dk, dv, gh1, first, out_grad, small_rows, rows, n_ctx, n_tp
    )
    input_grad = returned(came[0], came[1])

    stands = jnp.array([0, 1, 2, 3, 4, 6, 8, 10, 5, 7, 9, 11], jnp.int32)
    slots_all = jnp.arange(n_shard * held, dtype=jnp.int32)
    holder = 12 + jnp.sum(
        jnp.where(slot_of[None, :] == slots_all[:, None], stands[None, :] - 12, 0), axis=1
    )
    master_new, first_new, second_new, small_sum = owner(
        holder.astype(jnp.int32), ffn_rows, late_rows, small_late, master, moment_one, moment_two, n_shard
    )
    start = ((my_shard * n_ctx + my_ctx) * n_tp + my_tp) * span
    small_owned = lax.dynamic_slice_in_dim(small_sum.reshape(-1), start, span)
    small_new, small_first, small_second = adam_update(
        small_params, small_one, small_two, small_owned, 0.0, small_rate
    )
    return (
        layer_out,
        input_grad,
        master_new,
        first_new,
        second_new,
        small_new,
        small_first,
        small_second,
    )


def solution(mesh):
    tokens = P(("shard", "tp"), "ctx", None)
    stored = P("shard", ("ctx", "tp"), None)
    spread = P(("shard", "ctx", "tp"))
    return jax.shard_map(
        shards,
        mesh=mesh,
        in_specs=(tokens, tokens, P(), P(), stored, stored, stored, spread, spread, spread),
        out_specs=(tokens, tokens, stored, stored, stored, spread, spread, spread),
        check_vma=False,
    )
```

```python
import functools

import jax
import jax.numpy as jnp
from jax import lax
from jax.experimental import pallas as pl
from jax.experimental.pallas import tpu as pltpu
from jax.sharding import PartitionSpec as P

STEP = 5
norm_eps = 1e-12
beta_one = 0.9
beta_two = 0.999
adam_eps = 1e-08
rate_value = 0.04
small_rate = 0.25
score_scale = 0.125
gelu_root = 0.7978845608
gelu_cube = 0.044715

BLOCK = 64
HEAD = 64
PACK = 4
masked_score = -1e30


def wide_dot(a, b, dims):
    return lax.dot_general(a, b, (dims, ((), ())), preferred_element_type=jnp.float32)


def head_masks(rows):
    lane = lax.broadcasted_iota(jnp.int32, (rows, PACK * HEAD), 1) // HEAD
    return [lane == h for h in range(PACK)]


def spread_heads(block, masks):
    zero = jnp.zeros_like(block)
    return jnp.concatenate([jnp.where(m, block, zero) for m in masks], axis=0)


def own_heads(full, masks):
    total = None
    for h, m in enumerate(masks):
        piece = jnp.where(m, full[h * BLOCK : (h + 1) * BLOCK], 0.0)
        total = piece if total is None else total + piece
    return total


def rows_of(ref, index, count=1):
    return ref[pl.ds(pl.multiple_of(index * BLOCK, BLOCK), count * BLOCK), :]


def picked_rows(ref, picks, low_half):
    halves = []
    for pair in range(PACK // 2):
        cols = pl.ds(pair * 2 * HEAD, 2 * HEAD)
        first = ref[pl.ds(pl.multiple_of(picks[2 * pair] * BLOCK, BLOCK), BLOCK), cols]
        second = ref[pl.ds(pl.multiple_of(picks[2 * pair + 1] * BLOCK, BLOCK), BLOCK), cols]
        halves.append(jnp.where(low_half, first, second))
    return jnp.concatenate(halves, axis=1)


def gathered(ref, block, last, picks, low_half):
    pieces = [rows_of(ref, 0), rows_of(ref, last), rows_of(ref, block - 1, 3)]
    pieces += [picked_rows(ref, p, low_half) for p in picks]
    return jnp.concatenate(pieces, axis=0)


def middle_scores(keys, spread, block, last):
    scores = wide_dot(keys, spread, ((1,), (1,)))
    first_off = jnp.where(block == 1, masked_score, 0.0)
    last_off = jnp.where(block == last - 1, masked_score, 0.0)
    b = BLOCK
    return jnp.concatenate(
        [
            scores[: 2 * b],
            scores[2 * b : 3 * b] + first_off,
            scores[3 * b : 4 * b],
            scores[4 * b : 5 * b] + last_off,
            scores[5 * b :],
        ],
        axis=0,
    )


def attend_kernel(unroll, half_ref, table_ref, q_ref, k_ref, v_ref, out_ref, lse_ref, kept):
    half = half_ref[0]
    group = pl.program_id(0)
    nblocks = k_ref.shape[0] // BLOCK
    local = q_ref.shape[0] // BLOCK
    last = nblocks - 1
    picks_each = table_ref.shape[2]
    masks = head_masks(BLOCK)
    low_half = lax.broadcasted_iota(jnp.int32, (BLOCK, 2 * HEAD), 1) < HEAD

    def middle(step, carry):
        mine = step + 1 - half
        block = mine + local * half
        picks = [
            [table_ref[group * PACK + h, block - 1, r] for h in range(PACK)]
            for r in range(picks_each)
        ]
        spread = spread_heads(rows_of(q_ref, mine), masks)
        keys = gathered(k_ref, block, last, picks, low_half)
        values = gathered(v_ref, block, last, picks, low_half)
        scores = middle_scores(keys, spread, block, last)
        top = jnp.max(scores, axis=0, keepdims=True)
        probs = jnp.exp(scores - top)
        total = jnp.sum(probs, axis=0, keepdims=True)
        low = (probs * (1.0 / total)).astype(jnp.bfloat16)
        full = wide_dot(low, values, ((0,), (0,)))
        out_ref[pl.ds(pl.multiple_of(mine * BLOCK, BLOCK), BLOCK), :] = own_heads(
            full, masks
        ).astype(jnp.bfloat16)
        lse_ref[0, pl.ds(mine, 1), :] = top + jnp.log(total)
        return carry

    lax.fori_loop(0, local - 1, middle, 0, unroll=unroll)

    edge = (local - 1) * half
    spread = spread_heads(rows_of(q_ref, edge), masks)
    span = 8 * BLOCK
    chunks = nblocks // 8
    top = None
    for c in range(chunks):
        scores = wide_dot(k_ref[c * span : (c + 1) * span, :], spread, ((1,), (1,)))
        kept[c * span : (c + 1) * span, :] = scores
        high = jnp.max(scores, axis=0, keepdims=True)
        top = high if top is None else jnp.maximum(top, high)
    total = None
    for c in range(chunks):
        probs = jnp.exp(kept[c * span : (c + 1) * span, :] - top)
        kept[c * span : (c + 1) * span, :] = probs
        part = jnp.sum(probs, axis=0, keepdims=True)
        total = part if total is None else total + part
    scale = 1.0 / total
    full = None
    for c in range(chunks):
        low = (kept[c * span : (c + 1) * span, :] * scale).astype(jnp.bfloat16)
        part = wide_dot(low, v_ref[c * span : (c + 1) * span, :], ((0,), (0,)))
        full = part if full is None else full + part
    out_ref[pl.ds(pl.multiple_of(edge * BLOCK, BLOCK), BLOCK), :] = own_heads(
        full, masks
    ).astype(jnp.bfloat16)
    lse_ref[0, pl.ds(edge, 1), :] = top + jnp.log(total)


def attend(half, table, q, k, v, unroll=3):
    tokens, width = q.shape
    seq = k.shape[0]
    lanes = PACK * HEAD
    groups = width // lanes
    blocks = tokens // BLOCK
    spec = pltpu.PrefetchScalarGridSpec(
        num_scalar_prefetch=2,
        grid=(groups,),
        in_specs=[
            pl.BlockSpec((tokens, lanes), lambda g, *_: (0, g)),
            pl.BlockSpec((seq, lanes), lambda g, *_: (0, g)),
            pl.BlockSpec((seq, lanes), lambda g, *_: (0, g)),
        ],
        out_specs=[
            pl.BlockSpec((tokens, lanes), lambda g, *_: (0, g)),
            pl.BlockSpec((1, blocks, lanes), lambda g, *_: (g, 0, 0)),
        ],
        scratch_shapes=[pltpu.VMEM((seq, lanes), jnp.float32)],
    )
    return pl.pallas_call(
        functools.partial(attend_kernel, unroll),
        grid_spec=spec,
        out_shape=[
            jax.ShapeDtypeStruct((tokens, width), jnp.bfloat16),
            jax.ShapeDtypeStruct((groups, blocks, lanes), jnp.float32),
        ],
        name="attend",
        compiler_params=pltpu.CompilerParams(vmem_limit_bytes=56 << 20),
        cost_estimate=pl.CostEstimate(
            flops=60_000_000_000, bytes_accessed=12 << 20, transcendentals=16_000_000
        ),
    )(half, table, q, k, v)


def attend_back_kernel(
    unroll,
    half_ref,
    table_ref,
    q_ref,
    k_ref,
    v_ref,
    lse_ref,
    do_ref,
    dq_ref,
    dk_ref,
    dv_ref,
    dk_acc,
    dv_acc,
    kept_p,
    kept_g,
):
    half = half_ref[0]
    group = pl.program_id(0)
    nblocks = k_ref.shape[0] // BLOCK
    local = q_ref.shape[0] // BLOCK
    last = nblocks - 1
    picks_each = table_ref.shape[2]
    masks = head_masks(BLOCK)
    low_half = lax.broadcasted_iota(jnp.int32, (BLOCK, 2 * HEAD), 1) < HEAD
    span = 8 * BLOCK
    chunks = nblocks // 8

    edge = (local - 1) * half
    spread = spread_heads(rows_of(q_ref, edge), masks)
    spread_do = spread_heads(rows_of(do_ref, edge), masks)
    lse = lse_ref[0, pl.ds(edge, 1), :]
    delta = None
    for c in range(chunks):
        rows = slice(c * span, (c + 1) * span)
        probs = jnp.exp(wide_dot(k_ref[rows, :], spread, ((1,), (1,))) - lse)
        gp = wide_dot(v_ref[rows, :], spread_do, ((1,), (1,)))
        kept_p[rows, :] = probs
        kept_g[rows, :] = gp
        part = jnp.sum(probs * gp, axis=0, keepdims=True)
        delta = part if delta is None else delta + part
    full = None
    for c in range(chunks):
        rows = slice(c * span, (c + 1) * span)
        probs = kept_p[rows, :]
        ds = (probs * (kept_g[rows, :] - delta)).astype(jnp.bfloat16)
        dv_acc[rows, :] = wide_dot(probs.astype(jnp.bfloat16), spread_do, ((1,), (0,)))
        dk_acc[rows, :] = wide_dot(ds, spread, ((1,), (0,)))
        part = wide_dot(ds, k_ref[rows, :], ((0,), (0,)))
        full = part if full is None else full + part
    dq_ref[pl.ds(pl.multiple_of(edge * BLOCK, BLOCK), BLOCK), :] = (
        own_heads(full, masks) * 0.125
    ).astype(jnp.bfloat16)

    def scatter(acc, piece, block, picks):
        b = BLOCK
        acc[0:b, :] += piece[:b]
        acc[last * b : (last + 1) * b, :] += piece[b : 2 * b]
        window = pl.ds(pl.multiple_of((block - 1) * b, b), 3 * b)
        acc[window, :] += piece[2 * b : 5 * b]
        for r, p in enumerate(picks):
            part = piece[(5 + r) * b : (6 + r) * b]
            for pair in range(PACK // 2):
                lanes = slice(pair * 2 * HEAD, (pair + 1) * 2 * HEAD)
                cols = pl.ds(pair * 2 * HEAD, 2 * HEAD)
                sub = part[:, lanes]
                acc[pl.ds(pl.multiple_of(p[2 * pair] * b, b), b), cols] += jnp.where(
                    low_half, sub, 0.0
                )
                acc[pl.ds(pl.multiple_of(p[2 * pair + 1] * b, b), b), cols] += jnp.where(
                    low_half, 0.0, sub
                )

    def middle(step, carry):
        mine = step + 1 - half
        block = mine + local * half
        picks = [
            [table_ref[group * PACK + h, block - 1, r] for h in range(PACK)]
            for r in range(picks_each)
        ]
        spread = spread_heads(rows_of(q_ref, mine), masks)
        spread_do = spread_heads(rows_of(do_ref, mine), masks)
        keys = gathered(k_ref, block, last, picks, low_half)
        values = gathered(v_ref, block, last, picks, low_half)
        scores = middle_scores(keys, spread, block, last)
        probs = jnp.exp(scores - lse_ref[0, pl.ds(mine, 1), :])
        gp = wide_dot(values, spread_do, ((1,), (1,)))
        delta = jnp.sum(probs * gp, axis=0, keepdims=True)
        ds = (probs * (gp - delta)).astype(jnp.bfloat16)
        low = probs.astype(jnp.bfloat16)
        scatter(dv_acc, wide_dot(low, spread_do, ((1,), (0,))), block, picks)
        scatter(dk_acc, wide_dot(ds, spread, ((1,), (0,))), block, picks)
        full = wide_dot(ds, keys, ((0,), (0,)))
        dq_ref[pl.ds(pl.multiple_of(mine * BLOCK, BLOCK), BLOCK), :] = (
            own_heads(full, masks) * 0.125
        ).astype(jnp.bfloat16)
        return carry

    lax.fori_loop(0, local - 1, middle, 0, unroll=unroll)
    dk_ref[...] = dk_acc[...].astype(jnp.bfloat16)
    dv_ref[...] = dv_acc[...].astype(jnp.bfloat16)


def attend_back(half, table, q, k, v, lse, do, unroll=3):
    tokens, width = q.shape
    seq = k.shape[0]
    lanes = PACK * HEAD
    groups = width // lanes
    blocks = tokens // BLOCK
    mine = pl.BlockSpec((tokens, lanes), lambda g, *_: (0, g))
    whole = pl.BlockSpec((seq, lanes), lambda g, *_: (0, g))
    spec = pltpu.PrefetchScalarGridSpec(
        num_scalar_prefetch=2,
        grid=(groups,),
        in_specs=[
            mine,
            whole,
            whole,
            pl.BlockSpec((1, blocks, lanes), lambda g, *_: (g, 0, 0)),
            mine,
        ],
        out_specs=[mine, whole, whole],
        scratch_shapes=[pltpu.VMEM((seq, lanes), jnp.float32)] * 4,
    )
    return pl.pallas_call(
        functools.partial(attend_back_kernel, unroll),
        grid_spec=spec,
        out_shape=[
            jax.ShapeDtypeStruct((tokens, width), jnp.bfloat16),
            jax.ShapeDtypeStruct((seq, width), jnp.bfloat16),
            jax.ShapeDtypeStruct((seq, width), jnp.bfloat16),
        ],
        name="attend_back",
        compiler_params=pltpu.CompilerParams(vmem_limit_bytes=56 << 20),
        cost_estimate=pl.CostEstimate(
            flops=120_000_000_000, bytes_accessed=24 << 20, transcendentals=16_000_000
        ),
    )(half, table, q, k, v, lse, do)


TILE = 256
MID = 512


def cols_mean(value):
    return jnp.mean(value, axis=-1, keepdims=True)


def normed(field):
    centred = field - cols_mean(field)
    rate = lax.rsqrt(cols_mean(centred * centred) + norm_eps)
    return centred * rate, rate


def norm_back(cot, normal, rate, gain):
    dn = cot * gain
    return rate * (dn - cols_mean(dn) - normal * cols_mean(dn * normal))


def matrix(ref):
    value = ref[...]
    return value.reshape(-1, value.shape[-1])


def add_row(ref, row, value):
    ref[row : row + 1, :] += jnp.sum(value, axis=0, keepdims=True)


def first_spec(first, rows, which):
    groups, _, width = first.shape
    return pl.BlockSpec(
        (groups, rows, width), lambda step, info: (0, which, 0), pipeline_mode=pl.Buffered(1)
    )


def rest_spec(rest, which, single=True):
    groups, _, rows, width = rest.shape
    mode = pl.Buffered(1) if single else None
    return pl.BlockSpec(
        (groups, 1, rows, width), lambda step, info: (0, which(step) - 3, 0, 0), pipeline_mode=mode
    )


def fixed(shape):
    return pl.BlockSpec(shape, lambda step, info: (0,) * len(shape), pipeline_mode=pl.Buffered(1))


def resident(shape):
    return pl.BlockSpec(shape, lambda step, info: (0,) * len(shape))


def call(kernel, name, info, grid, in_specs, out_specs, out_shape, scratch, args, flops, moved):
    return pl.pallas_call(
        kernel,
        name=name,
        grid_spec=pltpu.PrefetchScalarGridSpec(
            num_scalar_prefetch=1,
            grid=(grid,),
            in_specs=in_specs,
            out_specs=out_specs,
            scratch_shapes=scratch,
        ),
        out_shape=out_shape,
        compiler_params=pltpu.CompilerParams(vmem_limit_bytes=60 << 20),
        cost_estimate=pl.CostEstimate(
            flops=flops, bytes_accessed=moved, transcendentals=0
        ),
    )(info, *args)


def bf16_of(*shape):
    return jax.ShapeDtypeStruct(shape, jnp.bfloat16)


def f32_of(*shape):
    return jax.ShapeDtypeStruct(shape, jnp.float32)


NN = ((1,), (0,))
NT = ((1,), (1,))
TN = ((0,), (0,))


def project_kernel(info, x_ref, small, wq, wk, wv, q_ref, k_ref, v_ref):
    x = x_ref[0]

    @pl.when(pl.program_id(0) < 2)
    def own():
        q = wide_dot(x, matrix(wq), NN) + small[0:1, :]
        q_ref[...] = q.astype(jnp.bfloat16) * jnp.bfloat16(score_scale)

    k_ref[...] = wide_dot(x, matrix(wk), NN).astype(jnp.bfloat16)
    v_ref[...] = (wide_dot(x, matrix(wv), NN) + small[1:2, :]).astype(jnp.bfloat16)


def project(info, x_all, small, first, rows):
    _, mid, width = x_all.shape

    def chunk(step, info):
        return lax.rem(step + 2 * info[0], 4)

    return call(
        project_kernel,
        "project",
        info,
        4,
        [
            pl.BlockSpec((1, mid, width), lambda g, info: (info[1 + chunk(g, info)], 0, 0)),
            fixed(small.shape),
            *[first_spec(first, rows, m) for m in range(3)],
        ],
        [
            pl.BlockSpec((mid, width), lambda g, info: (jnp.minimum(g, 1), 0)),
            pl.BlockSpec((mid, width), lambda g, info: (chunk(g, info), 0)),
            pl.BlockSpec((mid, width), lambda g, info: (chunk(g, info), 0)),
        ],
        [bf16_of(2 * mid, width), bf16_of(4 * mid, width), bf16_of(4 * mid, width)],
        [],
        (x_all, small, first, first, first),
        6_000_000_000,
        16 << 20,
    )


def front_kernel(
    info,
    ctx_ref,
    x_ref,
    cot_ref,
    small,
    wo,
    u0,
    u1,
    u2,
    u3,
    v0,
    v1,
    v2,
    v3,
    out_ref,
    n1_ref,
    r1_ref,
    fi_ref,
    fit_ref,
    hid_ref,
    gel_ref,
    gh2_ref,
    gmt_ref,
    sums_ref,
):
    attn_out = wide_dot(ctx_ref[...], matrix(wo), NN) + small[2:3, :]
    n1, r1 = normed(x_ref[0].astype(jnp.float32) + attn_out)
    n1_ref[...] = n1
    r1_ref[...] = jnp.broadcast_to(r1, r1_ref.shape)
    after = n1 * small[3:4, :] + small[4:5, :]
    ffn_in = after.astype(jnp.bfloat16)
    fi_ref[...] = ffn_in
    fit_ref[...] = ffn_in.T
    total = after + small[9:10, :]
    for b, (up_w, down_w) in enumerate(((u0, v0), (u1, v1), (u2, v2), (u3, v3))):
        up = wide_dot(ffn_in, matrix(up_w), NN) + small[5 + b : 6 + b, :]
        square = up * up
        bent = jnp.tanh(gelu_root * up * (1.0 + gelu_cube * square))
        rise = 0.5 * (1.0 + bent)
        hidden = (up * rise).astype(jnp.bfloat16)
        hid_ref[b] = hidden
        slope = rise + (0.5 * gelu_root) * up * (1.0 - bent * bent) * (
            1.0 + (3.0 * gelu_cube) * square
        )
        gel_ref[b] = slope.astype(jnp.bfloat16)
        total = total + wide_dot(hidden, matrix(down_w), NT)
    n2, r2 = normed(total)
    out_ref[0] = (n2 * small[10:11, :] + small[11:12, :]).astype(jnp.bfloat16)
    cot = cot_ref[0].astype(jnp.float32)
    gh2 = norm_back(cot, n2, r2, small[10:11, :])
    gh2_ref[...] = gh2
    mixed = gh2.astype(jnp.bfloat16)
    gmt_ref[...] = mixed.T

    @pl.when(pl.program_id(0) == 0)
    def clear():
        sums_ref[...] = jnp.zeros_like(sums_ref)

    add_row(sums_ref, 0, mixed.astype(jnp.float32))
    add_row(sums_ref, 1, cot * n2)
    add_row(sums_ref, 2, cot)


def front(info, ctx, x_all, cot, small, rest):
    tokens, width = ctx.shape
    mid = x_all.shape[1]
    per = mid // TILE
    steps = tokens // TILE

    def arrived(t, info):
        return (info[1 + 2 * info[0] + t // per], t % per, 0)

    def rows(dtype_shape):
        return pl.BlockSpec(dtype_shape, lambda t, info: (t, 0))

    specs = [rest_spec(rest, lambda t, m=m: m) for m in range(3, 12)]
    wide4 = pl.BlockSpec((4, TILE, width), lambda t, info: (0, t, 0))
    flipped = pl.BlockSpec((width, TILE), lambda t, info: (0, t))
    return call(
        front_kernel,
        "front",
        info,
        steps,
        [
            rows((TILE, width)),
            pl.BlockSpec((1, TILE, width), arrived),
            pl.BlockSpec((1, TILE, width), arrived),
            fixed(small.shape),
            *specs,
        ],
        [
            pl.BlockSpec((1, TILE, width), arrived),
            rows((TILE, width)),
            rows((TILE, 128)),
            rows((TILE, width)),
            flipped,
            wide4,
            wide4,
            rows((TILE, width)),
            flipped,
            resident((8, width)),
        ],
        [
            bf16_of(2, mid, width),
            f32_of(tokens, width),
            f32_of(tokens, 128),
            bf16_of(tokens, width),
            bf16_of(width, tokens),
            bf16_of(4, tokens, width),
            bf16_of(4, tokens, width),
            f32_of(tokens, width),
            bf16_of(width, tokens),
            f32_of(8, width),
        ],
        [],
        (ctx, x_all, cot, small, *([rest] * 9)),
        11_000_000_000,
        40 << 20,
    )


MESH = pl.DeviceIdType.MESH
KINDS = 3


def place_of():
    c, t = lax.axis_index("ctx"), lax.axis_index("tp")
    return lax.axis_index("shard"), c, t


def send(src, dst, sems, index, target):
    send_sems, recv_sems = sems
    return pltpu.make_async_remote_copy(
        src_ref=src,
        dst_ref=dst,
        send_sem=send_sems.at[index],
        recv_sem=recv_sems.at[index],
        device_id=target,
        device_id_type=MESH,
    )


def bring_kernel(
    n_shard,
    n_ctx,
    n_tp,
    slots,
    part_ref,
    low_ref,
    xs_ref,
    x_ref,
    first_ref,
    rest_ref,
    got,
    mine,
    total,
    pool,
    sel,
    x_s,
    x_r,
    xt_s,
    xt_r,
    za_s,
    za_r,
    zb_s,
    zb_r,
    zc_s,
    zc_r,
    q_s,
    q_r,
    qt_s,
    qt_r,
    r_s,
    r_r,
    rt_s,
    rt_r,
    own_sem,
):
    z, c, t = place_of()
    side, core, bit = t // 2, lax.rem(t, 2), lax.rem(c, 2)
    held = low_ref.shape[0]
    piece = mine.shape[0]
    chunks, per = 3, 3
    me = c * n_tp + t

    def far(dz):
        return (lax.rem(z + dz, n_shard), c, t)

    def across(mask):
        return (z, c ^ mask, t)

    def beside(dt):
        return (z, c, lax.rem(t + dt, n_tp))

    barrier = pltpu.get_barrier_semaphore()
    friends = [far(dz) for dz in range(1, n_shard)]
    friends += [(z, c ^ m, t) for m in range(1, n_ctx)]
    friends += [beside(dt) for dt in range(1, n_tp)]
    friends += [(z, c ^ m, t ^ 1) for m in range(1, n_ctx)]
    for friend in friends:
        pl.semaphore_signal(barrier, inc=1, device_id=friend, device_id_type=MESH)
    pl.semaphore_wait(barrier, len(friends))

    stays = c // 2 == core
    goes = [(z, 2 * core + (p ^ bit), 2 * side + c // 2) for p in range(2)]
    x_moves = [send(xs_ref.at[p], x_ref.at[p], (x_s, x_r), p, goes[p]) for p in range(2)]
    x_keep = pltpu.make_async_copy(xs_ref.at[0], x_ref.at[0], x_r.at[0])

    za = [
        send(
            part_ref.at[pl.ds(pl.multiple_of(far(dz)[0] * piece, piece), piece)],
            got.at[dz - 1],
            (za_s, za_r),
            dz - 1,
            far(dz),
        )
        for dz in range(1, n_shard)
    ]
    for copy in za:
        copy.start()

    @pl.when(stays)
    def keep():
        x_keep.start()

    @pl.when(jnp.logical_not(stays))
    def leave():
        x_moves[0].start()

    x_moves[1].start()
    summed = part_ref[pl.ds(pl.multiple_of(z * piece, piece), piece), :]
    for dz, copy in enumerate(za):
        copy.wait_recv()
        summed = summed + got[dz]
    mine[...] = summed
    here = pl.ds(pl.multiple_of(z * piece, piece), piece)
    zb = [
        send(mine, total.at[here], (zb_s, zb_r), dz - 1, far(dz)) for dz in range(1, n_shard)
    ]
    for copy in zb:
        copy.start()
    total[here, :] = summed
    pool_here = pl.ds(z * held, held)
    zc = [
        send(low_ref, pool.at[pool_here], (zc_s, zc_r), dz - 1, far(dz))
        for dz in range(1, n_shard)
    ]
    for copy in zc:
        copy.start()
    pool_own = pltpu.make_async_copy(low_ref, pool.at[pool_here], own_sem.at[0])
    pool_own.start()
    for copy in zb:
        copy.wait_recv()

    q_moves = [
        send(total, first_ref.at[me], (q_s, q_r), k, across(m)) for k, m in enumerate((1, 2, 3))
    ]
    for copy in q_moves:
        copy.start()
    first_own = pltpu.make_async_copy(total, first_ref.at[me], own_sem.at[1])
    first_own.start()
    qt_own = [
        send(total, first_ref.at[me], (qt_s, qt_r), dt - 1, beside(dt)) for dt in range(1, n_tp)
    ]
    for copy in qt_own:
        copy.start()

    x_over = [
        send(x_ref.at[p], x_ref.at[2 + p], (xt_s, xt_r), p, (z, c, t ^ 1)) for p in range(2)
    ]

    @pl.when(stays)
    def kept():
        x_keep.wait()

    @pl.when(jnp.logical_not(stays))
    def came():
        x_moves[0].wait_recv()

    x_over[0].start()
    x_moves[1].wait_recv()
    x_over[1].start()

    qt_on = []
    for k, m in enumerate((1, 2, 3)):
        q_moves[k].wait_recv()
        place = (c ^ m) * n_tp + t
        for dt in range(1, n_tp):
            copy = send(
                first_ref.at[place],
                first_ref.at[place],
                (qt_s, qt_r),
                (k + 1) * (n_tp - 1) + dt - 1,
                beside(dt),
            )
            copy.start()
            qt_on.append(copy)

    for copy in zc:
        copy.wait_recv()
    pool_own.wait()
    for m in range(chunks * per):
        sel[m] = pool[slots[KINDS + m]]
    rest_own = pltpu.make_async_copy(sel, rest_ref.at[me], own_sem.at[2])
    rest_own.start()
    r_moves = []
    rt_moves = []
    for k in range(chunks):
        span = pl.ds(k * per, per)
        pair = [
            send(
                sel.at[span],
                rest_ref.at[me, span],
                (r_s, r_r),
                k * 3 + j,
                across(m),
            )
            for j, m in enumerate((1, 2))
        ]
        for copy in pair:
            copy.start()
        r_moves.append(pair)
        for dt in range(1, n_tp):
            copy = send(
                sel.at[span],
                rest_ref.at[me, span],
                (rt_s, rt_r),
                (k * 4) * (n_tp - 1) + dt - 1,
                beside(dt),
            )
            copy.start()
            rt_moves.append(copy)

    def pass_on(k, which, place):
        span = pl.ds(k * per, per)
        for dt in range(1, n_tp):
            copy = send(
                rest_ref.at[place, span],
                rest_ref.at[place, span],
                (rt_s, rt_r),
                (k * 4 + which) * (n_tp - 1) + dt - 1,
                beside(dt),
            )
            copy.start()
            rt_moves.append(copy)

    onward = []
    for k in range(chunks):
        span = pl.ds(k * per, per)
        for j in range(2):
            r_moves[k][j].wait_recv()
        odd = lax.rem(core + k, 2)
        source = jnp.where(odd == 0, c ^ 1, c ^ 2) * n_tp + t
        target = (z, jnp.where(odd == 0, c ^ 2, c ^ 1), t)
        copy = send(
            rest_ref.at[source, span], rest_ref.at[source, span], (r_s, r_r), k * 3 + 2, target
        )
        copy.start()
        onward.append(copy)
        pass_on(k, 1, (c ^ 1) * n_tp + t)
        pass_on(k, 2, (c ^ 2) * n_tp + t)
    for k in range(chunks):
        onward[k].wait_recv()
        pass_on(k, 3, (c ^ 3) * n_tp + t)

    for copy in x_over:
        copy.wait()

    @pl.when(jnp.logical_not(stays))
    def left():
        x_moves[0].wait_send()

    x_moves[1].wait_send()
    for copy in (*za, *zb, *zc, *q_moves, *onward):
        copy.wait_send()
    for pair in r_moves:
        for copy in pair:
            copy.wait_send()
    for copy in (*qt_own, *qt_on, *rt_moves):
        copy.wait()
    first_own.wait()
    rest_own.wait()


def bring(slots, part, low, xs, n_shard, n_ctx, n_tp):
    held, rows, width = low.shape
    total_rows = part.shape[0]
    groups = n_ctx * n_tp
    mid = xs.shape[1]
    anywhere = pl.BlockSpec(memory_space=pl.ANY)
    dma = pltpu.SemaphoreType.DMA
    pairs = [2, 2, n_shard - 1, n_shard - 1, n_shard - 1, 3]
    pairs += [4 * (n_tp - 1), 9, 12 * (n_tp - 1)]
    sems = [dma((n,)) for n in pairs for _ in range(2)]
    return pl.pallas_call(
        functools.partial(bring_kernel, n_shard, n_ctx, n_tp),
        name="bring",
        in_specs=[
            pl.BlockSpec(memory_space=pltpu.SMEM),
            pl.BlockSpec(memory_space=pltpu.VMEM),
            anywhere,
            anywhere,
        ],
        out_specs=[anywhere, anywhere, anywhere],
        out_shape=[
            jax.ShapeDtypeStruct((4, mid, width), jnp.bfloat16),
            jax.ShapeDtypeStruct((groups, total_rows, width), jnp.bfloat16),
            jax.ShapeDtypeStruct((groups, 9, rows, width), jnp.bfloat16),
        ],
        scratch_shapes=[
            pltpu.VMEM((n_shard - 1, total_rows // n_shard, width), jnp.bfloat16),
            pltpu.VMEM((total_rows // n_shard, width), jnp.bfloat16),
            pltpu.VMEM((total_rows, width), jnp.bfloat16),
            pltpu.VMEM((n_shard * held, rows, width), jnp.bfloat16),
            pltpu.VMEM((9, rows, width), jnp.bfloat16),
            *sems,
            dma((3,)),
        ],
        compiler_params=pltpu.CompilerParams(
            collective_id=0, has_side_effects=True, vmem_limit_bytes=40 << 20
        ),
        cost_estimate=pl.CostEstimate(flops=0, bytes_accessed=40 << 20, transcendentals=0),
    )(slots, part, low, xs)


def back_kernel(
    n_ctx,
    n_tp,
    gh2_ref,
    hid_ref,
    gel_ref,
    fit_ref,
    gmt_ref,
    n1_ref,
    r1_ref,
    ctx_ref,
    small,
    up_w,
    down_w,
    wo,
    own_ref,
    x_ref,
    y_ref,
    xy_ref,
    gh1_ref,
    dctx_ref,
    sums_ref,
    gy,
    gu,
    grads,
    arrived,
    send_sem,
    recv_sem,
):
    z, c, t = place_of()
    step = pl.program_id(0)
    tokens, width = gh2_ref.shape
    tiles = tokens // TILE
    rows = own_ref.shape[1]
    others = n_tp - 1

    def beside(dt):
        return (z, c, lax.rem(t + dt, n_tp))

    @pl.when(step == 0)
    def start():
        barrier = pltpu.get_barrier_semaphore()
        for dt in range(1, n_tp):
            pl.semaphore_signal(barrier, inc=1, device_id=beside(dt), device_id_type=MESH)
        pl.semaphore_wait(barrier, others)
        sums_ref[...] = jnp.zeros_like(sums_ref)
        gy[...] = gh2_ref[...]

    def moves(b, count):
        slot = lax.rem(b, 2)
        return [
            send(
                grads.at[slot, :, lax.rem(t + dt, n_tp), 0:count],
                arrived.at[b, dt - 1, :, 0:count],
                (send_sem, recv_sem),
                b * others + dt - 1,
                beside(dt),
            )
            for dt in range(1, n_tp)
        ]

    def exchange(b, count):
        for copy in moves(b, count):
            copy.start()

    def keep(b, count):
        for copy in moves(b, count):
            copy.wait()
        slot = lax.rem(b, 2)
        for j, out in enumerate((own_ref, x_ref, y_ref, xy_ref)):
            for i in range(count):
                value = grads[slot, c ^ j, t, i]
                for dt in range(others):
                    value = value + arrived[b, dt, c ^ j, i]
                out[2 * b + i] = value

    def put(slot, i, value):
        low = value.astype(jnp.bfloat16)
        grads[slot, :, :, i] = low.reshape(n_ctx, n_tp, rows, width)

    @pl.when(step < 4)
    def ffn():
        up_block = matrix(up_w)
        down_block = matrix(down_w)
        slot = lax.rem(step, 2)

        def one(i, carry):
            at = pl.ds(pl.multiple_of(i * TILE, TILE), TILE)
            mixed = gh2_ref[at, :].astype(jnp.bfloat16)
            grad = wide_dot(mixed, down_block, NN) * gel_ref[0, at, :].astype(jnp.float32)
            low = grad.astype(jnp.bfloat16)
            gu[at, :] = low
            gy[at, :] += wide_dot(low, up_block, NT)
            sums_ref[pl.ds(step, 1), :] += jnp.sum(
                low.astype(jnp.float32), axis=0, keepdims=True
            )
            return carry

        lax.fori_loop(0, tiles, one, 0)
        put(slot, 0, wide_dot(fit_ref[...], gu[...], NN))
        put(slot, 1, wide_dot(gmt_ref[...], hid_ref[0], NN))
        exchange(step, 2)

    @pl.when(step > 0)
    def settle():
        keep(step - 1, 2)

    @pl.when(step == 4)
    def first_norm():
        def one(i, carry):
            at = pl.ds(pl.multiple_of(i * TILE, TILE), TILE)
            grad = gy[at, :]
            n1 = n1_ref[at, :]
            gh1 = norm_back(grad, n1, r1_ref[at, 0:1], small[3:4, :])
            gh1_ref[at, :] = gh1
            low = gh1.astype(jnp.bfloat16)
            gu[at, :] = low
            add_row(sums_ref, 4, low.astype(jnp.float32))
            add_row(sums_ref, 5, grad * n1)
            add_row(sums_ref, 6, grad)
            return carry

        lax.fori_loop(0, tiles, one, 0)
        put(0, 0, wide_dot(ctx_ref[...].T, gu[...], NN))
        exchange(4, 1)
        out_w = matrix(wo)

        def two(i, carry):
            at = pl.ds(pl.multiple_of(i * TILE, TILE), TILE)
            dctx_ref[at, :] = wide_dot(gu[at, :], out_w, NT).astype(jnp.bfloat16)
            return carry

        lax.fori_loop(0, tiles, two, 0)
        keep(4, 1)


def back(gh2, hid, gel, fit, gmt, n1, r1, ctx, small, rest, n_ctx, n_tp):
    tokens, width = gh2.shape
    rows = rest.shape[2]
    dma = pltpu.SemaphoreType.DMA

    def whole(shape):
        return pl.BlockSpec(shape, lambda b: (0,) * len(shape), pipeline_mode=pl.Buffered(1))

    def block(b):
        return (jnp.minimum(b, 3), 0, 0)

    def held(first, single=False):
        return pl.BlockSpec(
            (n_ctx * n_tp, 1, rows, width),
            (lambda b: (0, first, 0, 0))
            if single
            else (lambda b: (0, first + jnp.minimum(b, 3), 0, 0)),
            pipeline_mode=pl.Buffered(1) if single else None,
        )

    def out(shape):
        return pl.BlockSpec(shape, lambda b: (0,) * len(shape))

    return pl.pallas_call(
        functools.partial(back_kernel, n_ctx, n_tp),
        name="back",
        grid=(5,),
        in_specs=[
            whole((tokens, width)),
            pl.BlockSpec((1, tokens, width), block),
            pl.BlockSpec((1, tokens, width), block),
            whole((width, tokens)),
            whole((width, tokens)),
            whole((tokens, width)),
            whole((tokens, 128)),
            whole((tokens, width)),
            whole(small.shape),
            held(1),
            held(5),
            held(0, True),
        ],
        out_specs=[
            *[out((9, rows, width))] * 4,
            out((tokens, width)),
            out((tokens, width)),
            out((8, width)),
        ],
        out_shape=[
            *[bf16_of(9, rows, width)] * 4,
            f32_of(tokens, width),
            bf16_of(tokens, width),
            f32_of(8, width),
        ],
        scratch_shapes=[
            pltpu.VMEM((tokens, width), jnp.float32),
            pltpu.VMEM((tokens, width), jnp.bfloat16),
            pltpu.VMEM((2, n_ctx, n_tp, 2, rows, width), jnp.bfloat16),
            pltpu.VMEM((5, n_tp - 1, n_ctx, 2, rows, width), jnp.bfloat16),
            dma((5 * (n_tp - 1),)),
            dma((5 * (n_tp - 1),)),
        ],
        compiler_params=pltpu.CompilerParams(
            collective_id=3, has_side_effects=True, vmem_limit_bytes=62 << 20
        ),
        cost_estimate=pl.CostEstimate(
            flops=22_000_000_000, bytes_accessed=40 << 20, transcendentals=0
        ),
    )(gh2, hid, gel, fit, gmt, n1, r1, ctx, small, rest, rest, rest)


def late_kernel(
    n_ctx,
    n_tp,
    x_hbm,
    dq_hbm,
    dk_hbm,
    dv_hbm,
    gh1_hbm,
    first_hbm,
    small_ref,
    home_ref,
    rows_ref,
    total_ref,
    x_s,
    dq_s,
    dk_s,
    dv_s,
    gh1_s,
    first_s,
    flipped,
    grads,
    arrived,
    partial,
    met,
    over,
    more,
    back_s,
    small_s,
    small_t,
    small_p,
    in_sem,
    c_s,
    c_r,
    p_s,
    p_r,
    o_s,
    o_r,
    h_s,
    h_r,
    sc_s,
    sc_r,
    sp_s,
    sp_r,
    keep_sem,
):
    z, c, t = place_of()
    side, core, bit = t // 2, lax.rem(t, 2), lax.rem(c, 2)
    _, mid, width = x_s.shape
    tokens = 2 * mid
    rows = rows_ref.shape[1]
    groups = n_ctx * n_tp
    per = groups // 2
    band = width // 2
    tile = mid // 2

    loads = [
        pltpu.make_async_copy(src, dst, in_sem.at[i])
        for i, (src, dst) in enumerate(
            (
                (x_hbm, x_s),
                (dk_hbm, dk_s),
                (dv_hbm, dv_s),
                (dq_hbm, dq_s),
                (first_hbm, first_s),
                (gh1_hbm, gh1_s),
            )
        )
    ]
    for load in loads:
        load.start()

    def across(mask):
        return (z, c ^ mask, t)

    def beside(dt):
        return (z, c, lax.rem(t + dt, n_tp))

    barrier = pltpu.get_barrier_semaphore()
    friends = [(z, c ^ m, t) for m in range(1, n_ctx)]
    friends += [beside(dt) for dt in range(1, n_tp)]
    friends += [(z, c ^ m, t ^ 1) for m in range(1, n_ctx)]
    for friend in friends:
        pl.semaphore_signal(barrier, inc=1, device_id=friend, device_id_type=MESH)
    pl.semaphore_wait(barrier, len(friends))

    core_moves = []

    def exchange(m):
        for dt in range(1, n_tp):
            other = lax.rem(t + dt, n_tp)
            for k in range(n_ctx):
                copy = send(
                    grads.at[k * n_tp + other, m],
                    arrived.at[dt - 1, k, m],
                    (c_s, c_r),
                    ((dt - 1) * n_ctx + k) * 3 + m,
                    beside(dt),
                )
                copy.start()
                core_moves.append((m, copy))

    plane_moves = []

    def meet(m):
        for which, copy in core_moves:
            if which == m:
                copy.wait_recv()
        for k in range(n_ctx):
            value = grads[k * n_tp + t, m]
            for dt in range(1, n_tp):
                value = value + arrived[dt - 1, k, m]
            partial[k, m] = value
        for j in range(1, n_ctx):
            copy = send(
                partial.at[c ^ j, m], met.at[j - 1, m], (p_s, p_r), (j - 1) * 3 + m, across(j)
            )
            copy.start()
            plane_moves.append(copy)

    loads[0].wait()
    for a in range(4):
        own = 1 if a < 2 else 0
        chunk = 2 * (core if own else 1 - core) + ((a % 2) ^ bit)
        flipped[:, pl.ds(pl.multiple_of(chunk * mid, mid), mid)] = x_s[a].T

    mine = pl.ds(pl.multiple_of(core * tokens, tokens), tokens)
    def weight_grad(m, left_at, right):
        def one(i, carry):
            left = flipped[pl.ds(pl.multiple_of(i * band, band), band), left_at]
            value = wide_dot(left, right[...], NN).astype(jnp.bfloat16)
            grads[pl.ds(i * per, per), m] = value.reshape(per, rows, width)
            return carry

        lax.fori_loop(0, 2, one, 0)

    loads[1].wait()
    weight_grad(1, slice(None), dk_s)
    exchange(1)
    loads[2].wait()
    weight_grad(2, slice(None), dv_s)
    exchange(2)
    meet(1)
    loads[3].wait()
    weight_grad(0, mine, dq_s)
    exchange(0)
    meet(2)

    row = lax.broadcasted_iota(jnp.int32, small_ref.shape, 0)
    q_sum = jnp.sum(dq_s[...].astype(jnp.float32), axis=0, keepdims=True)
    v_sum = jnp.sum(dv_s[...].astype(jnp.float32), axis=0, keepdims=True)
    sums = jnp.where(row == 0, q_sum, jnp.where(row == 1, v_sum, small_ref[...]))
    small_s[...] = sums.astype(jnp.bfloat16)
    small_core = [
        send(small_s, small_t.at[dt - 1], (sc_s, sc_r), dt - 1, beside(dt)) for dt in range(1, n_tp)
    ]
    for copy in small_core:
        copy.start()

    loads[4].wait()

    def weight(m):
        return first_s[:, m * rows : (m + 1) * rows, :].reshape(width, width)

    wq, wk, wv = weight(0), weight(1), weight(2)
    over_moves = []
    for b in range(2):
        at = pl.ds(pl.multiple_of((1 - core) * tokens + b * mid, mid), mid)
        value = wide_dot(dk_s[at, :], wk, NT) + wide_dot(dv_s[at, :], wv, NT)
        over[b] = value.astype(jnp.bfloat16)
        copy = send(over.at[b], more.at[b], (o_s, o_r), b, (z, c, t ^ 1))
        copy.start()
        over_moves.append(copy)

    meet(0)
    value = small_s[...]
    for dt, copy in enumerate(small_core):
        copy.wait_recv()
        value = value + small_t[dt]
    total_ref[...] = value
    small_plane = [
        send(total_ref, small_p.at[j - 1], (sp_s, sp_r), j - 1, across(j)) for j in range(1, n_ctx)
    ]
    for copy in small_plane:
        copy.start()

    loads[5].wait()
    stays = c // 2 == core
    home_moves = []
    for copy in over_moves:
        copy.wait_recv()
    for move in range(2):
        chunk = move ^ bit
        for i in range(2):
            at = pl.ds(pl.multiple_of(core * tokens + chunk * mid + i * tile, tile), tile)
            here = pl.ds(pl.multiple_of(chunk * mid + i * tile, tile), tile)
            value = gh1_s[here, :]
            value = value + more[chunk, i * tile : (i + 1) * tile, :].astype(jnp.float32)
            value = value + wide_dot(dq_s[here, :], wq, NT)
            value = value + wide_dot(dk_s[at, :], wk, NT)
            value = value + wide_dot(dv_s[at, :], wv, NT)
            back_s[move, i * tile : (i + 1) * tile, :] = value.astype(jnp.bfloat16)
        target = (z, 2 * core + chunk, 2 * side + c // 2)
        home_moves.append(send(back_s.at[move], home_ref.at[move], (h_s, h_r), move, target))
        if move == 0:
            keep = pltpu.make_async_copy(back_s.at[0], home_ref.at[0], keep_sem.at[0])

            @pl.when(stays)
            def kept():
                keep.start()

            @pl.when(jnp.logical_not(stays))
            def left():
                home_moves[0].start()

        else:
            home_moves[1].start()

    for copy in plane_moves:
        copy.wait_recv()
    for m in range(3):
        value = partial[c, m]
        for j in range(n_ctx - 1):
            value = value + met[j, m]
        rows_ref[m] = value
    value = total_ref[...]
    for j, copy in enumerate(small_plane):
        copy.wait()
        value = value + small_p[j]
    total_ref[...] = value

    @pl.when(stays)
    def done():
        keep.wait()

    @pl.when(jnp.logical_not(stays))
    def gone():
        home_moves[0].wait()

    home_moves[1].wait()
    for _, copy in core_moves:
        copy.wait_send()
    for copy in (*plane_moves, *over_moves, *small_core):
        copy.wait_send()


def late(x_all, dq, dk, dv, gh1, first, small, rows, n_ctx, n_tp):
    _, mid, width = x_all.shape
    groups = n_ctx * n_tp
    anywhere = pl.BlockSpec(memory_space=pl.ANY)
    vmem = pl.BlockSpec(memory_space=pltpu.VMEM)
    dma = pltpu.SemaphoreType.DMA
    low = jnp.bfloat16
    pairs = [3 * n_ctx * (n_tp - 1), 3 * (n_ctx - 1), 2, 2, n_tp - 1, n_ctx - 1]
    return pl.pallas_call(
        functools.partial(late_kernel, n_ctx, n_tp),
        name="late",
        in_specs=[anywhere] * 6 + [vmem],
        out_specs=[anywhere, vmem, vmem],
        out_shape=[
            bf16_of(2, mid, width),
            bf16_of(3, rows, width),
            bf16_of(*small.shape),
        ],
        scratch_shapes=[
            pltpu.VMEM(x_all.shape, low),
            pltpu.VMEM(dq.shape, low),
            pltpu.VMEM(dk.shape, low),
            pltpu.VMEM(dv.shape, low),
            pltpu.VMEM(gh1.shape, jnp.float32),
            pltpu.VMEM(first.shape, low),
            pltpu.VMEM((width, 4 * mid), low),
            pltpu.VMEM((groups, 3, rows, width), low),
            pltpu.VMEM((n_tp - 1, n_ctx, 3, rows, width), low),
            pltpu.VMEM((n_ctx, 3, rows, width), low),
            pltpu.VMEM((n_ctx - 1, 3, rows, width), low),
            pltpu.VMEM((2, mid, width), low),
            pltpu.VMEM((2, mid, width), low),
            pltpu.VMEM((2, mid, width), low),
            pltpu.VMEM(small.shape, low),
            pltpu.VMEM((n_tp - 1, *small.shape), low),
            pltpu.VMEM((n_ctx - 1, *small.shape), low),
            dma((6,)),
            *[dma((n,)) for n in pairs for _ in range(2)],
            dma((1,)),
        ],
        compiler_params=pltpu.CompilerParams(
            collective_id=1, has_side_effects=True, vmem_limit_bytes=60 << 20
        ),
        cost_estimate=pl.CostEstimate(
            flops=12_000_000_000, bytes_accessed=30 << 20, transcendentals=0
        ),
    )(x_all, dq, dk, dv, gh1, first, small)


def adam_update(weight, first, second, grad, decay, rate):
    count = float(STEP)
    first_new = beta_one * first + (1.0 - beta_one) * grad
    second_new = beta_two * second + (1.0 - beta_two) * grad * grad
    first_hat = first_new / (1.0 - beta_one**count)
    second_hat = second_new / (1.0 - beta_two**count)
    weight_new = weight - rate * (first_hat / (jnp.sqrt(second_hat) + adam_eps) + decay * weight)
    return (weight_new, first_new, second_new)


def owner_kernel(
    n_shard,
    holder,
    own_ref,
    x_ref,
    y_ref,
    xy_ref,
    late_ref,
    small_ref,
    w_ref,
    one_ref,
    two_ref,
    w_out,
    one_out,
    two_out,
    small_out,
    every,
    packed,
    met,
    small_met,
    z_s,
    z_r,
    s_s,
    s_r,
):
    z, c, t = place_of()
    held = w_ref.shape[0]

    def far(dz):
        return (lax.rem(z + dz, n_shard), c, t)

    barrier = pltpu.get_barrier_semaphore()
    for dz in range(1, n_shard):
        pl.semaphore_signal(barrier, inc=1, device_id=far(dz), device_id_type=MESH)
    every[0:3] = late_ref[...]
    every[3:12] = own_ref[...] + x_ref[...] + y_ref[...] + xy_ref[...]
    every[12] = jnp.zeros_like(every[12])
    for s in range(n_shard * held):
        packed[s // held, s % held] = every[holder[s]]
    pl.semaphore_wait(barrier, n_shard - 1)
    moves = [
        send(packed.at[far(dz)[0]], met.at[dz - 1], (z_s, z_r), dz - 1, far(dz))
        for dz in range(1, n_shard)
    ]
    moves += [
        send(small_ref, small_met.at[dz - 1], (s_s, s_r), dz - 1, far(dz))
        for dz in range(1, n_shard)
    ]
    for copy in moves:
        copy.start()
    for copy in moves:
        copy.wait()
    for j in range(held):
        grad = packed[z, j].astype(jnp.float32)
        for dz in range(n_shard - 1):
            grad = grad + met[dz, j].astype(jnp.float32)
        w, one, two = adam_update(w_ref[j], one_ref[j], two_ref[j], grad, 0.01, rate_value)
        w_out[j] = w
        one_out[j] = one
        two_out[j] = two
    total = small_ref[...].astype(jnp.float32)
    for dz in range(n_shard - 1):
        total = total + small_met[dz].astype(jnp.float32)
    small_out[...] = total


def owner(holder, early, late_rows, small, master, one, two, n_shard):
    held, rows, width = master.shape
    vmem = pl.BlockSpec(memory_space=pltpu.VMEM)
    dma = pltpu.SemaphoreType.DMA
    return pl.pallas_call(
        functools.partial(owner_kernel, n_shard),
        name="owner",
        in_specs=[pl.BlockSpec(memory_space=pltpu.SMEM)] + [vmem] * 9,
        out_specs=[vmem] * 4,
        out_shape=[f32_of(held, rows, width)] * 3 + [f32_of(*small.shape)],
        scratch_shapes=[
            pltpu.VMEM((13, rows, width), jnp.bfloat16),
            pltpu.VMEM((n_shard, held, rows, width), jnp.bfloat16),
            pltpu.VMEM((n_shard - 1, held, rows, width), jnp.bfloat16),
            pltpu.VMEM((n_shard - 1, *small.shape), jnp.bfloat16),
            *[dma((n_shard - 1,)) for _ in range(4)],
        ],
        compiler_params=pltpu.CompilerParams(
            collective_id=2, has_side_effects=True, vmem_limit_bytes=40 << 20
        ),
        cost_estimate=pl.CostEstimate(flops=0, bytes_accessed=12 << 20, transcendentals=0),
    )(holder, *early, late_rows, small, master, one, two)


def moves(n_ctx, n_tp, pick):
    pairs = []
    for c in range(n_ctx):
        for t in range(n_tp):
            side, core = t // 2, t % 2
            to_ctx = 2 * core + (pick ^ (c & 1))
            to_tp = 2 * side + c // 2
            pairs.append((c * n_tp + t, to_ctx * n_tp + to_tp))
    return pairs


def shards(
    inputs,
    cotangent,
    rand_blocks,
    slot_of,
    master,
    moment_one,
    moment_two,
    small_params,
    small_one,
    small_two,
):
    n_shard = lax.axis_size("shard")
    n_ctx = lax.axis_size("ctx")
    n_tp = lax.axis_size("tp")
    groups = n_ctx * n_tp
    held, rows, width = master.shape
    span = small_params.shape[0]
    my_ctx = lax.axis_index("ctx")
    my_tp = lax.axis_index("tp")
    parity = lax.rem(my_ctx, 2)
    half = lax.rem(my_tp, 2)
    plane = ("ctx", "tp")
    forth = [moves(n_ctx, n_tp, pick) for pick in range(2)]
    home = [[(b, a) for a, b in pairs] for pairs in forth]
    swap = [(t, t ^ 1) for t in range(n_tp)]

    arrival = [(b ^ parity) + 2 * (half ^ (j // 2)) for j, b in enumerate((0, 1, 0, 1))]
    info = jnp.stack([half, *arrival]).astype(jnp.int32)
    half_one = info[:1]

    def sent(field, pick):
        low = field.astype(jnp.bfloat16)
        return jnp.where(parity == 0, low[pick], low[1 - pick])

    def returned(first, second):
        swapped = parity == 1
        out = jnp.stack(
            [jnp.where(swapped, second, first), jnp.where(swapped, first, second)]
        )
        return out.astype(jnp.float32)

    low = master.astype(jnp.bfloat16)
    my_shard = lax.axis_index("shard")
    mine = my_shard * held + jnp.arange(held, dtype=jnp.int32)
    zero = jnp.zeros_like(low)
    parts = [
        jnp.sum(jnp.where((slot_of[m] == mine)[:, None, None], low, zero), axis=0, dtype=jnp.float32)
        for m in range(3)
    ]
    spread = (jnp.arange(n_shard) == my_shard)[:, None]
    small_part = jnp.where(spread, small_params[None, :], 0.0).reshape(-1)
    used = 3 * rows * width + n_shard * span
    total_rows = -(-used // (width * 16 * n_shard)) * 16 * n_shard
    small_part = jnp.pad(small_part, (0, total_rows * width - used)).reshape(-1, width)
    part = jnp.concatenate([*parts, small_part]).astype(jnp.bfloat16)
    xs = jnp.stack([sent(inputs, pick) for pick in range(2)])
    x_all, first, rest = bring(slot_of, part, low, xs, n_shard, n_ctx, n_tp)
    small = first[:, 3 * rows :, :].reshape(groups, -1)[:, : n_shard * span]
    small = small.reshape(groups, n_shard, span).transpose(1, 0, 2)
    small = small.reshape(-1, width).astype(jnp.float32)

    cots, x_all = lax.optimization_barrier(
        ([sent(cotangent, pick) for pick in range(2)], x_all)
    )
    cot = jnp.stack([lax.ppermute(cots[pick], plane, forth[pick]) for pick in range(2)])

    q, k, v = project(info, x_all, small, first, rows)
    context, lse = attend(half_one, rand_blocks, q, k, v, 5)
    out_low, n1, r1, fi, fit, hid, gel, gh2, gmt, sums_two = front(
        info, context, x_all, cot, small, rest
    )
    layer_out = returned(*[lax.ppermute(out_low[p], plane, home[p]) for p in range(2)])
    *early, gh1, dctx, sums_one = back(
        gh2, hid, gel, fit, gmt, n1, r1, context, small, rest, n_ctx, n_tp
    )
    for j in range(1, n_ctx):
        crossing = [
            (a * n_tp + b, (a ^ j) * n_tp + b) for a in range(n_ctx) for b in range(n_tp)
        ]
        early[j] = lax.ppermute(early[j], plane, crossing)
    layer_out, dctx = lax.optimization_barrier((layer_out, dctx))
    dq, dk, dv = attend_back(half_one, rand_blocks, q, k, v, lse, dctx, 5)
    small_rows = jnp.pad(
        jnp.concatenate([sums_one[4:7], sums_one[0:4], sums_two[0:3]]), ((2, 4), (0, 0))
    )
    came, late_rows, small_late = late(
        x_all, dq, dk, dv, gh1, first, small_rows, rows, n_ctx, n_tp
    )
    input_grad = returned(came[0], came[1])

    stands = jnp.array([0, 1, 2, 11, 3, 5, 7, 9, 4, 6, 8, 10], jnp.int32)
    slots_all = jnp.arange(n_shard * held, dtype=jnp.int32)
    holder = 12 + jnp.sum(
        jnp.where(slot_of[None, :] == slots_all[:, None], stands[None, :] - 12, 0), axis=1
    )
    master_new, first_new, second_new, small_sum = owner(
        holder.astype(jnp.int32), early, late_rows, small_late, master, moment_one, moment_two, n_shard
    )
    start = ((my_shard * n_ctx + my_ctx) * n_tp + my_tp) * span
    small_owned = lax.dynamic_slice_in_dim(small_sum.reshape(-1), start, span)
    small_new, small_first, small_second = adam_update(
        small_params, small_one, small_two, small_owned, 0.0, small_rate
    )
    return (
        layer_out,
        input_grad,
        master_new,
        first_new,
        second_new,
        small_new,
        small_first,
        small_second,
    )


def solution(mesh):
    tokens = P(("shard", "tp"), "ctx", None)
    stored = P("shard", ("ctx", "tp"), None)
    spread = P(("shard", "ctx", "tp"))
    return jax.shard_map(
        shards,
        mesh=mesh,
        in_specs=(tokens, tokens, P(), P(), stored, stored, stored, spread, spread, spread),
        out_specs=(tokens, tokens, stored, stored, stored, spread, spread, spread),
        check_vma=False,
    )
```

```python
import functools

import jax
import jax.numpy as jnp
from jax import lax
from jax.experimental import pallas as pl
from jax.experimental.pallas import tpu as pltpu
from jax.sharding import PartitionSpec as P

STEP = 5
norm_eps = 1e-12
beta_one = 0.9
beta_two = 0.999
adam_eps = 1e-08
rate_value = 0.04
small_rate = 0.25
score_scale = 0.125
gelu_root = 0.7978845608
gelu_cube = 0.044715

BLOCK = 64
HEAD = 64
PACK = 4
masked_score = -1e30


def wide_dot(a, b, dims):
    return lax.dot_general(a, b, (dims, ((), ())), preferred_element_type=jnp.float32)


def head_masks(rows):
    lane = lax.broadcasted_iota(jnp.int32, (rows, PACK * HEAD), 1) // HEAD
    return [lane == h for h in range(PACK)]


def spread_heads(block, masks):
    zero = jnp.zeros_like(block)
    return jnp.concatenate([jnp.where(m, block, zero) for m in masks], axis=0)


def own_heads(full, masks):
    total = None
    for h, m in enumerate(masks):
        piece = jnp.where(m, full[h * BLOCK : (h + 1) * BLOCK], 0.0)
        total = piece if total is None else total + piece
    return total


def rows_of(ref, index, count=1):
    return ref[pl.ds(pl.multiple_of(index * BLOCK, BLOCK), count * BLOCK), :]


def picked_rows(ref, picks, low_half):
    halves = []
    for pair in range(PACK // 2):
        cols = pl.ds(pair * 2 * HEAD, 2 * HEAD)
        first = ref[pl.ds(pl.multiple_of(picks[2 * pair] * BLOCK, BLOCK), BLOCK), cols]
        second = ref[pl.ds(pl.multiple_of(picks[2 * pair + 1] * BLOCK, BLOCK), BLOCK), cols]
        halves.append(jnp.where(low_half, first, second))
    return jnp.concatenate(halves, axis=1)


def gathered(ref, block, last, picks, low_half):
    pieces = [rows_of(ref, 0), rows_of(ref, last), rows_of(ref, block - 1, 3)]
    pieces += [picked_rows(ref, p, low_half) for p in picks]
    return jnp.concatenate(pieces, axis=0)


def middle_scores(keys, spread, block, last):
    scores = wide_dot(keys, spread, ((1,), (1,)))
    first_off = jnp.where(block == 1, masked_score, 0.0)
    last_off = jnp.where(block == last - 1, masked_score, 0.0)
    b = BLOCK
    return jnp.concatenate(
        [
            scores[: 2 * b],
            scores[2 * b : 3 * b] + first_off,
            scores[3 * b : 4 * b],
            scores[4 * b : 5 * b] + last_off,
            scores[5 * b :],
        ],
        axis=0,
    )


def attend_kernel(unroll, half_ref, table_ref, q_ref, k_ref, v_ref, out_ref, lse_ref, kept):
    half = half_ref[0]
    group = pl.program_id(0)
    nblocks = k_ref.shape[0] // BLOCK
    local = q_ref.shape[0] // BLOCK
    last = nblocks - 1
    picks_each = table_ref.shape[2]
    masks = head_masks(BLOCK)
    low_half = lax.broadcasted_iota(jnp.int32, (BLOCK, 2 * HEAD), 1) < HEAD

    def middle(step, carry):
        mine = step + 1 - half
        block = mine + local * half
        picks = [
            [table_ref[group * PACK + h, block - 1, r] for h in range(PACK)]
            for r in range(picks_each)
        ]
        spread = spread_heads(rows_of(q_ref, mine), masks)
        keys = gathered(k_ref, block, last, picks, low_half)
        values = gathered(v_ref, block, last, picks, low_half)
        scores = middle_scores(keys, spread, block, last)
        top = jnp.max(scores, axis=0, keepdims=True)
        probs = jnp.exp(scores - top)
        total = jnp.sum(probs, axis=0, keepdims=True)
        low = (probs * (1.0 / total)).astype(jnp.bfloat16)
        full = wide_dot(low, values, ((0,), (0,)))
        out_ref[pl.ds(pl.multiple_of(mine * BLOCK, BLOCK), BLOCK), :] = own_heads(
            full, masks
        ).astype(jnp.bfloat16)
        lse_ref[0, pl.ds(mine, 1), :] = top + jnp.log(total)
        return carry

    lax.fori_loop(0, local - 1, middle, 0, unroll=unroll)

    edge = (local - 1) * half
    spread = spread_heads(rows_of(q_ref, edge), masks)
    span = 8 * BLOCK
    chunks = nblocks // 8
    top = None
    for c in range(chunks):
        scores = wide_dot(k_ref[c * span : (c + 1) * span, :], spread, ((1,), (1,)))
        kept[c * span : (c + 1) * span, :] = scores
        high = jnp.max(scores, axis=0, keepdims=True)
        top = high if top is None else jnp.maximum(top, high)
    total = None
    for c in range(chunks):
        probs = jnp.exp(kept[c * span : (c + 1) * span, :] - top)
        kept[c * span : (c + 1) * span, :] = probs
        part = jnp.sum(probs, axis=0, keepdims=True)
        total = part if total is None else total + part
    scale = 1.0 / total
    full = None
    for c in range(chunks):
        low = (kept[c * span : (c + 1) * span, :] * scale).astype(jnp.bfloat16)
        part = wide_dot(low, v_ref[c * span : (c + 1) * span, :], ((0,), (0,)))
        full = part if full is None else full + part
    out_ref[pl.ds(pl.multiple_of(edge * BLOCK, BLOCK), BLOCK), :] = own_heads(
        full, masks
    ).astype(jnp.bfloat16)
    lse_ref[0, pl.ds(edge, 1), :] = top + jnp.log(total)


def attend(half, table, q, k, v, unroll=3):
    tokens, width = q.shape
    seq = k.shape[0]
    lanes = PACK * HEAD
    groups = width // lanes
    blocks = tokens // BLOCK
    spec = pltpu.PrefetchScalarGridSpec(
        num_scalar_prefetch=2,
        grid=(groups,),
        in_specs=[
            pl.BlockSpec((tokens, lanes), lambda g, *_: (0, g)),
            pl.BlockSpec((seq, lanes), lambda g, *_: (0, g)),
            pl.BlockSpec((seq, lanes), lambda g, *_: (0, g)),
        ],
        out_specs=[
            pl.BlockSpec((tokens, lanes), lambda g, *_: (0, g)),
            pl.BlockSpec((1, blocks, lanes), lambda g, *_: (g, 0, 0)),
        ],
        scratch_shapes=[pltpu.VMEM((seq, lanes), jnp.float32)],
    )
    return pl.pallas_call(
        functools.partial(attend_kernel, unroll),
        grid_spec=spec,
        out_shape=[
            jax.ShapeDtypeStruct((tokens, width), jnp.bfloat16),
            jax.ShapeDtypeStruct((groups, blocks, lanes), jnp.float32),
        ],
        name="attend",
        compiler_params=pltpu.CompilerParams(vmem_limit_bytes=56 << 20),
        cost_estimate=pl.CostEstimate(
            flops=60_000_000_000, bytes_accessed=12 << 20, transcendentals=16_000_000
        ),
    )(half, table, q, k, v)


def attend_back_kernel(
    unroll,
    half_ref,
    table_ref,
    q_ref,
    k_ref,
    v_ref,
    lse_ref,
    do_ref,
    dq_ref,
    dk_ref,
    dv_ref,
    dk_acc,
    dv_acc,
    kept_p,
    kept_g,
):
    half = half_ref[0]
    group = pl.program_id(0)
    nblocks = k_ref.shape[0] // BLOCK
    local = q_ref.shape[0] // BLOCK
    last = nblocks - 1
    picks_each = table_ref.shape[2]
    masks = head_masks(BLOCK)
    low_half = lax.broadcasted_iota(jnp.int32, (BLOCK, 2 * HEAD), 1) < HEAD
    span = 8 * BLOCK
    chunks = nblocks // 8

    edge = (local - 1) * half
    spread = spread_heads(rows_of(q_ref, edge), masks)
    spread_do = spread_heads(rows_of(do_ref, edge), masks)
    lse = lse_ref[0, pl.ds(edge, 1), :]
    delta = None
    for c in range(chunks):
        rows = slice(c * span, (c + 1) * span)
        probs = jnp.exp(wide_dot(k_ref[rows, :], spread, ((1,), (1,))) - lse)
        gp = wide_dot(v_ref[rows, :], spread_do, ((1,), (1,)))
        kept_p[rows, :] = probs
        kept_g[rows, :] = gp
        part = jnp.sum(probs * gp, axis=0, keepdims=True)
        delta = part if delta is None else delta + part
    full = None
    for c in range(chunks):
        rows = slice(c * span, (c + 1) * span)
        probs = kept_p[rows, :]
        ds = (probs * (kept_g[rows, :] - delta)).astype(jnp.bfloat16)
        dv_acc[rows, :] = wide_dot(probs.astype(jnp.bfloat16), spread_do, ((1,), (0,)))
        dk_acc[rows, :] = wide_dot(ds, spread, ((1,), (0,)))
        part = wide_dot(ds, k_ref[rows, :], ((0,), (0,)))
        full = part if full is None else full + part
    dq_ref[pl.ds(pl.multiple_of(edge * BLOCK, BLOCK), BLOCK), :] = (
        own_heads(full, masks) * 0.125
    ).astype(jnp.bfloat16)

    def scatter(acc, piece, block, picks):
        b = BLOCK
        acc[0:b, :] += piece[:b]
        acc[last * b : (last + 1) * b, :] += piece[b : 2 * b]
        window = pl.ds(pl.multiple_of((block - 1) * b, b), 3 * b)
        acc[window, :] += piece[2 * b : 5 * b]
        for r, p in enumerate(picks):
            part = piece[(5 + r) * b : (6 + r) * b]
            for pair in range(PACK // 2):
                lanes = slice(pair * 2 * HEAD, (pair + 1) * 2 * HEAD)
                cols = pl.ds(pair * 2 * HEAD, 2 * HEAD)
                sub = part[:, lanes]
                acc[pl.ds(pl.multiple_of(p[2 * pair] * b, b), b), cols] += jnp.where(
                    low_half, sub, 0.0
                )
                acc[pl.ds(pl.multiple_of(p[2 * pair + 1] * b, b), b), cols] += jnp.where(
                    low_half, 0.0, sub
                )

    def middle(step, carry):
        mine = step + 1 - half
        block = mine + local * half
        picks = [
            [table_ref[group * PACK + h, block - 1, r] for h in range(PACK)]
            for r in range(picks_each)
        ]
        spread = spread_heads(rows_of(q_ref, mine), masks)
        spread_do = spread_heads(rows_of(do_ref, mine), masks)
        keys = gathered(k_ref, block, last, picks, low_half)
        values = gathered(v_ref, block, last, picks, low_half)
        scores = middle_scores(keys, spread, block, last)
        probs = jnp.exp(scores - lse_ref[0, pl.ds(mine, 1), :])
        gp = wide_dot(values, spread_do, ((1,), (1,)))
        delta = jnp.sum(probs * gp, axis=0, keepdims=True)
        ds = (probs * (gp - delta)).astype(jnp.bfloat16)
        low = probs.astype(jnp.bfloat16)
        scatter(dv_acc, wide_dot(low, spread_do, ((1,), (0,))), block, picks)
        scatter(dk_acc, wide_dot(ds, spread, ((1,), (0,))), block, picks)
        full = wide_dot(ds, keys, ((0,), (0,)))
        dq_ref[pl.ds(pl.multiple_of(mine * BLOCK, BLOCK), BLOCK), :] = (
            own_heads(full, masks) * 0.125
        ).astype(jnp.bfloat16)
        return carry

    lax.fori_loop(0, local - 1, middle, 0, unroll=unroll)
    dk_ref[...] = dk_acc[...].astype(jnp.bfloat16)
    dv_ref[...] = dv_acc[...].astype(jnp.bfloat16)


def attend_back(half, table, q, k, v, lse, do, unroll=3):
    tokens, width = q.shape
    seq = k.shape[0]
    lanes = PACK * HEAD
    groups = width // lanes
    blocks = tokens // BLOCK
    mine = pl.BlockSpec((tokens, lanes), lambda g, *_: (0, g))
    whole = pl.BlockSpec((seq, lanes), lambda g, *_: (0, g))
    spec = pltpu.PrefetchScalarGridSpec(
        num_scalar_prefetch=2,
        grid=(groups,),
        in_specs=[
            mine,
            whole,
            whole,
            pl.BlockSpec((1, blocks, lanes), lambda g, *_: (g, 0, 0)),
            mine,
        ],
        out_specs=[mine, whole, whole],
        scratch_shapes=[pltpu.VMEM((seq, lanes), jnp.float32)] * 4,
    )
    return pl.pallas_call(
        functools.partial(attend_back_kernel, unroll),
        grid_spec=spec,
        out_shape=[
            jax.ShapeDtypeStruct((tokens, width), jnp.bfloat16),
            jax.ShapeDtypeStruct((seq, width), jnp.bfloat16),
            jax.ShapeDtypeStruct((seq, width), jnp.bfloat16),
        ],
        name="attend_back",
        compiler_params=pltpu.CompilerParams(vmem_limit_bytes=56 << 20),
        cost_estimate=pl.CostEstimate(
            flops=120_000_000_000, bytes_accessed=24 << 20, transcendentals=16_000_000
        ),
    )(half, table, q, k, v, lse, do)


TILE = 256
MID = 512


def cols_mean(value):
    return jnp.mean(value, axis=-1, keepdims=True)


def normed(field):
    centred = field - cols_mean(field)
    rate = lax.rsqrt(cols_mean(centred * centred) + norm_eps)
    return centred * rate, rate


def norm_back(cot, normal, rate, gain):
    dn = cot * gain
    return rate * (dn - cols_mean(dn) - normal * cols_mean(dn * normal))


def matrix(ref):
    value = ref[...]
    return value.reshape(-1, value.shape[-1])


def add_row(ref, row, value):
    ref[row : row + 1, :] += jnp.sum(value, axis=0, keepdims=True)


def first_spec(first, rows, which):
    groups, _, width = first.shape
    return pl.BlockSpec(
        (groups, rows, width), lambda step, info: (0, which, 0), pipeline_mode=pl.Buffered(1)
    )


def rest_spec(rest, which, single=True):
    groups, _, rows, width = rest.shape
    mode = pl.Buffered(1) if single else None
    return pl.BlockSpec(
        (groups, 1, rows, width), lambda step, info: (0, which(step) - 3, 0, 0), pipeline_mode=mode
    )


def fixed(shape):
    return pl.BlockSpec(shape, lambda step, info: (0,) * len(shape), pipeline_mode=pl.Buffered(1))


def resident(shape):
    return pl.BlockSpec(shape, lambda step, info: (0,) * len(shape))


def call(kernel, name, info, grid, in_specs, out_specs, out_shape, scratch, args, flops, moved):
    return pl.pallas_call(
        kernel,
        name=name,
        grid_spec=pltpu.PrefetchScalarGridSpec(
            num_scalar_prefetch=1,
            grid=(grid,),
            in_specs=in_specs,
            out_specs=out_specs,
            scratch_shapes=scratch,
        ),
        out_shape=out_shape,
        compiler_params=pltpu.CompilerParams(vmem_limit_bytes=60 << 20),
        cost_estimate=pl.CostEstimate(
            flops=flops, bytes_accessed=moved, transcendentals=0
        ),
    )(info, *args)


def bf16_of(*shape):
    return jax.ShapeDtypeStruct(shape, jnp.bfloat16)


def f32_of(*shape):
    return jax.ShapeDtypeStruct(shape, jnp.float32)


NN = ((1,), (0,))
NT = ((1,), (1,))
TN = ((0,), (0,))


def project_kernel(info, x_ref, small, wq, wk, wv, q_ref, k_ref, v_ref):
    x = x_ref[0]

    @pl.when(pl.program_id(0) < 2)
    def own():
        q = wide_dot(x, matrix(wq), NN) + small[0:1, :]
        q_ref[...] = q.astype(jnp.bfloat16) * jnp.bfloat16(score_scale)

    k_ref[...] = wide_dot(x, matrix(wk), NN).astype(jnp.bfloat16)
    v_ref[...] = (wide_dot(x, matrix(wv), NN) + small[1:2, :]).astype(jnp.bfloat16)


def project(info, x_all, small, first, rows):
    _, mid, width = x_all.shape

    def chunk(step, info):
        return lax.rem(step + 2 * info[0], 4)

    return call(
        project_kernel,
        "project",
        info,
        4,
        [
            pl.BlockSpec((1, mid, width), lambda g, info: (info[1 + chunk(g, info)], 0, 0)),
            fixed(small.shape),
            *[first_spec(first, rows, m) for m in range(3)],
        ],
        [
            pl.BlockSpec((mid, width), lambda g, info: (jnp.minimum(g, 1), 0)),
            pl.BlockSpec((mid, width), lambda g, info: (chunk(g, info), 0)),
            pl.BlockSpec((mid, width), lambda g, info: (chunk(g, info), 0)),
        ],
        [bf16_of(2 * mid, width), bf16_of(4 * mid, width), bf16_of(4 * mid, width)],
        [],
        (x_all, small, first, first, first),
        6_000_000_000,
        16 << 20,
    )


def front_kernel(
    info,
    ctx_ref,
    x_ref,
    cot_ref,
    small,
    wo,
    u0,
    u1,
    u2,
    u3,
    v0,
    v1,
    v2,
    v3,
    out_ref,
    n1_ref,
    r1_ref,
    fi_ref,
    fit_ref,
    hid_ref,
    gel_ref,
    gh2_ref,
    gmt_ref,
    sums_ref,
):
    attn_out = wide_dot(ctx_ref[...], matrix(wo), NN) + small[2:3, :]
    n1, r1 = normed(x_ref[0].astype(jnp.float32) + attn_out)
    n1_ref[...] = n1
    r1_ref[...] = jnp.broadcast_to(r1, r1_ref.shape)
    after = n1 * small[3:4, :] + small[4:5, :]
    ffn_in = after.astype(jnp.bfloat16)
    fi_ref[...] = ffn_in
    fit_ref[...] = ffn_in.T
    total = after + small[9:10, :]
    for b, (up_w, down_w) in enumerate(((u0, v0), (u1, v1), (u2, v2), (u3, v3))):
        up = wide_dot(ffn_in, matrix(up_w), NN) + small[5 + b : 6 + b, :]
        square = up * up
        bent = jnp.tanh(gelu_root * up * (1.0 + gelu_cube * square))
        rise = 0.5 * (1.0 + bent)
        hidden = (up * rise).astype(jnp.bfloat16)
        hid_ref[b] = hidden
        slope = rise + (0.5 * gelu_root) * up * (1.0 - bent * bent) * (
            1.0 + (3.0 * gelu_cube) * square
        )
        gel_ref[b] = slope.astype(jnp.bfloat16)
        total = total + wide_dot(hidden, matrix(down_w), NT)
    n2, r2 = normed(total)
    out_ref[0] = (n2 * small[10:11, :] + small[11:12, :]).astype(jnp.bfloat16)
    cot = cot_ref[0].astype(jnp.float32)
    gh2 = norm_back(cot, n2, r2, small[10:11, :])
    gh2_ref[...] = gh2
    mixed = gh2.astype(jnp.bfloat16)
    gmt_ref[...] = mixed.T

    @pl.when(pl.program_id(0) == 0)
    def clear():
        sums_ref[...] = jnp.zeros_like(sums_ref)

    add_row(sums_ref, 0, mixed.astype(jnp.float32))
    add_row(sums_ref, 1, cot * n2)
    add_row(sums_ref, 2, cot)


def front(info, ctx, x_all, cot, small, rest):
    tokens, width = ctx.shape
    mid = x_all.shape[1]
    per = mid // TILE
    steps = tokens // TILE

    def arrived(t, info):
        return (info[1 + 2 * info[0] + t // per], t % per, 0)

    def rows(dtype_shape):
        return pl.BlockSpec(dtype_shape, lambda t, info: (t, 0))

    specs = [rest_spec(rest, lambda t, m=m: m) for m in range(3, 12)]
    wide4 = pl.BlockSpec((4, TILE, width), lambda t, info: (0, t, 0))
    flipped = pl.BlockSpec((width, TILE), lambda t, info: (0, t))
    return call(
        front_kernel,
        "front",
        info,
        steps,
        [
            rows((TILE, width)),
            pl.BlockSpec((1, TILE, width), arrived),
            pl.BlockSpec((1, TILE, width), arrived),
            fixed(small.shape),
            *specs,
        ],
        [
            pl.BlockSpec((1, TILE, width), arrived),
            rows((TILE, width)),
            rows((TILE, 128)),
            rows((TILE, width)),
            flipped,
            wide4,
            wide4,
            rows((TILE, width)),
            flipped,
            resident((8, width)),
        ],
        [
            bf16_of(2, mid, width),
            f32_of(tokens, width),
            f32_of(tokens, 128),
            bf16_of(tokens, width),
            bf16_of(width, tokens),
            bf16_of(4, tokens, width),
            bf16_of(4, tokens, width),
            f32_of(tokens, width),
            bf16_of(width, tokens),
            f32_of(8, width),
        ],
        [],
        (ctx, x_all, cot, small, *([rest] * 9)),
        11_000_000_000,
        40 << 20,
    )


MESH = pl.DeviceIdType.MESH
KINDS = 3


def place_of():
    c, t = lax.axis_index("ctx"), lax.axis_index("tp")
    return lax.axis_index("shard"), c, t


def send(src, dst, sems, index, target):
    send_sems, recv_sems = sems
    return pltpu.make_async_remote_copy(
        src_ref=src,
        dst_ref=dst,
        send_sem=send_sems.at[index],
        recv_sem=recv_sems.at[index],
        device_id=target,
        device_id_type=MESH,
    )


def bring_kernel(
    n_shard,
    n_ctx,
    n_tp,
    slots,
    part_ref,
    low_ref,
    xs_ref,
    x_ref,
    first_ref,
    rest_ref,
    got,
    mine,
    total,
    pool,
    sel,
    x_s,
    x_r,
    xt_s,
    xt_r,
    za_s,
    za_r,
    zb_s,
    zb_r,
    zc_s,
    zc_r,
    q_s,
    q_r,
    qt_s,
    qt_r,
    r_s,
    r_r,
    rt_s,
    rt_r,
    own_sem,
):
    z, c, t = place_of()
    side, core, bit = t // 2, lax.rem(t, 2), lax.rem(c, 2)
    held = low_ref.shape[0]
    piece = mine.shape[0]
    chunks, per = 3, 3
    me = c * n_tp + t

    def far(dz):
        return (lax.rem(z + dz, n_shard), c, t)

    def across(mask):
        return (z, c ^ mask, t)

    def beside(dt):
        return (z, c, lax.rem(t + dt, n_tp))

    barrier = pltpu.get_barrier_semaphore()
    friends = [far(dz) for dz in range(1, n_shard)]
    friends += [(z, c ^ m, t) for m in range(1, n_ctx)]
    friends += [beside(dt) for dt in range(1, n_tp)]
    friends += [(z, c ^ m, t ^ 1) for m in range(1, n_ctx)]
    for friend in friends:
        pl.semaphore_signal(barrier, inc=1, device_id=friend, device_id_type=MESH)
    pl.semaphore_wait(barrier, len(friends))

    stays = c // 2 == core
    goes = [(z, 2 * core + (p ^ bit), 2 * side + c // 2) for p in range(2)]
    x_moves = [send(xs_ref.at[p], x_ref.at[p], (x_s, x_r), p, goes[p]) for p in range(2)]
    x_keep = pltpu.make_async_copy(xs_ref.at[0], x_ref.at[0], x_r.at[0])

    za = [
        send(
            part_ref.at[pl.ds(pl.multiple_of(far(dz)[0] * piece, piece), piece)],
            got.at[dz - 1],
            (za_s, za_r),
            dz - 1,
            far(dz),
        )
        for dz in range(1, n_shard)
    ]
    for copy in za:
        copy.start()

    @pl.when(stays)
    def keep():
        x_keep.start()

    @pl.when(jnp.logical_not(stays))
    def leave():
        x_moves[0].start()

    x_moves[1].start()
    summed = part_ref[pl.ds(pl.multiple_of(z * piece, piece), piece), :]
    for dz, copy in enumerate(za):
        copy.wait_recv()
        summed = summed + got[dz]
    mine[...] = summed
    here = pl.ds(pl.multiple_of(z * piece, piece), piece)
    zb = [
        send(mine, total.at[here], (zb_s, zb_r), dz - 1, far(dz)) for dz in range(1, n_shard)
    ]
    for copy in zb:
        copy.start()
    total[here, :] = summed
    pool_here = pl.ds(z * held, held)
    zc = [
        send(low_ref, pool.at[pool_here], (zc_s, zc_r), dz - 1, far(dz))
        for dz in range(1, n_shard)
    ]
    for copy in zc:
        copy.start()
    pool_own = pltpu.make_async_copy(low_ref, pool.at[pool_here], own_sem.at[0])
    pool_own.start()
    for copy in zb:
        copy.wait_recv()

    q_moves = [
        send(total, first_ref.at[me], (q_s, q_r), k, across(m)) for k, m in enumerate((1, 2, 3))
    ]
    for copy in q_moves:
        copy.start()
    first_own = pltpu.make_async_copy(total, first_ref.at[me], own_sem.at[1])
    first_own.start()
    qt_own = [
        send(total, first_ref.at[me], (qt_s, qt_r), dt - 1, beside(dt)) for dt in range(1, n_tp)
    ]
    for copy in qt_own:
        copy.start()

    x_over = [
        send(x_ref.at[p], x_ref.at[2 + p], (xt_s, xt_r), p, (z, c, t ^ 1)) for p in range(2)
    ]

    @pl.when(stays)
    def kept():
        x_keep.wait()

    @pl.when(jnp.logical_not(stays))
    def came():
        x_moves[0].wait_recv()

    x_over[0].start()
    x_moves[1].wait_recv()
    x_over[1].start()

    qt_on = []
    for k, m in enumerate((1, 2, 3)):
        q_moves[k].wait_recv()
        place = (c ^ m) * n_tp + t
        for dt in range(1, n_tp):
            copy = send(
                first_ref.at[place],
                first_ref.at[place],
                (qt_s, qt_r),
                (k + 1) * (n_tp - 1) + dt - 1,
                beside(dt),
            )
            copy.start()
            qt_on.append(copy)

    for copy in zc:
        copy.wait_recv()
    pool_own.wait()
    for m in range(chunks * per):
        sel[m] = pool[slots[KINDS + m]]
    rest_own = pltpu.make_async_copy(sel, rest_ref.at[me], own_sem.at[2])
    rest_own.start()
    r_moves = []
    rt_moves = []
    for k in range(chunks):
        span = pl.ds(k * per, per)
        pair = [
            send(
                sel.at[span],
                rest_ref.at[me, span],
                (r_s, r_r),
                k * 3 + j,
                across(m),
            )
            for j, m in enumerate((1, 2))
        ]
        for copy in pair:
            copy.start()
        r_moves.append(pair)
        for dt in range(1, n_tp):
            copy = send(
                sel.at[span],
                rest_ref.at[me, span],
                (rt_s, rt_r),
                (k * 4) * (n_tp - 1) + dt - 1,
                beside(dt),
            )
            copy.start()
            rt_moves.append(copy)

    def pass_on(k, which, place):
        span = pl.ds(k * per, per)
        for dt in range(1, n_tp):
            copy = send(
                rest_ref.at[place, span],
                rest_ref.at[place, span],
                (rt_s, rt_r),
                (k * 4 + which) * (n_tp - 1) + dt - 1,
                beside(dt),
            )
            copy.start()
            rt_moves.append(copy)

    onward = []
    for k in range(chunks):
        span = pl.ds(k * per, per)
        for j in range(2):
            r_moves[k][j].wait_recv()
        odd = lax.rem(core + k, 2)
        source = jnp.where(odd == 0, c ^ 1, c ^ 2) * n_tp + t
        target = (z, jnp.where(odd == 0, c ^ 2, c ^ 1), t)
        copy = send(
            rest_ref.at[source, span], rest_ref.at[source, span], (r_s, r_r), k * 3 + 2, target
        )
        copy.start()
        onward.append(copy)
        pass_on(k, 1, (c ^ 1) * n_tp + t)
        pass_on(k, 2, (c ^ 2) * n_tp + t)
    for k in range(chunks):
        onward[k].wait_recv()
        pass_on(k, 3, (c ^ 3) * n_tp + t)

    for copy in x_over:
        copy.wait()

    @pl.when(jnp.logical_not(stays))
    def left():
        x_moves[0].wait_send()

    x_moves[1].wait_send()
    for copy in (*za, *zb, *zc, *q_moves, *onward):
        copy.wait_send()
    for pair in r_moves:
        for copy in pair:
            copy.wait_send()
    for copy in (*qt_own, *qt_on, *rt_moves):
        copy.wait()
    first_own.wait()
    rest_own.wait()


def bring(slots, part, low, xs, n_shard, n_ctx, n_tp):
    held, rows, width = low.shape
    total_rows = part.shape[0]
    groups = n_ctx * n_tp
    mid = xs.shape[1]
    anywhere = pl.BlockSpec(memory_space=pl.ANY)
    dma = pltpu.SemaphoreType.DMA
    pairs = [2, 2, n_shard - 1, n_shard - 1, n_shard - 1, 3]
    pairs += [4 * (n_tp - 1), 9, 12 * (n_tp - 1)]
    sems = [dma((n,)) for n in pairs for _ in range(2)]
    return pl.pallas_call(
        functools.partial(bring_kernel, n_shard, n_ctx, n_tp),
        name="bring",
        in_specs=[
            pl.BlockSpec(memory_space=pltpu.SMEM),
            pl.BlockSpec(memory_space=pltpu.VMEM),
            anywhere,
            anywhere,
        ],
        out_specs=[anywhere, anywhere, anywhere],
        out_shape=[
            jax.ShapeDtypeStruct((4, mid, width), jnp.bfloat16),
            jax.ShapeDtypeStruct((groups, total_rows, width), jnp.bfloat16),
            jax.ShapeDtypeStruct((groups, 9, rows, width), jnp.bfloat16),
        ],
        scratch_shapes=[
            pltpu.VMEM((n_shard - 1, total_rows // n_shard, width), jnp.bfloat16),
            pltpu.VMEM((total_rows // n_shard, width), jnp.bfloat16),
            pltpu.VMEM((total_rows, width), jnp.bfloat16),
            pltpu.VMEM((n_shard * held, rows, width), jnp.bfloat16),
            pltpu.VMEM((9, rows, width), jnp.bfloat16),
            *sems,
            dma((3,)),
        ],
        compiler_params=pltpu.CompilerParams(
            collective_id=0, has_side_effects=True, vmem_limit_bytes=40 << 20
        ),
        cost_estimate=pl.CostEstimate(flops=0, bytes_accessed=40 << 20, transcendentals=0),
    )(slots, part, low, xs)


def back_kernel(
    n_ctx,
    n_tp,
    gh2_ref,
    hid_ref,
    gel_ref,
    fit_ref,
    gmt_ref,
    n1_ref,
    r1_ref,
    ctx_ref,
    small,
    up_w,
    down_w,
    wo,
    layer_ref,
    own_ref,
    x_ref,
    y_ref,
    xy_ref,
    gh1_ref,
    dctx_ref,
    sums_ref,
    home_ref,
    gy,
    gu,
    grads,
    arrived,
    send_sem,
    recv_sem,
    h_s,
    h_r,
    keep_sem,
):
    z, c, t = place_of()
    step = pl.program_id(0)
    tokens, width = gh2_ref.shape
    tiles = tokens // TILE
    rows = own_ref.shape[1]
    others = n_tp - 1
    side, core, bit = t // 2, lax.rem(t, 2), lax.rem(c, 2)

    def beside(dt):
        return (z, c, lax.rem(t + dt, n_tp))

    stays = c // 2 == core
    keep_layer = pltpu.make_async_copy(layer_ref.at[0], home_ref.at[bit], keep_sem.at[0])
    layer_moves = [
        send(
            layer_ref.at[p],
            home_ref.at[bit],
            (h_s, h_r),
            p,
            (z, 2 * core + (p ^ bit), 2 * side + c // 2),
        )
        for p in range(2)
    ]

    @pl.when(step == 0)
    def start():
        barrier = pltpu.get_barrier_semaphore()
        friends = [beside(dt) for dt in range(1, n_tp)]
        friends += [(z, c ^ m, t) for m in range(1, n_ctx)]
        friends += [(z, c ^ m, t ^ 1) for m in range(1, n_ctx)]
        for friend in friends:
            pl.semaphore_signal(barrier, inc=1, device_id=friend, device_id_type=MESH)
        pl.semaphore_wait(barrier, len(friends))

        @pl.when(stays)
        def kept():
            keep_layer.start()

        @pl.when(jnp.logical_not(stays))
        def left():
            layer_moves[0].start()

        layer_moves[1].start()
        sums_ref[...] = jnp.zeros_like(sums_ref)
        gy[...] = gh2_ref[...]

    def moves(b, count):
        slot = lax.rem(b, 2)
        return [
            send(
                grads.at[slot, :, lax.rem(t + dt, n_tp), 0:count],
                arrived.at[b, dt - 1, :, 0:count],
                (send_sem, recv_sem),
                b * others + dt - 1,
                beside(dt),
            )
            for dt in range(1, n_tp)
        ]

    def exchange(b, count):
        for copy in moves(b, count):
            copy.start()

    def keep(b, count):
        for copy in moves(b, count):
            copy.wait()
        slot = lax.rem(b, 2)
        for j, out in enumerate((own_ref, x_ref, y_ref, xy_ref)):
            for i in range(count):
                value = grads[slot, c ^ j, t, i]
                for dt in range(others):
                    value = value + arrived[b, dt, c ^ j, i]
                out[2 * b + i] = value

    def put(slot, i, value):
        low = value.astype(jnp.bfloat16)
        grads[slot, :, :, i] = low.reshape(n_ctx, n_tp, rows, width)

    @pl.when(step < 4)
    def ffn():
        up_block = matrix(up_w)
        down_block = matrix(down_w)
        slot = lax.rem(step, 2)

        def one(i, carry):
            at = pl.ds(pl.multiple_of(i * TILE, TILE), TILE)
            mixed = gh2_ref[at, :].astype(jnp.bfloat16)
            grad = wide_dot(mixed, down_block, NN) * gel_ref[0, at, :].astype(jnp.float32)
            low = grad.astype(jnp.bfloat16)
            gu[at, :] = low
            gy[at, :] += wide_dot(low, up_block, NT)
            sums_ref[pl.ds(step, 1), :] += jnp.sum(
                low.astype(jnp.float32), axis=0, keepdims=True
            )
            return carry

        lax.fori_loop(0, tiles, one, 0)
        put(slot, 0, wide_dot(fit_ref[...], gu[...], NN))
        put(slot, 1, wide_dot(gmt_ref[...], hid_ref[0], NN))
        exchange(step, 2)

    @pl.when(step > 0)
    def settle():
        keep(step - 1, 2)

    @pl.when(step == 4)
    def first_norm():
        def one(i, carry):
            at = pl.ds(pl.multiple_of(i * TILE, TILE), TILE)
            grad = gy[at, :]
            n1 = n1_ref[at, :]
            gh1 = norm_back(grad, n1, r1_ref[at, 0:1], small[3:4, :])
            gh1_ref[at, :] = gh1
            low = gh1.astype(jnp.bfloat16)
            gu[at, :] = low
            add_row(sums_ref, 4, low.astype(jnp.float32))
            add_row(sums_ref, 5, grad * n1)
            add_row(sums_ref, 6, grad)
            return carry

        lax.fori_loop(0, tiles, one, 0)
        put(0, 0, wide_dot(ctx_ref[...].T, gu[...], NN))
        exchange(4, 1)
        out_w = matrix(wo)

        def two(i, carry):
            at = pl.ds(pl.multiple_of(i * TILE, TILE), TILE)
            dctx_ref[at, :] = wide_dot(gu[at, :], out_w, NT).astype(jnp.bfloat16)
            return carry

        lax.fori_loop(0, tiles, two, 0)
        keep(4, 1)

        @pl.when(stays)
        def done():
            keep_layer.wait()

        @pl.when(jnp.logical_not(stays))
        def gone():
            layer_moves[0].wait()

        layer_moves[1].wait()


def back(gh2, hid, gel, fit, gmt, n1, r1, ctx, small, rest, layer, n_ctx, n_tp):
    tokens, width = gh2.shape
    rows = rest.shape[2]
    dma = pltpu.SemaphoreType.DMA

    def whole(shape):
        return pl.BlockSpec(shape, lambda b: (0,) * len(shape), pipeline_mode=pl.Buffered(1))

    def block(b):
        return (jnp.minimum(b, 3), 0, 0)

    def held(first, single=False):
        return pl.BlockSpec(
            (n_ctx * n_tp, 1, rows, width),
            (lambda b: (0, first, 0, 0))
            if single
            else (lambda b: (0, first + jnp.minimum(b, 3), 0, 0)),
            pipeline_mode=pl.Buffered(1) if single else None,
        )

    def out(shape):
        return pl.BlockSpec(shape, lambda b: (0,) * len(shape))

    return pl.pallas_call(
        functools.partial(back_kernel, n_ctx, n_tp),
        name="back",
        grid=(5,),
        in_specs=[
            whole((tokens, width)),
            pl.BlockSpec((1, tokens, width), block),
            pl.BlockSpec((1, tokens, width), block),
            whole((width, tokens)),
            whole((width, tokens)),
            whole((tokens, width)),
            whole((tokens, 128)),
            whole((tokens, width)),
            whole(small.shape),
            held(1),
            held(5),
            held(0, True),
            pl.BlockSpec(memory_space=pl.ANY),
        ],
        out_specs=[
            *[out((9, rows, width))] * 4,
            out((tokens, width)),
            out((tokens, width)),
            out((8, width)),
            pl.BlockSpec(memory_space=pl.ANY),
        ],
        out_shape=[
            *[bf16_of(9, rows, width)] * 4,
            f32_of(tokens, width),
            bf16_of(tokens, width),
            f32_of(8, width),
            bf16_of(*layer.shape),
        ],
        scratch_shapes=[
            pltpu.VMEM((tokens, width), jnp.float32),
            pltpu.VMEM((tokens, width), jnp.bfloat16),
            pltpu.VMEM((2, n_ctx, n_tp, 2, rows, width), jnp.bfloat16),
            pltpu.VMEM((5, n_tp - 1, n_ctx, 2, rows, width), jnp.bfloat16),
            dma((5 * (n_tp - 1),)),
            dma((5 * (n_tp - 1),)),
            dma((2,)),
            dma((2,)),
            dma((1,)),
        ],
        compiler_params=pltpu.CompilerParams(
            collective_id=3, has_side_effects=True, vmem_limit_bytes=62 << 20
        ),
        cost_estimate=pl.CostEstimate(
            flops=22_000_000_000, bytes_accessed=40 << 20, transcendentals=0
        ),
    )(gh2, hid, gel, fit, gmt, n1, r1, ctx, small, rest, rest, rest, layer)


LATE = 3
EARLY = 9


def adam_update(weight, first, second, grad, decay, rate):
    count = float(STEP)
    first_new = beta_one * first + (1.0 - beta_one) * grad
    second_new = beta_two * second + (1.0 - beta_two) * grad * grad
    first_hat = first_new / (1.0 - beta_one**count)
    second_hat = second_new / (1.0 - beta_two**count)
    weight_new = weight - rate * (first_hat / (jnp.sqrt(second_hat) + adam_eps) + decay * weight)
    return (weight_new, first_new, second_new)


def finish_kernel(
    n_shard,
    n_ctx,
    n_tp,
    holder,
    late_at,
    x_hbm,
    dq_hbm,
    dk_hbm,
    dv_hbm,
    gh1_hbm,
    first_hbm,
    e0_hbm,
    e1_hbm,
    e2_hbm,
    e3_hbm,
    small_ref,
    w_ref,
    one_ref,
    two_ref,
    home_ref,
    w_out,
    one_out,
    two_out,
    small_out,
    x_s,
    dq_s,
    dk_s,
    dv_s,
    gh1_s,
    first_s,
    early,
    every,
    packed,
    slot_met,
    flipped,
    grads,
    arrived,
    partial,
    met,
    over,
    more,
    back_s,
    small_s,
    small_t,
    small_m,
    small_p,
    flat,
    flat_met,
    flat_sum,
    mine_s,
    pool,
    in_sem,
    c_s,
    c_r,
    p_s,
    p_r,
    o_s,
    o_r,
    h_s,
    h_r,
    sc_s,
    sc_r,
    sp_s,
    sp_r,
    e_s,
    e_r,
    a_s,
    a_r,
    b_s,
    b_r,
    keep_sem,
):
    z, c, t = place_of()
    side, core, bit = t // 2, lax.rem(t, 2), lax.rem(c, 2)
    _, mid, width = x_s.shape
    tokens = 2 * mid
    held, rows, _ = w_ref.shape
    per = n_ctx * n_tp // 2
    band = width // 2
    tile = mid // 2
    piece = mine_s.shape[0]

    loads = [
        pltpu.make_async_copy(src, dst, in_sem.at[i])
        for i, (src, dst) in enumerate(
            (
                (x_hbm, x_s),
                (dk_hbm, dk_s),
                (dv_hbm, dv_s),
                (dq_hbm, dq_s),
                (first_hbm, first_s),
                (gh1_hbm, gh1_s),
                (e0_hbm, early.at[0]),
                (e1_hbm, early.at[1]),
                (e2_hbm, early.at[2]),
                (e3_hbm, early.at[3]),
            )
        )
    ]
    for i in (6, 7, 8, 9, 0, 1, 2, 3, 4, 5):
        loads[i].start()

    def far(dz):
        return (lax.rem(z + dz, n_shard), c, t)

    def across(mask):
        return (z, c ^ mask, t)

    def beside(dt):
        return (z, c, lax.rem(t + dt, n_tp))

    barrier = pltpu.get_barrier_semaphore()
    friends = [far(dz) for dz in range(1, n_shard)]
    friends += [(z, c ^ m, t) for m in range(1, n_ctx)]
    friends += [beside(dt) for dt in range(1, n_tp)]
    friends += [(z, c ^ m, t ^ 1) for m in range(1, n_ctx)]
    for friend in friends:
        pl.semaphore_signal(barrier, inc=1, device_id=friend, device_id_type=MESH)

    for i in range(6, 10):
        loads[i].wait()
    every[0:EARLY] = early[0] + early[1] + early[2] + early[3]
    every[EARLY] = jnp.zeros_like(every[EARLY])
    for s in range(n_shard * held):
        packed[s // held, s % held] = every[holder[s]]
    pl.semaphore_wait(barrier, len(friends))
    slot_moves = [
        send(packed.at[far(dz)[0]], slot_met.at[dz - 1], (e_s, e_r), dz - 1, far(dz))
        for dz in range(1, n_shard)
    ]
    for copy in slot_moves:
        copy.start()

    core_moves = []

    def exchange(m):
        for dt in range(1, n_tp):
            other = lax.rem(t + dt, n_tp)
            for k in range(n_ctx):
                copy = send(
                    grads.at[k * n_tp + other, m],
                    arrived.at[dt - 1, k, m],
                    (c_s, c_r),
                    ((dt - 1) * n_ctx + k) * LATE + m,
                    beside(dt),
                )
                copy.start()
                core_moves.append((m, copy))

    plane_moves = []

    def meet(m):
        for which, copy in core_moves:
            if which == m:
                copy.wait_recv()
        for k in range(n_ctx):
            value = grads[k * n_tp + t, m]
            for dt in range(1, n_tp):
                value = value + arrived[dt - 1, k, m]
            partial[k, m] = value
        for j in range(1, n_ctx):
            copy = send(
                partial.at[c ^ j, m], met.at[j - 1, m], (p_s, p_r), (j - 1) * LATE + m, across(j)
            )
            copy.start()
            plane_moves.append(copy)

    loads[0].wait()
    for a in range(4):
        chunk = 2 * (core if a < 2 else 1 - core) + ((a % 2) ^ bit)
        flipped[:, pl.ds(pl.multiple_of(chunk * mid, mid), mid)] = x_s[a].T

    def weight_grad(m, left_at, right):
        def one(i, carry):
            left = flipped[pl.ds(pl.multiple_of(i * band, band), band), left_at]
            value = wide_dot(left, right[...], NN).astype(jnp.bfloat16)
            grads[pl.ds(i * per, per), m] = value.reshape(per, rows, width)
            return carry

        lax.fori_loop(0, 2, one, 0)

    loads[1].wait()
    weight_grad(1, slice(None), dk_s)
    exchange(1)
    loads[2].wait()
    weight_grad(2, slice(None), dv_s)
    exchange(2)
    meet(1)
    loads[3].wait()
    weight_grad(0, pl.ds(pl.multiple_of(core * tokens, tokens), tokens), dq_s)
    exchange(0)
    meet(2)

    row = lax.broadcasted_iota(jnp.int32, small_ref.shape, 0)
    q_sum = jnp.sum(dq_s[...].astype(jnp.float32), axis=0, keepdims=True)
    v_sum = jnp.sum(dv_s[...].astype(jnp.float32), axis=0, keepdims=True)
    sums = jnp.where(row == 0, q_sum, jnp.where(row == 1, v_sum, small_ref[...]))
    small_s[...] = sums.astype(jnp.bfloat16)
    small_core = [
        send(small_s, small_t.at[dt - 1], (sc_s, sc_r), dt - 1, beside(dt)) for dt in range(1, n_tp)
    ]
    for copy in small_core:
        copy.start()

    loads[4].wait()

    def weight(m):
        return first_s[:, m * rows : (m + 1) * rows, :].reshape(width, width)

    wq, wk, wv = weight(0), weight(1), weight(2)
    over_moves = []
    for b in range(2):
        at = pl.ds(pl.multiple_of((1 - core) * tokens + b * mid, mid), mid)
        value = wide_dot(dk_s[at, :], wk, NT) + wide_dot(dv_s[at, :], wv, NT)
        over[b] = value.astype(jnp.bfloat16)
        copy = send(over.at[b], more.at[b], (o_s, o_r), b, (z, c, t ^ 1))
        copy.start()
        over_moves.append(copy)
        if b == 0:
            meet(0)

    value = small_s[...]
    for dt, copy in enumerate(small_core):
        copy.wait_recv()
        value = value + small_t[dt]
    small_m[...] = value
    small_plane = [
        send(small_m, small_p.at[j - 1], (sp_s, sp_r), j - 1, across(j)) for j in range(1, n_ctx)
    ]
    for copy in small_plane:
        copy.start()

    loads[5].wait()
    stays = c // 2 == core
    home_moves = []
    for copy in over_moves:
        copy.wait_recv()
    keep = pltpu.make_async_copy(back_s.at[0], home_ref.at[bit], keep_sem.at[0])
    for move in range(2):
        chunk = move ^ bit
        for i in range(2):
            at = pl.ds(pl.multiple_of(core * tokens + chunk * mid + i * tile, tile), tile)
            here = pl.ds(pl.multiple_of(chunk * mid + i * tile, tile), tile)
            value = gh1_s[here, :]
            value = value + more[chunk, i * tile : (i + 1) * tile, :].astype(jnp.float32)
            value = value + wide_dot(dq_s[here, :], wq, NT)
            value = value + wide_dot(dk_s[at, :], wk, NT)
            value = value + wide_dot(dv_s[at, :], wv, NT)
            back_s[move, i * tile : (i + 1) * tile, :] = value.astype(jnp.bfloat16)
        target = (z, 2 * core + chunk, 2 * side + c // 2)
        home_moves.append(send(back_s.at[move], home_ref.at[bit], (h_s, h_r), move, target))
        if move == 0:

            @pl.when(stays)
            def kept():
                keep.start()

            @pl.when(jnp.logical_not(stays))
            def left():
                home_moves[0].start()

        else:
            home_moves[1].start()

    flat[...] = jnp.zeros_like(flat)
    for copy in plane_moves:
        copy.wait_recv()
    for m in range(LATE):
        value = partial[c, m]
        for j in range(n_ctx - 1):
            value = value + met[j, m]
        flat[m * rows : (m + 1) * rows, :] = value
    value = small_m[...]
    for j, copy in enumerate(small_plane):
        copy.wait_recv()
        value = value + small_p[j]
    small_rows = small_s.shape[0]
    flat[LATE * rows : LATE * rows + small_rows, :] = value

    def piece_at(k):
        return pl.ds(pl.multiple_of(k * piece, piece), piece)

    flat_out = [
        send(flat.at[piece_at(far(dz)[0])], flat_met.at[dz - 1], (a_s, a_r), dz - 1, far(dz))
        for dz in range(1, n_shard)
    ]
    for copy in flat_out:
        copy.start()
    total = flat[piece_at(z), :].astype(jnp.float32)
    for dz, copy in enumerate(flat_out):
        copy.wait_recv()
        total = total + flat_met[dz].astype(jnp.float32)
    mine_s[...] = total.astype(jnp.bfloat16)
    flat_back = [
        send(mine_s, flat_sum.at[piece_at(z)], (b_s, b_r), dz - 1, far(dz))
        for dz in range(1, n_shard)
    ]
    for copy in flat_back:
        copy.start()
    flat_sum[piece_at(z), :] = mine_s[...]
    for copy in slot_moves:
        copy.wait_recv()
    for copy in flat_back:
        copy.wait_recv()
    for m in range(LATE):
        pool[m] = flat_sum[m * rows : (m + 1) * rows, :]
    pool[LATE] = jnp.zeros_like(pool[LATE])
    for j in range(held):
        grad = packed[z, j].astype(jnp.float32)
        for dz in range(n_shard - 1):
            grad = grad + slot_met[dz, j].astype(jnp.float32)
        grad = grad + pool[late_at[z * held + j]].astype(jnp.float32)
        w, one, two = adam_update(w_ref[j], one_ref[j], two_ref[j], grad, 0.01, rate_value)
        w_out[j] = w
        one_out[j] = one
        two_out[j] = two
    small_out[...] = flat_sum[LATE * rows : LATE * rows + small_rows, :].astype(jnp.float32)

    @pl.when(stays)
    def done():
        keep.wait()

    @pl.when(jnp.logical_not(stays))
    def gone():
        home_moves[0].wait()

    home_moves[1].wait()
    for _, copy in core_moves:
        copy.wait_send()
    for copy in (
        *plane_moves,
        *over_moves,
        *small_core,
        *small_plane,
        *slot_moves,
        *flat_out,
        *flat_back,
    ):
        copy.wait_send()


def finish(
    holder,
    late_at,
    x_all,
    dq,
    dk,
    dv,
    gh1,
    first,
    early,
    small,
    master,
    one,
    two,
    n_shard,
    n_ctx,
    n_tp,
):
    _, mid, width = x_all.shape
    held, rows, _ = master.shape
    groups = n_ctx * n_tp
    span = 16 * n_shard
    long = -(-(LATE * rows + small.shape[0]) // span) * span
    smem = pl.BlockSpec(memory_space=pltpu.SMEM)
    anywhere = pl.BlockSpec(memory_space=pl.ANY)
    vmem = pl.BlockSpec(memory_space=pltpu.VMEM)
    dma = pltpu.SemaphoreType.DMA
    low = jnp.bfloat16
    pairs = [LATE * n_ctx * (n_tp - 1), LATE * (n_ctx - 1), 2, 2, n_tp - 1, n_ctx - 1]
    pairs += [n_shard - 1] * 3
    stored = f32_of(held, rows, width)
    shapes = [
        x_all.shape,
        dq.shape,
        dk.shape,
        dv.shape,
        None,
        first.shape,
        (4, EARLY, rows, width),
        (EARLY + 1, rows, width),
        (n_shard, held, rows, width),
        (n_shard - 1, held, rows, width),
        (width, 4 * mid),
        (groups, LATE, rows, width),
        (n_tp - 1, n_ctx, LATE, rows, width),
        (n_ctx, LATE, rows, width),
        (n_ctx - 1, LATE, rows, width),
        (2, mid, width),
        (2, mid, width),
        (2, mid, width),
        small.shape,
        (n_tp - 1, *small.shape),
        small.shape,
        (n_ctx - 1, *small.shape),
        (long, width),
        (n_shard - 1, long // n_shard, width),
        (long, width),
        (long // n_shard, width),
        (LATE + 1, rows, width),
    ]
    return pl.pallas_call(
        functools.partial(finish_kernel, n_shard, n_ctx, n_tp),
        name="finish",
        in_specs=[smem] * 2 + [anywhere] * 10 + [vmem] * 4,
        out_specs=[anywhere] + [vmem] * 4,
        out_shape=[bf16_of(2, mid, width), stored, stored, stored, f32_of(*small.shape)],
        scratch_shapes=[
            pltpu.VMEM(s, low) if s else pltpu.VMEM(gh1.shape, jnp.float32) for s in shapes
        ]
        + [dma((10,))]
        + [dma((n,)) for n in pairs for _ in range(2)]
        + [dma((1,))],
        compiler_params=pltpu.CompilerParams(
            collective_id=1, has_side_effects=True, vmem_limit_bytes=63 << 20
        ),
        cost_estimate=pl.CostEstimate(
            flops=12_000_000_000, bytes_accessed=40 << 20, transcendentals=0
        ),
    )(holder, late_at, x_all, dq, dk, dv, gh1, first, *early, small, master, one, two)


def moves(n_ctx, n_tp, pick):
    pairs = []
    for c in range(n_ctx):
        for t in range(n_tp):
            side, core = t // 2, t % 2
            to_ctx = 2 * core + (pick ^ (c & 1))
            to_tp = 2 * side + c // 2
            pairs.append((c * n_tp + t, to_ctx * n_tp + to_tp))
    return pairs


def shards(
    inputs,
    cotangent,
    rand_blocks,
    slot_of,
    master,
    moment_one,
    moment_two,
    small_params,
    small_one,
    small_two,
):
    n_shard = lax.axis_size("shard")
    n_ctx = lax.axis_size("ctx")
    n_tp = lax.axis_size("tp")
    groups = n_ctx * n_tp
    held, rows, width = master.shape
    span = small_params.shape[0]
    my_ctx = lax.axis_index("ctx")
    my_tp = lax.axis_index("tp")
    parity = lax.rem(my_ctx, 2)
    half = lax.rem(my_tp, 2)
    plane = ("ctx", "tp")
    forth = [moves(n_ctx, n_tp, pick) for pick in range(2)]

    arrival = [(b ^ parity) + 2 * (half ^ (j // 2)) for j, b in enumerate((0, 1, 0, 1))]
    info = jnp.stack([half, *arrival]).astype(jnp.int32)
    half_one = info[:1]

    def sent(field, pick):
        low = field.astype(jnp.bfloat16)
        return jnp.where(parity == 0, low[pick], low[1 - pick])

    low = master.astype(jnp.bfloat16)
    my_shard = lax.axis_index("shard")
    mine = my_shard * held + jnp.arange(held, dtype=jnp.int32)
    zero = jnp.zeros_like(low)
    parts = [
        jnp.sum(jnp.where((slot_of[m] == mine)[:, None, None], low, zero), axis=0, dtype=jnp.float32)
        for m in range(3)
    ]
    spread = (jnp.arange(n_shard) == my_shard)[:, None]
    small_part = jnp.where(spread, small_params[None, :], 0.0).reshape(-1)
    used = 3 * rows * width + n_shard * span
    total_rows = -(-used // (width * 16 * n_shard)) * 16 * n_shard
    small_part = jnp.pad(small_part, (0, total_rows * width - used)).reshape(-1, width)
    part = jnp.concatenate([*parts, small_part]).astype(jnp.bfloat16)
    xs = jnp.stack([sent(inputs, pick) for pick in range(2)])
    x_all, first, rest = bring(slot_of, part, low, xs, n_shard, n_ctx, n_tp)
    small = first[:, 3 * rows :, :].reshape(groups, -1)[:, : n_shard * span]
    small = small.reshape(groups, n_shard, span).transpose(1, 0, 2)
    small = small.reshape(-1, width).astype(jnp.float32)

    cots, x_all = lax.optimization_barrier(
        ([sent(cotangent, pick) for pick in range(2)], x_all)
    )
    cot = jnp.stack([lax.ppermute(cots[pick], plane, forth[pick]) for pick in range(2)])

    q, k, v = project(info, x_all, small, first, rows)
    context, lse = attend(half_one, rand_blocks, q, k, v, 5)
    out_low, n1, r1, fi, fit, hid, gel, gh2, gmt, sums_two = front(
        info, context, x_all, cot, small, rest
    )
    *early, gh1, dctx, sums_one, layer_home = back(
        gh2, hid, gel, fit, gmt, n1, r1, context, small, rest, out_low, n_ctx, n_tp
    )
    for j in range(1, n_ctx):
        crossing = [
            (a * n_tp + b, (a ^ j) * n_tp + b) for a in range(n_ctx) for b in range(n_tp)
        ]
        early[j] = lax.ppermute(early[j], plane, crossing)
    dq, dk, dv = attend_back(half_one, rand_blocks, q, k, v, lse, dctx, 5)
    small_rows = jnp.pad(
        jnp.concatenate([sums_one[4:7], sums_one[0:4], sums_two[0:3]]), ((2, 4), (0, 0))
    )
    stands = jnp.array([8, 0, 2, 4, 6, 1, 3, 5, 7], jnp.int32)
    slots_all = jnp.arange(n_shard * held, dtype=jnp.int32)
    hits = slot_of[None, :] == slots_all[:, None]
    holder = EARLY + jnp.sum(jnp.where(hits[:, LATE:], stands[None, :] - EARLY, 0), axis=1)
    ranks = jnp.arange(LATE, dtype=jnp.int32)[None, :]
    late_at = LATE + jnp.sum(jnp.where(hits[:, :LATE], ranks - LATE, 0), axis=1)
    came, master_new, first_new, second_new, small_sum = finish(
        holder.astype(jnp.int32),
        late_at.astype(jnp.int32),
        x_all,
        dq,
        dk,
        dv,
        gh1,
        first,
        early,
        small_rows,
        master,
        moment_one,
        moment_two,
        n_shard,
        n_ctx,
        n_tp,
    )
    layer_out = layer_home.astype(jnp.float32)
    input_grad = came.astype(jnp.float32)
    start = ((my_shard * n_ctx + my_ctx) * n_tp + my_tp) * span
    small_owned = lax.dynamic_slice_in_dim(small_sum.reshape(-1), start, span)
    small_new, small_first, small_second = adam_update(
        small_params, small_one, small_two, small_owned, 0.0, small_rate
    )
    return (
        layer_out,
        input_grad,
        master_new,
        first_new,
        second_new,
        small_new,
        small_first,
        small_second,
    )


def solution(mesh):
    tokens = P(("shard", "tp"), "ctx", None)
    stored = P("shard", ("ctx", "tp"), None)
    spread = P(("shard", "ctx", "tp"))
    return jax.shard_map(
        shards,
        mesh=mesh,
        in_specs=(tokens, tokens, P(), P(), stored, stored, stored, spread, spread, spread),
        out_specs=(tokens, tokens, stored, stored, stored, spread, spread, spread),
        check_vma=False,
    )
```

```python
import functools

import jax
import jax.numpy as jnp
from jax import lax
from jax.experimental import pallas as pl
from jax.experimental.pallas import tpu as pltpu
from jax.sharding import PartitionSpec as P

STEP = 5
norm_eps = 1e-12
beta_one = 0.9
beta_two = 0.999
adam_eps = 1e-08
rate_value = 0.04
small_rate = 0.25
score_scale = 0.125
gelu_root = 0.7978845608
gelu_cube = 0.044715

BLOCK = 64
HEAD = 64
PACK = 4
masked_score = -1e30


def wide_dot(a, b, dims):
    return lax.dot_general(a, b, (dims, ((), ())), preferred_element_type=jnp.float32)


def head_masks(rows):
    lane = lax.broadcasted_iota(jnp.int32, (rows, PACK * HEAD), 1) // HEAD
    return [lane == h for h in range(PACK)]


def spread_heads(block, masks):
    zero = jnp.zeros_like(block)
    return jnp.concatenate([jnp.where(m, block, zero) for m in masks], axis=0)


def own_heads(full, masks):
    total = None
    for h, m in enumerate(masks):
        piece = jnp.where(m, full[h * BLOCK : (h + 1) * BLOCK], 0.0)
        total = piece if total is None else total + piece
    return total


def rows_of(ref, index, count=1):
    return ref[pl.ds(index, count)].reshape(count * BLOCK, ref.shape[2])


def flat_rows(ref, index):
    return ref[pl.ds(pl.multiple_of(index * BLOCK, BLOCK), BLOCK), :]


def picked_rows(ref, picks, low_half):
    halves = []
    for pair in range(PACK // 2):
        cols = slice(pair * 2 * HEAD, (pair + 1) * 2 * HEAD)
        first = ref[picks[2 * pair], :, cols]
        second = ref[picks[2 * pair + 1], :, cols]
        halves.append(jnp.where(low_half, first, second))
    return jnp.concatenate(halves, axis=1)


def gathered(ref, block, last, picks, low_half):
    pieces = [rows_of(ref, 0), rows_of(ref, last), rows_of(ref, block - 1, 3)]
    pieces += [picked_rows(ref, p, low_half) for p in picks]
    return jnp.concatenate(pieces, axis=0)


def middle_scores(keys, spread, block, last):
    scores = wide_dot(keys, spread, ((1,), (1,)))
    first_off = jnp.where(block == 1, masked_score, 0.0)
    last_off = jnp.where(block == last - 1, masked_score, 0.0)
    b = BLOCK
    return jnp.concatenate(
        [
            scores[: 2 * b],
            scores[2 * b : 3 * b] + first_off,
            scores[3 * b : 4 * b],
            scores[4 * b : 5 * b] + last_off,
            scores[5 * b :],
        ],
        axis=0,
    )


def attend_back_kernel(
    unroll,
    half_ref,
    table_ref,
    q_ref,
    k_ref,
    v_ref,
    lse_ref,
    do_ref,
    dq_ref,
    dk_ref,
    dv_ref,
    dk_acc,
    dv_acc,
    kept_p,
    kept_g,
):
    half = half_ref[0]
    group = pl.program_id(0)
    q_ref, k_ref, v_ref = q_ref.at[0], k_ref.at[0], v_ref.at[0]
    nblocks, local = k_ref.shape[0], q_ref.shape[0]
    last = nblocks - 1
    picks_each = table_ref.shape[2]
    masks = head_masks(BLOCK)
    low_half = lax.broadcasted_iota(jnp.int32, (BLOCK, 2 * HEAD), 1) < HEAD
    span = 8 * BLOCK
    chunks = nblocks // 8

    edge = (local - 1) * half
    spread = spread_heads(rows_of(q_ref, edge), masks)
    spread_do = spread_heads(flat_rows(do_ref, edge), masks)
    lse = lse_ref[0, pl.ds(edge, 1), :]
    delta = None
    for c in range(chunks):
        rows = slice(c * span, (c + 1) * span)
        probs = jnp.exp(wide_dot(rows_of(k_ref, c * 8, 8), spread, ((1,), (1,))) - lse)
        gp = wide_dot(rows_of(v_ref, c * 8, 8), spread_do, ((1,), (1,)))
        kept_p[rows, :] = probs
        kept_g[rows, :] = gp
        part = jnp.sum(probs * gp, axis=0, keepdims=True)
        delta = part if delta is None else delta + part
    full = None
    for c in range(chunks):
        rows = slice(c * span, (c + 1) * span)
        probs = kept_p[rows, :]
        ds = (probs * (kept_g[rows, :] - delta)).astype(jnp.bfloat16)
        dv_acc[rows, :] = wide_dot(probs.astype(jnp.bfloat16), spread_do, ((1,), (0,)))
        dk_acc[rows, :] = wide_dot(ds, spread, ((1,), (0,)))
        part = wide_dot(ds, rows_of(k_ref, c * 8, 8), ((0,), (0,)))
        full = part if full is None else full + part
    dq_ref[pl.ds(pl.multiple_of(edge * BLOCK, BLOCK), BLOCK), :] = (
        own_heads(full, masks) * 0.125
    ).astype(jnp.bfloat16)

    def scatter(acc, piece, block, picks):
        b = BLOCK
        acc[0:b, :] += piece[:b]
        acc[last * b : (last + 1) * b, :] += piece[b : 2 * b]
        window = pl.ds(pl.multiple_of((block - 1) * b, b), 3 * b)
        acc[window, :] += piece[2 * b : 5 * b]
        for r, p in enumerate(picks):
            part = piece[(5 + r) * b : (6 + r) * b]
            for pair in range(PACK // 2):
                lanes = slice(pair * 2 * HEAD, (pair + 1) * 2 * HEAD)
                cols = pl.ds(pair * 2 * HEAD, 2 * HEAD)
                sub = part[:, lanes]
                acc[pl.ds(pl.multiple_of(p[2 * pair] * b, b), b), cols] += jnp.where(
                    low_half, sub, 0.0
                )
                acc[pl.ds(pl.multiple_of(p[2 * pair + 1] * b, b), b), cols] += jnp.where(
                    low_half, 0.0, sub
                )

    def middle(step, carry):
        mine = step + 1 - half
        block = mine + local * half
        picks = [
            [table_ref[group * PACK + h, block - 1, r] for h in range(PACK)]
            for r in range(picks_each)
        ]
        spread = spread_heads(rows_of(q_ref, mine), masks)
        spread_do = spread_heads(flat_rows(do_ref, mine), masks)
        keys = gathered(k_ref, block, last, picks, low_half)
        values = gathered(v_ref, block, last, picks, low_half)
        scores = middle_scores(keys, spread, block, last)
        probs = jnp.exp(scores - lse_ref[0, pl.ds(mine, 1), :])
        gp = wide_dot(values, spread_do, ((1,), (1,)))
        delta = jnp.sum(probs * gp, axis=0, keepdims=True)
        ds = (probs * (gp - delta)).astype(jnp.bfloat16)
        low = probs.astype(jnp.bfloat16)
        scatter(dv_acc, wide_dot(low, spread_do, ((1,), (0,))), block, picks)
        scatter(dk_acc, wide_dot(ds, spread, ((1,), (0,))), block, picks)
        full = wide_dot(ds, keys, ((0,), (0,)))
        dq_ref[pl.ds(pl.multiple_of(mine * BLOCK, BLOCK), BLOCK), :] = (
            own_heads(full, masks) * 0.125
        ).astype(jnp.bfloat16)
        return carry

    lax.fori_loop(0, local - 1, middle, 0, unroll=unroll)
    dk_ref[...] = dk_acc[...].astype(jnp.bfloat16)
    dv_ref[...] = dv_acc[...].astype(jnp.bfloat16)


def attend_back(half, table, q, k, v, lse, do, unroll=3):
    tokens, width = do.shape
    groups, nblocks, _, lanes = k.shape
    seq = nblocks * BLOCK
    blocks = tokens // BLOCK
    mine = pl.BlockSpec((tokens, lanes), lambda g, *_: (0, g))
    whole = pl.BlockSpec((seq, lanes), lambda g, *_: (0, g))
    spec = pltpu.PrefetchScalarGridSpec(
        num_scalar_prefetch=2,
        grid=(groups,),
        in_specs=[
            pl.BlockSpec((1, blocks, BLOCK, lanes), lambda g, *_: (g, 0, 0, 0)),
            pl.BlockSpec((1, nblocks, BLOCK, lanes), lambda g, *_: (g, 0, 0, 0)),
            pl.BlockSpec((1, nblocks, BLOCK, lanes), lambda g, *_: (g, 0, 0, 0)),
            pl.BlockSpec((1, blocks, lanes), lambda g, *_: (g, 0, 0)),
            mine,
        ],
        out_specs=[mine, whole, whole],
        scratch_shapes=[pltpu.VMEM((seq, lanes), jnp.float32)] * 4,
    )
    return pl.pallas_call(
        functools.partial(attend_back_kernel, unroll),
        grid_spec=spec,
        out_shape=[
            jax.ShapeDtypeStruct((tokens, width), jnp.bfloat16),
            jax.ShapeDtypeStruct((seq, width), jnp.bfloat16),
            jax.ShapeDtypeStruct((seq, width), jnp.bfloat16),
        ],
        name="attend_back",
        compiler_params=pltpu.CompilerParams(vmem_limit_bytes=56 << 20),
        cost_estimate=pl.CostEstimate(
            flops=120_000_000_000, bytes_accessed=24 << 20, transcendentals=16_000_000
        ),
    )(half, table, q, k, v, lse, do)


TILE = 256
MID = 512


def cols_mean(value):
    return jnp.mean(value, axis=-1, keepdims=True)


def normed(field):
    centred = field - cols_mean(field)
    rate = lax.rsqrt(cols_mean(centred * centred) + norm_eps)
    return centred * rate, rate


def norm_back(cot, normal, rate, gain):
    dn = cot * gain
    return rate * (dn - cols_mean(dn) - normal * cols_mean(dn * normal))


def matrix(ref):
    value = ref[...]
    return value.reshape(-1, value.shape[-1])


def add_row(ref, row, value):
    ref[row : row + 1, :] += jnp.sum(value, axis=0, keepdims=True)


def rest_spec(rest, which, single=True):
    groups, _, rows, width = rest.shape
    mode = pl.Buffered(1) if single else None
    return pl.BlockSpec(
        (groups, 1, rows, width), lambda step, info: (0, which(step) - 3, 0, 0), pipeline_mode=mode
    )


def fixed(shape):
    return pl.BlockSpec(shape, lambda step, info: (0,) * len(shape), pipeline_mode=pl.Buffered(1))


def call(kernel, name, info, grid, in_specs, out_specs, out_shape, scratch, args, flops, moved):
    return pl.pallas_call(
        kernel,
        name=name,
        grid_spec=pltpu.PrefetchScalarGridSpec(
            num_scalar_prefetch=1,
            grid=(grid,),
            in_specs=in_specs,
            out_specs=out_specs,
            scratch_shapes=scratch,
        ),
        out_shape=out_shape,
        compiler_params=pltpu.CompilerParams(vmem_limit_bytes=60 << 20),
        cost_estimate=pl.CostEstimate(
            flops=flops, bytes_accessed=moved, transcendentals=0
        ),
    )(info, *args)


def bf16_of(*shape):
    return jax.ShapeDtypeStruct(shape, jnp.bfloat16)


def f32_of(*shape):
    return jax.ShapeDtypeStruct(shape, jnp.float32)


NN = ((1,), (0,))
NT = ((1,), (1,))
TN = ((0,), (0,))


def front_kernel(
    info,
    ctx_ref,
    x_ref,
    small,
    wo,
    u0,
    u1,
    u2,
    u3,
    v0,
    v1,
    v2,
    v3,
    out_ref,
    n1_ref,
    r1_ref,
    fit_ref,
    hid_ref,
    gel_ref,
    n2_ref,
    r2_ref,
):
    attn_out = wide_dot(ctx_ref[...], matrix(wo), NN) + small[2:3, :]
    n1, r1 = normed(x_ref[0].astype(jnp.float32) + attn_out)
    n1_ref[...] = n1
    r1_ref[...] = jnp.broadcast_to(r1, r1_ref.shape)
    after = n1 * small[3:4, :] + small[4:5, :]
    ffn_in = after.astype(jnp.bfloat16)
    fit_ref[...] = ffn_in.T
    total = after + small[9:10, :]
    for b, (up_w, down_w) in enumerate(((u0, v0), (u1, v1), (u2, v2), (u3, v3))):
        up = wide_dot(ffn_in, matrix(up_w), NN) + small[5 + b : 6 + b, :]
        square = up * up
        bent = jnp.tanh(gelu_root * up * (1.0 + gelu_cube * square))
        rise = 0.5 * (1.0 + bent)
        hidden = (up * rise).astype(jnp.bfloat16)
        hid_ref[b] = hidden
        slope = rise + (0.5 * gelu_root) * up * (1.0 - bent * bent) * (
            1.0 + (3.0 * gelu_cube) * square
        )
        gel_ref[b] = slope.astype(jnp.bfloat16)
        total = total + wide_dot(hidden, matrix(down_w), NT)
    n2, r2 = normed(total)
    out_ref[0] = (n2 * small[10:11, :] + small[11:12, :]).astype(jnp.bfloat16)
    n2_ref[...] = n2
    r2_ref[...] = jnp.broadcast_to(r2, r2_ref.shape)


def front(info, ctx, x_all, small, rest):
    tokens, width = ctx.shape
    mid = x_all.shape[1]
    per = mid // TILE
    steps = tokens // TILE

    def arrived(t, info):
        return (info[1 + 2 * info[0] + t // per], t % per, 0)

    def rows(dtype_shape):
        return pl.BlockSpec(dtype_shape, lambda t, info: (t, 0))

    specs = [rest_spec(rest, lambda t, m=m: m) for m in range(3, 12)]
    wide4 = pl.BlockSpec((4, TILE, width), lambda t, info: (0, t, 0))
    flipped = pl.BlockSpec((width, TILE), lambda t, info: (0, t))
    return call(
        front_kernel,
        "front",
        info,
        steps,
        [
            rows((TILE, width)),
            pl.BlockSpec((1, TILE, width), arrived),
            fixed(small.shape),
            *specs,
        ],
        [
            pl.BlockSpec((1, TILE, width), arrived),
            rows((TILE, width)),
            rows((TILE, 128)),
            flipped,
            wide4,
            wide4,
            rows((TILE, width)),
            rows((TILE, 128)),
        ],
        [
            bf16_of(2, mid, width),
            f32_of(tokens, width),
            f32_of(tokens, 128),
            bf16_of(width, tokens),
            bf16_of(4, tokens, width),
            bf16_of(4, tokens, width),
            f32_of(tokens, width),
            f32_of(tokens, 128),
        ],
        [],
        (ctx, x_all, small, *([rest] * 9)),
        11_000_000_000,
        40 << 20,
    )


MESH = pl.DeviceIdType.MESH
KINDS = 3
CHUNKS = 3
PER = 3


def place_of():
    c, t = lax.axis_index("ctx"), lax.axis_index("tp")
    return lax.axis_index("shard"), c, t


def send(src, dst, sems, index, target):
    send_sems, recv_sems = sems
    return pltpu.make_async_remote_copy(
        src_ref=src,
        dst_ref=dst,
        send_sem=send_sems.at[index],
        recv_sem=recv_sems.at[index],
        device_id=target,
        device_id_type=MESH,
    )


def begin_kernel(
    n_shard,
    n_ctx,
    n_tp,
    slots,
    local_at,
    table,
    master_hbm,
    small_in,
    input_hbm,
    x_ref,
    first_ref,
    rest_ref,
    small_ref,
    q_ref,
    k_ref,
    v_ref,
    ctx_ref,
    lse_ref,
    raw,
    low,
    given,
    xs,
    x_all,
    part,
    got,
    mine,
    total,
    pool,
    sel,
    first,
    weights,
    small,
    q_s,
    k_s,
    v_s,
    ctx_s,
    kept,
    x_s,
    x_r,
    xt_s,
    xt_r,
    za_s,
    za_r,
    zb_s,
    zb_r,
    zc_s,
    zc_r,
    qm_s,
    qm_r,
    qt_s,
    qt_r,
    r_s,
    r_r,
    rt_s,
    rt_r,
    own_sem,
    out_sem,
):
    z, c, t = place_of()
    side, core, bit = t // 2, lax.rem(t, 2), lax.rem(c, 2)
    held, rows, width = low.shape[0] - 1, low.shape[1], low.shape[2]
    piece = mine.shape[0]
    me = c * n_tp + t
    _, mid, _ = xs.shape
    nblocks = 4 * mid // BLOCK
    local = nblocks // 2
    lanes = PACK * HEAD
    groups = width // lanes
    others = n_tp - 1

    take_raw = pltpu.make_async_copy(master_hbm, raw, own_sem.at[0])
    take_given = pltpu.make_async_copy(input_hbm, given, own_sem.at[1])
    take_raw.start()
    take_given.start()

    def far(dz):
        return (lax.rem(z + dz, n_shard), c, t)

    def across(mask):
        return (z, c ^ mask, t)

    def beside(dt):
        return (z, c, lax.rem(t + dt, n_tp))

    barrier = pltpu.get_barrier_semaphore()
    friends = [far(dz) for dz in range(1, n_shard)]
    friends += [(z, c ^ m, t) for m in range(1, n_ctx)]
    friends += [beside(dt) for dt in range(1, n_tp)]
    friends += [(z, c ^ m, t ^ 1) for m in range(1, n_ctx)]
    for friend in friends:
        pl.semaphore_signal(barrier, inc=1, device_id=friend, device_id_type=MESH)

    take_raw.wait()
    for j in range(held):
        low[j] = raw[j].astype(jnp.bfloat16)
    low[held] = jnp.zeros_like(low[held])
    part[...] = jnp.zeros_like(part)
    for m in range(KINDS):
        part[m * rows : (m + 1) * rows, :] = low[local_at[m]]
    part[KINDS * rows : KINDS * rows + 16, :] = small_in[...].astype(jnp.bfloat16)
    pl.semaphore_wait(barrier, len(friends))

    def piece_at(k):
        return pl.ds(pl.multiple_of(k * piece, piece), piece)

    za = [
        send(part.at[piece_at(far(dz)[0])], got.at[dz - 1], (za_s, za_r), dz - 1, far(dz))
        for dz in range(1, n_shard)
    ]
    for copy in za:
        copy.start()

    stays = c // 2 == core
    goes = [(z, 2 * core + (p ^ bit), 2 * side + c // 2) for p in range(2)]
    x_moves = [send(xs.at[p], x_all.at[p], (x_s, x_r), p, goes[p]) for p in range(2)]
    x_keep = pltpu.make_async_copy(xs.at[0], x_all.at[0], own_sem.at[2])
    take_given.wait()
    xs[0] = given[bit].astype(jnp.bfloat16)

    @pl.when(stays)
    def keep():
        x_keep.start()

    @pl.when(jnp.logical_not(stays))
    def leave():
        x_moves[0].start()

    xs[1] = given[1 - bit].astype(jnp.bfloat16)
    x_moves[1].start()

    summed = part[piece_at(z), :]
    for dz, copy in enumerate(za):
        copy.wait_recv()
        summed = summed + got[dz]
    mine[...] = summed
    zb = [
        send(mine, total.at[piece_at(z)], (zb_s, zb_r), dz - 1, far(dz))
        for dz in range(1, n_shard)
    ]
    for copy in zb:
        copy.start()
    total[piece_at(z), :] = summed
    pool_here = pl.ds(z * held, held)
    zc = [
        send(low.at[0:held], pool.at[pool_here], (zc_s, zc_r), dz - 1, far(dz))
        for dz in range(1, n_shard)
    ]
    for copy in zc:
        copy.start()
    pool[pool_here] = low[0:held]
    for copy in zb:
        copy.wait_recv()

    q_moves = [
        send(total, first.at[me], (qm_s, qm_r), k, across(m)) for k, m in enumerate((1, 2, 3))
    ]
    for copy in q_moves:
        copy.start()
    qt_moves = [
        send(total, first.at[me], (qt_s, qt_r), dt - 1, beside(dt)) for dt in range(1, n_tp)
    ]
    for copy in qt_moves:
        copy.start()
    first[me] = total[...]

    x_over = [
        send(x_all.at[p], x_all.at[2 + p], (xt_s, xt_r), p, (z, c, t ^ 1)) for p in range(2)
    ]

    @pl.when(stays)
    def stayed():
        x_keep.wait()

    @pl.when(jnp.logical_not(stays))
    def came():
        x_moves[0].wait_recv()

    x_over[0].start()
    x_moves[1].wait_recv()
    x_over[1].start()

    for k, m in enumerate((1, 2, 3)):
        q_moves[k].wait_recv()
        place = (c ^ m) * n_tp + t
        for dt in range(1, n_tp):
            copy = send(
                first.at[place],
                first.at[place],
                (qt_s, qt_r),
                (k + 1) * others + dt - 1,
                beside(dt),
            )
            copy.start()
            qt_moves.append(copy)
    for copy in qt_moves:
        copy.wait_recv()
    outs = [pltpu.make_async_copy(first, first_ref, out_sem.at[0])]
    outs[0].start()

    sums = None
    for g in range(n_ctx * n_tp):
        here = first[g, KINDS * rows : KINDS * rows + 16, :].astype(jnp.float32)
        sums = here if sums is None else sums + here
    small[...] = sums
    small_ref[...] = sums
    for m in range(KINDS):
        weights[m] = first[:, m * rows : (m + 1) * rows, :].reshape(width, width)

    def split(dst, start, value):
        low_value = value.astype(jnp.bfloat16)
        per = TILE // BLOCK
        for g in range(groups):
            piece_value = low_value[:, g * lanes : (g + 1) * lanes]
            dst[g, pl.ds(start, per)] = piece_value.reshape(per, BLOCK, lanes)

    def project(a, chunk, own):
        def one(i, carry):
            x = x_all[a, pl.ds(pl.multiple_of(i * TILE, TILE), TILE), :]
            start = chunk * (mid // BLOCK) + i * (TILE // BLOCK)
            if own:
                q_start = (chunk - 2 * core) * (mid // BLOCK) + i * (TILE // BLOCK)
                q = wide_dot(x, weights[0], NN) + small[0:1, :]
                split(q_s, q_start, q.astype(jnp.bfloat16) * jnp.bfloat16(score_scale))
            split(k_s, start, wide_dot(x, weights[1], NN))
            split(v_s, start, wide_dot(x, weights[2], NN) + small[1:2, :])
            return carry

        lax.fori_loop(0, mid // TILE, one, 0)

    def own_project(a, carry):
        project(a, 2 * core + (a ^ bit), True)
        return carry

    def other_project(a, carry):
        project(2 + a, 2 * (1 - core) + (a ^ bit), False)
        return carry

    lax.fori_loop(0, 2, own_project, 0)
    for copy in x_over:
        copy.wait_recv()
    outs.append(pltpu.make_async_copy(x_all, x_ref, out_sem.at[1]))
    outs[1].start()
    lax.fori_loop(0, 2, other_project, 0)
    for i, (src, dst) in enumerate(((q_s, q_ref), (k_s, k_ref), (v_s, v_ref))):
        outs.append(pltpu.make_async_copy(src, dst, out_sem.at[2 + i]))
        outs[-1].start()

    def span_of(k):
        return pl.ds(k * PER, PER)

    rest_own = pltpu.make_async_copy(sel, rest_ref.at[me], own_sem.at[3])
    direct = [
        [
            send(
                sel.at[span_of(k)], rest_ref.at[me, span_of(k)], (r_s, r_r), k * 3 + j, across(m)
            )
            for j, m in enumerate((1, 2))
        ]
        for k in range(CHUNKS)
    ]
    onward = []
    for k in range(CHUNKS):
        odd = lax.rem(core + k, 2)
        source = jnp.where(odd == 0, c ^ 1, c ^ 2) * n_tp + t
        target = (z, jnp.where(odd == 0, c ^ 2, c ^ 1), t)
        view = rest_ref.at[source, span_of(k)]
        onward.append(send(view, view, (r_s, r_r), k * 3 + 2, target))

    def passing(k, which):
        if which == 0:
            src = sel.at[span_of(k)]
        else:
            src = rest_ref.at[(c ^ which) * n_tp + t, span_of(k)]
        dst = rest_ref.at[(c ^ which) * n_tp + t, span_of(k)]
        return [
            send(src, dst, (rt_s, rt_r), (k * 4 + which) * others + dt - 1, beside(dt))
            for dt in range(1, n_tp)
        ]

    passed = [[passing(k, which) for which in range(4)] for k in range(CHUNKS)]

    def begin_rest():
        for copy in zc:
            copy.wait_recv()
        for m in range(CHUNKS * PER):
            sel[m] = pool[slots[KINDS + m]]
        rest_own.start()
        for k in range(CHUNKS):
            for copy in direct[k]:
                copy.start()
            for copy in passed[k][0]:
                copy.start()

    def relay(k):
        for copy in direct[k]:
            copy.wait_recv()
        onward[k].start()
        for copy in passed[k][1] + passed[k][2]:
            copy.start()

    def last_relay(k):
        onward[k].wait_recv()
        for copy in passed[k][3]:
            copy.start()

    begin_rest()

    last = nblocks - 1
    picks_each = table.shape[2]
    masks = head_masks(BLOCK)
    low_half = lax.broadcasted_iota(jnp.int32, (BLOCK, 2 * HEAD), 1) < HEAD
    each = 5
    subs = (local - 1) // each

    def attend_round(i, carry):
        g = i // subs
        sub = lax.rem(i, subs)
        qg, kg, vg = q_s.at[g], k_s.at[g], v_s.at[g]
        for k in range(CHUNKS):

            @pl.when(i == 3 + 2 * k)
            def hook(k=k):
                relay(k)

        @pl.when(sub == 0)
        def edge_block():
            edge = (local - 1) * core
            spread = spread_heads(rows_of(qg, edge), masks)
            span = 8 * BLOCK
            pieces = nblocks // 8
            top = None
            for n in range(pieces):
                scores = wide_dot(rows_of(kg, n * 8, 8), spread, NT)
                kept[n * span : (n + 1) * span, :] = scores
                high = jnp.max(scores, axis=0, keepdims=True)
                top = high if top is None else jnp.maximum(top, high)
            total_p = None
            for n in range(pieces):
                probs = jnp.exp(kept[n * span : (n + 1) * span, :] - top)
                kept[n * span : (n + 1) * span, :] = probs
                some = jnp.sum(probs, axis=0, keepdims=True)
                total_p = some if total_p is None else total_p + some
            scale = 1.0 / total_p
            full = None
            for n in range(pieces):
                probs = (kept[n * span : (n + 1) * span, :] * scale).astype(jnp.bfloat16)
                some = wide_dot(probs, rows_of(vg, n * 8, 8), TN)
                full = some if full is None else full + some
            at = pl.ds(pl.multiple_of(edge * BLOCK, BLOCK), BLOCK)
            ctx_s[g, at, :] = own_heads(full, masks).astype(jnp.bfloat16)
            lse_ref[g, pl.ds(edge, 1), :] = top + jnp.log(total_p)

        for u in range(each):
            spot = sub * each + u + 1 - core
            block = spot + local * core
            picks = [
                [table[g * PACK + h, block - 1, r] for h in range(PACK)]
                for r in range(picks_each)
            ]
            spread = spread_heads(rows_of(qg, spot), masks)
            keys = gathered(kg, block, last, picks, low_half)
            values = gathered(vg, block, last, picks, low_half)
            scores = middle_scores(keys, spread, block, last)
            top = jnp.max(scores, axis=0, keepdims=True)
            probs = jnp.exp(scores - top)
            total_p = jnp.sum(probs, axis=0, keepdims=True)
            probs = (probs * (1.0 / total_p)).astype(jnp.bfloat16)
            full = wide_dot(probs, values, TN)
            at = pl.ds(pl.multiple_of(spot * BLOCK, BLOCK), BLOCK)
            ctx_s[g, at, :] = own_heads(full, masks).astype(jnp.bfloat16)
            lse_ref[g, pl.ds(spot, 1), :] = top + jnp.log(total_p)
        return carry

    lax.fori_loop(0, groups * subs, attend_round, 0)
    for g in range(groups):
        outs.append(
            pltpu.make_async_copy(
                ctx_s.at[g], ctx_ref.at[:, g * lanes : (g + 1) * lanes], out_sem.at[5 + g]
            )
        )
        outs[-1].start()
    for k in range(CHUNKS):
        last_relay(k)

    @pl.when(jnp.logical_not(stays))
    def left():
        x_moves[0].wait_send()

    x_moves[1].wait_send()
    for copy in (*x_over, *za, *zb, *zc, *q_moves, *qt_moves, *onward):
        copy.wait_send()
    for pair in direct:
        for copy in pair:
            copy.wait_send()
    for chunk in passed:
        for group in chunk:
            for copy in group:
                copy.wait()
    rest_own.wait()
    for copy in outs:
        copy.wait()


def begin(slots, local_at, table, master, small_in, inputs, n_shard, n_ctx, n_tp):
    held, rows, width = master.shape
    _, mid, _ = inputs.shape
    groups = n_ctx * n_tp
    long = -(-(KINDS * rows + 16) // (16 * n_shard)) * 16 * n_shard
    lanes = PACK * HEAD
    packs = width // lanes
    tokens, seq = 2 * mid, 4 * mid
    anywhere = pl.BlockSpec(memory_space=pl.ANY)
    vmem = pl.BlockSpec(memory_space=pltpu.VMEM)
    smem = pl.BlockSpec(memory_space=pltpu.SMEM)
    dma = pltpu.SemaphoreType.DMA
    low = jnp.bfloat16
    f32 = jnp.float32
    pairs = [2, 2, n_shard - 1, n_shard - 1, n_shard - 1, 3]
    pairs += [4 * (n_tp - 1), 3 * CHUNKS, 4 * CHUNKS * (n_tp - 1)]
    return pl.pallas_call(
        functools.partial(begin_kernel, n_shard, n_ctx, n_tp),
        name="begin",
        in_specs=[smem, smem, smem, anywhere, vmem, anywhere],
        out_specs=[anywhere, anywhere, anywhere, vmem, anywhere, anywhere, anywhere, anywhere, vmem],
        out_shape=[
            bf16_of(4, mid, width),
            bf16_of(groups, long, width),
            bf16_of(groups, 9, rows, width),
            f32_of(16, width),
            bf16_of(packs, tokens // BLOCK, BLOCK, lanes),
            bf16_of(packs, seq // BLOCK, BLOCK, lanes),
            bf16_of(packs, seq // BLOCK, BLOCK, lanes),
            bf16_of(tokens, width),
            f32_of(packs, tokens // BLOCK, lanes),
        ],
        scratch_shapes=[
            pltpu.VMEM((held, rows, width), f32),
            pltpu.VMEM((held + 1, rows, width), low),
            pltpu.VMEM((2, mid, width), f32),
            pltpu.VMEM((2, mid, width), low),
            pltpu.VMEM((4, mid, width), low),
            pltpu.VMEM((long, width), low),
            pltpu.VMEM((n_shard - 1, long // n_shard, width), low),
            pltpu.VMEM((long // n_shard, width), low),
            pltpu.VMEM((long, width), low),
            pltpu.VMEM((n_shard * held, rows, width), low),
            pltpu.VMEM((9, rows, width), low),
            pltpu.VMEM((groups, long, width), low),
            pltpu.VMEM((3, width, width), low),
            pltpu.VMEM((16, width), f32),
            pltpu.VMEM((packs, tokens // BLOCK, BLOCK, lanes), low),
            pltpu.VMEM((packs, seq // BLOCK, BLOCK, lanes), low),
            pltpu.VMEM((packs, seq // BLOCK, BLOCK, lanes), low),
            pltpu.VMEM((packs, tokens, lanes), low),
            pltpu.VMEM((seq, lanes), f32),
            *[dma((n,)) for n in pairs for _ in range(2)],
            dma((4,)),
            dma((8,)),
        ],
        compiler_params=pltpu.CompilerParams(
            collective_id=0, has_side_effects=True, vmem_limit_bytes=62 << 20
        ),
        cost_estimate=pl.CostEstimate(
            flops=60_000_000_000, bytes_accessed=60 << 20, transcendentals=16_000_000
        ),
    )(slots, local_at, table, master, small_in, inputs)


def back_kernel(
    n_ctx,
    n_tp,
    n2_hbm,
    r2_ref,
    cot0_ref,
    cot1_ref,
    hid_ref,
    gel_ref,
    fit_ref,
    n1_ref,
    r1_ref,
    ctx_ref,
    small,
    up_w,
    down_w,
    wo,
    layer_ref,
    own_ref,
    x_ref,
    y_ref,
    xy_ref,
    gh1_ref,
    dctx_ref,
    sums_ref,
    home_ref,
    gy,
    gu,
    mixed,
    mixed_t,
    grads,
    arrived,
    send_sem,
    recv_sem,
    h_s,
    h_r,
    keep_sem,
):
    z, c, t = place_of()
    step = pl.program_id(0)
    tokens, width = gy.shape
    tiles = tokens // TILE
    rows = own_ref.shape[1]
    others = n_tp - 1
    side, core, bit = t // 2, lax.rem(t, 2), lax.rem(c, 2)

    def beside(dt):
        return (z, c, lax.rem(t + dt, n_tp))

    stays = c // 2 == core
    keep_layer = pltpu.make_async_copy(layer_ref.at[0], home_ref.at[bit], keep_sem.at[0])
    layer_moves = [
        send(
            layer_ref.at[p],
            home_ref.at[bit],
            (h_s, h_r),
            p,
            (z, 2 * core + (p ^ bit), 2 * side + c // 2),
        )
        for p in range(2)
    ]

    @pl.when(step == 0)
    def start():
        take = pltpu.make_async_copy(n2_hbm, gy, keep_sem.at[1])
        take.start()
        barrier = pltpu.get_barrier_semaphore()
        friends = [beside(dt) for dt in range(1, n_tp)]
        friends += [(z, c ^ m, t) for m in range(1, n_ctx)]
        friends += [(z, c ^ m, t ^ 1) for m in range(1, n_ctx)]
        for friend in friends:
            pl.semaphore_signal(barrier, inc=1, device_id=friend, device_id_type=MESH)
        pl.semaphore_wait(barrier, len(friends))

        @pl.when(stays)
        def kept():
            keep_layer.start()

        @pl.when(jnp.logical_not(stays))
        def left():
            layer_moves[0].start()

        layer_moves[1].start()
        sums_ref[...] = jnp.zeros_like(sums_ref)
        take.wait()
        mid = tokens // 2
        for p, cot_ref in enumerate((cot0_ref, cot1_ref)):

            def one(i, carry, p=p, cot_ref=cot_ref):
                inside = pl.ds(pl.multiple_of(i * TILE, TILE), TILE)
                at = pl.ds(pl.multiple_of((p ^ bit) * mid + i * TILE, TILE), TILE)
                cot = cot_ref[inside, :].astype(jnp.float32)
                n2 = gy[at, :]
                add_row(sums_ref, 10, cot * n2)
                add_row(sums_ref, 11, cot)
                gh2 = norm_back(cot, n2, r2_ref[at, 0:1], small[10:11, :])
                gy[at, :] = gh2
                low = gh2.astype(jnp.bfloat16)
                mixed[at, :] = low
                mixed_t[:, at] = low.T
                add_row(sums_ref, 9, low.astype(jnp.float32))
                return carry

            lax.fori_loop(0, mid // TILE, one, 0)

    def moves(b, count):
        slot = lax.rem(b, 2)
        return [
            send(
                grads.at[slot, :, lax.rem(t + dt, n_tp), 0:count],
                arrived.at[b, dt - 1, :, 0:count],
                (send_sem, recv_sem),
                b * others + dt - 1,
                beside(dt),
            )
            for dt in range(1, n_tp)
        ]

    def exchange(b, count):
        for copy in moves(b, count):
            copy.start()

    def keep(b, count):
        for copy in moves(b, count):
            copy.wait()
        slot = lax.rem(b, 2)
        for j, out in enumerate((own_ref, x_ref, y_ref, xy_ref)):
            for i in range(count):
                value = grads[slot, c ^ j, t, i]
                for dt in range(others):
                    value = value + arrived[b, dt, c ^ j, i]
                out[2 * b + i] = value

    def put(slot, i, value):
        low = value.astype(jnp.bfloat16)
        grads[slot, :, :, i] = low.reshape(n_ctx, n_tp, rows, width)

    @pl.when(step < 4)
    def ffn():
        up_block = matrix(up_w)
        down_block = matrix(down_w)
        slot = lax.rem(step, 2)

        def one(i, carry):
            at = pl.ds(pl.multiple_of(i * TILE, TILE), TILE)
            grad = wide_dot(mixed[at, :], down_block, NN) * gel_ref[0, at, :].astype(jnp.float32)
            low = grad.astype(jnp.bfloat16)
            gu[at, :] = low
            gy[at, :] += wide_dot(low, up_block, NT)
            sums_ref[pl.ds(5 + step, 1), :] += jnp.sum(
                low.astype(jnp.float32), axis=0, keepdims=True
            )
            return carry

        lax.fori_loop(0, tiles, one, 0)
        put(slot, 0, wide_dot(fit_ref[...], gu[...], NN))
        put(slot, 1, wide_dot(mixed_t[...], hid_ref[0], NN))
        exchange(step, 2)

    @pl.when(step > 0)
    def settle():
        keep(step - 1, 2)

    @pl.when(step == 4)
    def first_norm():
        def one(i, carry):
            at = pl.ds(pl.multiple_of(i * TILE, TILE), TILE)
            grad = gy[at, :]
            n1 = n1_ref[at, :]
            gh1 = norm_back(grad, n1, r1_ref[at, 0:1], small[3:4, :])
            gh1_ref[at, :] = gh1
            low = gh1.astype(jnp.bfloat16)
            gu[at, :] = low
            add_row(sums_ref, 2, low.astype(jnp.float32))
            add_row(sums_ref, 3, grad * n1)
            add_row(sums_ref, 4, grad)
            return carry

        lax.fori_loop(0, tiles, one, 0)
        put(0, 0, wide_dot(ctx_ref[...].T, gu[...], NN))
        exchange(4, 1)
        out_w = matrix(wo)

        def two(i, carry):
            at = pl.ds(pl.multiple_of(i * TILE, TILE), TILE)
            dctx_ref[at, :] = wide_dot(gu[at, :], out_w, NT).astype(jnp.bfloat16)
            return carry

        lax.fori_loop(0, tiles, two, 0)
        keep(4, 1)

        @pl.when(stays)
        def done():
            keep_layer.wait()

        @pl.when(jnp.logical_not(stays))
        def gone():
            layer_moves[0].wait()

        layer_moves[1].wait()


def back(n2, r2, cots, hid, gel, fit, n1, r1, ctx, small, rest, layer, n_ctx, n_tp):
    tokens, width = n2.shape
    rows = rest.shape[2]
    dma = pltpu.SemaphoreType.DMA

    def whole(shape):
        return pl.BlockSpec(shape, lambda b: (0,) * len(shape), pipeline_mode=pl.Buffered(1))

    def block(b):
        return (jnp.minimum(b, 3), 0, 0)

    def held(first, single=False):
        return pl.BlockSpec(
            (n_ctx * n_tp, 1, rows, width),
            (lambda b: (0, first, 0, 0))
            if single
            else (lambda b: (0, first + jnp.minimum(b, 3), 0, 0)),
            pipeline_mode=pl.Buffered(1) if single else None,
        )

    def out(shape):
        return pl.BlockSpec(shape, lambda b: (0,) * len(shape))

    return pl.pallas_call(
        functools.partial(back_kernel, n_ctx, n_tp),
        name="back",
        grid=(5,),
        in_specs=[
            pl.BlockSpec(memory_space=pl.ANY),
            whole((tokens, 128)),
            whole((tokens // 2, width)),
            whole((tokens // 2, width)),
            pl.BlockSpec((1, tokens, width), block),
            pl.BlockSpec((1, tokens, width), block),
            whole((width, tokens)),
            whole((tokens, width)),
            whole((tokens, 128)),
            whole((tokens, width)),
            whole(small.shape),
            held(1),
            held(5),
            held(0, True),
            pl.BlockSpec(memory_space=pl.ANY),
        ],
        out_specs=[
            *[out((9, rows, width))] * 4,
            out((tokens, width)),
            out((tokens, width)),
            out((16, width)),
            pl.BlockSpec(memory_space=pl.ANY),
        ],
        out_shape=[
            *[bf16_of(9, rows, width)] * 4,
            f32_of(tokens, width),
            bf16_of(tokens, width),
            f32_of(16, width),
            bf16_of(*layer.shape),
        ],
        scratch_shapes=[
            pltpu.VMEM((tokens, width), jnp.float32),
            pltpu.VMEM((tokens, width), jnp.bfloat16),
            pltpu.VMEM((tokens, width), jnp.bfloat16),
            pltpu.VMEM((width, tokens), jnp.bfloat16),
            pltpu.VMEM((2, n_ctx, n_tp, 2, rows, width), jnp.bfloat16),
            pltpu.VMEM((5, n_tp - 1, n_ctx, 2, rows, width), jnp.bfloat16),
            dma((5 * (n_tp - 1),)),
            dma((5 * (n_tp - 1),)),
            dma((2,)),
            dma((2,)),
            dma((2,)),
        ],
        compiler_params=pltpu.CompilerParams(
            collective_id=3, has_side_effects=True, vmem_limit_bytes=62 << 20
        ),
        cost_estimate=pl.CostEstimate(
            flops=22_000_000_000, bytes_accessed=40 << 20, transcendentals=0
        ),
    )(n2, r2, *cots, hid, gel, fit, n1, r1, ctx, small, rest, rest, rest, layer)


LATE = 3
EARLY = 9


def adam_update(weight, first, second, grad, decay, rate):
    count = float(STEP)
    first_new = beta_one * first + (1.0 - beta_one) * grad
    second_new = beta_two * second + (1.0 - beta_two) * grad * grad
    first_hat = first_new / (1.0 - beta_one**count)
    second_hat = second_new / (1.0 - beta_two**count)
    weight_new = weight - rate * (first_hat / (jnp.sqrt(second_hat) + adam_eps) + decay * weight)
    return (weight_new, first_new, second_new)


def finish_kernel(
    n_shard,
    n_ctx,
    n_tp,
    holder,
    late_at,
    x_hbm,
    dq_hbm,
    dk_hbm,
    dv_hbm,
    gh1_hbm,
    first_hbm,
    e0_hbm,
    e1_hbm,
    e2_hbm,
    e3_hbm,
    small_ref,
    w_ref,
    one_ref,
    two_ref,
    home_ref,
    w_out,
    one_out,
    two_out,
    small_out,
    x_s,
    dq_s,
    dk_s,
    dv_s,
    gh1_s,
    first_s,
    early,
    every,
    packed,
    slot_met,
    flipped,
    grads,
    arrived,
    partial,
    met,
    over,
    more,
    back_s,
    small_s,
    small_t,
    small_m,
    small_p,
    flat,
    flat_met,
    flat_sum,
    mine_s,
    pool,
    in_sem,
    c_s,
    c_r,
    p_s,
    p_r,
    o_s,
    o_r,
    h_s,
    h_r,
    sc_s,
    sc_r,
    sp_s,
    sp_r,
    e_s,
    e_r,
    a_s,
    a_r,
    b_s,
    b_r,
    keep_sem,
):
    z, c, t = place_of()
    side, core, bit = t // 2, lax.rem(t, 2), lax.rem(c, 2)
    _, mid, width = x_s.shape
    tokens = 2 * mid
    held, rows, _ = w_ref.shape
    per = n_ctx * n_tp // 2
    band = width // 2
    tile = mid // 2
    piece = mine_s.shape[0]

    loads = [
        pltpu.make_async_copy(src, dst, in_sem.at[i])
        for i, (src, dst) in enumerate(
            (
                (x_hbm, x_s),
                (dk_hbm, dk_s),
                (dv_hbm, dv_s),
                (dq_hbm, dq_s),
                (first_hbm, first_s),
                (gh1_hbm, gh1_s),
                (e0_hbm, early.at[0]),
                (e1_hbm, early.at[1]),
                (e2_hbm, early.at[2]),
                (e3_hbm, early.at[3]),
            )
        )
    ]
    for i in (6, 7, 8, 9, 0, 1, 2, 3, 4, 5):
        loads[i].start()

    def far(dz):
        return (lax.rem(z + dz, n_shard), c, t)

    def across(mask):
        return (z, c ^ mask, t)

    def beside(dt):
        return (z, c, lax.rem(t + dt, n_tp))

    barrier = pltpu.get_barrier_semaphore()
    friends = [far(dz) for dz in range(1, n_shard)]
    friends += [(z, c ^ m, t) for m in range(1, n_ctx)]
    friends += [beside(dt) for dt in range(1, n_tp)]
    friends += [(z, c ^ m, t ^ 1) for m in range(1, n_ctx)]
    for friend in friends:
        pl.semaphore_signal(barrier, inc=1, device_id=friend, device_id_type=MESH)

    for i in range(6, 10):
        loads[i].wait()
    every[0:EARLY] = early[0] + early[1] + early[2] + early[3]
    every[EARLY] = jnp.zeros_like(every[EARLY])
    for s in range(n_shard * held):
        packed[s // held, s % held] = every[holder[s]]
    pl.semaphore_wait(barrier, len(friends))
    slot_moves = [
        send(packed.at[far(dz)[0]], slot_met.at[dz - 1], (e_s, e_r), dz - 1, far(dz))
        for dz in range(1, n_shard)
    ]
    for copy in slot_moves:
        copy.start()

    core_moves = []

    def exchange(m):
        for dt in range(1, n_tp):
            other = lax.rem(t + dt, n_tp)
            for k in range(n_ctx):
                copy = send(
                    grads.at[k * n_tp + other, m],
                    arrived.at[dt - 1, k, m],
                    (c_s, c_r),
                    ((dt - 1) * n_ctx + k) * LATE + m,
                    beside(dt),
                )
                copy.start()
                core_moves.append((m, copy))

    plane_moves = []

    def meet(m):
        for which, copy in core_moves:
            if which == m:
                copy.wait_recv()
        for k in range(n_ctx):
            value = grads[k * n_tp + t, m]
            for dt in range(1, n_tp):
                value = value + arrived[dt - 1, k, m]
            partial[k, m] = value
        for j in range(1, n_ctx):
            copy = send(
                partial.at[c ^ j, m], met.at[j - 1, m], (p_s, p_r), (j - 1) * LATE + m, across(j)
            )
            copy.start()
            plane_moves.append(copy)

    loads[0].wait()
    for a in range(4):
        chunk = 2 * (core if a < 2 else 1 - core) + ((a % 2) ^ bit)
        flipped[:, pl.ds(pl.multiple_of(chunk * mid, mid), mid)] = x_s[a].T

    def weight_grad(m, left_at, right):
        def one(i, carry):
            left = flipped[pl.ds(pl.multiple_of(i * band, band), band), left_at]
            value = wide_dot(left, right[...], NN).astype(jnp.bfloat16)
            grads[pl.ds(i * per, per), m] = value.reshape(per, rows, width)
            return carry

        lax.fori_loop(0, 2, one, 0)

    loads[1].wait()
    weight_grad(1, slice(None), dk_s)
    exchange(1)
    loads[2].wait()
    weight_grad(2, slice(None), dv_s)
    exchange(2)
    meet(1)
    loads[3].wait()
    weight_grad(0, pl.ds(pl.multiple_of(core * tokens, tokens), tokens), dq_s)
    exchange(0)
    meet(2)

    row = lax.broadcasted_iota(jnp.int32, small_ref.shape, 0)
    q_sum = jnp.sum(dq_s[...].astype(jnp.float32), axis=0, keepdims=True)
    v_sum = jnp.sum(dv_s[...].astype(jnp.float32), axis=0, keepdims=True)
    sums = jnp.where(row == 0, q_sum, jnp.where(row == 1, v_sum, small_ref[...]))
    small_s[...] = sums.astype(jnp.bfloat16)
    small_core = [
        send(small_s, small_t.at[dt - 1], (sc_s, sc_r), dt - 1, beside(dt)) for dt in range(1, n_tp)
    ]
    for copy in small_core:
        copy.start()

    loads[4].wait()

    def weight(m):
        return first_s[:, m * rows : (m + 1) * rows, :].reshape(width, width)

    wq, wk, wv = weight(0), weight(1), weight(2)
    over_moves = []
    for b in range(2):
        at = pl.ds(pl.multiple_of((1 - core) * tokens + b * mid, mid), mid)
        value = wide_dot(dk_s[at, :], wk, NT) + wide_dot(dv_s[at, :], wv, NT)
        over[b] = value.astype(jnp.bfloat16)
        copy = send(over.at[b], more.at[b], (o_s, o_r), b, (z, c, t ^ 1))
        copy.start()
        over_moves.append(copy)
        if b == 0:
            meet(0)

    value = small_s[...]
    for dt, copy in enumerate(small_core):
        copy.wait_recv()
        value = value + small_t[dt]
    small_m[...] = value
    small_plane = [
        send(small_m, small_p.at[j - 1], (sp_s, sp_r), j - 1, across(j)) for j in range(1, n_ctx)
    ]
    for copy in small_plane:
        copy.start()

    loads[5].wait()
    stays = c // 2 == core
    home_moves = []
    for copy in over_moves:
        copy.wait_recv()
    keep = pltpu.make_async_copy(back_s.at[0], home_ref.at[bit], keep_sem.at[0])
    for move in range(2):
        chunk = move ^ bit
        for i in range(2):
            at = pl.ds(pl.multiple_of(core * tokens + chunk * mid + i * tile, tile), tile)
            here = pl.ds(pl.multiple_of(chunk * mid + i * tile, tile), tile)
            value = gh1_s[here, :]
            value = value + more[chunk, i * tile : (i + 1) * tile, :].astype(jnp.float32)
            value = value + wide_dot(dq_s[here, :], wq, NT)
            value = value + wide_dot(dk_s[at, :], wk, NT)
            value = value + wide_dot(dv_s[at, :], wv, NT)
            back_s[move, i * tile : (i + 1) * tile, :] = value.astype(jnp.bfloat16)
        target = (z, 2 * core + chunk, 2 * side + c // 2)
        home_moves.append(send(back_s.at[move], home_ref.at[bit], (h_s, h_r), move, target))
        if move == 0:

            @pl.when(stays)
            def kept():
                keep.start()

            @pl.when(jnp.logical_not(stays))
            def left():
                home_moves[0].start()

        else:
            home_moves[1].start()

    flat[...] = jnp.zeros_like(flat)
    for copy in plane_moves:
        copy.wait_recv()
    for m in range(LATE):
        value = partial[c, m]
        for j in range(n_ctx - 1):
            value = value + met[j, m]
        flat[m * rows : (m + 1) * rows, :] = value
    value = small_m[...]
    for j, copy in enumerate(small_plane):
        copy.wait_recv()
        value = value + small_p[j]
    small_rows = small_s.shape[0]
    flat[LATE * rows : LATE * rows + small_rows, :] = value

    def piece_at(k):
        return pl.ds(pl.multiple_of(k * piece, piece), piece)

    flat_out = [
        send(flat.at[piece_at(far(dz)[0])], flat_met.at[dz - 1], (a_s, a_r), dz - 1, far(dz))
        for dz in range(1, n_shard)
    ]
    for copy in flat_out:
        copy.start()
    total = flat[piece_at(z), :].astype(jnp.float32)
    for dz, copy in enumerate(flat_out):
        copy.wait_recv()
        total = total + flat_met[dz].astype(jnp.float32)
    mine_s[...] = total.astype(jnp.bfloat16)
    flat_back = [
        send(mine_s, flat_sum.at[piece_at(z)], (b_s, b_r), dz - 1, far(dz))
        for dz in range(1, n_shard)
    ]
    for copy in flat_back:
        copy.start()
    flat_sum[piece_at(z), :] = mine_s[...]
    for copy in slot_moves:
        copy.wait_recv()
    for copy in flat_back:
        copy.wait_recv()
    for m in range(LATE):
        pool[m] = flat_sum[m * rows : (m + 1) * rows, :]
    pool[LATE] = jnp.zeros_like(pool[LATE])
    for j in range(held):
        grad = packed[z, j].astype(jnp.float32)
        for dz in range(n_shard - 1):
            grad = grad + slot_met[dz, j].astype(jnp.float32)
        grad = grad + pool[late_at[z * held + j]].astype(jnp.float32)
        w, one, two = adam_update(w_ref[j], one_ref[j], two_ref[j], grad, 0.01, rate_value)
        w_out[j] = w
        one_out[j] = one
        two_out[j] = two
    small_out[...] = flat_sum[LATE * rows : LATE * rows + small_rows, :].astype(jnp.float32)

    @pl.when(stays)
    def done():
        keep.wait()

    @pl.when(jnp.logical_not(stays))
    def gone():
        home_moves[0].wait()

    home_moves[1].wait()
    for _, copy in core_moves:
        copy.wait_send()
    for copy in (
        *plane_moves,
        *over_moves,
        *small_core,
        *small_plane,
        *slot_moves,
        *flat_out,
        *flat_back,
    ):
        copy.wait_send()


def finish(
    holder,
    late_at,
    x_all,
    dq,
    dk,
    dv,
    gh1,
    first,
    early,
    small,
    master,
    one,
    two,
    n_shard,
    n_ctx,
    n_tp,
):
    _, mid, width = x_all.shape
    held, rows, _ = master.shape
    groups = n_ctx * n_tp
    span = 16 * n_shard
    long = -(-(LATE * rows + small.shape[0]) // span) * span
    smem = pl.BlockSpec(memory_space=pltpu.SMEM)
    anywhere = pl.BlockSpec(memory_space=pl.ANY)
    vmem = pl.BlockSpec(memory_space=pltpu.VMEM)
    dma = pltpu.SemaphoreType.DMA
    low = jnp.bfloat16
    pairs = [LATE * n_ctx * (n_tp - 1), LATE * (n_ctx - 1), 2, 2, n_tp - 1, n_ctx - 1]
    pairs += [n_shard - 1] * 3
    stored = f32_of(held, rows, width)
    shapes = [
        x_all.shape,
        dq.shape,
        dk.shape,
        dv.shape,
        None,
        first.shape,
        (4, EARLY, rows, width),
        (EARLY + 1, rows, width),
        (n_shard, held, rows, width),
        (n_shard - 1, held, rows, width),
        (width, 4 * mid),
        (groups, LATE, rows, width),
        (n_tp - 1, n_ctx, LATE, rows, width),
        (n_ctx, LATE, rows, width),
        (n_ctx - 1, LATE, rows, width),
        (2, mid, width),
        (2, mid, width),
        (2, mid, width),
        small.shape,
        (n_tp - 1, *small.shape),
        small.shape,
        (n_ctx - 1, *small.shape),
        (long, width),
        (n_shard - 1, long // n_shard, width),
        (long, width),
        (long // n_shard, width),
        (LATE + 1, rows, width),
    ]
    return pl.pallas_call(
        functools.partial(finish_kernel, n_shard, n_ctx, n_tp),
        name="finish",
        in_specs=[smem] * 2 + [anywhere] * 10 + [vmem] * 4,
        out_specs=[anywhere] + [vmem] * 4,
        out_shape=[bf16_of(2, mid, width), stored, stored, stored, f32_of(*small.shape)],
        scratch_shapes=[
            pltpu.VMEM(s, low) if s else pltpu.VMEM(gh1.shape, jnp.float32) for s in shapes
        ]
        + [dma((10,))]
        + [dma((n,)) for n in pairs for _ in range(2)]
        + [dma((1,))],
        compiler_params=pltpu.CompilerParams(
            collective_id=1, has_side_effects=True, vmem_limit_bytes=63 << 20
        ),
        cost_estimate=pl.CostEstimate(
            flops=12_000_000_000, bytes_accessed=40 << 20, transcendentals=0
        ),
    )(holder, late_at, x_all, dq, dk, dv, gh1, first, *early, small, master, one, two)


def moves(n_ctx, n_tp, pick):
    pairs = []
    for c in range(n_ctx):
        for t in range(n_tp):
            side, core = t // 2, t % 2
            to_ctx = 2 * core + (pick ^ (c & 1))
            to_tp = 2 * side + c // 2
            pairs.append((c * n_tp + t, to_ctx * n_tp + to_tp))
    return pairs


def shards(
    inputs,
    cotangent,
    rand_blocks,
    slot_of,
    master,
    moment_one,
    moment_two,
    small_params,
    small_one,
    small_two,
):
    n_shard = lax.axis_size("shard")
    n_ctx = lax.axis_size("ctx")
    n_tp = lax.axis_size("tp")
    groups = n_ctx * n_tp
    held, rows, width = master.shape
    span = small_params.shape[0]
    my_ctx = lax.axis_index("ctx")
    my_tp = lax.axis_index("tp")
    parity = lax.rem(my_ctx, 2)
    half = lax.rem(my_tp, 2)
    plane = ("ctx", "tp")
    forth = [moves(n_ctx, n_tp, pick) for pick in range(2)]

    arrival = [(b ^ parity) + 2 * (half ^ (j // 2)) for j, b in enumerate((0, 1, 0, 1))]
    info = jnp.stack([half, *arrival]).astype(jnp.int32)
    half_one = info[:1]

    def sent(field, pick):
        low = field.astype(jnp.bfloat16)
        return jnp.where(parity == 0, low[pick], low[1 - pick])

    my_shard = lax.axis_index("shard")
    start = ((my_shard * n_ctx + my_ctx) * n_tp + my_tp) * span
    lone = lax.dynamic_update_slice(
        jnp.zeros((16 * width,), jnp.float32), small_params, (start,)
    ).reshape(16, width)
    local_at = slot_of[:LATE] - my_shard * held
    local_at = jnp.where((local_at >= 0) & (local_at < held), local_at, held)
    x_all, first, rest, small, q, k, v, context, lse = begin(
        slot_of, local_at, rand_blocks, master, lone, inputs, n_shard, n_ctx, n_tp
    )
    cots, context = lax.optimization_barrier(
        ([sent(cotangent, pick) for pick in range(2)], context)
    )
    cots = [lax.ppermute(cots[pick], plane, forth[pick]) for pick in range(2)]
    out_low, n1, r1, fit, hid, gel, n2, r2 = front(info, context, x_all, small, rest)
    *early, gh1, dctx, sums, layer_home = back(
        n2, r2, cots, hid, gel, fit, n1, r1, context, small, rest, out_low, n_ctx, n_tp
    )
    for j in range(1, n_ctx):
        crossing = [
            (a * n_tp + b, (a ^ j) * n_tp + b) for a in range(n_ctx) for b in range(n_tp)
        ]
        early[j] = lax.ppermute(early[j], plane, crossing)
    dq, dk, dv = attend_back(half_one, rand_blocks, q, k, v, lse, dctx, 5)
    stands = jnp.array([8, 0, 2, 4, 6, 1, 3, 5, 7], jnp.int32)
    slots_all = jnp.arange(n_shard * held, dtype=jnp.int32)
    hits = slot_of[None, :] == slots_all[:, None]
    holder = EARLY + jnp.sum(jnp.where(hits[:, LATE:], stands[None, :] - EARLY, 0), axis=1)
    ranks = jnp.arange(LATE, dtype=jnp.int32)[None, :]
    late_at = LATE + jnp.sum(jnp.where(hits[:, :LATE], ranks - LATE, 0), axis=1)
    came, master_new, first_new, second_new, small_sum = finish(
        holder.astype(jnp.int32),
        late_at.astype(jnp.int32),
        x_all,
        dq,
        dk,
        dv,
        gh1,
        first,
        early,
        sums,
        master,
        moment_one,
        moment_two,
        n_shard,
        n_ctx,
        n_tp,
    )
    layer_out = layer_home.astype(jnp.float32)
    input_grad = came.astype(jnp.float32)
    small_owned = lax.dynamic_slice_in_dim(small_sum.reshape(-1), start, span)
    small_new, small_first, small_second = adam_update(
        small_params, small_one, small_two, small_owned, 0.0, small_rate
    )
    return (
        layer_out,
        input_grad,
        master_new,
        first_new,
        second_new,
        small_new,
        small_first,
        small_second,
    )


def solution(mesh):
    tokens = P(("shard", "tp"), "ctx", None)
    stored = P("shard", ("ctx", "tp"), None)
    spread = P(("shard", "ctx", "tp"))
    return jax.shard_map(
        shards,
        mesh=mesh,
        in_specs=(tokens, tokens, P(), P(), stored, stored, stored, spread, spread, spread),
        out_specs=(tokens, tokens, stored, stored, stored, spread, spread, spread),
        check_vma=False,
    )
```

```python
import functools

import jax
import jax.numpy as jnp
from jax import lax
from jax.experimental import pallas as pl
from jax.experimental.pallas import tpu as pltpu
from jax.sharding import PartitionSpec as P

STEP = 5
norm_eps = 1e-12
beta_one = 0.9
beta_two = 0.999
adam_eps = 1e-08
rate_value = 0.04
small_rate = 0.25
score_scale = 0.125
gelu_root = 0.7978845608
gelu_cube = 0.044715

BLOCK = 64
HEAD = 64
PACK = 4
masked_score = -1e30


def wide_dot(a, b, dims):
    return lax.dot_general(a, b, (dims, ((), ())), preferred_element_type=jnp.float32)


def head_masks(rows):
    lane = lax.broadcasted_iota(jnp.int32, (rows, PACK * HEAD), 1) // HEAD
    return [lane == h for h in range(PACK)]


def spread_heads(block, masks):
    zero = jnp.zeros_like(block)
    return jnp.concatenate([jnp.where(m, block, zero) for m in masks], axis=0)


def own_heads(full, masks):
    total = None
    for h, m in enumerate(masks):
        piece = jnp.where(m, full[h * BLOCK : (h + 1) * BLOCK], 0.0)
        total = piece if total is None else total + piece
    return total


def rows_of(ref, index, count=1):
    return ref[pl.ds(index, count)].reshape(count * BLOCK, ref.shape[2])


def flat_rows(ref, index):
    return ref[pl.ds(pl.multiple_of(index * BLOCK, BLOCK), BLOCK), :]


def picked_rows(ref, picks, low_half):
    halves = []
    for pair in range(PACK // 2):
        cols = slice(pair * 2 * HEAD, (pair + 1) * 2 * HEAD)
        first = ref[picks[2 * pair], :, cols]
        second = ref[picks[2 * pair + 1], :, cols]
        halves.append(jnp.where(low_half, first, second))
    return jnp.concatenate(halves, axis=1)


def gathered(ref, block, last, picks, low_half):
    pieces = [rows_of(ref, 0), rows_of(ref, last), rows_of(ref, block - 1, 3)]
    pieces += [picked_rows(ref, p, low_half) for p in picks]
    return jnp.concatenate(pieces, axis=0)


def middle_scores(keys, spread, block, last):
    scores = wide_dot(keys, spread, ((1,), (1,)))
    first_off = jnp.where(block == 1, masked_score, 0.0)
    last_off = jnp.where(block == last - 1, masked_score, 0.0)
    b = BLOCK
    return jnp.concatenate(
        [
            scores[: 2 * b],
            scores[2 * b : 3 * b] + first_off,
            scores[3 * b : 4 * b],
            scores[4 * b : 5 * b] + last_off,
            scores[5 * b :],
        ],
        axis=0,
    )


def attend_back_kernel(
    unroll,
    half_ref,
    table_ref,
    q_ref,
    k_ref,
    v_ref,
    lse_ref,
    do_ref,
    dq_ref,
    dk_ref,
    dv_ref,
    dk_acc,
    dv_acc,
    kept_p,
    kept_g,
):
    half = half_ref[0]
    group = pl.program_id(0)
    q_ref, k_ref, v_ref = q_ref.at[0], k_ref.at[0], v_ref.at[0]
    nblocks, local = k_ref.shape[0], q_ref.shape[0]
    last = nblocks - 1
    picks_each = table_ref.shape[2]
    masks = head_masks(BLOCK)
    low_half = lax.broadcasted_iota(jnp.int32, (BLOCK, 2 * HEAD), 1) < HEAD
    span = 8 * BLOCK
    chunks = nblocks // 8

    edge = (local - 1) * half
    spread = spread_heads(rows_of(q_ref, edge), masks)
    spread_do = spread_heads(flat_rows(do_ref, edge), masks)
    lse = lse_ref[0, pl.ds(edge, 1), :]
    delta = None
    for c in range(chunks):
        rows = slice(c * span, (c + 1) * span)
        probs = jnp.exp(wide_dot(rows_of(k_ref, c * 8, 8), spread, ((1,), (1,))) - lse)
        gp = wide_dot(rows_of(v_ref, c * 8, 8), spread_do, ((1,), (1,)))
        kept_p[rows, :] = probs
        kept_g[rows, :] = gp
        part = jnp.sum(probs * gp, axis=0, keepdims=True)
        delta = part if delta is None else delta + part
    full = None
    for c in range(chunks):
        rows = slice(c * span, (c + 1) * span)
        probs = kept_p[rows, :]
        ds = (probs * (kept_g[rows, :] - delta)).astype(jnp.bfloat16)
        dv_acc[rows, :] = wide_dot(probs.astype(jnp.bfloat16), spread_do, ((1,), (0,)))
        dk_acc[rows, :] = wide_dot(ds, spread, ((1,), (0,)))
        part = wide_dot(ds, rows_of(k_ref, c * 8, 8), ((0,), (0,)))
        full = part if full is None else full + part
    dq_ref[pl.ds(pl.multiple_of(edge * BLOCK, BLOCK), BLOCK), :] = (
        own_heads(full, masks) * 0.125
    ).astype(jnp.bfloat16)

    def scatter(acc, piece, block, picks):
        b = BLOCK
        acc[0:b, :] += piece[:b]
        acc[last * b : (last + 1) * b, :] += piece[b : 2 * b]
        window = pl.ds(pl.multiple_of((block - 1) * b, b), 3 * b)
        acc[window, :] += piece[2 * b : 5 * b]
        for r, p in enumerate(picks):
            part = piece[(5 + r) * b : (6 + r) * b]
            for pair in range(PACK // 2):
                lanes = slice(pair * 2 * HEAD, (pair + 1) * 2 * HEAD)
                cols = pl.ds(pair * 2 * HEAD, 2 * HEAD)
                sub = part[:, lanes]
                acc[pl.ds(pl.multiple_of(p[2 * pair] * b, b), b), cols] += jnp.where(
                    low_half, sub, 0.0
                )
                acc[pl.ds(pl.multiple_of(p[2 * pair + 1] * b, b), b), cols] += jnp.where(
                    low_half, 0.0, sub
                )

    def middle(step, carry):
        mine = step + 1 - half
        block = mine + local * half
        picks = [
            [table_ref[group * PACK + h, block - 1, r] for h in range(PACK)]
            for r in range(picks_each)
        ]
        spread = spread_heads(rows_of(q_ref, mine), masks)
        spread_do = spread_heads(flat_rows(do_ref, mine), masks)
        keys = gathered(k_ref, block, last, picks, low_half)
        values = gathered(v_ref, block, last, picks, low_half)
        scores = middle_scores(keys, spread, block, last)
        probs = jnp.exp(scores - lse_ref[0, pl.ds(mine, 1), :])
        gp = wide_dot(values, spread_do, ((1,), (1,)))
        delta = jnp.sum(probs * gp, axis=0, keepdims=True)
        ds = (probs * (gp - delta)).astype(jnp.bfloat16)
        low = probs.astype(jnp.bfloat16)
        scatter(dv_acc, wide_dot(low, spread_do, ((1,), (0,))), block, picks)
        scatter(dk_acc, wide_dot(ds, spread, ((1,), (0,))), block, picks)
        full = wide_dot(ds, keys, ((0,), (0,)))
        dq_ref[pl.ds(pl.multiple_of(mine * BLOCK, BLOCK), BLOCK), :] = (
            own_heads(full, masks) * 0.125
        ).astype(jnp.bfloat16)
        return carry

    lax.fori_loop(0, local - 1, middle, 0, unroll=unroll)
    dk_ref[...] = dk_acc[...].astype(jnp.bfloat16)
    dv_ref[...] = dv_acc[...].astype(jnp.bfloat16)


def attend_back(half, table, q, k, v, lse, do, unroll=3):
    tokens, width = do.shape
    groups, nblocks, _, lanes = k.shape
    seq = nblocks * BLOCK
    blocks = tokens // BLOCK
    mine = pl.BlockSpec((tokens, lanes), lambda g, *_: (0, g))
    whole = pl.BlockSpec((seq, lanes), lambda g, *_: (0, g))
    spec = pltpu.PrefetchScalarGridSpec(
        num_scalar_prefetch=2,
        grid=(groups,),
        in_specs=[
            pl.BlockSpec((1, blocks, BLOCK, lanes), lambda g, *_: (g, 0, 0, 0)),
            pl.BlockSpec((1, nblocks, BLOCK, lanes), lambda g, *_: (g, 0, 0, 0)),
            pl.BlockSpec((1, nblocks, BLOCK, lanes), lambda g, *_: (g, 0, 0, 0)),
            pl.BlockSpec((1, blocks, lanes), lambda g, *_: (g, 0, 0)),
            mine,
        ],
        out_specs=[mine, whole, whole],
        scratch_shapes=[pltpu.VMEM((seq, lanes), jnp.float32)] * 4,
    )
    return pl.pallas_call(
        functools.partial(attend_back_kernel, unroll),
        grid_spec=spec,
        out_shape=[
            jax.ShapeDtypeStruct((tokens, width), jnp.bfloat16),
            jax.ShapeDtypeStruct((seq, width), jnp.bfloat16),
            jax.ShapeDtypeStruct((seq, width), jnp.bfloat16),
        ],
        name="attend_back",
        compiler_params=pltpu.CompilerParams(vmem_limit_bytes=56 << 20),
        cost_estimate=pl.CostEstimate(
            flops=120_000_000_000, bytes_accessed=24 << 20, transcendentals=16_000_000
        ),
    )(half, table, q, k, v, lse, do)


TILE = 256
MID = 512


def cols_mean(value):
    return jnp.mean(value, axis=-1, keepdims=True)


def normed(field):
    centred = field - cols_mean(field)
    rate = lax.rsqrt(cols_mean(centred * centred) + norm_eps)
    return centred * rate, rate


def norm_back(cot, normal, rate, gain):
    dn = cot * gain
    return rate * (dn - cols_mean(dn) - normal * cols_mean(dn * normal))


def matrix(ref):
    value = ref[...]
    return value.reshape(-1, value.shape[-1])


def add_row(ref, row, value):
    ref[row : row + 1, :] += jnp.sum(value, axis=0, keepdims=True)


def rest_spec(rest, which, single=True):
    groups, _, rows, width = rest.shape
    mode = pl.Buffered(1) if single else None
    return pl.BlockSpec(
        (groups, 1, rows, width), lambda step, info: (0, which(step) - 3, 0, 0), pipeline_mode=mode
    )


def fixed(shape):
    return pl.BlockSpec(shape, lambda step, info: (0,) * len(shape), pipeline_mode=pl.Buffered(1))


def call(kernel, name, info, grid, in_specs, out_specs, out_shape, scratch, args, flops, moved):
    return pl.pallas_call(
        kernel,
        name=name,
        grid_spec=pltpu.PrefetchScalarGridSpec(
            num_scalar_prefetch=1,
            grid=(grid,),
            in_specs=in_specs,
            out_specs=out_specs,
            scratch_shapes=scratch,
        ),
        out_shape=out_shape,
        compiler_params=pltpu.CompilerParams(vmem_limit_bytes=60 << 20),
        cost_estimate=pl.CostEstimate(
            flops=flops, bytes_accessed=moved, transcendentals=0
        ),
    )(info, *args)


def bf16_of(*shape):
    return jax.ShapeDtypeStruct(shape, jnp.bfloat16)


def f32_of(*shape):
    return jax.ShapeDtypeStruct(shape, jnp.float32)


NN = ((1,), (0,))
NT = ((1,), (1,))
TN = ((0,), (0,))


def front_kernel(
    info,
    ctx_ref,
    x_ref,
    small,
    wo,
    u0,
    u1,
    u2,
    u3,
    v0,
    v1,
    v2,
    v3,
    out_ref,
    n1_ref,
    r1_ref,
    fit_ref,
    hid_ref,
    gel_ref,
    n2_ref,
    r2_ref,
):
    attn_out = wide_dot(ctx_ref[...], matrix(wo), NN) + small[2:3, :]
    n1, r1 = normed(x_ref[0].astype(jnp.float32) + attn_out)
    n1_ref[...] = n1
    r1_ref[...] = jnp.broadcast_to(r1, r1_ref.shape)
    after = n1 * small[3:4, :] + small[4:5, :]
    ffn_in = after.astype(jnp.bfloat16)
    fit_ref[...] = ffn_in.T
    total = after + small[9:10, :]
    for b, (up_w, down_w) in enumerate(((u0, v0), (u1, v1), (u2, v2), (u3, v3))):
        up = wide_dot(ffn_in, matrix(up_w), NN) + small[5 + b : 6 + b, :]
        square = up * up
        bent = jnp.tanh(gelu_root * up * (1.0 + gelu_cube * square))
        rise = 0.5 * (1.0 + bent)
        hidden = (up * rise).astype(jnp.bfloat16)
        hid_ref[b] = hidden
        slope = rise + (0.5 * gelu_root) * up * (1.0 - bent * bent) * (
            1.0 + (3.0 * gelu_cube) * square
        )
        gel_ref[b] = slope.astype(jnp.bfloat16)
        total = total + wide_dot(hidden, matrix(down_w), NT)
    n2, r2 = normed(total)
    out_ref[0] = (n2 * small[10:11, :] + small[11:12, :]).astype(jnp.bfloat16)
    n2_ref[...] = n2
    r2_ref[...] = jnp.broadcast_to(r2, r2_ref.shape)


def front(info, ctx, x_all, small, rest):
    tokens, width = ctx.shape
    mid = x_all.shape[1]
    per = mid // TILE
    steps = tokens // TILE

    def arrived(t, info):
        return (info[1 + 2 * info[0] + t // per], t % per, 0)

    def rows(dtype_shape):
        return pl.BlockSpec(dtype_shape, lambda t, info: (t, 0))

    specs = [rest_spec(rest, lambda t, m=m: m) for m in range(3, 12)]
    wide4 = pl.BlockSpec((4, TILE, width), lambda t, info: (0, t, 0))
    flipped = pl.BlockSpec((width, TILE), lambda t, info: (0, t))
    return call(
        front_kernel,
        "front",
        info,
        steps,
        [
            rows((TILE, width)),
            pl.BlockSpec((1, TILE, width), arrived),
            fixed(small.shape),
            *specs,
        ],
        [
            pl.BlockSpec((1, TILE, width), arrived),
            rows((TILE, width)),
            rows((TILE, 128)),
            flipped,
            wide4,
            wide4,
            rows((TILE, width)),
            rows((TILE, 128)),
        ],
        [
            bf16_of(2, mid, width),
            f32_of(tokens, width),
            f32_of(tokens, 128),
            bf16_of(width, tokens),
            bf16_of(4, tokens, width),
            bf16_of(4, tokens, width),
            f32_of(tokens, width),
            f32_of(tokens, 128),
        ],
        [],
        (ctx, x_all, small, *([rest] * 9)),
        11_000_000_000,
        40 << 20,
    )


MESH = pl.DeviceIdType.MESH
KINDS = 3
CHUNKS = 3
PER = 3


def place_of():
    c, t = lax.axis_index("ctx"), lax.axis_index("tp")
    return lax.axis_index("shard"), c, t


def send(src, dst, sems, index, target):
    send_sems, recv_sems = sems
    return pltpu.make_async_remote_copy(
        src_ref=src,
        dst_ref=dst,
        send_sem=send_sems.at[index],
        recv_sem=recv_sems.at[index],
        device_id=target,
        device_id_type=MESH,
    )


def begin_kernel(
    n_shard,
    n_ctx,
    n_tp,
    slots,
    local_at,
    table,
    master_hbm,
    small_in,
    input_hbm,
    x_ref,
    first_ref,
    rest_ref,
    small_ref,
    q_ref,
    k_ref,
    v_ref,
    ctx_ref,
    lse_ref,
    raw,
    low,
    given,
    xs,
    x_all,
    part,
    got,
    mine,
    total,
    pool,
    sel,
    first,
    weights,
    small,
    q_s,
    k_s,
    v_s,
    ctx_s,
    kept,
    x_s,
    x_r,
    xt_s,
    xt_r,
    za_s,
    za_r,
    zb_s,
    zb_r,
    zc_s,
    zc_r,
    zd_s,
    zd_r,
    qm_s,
    qm_r,
    qt_s,
    qt_r,
    r_s,
    r_r,
    rt_s,
    rt_r,
    own_sem,
    out_sem,
):
    z, c, t = place_of()
    side, core, bit = t // 2, lax.rem(t, 2), lax.rem(c, 2)
    held, rows, width = low.shape[0] - 1, low.shape[1], low.shape[2]
    piece = mine.shape[0]
    me = c * n_tp + t
    _, mid, _ = xs.shape
    nblocks = 4 * mid // BLOCK
    local = nblocks // 2
    lanes = PACK * HEAD
    groups = width // lanes
    others = n_tp - 1

    take_raw = pltpu.make_async_copy(master_hbm, raw, own_sem.at[0])
    take_given = pltpu.make_async_copy(input_hbm, given, own_sem.at[1])
    take_raw.start()
    take_given.start()

    def far(dz):
        return (lax.rem(z + dz, n_shard), c, t)

    def across(mask):
        return (z, c ^ mask, t)

    def beside(dt):
        return (z, c, lax.rem(t + dt, n_tp))

    barrier = pltpu.get_barrier_semaphore()
    friends = [far(dz) for dz in range(1, n_shard)]
    friends += [(z, c ^ m, t) for m in range(1, n_ctx)]
    friends += [beside(dt) for dt in range(1, n_tp)]
    friends += [(z, c ^ m, t ^ 1) for m in range(1, n_ctx)]
    for friend in friends:
        pl.semaphore_signal(barrier, inc=1, device_id=friend, device_id_type=MESH)

    take_raw.wait()
    for j in range(held):
        low[j] = raw[j].astype(jnp.bfloat16)
    low[held] = jnp.zeros_like(low[held])
    part[...] = jnp.zeros_like(part)
    for m in range(KINDS):
        part[m * rows : (m + 1) * rows, :] = low[local_at[m]]
    part[KINDS * rows : KINDS * rows + 16, :] = small_in[...].astype(jnp.bfloat16)
    pl.semaphore_wait(barrier, len(friends))

    def piece_at(k):
        return pl.ds(pl.multiple_of(k * piece, piece), piece)

    za = [
        send(part.at[piece_at(far(dz)[0])], got.at[dz - 1], (za_s, za_r), dz - 1, far(dz))
        for dz in range(1, n_shard)
    ]
    for copy in za:
        copy.start()

    stays = c // 2 == core
    goes = [(z, 2 * core + (p ^ bit), 2 * side + c // 2) for p in range(2)]
    x_moves = [send(xs.at[p], x_all.at[p], (x_s, x_r), p, goes[p]) for p in range(2)]
    x_keep = pltpu.make_async_copy(xs.at[0], x_all.at[0], own_sem.at[2])
    take_given.wait()
    xs[0] = given[bit].astype(jnp.bfloat16)

    @pl.when(stays)
    def keep():
        x_keep.start()

    @pl.when(jnp.logical_not(stays))
    def leave():
        x_moves[0].start()

    xs[1] = given[1 - bit].astype(jnp.bfloat16)
    x_moves[1].start()

    summed = part[piece_at(z), :]
    for dz, copy in enumerate(za):
        copy.wait_recv()
        summed = summed + got[dz]
    mine[...] = summed
    zb = [
        send(mine, total.at[piece_at(z)], (zb_s, zb_r), dz - 1, far(dz))
        for dz in range(1, n_shard)
    ]
    for copy in zb:
        copy.start()
    total[piece_at(z), :] = summed
    pool_here = pl.ds(z * held, held)

    def hop_copy(s, way):
        sems = (zc_s, zc_r) if way > 0 else (zd_s, zd_r)
        slot = pl.ds((z - way * (s - 1)) * held, held)
        return send(
            pool.at[slot], pool.at[slot], sems, s - 1, (lax.rem(z + way + n_shard, n_shard), c, t)
        )

    def hop_on(s, way):
        start = z - way * (s - 1)
        end = z + way
        return (start >= 0) & (start < n_shard) & (end >= 0) & (end < n_shard)

    def hop(s):
        for way in (1, -1):

            @pl.when(hop_on(s, way))
            def move(way=way):
                if s > 1:
                    hop_copy(s - 1, way).wait_recv()
                hop_copy(s, way).start()

    def hops_end():
        for way, end in ((1, n_shard - 1), (-1, 0)):

            @pl.when(z == end)
            def gather(way=way):
                for s in range(1, n_shard):
                    hop_copy(s, way).wait_recv()

    def hops_sent():
        for s in range(1, n_shard):
            for way in (1, -1):

                @pl.when(hop_on(s, way))
                def sent(s=s, way=way):
                    hop_copy(s, way).wait_send()

    pool[pool_here] = low[0:held]
    for copy in zb:
        copy.wait_recv()

    q_moves = [
        send(total, first.at[me], (qm_s, qm_r), k, across(m)) for k, m in enumerate((1, 2, 3))
    ]
    for copy in q_moves:
        copy.start()
    hop(1)
    qt_moves = [
        send(total, first.at[me], (qt_s, qt_r), dt - 1, beside(dt)) for dt in range(1, n_tp)
    ]
    for copy in qt_moves:
        copy.start()
    first[me] = total[...]

    x_over = [
        send(x_all.at[p], x_all.at[2 + p], (xt_s, xt_r), p, (z, c, t ^ 1)) for p in range(2)
    ]

    @pl.when(stays)
    def stayed():
        x_keep.wait()

    @pl.when(jnp.logical_not(stays))
    def came():
        x_moves[0].wait_recv()

    x_over[0].start()
    x_moves[1].wait_recv()
    x_over[1].start()

    for k, m in enumerate((1, 2, 3)):
        q_moves[k].wait_recv()
        place = (c ^ m) * n_tp + t
        for dt in range(1, n_tp):
            copy = send(
                first.at[place],
                first.at[place],
                (qt_s, qt_r),
                (k + 1) * others + dt - 1,
                beside(dt),
            )
            copy.start()
            qt_moves.append(copy)
        if k == 1:
            hop(2)
    for copy in qt_moves:
        copy.wait_recv()
    for s in range(3, n_shard):
        hop(s)
    outs = [pltpu.make_async_copy(first, first_ref, out_sem.at[0])]
    outs[0].start()

    sums = None
    for g in range(n_ctx * n_tp):
        here = first[g, KINDS * rows : KINDS * rows + 16, :].astype(jnp.float32)
        sums = here if sums is None else sums + here
    small[...] = sums
    small_ref[...] = sums
    for m in range(KINDS):
        weights[m] = first[:, m * rows : (m + 1) * rows, :].reshape(width, width)

    def split(dst, start, value):
        low_value = value.astype(jnp.bfloat16)
        per = TILE // BLOCK
        for g in range(groups):
            piece_value = low_value[:, g * lanes : (g + 1) * lanes]
            dst[g, pl.ds(start, per)] = piece_value.reshape(per, BLOCK, lanes)

    def project(a, chunk, own):
        def one(i, carry):
            x = x_all[a, pl.ds(pl.multiple_of(i * TILE, TILE), TILE), :]
            start = chunk * (mid // BLOCK) + i * (TILE // BLOCK)
            if own:
                q_start = (chunk - 2 * core) * (mid // BLOCK) + i * (TILE // BLOCK)
                q = wide_dot(x, weights[0], NN) + small[0:1, :]
                split(q_s, q_start, q.astype(jnp.bfloat16) * jnp.bfloat16(score_scale))
            split(k_s, start, wide_dot(x, weights[1], NN))
            split(v_s, start, wide_dot(x, weights[2], NN) + small[1:2, :])
            return carry

        lax.fori_loop(0, mid // TILE, one, 0)

    def own_project(a, carry):
        project(a, 2 * core + (a ^ bit), True)
        return carry

    def other_project(a, carry):
        project(2 + a, 2 * (1 - core) + (a ^ bit), False)
        return carry

    lax.fori_loop(0, 2, own_project, 0)
    for copy in x_over:
        copy.wait_recv()
    outs.append(pltpu.make_async_copy(x_all, x_ref, out_sem.at[1]))
    outs[1].start()
    lax.fori_loop(0, 2, other_project, 0)
    for i, (src, dst) in enumerate(((q_s, q_ref), (k_s, k_ref), (v_s, v_ref))):
        outs.append(pltpu.make_async_copy(src, dst, out_sem.at[2 + i]))
        outs[-1].start()

    def span_of(k):
        return pl.ds(k * PER, PER)

    rest_own = pltpu.make_async_copy(sel, rest_ref.at[me], own_sem.at[3])
    direct = [
        [
            send(
                sel.at[span_of(k)], rest_ref.at[me, span_of(k)], (r_s, r_r), k * 3 + j, across(m)
            )
            for j, m in enumerate((1, 2))
        ]
        for k in range(CHUNKS)
    ]
    onward = []
    for k in range(CHUNKS):
        odd = lax.rem(core + k, 2)
        source = jnp.where(odd == 0, c ^ 1, c ^ 2) * n_tp + t
        target = (z, jnp.where(odd == 0, c ^ 2, c ^ 1), t)
        view = rest_ref.at[source, span_of(k)]
        onward.append(send(view, view, (r_s, r_r), k * 3 + 2, target))

    def passing(k, which):
        if which == 0:
            src = sel.at[span_of(k)]
        else:
            src = rest_ref.at[(c ^ which) * n_tp + t, span_of(k)]
        dst = rest_ref.at[(c ^ which) * n_tp + t, span_of(k)]
        return [
            send(src, dst, (rt_s, rt_r), (k * 4 + which) * others + dt - 1, beside(dt))
            for dt in range(1, n_tp)
        ]

    passed = [[passing(k, which) for which in range(4)] for k in range(CHUNKS)]

    def begin_rest():
        hops_end()
        for m in range(CHUNKS * PER):
            sel[m] = pool[slots[KINDS + m]]
        rest_own.start()
        for k in range(CHUNKS):
            for copy in direct[k]:
                copy.start()
            for copy in passed[k][0]:
                copy.start()

    def relay(k):
        for copy in direct[k]:
            copy.wait_recv()
        onward[k].start()
        for copy in passed[k][1] + passed[k][2]:
            copy.start()

    def last_relay(k):
        onward[k].wait_recv()
        for copy in passed[k][3]:
            copy.start()

    begin_rest()

    last = nblocks - 1
    picks_each = table.shape[2]
    masks = head_masks(BLOCK)
    low_half = lax.broadcasted_iota(jnp.int32, (BLOCK, 2 * HEAD), 1) < HEAD
    each = 5
    subs = (local - 1) // each

    def attend_round(i, carry):
        g = i // subs
        sub = lax.rem(i, subs)
        qg, kg, vg = q_s.at[g], k_s.at[g], v_s.at[g]
        for k in range(CHUNKS):

            @pl.when(i == 3 + 2 * k)
            def hook(k=k):
                relay(k)

        @pl.when(sub == 0)
        def edge_block():
            edge = (local - 1) * core
            spread = spread_heads(rows_of(qg, edge), masks)
            span = 8 * BLOCK
            pieces = nblocks // 8
            top = None
            for n in range(pieces):
                scores = wide_dot(rows_of(kg, n * 8, 8), spread, NT)
                kept[n * span : (n + 1) * span, :] = scores
                high = jnp.max(scores, axis=0, keepdims=True)
                top = high if top is None else jnp.maximum(top, high)
            total_p = None
            for n in range(pieces):
                probs = jnp.exp(kept[n * span : (n + 1) * span, :] - top)
                kept[n * span : (n + 1) * span, :] = probs
                some = jnp.sum(probs, axis=0, keepdims=True)
                total_p = some if total_p is None else total_p + some
            scale = 1.0 / total_p
            full = None
            for n in range(pieces):
                probs = (kept[n * span : (n + 1) * span, :] * scale).astype(jnp.bfloat16)
                some = wide_dot(probs, rows_of(vg, n * 8, 8), TN)
                full = some if full is None else full + some
            at = pl.ds(pl.multiple_of(edge * BLOCK, BLOCK), BLOCK)
            ctx_s[g, at, :] = own_heads(full, masks).astype(jnp.bfloat16)
            lse_ref[g, pl.ds(edge, 1), :] = top + jnp.log(total_p)

        for u in range(each):
            spot = sub * each + u + 1 - core
            block = spot + local * core
            picks = [
                [table[g * PACK + h, block - 1, r] for h in range(PACK)]
                for r in range(picks_each)
            ]
            spread = spread_heads(rows_of(qg, spot), masks)
            keys = gathered(kg, block, last, picks, low_half)
            values = gathered(vg, block, last, picks, low_half)
            scores = middle_scores(keys, spread, block, last)
            top = jnp.max(scores, axis=0, keepdims=True)
            probs = jnp.exp(scores - top)
            total_p = jnp.sum(probs, axis=0, keepdims=True)
            probs = (probs * (1.0 / total_p)).astype(jnp.bfloat16)
            full = wide_dot(probs, values, TN)
            at = pl.ds(pl.multiple_of(spot * BLOCK, BLOCK), BLOCK)
            ctx_s[g, at, :] = own_heads(full, masks).astype(jnp.bfloat16)
            lse_ref[g, pl.ds(spot, 1), :] = top + jnp.log(total_p)
        return carry

    lax.fori_loop(0, groups * subs, attend_round, 0)
    for g in range(groups):
        outs.append(
            pltpu.make_async_copy(
                ctx_s.at[g], ctx_ref.at[:, g * lanes : (g + 1) * lanes], out_sem.at[5 + g]
            )
        )
        outs[-1].start()
    for k in range(CHUNKS):
        last_relay(k)

    @pl.when(jnp.logical_not(stays))
    def left():
        x_moves[0].wait_send()

    x_moves[1].wait_send()
    for copy in (*x_over, *za, *zb, *q_moves, *qt_moves, *onward):
        copy.wait_send()
    for pair in direct:
        for copy in pair:
            copy.wait_send()
    for chunk in passed:
        for group in chunk:
            for copy in group:
                copy.wait()
    hops_sent()
    rest_own.wait()
    for copy in outs:
        copy.wait()


def begin(slots, local_at, table, master, small_in, inputs, n_shard, n_ctx, n_tp):
    held, rows, width = master.shape
    _, mid, _ = inputs.shape
    groups = n_ctx * n_tp
    long = -(-(KINDS * rows + 16) // (16 * n_shard)) * 16 * n_shard
    lanes = PACK * HEAD
    packs = width // lanes
    tokens, seq = 2 * mid, 4 * mid
    anywhere = pl.BlockSpec(memory_space=pl.ANY)
    vmem = pl.BlockSpec(memory_space=pltpu.VMEM)
    smem = pl.BlockSpec(memory_space=pltpu.SMEM)
    dma = pltpu.SemaphoreType.DMA
    low = jnp.bfloat16
    f32 = jnp.float32
    pairs = [2, 2, n_shard - 1, n_shard - 1, n_shard - 1, n_shard - 1, 3]
    pairs += [4 * (n_tp - 1), 3 * CHUNKS, 4 * CHUNKS * (n_tp - 1)]
    return pl.pallas_call(
        functools.partial(begin_kernel, n_shard, n_ctx, n_tp),
        name="begin",
        in_specs=[smem, smem, smem, anywhere, vmem, anywhere],
        out_specs=[anywhere, anywhere, anywhere, vmem, anywhere, anywhere, anywhere, anywhere, vmem],
        out_shape=[
            bf16_of(4, mid, width),
            bf16_of(groups, long, width),
            bf16_of(groups, 9, rows, width),
            f32_of(16, width),
            bf16_of(packs, tokens // BLOCK, BLOCK, lanes),
            bf16_of(packs, seq // BLOCK, BLOCK, lanes),
            bf16_of(packs, seq // BLOCK, BLOCK, lanes),
            bf16_of(tokens, width),
            f32_of(packs, tokens // BLOCK, lanes),
        ],
        scratch_shapes=[
            pltpu.VMEM((held, rows, width), f32),
            pltpu.VMEM((held + 1, rows, width), low),
            pltpu.VMEM((2, mid, width), f32),
            pltpu.VMEM((2, mid, width), low),
            pltpu.VMEM((4, mid, width), low),
            pltpu.VMEM((long, width), low),
            pltpu.VMEM((n_shard - 1, long // n_shard, width), low),
            pltpu.VMEM((long // n_shard, width), low),
            pltpu.VMEM((long, width), low),
            pltpu.VMEM((n_shard * held, rows, width), low),
            pltpu.VMEM((9, rows, width), low),
            pltpu.VMEM((groups, long, width), low),
            pltpu.VMEM((3, width, width), low),
            pltpu.VMEM((16, width), f32),
            pltpu.VMEM((packs, tokens // BLOCK, BLOCK, lanes), low),
            pltpu.VMEM((packs, seq // BLOCK, BLOCK, lanes), low),
            pltpu.VMEM((packs, seq // BLOCK, BLOCK, lanes), low),
            pltpu.VMEM((packs, tokens, lanes), low),
            pltpu.VMEM((seq, lanes), f32),
            *[dma((n,)) for n in pairs for _ in range(2)],
            dma((4,)),
            dma((8,)),
        ],
        compiler_params=pltpu.CompilerParams(
            collective_id=0, has_side_effects=True, vmem_limit_bytes=62 << 20
        ),
        cost_estimate=pl.CostEstimate(
            flops=60_000_000_000, bytes_accessed=60 << 20, transcendentals=16_000_000
        ),
    )(slots, local_at, table, master, small_in, inputs)


NEAR = 4


def back_kernel(
    n_ctx,
    n_tp,
    n2_hbm,
    r2_ref,
    cot0_ref,
    cot1_ref,
    hid_ref,
    gel_ref,
    fit_ref,
    n1_ref,
    r1_ref,
    ctx_ref,
    small,
    up_w,
    down_w,
    wo,
    layer_ref,
    own_ref,
    near_ref,
    x_ref,
    y_ref,
    xy_ref,
    gh1_ref,
    dctx_ref,
    sums_ref,
    home_ref,
    gy,
    gu,
    mixed,
    mixed_t,
    grads,
    arrived,
    sums,
    send_sem,
    recv_sem,
    h_s,
    h_r,
    n_s,
    n_r,
    keep_sem,
    out_sem,
):
    z, c, t = place_of()
    step = pl.program_id(0)
    tokens, width = gy.shape
    tiles = tokens // TILE
    rows = grads.shape[4]
    others = n_tp - 1
    side, core, bit = t // 2, lax.rem(t, 2), lax.rem(c, 2)

    def beside(dt):
        return (z, c, lax.rem(t + dt, n_tp))

    stays = c // 2 == core
    keep_layer = pltpu.make_async_copy(layer_ref.at[0], home_ref.at[bit], keep_sem.at[0])
    layer_moves = [
        send(
            layer_ref.at[p],
            home_ref.at[bit],
            (h_s, h_r),
            p,
            (z, 2 * core + (p ^ bit), 2 * side + c // 2),
        )
        for p in range(2)
    ]

    @pl.when(step == 0)
    def start():
        take = pltpu.make_async_copy(n2_hbm, gy, keep_sem.at[1])
        take.start()
        barrier = pltpu.get_barrier_semaphore()
        friends = [beside(dt) for dt in range(1, n_tp)]
        friends += [(z, c ^ m, t) for m in range(1, n_ctx)]
        friends += [(z, c ^ m, t ^ 1) for m in range(1, n_ctx)]
        for friend in friends:
            pl.semaphore_signal(barrier, inc=1, device_id=friend, device_id_type=MESH)
        pl.semaphore_wait(barrier, len(friends))

        @pl.when(stays)
        def kept():
            keep_layer.start()

        @pl.when(jnp.logical_not(stays))
        def left():
            layer_moves[0].start()

        layer_moves[1].start()
        sums_ref[...] = jnp.zeros_like(sums_ref)
        take.wait()
        mid = tokens // 2
        for p, cot_ref in enumerate((cot0_ref, cot1_ref)):

            def one(i, carry, p=p, cot_ref=cot_ref):
                inside = pl.ds(pl.multiple_of(i * TILE, TILE), TILE)
                at = pl.ds(pl.multiple_of((p ^ bit) * mid + i * TILE, TILE), TILE)
                cot = cot_ref[inside, :].astype(jnp.float32)
                n2 = gy[at, :]
                add_row(sums_ref, 10, cot * n2)
                add_row(sums_ref, 11, cot)
                gh2 = norm_back(cot, n2, r2_ref[at, 0:1], small[10:11, :])
                gy[at, :] = gh2
                low = gh2.astype(jnp.bfloat16)
                mixed[at, :] = low
                mixed_t[:, at] = low.T
                add_row(sums_ref, 9, low.astype(jnp.float32))
                return carry

            lax.fori_loop(0, mid // TILE, one, 0)

    def moves(b, count):
        slot = lax.rem(b, 2)
        return [
            send(
                grads.at[slot, :, lax.rem(t + dt, n_tp), 0:count],
                arrived.at[b, dt - 1, :, 0:count],
                (send_sem, recv_sem),
                b * others + dt - 1,
                beside(dt),
            )
            for dt in range(1, n_tp)
        ]

    def exchange(b, count):
        for copy in moves(b, count):
            copy.start()

    def keep(b, count):
        for copy in moves(b, count):
            copy.wait()
        slot = lax.rem(b, 2)
        for j in range(n_ctx):
            for i in range(count):
                value = grads[slot, c ^ j, t, i]
                for dt in range(others):
                    value = value + arrived[b, dt, c ^ j, i]
                sums[j, 2 * b + i] = value

    near = [
        send(sums.at[j, 0:NEAR], near_ref.at[j - 1], (n_s, n_r), j - 1, (z, c ^ j, t))
        for j in range(1, n_ctx)
    ]

    def outward(part, first, count):
        moved = [
            pltpu.make_async_copy(
                sums.at[0, first : first + count],
                own_ref.at[first : first + count],
                out_sem.at[part * n_ctx],
            )
        ]
        begin_at = max(first, NEAR)
        count -= begin_at - first
        for j, out in enumerate((x_ref, y_ref, xy_ref)):
            moved.append(
                pltpu.make_async_copy(
                    sums.at[j + 1, begin_at : begin_at + count],
                    out.at[begin_at - NEAR : begin_at - NEAR + count],
                    out_sem.at[part * n_ctx + j + 1],
                )
            )
        return moved

    def put(slot, i, value):
        low = value.astype(jnp.bfloat16)
        grads[slot, :, :, i] = low.reshape(n_ctx, n_tp, rows, width)

    @pl.when(step < 4)
    def ffn():
        up_block = matrix(up_w)
        down_block = matrix(down_w)
        slot = lax.rem(step, 2)

        def one(i, carry):
            at = pl.ds(pl.multiple_of(i * MID, MID), MID)
            grad = wide_dot(mixed[at, :], down_block, NN) * gel_ref[0, at, :].astype(jnp.float32)
            low = grad.astype(jnp.bfloat16)
            gu[at, :] = low
            gy[at, :] += wide_dot(low, up_block, NT)
            sums_ref[pl.ds(5 + step, 1), :] += jnp.sum(
                low.astype(jnp.float32), axis=0, keepdims=True
            )
            return carry

        lax.fori_loop(0, tokens // MID, one, 0)
        put(slot, 0, wide_dot(fit_ref[...], gu[...], NN))
        put(slot, 1, wide_dot(mixed_t[...], hid_ref[0], NN))
        exchange(step, 2)

    @pl.when(step > 0)
    def settle():
        keep(step - 1, 2)

    @pl.when(step == NEAR // 2)
    def cross():
        for copy in near:
            copy.start()

    @pl.when(step == 4)
    def first_norm():
        for copy in outward(0, 0, 8):
            copy.start()

        def one(i, carry):
            at = pl.ds(pl.multiple_of(i * TILE, TILE), TILE)
            grad = gy[at, :]
            n1 = n1_ref[at, :]
            gh1 = norm_back(grad, n1, r1_ref[at, 0:1], small[3:4, :])
            gh1_ref[at, :] = gh1
            low = gh1.astype(jnp.bfloat16)
            gu[at, :] = low
            add_row(sums_ref, 2, low.astype(jnp.float32))
            add_row(sums_ref, 3, grad * n1)
            add_row(sums_ref, 4, grad)
            return carry

        lax.fori_loop(0, tiles, one, 0)
        put(0, 0, wide_dot(ctx_ref[...].T, gu[...], NN))
        exchange(4, 1)
        out_w = matrix(wo)

        def two(i, carry):
            at = pl.ds(pl.multiple_of(i * TILE, TILE), TILE)
            dctx_ref[at, :] = wide_dot(gu[at, :], out_w, NT).astype(jnp.bfloat16)
            return carry

        lax.fori_loop(0, tiles, two, 0)
        keep(4, 1)
        for copy in outward(1, 8, 1):
            copy.start()
        for copy in (*near, *outward(0, 0, 8), *outward(1, 8, 1)):
            copy.wait()

        @pl.when(stays)
        def done():
            keep_layer.wait()

        @pl.when(jnp.logical_not(stays))
        def gone():
            layer_moves[0].wait()

        layer_moves[1].wait()


def back(n2, r2, cots, hid, gel, fit, n1, r1, ctx, small, rest, layer, n_ctx, n_tp):
    tokens, width = n2.shape
    rows = rest.shape[2]
    dma = pltpu.SemaphoreType.DMA

    def whole(shape):
        return pl.BlockSpec(shape, lambda b: (0,) * len(shape), pipeline_mode=pl.Buffered(1))

    def block(b):
        return (jnp.minimum(b, 3), 0, 0)

    def held(first, single=False):
        return pl.BlockSpec(
            (n_ctx * n_tp, 1, rows, width),
            (lambda b: (0, first, 0, 0))
            if single
            else (lambda b: (0, first + jnp.minimum(b, 3), 0, 0)),
            pipeline_mode=pl.Buffered(1) if single else None,
        )

    def out(shape):
        return pl.BlockSpec(shape, lambda b: (0,) * len(shape))

    return pl.pallas_call(
        functools.partial(back_kernel, n_ctx, n_tp),
        name="back",
        grid=(5,),
        in_specs=[
            pl.BlockSpec(memory_space=pl.ANY),
            whole((tokens, 128)),
            whole((tokens // 2, width)),
            whole((tokens // 2, width)),
            pl.BlockSpec((1, tokens, width), block),
            pl.BlockSpec((1, tokens, width), block),
            whole((width, tokens)),
            whole((tokens, width)),
            whole((tokens, 128)),
            whole((tokens, width)),
            whole(small.shape),
            held(1),
            held(5),
            held(0, True),
            pl.BlockSpec(memory_space=pl.ANY),
        ],
        out_specs=[
            *[pl.BlockSpec(memory_space=pl.ANY)] * 5,
            out((tokens, width)),
            out((tokens, width)),
            out((16, width)),
            pl.BlockSpec(memory_space=pl.ANY),
        ],
        out_shape=[
            bf16_of(9, rows, width),
            bf16_of(n_ctx - 1, NEAR, rows, width),
            *[bf16_of(9 - NEAR, rows, width)] * 3,
            f32_of(tokens, width),
            bf16_of(tokens, width),
            f32_of(16, width),
            bf16_of(*layer.shape),
        ],
        scratch_shapes=[
            pltpu.VMEM((tokens, width), jnp.float32),
            pltpu.VMEM((tokens, width), jnp.bfloat16),
            pltpu.VMEM((tokens, width), jnp.bfloat16),
            pltpu.VMEM((width, tokens), jnp.bfloat16),
            pltpu.VMEM((2, n_ctx, n_tp, 2, rows, width), jnp.bfloat16),
            pltpu.VMEM((5, n_tp - 1, n_ctx, 2, rows, width), jnp.bfloat16),
            pltpu.VMEM((n_ctx, 9 + 1, rows, width), jnp.bfloat16),
            dma((5 * (n_tp - 1),)),
            dma((5 * (n_tp - 1),)),
            dma((2,)),
            dma((2,)),
            dma((n_ctx - 1,)),
            dma((n_ctx - 1,)),
            dma((2,)),
            dma((2 * n_ctx,)),
        ],
        compiler_params=pltpu.CompilerParams(
            collective_id=3, has_side_effects=True, vmem_limit_bytes=62 << 20
        ),
        cost_estimate=pl.CostEstimate(
            flops=22_000_000_000, bytes_accessed=40 << 20, transcendentals=0
        ),
    )(n2, r2, *cots, hid, gel, fit, n1, r1, ctx, small, rest, rest, rest, layer)


LATE = 3
EARLY = 9


def adam_update(weight, first, second, grad, decay, rate):
    count = float(STEP)
    first_new = beta_one * first + (1.0 - beta_one) * grad
    second_new = beta_two * second + (1.0 - beta_two) * grad * grad
    first_hat = first_new / (1.0 - beta_one**count)
    second_hat = second_new / (1.0 - beta_two**count)
    weight_new = weight - rate * (first_hat / (jnp.sqrt(second_hat) + adam_eps) + decay * weight)
    return (weight_new, first_new, second_new)


def finish_kernel(
    n_shard,
    n_ctx,
    n_tp,
    holder,
    late_at,
    x_hbm,
    dq_hbm,
    dk_hbm,
    dv_hbm,
    gh1_hbm,
    first_hbm,
    e0_hbm,
    near_hbm,
    e1_hbm,
    e2_hbm,
    e3_hbm,
    small_ref,
    w_ref,
    one_ref,
    two_ref,
    home_ref,
    w_out,
    one_out,
    two_out,
    small_out,
    x_s,
    dq_s,
    dk_s,
    dv_s,
    gh1_s,
    first_s,
    early,
    every,
    packed,
    slot_met,
    flipped,
    grads,
    arrived,
    partial,
    met,
    over,
    more,
    back_s,
    small_s,
    small_t,
    small_m,
    small_p,
    flat,
    flat_met,
    flat_sum,
    mine_s,
    pool,
    in_sem,
    c_s,
    c_r,
    p_s,
    p_r,
    o_s,
    o_r,
    h_s,
    h_r,
    sc_s,
    sc_r,
    sp_s,
    sp_r,
    e_s,
    e_r,
    a_s,
    a_r,
    b_s,
    b_r,
    keep_sem,
):
    z, c, t = place_of()
    side, core, bit = t // 2, lax.rem(t, 2), lax.rem(c, 2)
    _, mid, width = x_s.shape
    tokens = 2 * mid
    held, rows, _ = w_ref.shape
    per = n_ctx * n_tp // 2
    band = width // 2
    tile = mid // 2
    piece = mine_s.shape[0]

    loads = [
        pltpu.make_async_copy(src, dst, in_sem.at[i])
        for i, (src, dst) in enumerate(
            (
                (x_hbm, x_s),
                (dk_hbm, dk_s),
                (dv_hbm, dv_s),
                (dq_hbm, dq_s),
                (first_hbm, first_s),
                (gh1_hbm, gh1_s),
                (e0_hbm, early.at[0]),
                (near_hbm, early.at[1:4, 0:NEAR]),
                (e1_hbm, early.at[1, NEAR:EARLY]),
                (e2_hbm, early.at[2, NEAR:EARLY]),
                (e3_hbm, early.at[3, NEAR:EARLY]),
            )
        )
    ]
    for i in (6, 7, 8, 9, 10, 0, 1, 2, 3, 4, 5):
        loads[i].start()

    def far(dz):
        return (lax.rem(z + dz, n_shard), c, t)

    def across(mask):
        return (z, c ^ mask, t)

    def beside(dt):
        return (z, c, lax.rem(t + dt, n_tp))

    barrier = pltpu.get_barrier_semaphore()
    friends = [far(dz) for dz in range(1, n_shard)]
    friends += [(z, c ^ m, t) for m in range(1, n_ctx)]
    friends += [beside(dt) for dt in range(1, n_tp)]
    friends += [(z, c ^ m, t ^ 1) for m in range(1, n_ctx)]
    for friend in friends:
        pl.semaphore_signal(barrier, inc=1, device_id=friend, device_id_type=MESH)

    for i in range(6, 11):
        loads[i].wait()
    every[0:EARLY] = early[0] + early[1] + early[2] + early[3]
    every[EARLY] = jnp.zeros_like(every[EARLY])
    for s in range(n_shard * held):
        packed[s // held, s % held] = every[holder[s]]
    pl.semaphore_wait(barrier, len(friends))
    slot_moves = [
        send(packed.at[far(dz)[0]], slot_met.at[dz - 1], (e_s, e_r), dz - 1, far(dz))
        for dz in range(1, n_shard)
    ]
    for copy in slot_moves:
        copy.start()

    core_moves = []

    def exchange(m):
        for dt in range(1, n_tp):
            other = lax.rem(t + dt, n_tp)
            for k in range(n_ctx):
                copy = send(
                    grads.at[k * n_tp + other, m],
                    arrived.at[dt - 1, k, m],
                    (c_s, c_r),
                    ((dt - 1) * n_ctx + k) * LATE + m,
                    beside(dt),
                )
                copy.start()
                core_moves.append((m, copy))

    plane_moves = []

    def meet(m):
        for which, copy in core_moves:
            if which == m:
                copy.wait_recv()
        for k in range(n_ctx):
            value = grads[k * n_tp + t, m]
            for dt in range(1, n_tp):
                value = value + arrived[dt - 1, k, m]
            partial[k, m] = value
        for j in range(1, n_ctx):
            copy = send(
                partial.at[c ^ j, m], met.at[j - 1, m], (p_s, p_r), (j - 1) * LATE + m, across(j)
            )
            copy.start()
            plane_moves.append(copy)

    loads[0].wait()
    for a in range(4):
        chunk = 2 * (core if a < 2 else 1 - core) + ((a % 2) ^ bit)
        flipped[:, pl.ds(pl.multiple_of(chunk * mid, mid), mid)] = x_s[a].T

    def weight_grad(m, left_at, right):
        def one(i, carry):
            left = flipped[pl.ds(pl.multiple_of(i * band, band), band), left_at]
            value = wide_dot(left, right[...], NN).astype(jnp.bfloat16)
            grads[pl.ds(i * per, per), m] = value.reshape(per, rows, width)
            return carry

        lax.fori_loop(0, 2, one, 0)

    loads[1].wait()
    weight_grad(1, slice(None), dk_s)
    exchange(1)
    loads[2].wait()
    weight_grad(2, slice(None), dv_s)
    exchange(2)
    meet(1)
    loads[3].wait()
    weight_grad(0, pl.ds(pl.multiple_of(core * tokens, tokens), tokens), dq_s)
    exchange(0)
    meet(2)

    row = lax.broadcasted_iota(jnp.int32, small_ref.shape, 0)
    q_sum = jnp.sum(dq_s[...].astype(jnp.float32), axis=0, keepdims=True)
    v_sum = jnp.sum(dv_s[...].astype(jnp.float32), axis=0, keepdims=True)
    sums = jnp.where(row == 0, q_sum, jnp.where(row == 1, v_sum, small_ref[...]))
    small_s[...] = sums.astype(jnp.bfloat16)
    small_core = [
        send(small_s, small_t.at[dt - 1], (sc_s, sc_r), dt - 1, beside(dt)) for dt in range(1, n_tp)
    ]
    for copy in small_core:
        copy.start()

    loads[4].wait()

    def weight(m):
        return first_s[:, m * rows : (m + 1) * rows, :].reshape(width, width)

    wq, wk, wv = weight(0), weight(1), weight(2)
    over_moves = []
    for b in range(2):
        at = pl.ds(pl.multiple_of((1 - core) * tokens + b * mid, mid), mid)
        value = wide_dot(dk_s[at, :], wk, NT) + wide_dot(dv_s[at, :], wv, NT)
        over[b] = value.astype(jnp.bfloat16)
        copy = send(over.at[b], more.at[b], (o_s, o_r), b, (z, c, t ^ 1))
        copy.start()
        over_moves.append(copy)
        if b == 0:
            meet(0)

    value = small_s[...]
    for dt, copy in enumerate(small_core):
        copy.wait_recv()
        value = value + small_t[dt]
    small_m[...] = value
    small_plane = [
        send(small_m, small_p.at[j - 1], (sp_s, sp_r), j - 1, across(j)) for j in range(1, n_ctx)
    ]
    for copy in small_plane:
        copy.start()

    loads[5].wait()
    stays = c // 2 == core
    home_moves = []
    for copy in over_moves:
        copy.wait_recv()
    keep = pltpu.make_async_copy(back_s.at[0], home_ref.at[bit], keep_sem.at[0])
    for move in range(2):
        chunk = move ^ bit
        for i in range(2):
            at = pl.ds(pl.multiple_of(core * tokens + chunk * mid + i * tile, tile), tile)
            here = pl.ds(pl.multiple_of(chunk * mid + i * tile, tile), tile)
            value = gh1_s[here, :]
            value = value + more[chunk, i * tile : (i + 1) * tile, :].astype(jnp.float32)
            value = value + wide_dot(dq_s[here, :], wq, NT)
            value = value + wide_dot(dk_s[at, :], wk, NT)
            value = value + wide_dot(dv_s[at, :], wv, NT)
            back_s[move, i * tile : (i + 1) * tile, :] = value.astype(jnp.bfloat16)
        target = (z, 2 * core + chunk, 2 * side + c // 2)
        home_moves.append(send(back_s.at[move], home_ref.at[bit], (h_s, h_r), move, target))
        if move == 0:

            @pl.when(stays)
            def kept():
                keep.start()

            @pl.when(jnp.logical_not(stays))
            def left():
                home_moves[0].start()

        else:
            home_moves[1].start()

    flat[...] = jnp.zeros_like(flat)
    for copy in plane_moves:
        copy.wait_recv()
    for m in range(LATE):
        value = partial[c, m]
        for j in range(n_ctx - 1):
            value = value + met[j, m]
        flat[m * rows : (m + 1) * rows, :] = value
    value = small_m[...]
    for j, copy in enumerate(small_plane):
        copy.wait_recv()
        value = value + small_p[j]
    small_rows = small_s.shape[0]
    flat[LATE * rows : LATE * rows + small_rows, :] = value

    def piece_at(k):
        return pl.ds(pl.multiple_of(k * piece, piece), piece)

    flat_out = [
        send(flat.at[piece_at(far(dz)[0])], flat_met.at[dz - 1], (a_s, a_r), dz - 1, far(dz))
        for dz in range(1, n_shard)
    ]
    for copy in flat_out:
        copy.start()
    total = flat[piece_at(z), :].astype(jnp.float32)
    for dz, copy in enumerate(flat_out):
        copy.wait_recv()
        total = total + flat_met[dz].astype(jnp.float32)
    mine_s[...] = total.astype(jnp.bfloat16)
    flat_back = [
        send(mine_s, flat_sum.at[piece_at(z)], (b_s, b_r), dz - 1, far(dz))
        for dz in range(1, n_shard)
    ]
    for copy in flat_back:
        copy.start()
    flat_sum[piece_at(z), :] = mine_s[...]
    for copy in slot_moves:
        copy.wait_recv()
    for copy in flat_back:
        copy.wait_recv()
    for m in range(LATE):
        pool[m] = flat_sum[m * rows : (m + 1) * rows, :]
    pool[LATE] = jnp.zeros_like(pool[LATE])
    for j in range(held):
        grad = packed[z, j].astype(jnp.float32)
        for dz in range(n_shard - 1):
            grad = grad + slot_met[dz, j].astype(jnp.float32)
        grad = grad + pool[late_at[z * held + j]].astype(jnp.float32)
        w, one, two = adam_update(w_ref[j], one_ref[j], two_ref[j], grad, 0.01, rate_value)
        w_out[j] = w
        one_out[j] = one
        two_out[j] = two
    small_out[...] = flat_sum[LATE * rows : LATE * rows + small_rows, :].astype(jnp.float32)

    @pl.when(stays)
    def done():
        keep.wait()

    @pl.when(jnp.logical_not(stays))
    def gone():
        home_moves[0].wait()

    home_moves[1].wait()
    for _, copy in core_moves:
        copy.wait_send()
    for copy in (
        *plane_moves,
        *over_moves,
        *small_core,
        *small_plane,
        *slot_moves,
        *flat_out,
        *flat_back,
    ):
        copy.wait_send()


def finish(
    holder,
    late_at,
    x_all,
    dq,
    dk,
    dv,
    gh1,
    first,
    early,
    small,
    master,
    one,
    two,
    n_shard,
    n_ctx,
    n_tp,
):
    _, mid, width = x_all.shape
    held, rows, _ = master.shape
    groups = n_ctx * n_tp
    span = 16 * n_shard
    long = -(-(LATE * rows + small.shape[0]) // span) * span
    smem = pl.BlockSpec(memory_space=pltpu.SMEM)
    anywhere = pl.BlockSpec(memory_space=pl.ANY)
    vmem = pl.BlockSpec(memory_space=pltpu.VMEM)
    dma = pltpu.SemaphoreType.DMA
    low = jnp.bfloat16
    pairs = [LATE * n_ctx * (n_tp - 1), LATE * (n_ctx - 1), 2, 2, n_tp - 1, n_ctx - 1]
    pairs += [n_shard - 1] * 3
    stored = f32_of(held, rows, width)
    shapes = [
        x_all.shape,
        dq.shape,
        dk.shape,
        dv.shape,
        None,
        first.shape,
        (4, EARLY, rows, width),
        (EARLY + 1, rows, width),
        (n_shard, held, rows, width),
        (n_shard - 1, held, rows, width),
        (width, 4 * mid),
        (groups, LATE, rows, width),
        (n_tp - 1, n_ctx, LATE, rows, width),
        (n_ctx, LATE, rows, width),
        (n_ctx - 1, LATE, rows, width),
        (2, mid, width),
        (2, mid, width),
        (2, mid, width),
        small.shape,
        (n_tp - 1, *small.shape),
        small.shape,
        (n_ctx - 1, *small.shape),
        (long, width),
        (n_shard - 1, long // n_shard, width),
        (long, width),
        (long // n_shard, width),
        (LATE + 1, rows, width),
    ]
    return pl.pallas_call(
        functools.partial(finish_kernel, n_shard, n_ctx, n_tp),
        name="finish",
        in_specs=[smem] * 2 + [anywhere] * 11 + [vmem] * 4,
        out_specs=[anywhere] + [vmem] * 4,
        out_shape=[bf16_of(2, mid, width), stored, stored, stored, f32_of(*small.shape)],
        scratch_shapes=[
            pltpu.VMEM(s, low) if s else pltpu.VMEM(gh1.shape, jnp.float32) for s in shapes
        ]
        + [dma((11,))]
        + [dma((n,)) for n in pairs for _ in range(2)]
        + [dma((1,))],
        compiler_params=pltpu.CompilerParams(
            collective_id=1, has_side_effects=True, vmem_limit_bytes=63 << 20
        ),
        cost_estimate=pl.CostEstimate(
            flops=12_000_000_000, bytes_accessed=40 << 20, transcendentals=0
        ),
    )(holder, late_at, x_all, dq, dk, dv, gh1, first, *early, small, master, one, two)


def moves(n_ctx, n_tp, pick):
    pairs = []
    for c in range(n_ctx):
        for t in range(n_tp):
            side, core = t // 2, t % 2
            to_ctx = 2 * core + (pick ^ (c & 1))
            to_tp = 2 * side + c // 2
            pairs.append((c * n_tp + t, to_ctx * n_tp + to_tp))
    return pairs


def shards(
    inputs,
    cotangent,
    rand_blocks,
    slot_of,
    master,
    moment_one,
    moment_two,
    small_params,
    small_one,
    small_two,
):
    n_shard = lax.axis_size("shard")
    n_ctx = lax.axis_size("ctx")
    n_tp = lax.axis_size("tp")
    groups = n_ctx * n_tp
    held, rows, width = master.shape
    span = small_params.shape[0]
    my_ctx = lax.axis_index("ctx")
    my_tp = lax.axis_index("tp")
    parity = lax.rem(my_ctx, 2)
    half = lax.rem(my_tp, 2)
    plane = ("ctx", "tp")
    forth = [moves(n_ctx, n_tp, pick) for pick in range(2)]

    arrival = [(b ^ parity) + 2 * (half ^ (j // 2)) for j, b in enumerate((0, 1, 0, 1))]
    info = jnp.stack([half, *arrival]).astype(jnp.int32)
    half_one = info[:1]

    def sent(field, pick):
        low = field.astype(jnp.bfloat16)
        return jnp.where(parity == 0, low[pick], low[1 - pick])

    my_shard = lax.axis_index("shard")
    start = ((my_shard * n_ctx + my_ctx) * n_tp + my_tp) * span
    lone = lax.dynamic_update_slice(
        jnp.zeros((16 * width,), jnp.float32), small_params, (start,)
    ).reshape(16, width)
    local_at = slot_of[:LATE] - my_shard * held
    local_at = jnp.where((local_at >= 0) & (local_at < held), local_at, held)
    x_all, first, rest, small, q, k, v, context, lse = begin(
        slot_of, local_at, rand_blocks, master, lone, inputs, n_shard, n_ctx, n_tp
    )
    cots, context = lax.optimization_barrier(
        ([sent(cotangent, pick) for pick in range(2)], context)
    )
    cots = [lax.ppermute(cots[pick], plane, forth[pick]) for pick in range(2)]
    out_low, n1, r1, fit, hid, gel, n2, r2 = front(info, context, x_all, small, rest)
    *early, gh1, dctx, sums, layer_home = back(
        n2, r2, cots, hid, gel, fit, n1, r1, context, small, rest, out_low, n_ctx, n_tp
    )
    for j in range(1, n_ctx):
        crossing = [
            (a * n_tp + b, (a ^ j) * n_tp + b) for a in range(n_ctx) for b in range(n_tp)
        ]
        early[j + 1] = lax.ppermute(early[j + 1], plane, crossing)
    dq, dk, dv = attend_back(half_one, rand_blocks, q, k, v, lse, dctx, 5)
    stands = jnp.array([8, 0, 2, 4, 6, 1, 3, 5, 7], jnp.int32)
    slots_all = jnp.arange(n_shard * held, dtype=jnp.int32)
    hits = slot_of[None, :] == slots_all[:, None]
    holder = EARLY + jnp.sum(jnp.where(hits[:, LATE:], stands[None, :] - EARLY, 0), axis=1)
    ranks = jnp.arange(LATE, dtype=jnp.int32)[None, :]
    late_at = LATE + jnp.sum(jnp.where(hits[:, :LATE], ranks - LATE, 0), axis=1)
    came, master_new, first_new, second_new, small_sum = finish(
        holder.astype(jnp.int32),
        late_at.astype(jnp.int32),
        x_all,
        dq,
        dk,
        dv,
        gh1,
        first,
        early,
        sums,
        master,
        moment_one,
        moment_two,
        n_shard,
        n_ctx,
        n_tp,
    )
    layer_out = layer_home.astype(jnp.float32)
    input_grad = came.astype(jnp.float32)
    small_owned = lax.dynamic_slice_in_dim(small_sum.reshape(-1), start, span)
    small_new, small_first, small_second = adam_update(
        small_params, small_one, small_two, small_owned, 0.0, small_rate
    )
    return (
        layer_out,
        input_grad,
        master_new,
        first_new,
        second_new,
        small_new,
        small_first,
        small_second,
    )


def solution(mesh):
    tokens = P(("shard", "tp"), "ctx", None)
    stored = P("shard", ("ctx", "tp"), None)
    spread = P(("shard", "ctx", "tp"))
    return jax.shard_map(
        shards,
        mesh=mesh,
        in_specs=(tokens, tokens, P(), P(), stored, stored, stored, spread, spread, spread),
        out_specs=(tokens, tokens, stored, stored, stored, spread, spread, spread),
        check_vma=False,
    )
```

```python
import functools

import jax
import jax.numpy as jnp
from jax import lax
from jax.experimental import pallas as pl
from jax.experimental.pallas import tpu as pltpu
from jax.sharding import PartitionSpec as P

STEP = 5
norm_eps = 1e-12
beta_one = 0.9
beta_two = 0.999
adam_eps = 1e-08
rate_value = 0.04
small_rate = 0.25
score_scale = 0.125
gelu_root = 0.7978845608
gelu_cube = 0.044715

BLOCK = 64
HEAD = 64
PACK = 4
masked_score = -1e30


def wide_dot(a, b, dims):
    return lax.dot_general(a, b, (dims, ((), ())), preferred_element_type=jnp.float32)


def head_masks(rows):
    lane = lax.broadcasted_iota(jnp.int32, (rows, PACK * HEAD), 1) // HEAD
    return [lane == h for h in range(PACK)]


def spread_heads(block, masks):
    zero = jnp.zeros_like(block)
    return jnp.concatenate([jnp.where(m, block, zero) for m in masks], axis=0)


def own_heads(full, masks):
    total = None
    for h, m in enumerate(masks):
        piece = jnp.where(m, full[h * BLOCK : (h + 1) * BLOCK], 0.0)
        total = piece if total is None else total + piece
    return total


def rows_of(ref, index, count=1):
    return ref[pl.ds(index, count)].reshape(count * BLOCK, ref.shape[2])


def flat_rows(ref, index):
    return ref[pl.ds(pl.multiple_of(index * BLOCK, BLOCK), BLOCK), :]


def picked_rows(ref, picks, low_half):
    halves = []
    for pair in range(PACK // 2):
        cols = slice(pair * 2 * HEAD, (pair + 1) * 2 * HEAD)
        first = ref[picks[2 * pair], :, cols]
        second = ref[picks[2 * pair + 1], :, cols]
        halves.append(jnp.where(low_half, first, second))
    return jnp.concatenate(halves, axis=1)


def gathered(ref, block, last, picks, low_half):
    pieces = [rows_of(ref, 0), rows_of(ref, last), rows_of(ref, block - 1, 3)]
    pieces += [picked_rows(ref, p, low_half) for p in picks]
    return jnp.concatenate(pieces, axis=0)


def middle_scores(keys, spread, block, last):
    scores = wide_dot(keys, spread, ((1,), (1,)))
    first_off = jnp.where(block == 1, masked_score, 0.0)
    last_off = jnp.where(block == last - 1, masked_score, 0.0)
    b = BLOCK
    return jnp.concatenate(
        [
            scores[: 2 * b],
            scores[2 * b : 3 * b] + first_off,
            scores[3 * b : 4 * b],
            scores[4 * b : 5 * b] + last_off,
            scores[5 * b :],
        ],
        axis=0,
    )


def attend_back_kernel(
    unroll,
    half_ref,
    table_ref,
    q_ref,
    k_ref,
    v_ref,
    lse_ref,
    do_ref,
    dq_ref,
    dk_ref,
    dv_ref,
    dk_acc,
    dv_acc,
    kept_p,
    kept_g,
):
    half = half_ref[0]
    group = pl.program_id(0)
    q_ref, k_ref, v_ref = q_ref.at[0], k_ref.at[0], v_ref.at[0]
    nblocks, local = k_ref.shape[0], q_ref.shape[0]
    last = nblocks - 1
    picks_each = table_ref.shape[2]
    masks = head_masks(BLOCK)
    low_half = lax.broadcasted_iota(jnp.int32, (BLOCK, 2 * HEAD), 1) < HEAD
    span = 8 * BLOCK
    chunks = nblocks // 8

    edge = (local - 1) * half
    spread = spread_heads(rows_of(q_ref, edge), masks)
    spread_do = spread_heads(flat_rows(do_ref, edge), masks)
    lse = lse_ref[0, pl.ds(edge, 1), :]
    delta = None
    for c in range(chunks):
        rows = slice(c * span, (c + 1) * span)
        probs = jnp.exp(wide_dot(rows_of(k_ref, c * 8, 8), spread, ((1,), (1,))) - lse)
        gp = wide_dot(rows_of(v_ref, c * 8, 8), spread_do, ((1,), (1,)))
        kept_p[rows, :] = probs
        kept_g[rows, :] = gp
        part = jnp.sum(probs * gp, axis=0, keepdims=True)
        delta = part if delta is None else delta + part
    full = None
    for c in range(chunks):
        rows = slice(c * span, (c + 1) * span)
        probs = kept_p[rows, :]
        ds = (probs * (kept_g[rows, :] - delta)).astype(jnp.bfloat16)
        dv_acc[rows, :] = wide_dot(probs.astype(jnp.bfloat16), spread_do, ((1,), (0,)))
        dk_acc[rows, :] = wide_dot(ds, spread, ((1,), (0,)))
        part = wide_dot(ds, rows_of(k_ref, c * 8, 8), ((0,), (0,)))
        full = part if full is None else full + part
    dq_ref[pl.ds(pl.multiple_of(edge * BLOCK, BLOCK), BLOCK), :] = (
        own_heads(full, masks) * 0.125
    ).astype(jnp.bfloat16)

    def scatter(acc, piece, block, picks):
        b = BLOCK
        acc[0:b, :] += piece[:b]
        acc[last * b : (last + 1) * b, :] += piece[b : 2 * b]
        window = pl.ds(pl.multiple_of((block - 1) * b, b), 3 * b)
        acc[window, :] += piece[2 * b : 5 * b]
        for r, p in enumerate(picks):
            part = piece[(5 + r) * b : (6 + r) * b]
            for pair in range(PACK // 2):
                lanes = slice(pair * 2 * HEAD, (pair + 1) * 2 * HEAD)
                cols = pl.ds(pair * 2 * HEAD, 2 * HEAD)
                sub = part[:, lanes]
                acc[pl.ds(pl.multiple_of(p[2 * pair] * b, b), b), cols] += jnp.where(
                    low_half, sub, 0.0
                )
                acc[pl.ds(pl.multiple_of(p[2 * pair + 1] * b, b), b), cols] += jnp.where(
                    low_half, 0.0, sub
                )

    def middle(step, carry):
        mine = step + 1 - half
        block = mine + local * half
        picks = [
            [table_ref[group * PACK + h, block - 1, r] for h in range(PACK)]
            for r in range(picks_each)
        ]
        spread = spread_heads(rows_of(q_ref, mine), masks)
        spread_do = spread_heads(flat_rows(do_ref, mine), masks)
        keys = gathered(k_ref, block, last, picks, low_half)
        values = gathered(v_ref, block, last, picks, low_half)
        scores = middle_scores(keys, spread, block, last)
        probs = jnp.exp(scores - lse_ref[0, pl.ds(mine, 1), :])
        gp = wide_dot(values, spread_do, ((1,), (1,)))
        delta = jnp.sum(probs * gp, axis=0, keepdims=True)
        ds = (probs * (gp - delta)).astype(jnp.bfloat16)
        low = probs.astype(jnp.bfloat16)
        scatter(dv_acc, wide_dot(low, spread_do, ((1,), (0,))), block, picks)
        scatter(dk_acc, wide_dot(ds, spread, ((1,), (0,))), block, picks)
        full = wide_dot(ds, keys, ((0,), (0,)))
        dq_ref[pl.ds(pl.multiple_of(mine * BLOCK, BLOCK), BLOCK), :] = (
            own_heads(full, masks) * 0.125
        ).astype(jnp.bfloat16)
        return carry

    lax.fori_loop(0, local - 1, middle, 0, unroll=unroll)
    dk_ref[...] = dk_acc[...].astype(jnp.bfloat16)
    dv_ref[...] = dv_acc[...].astype(jnp.bfloat16)


def attend_back(half, table, q, k, v, lse, do, unroll=3):
    tokens, width = do.shape
    groups, nblocks, _, lanes = k.shape
    seq = nblocks * BLOCK
    blocks = tokens // BLOCK
    mine = pl.BlockSpec((tokens, lanes), lambda g, *_: (0, g))
    whole = pl.BlockSpec((seq, lanes), lambda g, *_: (0, g))
    spec = pltpu.PrefetchScalarGridSpec(
        num_scalar_prefetch=2,
        grid=(groups,),
        in_specs=[
            pl.BlockSpec((1, blocks, BLOCK, lanes), lambda g, *_: (g, 0, 0, 0)),
            pl.BlockSpec((1, nblocks, BLOCK, lanes), lambda g, *_: (g, 0, 0, 0)),
            pl.BlockSpec((1, nblocks, BLOCK, lanes), lambda g, *_: (g, 0, 0, 0)),
            pl.BlockSpec((1, blocks, lanes), lambda g, *_: (g, 0, 0)),
            mine,
        ],
        out_specs=[mine, whole, whole],
        scratch_shapes=[pltpu.VMEM((seq, lanes), jnp.float32)] * 4,
    )
    return pl.pallas_call(
        functools.partial(attend_back_kernel, unroll),
        grid_spec=spec,
        out_shape=[
            jax.ShapeDtypeStruct((tokens, width), jnp.bfloat16),
            jax.ShapeDtypeStruct((seq, width), jnp.bfloat16),
            jax.ShapeDtypeStruct((seq, width), jnp.bfloat16),
        ],
        name="attend_back",
        compiler_params=pltpu.CompilerParams(vmem_limit_bytes=56 << 20),
        cost_estimate=pl.CostEstimate(
            flops=120_000_000_000, bytes_accessed=24 << 20, transcendentals=16_000_000
        ),
    )(half, table, q, k, v, lse, do)


TILE = 256
MID = 512


def cols_mean(value):
    return jnp.mean(value, axis=-1, keepdims=True)


def normed(field):
    centred = field - cols_mean(field)
    rate = lax.rsqrt(cols_mean(centred * centred) + norm_eps)
    return centred * rate, rate


def norm_back(cot, normal, rate, gain):
    dn = cot * gain
    return rate * (dn - cols_mean(dn) - normal * cols_mean(dn * normal))


def matrix(ref):
    value = ref[...]
    return value.reshape(-1, value.shape[-1])


def add_row(ref, row, value):
    ref[row : row + 1, :] += jnp.sum(value, axis=0, keepdims=True)


def rest_spec(rest, which, single=True):
    groups, _, rows, width = rest.shape
    mode = pl.Buffered(1) if single else None
    return pl.BlockSpec(
        (groups, 1, rows, width), lambda step, info: (0, which(step) - 3, 0, 0), pipeline_mode=mode
    )


def fixed(shape):
    return pl.BlockSpec(shape, lambda step, info: (0,) * len(shape), pipeline_mode=pl.Buffered(1))


def call(kernel, name, info, grid, in_specs, out_specs, out_shape, scratch, args, flops, moved):
    return pl.pallas_call(
        kernel,
        name=name,
        grid_spec=pltpu.PrefetchScalarGridSpec(
            num_scalar_prefetch=1,
            grid=(grid,),
            in_specs=in_specs,
            out_specs=out_specs,
            scratch_shapes=scratch,
        ),
        out_shape=out_shape,
        compiler_params=pltpu.CompilerParams(vmem_limit_bytes=60 << 20),
        cost_estimate=pl.CostEstimate(
            flops=flops, bytes_accessed=moved, transcendentals=0
        ),
    )(info, *args)


def bf16_of(*shape):
    return jax.ShapeDtypeStruct(shape, jnp.bfloat16)


def f32_of(*shape):
    return jax.ShapeDtypeStruct(shape, jnp.float32)


NN = ((1,), (0,))
NT = ((1,), (1,))
TN = ((0,), (0,))


def front_kernel(
    info,
    ctx_ref,
    x_ref,
    small,
    wo,
    u0,
    u1,
    u2,
    u3,
    v0,
    v1,
    v2,
    v3,
    out_ref,
    n1_ref,
    r1_ref,
    fit_ref,
    hid_ref,
    gel_ref,
    n2_ref,
    r2_ref,
):
    attn_out = wide_dot(ctx_ref[...], matrix(wo), NN) + small[2:3, :]
    n1, r1 = normed(x_ref[0].astype(jnp.float32) + attn_out)
    n1_ref[...] = n1
    r1_ref[...] = jnp.broadcast_to(r1, r1_ref.shape)
    after = n1 * small[3:4, :] + small[4:5, :]
    ffn_in = after.astype(jnp.bfloat16)
    fit_ref[...] = ffn_in.T
    total = after + small[9:10, :]
    for b, (up_w, down_w) in enumerate(((u0, v0), (u1, v1), (u2, v2), (u3, v3))):
        up = wide_dot(ffn_in, matrix(up_w), NN) + small[5 + b : 6 + b, :]
        square = up * up
        bent = jnp.tanh(gelu_root * up * (1.0 + gelu_cube * square))
        rise = 0.5 * (1.0 + bent)
        hidden = (up * rise).astype(jnp.bfloat16)
        hid_ref[b] = hidden
        slope = rise + (0.5 * gelu_root) * up * (1.0 - bent * bent) * (
            1.0 + (3.0 * gelu_cube) * square
        )
        gel_ref[b] = slope.astype(jnp.bfloat16)
        total = total + wide_dot(hidden, matrix(down_w), NT)
    n2, r2 = normed(total)
    out_ref[0] = (n2 * small[10:11, :] + small[11:12, :]).astype(jnp.bfloat16)
    n2_ref[...] = n2
    r2_ref[...] = jnp.broadcast_to(r2, r2_ref.shape)


def front(info, ctx, x_all, small, rest):
    tokens, width = ctx.shape
    mid = x_all.shape[1]
    per = mid // TILE
    steps = tokens // TILE

    def arrived(t, info):
        return (info[1 + 2 * info[0] + t // per], t % per, 0)

    def rows(dtype_shape):
        return pl.BlockSpec(dtype_shape, lambda t, info: (t, 0))

    specs = [rest_spec(rest, lambda t, m=m: m) for m in range(3, 12)]
    wide4 = pl.BlockSpec((4, TILE, width), lambda t, info: (0, t, 0))
    flipped = pl.BlockSpec((width, TILE), lambda t, info: (0, t))
    return call(
        front_kernel,
        "front",
        info,
        steps,
        [
            rows((TILE, width)),
            pl.BlockSpec((1, TILE, width), arrived),
            fixed(small.shape),
            *specs,
        ],
        [
            pl.BlockSpec((1, TILE, width), arrived),
            rows((TILE, width)),
            rows((TILE, 128)),
            flipped,
            wide4,
            wide4,
            rows((TILE, width)),
            rows((TILE, 128)),
        ],
        [
            bf16_of(2, mid, width),
            f32_of(tokens, width),
            f32_of(tokens, 128),
            bf16_of(width, tokens),
            bf16_of(4, tokens, width),
            bf16_of(4, tokens, width),
            f32_of(tokens, width),
            f32_of(tokens, 128),
        ],
        [],
        (ctx, x_all, small, *([rest] * 9)),
        11_000_000_000,
        40 << 20,
    )


MESH = pl.DeviceIdType.MESH
KINDS = 3
CHUNKS = 3
HOOKS = (4, 5, 6)
PER = 3


def place_of():
    c, t = lax.axis_index("ctx"), lax.axis_index("tp")
    return lax.axis_index("shard"), c, t


def send(src, dst, sems, index, target):
    send_sems, recv_sems = sems
    return pltpu.make_async_remote_copy(
        src_ref=src,
        dst_ref=dst,
        send_sem=send_sems.at[index],
        recv_sem=recv_sems.at[index],
        device_id=target,
        device_id_type=MESH,
    )


def begin_kernel(
    n_shard,
    n_ctx,
    n_tp,
    slots,
    local_at,
    table,
    master_hbm,
    small_in,
    input_hbm,
    x_ref,
    first_ref,
    rest_ref,
    small_ref,
    q_ref,
    k_ref,
    v_ref,
    ctx_ref,
    lse_ref,
    raw,
    low,
    given,
    xs,
    x_all,
    part,
    got,
    mine,
    total,
    pool,
    sel,
    first,
    weights,
    small,
    q_s,
    k_s,
    v_s,
    ctx_s,
    kept,
    x_s,
    x_r,
    xt_s,
    xt_r,
    za_s,
    za_r,
    zb_s,
    zb_r,
    zc_s,
    zc_r,
    zd_s,
    zd_r,
    qm_s,
    qm_r,
    qt_s,
    qt_r,
    r_s,
    r_r,
    rt_s,
    rt_r,
    own_sem,
    out_sem,
):
    z, c, t = place_of()
    side, core, bit = t // 2, lax.rem(t, 2), lax.rem(c, 2)
    held, rows, width = low.shape[0] - 1, low.shape[1], low.shape[2]
    piece = mine.shape[0]
    me = c * n_tp + t
    _, mid, _ = xs.shape
    nblocks = 4 * mid // BLOCK
    local = nblocks // 2
    lanes = PACK * HEAD
    groups = width // lanes
    others = n_tp - 1

    take_raw = pltpu.make_async_copy(master_hbm, raw, own_sem.at[0])
    take_given = pltpu.make_async_copy(input_hbm, given, own_sem.at[1])
    take_raw.start()
    take_given.start()

    def far(dz):
        return (lax.rem(z + dz, n_shard), c, t)

    def across(mask):
        return (z, c ^ mask, t)

    def beside(dt):
        return (z, c, lax.rem(t + dt, n_tp))

    barrier = pltpu.get_barrier_semaphore()
    friends = [far(dz) for dz in range(1, n_shard)]
    friends += [(z, c ^ m, t) for m in range(1, n_ctx)]
    friends += [beside(dt) for dt in range(1, n_tp)]
    friends += [(z, c ^ m, t ^ 1) for m in range(1, n_ctx)]
    for friend in friends:
        pl.semaphore_signal(barrier, inc=1, device_id=friend, device_id_type=MESH)

    take_raw.wait()
    for j in range(held):
        low[j] = raw[j].astype(jnp.bfloat16)
    low[held] = jnp.zeros_like(low[held])
    pool[pl.ds(z * held, held)] = low[0:held]
    part[...] = jnp.zeros_like(part)
    for m in range(KINDS):
        part[m * rows : (m + 1) * rows, :] = low[local_at[m]]
    part[KINDS * rows : KINDS * rows + 16, :] = small_in[...].astype(jnp.bfloat16)
    pl.semaphore_wait(barrier, len(friends))

    def piece_at(k):
        return pl.ds(pl.multiple_of(k * piece, piece), piece)

    def hop_copy(s, way):
        sems = (zc_s, zc_r) if way > 0 else (zd_s, zd_r)
        slot = pl.ds((z - way * (s - 1)) * held, held)
        return send(
            pool.at[slot], pool.at[slot], sems, s - 1, (lax.rem(z + way + n_shard, n_shard), c, t)
        )

    def hop_on(s, way):
        start = z - way * (s - 1)
        end = z + way
        return (start >= 0) & (start < n_shard) & (end >= 0) & (end < n_shard)

    def hop(s):
        for way in (1, -1):

            @pl.when(hop_on(s, way))
            def move(way=way):
                if s > 1:
                    hop_copy(s - 1, way).wait_recv()
                hop_copy(s, way).start()

    za = [
        send(part.at[piece_at(far(dz)[0])], got.at[dz - 1], (za_s, za_r), dz - 1, far(dz))
        for dz in range(1, n_shard)
    ]
    for copy in za:
        copy.start()

    stays = c // 2 == core
    goes = [(z, 2 * core + (p ^ bit), 2 * side + c // 2) for p in range(2)]
    x_moves = [send(xs.at[p], x_all.at[p], (x_s, x_r), p, goes[p]) for p in range(2)]
    x_keep = pltpu.make_async_copy(xs.at[0], x_all.at[0], own_sem.at[2])
    take_given.wait()
    xs[0] = given[bit].astype(jnp.bfloat16)

    @pl.when(stays)
    def keep():
        x_keep.start()

    @pl.when(jnp.logical_not(stays))
    def leave():
        x_moves[0].start()

    xs[1] = given[1 - bit].astype(jnp.bfloat16)
    x_moves[1].start()

    summed = part[piece_at(z), :]
    for dz, copy in enumerate(za):
        copy.wait_recv()
        summed = summed + got[dz]
    mine[...] = summed
    zb = [
        send(mine, total.at[piece_at(z)], (zb_s, zb_r), dz - 1, far(dz))
        for dz in range(1, n_shard)
    ]
    for copy in zb:
        copy.start()
    hop(1)
    total[piece_at(z), :] = summed
    def hops_end():
        for way, end in ((1, n_shard - 1), (-1, 0)):

            @pl.when(z == end)
            def gather(way=way):
                for s in range(1, n_shard):
                    hop_copy(s, way).wait_recv()

    def hops_sent():
        for s in range(1, n_shard):
            for way in (1, -1):

                @pl.when(hop_on(s, way))
                def sent(s=s, way=way):
                    hop_copy(s, way).wait_send()

    for copy in zb:
        copy.wait_recv()
    hop(2)

    q_moves = [
        send(total, first.at[me], (qm_s, qm_r), k, across(m)) for k, m in enumerate((1, 2, 3))
    ]
    for copy in q_moves:
        copy.start()
    qt_moves = [
        send(total, first.at[me], (qt_s, qt_r), dt - 1, beside(dt)) for dt in range(1, n_tp)
    ]
    for copy in qt_moves:
        copy.start()
    first[me] = total[...]

    x_over = [
        send(x_all.at[p], x_all.at[2 + p], (xt_s, xt_r), p, (z, c, t ^ 1)) for p in range(2)
    ]

    @pl.when(stays)
    def stayed():
        x_keep.wait()

    @pl.when(jnp.logical_not(stays))
    def came():
        x_moves[0].wait_recv()

    x_over[0].start()
    x_moves[1].wait_recv()
    x_over[1].start()
    for s in range(3, n_shard):
        hop(s)

    for k, m in enumerate((1, 2, 3)):
        q_moves[k].wait_recv()
        place = (c ^ m) * n_tp + t
        for dt in range(1, n_tp):
            copy = send(
                first.at[place],
                first.at[place],
                (qt_s, qt_r),
                (k + 1) * others + dt - 1,
                beside(dt),
            )
            copy.start()
            qt_moves.append(copy)
    for copy in qt_moves:
        copy.wait_recv()
    def span_of(k):
        return pl.ds(k * PER, PER)

    rest_own = pltpu.make_async_copy(sel, rest_ref.at[me], own_sem.at[3])
    direct = [
        [
            send(
                sel.at[span_of(k)], rest_ref.at[me, span_of(k)], (r_s, r_r), k * 3 + j, across(m)
            )
            for j, m in enumerate((1, 2))
        ]
        for k in range(CHUNKS)
    ]
    onward = []
    for k in range(CHUNKS):
        odd = lax.rem(core + k, 2)
        source = jnp.where(odd == 0, c ^ 1, c ^ 2) * n_tp + t
        target = (z, jnp.where(odd == 0, c ^ 2, c ^ 1), t)
        view = rest_ref.at[source, span_of(k)]
        onward.append(send(view, view, (r_s, r_r), k * 3 + 2, target))

    def passing(k, which):
        if which == 0:
            src = sel.at[span_of(k)]
        else:
            src = rest_ref.at[(c ^ which) * n_tp + t, span_of(k)]
        dst = rest_ref.at[(c ^ which) * n_tp + t, span_of(k)]
        return [
            send(src, dst, (rt_s, rt_r), (k * 4 + which) * others + dt - 1, beside(dt))
            for dt in range(1, n_tp)
        ]

    passed = [[passing(k, which) for which in range(4)] for k in range(CHUNKS)]

    def begin_rest():
        hops_end()
        for m in range(CHUNKS * PER):
            sel[m] = pool[slots[KINDS + m]]
        rest_own.start()
        for k in range(CHUNKS):
            for copy in direct[k]:
                copy.start()
            for copy in passed[k][0]:
                copy.start()

    def relay(k):
        for copy in direct[k]:
            copy.wait_recv()
        onward[k].start()
        for copy in passed[k][1] + passed[k][2]:
            copy.start()

    def last_relay(k):
        onward[k].wait_recv()
        for copy in passed[k][3]:
            copy.start()

    begin_rest()
    outs = [pltpu.make_async_copy(first, first_ref, out_sem.at[0])]
    outs[0].start()

    sums = None
    for g in range(n_ctx * n_tp):
        here = first[g, KINDS * rows : KINDS * rows + 16, :].astype(jnp.float32)
        sums = here if sums is None else sums + here
    small[...] = sums
    small_ref[...] = sums
    for m in range(KINDS):
        weights[m] = first[:, m * rows : (m + 1) * rows, :].reshape(width, width)

    def split(dst, start, value):
        low_value = value.astype(jnp.bfloat16)
        per = TILE // BLOCK
        for g in range(groups):
            piece_value = low_value[:, g * lanes : (g + 1) * lanes]
            dst[g, pl.ds(start, per)] = piece_value.reshape(per, BLOCK, lanes)

    def project(a, chunk, own):
        def one(i, carry):
            x = x_all[a, pl.ds(pl.multiple_of(i * TILE, TILE), TILE), :]
            start = chunk * (mid // BLOCK) + i * (TILE // BLOCK)
            if own:
                q_start = (chunk - 2 * core) * (mid // BLOCK) + i * (TILE // BLOCK)
                q = wide_dot(x, weights[0], NN) + small[0:1, :]
                split(q_s, q_start, q.astype(jnp.bfloat16) * jnp.bfloat16(score_scale))
            split(k_s, start, wide_dot(x, weights[1], NN))
            split(v_s, start, wide_dot(x, weights[2], NN) + small[1:2, :])
            return carry

        lax.fori_loop(0, mid // TILE, one, 0)

    def own_project(a, carry):
        project(a, 2 * core + (a ^ bit), True)
        return carry

    def other_project(a, carry):
        project(2 + a, 2 * (1 - core) + (a ^ bit), False)
        return carry

    lax.fori_loop(0, 2, own_project, 0)
    for copy in x_over:
        copy.wait_recv()
    outs.append(pltpu.make_async_copy(x_all, x_ref, out_sem.at[1]))
    outs[1].start()
    lax.fori_loop(0, 2, other_project, 0)
    for i, (src, dst) in enumerate(((q_s, q_ref), (k_s, k_ref), (v_s, v_ref))):
        outs.append(pltpu.make_async_copy(src, dst, out_sem.at[2 + i]))
        outs[-1].start()

    last = nblocks - 1
    picks_each = table.shape[2]
    masks = head_masks(BLOCK)
    low_half = lax.broadcasted_iota(jnp.int32, (BLOCK, 2 * HEAD), 1) < HEAD
    each = 5
    subs = (local - 1) // each

    def attend_round(i, carry):
        g = i // subs
        sub = lax.rem(i, subs)
        qg, kg, vg = q_s.at[g], k_s.at[g], v_s.at[g]
        for k in range(CHUNKS):

            @pl.when(i == HOOKS[k])
            def hook(k=k):
                relay(k)

        @pl.when(sub == 0)
        def edge_block():
            edge = (local - 1) * core
            spread = spread_heads(rows_of(qg, edge), masks)
            span = 8 * BLOCK
            pieces = nblocks // 8
            top = None
            for n in range(pieces):
                scores = wide_dot(rows_of(kg, n * 8, 8), spread, NT)
                kept[n * span : (n + 1) * span, :] = scores
                high = jnp.max(scores, axis=0, keepdims=True)
                top = high if top is None else jnp.maximum(top, high)
            total_p = None
            for n in range(pieces):
                probs = jnp.exp(kept[n * span : (n + 1) * span, :] - top)
                kept[n * span : (n + 1) * span, :] = probs
                some = jnp.sum(probs, axis=0, keepdims=True)
                total_p = some if total_p is None else total_p + some
            scale = 1.0 / total_p
            full = None
            for n in range(pieces):
                probs = (kept[n * span : (n + 1) * span, :] * scale).astype(jnp.bfloat16)
                some = wide_dot(probs, rows_of(vg, n * 8, 8), TN)
                full = some if full is None else full + some
            at = pl.ds(pl.multiple_of(edge * BLOCK, BLOCK), BLOCK)
            ctx_s[g, at, :] = own_heads(full, masks).astype(jnp.bfloat16)
            lse_ref[g, pl.ds(edge, 1), :] = top + jnp.log(total_p)

        for u in range(each):
            spot = sub * each + u + 1 - core
            block = spot + local * core
            picks = [
                [table[g * PACK + h, block - 1, r] for h in range(PACK)]
                for r in range(picks_each)
            ]
            spread = spread_heads(rows_of(qg, spot), masks)
            keys = gathered(kg, block, last, picks, low_half)
            values = gathered(vg, block, last, picks, low_half)
            scores = middle_scores(keys, spread, block, last)
            top = jnp.max(scores, axis=0, keepdims=True)
            probs = jnp.exp(scores - top)
            total_p = jnp.sum(probs, axis=0, keepdims=True)
            probs = (probs * (1.0 / total_p)).astype(jnp.bfloat16)
            full = wide_dot(probs, values, TN)
            at = pl.ds(pl.multiple_of(spot * BLOCK, BLOCK), BLOCK)
            ctx_s[g, at, :] = own_heads(full, masks).astype(jnp.bfloat16)
            lse_ref[g, pl.ds(spot, 1), :] = top + jnp.log(total_p)
        return carry

    lax.fori_loop(0, groups * subs, attend_round, 0)
    for g in range(groups):
        outs.append(
            pltpu.make_async_copy(
                ctx_s.at[g], ctx_ref.at[:, g * lanes : (g + 1) * lanes], out_sem.at[5 + g]
            )
        )
        outs[-1].start()
    for k in range(CHUNKS):
        last_relay(k)

    @pl.when(jnp.logical_not(stays))
    def left():
        x_moves[0].wait_send()

    x_moves[1].wait_send()
    for copy in (*x_over, *za, *zb, *q_moves, *qt_moves, *onward):
        copy.wait_send()
    for pair in direct:
        for copy in pair:
            copy.wait_send()
    for chunk in passed:
        for group in chunk:
            for copy in group:
                copy.wait()
    hops_sent()
    rest_own.wait()
    for copy in outs:
        copy.wait()


def begin(slots, local_at, table, master, small_in, inputs, n_shard, n_ctx, n_tp):
    held, rows, width = master.shape
    _, mid, _ = inputs.shape
    groups = n_ctx * n_tp
    long = -(-(KINDS * rows + 16) // (16 * n_shard)) * 16 * n_shard
    lanes = PACK * HEAD
    packs = width // lanes
    tokens, seq = 2 * mid, 4 * mid
    anywhere = pl.BlockSpec(memory_space=pl.ANY)
    vmem = pl.BlockSpec(memory_space=pltpu.VMEM)
    smem = pl.BlockSpec(memory_space=pltpu.SMEM)
    dma = pltpu.SemaphoreType.DMA
    low = jnp.bfloat16
    f32 = jnp.float32
    pairs = [2, 2, n_shard - 1, n_shard - 1, n_shard - 1, n_shard - 1, 3]
    pairs += [4 * (n_tp - 1), 3 * CHUNKS, 4 * CHUNKS * (n_tp - 1)]
    return pl.pallas_call(
        functools.partial(begin_kernel, n_shard, n_ctx, n_tp),
        name="begin",
        in_specs=[smem, smem, smem, anywhere, vmem, anywhere],
        out_specs=[anywhere, anywhere, anywhere, vmem, anywhere, anywhere, anywhere, anywhere, vmem],
        out_shape=[
            bf16_of(4, mid, width),
            bf16_of(groups, long, width),
            bf16_of(groups, 9, rows, width),
            f32_of(16, width),
            bf16_of(packs, tokens // BLOCK, BLOCK, lanes),
            bf16_of(packs, seq // BLOCK, BLOCK, lanes),
            bf16_of(packs, seq // BLOCK, BLOCK, lanes),
            bf16_of(tokens, width),
            f32_of(packs, tokens // BLOCK, lanes),
        ],
        scratch_shapes=[
            pltpu.VMEM((held, rows, width), f32),
            pltpu.VMEM((held + 1, rows, width), low),
            pltpu.VMEM((2, mid, width), f32),
            pltpu.VMEM((2, mid, width), low),
            pltpu.VMEM((4, mid, width), low),
            pltpu.VMEM((long, width), low),
            pltpu.VMEM((n_shard - 1, long // n_shard, width), low),
            pltpu.VMEM((long // n_shard, width), low),
            pltpu.VMEM((long, width), low),
            pltpu.VMEM((n_shard * held, rows, width), low),
            pltpu.VMEM((9, rows, width), low),
            pltpu.VMEM((groups, long, width), low),
            pltpu.VMEM((3, width, width), low),
            pltpu.VMEM((16, width), f32),
            pltpu.VMEM((packs, tokens // BLOCK, BLOCK, lanes), low),
            pltpu.VMEM((packs, seq // BLOCK, BLOCK, lanes), low),
            pltpu.VMEM((packs, seq // BLOCK, BLOCK, lanes), low),
            pltpu.VMEM((packs, tokens, lanes), low),
            pltpu.VMEM((seq, lanes), f32),
            *[dma((n,)) for n in pairs for _ in range(2)],
            dma((4,)),
            dma((8,)),
        ],
        compiler_params=pltpu.CompilerParams(
            collective_id=0, has_side_effects=True, vmem_limit_bytes=62 << 20
        ),
        cost_estimate=pl.CostEstimate(
            flops=60_000_000_000, bytes_accessed=60 << 20, transcendentals=16_000_000
        ),
    )(slots, local_at, table, master, small_in, inputs)


NEAR = 2


def back_kernel(
    n_ctx,
    n_tp,
    n2_hbm,
    r2_ref,
    cot0_ref,
    cot1_ref,
    hid_ref,
    gel_ref,
    fit_ref,
    n1_ref,
    r1_ref,
    ctx_ref,
    small,
    up_w,
    down_w,
    wo,
    layer_ref,
    own_ref,
    near_ref,
    x_ref,
    y_ref,
    xy_ref,
    gh1_ref,
    dctx_ref,
    sums_ref,
    home_ref,
    gy,
    gu,
    mixed,
    mixed_t,
    grads,
    arrived,
    sums,
    send_sem,
    recv_sem,
    h_s,
    h_r,
    n_s,
    n_r,
    keep_sem,
    out_sem,
):
    z, c, t = place_of()
    step = pl.program_id(0)
    tokens, width = gy.shape
    tiles = tokens // TILE
    rows = grads.shape[4]
    others = n_tp - 1
    side, core, bit = t // 2, lax.rem(t, 2), lax.rem(c, 2)

    def beside(dt):
        return (z, c, lax.rem(t + dt, n_tp))

    stays = c // 2 == core
    keep_layer = pltpu.make_async_copy(layer_ref.at[0], home_ref.at[bit], keep_sem.at[0])
    layer_moves = [
        send(
            layer_ref.at[p],
            home_ref.at[bit],
            (h_s, h_r),
            p,
            (z, 2 * core + (p ^ bit), 2 * side + c // 2),
        )
        for p in range(2)
    ]

    @pl.when(step == 0)
    def start():
        take = pltpu.make_async_copy(n2_hbm, gy, keep_sem.at[1])
        take.start()
        barrier = pltpu.get_barrier_semaphore()
        friends = [beside(dt) for dt in range(1, n_tp)]
        friends += [(z, c ^ m, t) for m in range(1, n_ctx)]
        friends += [(z, c ^ m, t ^ 1) for m in range(1, n_ctx)]
        for friend in friends:
            pl.semaphore_signal(barrier, inc=1, device_id=friend, device_id_type=MESH)
        pl.semaphore_wait(barrier, len(friends))

        @pl.when(stays)
        def kept():
            keep_layer.start()

        @pl.when(jnp.logical_not(stays))
        def left():
            layer_moves[0].start()

        layer_moves[1].start()
        sums_ref[...] = jnp.zeros_like(sums_ref)
        take.wait()
        mid = tokens // 2
        for p, cot_ref in enumerate((cot0_ref, cot1_ref)):

            def one(i, carry, p=p, cot_ref=cot_ref):
                inside = pl.ds(pl.multiple_of(i * TILE, TILE), TILE)
                at = pl.ds(pl.multiple_of((p ^ bit) * mid + i * TILE, TILE), TILE)
                cot = cot_ref[inside, :].astype(jnp.float32)
                n2 = gy[at, :]
                add_row(sums_ref, 10, cot * n2)
                add_row(sums_ref, 11, cot)
                gh2 = norm_back(cot, n2, r2_ref[at, 0:1], small[10:11, :])
                gy[at, :] = gh2
                low = gh2.astype(jnp.bfloat16)
                mixed[at, :] = low
                mixed_t[:, at] = low.T
                add_row(sums_ref, 9, low.astype(jnp.float32))
                return carry

            lax.fori_loop(0, mid // TILE, one, 0)

    def moves(b, count):
        slot = lax.rem(b, 2)
        return [
            send(
                grads.at[slot, :, lax.rem(t + dt, n_tp), 0:count],
                arrived.at[b, dt - 1, :, 0:count],
                (send_sem, recv_sem),
                b * others + dt - 1,
                beside(dt),
            )
            for dt in range(1, n_tp)
        ]

    def exchange(b, count):
        for copy in moves(b, count):
            copy.start()

    def keep(b, count):
        for copy in moves(b, count):
            copy.wait()
        slot = lax.rem(b, 2)
        for j in range(n_ctx):
            for i in range(count):
                value = grads[slot, c ^ j, t, i]
                for dt in range(others):
                    value = value + arrived[b, dt, c ^ j, i]
                sums[j, 2 * b + i] = value

    def near(b):
        pair = slice(2 * b, 2 * b + 2)
        return [
            send(
                sums.at[j, pair],
                near_ref.at[j - 1, pair],
                (n_s, n_r),
                b * (n_ctx - 1) + j - 1,
                (z, c ^ j, t),
            )
            for j in range(1, n_ctx)
        ]

    def outward(part, first, count):
        moved = [
            pltpu.make_async_copy(
                sums.at[0, first : first + count],
                own_ref.at[first : first + count],
                out_sem.at[part * n_ctx],
            )
        ]
        begin_at = max(first, NEAR)
        count -= begin_at - first
        for j, out in enumerate((x_ref, y_ref, xy_ref)):
            moved.append(
                pltpu.make_async_copy(
                    sums.at[j + 1, begin_at : begin_at + count],
                    out.at[begin_at - NEAR : begin_at - NEAR + count],
                    out_sem.at[part * n_ctx + j + 1],
                )
            )
        return moved

    def put(slot, i, value):
        low = value.astype(jnp.bfloat16)
        grads[slot, :, :, i] = low.reshape(n_ctx, n_tp, rows, width)

    @pl.when(step < 4)
    def ffn():
        up_block = matrix(up_w)
        down_block = matrix(down_w)
        slot = lax.rem(step, 2)

        def one(i, carry):
            at = pl.ds(pl.multiple_of(i * MID, MID), MID)
            grad = wide_dot(mixed[at, :], down_block, NN) * gel_ref[0, at, :].astype(jnp.float32)
            low = grad.astype(jnp.bfloat16)
            gu[at, :] = low
            gy[at, :] += wide_dot(low, up_block, NT)
            sums_ref[pl.ds(5 + step, 1), :] += jnp.sum(
                low.astype(jnp.float32), axis=0, keepdims=True
            )
            return carry

        lax.fori_loop(0, tokens // MID, one, 0)
        put(slot, 0, wide_dot(fit_ref[...], gu[...], NN))
        put(slot, 1, wide_dot(mixed_t[...], hid_ref[0], NN))
        exchange(step, 2)

    @pl.when(step > 0)
    def settle():
        keep(step - 1, 2)

    for b in range(NEAR // 2):

        @pl.when(step == b + 1)
        def cross(b=b):
            for copy in near(b):
                copy.start()

    @pl.when(step == 4)
    def first_norm():
        for copy in outward(0, 0, 8):
            copy.start()

        def one(i, carry):
            at = pl.ds(pl.multiple_of(i * TILE, TILE), TILE)
            grad = gy[at, :]
            n1 = n1_ref[at, :]
            gh1 = norm_back(grad, n1, r1_ref[at, 0:1], small[3:4, :])
            gh1_ref[at, :] = gh1
            low = gh1.astype(jnp.bfloat16)
            gu[at, :] = low
            add_row(sums_ref, 2, low.astype(jnp.float32))
            add_row(sums_ref, 3, grad * n1)
            add_row(sums_ref, 4, grad)
            return carry

        lax.fori_loop(0, tiles, one, 0)
        put(0, 0, wide_dot(ctx_ref[...].T, gu[...], NN))
        exchange(4, 1)
        out_w = matrix(wo)

        def two(i, carry):
            at = pl.ds(pl.multiple_of(i * TILE, TILE), TILE)
            dctx_ref[at, :] = wide_dot(gu[at, :], out_w, NT).astype(jnp.bfloat16)
            return carry

        lax.fori_loop(0, tiles, two, 0)
        keep(4, 1)
        for copy in outward(1, 8, 1):
            copy.start()
        for copy in (*near(0), *outward(0, 0, 8), *outward(1, 8, 1)):
            copy.wait()

        @pl.when(stays)
        def done():
            keep_layer.wait()

        @pl.when(jnp.logical_not(stays))
        def gone():
            layer_moves[0].wait()

        layer_moves[1].wait()


def back(n2, r2, cots, hid, gel, fit, n1, r1, ctx, small, rest, layer, n_ctx, n_tp):
    tokens, width = n2.shape
    rows = rest.shape[2]
    dma = pltpu.SemaphoreType.DMA

    def whole(shape):
        return pl.BlockSpec(shape, lambda b: (0,) * len(shape), pipeline_mode=pl.Buffered(1))

    def block(b):
        return (jnp.minimum(b, 3), 0, 0)

    def held(first, single=False):
        return pl.BlockSpec(
            (n_ctx * n_tp, 1, rows, width),
            (lambda b: (0, first, 0, 0))
            if single
            else (lambda b: (0, first + jnp.minimum(b, 3), 0, 0)),
            pipeline_mode=pl.Buffered(1) if single else None,
        )

    def out(shape):
        return pl.BlockSpec(shape, lambda b: (0,) * len(shape))

    return pl.pallas_call(
        functools.partial(back_kernel, n_ctx, n_tp),
        name="back",
        grid=(5,),
        in_specs=[
            pl.BlockSpec(memory_space=pl.ANY),
            whole((tokens, 128)),
            whole((tokens // 2, width)),
            whole((tokens // 2, width)),
            pl.BlockSpec((1, tokens, width), block),
            pl.BlockSpec((1, tokens, width), block),
            whole((width, tokens)),
            whole((tokens, width)),
            whole((tokens, 128)),
            whole((tokens, width)),
            whole(small.shape),
            held(1),
            held(5),
            held(0, True),
            pl.BlockSpec(memory_space=pl.ANY),
        ],
        out_specs=[
            *[pl.BlockSpec(memory_space=pl.ANY)] * 5,
            out((tokens, width)),
            out((tokens, width)),
            out((16, width)),
            pl.BlockSpec(memory_space=pl.ANY),
        ],
        out_shape=[
            bf16_of(9, rows, width),
            bf16_of(n_ctx - 1, NEAR, rows, width),
            *[bf16_of(9 - NEAR, rows, width)] * 3,
            f32_of(tokens, width),
            bf16_of(tokens, width),
            f32_of(16, width),
            bf16_of(*layer.shape),
        ],
        scratch_shapes=[
            pltpu.VMEM((tokens, width), jnp.float32),
            pltpu.VMEM((tokens, width), jnp.bfloat16),
            pltpu.VMEM((tokens, width), jnp.bfloat16),
            pltpu.VMEM((width, tokens), jnp.bfloat16),
            pltpu.VMEM((2, n_ctx, n_tp, 2, rows, width), jnp.bfloat16),
            pltpu.VMEM((5, n_tp - 1, n_ctx, 2, rows, width), jnp.bfloat16),
            pltpu.VMEM((n_ctx, 9 + 1, rows, width), jnp.bfloat16),
            dma((5 * (n_tp - 1),)),
            dma((5 * (n_tp - 1),)),
            dma((2,)),
            dma((2,)),
            dma((n_ctx - 1,)),
            dma((n_ctx - 1,)),
            dma((2,)),
            dma((2 * n_ctx,)),
        ],
        compiler_params=pltpu.CompilerParams(
            collective_id=3, has_side_effects=True, vmem_limit_bytes=62 << 20
        ),
        cost_estimate=pl.CostEstimate(
            flops=22_000_000_000, bytes_accessed=40 << 20, transcendentals=0
        ),
    )(n2, r2, *cots, hid, gel, fit, n1, r1, ctx, small, rest, rest, rest, layer)


LATE = 3
EARLY = 9


def adam_update(weight, first, second, grad, decay, rate):
    count = float(STEP)
    first_new = beta_one * first + (1.0 - beta_one) * grad
    second_new = beta_two * second + (1.0 - beta_two) * grad * grad
    first_hat = first_new / (1.0 - beta_one**count)
    second_hat = second_new / (1.0 - beta_two**count)
    weight_new = weight - rate * (first_hat / (jnp.sqrt(second_hat) + adam_eps) + decay * weight)
    return (weight_new, first_new, second_new)


def finish_kernel(
    n_shard,
    n_ctx,
    n_tp,
    holder,
    late_at,
    x_hbm,
    dq_hbm,
    dk_hbm,
    dv_hbm,
    gh1_hbm,
    first_hbm,
    e0_hbm,
    near_hbm,
    e1_hbm,
    e2_hbm,
    e3_hbm,
    small_ref,
    w_ref,
    one_ref,
    two_ref,
    home_ref,
    w_out,
    one_out,
    two_out,
    small_out,
    x_s,
    dq_s,
    dk_s,
    dv_s,
    gh1_s,
    first_s,
    early,
    every,
    packed,
    right_met,
    left_met,
    flipped,
    grads,
    arrived,
    partial,
    met,
    over,
    more,
    back_s,
    small_s,
    small_t,
    small_m,
    small_p,
    flat_a,
    met_a,
    sum_a,
    mine_a,
    flat_b,
    met_b,
    sum_b,
    mine_b,
    pool,
    in_sem,
    c_s,
    c_r,
    p_s,
    p_r,
    o_s,
    o_r,
    h_s,
    h_r,
    sc_s,
    sc_r,
    sp_s,
    sp_r,
    e_s,
    e_r,
    l_s,
    l_r,
    a_s,
    a_r,
    b_s,
    b_r,
    d_s,
    d_r,
    f_s,
    f_r,
    keep_sem,
):
    z, c, t = place_of()
    side, core, bit = t // 2, lax.rem(t, 2), lax.rem(c, 2)
    _, mid, width = x_s.shape
    tokens = 2 * mid
    held, rows, _ = w_ref.shape
    per = n_ctx * n_tp // 2
    band = width // 2
    tile = mid

    loads = [
        pltpu.make_async_copy(src, dst, in_sem.at[i])
        for i, (src, dst) in enumerate(
            (
                (x_hbm, x_s),
                (dk_hbm, dk_s),
                (dv_hbm, dv_s),
                (dq_hbm, dq_s),
                (first_hbm, first_s),
                (gh1_hbm, gh1_s),
                (e0_hbm, early.at[0]),
                (near_hbm, early.at[1:4, 0:NEAR]),
                (e1_hbm, early.at[1, NEAR:EARLY]),
                (e2_hbm, early.at[2, NEAR:EARLY]),
                (e3_hbm, early.at[3, NEAR:EARLY]),
            )
        )
    ]
    for i in (6, 7, 8, 9, 10, 0, 1, 2, 3, 4, 5):
        loads[i].start()

    def far(dz):
        return (lax.rem(z + dz, n_shard), c, t)

    def across(mask):
        return (z, c ^ mask, t)

    def beside(dt):
        return (z, c, lax.rem(t + dt, n_tp))

    barrier = pltpu.get_barrier_semaphore()
    friends = [far(dz) for dz in range(1, n_shard)]
    friends += [(z, c ^ m, t) for m in range(1, n_ctx)]
    friends += [beside(dt) for dt in range(1, n_tp)]
    friends += [(z, c ^ m, t ^ 1) for m in range(1, n_ctx)]
    for friend in friends:
        pl.semaphore_signal(barrier, inc=1, device_id=friend, device_id_type=MESH)

    for i in range(6, 11):
        loads[i].wait()
    every[0:EARLY] = early[0] + early[1] + early[2] + early[3]
    every[EARLY] = jnp.zeros_like(every[EARLY])
    for s in range(n_shard * held):
        packed[s // held, s % held] = every[holder[s]]
    pl.semaphore_wait(barrier, len(friends))

    def run(owner_at, s, way):
        met, sems = (right_met, (e_s, e_r)) if way > 0 else (left_met, (l_s, l_r))
        target = (lax.rem(z + way + n_shard, n_shard), c, t)
        return send(packed.at[owner_at], met.at[s], sems, s, target)

    def each_run(hop):
        for s in range(hop + 1):
            for way in (1, -1):
                place = hop - s if way > 0 else n_shard - 1 - (hop - s)
                owner_at = n_shard - 1 - s if way > 0 else s
                yield s, way, place, owner_at

    def hop(h):
        for s, way, place, owner_at in each_run(h):

            @pl.when(z == place)
            def move(s=s, way=way, place=place, owner_at=owner_at):
                copy = run(owner_at, s, way)
                if h > s:
                    copy.wait_recv()
                    met = right_met if way > 0 else left_met
                    for j in range(held):
                        packed[owner_at, j] = packed[owner_at, j] + met[s, j]
                copy.start()

    def hops_end():
        for h in range(n_shard - 1):
            for s, way, place, owner_at in each_run(h):

                @pl.when(z == place)
                def sent(s=s, way=way, owner_at=owner_at):
                    run(owner_at, s, way).wait_send()

        for s in range(n_shard - 1):
            for way in (1, -1):
                owner_at = n_shard - 1 - s if way > 0 else s

                @pl.when(z == owner_at)
                def last(s=s, way=way, owner_at=owner_at):
                    run(owner_at, s, way).wait_recv()
                    met = right_met if way > 0 else left_met
                    for j in range(held):
                        packed[owner_at, j] = packed[owner_at, j] + met[s, j]

    hop(0)

    core_moves = []

    def exchange(m):
        for dt in range(1, n_tp):
            other = lax.rem(t + dt, n_tp)
            for k in range(n_ctx):
                copy = send(
                    grads.at[k * n_tp + other, m],
                    arrived.at[dt - 1, k, m],
                    (c_s, c_r),
                    ((dt - 1) * n_ctx + k) * LATE + m,
                    beside(dt),
                )
                copy.start()
                core_moves.append((m, copy))

    plane_moves = []

    def meet(m):
        for which, copy in core_moves:
            if which == m:
                copy.wait_recv()
        for k in range(n_ctx):
            value = grads[k * n_tp + t, m]
            for dt in range(1, n_tp):
                value = value + arrived[dt - 1, k, m]
            partial[k, m] = value
        for j in range(1, n_ctx):
            copy = send(
                partial.at[c ^ j, m], met.at[j - 1, m], (p_s, p_r), (j - 1) * LATE + m, across(j)
            )
            copy.start()
            plane_moves.append((m, copy))

    loads[0].wait()
    for a in range(4):
        chunk = 2 * (core if a < 2 else 1 - core) + ((a % 2) ^ bit)
        flipped[:, pl.ds(pl.multiple_of(chunk * mid, mid), mid)] = x_s[a].T

    def weight_grad(m, left_at, right):
        def one(i, carry):
            left = flipped[pl.ds(pl.multiple_of(i * band, band), band), left_at]
            value = wide_dot(left, right[...], NN).astype(jnp.bfloat16)
            grads[pl.ds(i * per, per), m] = value.reshape(per, rows, width)
            return carry

        lax.fori_loop(0, 2, one, 0)

    loads[1].wait()
    weight_grad(1, slice(None), dk_s)
    exchange(1)
    loads[2].wait()
    weight_grad(2, slice(None), dv_s)
    exchange(2)
    meet(1)
    loads[3].wait()
    weight_grad(0, pl.ds(pl.multiple_of(core * tokens, tokens), tokens), dq_s)
    exchange(0)
    meet(2)
    for h in range(1, n_shard - 2):
        hop(h)

    row = lax.broadcasted_iota(jnp.int32, small_ref.shape, 0)
    q_sum = jnp.sum(dq_s[...].astype(jnp.float32), axis=0, keepdims=True)
    v_sum = jnp.sum(dv_s[...].astype(jnp.float32), axis=0, keepdims=True)
    sums = jnp.where(row == 0, q_sum, jnp.where(row == 1, v_sum, small_ref[...]))
    small_s[...] = sums.astype(jnp.bfloat16)
    small_core = [
        send(small_s, small_t.at[dt - 1], (sc_s, sc_r), dt - 1, beside(dt)) for dt in range(1, n_tp)
    ]
    for copy in small_core:
        copy.start()

    loads[4].wait()

    def weight(m):
        return first_s[:, m * rows : (m + 1) * rows, :].reshape(width, width)

    wq, wk, wv = weight(0), weight(1), weight(2)
    over_moves = []
    for b in range(2):
        at = pl.ds(pl.multiple_of((1 - core) * tokens + b * mid, mid), mid)
        value = wide_dot(dk_s[at, :], wk, NT) + wide_dot(dv_s[at, :], wv, NT)
        over[b] = value.astype(jnp.bfloat16)
        copy = send(over.at[b], more.at[b], (o_s, o_r), b, (z, c, t ^ 1))
        copy.start()
        over_moves.append(copy)
        if b == 0:
            meet(0)

    value = small_s[...]
    for dt, copy in enumerate(small_core):
        copy.wait_recv()
        value = value + small_t[dt]
    small_m[...] = value
    small_plane = [
        send(small_m, small_p.at[j - 1], (sp_s, sp_r), j - 1, across(j)) for j in range(1, n_ctx)
    ]
    for copy in small_plane:
        copy.start()

    if n_shard > 2:
        hop(n_shard - 2)
    loads[5].wait()
    stays = c // 2 == core
    home_moves = []
    for copy in over_moves:
        copy.wait_recv()
    keep = pltpu.make_async_copy(back_s.at[0], home_ref.at[bit], keep_sem.at[0])
    for move in range(2):
        chunk = move ^ bit
        for i in range(mid // tile):
            at = pl.ds(pl.multiple_of(core * tokens + chunk * mid + i * tile, tile), tile)
            here = pl.ds(pl.multiple_of(chunk * mid + i * tile, tile), tile)
            value = gh1_s[here, :]
            value = value + more[chunk, i * tile : (i + 1) * tile, :].astype(jnp.float32)
            value = value + wide_dot(dq_s[here, :], wq, NT)
            value = value + wide_dot(dk_s[at, :], wk, NT)
            value = value + wide_dot(dv_s[at, :], wv, NT)
            back_s[move, i * tile : (i + 1) * tile, :] = value.astype(jnp.bfloat16)
        target = (z, 2 * core + chunk, 2 * side + c // 2)
        home_moves.append(send(back_s.at[move], home_ref.at[bit], (h_s, h_r), move, target))
        if move == 0:

            @pl.when(stays)
            def kept():
                keep.start()

            @pl.when(jnp.logical_not(stays))
            def left():
                home_moves[0].start()

        else:
            home_moves[1].start()

    def gathered_rows(m):
        for which, copy in plane_moves:
            if which == m:
                copy.wait_recv()
        value = partial[c, m]
        for j in range(n_ctx - 1):
            value = value + met[j, m]
        return value

    def piece_at(ref, k):
        piece = ref.shape[0] // n_shard
        return pl.ds(pl.multiple_of(k * piece, piece), piece)

    def scatter_lot(flat, lot_met, sems):
        moves = [
            send(flat.at[piece_at(flat, far(dz)[0])], lot_met.at[dz - 1], sems, dz - 1, far(dz))
            for dz in range(1, n_shard)
        ]
        for copy in moves:
            copy.start()
        return moves

    def spread_lot(moves, flat, lot_met, lot_sum, lot_mine, sems):
        total = flat[piece_at(flat, z), :].astype(jnp.float32)
        for dz, copy in enumerate(moves):
            copy.wait_recv()
            total = total + lot_met[dz].astype(jnp.float32)
        lot_mine[...] = total.astype(jnp.bfloat16)
        spreads = [
            send(lot_mine, lot_sum.at[piece_at(flat, z)], sems, dz - 1, far(dz))
            for dz in range(1, n_shard)
        ]
        for copy in spreads:
            copy.start()
        lot_sum[piece_at(flat, z), :] = lot_mine[...]
        return spreads

    small_rows = small_s.shape[0]
    flat_a[...] = jnp.zeros_like(flat_a)
    flat_b[...] = jnp.zeros_like(flat_b)
    flat_a[0:rows, :] = gathered_rows(1)
    flat_a[rows : 2 * rows, :] = gathered_rows(2)
    scatter_a = scatter_lot(flat_a, met_a, (a_s, a_r))
    flat_b[0:rows, :] = gathered_rows(0)
    value = small_m[...]
    for j, copy in enumerate(small_plane):
        copy.wait_recv()
        value = value + small_p[j]
    flat_b[rows : rows + small_rows, :] = value
    scatter_b = scatter_lot(flat_b, met_b, (b_s, b_r))
    spread_a = spread_lot(scatter_a, flat_a, met_a, sum_a, mine_a, (d_s, d_r))
    spread_b = spread_lot(scatter_b, flat_b, met_b, sum_b, mine_b, (f_s, f_r))
    hops_end()
    for copy in (*spread_a, *spread_b):
        copy.wait_recv()
    pool[0] = sum_b[0:rows, :]
    pool[1] = sum_a[0:rows, :]
    pool[2] = sum_a[rows : 2 * rows, :]
    pool[LATE] = jnp.zeros_like(pool[LATE])
    for j in range(held):
        grad = packed[z, j].astype(jnp.float32)
        grad = grad + pool[late_at[z * held + j]].astype(jnp.float32)
        w, one, two = adam_update(w_ref[j], one_ref[j], two_ref[j], grad, 0.01, rate_value)
        w_out[j] = w
        one_out[j] = one
        two_out[j] = two
    small_out[...] = sum_b[rows : rows + small_rows, :].astype(jnp.float32)

    @pl.when(stays)
    def done():
        keep.wait()

    @pl.when(jnp.logical_not(stays))
    def gone():
        home_moves[0].wait()

    home_moves[1].wait()
    for _, copy in (*core_moves, *plane_moves):
        copy.wait_send()
    for copy in (
        *over_moves,
        *small_core,
        *small_plane,
        *scatter_a,
        *scatter_b,
        *spread_a,
        *spread_b,
    ):
        copy.wait_send()


def finish(
    holder,
    late_at,
    x_all,
    dq,
    dk,
    dv,
    gh1,
    first,
    early,
    small,
    master,
    one,
    two,
    n_shard,
    n_ctx,
    n_tp,
):
    _, mid, width = x_all.shape
    held, rows, _ = master.shape
    groups = n_ctx * n_tp
    span = 16 * n_shard
    long_a = -(-2 * rows // span) * span
    long_b = -(-(rows + small.shape[0]) // span) * span
    smem = pl.BlockSpec(memory_space=pltpu.SMEM)
    anywhere = pl.BlockSpec(memory_space=pl.ANY)
    vmem = pl.BlockSpec(memory_space=pltpu.VMEM)
    dma = pltpu.SemaphoreType.DMA
    low = jnp.bfloat16
    pairs = [LATE * n_ctx * (n_tp - 1), LATE * (n_ctx - 1), 2, 2, n_tp - 1, n_ctx - 1]
    pairs += [n_shard - 1] * 6
    stored = f32_of(held, rows, width)
    shapes = [
        x_all.shape,
        dq.shape,
        dk.shape,
        dv.shape,
        None,
        first.shape,
        (4, EARLY, rows, width),
        (EARLY + 1, rows, width),
        (n_shard, held, rows, width),
        (n_shard - 1, held, rows, width),
        (n_shard - 1, held, rows, width),
        (width, 4 * mid),
        (groups, LATE, rows, width),
        (n_tp - 1, n_ctx, LATE, rows, width),
        (n_ctx, LATE, rows, width),
        (n_ctx - 1, LATE, rows, width),
        (2, mid, width),
        (2, mid, width),
        (2, mid, width),
        small.shape,
        (n_tp - 1, *small.shape),
        small.shape,
        (n_ctx - 1, *small.shape),
        *[
            shape
            for long in (long_a, long_b)
            for shape in (
                (long, width),
                (n_shard - 1, long // n_shard, width),
                (long, width),
                (long // n_shard, width),
            )
        ],
        (LATE + 1, rows, width),
    ]
    return pl.pallas_call(
        functools.partial(finish_kernel, n_shard, n_ctx, n_tp),
        name="finish",
        in_specs=[smem] * 2 + [anywhere] * 11 + [vmem] * 4,
        out_specs=[anywhere] + [vmem] * 4,
        out_shape=[bf16_of(2, mid, width), stored, stored, stored, f32_of(*small.shape)],
        scratch_shapes=[
            pltpu.VMEM(s, low) if s else pltpu.VMEM(gh1.shape, jnp.float32) for s in shapes
        ]
        + [dma((11,))]
        + [dma((n,)) for n in pairs for _ in range(2)]
        + [dma((1,))],
        compiler_params=pltpu.CompilerParams(
            collective_id=1, has_side_effects=True, vmem_limit_bytes=63 << 20
        ),
        cost_estimate=pl.CostEstimate(
            flops=12_000_000_000, bytes_accessed=40 << 20, transcendentals=0
        ),
    )(holder, late_at, x_all, dq, dk, dv, gh1, first, *early, small, master, one, two)


def moves(n_ctx, n_tp, pick):
    pairs = []
    for c in range(n_ctx):
        for t in range(n_tp):
            side, core = t // 2, t % 2
            to_ctx = 2 * core + (pick ^ (c & 1))
            to_tp = 2 * side + c // 2
            pairs.append((c * n_tp + t, to_ctx * n_tp + to_tp))
    return pairs


def shards(
    inputs,
    cotangent,
    rand_blocks,
    slot_of,
    master,
    moment_one,
    moment_two,
    small_params,
    small_one,
    small_two,
):
    n_shard = lax.axis_size("shard")
    n_ctx = lax.axis_size("ctx")
    n_tp = lax.axis_size("tp")
    groups = n_ctx * n_tp
    held, rows, width = master.shape
    span = small_params.shape[0]
    my_ctx = lax.axis_index("ctx")
    my_tp = lax.axis_index("tp")
    parity = lax.rem(my_ctx, 2)
    half = lax.rem(my_tp, 2)
    plane = ("ctx", "tp")
    forth = [moves(n_ctx, n_tp, pick) for pick in range(2)]

    arrival = [(b ^ parity) + 2 * (half ^ (j // 2)) for j, b in enumerate((0, 1, 0, 1))]
    info = jnp.stack([half, *arrival]).astype(jnp.int32)
    half_one = info[:1]

    def sent(field, pick):
        low = field.astype(jnp.bfloat16)
        return jnp.where(parity == 0, low[pick], low[1 - pick])

    my_shard = lax.axis_index("shard")
    start = ((my_shard * n_ctx + my_ctx) * n_tp + my_tp) * span
    lone = lax.dynamic_update_slice(
        jnp.zeros((16 * width,), jnp.float32), small_params, (start,)
    ).reshape(16, width)
    local_at = slot_of[:LATE] - my_shard * held
    local_at = jnp.where((local_at >= 0) & (local_at < held), local_at, held)
    x_all, first, rest, small, q, k, v, context, lse = begin(
        slot_of, local_at, rand_blocks, master, lone, inputs, n_shard, n_ctx, n_tp
    )
    cots, context = lax.optimization_barrier(
        ([sent(cotangent, pick) for pick in range(2)], context)
    )
    cots = [lax.ppermute(cots[pick], plane, forth[pick]) for pick in range(2)]
    out_low, n1, r1, fit, hid, gel, n2, r2 = front(info, context, x_all, small, rest)
    *early, gh1, dctx, sums, layer_home = back(
        n2, r2, cots, hid, gel, fit, n1, r1, context, small, rest, out_low, n_ctx, n_tp
    )
    for j in range(1, n_ctx):
        crossing = [
            (a * n_tp + b, (a ^ j) * n_tp + b) for a in range(n_ctx) for b in range(n_tp)
        ]
        early[j + 1] = lax.ppermute(early[j + 1], plane, crossing)
    dq, dk, dv = attend_back(half_one, rand_blocks, q, k, v, lse, dctx, 5)
    stands = jnp.array([8, 0, 2, 4, 6, 1, 3, 5, 7], jnp.int32)
    slots_all = jnp.arange(n_shard * held, dtype=jnp.int32)
    hits = slot_of[None, :] == slots_all[:, None]
    holder = EARLY + jnp.sum(jnp.where(hits[:, LATE:], stands[None, :] - EARLY, 0), axis=1)
    ranks = jnp.arange(LATE, dtype=jnp.int32)[None, :]
    late_at = LATE + jnp.sum(jnp.where(hits[:, :LATE], ranks - LATE, 0), axis=1)
    came, master_new, first_new, second_new, small_sum = finish(
        holder.astype(jnp.int32),
        late_at.astype(jnp.int32),
        x_all,
        dq,
        dk,
        dv,
        gh1,
        first,
        early,
        sums,
        master,
        moment_one,
        moment_two,
        n_shard,
        n_ctx,
        n_tp,
    )
    layer_out = layer_home.astype(jnp.float32)
    input_grad = came.astype(jnp.float32)
    small_owned = lax.dynamic_slice_in_dim(small_sum.reshape(-1), start, span)
    small_new, small_first, small_second = adam_update(
        small_params, small_one, small_two, small_owned, 0.0, small_rate
    )
    return (
        layer_out,
        input_grad,
        master_new,
        first_new,
        second_new,
        small_new,
        small_first,
        small_second,
    )


def solution(mesh):
    tokens = P(("shard", "tp"), "ctx", None)
    stored = P("shard", ("ctx", "tp"), None)
    spread = P(("shard", "ctx", "tp"))
    return jax.shard_map(
        shards,
        mesh=mesh,
        in_specs=(tokens, tokens, P(), P(), stored, stored, stored, spread, spread, spread),
        out_specs=(tokens, tokens, stored, stored, stored, spread, spread, spread),
        check_vma=False,
    )
```

```python
import functools

import jax
import jax.numpy as jnp
from jax import lax
from jax.experimental import pallas as pl
from jax.experimental.pallas import tpu as pltpu
from jax.sharding import PartitionSpec as P

STEP = 5
norm_eps = 1e-12
beta_one = 0.9
beta_two = 0.999
adam_eps = 1e-08
rate_value = 0.04
small_rate = 0.25
score_scale = 0.125
gelu_root = 0.7978845608
gelu_cube = 0.044715

BLOCK = 64
HEAD = 64
PACK = 4
masked_score = -1e30


def wide_dot(a, b, dims):
    return lax.dot_general(a, b, (dims, ((), ())), preferred_element_type=jnp.float32)


def head_masks(rows):
    lane = lax.broadcasted_iota(jnp.int32, (rows, PACK * HEAD), 1) // HEAD
    return [lane == h for h in range(PACK)]


def spread_heads(block, masks):
    zero = jnp.zeros_like(block)
    return jnp.concatenate([jnp.where(m, block, zero) for m in masks], axis=0)


def own_heads(full, masks):
    total = None
    for h, m in enumerate(masks):
        piece = jnp.where(m, full[h * BLOCK : (h + 1) * BLOCK], 0.0)
        total = piece if total is None else total + piece
    return total


def rows_of(ref, index, count=1):
    return ref[pl.ds(index, count)].reshape(count * BLOCK, ref.shape[2])


def flat_rows(ref, index):
    return ref[pl.ds(pl.multiple_of(index * BLOCK, BLOCK), BLOCK), :]


def picked_rows(ref, picks, low_half):
    halves = []
    for pair in range(PACK // 2):
        cols = slice(pair * 2 * HEAD, (pair + 1) * 2 * HEAD)
        first = ref[picks[2 * pair], :, cols]
        second = ref[picks[2 * pair + 1], :, cols]
        halves.append(jnp.where(low_half, first, second))
    return jnp.concatenate(halves, axis=1)


def gathered(ref, block, last, picks, low_half):
    pieces = [rows_of(ref, 0), rows_of(ref, last), rows_of(ref, block - 1, 3)]
    pieces += [picked_rows(ref, p, low_half) for p in picks]
    return jnp.concatenate(pieces, axis=0)


def middle_scores(keys, spread, block, last):
    scores = wide_dot(keys, spread, ((1,), (1,)))
    first_off = jnp.where(block == 1, masked_score, 0.0)
    last_off = jnp.where(block == last - 1, masked_score, 0.0)
    b = BLOCK
    return jnp.concatenate(
        [
            scores[: 2 * b],
            scores[2 * b : 3 * b] + first_off,
            scores[3 * b : 4 * b],
            scores[4 * b : 5 * b] + last_off,
            scores[5 * b :],
        ],
        axis=0,
    )


def attend_back_kernel(
    unroll,
    half_ref,
    table_ref,
    q_ref,
    k_ref,
    v_ref,
    lse_ref,
    do_ref,
    dq_ref,
    dk_ref,
    dv_ref,
    dk_acc,
    dv_acc,
    kept_p,
    kept_g,
):
    half = half_ref[0]
    group = pl.program_id(0)
    q_ref, k_ref, v_ref = q_ref.at[0], k_ref.at[0], v_ref.at[0]
    nblocks, local = k_ref.shape[0], q_ref.shape[0]
    last = nblocks - 1
    picks_each = table_ref.shape[2]
    masks = head_masks(BLOCK)
    low_half = lax.broadcasted_iota(jnp.int32, (BLOCK, 2 * HEAD), 1) < HEAD
    span = 8 * BLOCK
    chunks = nblocks // 8

    edge = (local - 1) * half
    spread = spread_heads(rows_of(q_ref, edge), masks)
    spread_do = spread_heads(flat_rows(do_ref, edge), masks)
    lse = lse_ref[0, pl.ds(edge, 1), :]
    delta = None
    for c in range(chunks):
        rows = slice(c * span, (c + 1) * span)
        probs = jnp.exp(wide_dot(rows_of(k_ref, c * 8, 8), spread, ((1,), (1,))) - lse)
        gp = wide_dot(rows_of(v_ref, c * 8, 8), spread_do, ((1,), (1,)))
        kept_p[rows, :] = probs
        kept_g[rows, :] = gp
        part = jnp.sum(probs * gp, axis=0, keepdims=True)
        delta = part if delta is None else delta + part
    full = None
    for c in range(chunks):
        rows = slice(c * span, (c + 1) * span)
        probs = kept_p[rows, :]
        ds = (probs * (kept_g[rows, :] - delta)).astype(jnp.bfloat16)
        dv_acc[rows, :] = wide_dot(probs.astype(jnp.bfloat16), spread_do, ((1,), (0,)))
        dk_acc[rows, :] = wide_dot(ds, spread, ((1,), (0,)))
        part = wide_dot(ds, rows_of(k_ref, c * 8, 8), ((0,), (0,)))
        full = part if full is None else full + part
    dq_ref[pl.ds(pl.multiple_of(edge * BLOCK, BLOCK), BLOCK), :] = (
        own_heads(full, masks) * 0.125
    ).astype(jnp.bfloat16)

    def scatter(acc, piece, block, picks):
        b = BLOCK
        acc[0:b, :] += piece[:b]
        acc[last * b : (last + 1) * b, :] += piece[b : 2 * b]
        window = pl.ds(pl.multiple_of((block - 1) * b, b), 3 * b)
        acc[window, :] += piece[2 * b : 5 * b]
        for r, p in enumerate(picks):
            part = piece[(5 + r) * b : (6 + r) * b]
            for pair in range(PACK // 2):
                lanes = slice(pair * 2 * HEAD, (pair + 1) * 2 * HEAD)
                cols = pl.ds(pair * 2 * HEAD, 2 * HEAD)
                sub = part[:, lanes]
                acc[pl.ds(pl.multiple_of(p[2 * pair] * b, b), b), cols] += jnp.where(
                    low_half, sub, 0.0
                )
                acc[pl.ds(pl.multiple_of(p[2 * pair + 1] * b, b), b), cols] += jnp.where(
                    low_half, 0.0, sub
                )

    def middle(step, carry):
        mine = step + 1 - half
        block = mine + local * half
        picks = [
            [table_ref[group * PACK + h, block - 1, r] for h in range(PACK)]
            for r in range(picks_each)
        ]
        spread = spread_heads(rows_of(q_ref, mine), masks)
        spread_do = spread_heads(flat_rows(do_ref, mine), masks)
        keys = gathered(k_ref, block, last, picks, low_half)
        values = gathered(v_ref, block, last, picks, low_half)
        scores = middle_scores(keys, spread, block, last)
        probs = jnp.exp(scores - lse_ref[0, pl.ds(mine, 1), :])
        gp = wide_dot(values, spread_do, ((1,), (1,)))
        delta = jnp.sum(probs * gp, axis=0, keepdims=True)
        ds = (probs * (gp - delta)).astype(jnp.bfloat16)
        low = probs.astype(jnp.bfloat16)
        scatter(dv_acc, wide_dot(low, spread_do, ((1,), (0,))), block, picks)
        scatter(dk_acc, wide_dot(ds, spread, ((1,), (0,))), block, picks)
        full = wide_dot(ds, keys, ((0,), (0,)))
        dq_ref[pl.ds(pl.multiple_of(mine * BLOCK, BLOCK), BLOCK), :] = (
            own_heads(full, masks) * 0.125
        ).astype(jnp.bfloat16)
        return carry

    lax.fori_loop(0, local - 1, middle, 0, unroll=unroll)
    dk_ref[...] = dk_acc[...].astype(jnp.bfloat16)
    dv_ref[...] = dv_acc[...].astype(jnp.bfloat16)


def attend_back(half, table, q, k, v, lse, do, unroll=3):
    tokens, width = do.shape
    groups, nblocks, _, lanes = k.shape
    seq = nblocks * BLOCK
    blocks = tokens // BLOCK
    mine = pl.BlockSpec((tokens, lanes), lambda g, *_: (0, g))
    whole = pl.BlockSpec((seq, lanes), lambda g, *_: (0, g))
    spec = pltpu.PrefetchScalarGridSpec(
        num_scalar_prefetch=2,
        grid=(groups,),
        in_specs=[
            pl.BlockSpec((1, blocks, BLOCK, lanes), lambda g, *_: (g, 0, 0, 0)),
            pl.BlockSpec((1, nblocks, BLOCK, lanes), lambda g, *_: (g, 0, 0, 0)),
            pl.BlockSpec((1, nblocks, BLOCK, lanes), lambda g, *_: (g, 0, 0, 0)),
            pl.BlockSpec((1, blocks, lanes), lambda g, *_: (g, 0, 0)),
            mine,
        ],
        out_specs=[mine, whole, whole],
        scratch_shapes=[pltpu.VMEM((seq, lanes), jnp.float32)] * 4,
    )
    return pl.pallas_call(
        functools.partial(attend_back_kernel, unroll),
        grid_spec=spec,
        out_shape=[
            jax.ShapeDtypeStruct((tokens, width), jnp.bfloat16),
            jax.ShapeDtypeStruct((seq, width), jnp.bfloat16),
            jax.ShapeDtypeStruct((seq, width), jnp.bfloat16),
        ],
        name="attend_back",
        compiler_params=pltpu.CompilerParams(vmem_limit_bytes=56 << 20),
        cost_estimate=pl.CostEstimate(
            flops=120_000_000_000, bytes_accessed=24 << 20, transcendentals=16_000_000
        ),
    )(half, table, q, k, v, lse, do)


TILE = 256
MID = 512


def cols_mean(value):
    return jnp.mean(value, axis=-1, keepdims=True)


def normed(field):
    centred = field - cols_mean(field)
    rate = lax.rsqrt(cols_mean(centred * centred) + norm_eps)
    return centred * rate, rate


def norm_back(cot, normal, rate, gain):
    dn = cot * gain
    return rate * (dn - cols_mean(dn) - normal * cols_mean(dn * normal))


def matrix(ref):
    value = ref[...]
    return value.reshape(-1, value.shape[-1])


def add_row(ref, row, value):
    ref[row : row + 1, :] += jnp.sum(value, axis=0, keepdims=True)


def bf16_of(*shape):
    return jax.ShapeDtypeStruct(shape, jnp.bfloat16)


def f32_of(*shape):
    return jax.ShapeDtypeStruct(shape, jnp.float32)


NN = ((1,), (0,))
NT = ((1,), (1,))
TN = ((0,), (0,))


MESH = pl.DeviceIdType.MESH
KINDS = 3
CHUNKS = 3
HOOKS = (2, 3, 7)
PER = 3


def place_of():
    c, t = lax.axis_index("ctx"), lax.axis_index("tp")
    return lax.axis_index("shard"), c, t


def send(src, dst, sems, index, target):
    send_sems, recv_sems = sems
    return pltpu.make_async_remote_copy(
        src_ref=src,
        dst_ref=dst,
        send_sem=send_sems.at[index],
        recv_sem=recv_sems.at[index],
        device_id=target,
        device_id_type=MESH,
    )


def begin_kernel(
    n_shard,
    n_ctx,
    n_tp,
    slots,
    local_at,
    table,
    master_hbm,
    small_in,
    input_hbm,
    cot_hbm,
    x_ref,
    first_ref,
    rest_out,
    small_ref,
    q_ref,
    k_ref,
    v_ref,
    ctx_ref,
    lse_ref,
    cot_ref,
    layer_ref,
    n1_ref,
    r1_ref,
    n2_ref,
    r2_ref,
    fit_ref,
    hid_ref,
    gel_ref,
    raw,
    low,
    given,
    xs,
    x_all,
    part,
    got,
    mine,
    total,
    pool,
    sel,
    first,
    rest_ref,
    small,
    q_s,
    k_s,
    v_s,
    ctx_s,
    kept,
    n1_s,
    gel_s,
    hid_s,
    fit_s,
    layer_s,
    x_s,
    x_r,
    xt_s,
    xt_r,
    za_s,
    za_r,
    zb_s,
    zb_r,
    zc_s,
    zc_r,
    zd_s,
    zd_r,
    qm_s,
    qm_r,
    qt_s,
    qt_r,
    r_s,
    r_r,
    rt_s,
    rt_r,
    y_s,
    y_r,
    own_sem,
    out_sem,
    tile_sem,
    end_sem,
):
    z, c, t = place_of()
    side, core, bit = t // 2, lax.rem(t, 2), lax.rem(c, 2)
    held, rows, width = low.shape[0] - 1, low.shape[1], low.shape[2]
    piece = mine.shape[0]
    me = c * n_tp + t
    _, mid, _ = xs.shape
    nblocks = 4 * mid // BLOCK
    local = nblocks // 2
    lanes = PACK * HEAD
    groups = width // lanes
    others = n_tp - 1

    take_raw = pltpu.make_async_copy(master_hbm, raw, own_sem.at[0])
    take_given = pltpu.make_async_copy(input_hbm, given, own_sem.at[1])
    take_raw.start()
    take_given.start()

    def far(dz):
        return (lax.rem(z + dz, n_shard), c, t)

    def across(mask):
        return (z, c ^ mask, t)

    def beside(dt):
        return (z, c, lax.rem(t + dt, n_tp))

    barrier = pltpu.get_barrier_semaphore()
    friends = [far(dz) for dz in range(1, n_shard)]
    friends += [(z, c ^ m, t) for m in range(1, n_ctx)]
    friends += [beside(dt) for dt in range(1, n_tp)]
    friends += [(z, c ^ m, t ^ 1) for m in range(1, n_ctx)]
    for friend in friends:
        pl.semaphore_signal(barrier, inc=1, device_id=friend, device_id_type=MESH)

    take_raw.wait()
    for j in range(held):
        low[j] = raw[j].astype(jnp.bfloat16)
    low[held] = jnp.zeros_like(low[held])
    pool[pl.ds(z * held, held)] = low[0:held]
    part[...] = jnp.zeros_like(part)
    for m in range(KINDS):
        part[m * rows : (m + 1) * rows, :] = low[local_at[m]]
    part[KINDS * rows : KINDS * rows + 16, :] = small_in[...].astype(jnp.bfloat16)
    pl.semaphore_wait(barrier, len(friends))

    def piece_at(k):
        return pl.ds(pl.multiple_of(k * piece, piece), piece)

    def hop_copy(s, way):
        sems = (zc_s, zc_r) if way > 0 else (zd_s, zd_r)
        slot = pl.ds((z - way * (s - 1)) * held, held)
        return send(
            pool.at[slot], pool.at[slot], sems, s - 1, (lax.rem(z + way + n_shard, n_shard), c, t)
        )

    def hop_on(s, way):
        start = z - way * (s - 1)
        end = z + way
        return (start >= 0) & (start < n_shard) & (end >= 0) & (end < n_shard)

    def hop(s):
        for way in (1, -1):

            @pl.when(hop_on(s, way))
            def move(way=way):
                if s > 1:
                    hop_copy(s - 1, way).wait_recv()
                hop_copy(s, way).start()

    za = [
        send(part.at[piece_at(far(dz)[0])], got.at[dz - 1], (za_s, za_r), dz - 1, far(dz))
        for dz in range(1, n_shard)
    ]
    for copy in za:
        copy.start()

    stays = c // 2 == core
    goes = [(z, 2 * core + (p ^ bit), 2 * side + c // 2) for p in range(2)]
    x_moves = [send(xs.at[p], x_all.at[p], (x_s, x_r), p, goes[p]) for p in range(2)]
    x_keep = pltpu.make_async_copy(xs.at[0], x_all.at[0], own_sem.at[2])
    take_given.wait()
    xs[0] = given[bit].astype(jnp.bfloat16)

    @pl.when(stays)
    def keep():
        x_keep.start()

    @pl.when(jnp.logical_not(stays))
    def leave():
        x_moves[0].start()

    xs[1] = given[1 - bit].astype(jnp.bfloat16)
    x_moves[1].start()

    summed = part[piece_at(z), :]
    for dz, copy in enumerate(za):
        copy.wait_recv()
        summed = summed + got[dz]
    mine[...] = summed
    zb = [
        send(mine, total.at[piece_at(z)], (zb_s, zb_r), dz - 1, far(dz))
        for dz in range(1, n_shard)
    ]
    for copy in zb:
        copy.start()
    hop(1)
    total[piece_at(z), :] = summed
    def hops_end():
        for way, end in ((1, n_shard - 1), (-1, 0)):

            @pl.when(z == end)
            def gather(way=way):
                for s in range(1, n_shard):
                    hop_copy(s, way).wait_recv()

    def hops_sent():
        for s in range(1, n_shard):
            for way in (1, -1):

                @pl.when(hop_on(s, way))
                def sent(s=s, way=way):
                    hop_copy(s, way).wait_send()

    for copy in zb:
        copy.wait_recv()
    hop(2)

    q_moves = [
        send(total, first.at[me], (qm_s, qm_r), k, across(m)) for k, m in enumerate((1, 2, 3))
    ]
    for copy in q_moves:
        copy.start()
    qt_moves = [
        send(total, first.at[me], (qt_s, qt_r), dt - 1, beside(dt)) for dt in range(1, n_tp)
    ]
    for copy in qt_moves:
        copy.start()
    first[me] = total[...]

    x_over = [
        send(x_all.at[p], x_all.at[2 + p], (xt_s, xt_r), p, (z, c, t ^ 1)) for p in range(2)
    ]

    @pl.when(stays)
    def stayed():
        x_keep.wait()

    @pl.when(jnp.logical_not(stays))
    def came():
        x_moves[0].wait_recv()

    x_over[0].start()
    x_moves[1].wait_recv()
    x_over[1].start()
    for s in range(3, n_shard):
        hop(s)

    for k, m in enumerate((1, 2, 3)):
        q_moves[k].wait_recv()
        place = (c ^ m) * n_tp + t
        for dt in range(1, n_tp):
            copy = send(
                first.at[place],
                first.at[place],
                (qt_s, qt_r),
                (k + 1) * others + dt - 1,
                beside(dt),
            )
            copy.start()
            qt_moves.append(copy)
    for copy in qt_moves:
        copy.wait_recv()
    def span_of(k):
        return pl.ds(k * PER, PER)

    rest_own = pltpu.make_async_copy(sel, rest_ref.at[me], own_sem.at[3])
    direct = [
        [
            send(
                sel.at[span_of(k)], rest_ref.at[me, span_of(k)], (r_s, r_r), k * 3 + j, across(m)
            )
            for j, m in enumerate((1, 2))
        ]
        for k in range(CHUNKS)
    ]
    onward = []
    for k in range(CHUNKS):
        odd = lax.rem(core + k, 2)
        source = jnp.where(odd == 0, c ^ 1, c ^ 2) * n_tp + t
        target = (z, jnp.where(odd == 0, c ^ 2, c ^ 1), t)
        view = rest_ref.at[source, span_of(k)]
        onward.append(send(view, view, (r_s, r_r), k * 3 + 2, target))

    def passing(k, which):
        if which == 0:
            src = sel.at[span_of(k)]
        else:
            src = rest_ref.at[(c ^ which) * n_tp + t, span_of(k)]
        dst = rest_ref.at[(c ^ which) * n_tp + t, span_of(k)]
        return [
            send(src, dst, (rt_s, rt_r), (k * 4 + which) * others + dt - 1, beside(dt))
            for dt in range(1, n_tp)
        ]

    passed = [[passing(k, which) for which in range(4)] for k in range(CHUNKS)]

    def begin_rest():
        hops_end()
        for m in range(CHUNKS * PER):
            sel[m] = pool[slots[KINDS + m]]
        rest_own.start()
        launch(0)
        launch(1)

    def launch(k):
        for copy in (*direct[k], *passed[k][0]):
            copy.start()

    def relay(k):
        for copy in direct[k]:
            copy.wait_recv()
        onward[k].start()
        for copy in passed[k][1] + passed[k][2]:
            copy.start()

    def last_relay(k):
        onward[k].wait_recv()
        for copy in passed[k][3]:
            copy.start()

    begin_rest()
    outs = [pltpu.make_async_copy(first, first_ref, out_sem.at[0])]
    outs[0].start()

    sums = None
    for g in range(n_ctx * n_tp):
        here = first[g, KINDS * rows : KINDS * rows + 16, :].astype(jnp.float32)
        sums = here if sums is None else sums + here
    small[...] = sums
    small_ref[...] = sums
    def weight(m):
        return first[:, m * rows : (m + 1) * rows, :].reshape(width, width)

    def split(dst, start, value):
        low_value = value.astype(jnp.bfloat16)
        per = TILE // BLOCK
        for g in range(groups):
            piece_value = low_value[:, g * lanes : (g + 1) * lanes]
            dst[g, pl.ds(start, per)] = piece_value.reshape(per, BLOCK, lanes)

    def project(a, chunk, own):
        def one(i, carry):
            x = x_all[a, pl.ds(pl.multiple_of(i * TILE, TILE), TILE), :]
            start = chunk * (mid // BLOCK) + i * (TILE // BLOCK)
            if own:
                q_start = (chunk - 2 * core) * (mid // BLOCK) + i * (TILE // BLOCK)
                q = wide_dot(x, weight(0), NN) + small[0:1, :]
                split(q_s, q_start, q.astype(jnp.bfloat16) * jnp.bfloat16(score_scale))
            split(k_s, start, wide_dot(x, weight(1), NN))
            split(v_s, start, wide_dot(x, weight(2), NN) + small[1:2, :])
            return carry

        lax.fori_loop(0, mid // TILE, one, 0)

    def own_project(a, carry):
        project(a, 2 * core + (a ^ bit), True)
        return carry

    def other_project(a, carry):
        project(2 + a, 2 * (1 - core) + (a ^ bit), False)
        return carry

    @pl.when(jnp.logical_not(stays))
    def left():
        x_moves[0].wait_send()

    x_moves[1].wait_send()
    take_cot = pltpu.make_async_copy(cot_hbm, given, own_sem.at[2])
    take_cot.start()
    lax.fori_loop(0, 2, own_project, 0)
    for copy in x_over:
        copy.wait_recv()
    outs.append(pltpu.make_async_copy(x_all, x_ref, out_sem.at[1]))
    outs[1].start()
    lax.fori_loop(0, 2, other_project, 0)
    take_cot.wait()
    xs[0] = given[bit].astype(jnp.bfloat16)
    xs[1] = given[1 - bit].astype(jnp.bfloat16)
    for i, (src, dst) in enumerate(((q_s, q_ref), (k_s, k_ref), (v_s, v_ref))):
        outs.append(pltpu.make_async_copy(src, dst, out_sem.at[2 + i]))
        outs[-1].start()

    last = nblocks - 1
    picks_each = table.shape[2]
    masks = head_masks(BLOCK)
    low_half = lax.broadcasted_iota(jnp.int32, (BLOCK, 2 * HEAD), 1) < HEAD
    each = 5
    subs = (local - 1) // each

    def attend_round(i, carry):
        g = i // subs
        sub = lax.rem(i, subs)
        qg, kg, vg = q_s.at[g], k_s.at[g], v_s.at[g]
        for k in range(CHUNKS):

            @pl.when(i == HOOKS[k])
            def hook(k=k):
                relay(k)
                if k == 0:
                    launch(2)

        @pl.when(i == groups * subs - 1)
        def late_hook():
            last_relay(0)
            last_relay(1)

        @pl.when(sub == 0)
        def edge_block():
            edge = (local - 1) * core
            spread = spread_heads(rows_of(qg, edge), masks)
            span = 8 * BLOCK
            pieces = nblocks // 8
            top = None
            for n in range(pieces):
                scores = wide_dot(rows_of(kg, n * 8, 8), spread, NT)
                kept[n * span : (n + 1) * span, :] = scores
                high = jnp.max(scores, axis=0, keepdims=True)
                top = high if top is None else jnp.maximum(top, high)
            total_p = None
            for n in range(pieces):
                probs = jnp.exp(kept[n * span : (n + 1) * span, :] - top)
                kept[n * span : (n + 1) * span, :] = probs
                some = jnp.sum(probs, axis=0, keepdims=True)
                total_p = some if total_p is None else total_p + some
            scale = 1.0 / total_p
            full = None
            for n in range(pieces):
                probs = (kept[n * span : (n + 1) * span, :] * scale).astype(jnp.bfloat16)
                some = wide_dot(probs, rows_of(vg, n * 8, 8), TN)
                full = some if full is None else full + some
            at = pl.ds(pl.multiple_of(edge * BLOCK, BLOCK), BLOCK)
            ctx_s[g, at, :] = own_heads(full, masks).astype(jnp.bfloat16)
            lse_ref[g, pl.ds(edge, 1), :] = top + jnp.log(total_p)

        for u in range(each):
            spot = sub * each + u + 1 - core
            block = spot + local * core
            picks = [
                [table[g * PACK + h, block - 1, r] for h in range(PACK)]
                for r in range(picks_each)
            ]
            spread = spread_heads(rows_of(qg, spot), masks)
            keys = gathered(kg, block, last, picks, low_half)
            values = gathered(vg, block, last, picks, low_half)
            scores = middle_scores(keys, spread, block, last)
            top = jnp.max(scores, axis=0, keepdims=True)
            probs = jnp.exp(scores - top)
            total_p = jnp.sum(probs, axis=0, keepdims=True)
            probs = (probs * (1.0 / total_p)).astype(jnp.bfloat16)
            full = wide_dot(probs, values, TN)
            at = pl.ds(pl.multiple_of(spot * BLOCK, BLOCK), BLOCK)
            ctx_s[g, at, :] = own_heads(full, masks).astype(jnp.bfloat16)
            lse_ref[g, pl.ds(spot, 1), :] = top + jnp.log(total_p)
        return carry

    lax.fori_loop(0, groups * subs, attend_round, 0)
    for g in range(groups):
        outs.append(
            pltpu.make_async_copy(
                ctx_s.at[g], ctx_ref.at[:, g * lanes : (g + 1) * lanes], out_sem.at[5 + g]
            )
        )
        outs[-1].start()
    last_relay(2)

    cot_moves = [send(xs.at[p], cot_ref.at[p], (y_s, y_r), p, goes[p]) for p in range(2)]
    cot_keep = pltpu.make_async_copy(xs.at[0], cot_ref.at[0], own_sem.at[1])

    @pl.when(stays)
    def keep_cot():
        cot_keep.start()

    @pl.when(jnp.logical_not(stays))
    def leave_cot():
        cot_moves[0].start()

    cot_moves[1].start()

    for k in range(2):
        for group in passed[k]:
            for copy in group:
                copy.wait_recv()
    rest_own.wait()
    tiles = 2 * mid // TILE
    per = mid // TILE

    def held_out(m):
        return rest_ref[:, m].reshape(width, width)

    def tile_out(i, slot):
        at = pl.ds(pl.multiple_of(i * TILE, TILE), TILE)
        return (
            pltpu.make_async_copy(n1_s.at[slot], n1_ref.at[at], tile_sem.at[slot]),
            pltpu.make_async_copy(gel_s.at[slot], gel_ref.at[:, at], tile_sem.at[2 + slot]),
        )

    def rise_tile(i, carry):
        slot = lax.rem(i, 2)
        at = pl.ds(pl.multiple_of(i * TILE, TILE), TILE)
        inside = pl.ds(pl.multiple_of(lax.rem(i, per) * TILE, TILE), TILE)

        @pl.when(i >= 2)
        def free():
            for copy in tile_out(i - 2, slot):
                copy.wait()

        context = jnp.concatenate([ctx_s[g, at, :] for g in range(groups)], axis=1)
        attn_out = wide_dot(context, held_out(0), NN) + small[2:3, :]
        x = x_all[(i // per) ^ bit, inside, :].astype(jnp.float32)
        n1, r1 = normed(x + attn_out)
        n1_s[slot] = n1
        r1_ref[at, :] = jnp.broadcast_to(r1, (TILE, r1_ref.shape[1]))
        after = n1 * small[3:4, :] + small[4:5, :]
        ffn_in = after.astype(jnp.bfloat16)
        fit_s[:, at] = ffn_in.T
        given[i // per, inside, :] = after + small[9:10, :]
        for b in range(4):
            up = wide_dot(ffn_in, held_out(1 + b), NN) + small[5 + b : 6 + b, :]
            square = up * up
            bent = jnp.tanh(gelu_root * up * (1.0 + gelu_cube * square))
            rise = 0.5 * (1.0 + bent)
            hid_s[b, at, :] = (up * rise).astype(jnp.bfloat16)
            slope = rise + (0.5 * gelu_root) * up * (1.0 - bent * bent) * (
                1.0 + (3.0 * gelu_cube) * square
            )
            gel_s[slot, b] = slope.astype(jnp.bfloat16)
        for copy in tile_out(i, slot):
            copy.start()
        return carry

    lax.fori_loop(0, tiles, rise_tile, 0)
    for i in range(tiles - 2, tiles):
        for copy in tile_out(i, i % 2):
            copy.wait()
    for i, (src, dst) in enumerate(((hid_s, hid_ref), (fit_s, fit_ref))):
        outs.append(pltpu.make_async_copy(src, dst, out_sem.at[5 + groups + i]))
        outs[-1].start()
    for group in passed[2]:
        for copy in group:
            copy.wait_recv()
    outs.append(pltpu.make_async_copy(rest_ref, rest_out, out_sem.at[7 + groups]))
    outs[-1].start()

    def end_out(i):
        at = pl.ds(pl.multiple_of(i * TILE, TILE), TILE)
        inside = pl.ds(pl.multiple_of(lax.rem(i, per) * TILE, TILE), TILE)
        chunk = i // per
        return (
            pltpu.make_async_copy(given.at[chunk, inside], n2_ref.at[at], end_sem.at[i]),
            pltpu.make_async_copy(
                layer_s.at[chunk ^ bit, inside],
                layer_ref.at[chunk ^ bit, inside],
                end_sem.at[tiles + i],
            ),
        )

    def fall_tile(i, carry):
        at = pl.ds(pl.multiple_of(i * TILE, TILE), TILE)
        inside = pl.ds(pl.multiple_of(lax.rem(i, per) * TILE, TILE), TILE)
        summed = given[i // per, inside, :]
        for b in range(4):
            summed = summed + wide_dot(hid_s[b, at, :], held_out(5 + b), NT)
        n2, r2 = normed(summed)
        layer_s[(i // per) ^ bit, inside, :] = (n2 * small[10:11, :] + small[11:12, :]).astype(
            jnp.bfloat16
        )
        given[i // per, inside, :] = n2
        r2_ref[at, :] = jnp.broadcast_to(r2, (TILE, r2_ref.shape[1]))
        for copy in end_out(i):
            copy.start()
        return carry

    lax.fori_loop(0, tiles, fall_tile, 0)
    for i in range(tiles):
        for copy in end_out(i):
            copy.wait()

    @pl.when(stays)
    def kept_cot():
        cot_keep.wait()

    @pl.when(jnp.logical_not(stays))
    def left_cot():
        cot_moves[0].wait()

    cot_moves[1].wait()
    for copy in (*x_over, *za, *zb, *q_moves, *qt_moves, *onward):
        copy.wait_send()
    for pair in direct:
        for copy in pair:
            copy.wait_send()
    for chunk in passed:
        for group in chunk:
            for copy in group:
                copy.wait_send()
    hops_sent()
    for copy in outs:
        copy.wait()


def begin(slots, local_at, table, master, small_in, inputs, cot, n_shard, n_ctx, n_tp):
    held, rows, width = master.shape
    _, mid, _ = inputs.shape
    groups = n_ctx * n_tp
    long = -(-(KINDS * rows + 16) // (16 * n_shard)) * 16 * n_shard
    lanes = PACK * HEAD
    packs = width // lanes
    tokens, seq = 2 * mid, 4 * mid
    anywhere = pl.BlockSpec(memory_space=pl.ANY)
    vmem = pl.BlockSpec(memory_space=pltpu.VMEM)
    smem = pl.BlockSpec(memory_space=pltpu.SMEM)
    dma = pltpu.SemaphoreType.DMA
    low = jnp.bfloat16
    f32 = jnp.float32
    pairs = [2, 2, n_shard - 1, n_shard - 1, n_shard - 1, n_shard - 1, 3]
    pairs += [4 * (n_tp - 1), 3 * CHUNKS, 4 * CHUNKS * (n_tp - 1), 2]
    return pl.pallas_call(
        functools.partial(begin_kernel, n_shard, n_ctx, n_tp),
        name="begin",
        in_specs=[smem, smem, smem, anywhere, vmem, anywhere, anywhere],
        out_specs=[anywhere] * 3
        + [vmem]
        + [anywhere] * 4
        + [vmem]
        + [anywhere] * 3
        + [vmem, anywhere, vmem]
        + [anywhere] * 3,
        out_shape=[
            bf16_of(4, mid, width),
            bf16_of(groups, long, width),
            bf16_of(groups, 9, rows, width),
            f32_of(16, width),
            bf16_of(packs, tokens // BLOCK, BLOCK, lanes),
            bf16_of(packs, seq // BLOCK, BLOCK, lanes),
            bf16_of(packs, seq // BLOCK, BLOCK, lanes),
            bf16_of(tokens, width),
            f32_of(packs, tokens // BLOCK, lanes),
            bf16_of(2, mid, width),
            bf16_of(2, mid, width),
            f32_of(tokens, width),
            f32_of(tokens, 128),
            f32_of(tokens, width),
            f32_of(tokens, 128),
            bf16_of(width, tokens),
            bf16_of(4, tokens, width),
            bf16_of(4, tokens, width),
        ],
        scratch_shapes=[
            pltpu.VMEM((held, rows, width), f32),
            pltpu.VMEM((held + 1, rows, width), low),
            pltpu.VMEM((2, mid, width), f32),
            pltpu.VMEM((2, mid, width), low),
            pltpu.VMEM((4, mid, width), low),
            pltpu.VMEM((long, width), low),
            pltpu.VMEM((n_shard - 1, long // n_shard, width), low),
            pltpu.VMEM((long // n_shard, width), low),
            pltpu.VMEM((long, width), low),
            pltpu.VMEM((n_shard * held, rows, width), low),
            pltpu.VMEM((9, rows, width), low),
            pltpu.VMEM((groups, long, width), low),
            pltpu.VMEM((groups, 9, rows, width), low),
            pltpu.VMEM((16, width), f32),
            pltpu.VMEM((packs, tokens // BLOCK, BLOCK, lanes), low),
            pltpu.VMEM((packs, seq // BLOCK, BLOCK, lanes), low),
            pltpu.VMEM((packs, seq // BLOCK, BLOCK, lanes), low),
            pltpu.VMEM((packs, tokens, lanes), low),
            pltpu.VMEM((seq, lanes), f32),
            pltpu.VMEM((2, TILE, width), f32),
            pltpu.VMEM((2, 4, TILE, width), low),
            pltpu.VMEM((4, tokens, width), low),
            pltpu.VMEM((width, tokens), low),
            pltpu.VMEM((2, mid, width), low),
            *[dma((n,)) for n in pairs for _ in range(2)],
            dma((4,)),
            dma((8 + packs,)),
            dma((4,)),
            dma((2 * (tokens // TILE),)),
        ],
        compiler_params=pltpu.CompilerParams(
            collective_id=0, has_side_effects=True, vmem_limit_bytes=64000 << 10
        ),
        cost_estimate=pl.CostEstimate(
            flops=60_000_000_000, bytes_accessed=60 << 20, transcendentals=16_000_000
        ),
    )(slots, local_at, table, master, small_in, inputs, cot)


NEAR = 2


def back_kernel(
    n_ctx,
    n_tp,
    n2_hbm,
    r2_ref,
    cots_ref,
    hid_ref,
    gel_ref,
    fit_ref,
    n1_ref,
    r1_ref,
    ctx_ref,
    small,
    up_w,
    down_w,
    wo,
    layer_ref,
    own_ref,
    near_ref,
    x_ref,
    y_ref,
    xy_ref,
    gh1_ref,
    dctx_ref,
    sums_ref,
    home_ref,
    gy,
    gu,
    mixed,
    mixed_t,
    grads,
    arrived,
    sums,
    send_sem,
    recv_sem,
    h_s,
    h_r,
    n_s,
    n_r,
    keep_sem,
    out_sem,
):
    z, c, t = place_of()
    step = pl.program_id(0)
    tokens, width = gy.shape
    tiles = tokens // TILE
    rows = grads.shape[4]
    others = n_tp - 1
    side, core, bit = t // 2, lax.rem(t, 2), lax.rem(c, 2)

    def beside(dt):
        return (z, c, lax.rem(t + dt, n_tp))

    stays = c // 2 == core
    keep_layer = pltpu.make_async_copy(layer_ref.at[0], home_ref.at[bit], keep_sem.at[0])
    layer_moves = [
        send(
            layer_ref.at[p],
            home_ref.at[bit],
            (h_s, h_r),
            p,
            (z, 2 * core + (p ^ bit), 2 * side + c // 2),
        )
        for p in range(2)
    ]

    @pl.when(step == 0)
    def start():
        take = pltpu.make_async_copy(n2_hbm, gy, keep_sem.at[1])
        take.start()
        barrier = pltpu.get_barrier_semaphore()
        friends = [beside(dt) for dt in range(1, n_tp)]
        friends += [(z, c ^ m, t) for m in range(1, n_ctx)]
        friends += [(z, c ^ m, t ^ 1) for m in range(1, n_ctx)]
        for friend in friends:
            pl.semaphore_signal(barrier, inc=1, device_id=friend, device_id_type=MESH)
        pl.semaphore_wait(barrier, len(friends))

        @pl.when(stays)
        def kept():
            keep_layer.start()

        @pl.when(jnp.logical_not(stays))
        def left():
            layer_moves[0].start()

        layer_moves[1].start()
        sums_ref[...] = jnp.zeros_like(sums_ref)
        take.wait()
        mid = tokens // 2
        for p in range(2):

            def one(i, carry, p=p):
                inside = pl.ds(pl.multiple_of(i * TILE, TILE), TILE)
                at = pl.ds(pl.multiple_of((p ^ bit) * mid + i * TILE, TILE), TILE)
                cot = cots_ref[p, inside, :].astype(jnp.float32)
                n2 = gy[at, :]
                add_row(sums_ref, 10, cot * n2)
                add_row(sums_ref, 11, cot)
                gh2 = norm_back(cot, n2, r2_ref[at, 0:1], small[10:11, :])
                gy[at, :] = gh2
                low = gh2.astype(jnp.bfloat16)
                mixed[at, :] = low
                mixed_t[:, at] = low.T
                add_row(sums_ref, 9, low.astype(jnp.float32))
                return carry

            lax.fori_loop(0, mid // TILE, one, 0)

    def moves(b, count):
        slot = lax.rem(b, 2)
        return [
            send(
                grads.at[slot, :, lax.rem(t + dt, n_tp), 0:count],
                arrived.at[b, dt - 1, :, 0:count],
                (send_sem, recv_sem),
                b * others + dt - 1,
                beside(dt),
            )
            for dt in range(1, n_tp)
        ]

    def exchange(b, count):
        for copy in moves(b, count):
            copy.start()

    def keep(b, count):
        for copy in moves(b, count):
            copy.wait()
        slot = lax.rem(b, 2)
        for j in range(n_ctx):
            for i in range(count):
                value = grads[slot, c ^ j, t, i]
                for dt in range(others):
                    value = value + arrived[b, dt, c ^ j, i]
                sums[j, 2 * b + i] = value

    def near(b):
        pair = slice(2 * b, 2 * b + 2)
        return [
            send(
                sums.at[j, pair],
                near_ref.at[j - 1, pair],
                (n_s, n_r),
                b * (n_ctx - 1) + j - 1,
                (z, c ^ j, t),
            )
            for j in range(1, n_ctx)
        ]

    def outward(part, first, count):
        moved = [
            pltpu.make_async_copy(
                sums.at[0, first : first + count],
                own_ref.at[first : first + count],
                out_sem.at[part * n_ctx],
            )
        ]
        begin_at = max(first, NEAR)
        count -= begin_at - first
        for j, out in enumerate((x_ref, y_ref, xy_ref)):
            moved.append(
                pltpu.make_async_copy(
                    sums.at[j + 1, begin_at : begin_at + count],
                    out.at[begin_at - NEAR : begin_at - NEAR + count],
                    out_sem.at[part * n_ctx + j + 1],
                )
            )
        return moved

    def put(slot, i, value):
        low = value.astype(jnp.bfloat16)
        grads[slot, :, :, i] = low.reshape(n_ctx, n_tp, rows, width)

    @pl.when(step < 4)
    def ffn():
        up_block = matrix(up_w)
        down_block = matrix(down_w)
        slot = lax.rem(step, 2)

        def one(i, carry):
            at = pl.ds(pl.multiple_of(i * MID, MID), MID)
            grad = wide_dot(mixed[at, :], down_block, NN) * gel_ref[0, at, :].astype(jnp.float32)
            low = grad.astype(jnp.bfloat16)
            gu[at, :] = low
            gy[at, :] += wide_dot(low, up_block, NT)
            sums_ref[pl.ds(5 + step, 1), :] += jnp.sum(
                low.astype(jnp.float32), axis=0, keepdims=True
            )
            return carry

        lax.fori_loop(0, tokens // MID, one, 0)
        put(slot, 0, wide_dot(fit_ref[...], gu[...], NN))
        put(slot, 1, wide_dot(mixed_t[...], hid_ref[0], NN))
        exchange(step, 2)

    @pl.when(step > 0)
    def settle():
        keep(step - 1, 2)

    for b in range(NEAR // 2):

        @pl.when(step == b + 1)
        def cross(b=b):
            for copy in near(b):
                copy.start()

    @pl.when(step == 4)
    def first_norm():
        for copy in outward(0, 0, 8):
            copy.start()

        def one(i, carry):
            at = pl.ds(pl.multiple_of(i * TILE, TILE), TILE)
            grad = gy[at, :]
            n1 = n1_ref[at, :]
            gh1 = norm_back(grad, n1, r1_ref[at, 0:1], small[3:4, :])
            gh1_ref[at, :] = gh1
            low = gh1.astype(jnp.bfloat16)
            gu[at, :] = low
            add_row(sums_ref, 2, low.astype(jnp.float32))
            add_row(sums_ref, 3, grad * n1)
            add_row(sums_ref, 4, grad)
            return carry

        lax.fori_loop(0, tiles, one, 0)
        put(0, 0, wide_dot(ctx_ref[...].T, gu[...], NN))
        exchange(4, 1)
        out_w = matrix(wo)

        def two(i, carry):
            at = pl.ds(pl.multiple_of(i * TILE, TILE), TILE)
            dctx_ref[at, :] = wide_dot(gu[at, :], out_w, NT).astype(jnp.bfloat16)
            return carry

        lax.fori_loop(0, tiles, two, 0)
        keep(4, 1)
        for copy in outward(1, 8, 1):
            copy.start()
        for copy in (*near(0), *outward(0, 0, 8), *outward(1, 8, 1)):
            copy.wait()

        @pl.when(stays)
        def done():
            keep_layer.wait()

        @pl.when(jnp.logical_not(stays))
        def gone():
            layer_moves[0].wait()

        layer_moves[1].wait()


def back(n2, r2, cots, hid, gel, fit, n1, r1, ctx, small, rest, layer, n_ctx, n_tp):
    tokens, width = n2.shape
    rows = rest.shape[2]
    dma = pltpu.SemaphoreType.DMA

    def whole(shape):
        return pl.BlockSpec(shape, lambda b: (0,) * len(shape), pipeline_mode=pl.Buffered(1))

    def block(b):
        return (jnp.minimum(b, 3), 0, 0)

    def held(first, single=False):
        return pl.BlockSpec(
            (n_ctx * n_tp, 1, rows, width),
            (lambda b: (0, first, 0, 0))
            if single
            else (lambda b: (0, first + jnp.minimum(b, 3), 0, 0)),
            pipeline_mode=pl.Buffered(1) if single else None,
        )

    def out(shape):
        return pl.BlockSpec(shape, lambda b: (0,) * len(shape))

    return pl.pallas_call(
        functools.partial(back_kernel, n_ctx, n_tp),
        name="back",
        grid=(5,),
        in_specs=[
            pl.BlockSpec(memory_space=pl.ANY),
            whole((tokens, 128)),
            whole((2, tokens // 2, width)),
            pl.BlockSpec((1, tokens, width), block),
            pl.BlockSpec((1, tokens, width), block),
            whole((width, tokens)),
            whole((tokens, width)),
            whole((tokens, 128)),
            whole((tokens, width)),
            whole(small.shape),
            held(1),
            held(5),
            held(0, True),
            pl.BlockSpec(memory_space=pl.ANY),
        ],
        out_specs=[
            *[pl.BlockSpec(memory_space=pl.ANY)] * 5,
            out((tokens, width)),
            out((tokens, width)),
            out((16, width)),
            pl.BlockSpec(memory_space=pl.ANY),
        ],
        out_shape=[
            bf16_of(9, rows, width),
            bf16_of(n_ctx - 1, NEAR, rows, width),
            *[bf16_of(9 - NEAR, rows, width)] * 3,
            f32_of(tokens, width),
            bf16_of(tokens, width),
            f32_of(16, width),
            bf16_of(*layer.shape),
        ],
        scratch_shapes=[
            pltpu.VMEM((tokens, width), jnp.float32),
            pltpu.VMEM((tokens, width), jnp.bfloat16),
            pltpu.VMEM((tokens, width), jnp.bfloat16),
            pltpu.VMEM((width, tokens), jnp.bfloat16),
            pltpu.VMEM((2, n_ctx, n_tp, 2, rows, width), jnp.bfloat16),
            pltpu.VMEM((5, n_tp - 1, n_ctx, 2, rows, width), jnp.bfloat16),
            pltpu.VMEM((n_ctx, 9 + 1, rows, width), jnp.bfloat16),
            dma((5 * (n_tp - 1),)),
            dma((5 * (n_tp - 1),)),
            dma((2,)),
            dma((2,)),
            dma((n_ctx - 1,)),
            dma((n_ctx - 1,)),
            dma((2,)),
            dma((2 * n_ctx,)),
        ],
        compiler_params=pltpu.CompilerParams(
            collective_id=3, has_side_effects=True, vmem_limit_bytes=62 << 20
        ),
        cost_estimate=pl.CostEstimate(
            flops=22_000_000_000, bytes_accessed=40 << 20, transcendentals=0
        ),
    )(n2, r2, cots, hid, gel, fit, n1, r1, ctx, small, rest, rest, rest, layer)


LATE = 3
EARLY = 9


def adam_update(weight, first, second, grad, decay, rate):
    count = float(STEP)
    first_new = beta_one * first + (1.0 - beta_one) * grad
    second_new = beta_two * second + (1.0 - beta_two) * grad * grad
    first_hat = first_new / (1.0 - beta_one**count)
    second_hat = second_new / (1.0 - beta_two**count)
    weight_new = weight - rate * (first_hat / (jnp.sqrt(second_hat) + adam_eps) + decay * weight)
    return (weight_new, first_new, second_new)


def finish_kernel(
    n_shard,
    n_ctx,
    n_tp,
    holder,
    late_at,
    x_hbm,
    dq_hbm,
    dk_hbm,
    dv_hbm,
    gh1_hbm,
    first_hbm,
    e0_hbm,
    near_hbm,
    e1_hbm,
    e2_hbm,
    e3_hbm,
    small_ref,
    w_ref,
    one_ref,
    two_ref,
    home_ref,
    w_out,
    one_out,
    two_out,
    small_out,
    x_s,
    dq_s,
    dk_s,
    dv_s,
    gh1_s,
    first_s,
    early,
    every,
    packed,
    right_met,
    left_met,
    flipped,
    grads,
    arrived,
    partial,
    met,
    over,
    more,
    back_s,
    small_s,
    small_t,
    small_m,
    small_p,
    flat_a,
    met_a,
    sum_a,
    mine_a,
    flat_b,
    met_b,
    sum_b,
    mine_b,
    pool,
    in_sem,
    c_s,
    c_r,
    p_s,
    p_r,
    o_s,
    o_r,
    h_s,
    h_r,
    sc_s,
    sc_r,
    sp_s,
    sp_r,
    e_s,
    e_r,
    l_s,
    l_r,
    a_s,
    a_r,
    b_s,
    b_r,
    d_s,
    d_r,
    f_s,
    f_r,
    keep_sem,
):
    z, c, t = place_of()
    side, core, bit = t // 2, lax.rem(t, 2), lax.rem(c, 2)
    _, mid, width = x_s.shape
    tokens = 2 * mid
    held, rows, _ = w_ref.shape
    per = n_ctx * n_tp // 2
    band = width // 2
    tile = mid

    loads = [
        pltpu.make_async_copy(src, dst, in_sem.at[i])
        for i, (src, dst) in enumerate(
            (
                (x_hbm, x_s),
                (dk_hbm, dk_s),
                (dv_hbm, dv_s),
                (dq_hbm, dq_s),
                (first_hbm, first_s),
                (gh1_hbm, gh1_s),
                (e0_hbm, early.at[0]),
                (near_hbm, early.at[1:4, 0:NEAR]),
                (e1_hbm, early.at[1, NEAR:EARLY]),
                (e2_hbm, early.at[2, NEAR:EARLY]),
                (e3_hbm, early.at[3, NEAR:EARLY]),
            )
        )
    ]
    for i in (6, 7, 8, 9, 10, 0, 1, 2, 3, 4, 5):
        loads[i].start()

    def far(dz):
        return (lax.rem(z + dz, n_shard), c, t)

    def across(mask):
        return (z, c ^ mask, t)

    def beside(dt):
        return (z, c, lax.rem(t + dt, n_tp))

    barrier = pltpu.get_barrier_semaphore()
    friends = [far(dz) for dz in range(1, n_shard)]
    friends += [(z, c ^ m, t) for m in range(1, n_ctx)]
    friends += [beside(dt) for dt in range(1, n_tp)]
    friends += [(z, c ^ m, t ^ 1) for m in range(1, n_ctx)]
    for friend in friends:
        pl.semaphore_signal(barrier, inc=1, device_id=friend, device_id_type=MESH)

    for i in range(6, 11):
        loads[i].wait()
    every[0:EARLY] = early[0] + early[1] + early[2] + early[3]
    every[EARLY] = jnp.zeros_like(every[EARLY])
    for s in range(n_shard * held):
        packed[s // held, s % held] = every[holder[s]]
    pl.semaphore_wait(barrier, len(friends))

    def run(owner_at, s, way):
        met, sems = (right_met, (e_s, e_r)) if way > 0 else (left_met, (l_s, l_r))
        target = (lax.rem(z + way + n_shard, n_shard), c, t)
        return send(packed.at[owner_at], met.at[s], sems, s, target)

    def each_run(hop):
        for s in range(hop + 1):
            for way in (1, -1):
                place = hop - s if way > 0 else n_shard - 1 - (hop - s)
                owner_at = n_shard - 1 - s if way > 0 else s
                yield s, way, place, owner_at

    def hop(h):
        for s, way, place, owner_at in each_run(h):

            @pl.when(z == place)
            def move(s=s, way=way, place=place, owner_at=owner_at):
                copy = run(owner_at, s, way)
                if h > s:
                    copy.wait_recv()
                    met = right_met if way > 0 else left_met
                    for j in range(held):
                        packed[owner_at, j] = packed[owner_at, j] + met[s, j]
                copy.start()

    def hops_end():
        for h in range(n_shard - 1):
            for s, way, place, owner_at in each_run(h):

                @pl.when(z == place)
                def sent(s=s, way=way, owner_at=owner_at):
                    run(owner_at, s, way).wait_send()

        for s in range(n_shard - 1):
            for way in (1, -1):
                owner_at = n_shard - 1 - s if way > 0 else s

                @pl.when(z == owner_at)
                def last(s=s, way=way, owner_at=owner_at):
                    run(owner_at, s, way).wait_recv()
                    met = right_met if way > 0 else left_met
                    for j in range(held):
                        packed[owner_at, j] = packed[owner_at, j] + met[s, j]

    hop(0)

    core_moves = []

    def exchange(m):
        for dt in range(1, n_tp):
            other = lax.rem(t + dt, n_tp)
            for k in range(n_ctx):
                copy = send(
                    grads.at[k * n_tp + other, m],
                    arrived.at[dt - 1, k, m],
                    (c_s, c_r),
                    ((dt - 1) * n_ctx + k) * LATE + m,
                    beside(dt),
                )
                copy.start()
                core_moves.append((m, copy))

    plane_moves = []

    def meet(m):
        for which, copy in core_moves:
            if which == m:
                copy.wait_recv()
        for k in range(n_ctx):
            value = grads[k * n_tp + t, m]
            for dt in range(1, n_tp):
                value = value + arrived[dt - 1, k, m]
            partial[k, m] = value
        for j in range(1, n_ctx):
            copy = send(
                partial.at[c ^ j, m], met.at[j - 1, m], (p_s, p_r), (j - 1) * LATE + m, across(j)
            )
            copy.start()
            plane_moves.append((m, copy))

    loads[0].wait()
    for a in range(4):
        chunk = 2 * (core if a < 2 else 1 - core) + ((a % 2) ^ bit)
        flipped[:, pl.ds(pl.multiple_of(chunk * mid, mid), mid)] = x_s[a].T

    def weight_grad(m, left_at, right):
        def one(i, carry):
            left = flipped[pl.ds(pl.multiple_of(i * band, band), band), left_at]
            value = wide_dot(left, right[...], NN).astype(jnp.bfloat16)
            grads[pl.ds(i * per, per), m] = value.reshape(per, rows, width)
            return carry

        lax.fori_loop(0, 2, one, 0)

    loads[1].wait()
    weight_grad(1, slice(None), dk_s)
    exchange(1)
    loads[2].wait()
    weight_grad(2, slice(None), dv_s)
    exchange(2)
    meet(1)
    for h in range(1, n_shard - 2):
        hop(h)
    loads[3].wait()
    weight_grad(0, pl.ds(pl.multiple_of(core * tokens, tokens), tokens), dq_s)
    exchange(0)
    meet(2)

    row = lax.broadcasted_iota(jnp.int32, small_ref.shape, 0)
    q_sum = jnp.sum(dq_s[...].astype(jnp.float32), axis=0, keepdims=True)
    v_sum = jnp.sum(dv_s[...].astype(jnp.float32), axis=0, keepdims=True)
    sums = jnp.where(row == 0, q_sum, jnp.where(row == 1, v_sum, small_ref[...]))
    small_s[...] = sums.astype(jnp.bfloat16)
    small_core = [
        send(small_s, small_t.at[dt - 1], (sc_s, sc_r), dt - 1, beside(dt)) for dt in range(1, n_tp)
    ]
    for copy in small_core:
        copy.start()

    loads[4].wait()

    def weight(m):
        return first_s[:, m * rows : (m + 1) * rows, :].reshape(width, width)

    wq, wk, wv = weight(0), weight(1), weight(2)
    over_moves = []
    for b in range(2):
        at = pl.ds(pl.multiple_of((1 - core) * tokens + b * mid, mid), mid)
        value = wide_dot(dk_s[at, :], wk, NT) + wide_dot(dv_s[at, :], wv, NT)
        over[b] = value.astype(jnp.bfloat16)
        copy = send(over.at[b], more.at[b], (o_s, o_r), b, (z, c, t ^ 1))
        copy.start()
        over_moves.append(copy)
        if b == 0:
            meet(0)
            if n_shard > 2:
                hop(n_shard - 2)

    value = small_s[...]
    for dt, copy in enumerate(small_core):
        copy.wait_recv()
        value = value + small_t[dt]
    small_m[...] = value
    small_plane = [
        send(small_m, small_p.at[j - 1], (sp_s, sp_r), j - 1, across(j)) for j in range(1, n_ctx)
    ]
    for copy in small_plane:
        copy.start()

    loads[5].wait()
    stays = c // 2 == core
    home_moves = []
    for copy in over_moves:
        copy.wait_recv()
    keep = pltpu.make_async_copy(back_s.at[0], home_ref.at[bit], keep_sem.at[0])
    for move in range(2):
        chunk = move ^ bit
        for i in range(mid // tile):
            at = pl.ds(pl.multiple_of(core * tokens + chunk * mid + i * tile, tile), tile)
            here = pl.ds(pl.multiple_of(chunk * mid + i * tile, tile), tile)
            value = gh1_s[here, :]
            value = value + more[chunk, i * tile : (i + 1) * tile, :].astype(jnp.float32)
            value = value + wide_dot(dq_s[here, :], wq, NT)
            value = value + wide_dot(dk_s[at, :], wk, NT)
            value = value + wide_dot(dv_s[at, :], wv, NT)
            back_s[move, i * tile : (i + 1) * tile, :] = value.astype(jnp.bfloat16)
        target = (z, 2 * core + chunk, 2 * side + c // 2)
        home_moves.append(send(back_s.at[move], home_ref.at[bit], (h_s, h_r), move, target))
        if move == 0:

            @pl.when(stays)
            def kept():
                keep.start()

            @pl.when(jnp.logical_not(stays))
            def left():
                home_moves[0].start()

        else:
            home_moves[1].start()

    def gathered_rows(m):
        for which, copy in plane_moves:
            if which == m:
                copy.wait_recv()
        value = partial[c, m]
        for j in range(n_ctx - 1):
            value = value + met[j, m]
        return value

    def piece_at(ref, k):
        piece = ref.shape[0] // n_shard
        return pl.ds(pl.multiple_of(k * piece, piece), piece)

    def scatter_lot(flat, lot_met, sems):
        moves = [
            send(flat.at[piece_at(flat, far(dz)[0])], lot_met.at[dz - 1], sems, dz - 1, far(dz))
            for dz in range(1, n_shard)
        ]
        for copy in moves:
            copy.start()
        return moves

    def spread_lot(moves, flat, lot_met, lot_sum, lot_mine, sems):
        total = flat[piece_at(flat, z), :].astype(jnp.float32)
        for dz, copy in enumerate(moves):
            copy.wait_recv()
            total = total + lot_met[dz].astype(jnp.float32)
        lot_mine[...] = total.astype(jnp.bfloat16)
        spreads = [
            send(lot_mine, lot_sum.at[piece_at(flat, z)], sems, dz - 1, far(dz))
            for dz in range(1, n_shard)
        ]
        for copy in spreads:
            copy.start()
        lot_sum[piece_at(flat, z), :] = lot_mine[...]
        return spreads

    small_rows = small_s.shape[0]
    flat_a[...] = jnp.zeros_like(flat_a)
    flat_b[...] = jnp.zeros_like(flat_b)
    flat_a[0:rows, :] = gathered_rows(1)
    flat_a[rows : 2 * rows, :] = gathered_rows(2)
    scatter_a = scatter_lot(flat_a, met_a, (a_s, a_r))
    flat_b[0:rows, :] = gathered_rows(0)
    value = small_m[...]
    for j, copy in enumerate(small_plane):
        copy.wait_recv()
        value = value + small_p[j]
    flat_b[rows : rows + small_rows, :] = value
    scatter_b = scatter_lot(flat_b, met_b, (b_s, b_r))
    spread_a = spread_lot(scatter_a, flat_a, met_a, sum_a, mine_a, (d_s, d_r))
    spread_b = spread_lot(scatter_b, flat_b, met_b, sum_b, mine_b, (f_s, f_r))
    hops_end()
    for copy in (*spread_a, *spread_b):
        copy.wait_recv()
    pool[0] = sum_b[0:rows, :]
    pool[1] = sum_a[0:rows, :]
    pool[2] = sum_a[rows : 2 * rows, :]
    pool[LATE] = jnp.zeros_like(pool[LATE])
    for j in range(held):
        grad = packed[z, j].astype(jnp.float32)
        grad = grad + pool[late_at[z * held + j]].astype(jnp.float32)
        w, one, two = adam_update(w_ref[j], one_ref[j], two_ref[j], grad, 0.01, rate_value)
        w_out[j] = w
        one_out[j] = one
        two_out[j] = two
    small_out[...] = sum_b[rows : rows + small_rows, :].astype(jnp.float32)

    @pl.when(stays)
    def done():
        keep.wait()

    @pl.when(jnp.logical_not(stays))
    def gone():
        home_moves[0].wait()

    home_moves[1].wait()
    for _, copy in (*core_moves, *plane_moves):
        copy.wait_send()
    for copy in (
        *over_moves,
        *small_core,
        *small_plane,
        *scatter_a,
        *scatter_b,
        *spread_a,
        *spread_b,
    ):
        copy.wait_send()


def finish(
    holder,
    late_at,
    x_all,
    dq,
    dk,
    dv,
    gh1,
    first,
    early,
    small,
    master,
    one,
    two,
    n_shard,
    n_ctx,
    n_tp,
):
    _, mid, width = x_all.shape
    held, rows, _ = master.shape
    groups = n_ctx * n_tp
    span = 16 * n_shard
    long_a = -(-2 * rows // span) * span
    long_b = -(-(rows + small.shape[0]) // span) * span
    smem = pl.BlockSpec(memory_space=pltpu.SMEM)
    anywhere = pl.BlockSpec(memory_space=pl.ANY)
    vmem = pl.BlockSpec(memory_space=pltpu.VMEM)
    dma = pltpu.SemaphoreType.DMA
    low = jnp.bfloat16
    pairs = [LATE * n_ctx * (n_tp - 1), LATE * (n_ctx - 1), 2, 2, n_tp - 1, n_ctx - 1]
    pairs += [n_shard - 1] * 6
    stored = f32_of(held, rows, width)
    shapes = [
        x_all.shape,
        dq.shape,
        dk.shape,
        dv.shape,
        None,
        first.shape,
        (4, EARLY, rows, width),
        (EARLY + 1, rows, width),
        (n_shard, held, rows, width),
        (n_shard - 1, held, rows, width),
        (n_shard - 1, held, rows, width),
        (width, 4 * mid),
        (groups, LATE, rows, width),
        (n_tp - 1, n_ctx, LATE, rows, width),
        (n_ctx, LATE, rows, width),
        (n_ctx - 1, LATE, rows, width),
        (2, mid, width),
        (2, mid, width),
        (2, mid, width),
        small.shape,
        (n_tp - 1, *small.shape),
        small.shape,
        (n_ctx - 1, *small.shape),
        *[
            shape
            for long in (long_a, long_b)
            for shape in (
                (long, width),
                (n_shard - 1, long // n_shard, width),
                (long, width),
                (long // n_shard, width),
            )
        ],
        (LATE + 1, rows, width),
    ]
    return pl.pallas_call(
        functools.partial(finish_kernel, n_shard, n_ctx, n_tp),
        name="finish",
        in_specs=[smem] * 2 + [anywhere] * 11 + [vmem] * 4,
        out_specs=[anywhere] + [vmem] * 4,
        out_shape=[bf16_of(2, mid, width), stored, stored, stored, f32_of(*small.shape)],
        scratch_shapes=[
            pltpu.VMEM(s, low) if s else pltpu.VMEM(gh1.shape, jnp.float32) for s in shapes
        ]
        + [dma((11,))]
        + [dma((n,)) for n in pairs for _ in range(2)]
        + [dma((1,))],
        compiler_params=pltpu.CompilerParams(
            collective_id=1, has_side_effects=True, vmem_limit_bytes=63 << 20
        ),
        cost_estimate=pl.CostEstimate(
            flops=12_000_000_000, bytes_accessed=40 << 20, transcendentals=0
        ),
    )(holder, late_at, x_all, dq, dk, dv, gh1, first, *early, small, master, one, two)


def shards(
    inputs,
    cotangent,
    rand_blocks,
    slot_of,
    master,
    moment_one,
    moment_two,
    small_params,
    small_one,
    small_two,
):
    n_shard = lax.axis_size("shard")
    n_ctx = lax.axis_size("ctx")
    n_tp = lax.axis_size("tp")
    groups = n_ctx * n_tp
    held, rows, width = master.shape
    span = small_params.shape[0]
    my_ctx = lax.axis_index("ctx")
    my_tp = lax.axis_index("tp")
    half = lax.rem(my_tp, 2)
    plane = ("ctx", "tp")

    half_one = half.astype(jnp.int32).reshape(1)
    my_shard = lax.axis_index("shard")
    start = ((my_shard * n_ctx + my_ctx) * n_tp + my_tp) * span
    lone = lax.dynamic_update_slice(
        jnp.zeros((16 * width,), jnp.float32), small_params, (start,)
    ).reshape(16, width)
    local_at = slot_of[:LATE] - my_shard * held
    local_at = jnp.where((local_at >= 0) & (local_at < held), local_at, held)
    begun = begin(
        slot_of,
        local_at,
        rand_blocks,
        master,
        lone,
        inputs,
        cotangent,
        n_shard,
        n_ctx,
        n_tp,
    )
    x_all, first, rest, small, q, k, v, context, lse = begun[:9]
    cots, out_low, n1, r1, n2, r2, fit, hid, gel = begun[9:]
    *early, gh1, dctx, sums, layer_home = back(
        n2, r2, cots, hid, gel, fit, n1, r1, context, small, rest, out_low, n_ctx, n_tp
    )
    for j in range(1, n_ctx):
        crossing = [
            (a * n_tp + b, (a ^ j) * n_tp + b) for a in range(n_ctx) for b in range(n_tp)
        ]
        early[j + 1] = lax.ppermute(early[j + 1], plane, crossing)
    dq, dk, dv = attend_back(half_one, rand_blocks, q, k, v, lse, dctx, 5)
    stands = jnp.array([8, 0, 2, 4, 6, 1, 3, 5, 7], jnp.int32)
    slots_all = jnp.arange(n_shard * held, dtype=jnp.int32)
    hits = slot_of[None, :] == slots_all[:, None]
    holder = EARLY + jnp.sum(jnp.where(hits[:, LATE:], stands[None, :] - EARLY, 0), axis=1)
    ranks = jnp.arange(LATE, dtype=jnp.int32)[None, :]
    late_at = LATE + jnp.sum(jnp.where(hits[:, :LATE], ranks - LATE, 0), axis=1)
    came, master_new, first_new, second_new, small_sum = finish(
        holder.astype(jnp.int32),
        late_at.astype(jnp.int32),
        x_all,
        dq,
        dk,
        dv,
        gh1,
        first,
        early,
        sums,
        master,
        moment_one,
        moment_two,
        n_shard,
        n_ctx,
        n_tp,
    )
    layer_out = layer_home.astype(jnp.float32)
    input_grad = came.astype(jnp.float32)
    small_owned = lax.dynamic_slice_in_dim(small_sum.reshape(-1), start, span)
    small_new, small_first, small_second = adam_update(
        small_params, small_one, small_two, small_owned, 0.0, small_rate
    )
    return (
        layer_out,
        input_grad,
        master_new,
        first_new,
        second_new,
        small_new,
        small_first,
        small_second,
    )


def solution(mesh):
    tokens = P(("shard", "tp"), "ctx", None)
    stored = P("shard", ("ctx", "tp"), None)
    spread = P(("shard", "ctx", "tp"))
    return jax.shard_map(
        shards,
        mesh=mesh,
        in_specs=(tokens, tokens, P(), P(), stored, stored, stored, spread, spread, spread),
        out_specs=(tokens, tokens, stored, stored, stored, spread, spread, spread),
        check_vma=False,
    )
```

```python
import functools

import jax
import jax.numpy as jnp
from jax import lax
from jax.experimental import pallas as pl
from jax.experimental.pallas import tpu as pltpu
from jax.sharding import PartitionSpec as P

STEP = 5
norm_eps = 1e-12
beta_one = 0.9
beta_two = 0.999
adam_eps = 1e-08
rate_value = 0.04
small_rate = 0.25
score_scale = 0.125
gelu_root = 0.7978845608
gelu_cube = 0.044715

BLOCK = 64
HEAD = 64
PACK = 4
masked_score = -1e30


def wide_dot(a, b, dims):
    return lax.dot_general(a, b, (dims, ((), ())), preferred_element_type=jnp.float32)


def head_masks(rows):
    lane = lax.broadcasted_iota(jnp.int32, (rows, PACK * HEAD), 1) // HEAD
    return [lane == h for h in range(PACK)]


def spread_heads(block, masks):
    zero = jnp.zeros_like(block)
    return jnp.concatenate([jnp.where(m, block, zero) for m in masks], axis=0)


def own_heads(full, masks):
    total = None
    for h, m in enumerate(masks):
        piece = jnp.where(m, full[h * BLOCK : (h + 1) * BLOCK], 0.0)
        total = piece if total is None else total + piece
    return total


def rows_of(ref, index, count=1):
    return ref[pl.ds(index, count)].reshape(count * BLOCK, ref.shape[2])


def flat_rows(ref, index):
    return ref[pl.ds(pl.multiple_of(index * BLOCK, BLOCK), BLOCK), :]


def picked_rows(ref, picks, low_half):
    halves = []
    for pair in range(PACK // 2):
        cols = slice(pair * 2 * HEAD, (pair + 1) * 2 * HEAD)
        first = ref[picks[2 * pair], :, cols]
        second = ref[picks[2 * pair + 1], :, cols]
        halves.append(jnp.where(low_half, first, second))
    return jnp.concatenate(halves, axis=1)


def gathered(ref, block, last, picks, low_half):
    pieces = [rows_of(ref, 0), rows_of(ref, last), rows_of(ref, block - 1, 3)]
    pieces += [picked_rows(ref, p, low_half) for p in picks]
    return jnp.concatenate(pieces, axis=0)


def middle_scores(keys, spread, block, last):
    scores = wide_dot(keys, spread, ((1,), (1,)))
    first_off = jnp.where(block == 1, masked_score, 0.0)
    last_off = jnp.where(block == last - 1, masked_score, 0.0)
    b = BLOCK
    return jnp.concatenate(
        [
            scores[: 2 * b],
            scores[2 * b : 3 * b] + first_off,
            scores[3 * b : 4 * b],
            scores[4 * b : 5 * b] + last_off,
            scores[5 * b :],
        ],
        axis=0,
    )


def attend_back_kernel(
    unroll,
    half_ref,
    table_ref,
    q_ref,
    k_ref,
    v_ref,
    lse_ref,
    do_ref,
    layer_ref,
    dq_ref,
    dk_ref,
    dv_ref,
    wide_ref,
    dk_acc,
    dv_acc,
    kept_p,
    kept_g,
):
    wide_ref[...] = layer_ref[...].astype(jnp.float32)
    half = half_ref[0]
    group = pl.program_id(0)
    q_ref, k_ref, v_ref = q_ref.at[0], k_ref.at[0], v_ref.at[0]
    nblocks, local = k_ref.shape[0], q_ref.shape[0]
    last = nblocks - 1
    picks_each = table_ref.shape[2]
    masks = head_masks(BLOCK)
    low_half = lax.broadcasted_iota(jnp.int32, (BLOCK, 2 * HEAD), 1) < HEAD
    span = 8 * BLOCK
    chunks = nblocks // 8

    edge = (local - 1) * half
    spread = spread_heads(rows_of(q_ref, edge), masks)
    spread_do = spread_heads(flat_rows(do_ref, edge), masks)
    lse = lse_ref[0, pl.ds(edge, 1), :]
    delta = None
    for c in range(chunks):
        rows = slice(c * span, (c + 1) * span)
        probs = jnp.exp(wide_dot(rows_of(k_ref, c * 8, 8), spread, ((1,), (1,))) - lse)
        gp = wide_dot(rows_of(v_ref, c * 8, 8), spread_do, ((1,), (1,)))
        kept_p[rows, :] = probs
        kept_g[rows, :] = gp
        part = jnp.sum(probs * gp, axis=0, keepdims=True)
        delta = part if delta is None else delta + part
    full = None
    for c in range(chunks):
        rows = slice(c * span, (c + 1) * span)
        probs = kept_p[rows, :]
        ds = (probs * (kept_g[rows, :] - delta)).astype(jnp.bfloat16)
        dv_acc[rows, :] = wide_dot(probs.astype(jnp.bfloat16), spread_do, ((1,), (0,)))
        dk_acc[rows, :] = wide_dot(ds, spread, ((1,), (0,)))
        part = wide_dot(ds, rows_of(k_ref, c * 8, 8), ((0,), (0,)))
        full = part if full is None else full + part
    dq_ref[pl.ds(pl.multiple_of(edge * BLOCK, BLOCK), BLOCK), :] = (
        own_heads(full, masks) * 0.125
    ).astype(jnp.bfloat16)

    def scatter(acc, piece, block, picks):
        b = BLOCK
        acc[0:b, :] += piece[:b]
        acc[last * b : (last + 1) * b, :] += piece[b : 2 * b]
        window = pl.ds(pl.multiple_of((block - 1) * b, b), 3 * b)
        acc[window, :] += piece[2 * b : 5 * b]
        for r, p in enumerate(picks):
            part = piece[(5 + r) * b : (6 + r) * b]
            for pair in range(PACK // 2):
                lanes = slice(pair * 2 * HEAD, (pair + 1) * 2 * HEAD)
                cols = pl.ds(pair * 2 * HEAD, 2 * HEAD)
                sub = part[:, lanes]
                acc[pl.ds(pl.multiple_of(p[2 * pair] * b, b), b), cols] += jnp.where(
                    low_half, sub, 0.0
                )
                acc[pl.ds(pl.multiple_of(p[2 * pair + 1] * b, b), b), cols] += jnp.where(
                    low_half, 0.0, sub
                )

    def middle(step, carry):
        mine = step + 1 - half
        block = mine + local * half
        picks = [
            [table_ref[group * PACK + h, block - 1, r] for h in range(PACK)]
            for r in range(picks_each)
        ]
        spread = spread_heads(rows_of(q_ref, mine), masks)
        spread_do = spread_heads(flat_rows(do_ref, mine), masks)
        keys = gathered(k_ref, block, last, picks, low_half)
        values = gathered(v_ref, block, last, picks, low_half)
        scores = middle_scores(keys, spread, block, last)
        probs = jnp.exp(scores - lse_ref[0, pl.ds(mine, 1), :])
        gp = wide_dot(values, spread_do, ((1,), (1,)))
        delta = jnp.sum(probs * gp, axis=0, keepdims=True)
        ds = (probs * (gp - delta)).astype(jnp.bfloat16)
        low = probs.astype(jnp.bfloat16)
        scatter(dv_acc, wide_dot(low, spread_do, ((1,), (0,))), block, picks)
        scatter(dk_acc, wide_dot(ds, spread, ((1,), (0,))), block, picks)
        full = wide_dot(ds, keys, ((0,), (0,)))
        dq_ref[pl.ds(pl.multiple_of(mine * BLOCK, BLOCK), BLOCK), :] = (
            own_heads(full, masks) * 0.125
        ).astype(jnp.bfloat16)
        return carry

    lax.fori_loop(0, local - 1, middle, 0, unroll=unroll)
    dk_ref[...] = dk_acc[...].astype(jnp.bfloat16)
    dv_ref[...] = dv_acc[...].astype(jnp.bfloat16)


def attend_back(half, table, q, k, v, lse, do, layer, unroll=3):
    tokens, width = do.shape
    groups, nblocks, _, lanes = k.shape
    seq = nblocks * BLOCK
    blocks = tokens // BLOCK
    mine = pl.BlockSpec((tokens, lanes), lambda g, *_: (0, g))
    whole = pl.BlockSpec((seq, lanes), lambda g, *_: (0, g))
    spec = pltpu.PrefetchScalarGridSpec(
        num_scalar_prefetch=2,
        grid=(groups,),
        in_specs=[
            pl.BlockSpec((1, blocks, BLOCK, lanes), lambda g, *_: (g, 0, 0, 0)),
            pl.BlockSpec((1, nblocks, BLOCK, lanes), lambda g, *_: (g, 0, 0, 0)),
            pl.BlockSpec((1, nblocks, BLOCK, lanes), lambda g, *_: (g, 0, 0, 0)),
            pl.BlockSpec((1, blocks, lanes), lambda g, *_: (g, 0, 0)),
            mine,
            pl.BlockSpec((*layer.shape[:2], lanes), lambda g, *_: (0, 0, g)),
        ],
        out_specs=[
            mine,
            whole,
            whole,
            pl.BlockSpec((*layer.shape[:2], lanes), lambda g, *_: (0, 0, g)),
        ],
        scratch_shapes=[pltpu.VMEM((seq, lanes), jnp.float32)] * 4,
    )
    return pl.pallas_call(
        functools.partial(attend_back_kernel, unroll),
        grid_spec=spec,
        out_shape=[
            jax.ShapeDtypeStruct((tokens, width), jnp.bfloat16),
            jax.ShapeDtypeStruct((seq, width), jnp.bfloat16),
            jax.ShapeDtypeStruct((seq, width), jnp.bfloat16),
            jax.ShapeDtypeStruct(layer.shape, jnp.float32),
        ],
        name="attend_back",
        compiler_params=pltpu.CompilerParams(vmem_limit_bytes=56 << 20),
        cost_estimate=pl.CostEstimate(
            flops=120_000_000_000, bytes_accessed=24 << 20, transcendentals=16_000_000
        ),
    )(half, table, q, k, v, lse, do, layer)


TILE = 256
MID = 512


def cols_mean(value):
    return jnp.mean(value, axis=-1, keepdims=True)


def normed(field):
    centred = field - cols_mean(field)
    rate = lax.rsqrt(cols_mean(centred * centred) + norm_eps)
    return centred * rate, rate


def norm_back(cot, normal, rate, gain):
    dn = cot * gain
    return rate * (dn - cols_mean(dn) - normal * cols_mean(dn * normal))


def matrix(ref):
    value = ref[...]
    return value.reshape(-1, value.shape[-1])


def add_row(ref, row, value):
    ref[row : row + 1, :] += jnp.sum(value, axis=0, keepdims=True)


def bf16_of(*shape):
    return jax.ShapeDtypeStruct(shape, jnp.bfloat16)


def f32_of(*shape):
    return jax.ShapeDtypeStruct(shape, jnp.float32)


NN = ((1,), (0,))
NT = ((1,), (1,))
TN = ((0,), (0,))


MESH = pl.DeviceIdType.MESH
KINDS = 3
CHUNKS = 3
HOOKS = (2, 3, 7)
PER = 3


def place_of():
    c, t = lax.axis_index("ctx"), lax.axis_index("tp")
    return lax.axis_index("shard"), c, t


def send(src, dst, sems, index, target):
    send_sems, recv_sems = sems
    return pltpu.make_async_remote_copy(
        src_ref=src,
        dst_ref=dst,
        send_sem=send_sems.at[index],
        recv_sem=recv_sems.at[index],
        device_id=target,
        device_id_type=MESH,
    )


def begin_kernel(
    n_shard,
    n_ctx,
    n_tp,
    slots,
    local_at,
    table,
    master_hbm,
    small_in,
    input_hbm,
    cot_hbm,
    x_ref,
    first_ref,
    rest_out,
    small_ref,
    q_ref,
    k_ref,
    v_ref,
    ctx_ref,
    lse_ref,
    cot_ref,
    layer_ref,
    n1_ref,
    r1_ref,
    n2_ref,
    r2_ref,
    fit_ref,
    hid_ref,
    gel_ref,
    raw,
    low,
    given,
    xs,
    x_all,
    part,
    got,
    mine,
    total,
    pool,
    sel,
    first,
    rest_ref,
    small,
    q_s,
    k_s,
    v_s,
    ctx_s,
    kept,
    n1_s,
    gel_s,
    hid_s,
    fit_s,
    layer_s,
    x_s,
    x_r,
    xt_s,
    xt_r,
    za_s,
    za_r,
    zb_s,
    zb_r,
    zc_s,
    zc_r,
    zd_s,
    zd_r,
    qm_s,
    qm_r,
    qt_s,
    qt_r,
    r_s,
    r_r,
    rt_s,
    rt_r,
    y_s,
    y_r,
    own_sem,
    out_sem,
    tile_sem,
    end_sem,
):
    z, c, t = place_of()
    side, core, bit = t // 2, lax.rem(t, 2), lax.rem(c, 2)
    held, rows, width = low.shape[0] - 1, low.shape[1], low.shape[2]
    piece = mine.shape[0]
    me = c * n_tp + t
    _, mid, _ = xs.shape
    nblocks = 4 * mid // BLOCK
    local = nblocks // 2
    lanes = PACK * HEAD
    groups = width // lanes
    others = n_tp - 1

    take_raw = pltpu.make_async_copy(master_hbm, raw, own_sem.at[0])
    take_given = pltpu.make_async_copy(input_hbm, given, own_sem.at[1])
    take_raw.start()
    take_given.start()

    def far(dz):
        return (lax.rem(z + dz, n_shard), c, t)

    def across(mask):
        return (z, c ^ mask, t)

    def beside(dt):
        return (z, c, lax.rem(t + dt, n_tp))

    barrier = pltpu.get_barrier_semaphore()
    friends = [far(dz) for dz in range(1, n_shard)]
    friends += [(z, c ^ m, t) for m in range(1, n_ctx)]
    friends += [beside(dt) for dt in range(1, n_tp)]
    friends += [(z, c ^ m, t ^ 1) for m in range(1, n_ctx)]
    for friend in friends:
        pl.semaphore_signal(barrier, inc=1, device_id=friend, device_id_type=MESH)

    take_raw.wait()
    for j in range(held):
        low[j] = raw[j].astype(jnp.bfloat16)
    low[held] = jnp.zeros_like(low[held])
    pool[pl.ds(z * held, held)] = low[0:held]
    part[...] = jnp.zeros_like(part)
    for m in range(KINDS):
        part[m * rows : (m + 1) * rows, :] = low[local_at[m]]
    part[KINDS * rows : KINDS * rows + 16, :] = small_in[...].astype(jnp.bfloat16)
    pl.semaphore_wait(barrier, len(friends))

    def piece_at(k):
        return pl.ds(pl.multiple_of(k * piece, piece), piece)

    def hop_copy(s, way):
        sems = (zc_s, zc_r) if way > 0 else (zd_s, zd_r)
        slot = pl.ds((z - way * (s - 1)) * held, held)
        return send(
            pool.at[slot], pool.at[slot], sems, s - 1, (lax.rem(z + way + n_shard, n_shard), c, t)
        )

    def hop_on(s, way):
        start = z - way * (s - 1)
        end = z + way
        return (start >= 0) & (start < n_shard) & (end >= 0) & (end < n_shard)

    def hop(s):
        for way in (1, -1):

            @pl.when(hop_on(s, way))
            def move(way=way):
                if s > 1:
                    hop_copy(s - 1, way).wait_recv()
                hop_copy(s, way).start()

    za = [
        send(part.at[piece_at(far(dz)[0])], got.at[dz - 1], (za_s, za_r), dz - 1, far(dz))
        for dz in range(1, n_shard)
    ]
    for copy in za:
        copy.start()

    stays = c // 2 == core
    goes = [(z, 2 * core + (p ^ bit), 2 * side + c // 2) for p in range(2)]
    x_moves = [send(xs.at[p], x_all.at[p], (x_s, x_r), p, goes[p]) for p in range(2)]
    x_keep = pltpu.make_async_copy(xs.at[0], x_all.at[0], own_sem.at[2])
    take_given.wait()
    xs[0] = given[bit].astype(jnp.bfloat16)

    @pl.when(stays)
    def keep():
        x_keep.start()

    @pl.when(jnp.logical_not(stays))
    def leave():
        x_moves[0].start()

    xs[1] = given[1 - bit].astype(jnp.bfloat16)
    x_moves[1].start()

    summed = part[piece_at(z), :]
    for dz, copy in enumerate(za):
        copy.wait_recv()
        summed = summed + got[dz]
    mine[...] = summed
    zb = [
        send(mine, total.at[piece_at(z)], (zb_s, zb_r), dz - 1, far(dz))
        for dz in range(1, n_shard)
    ]
    for copy in zb:
        copy.start()
    hop(1)
    total[piece_at(z), :] = summed
    def hops_end():
        for way, end in ((1, n_shard - 1), (-1, 0)):

            @pl.when(z == end)
            def gather(way=way):
                for s in range(1, n_shard):
                    hop_copy(s, way).wait_recv()

    def hops_sent():
        for s in range(1, n_shard):
            for way in (1, -1):

                @pl.when(hop_on(s, way))
                def sent(s=s, way=way):
                    hop_copy(s, way).wait_send()

    for copy in zb:
        copy.wait_recv()
    hop(2)

    q_moves = [
        send(total, first.at[me], (qm_s, qm_r), k, across(m)) for k, m in enumerate((1, 2, 3))
    ]
    for copy in q_moves:
        copy.start()
    qt_moves = [
        send(total, first.at[me], (qt_s, qt_r), dt - 1, beside(dt)) for dt in range(1, n_tp)
    ]
    for copy in qt_moves:
        copy.start()
    first[me] = total[...]

    x_over = [
        send(x_all.at[p], x_all.at[2 + p], (xt_s, xt_r), p, (z, c, t ^ 1)) for p in range(2)
    ]

    @pl.when(stays)
    def stayed():
        x_keep.wait()

    @pl.when(jnp.logical_not(stays))
    def came():
        x_moves[0].wait_recv()

    x_over[0].start()
    x_moves[1].wait_recv()
    x_over[1].start()
    for s in range(3, n_shard):
        hop(s)

    for k, m in enumerate((1, 2, 3)):
        q_moves[k].wait_recv()
        place = (c ^ m) * n_tp + t
        for dt in range(1, n_tp):
            copy = send(
                first.at[place],
                first.at[place],
                (qt_s, qt_r),
                (k + 1) * others + dt - 1,
                beside(dt),
            )
            copy.start()
            qt_moves.append(copy)
    for copy in qt_moves:
        copy.wait_recv()
    def span_of(k):
        return pl.ds(k * PER, PER)

    rest_own = pltpu.make_async_copy(sel, rest_ref.at[me], own_sem.at[3])
    direct = [
        [
            send(
                sel.at[span_of(k)], rest_ref.at[me, span_of(k)], (r_s, r_r), k * 3 + j, across(m)
            )
            for j, m in enumerate((1, 2))
        ]
        for k in range(CHUNKS)
    ]
    onward = []
    for k in range(CHUNKS):
        odd = lax.rem(core + k, 2)
        source = jnp.where(odd == 0, c ^ 1, c ^ 2) * n_tp + t
        target = (z, jnp.where(odd == 0, c ^ 2, c ^ 1), t)
        view = rest_ref.at[source, span_of(k)]
        onward.append(send(view, view, (r_s, r_r), k * 3 + 2, target))

    def passing(k, which):
        if which == 0:
            src = sel.at[span_of(k)]
        else:
            src = rest_ref.at[(c ^ which) * n_tp + t, span_of(k)]
        dst = rest_ref.at[(c ^ which) * n_tp + t, span_of(k)]
        return [
            send(src, dst, (rt_s, rt_r), (k * 4 + which) * others + dt - 1, beside(dt))
            for dt in range(1, n_tp)
        ]

    passed = [[passing(k, which) for which in range(4)] for k in range(CHUNKS)]

    def begin_rest():
        hops_end()
        for m in range(CHUNKS * PER):
            sel[m] = pool[slots[KINDS + m]]
        rest_own.start()
        launch(0)
        launch(1)

    def launch(k):
        for copy in (*direct[k], *passed[k][0]):
            copy.start()

    def relay(k):
        for copy in direct[k]:
            copy.wait_recv()
        onward[k].start()
        for copy in passed[k][1] + passed[k][2]:
            copy.start()

    def last_relay(k):
        onward[k].wait_recv()
        for copy in passed[k][3]:
            copy.start()

    begin_rest()
    outs = [pltpu.make_async_copy(first, first_ref, out_sem.at[0])]
    outs[0].start()

    sums = None
    for g in range(n_ctx * n_tp):
        here = first[g, KINDS * rows : KINDS * rows + 16, :].astype(jnp.float32)
        sums = here if sums is None else sums + here
    small[...] = sums
    small_ref[...] = sums
    def weight(m):
        return first[:, m * rows : (m + 1) * rows, :].reshape(width, width)

    def split(dst, start, value):
        low_value = value.astype(jnp.bfloat16)
        per = TILE // BLOCK
        for g in range(groups):
            piece_value = low_value[:, g * lanes : (g + 1) * lanes]
            dst[g, pl.ds(start, per)] = piece_value.reshape(per, BLOCK, lanes)

    def project(a, chunk, own):
        def one(i, carry):
            x = x_all[a, pl.ds(pl.multiple_of(i * TILE, TILE), TILE), :]
            start = chunk * (mid // BLOCK) + i * (TILE // BLOCK)
            if own:
                q_start = (chunk - 2 * core) * (mid // BLOCK) + i * (TILE // BLOCK)
                q = wide_dot(x, weight(0), NN) + small[0:1, :]
                split(q_s, q_start, q.astype(jnp.bfloat16) * jnp.bfloat16(score_scale))
            split(k_s, start, wide_dot(x, weight(1), NN))
            split(v_s, start, wide_dot(x, weight(2), NN) + small[1:2, :])
            return carry

        lax.fori_loop(0, mid // TILE, one, 0)

    def own_project(a, carry):
        project(a, 2 * core + (a ^ bit), True)
        return carry

    def other_project(a, carry):
        project(2 + a, 2 * (1 - core) + (a ^ bit), False)
        return carry

    @pl.when(jnp.logical_not(stays))
    def left():
        x_moves[0].wait_send()

    x_moves[1].wait_send()
    take_cot = pltpu.make_async_copy(cot_hbm, given, own_sem.at[2])
    take_cot.start()
    lax.fori_loop(0, 2, own_project, 0)
    for copy in x_over:
        copy.wait_recv()
    outs.append(pltpu.make_async_copy(x_all, x_ref, out_sem.at[1]))
    outs[1].start()
    lax.fori_loop(0, 2, other_project, 0)
    take_cot.wait()
    xs[0] = given[bit].astype(jnp.bfloat16)
    xs[1] = given[1 - bit].astype(jnp.bfloat16)
    for i, (src, dst) in enumerate(((q_s, q_ref), (k_s, k_ref), (v_s, v_ref))):
        outs.append(pltpu.make_async_copy(src, dst, out_sem.at[2 + i]))
        outs[-1].start()

    last = nblocks - 1
    picks_each = table.shape[2]
    masks = head_masks(BLOCK)
    low_half = lax.broadcasted_iota(jnp.int32, (BLOCK, 2 * HEAD), 1) < HEAD
    each = 5
    subs = (local - 1) // each

    def attend_round(i, carry):
        g = i // subs
        sub = lax.rem(i, subs)
        qg, kg, vg = q_s.at[g], k_s.at[g], v_s.at[g]
        for k in range(CHUNKS):

            @pl.when(i == HOOKS[k])
            def hook(k=k):
                relay(k)
                if k == 0:
                    launch(2)

        @pl.when(i == groups * subs - 1)
        def late_hook():
            last_relay(0)
            last_relay(1)

        @pl.when(sub == 0)
        def edge_block():
            edge = (local - 1) * core
            spread = spread_heads(rows_of(qg, edge), masks)
            span = 8 * BLOCK
            pieces = nblocks // 8
            top = None
            for n in range(pieces):
                scores = wide_dot(rows_of(kg, n * 8, 8), spread, NT)
                kept[n * span : (n + 1) * span, :] = scores
                high = jnp.max(scores, axis=0, keepdims=True)
                top = high if top is None else jnp.maximum(top, high)
            total_p = None
            for n in range(pieces):
                probs = jnp.exp(kept[n * span : (n + 1) * span, :] - top)
                kept[n * span : (n + 1) * span, :] = probs
                some = jnp.sum(probs, axis=0, keepdims=True)
                total_p = some if total_p is None else total_p + some
            scale = 1.0 / total_p
            full = None
            for n in range(pieces):
                probs = (kept[n * span : (n + 1) * span, :] * scale).astype(jnp.bfloat16)
                some = wide_dot(probs, rows_of(vg, n * 8, 8), TN)
                full = some if full is None else full + some
            at = pl.ds(pl.multiple_of(edge * BLOCK, BLOCK), BLOCK)
            ctx_s[g, at, :] = own_heads(full, masks).astype(jnp.bfloat16)
            lse_ref[g, pl.ds(edge, 1), :] = top + jnp.log(total_p)

        for u in range(each):
            spot = sub * each + u + 1 - core
            block = spot + local * core
            picks = [
                [table[g * PACK + h, block - 1, r] for h in range(PACK)]
                for r in range(picks_each)
            ]
            spread = spread_heads(rows_of(qg, spot), masks)
            keys = gathered(kg, block, last, picks, low_half)
            values = gathered(vg, block, last, picks, low_half)
            scores = middle_scores(keys, spread, block, last)
            top = jnp.max(scores, axis=0, keepdims=True)
            probs = jnp.exp(scores - top)
            total_p = jnp.sum(probs, axis=0, keepdims=True)
            probs = (probs * (1.0 / total_p)).astype(jnp.bfloat16)
            full = wide_dot(probs, values, TN)
            at = pl.ds(pl.multiple_of(spot * BLOCK, BLOCK), BLOCK)
            ctx_s[g, at, :] = own_heads(full, masks).astype(jnp.bfloat16)
            lse_ref[g, pl.ds(spot, 1), :] = top + jnp.log(total_p)
        return carry

    lax.fori_loop(0, groups * subs, attend_round, 0)
    for g in range(groups):
        outs.append(
            pltpu.make_async_copy(
                ctx_s.at[g], ctx_ref.at[:, g * lanes : (g + 1) * lanes], out_sem.at[5 + g]
            )
        )
        outs[-1].start()
    last_relay(2)

    cot_moves = [send(xs.at[p], cot_ref.at[p], (y_s, y_r), p, goes[p]) for p in range(2)]
    cot_keep = pltpu.make_async_copy(xs.at[0], cot_ref.at[0], own_sem.at[1])

    @pl.when(stays)
    def keep_cot():
        cot_keep.start()

    @pl.when(jnp.logical_not(stays))
    def leave_cot():
        cot_moves[0].start()

    cot_moves[1].start()

    for k in range(2):
        for group in passed[k]:
            for copy in group:
                copy.wait_recv()
    rest_own.wait()
    tiles = 2 * mid // TILE
    per = mid // TILE

    def held_out(m):
        return rest_ref[:, m].reshape(width, width)

    def tile_out(i, slot):
        at = pl.ds(pl.multiple_of(i * TILE, TILE), TILE)
        return (
            pltpu.make_async_copy(n1_s.at[slot], n1_ref.at[at], tile_sem.at[slot]),
            pltpu.make_async_copy(gel_s.at[slot], gel_ref.at[:, at], tile_sem.at[2 + slot]),
        )

    def rise_tile(i, carry):
        slot = lax.rem(i, 2)
        at = pl.ds(pl.multiple_of(i * TILE, TILE), TILE)
        inside = pl.ds(pl.multiple_of(lax.rem(i, per) * TILE, TILE), TILE)

        @pl.when(i >= 2)
        def free():
            for copy in tile_out(i - 2, slot):
                copy.wait()

        context = jnp.concatenate([ctx_s[g, at, :] for g in range(groups)], axis=1)
        attn_out = wide_dot(context, held_out(0), NN) + small[2:3, :]
        x = x_all[(i // per) ^ bit, inside, :].astype(jnp.float32)
        n1, r1 = normed(x + attn_out)
        n1_s[slot] = n1
        r1_ref[at, :] = jnp.broadcast_to(r1, (TILE, r1_ref.shape[1]))
        after = n1 * small[3:4, :] + small[4:5, :]
        ffn_in = after.astype(jnp.bfloat16)
        fit_s[:, at] = ffn_in.T
        given[i // per, inside, :] = after + small[9:10, :]
        for b in range(4):
            up = wide_dot(ffn_in, held_out(1 + b), NN) + small[5 + b : 6 + b, :]
            square = up * up
            bent = jnp.tanh(gelu_root * up * (1.0 + gelu_cube * square))
            rise = 0.5 * (1.0 + bent)
            hid_s[b, at, :] = (up * rise).astype(jnp.bfloat16)
            slope = rise + (0.5 * gelu_root) * up * (1.0 - bent * bent) * (
                1.0 + (3.0 * gelu_cube) * square
            )
            gel_s[slot, b] = slope.astype(jnp.bfloat16)
        for copy in tile_out(i, slot):
            copy.start()
        return carry

    lax.fori_loop(0, tiles, rise_tile, 0)
    for i in range(tiles - 2, tiles):
        for copy in tile_out(i, i % 2):
            copy.wait()
    for i, (src, dst) in enumerate(((hid_s, hid_ref), (fit_s, fit_ref))):
        outs.append(pltpu.make_async_copy(src, dst, out_sem.at[5 + groups + i]))
        outs[-1].start()
    for group in passed[2]:
        for copy in group:
            copy.wait_recv()
    outs.append(pltpu.make_async_copy(rest_ref, rest_out, out_sem.at[7 + groups]))
    outs[-1].start()

    def end_out(i):
        at = pl.ds(pl.multiple_of(i * TILE, TILE), TILE)
        inside = pl.ds(pl.multiple_of(lax.rem(i, per) * TILE, TILE), TILE)
        chunk = i // per
        return (
            pltpu.make_async_copy(given.at[chunk, inside], n2_ref.at[at], end_sem.at[i]),
            pltpu.make_async_copy(
                layer_s.at[chunk ^ bit, inside],
                layer_ref.at[chunk ^ bit, inside],
                end_sem.at[tiles + i],
            ),
        )

    def fall_tile(i, carry):
        at = pl.ds(pl.multiple_of(i * TILE, TILE), TILE)
        inside = pl.ds(pl.multiple_of(lax.rem(i, per) * TILE, TILE), TILE)
        summed = given[i // per, inside, :]
        for b in range(4):
            summed = summed + wide_dot(hid_s[b, at, :], held_out(5 + b), NT)
        n2, r2 = normed(summed)
        layer_s[(i // per) ^ bit, inside, :] = (n2 * small[10:11, :] + small[11:12, :]).astype(
            jnp.bfloat16
        )
        given[i // per, inside, :] = n2
        r2_ref[at, :] = jnp.broadcast_to(r2, (TILE, r2_ref.shape[1]))
        for copy in end_out(i):
            copy.start()
        return carry

    lax.fori_loop(0, tiles, fall_tile, 0)
    for i in range(tiles):
        for copy in end_out(i):
            copy.wait()

    @pl.when(stays)
    def kept_cot():
        cot_keep.wait()

    @pl.when(jnp.logical_not(stays))
    def left_cot():
        cot_moves[0].wait()

    cot_moves[1].wait()
    for copy in (*x_over, *za, *zb, *q_moves, *qt_moves, *onward):
        copy.wait_send()
    for pair in direct:
        for copy in pair:
            copy.wait_send()
    for chunk in passed:
        for group in chunk:
            for copy in group:
                copy.wait_send()
    hops_sent()
    for copy in outs:
        copy.wait()


def begin(slots, local_at, table, master, small_in, inputs, cot, n_shard, n_ctx, n_tp):
    held, rows, width = master.shape
    _, mid, _ = inputs.shape
    groups = n_ctx * n_tp
    long = -(-(KINDS * rows + 16) // (16 * n_shard)) * 16 * n_shard
    lanes = PACK * HEAD
    packs = width // lanes
    tokens, seq = 2 * mid, 4 * mid
    anywhere = pl.BlockSpec(memory_space=pl.ANY)
    vmem = pl.BlockSpec(memory_space=pltpu.VMEM)
    smem = pl.BlockSpec(memory_space=pltpu.SMEM)
    dma = pltpu.SemaphoreType.DMA
    low = jnp.bfloat16
    f32 = jnp.float32
    pairs = [2, 2, n_shard - 1, n_shard - 1, n_shard - 1, n_shard - 1, 3]
    pairs += [4 * (n_tp - 1), 3 * CHUNKS, 4 * CHUNKS * (n_tp - 1), 2]
    return pl.pallas_call(
        functools.partial(begin_kernel, n_shard, n_ctx, n_tp),
        name="begin",
        in_specs=[smem, smem, smem, anywhere, vmem, anywhere, anywhere],
        out_specs=[anywhere] * 3
        + [vmem]
        + [anywhere] * 4
        + [vmem]
        + [anywhere] * 3
        + [vmem, anywhere, vmem]
        + [anywhere] * 3,
        out_shape=[
            bf16_of(4, mid, width),
            bf16_of(groups, long, width),
            bf16_of(groups, 9, rows, width),
            f32_of(16, width),
            bf16_of(packs, tokens // BLOCK, BLOCK, lanes),
            bf16_of(packs, seq // BLOCK, BLOCK, lanes),
            bf16_of(packs, seq // BLOCK, BLOCK, lanes),
            bf16_of(tokens, width),
            f32_of(packs, tokens // BLOCK, lanes),
            bf16_of(2, mid, width),
            bf16_of(2, mid, width),
            f32_of(tokens, width),
            f32_of(tokens, 128),
            f32_of(tokens, width),
            f32_of(tokens, 128),
            bf16_of(width, tokens),
            bf16_of(4, tokens, width),
            bf16_of(4, tokens, width),
        ],
        scratch_shapes=[
            pltpu.VMEM((held, rows, width), f32),
            pltpu.VMEM((held + 1, rows, width), low),
            pltpu.VMEM((2, mid, width), f32),
            pltpu.VMEM((2, mid, width), low),
            pltpu.VMEM((4, mid, width), low),
            pltpu.VMEM((long, width), low),
            pltpu.VMEM((n_shard - 1, long // n_shard, width), low),
            pltpu.VMEM((long // n_shard, width), low),
            pltpu.VMEM((long, width), low),
            pltpu.VMEM((n_shard * held, rows, width), low),
            pltpu.VMEM((9, rows, width), low),
            pltpu.VMEM((groups, long, width), low),
            pltpu.VMEM((groups, 9, rows, width), low),
            pltpu.VMEM((16, width), f32),
            pltpu.VMEM((packs, tokens // BLOCK, BLOCK, lanes), low),
            pltpu.VMEM((packs, seq // BLOCK, BLOCK, lanes), low),
            pltpu.VMEM((packs, seq // BLOCK, BLOCK, lanes), low),
            pltpu.VMEM((packs, tokens, lanes), low),
            pltpu.VMEM((seq, lanes), f32),
            pltpu.VMEM((2, TILE, width), f32),
            pltpu.VMEM((2, 4, TILE, width), low),
            pltpu.VMEM((4, tokens, width), low),
            pltpu.VMEM((width, tokens), low),
            pltpu.VMEM((2, mid, width), low),
            *[dma((n,)) for n in pairs for _ in range(2)],
            dma((4,)),
            dma((8 + packs,)),
            dma((4,)),
            dma((2 * (tokens // TILE),)),
        ],
        compiler_params=pltpu.CompilerParams(
            collective_id=0, has_side_effects=True, vmem_limit_bytes=64000 << 10
        ),
        cost_estimate=pl.CostEstimate(
            flops=60_000_000_000, bytes_accessed=60 << 20, transcendentals=16_000_000
        ),
    )(slots, local_at, table, master, small_in, inputs, cot)


NEAR = 3
CROSSINGS = -(-NEAR // 2)


def back_kernel(
    n_ctx,
    n_tp,
    n2_hbm,
    r2_ref,
    cots_ref,
    hid_ref,
    gel_ref,
    fit_ref,
    n1_ref,
    r1_ref,
    ctx_ref,
    small,
    up_w,
    down_w,
    wo,
    layer_ref,
    own_ref,
    near_ref,
    x_ref,
    y_ref,
    xy_ref,
    gh1_ref,
    dctx_ref,
    sums_ref,
    home_ref,
    gy,
    gu,
    mixed,
    mixed_t,
    grads,
    arrived,
    sums,
    send_sem,
    recv_sem,
    h_s,
    h_r,
    n_s,
    n_r,
    keep_sem,
    out_sem,
):
    z, c, t = place_of()
    step = pl.program_id(0)
    tokens, width = gy.shape
    tiles = tokens // TILE
    rows = grads.shape[4]
    others = n_tp - 1
    side, core, bit = t // 2, lax.rem(t, 2), lax.rem(c, 2)

    def beside(dt):
        return (z, c, lax.rem(t + dt, n_tp))

    stays = c // 2 == core
    keep_layer = pltpu.make_async_copy(layer_ref.at[0], home_ref.at[bit], keep_sem.at[0])
    layer_moves = [
        send(
            layer_ref.at[p],
            home_ref.at[bit],
            (h_s, h_r),
            p,
            (z, 2 * core + (p ^ bit), 2 * side + c // 2),
        )
        for p in range(2)
    ]

    @pl.when(step == 0)
    def start():
        take = pltpu.make_async_copy(n2_hbm, gy, keep_sem.at[1])
        take.start()
        barrier = pltpu.get_barrier_semaphore()
        friends = [beside(dt) for dt in range(1, n_tp)]
        friends += [(z, c ^ m, t) for m in range(1, n_ctx)]
        friends += [(z, c ^ m, t ^ 1) for m in range(1, n_ctx)]
        for friend in friends:
            pl.semaphore_signal(barrier, inc=1, device_id=friend, device_id_type=MESH)
        pl.semaphore_wait(barrier, len(friends))

        @pl.when(stays)
        def kept():
            keep_layer.start()

        @pl.when(jnp.logical_not(stays))
        def left():
            layer_moves[0].start()

        layer_moves[1].start()
        sums_ref[...] = jnp.zeros_like(sums_ref)
        take.wait()
        mid = tokens // 2
        for p in range(2):

            def one(i, carry, p=p):
                inside = pl.ds(pl.multiple_of(i * TILE, TILE), TILE)
                at = pl.ds(pl.multiple_of((p ^ bit) * mid + i * TILE, TILE), TILE)
                cot = cots_ref[p, inside, :].astype(jnp.float32)
                n2 = gy[at, :]
                add_row(sums_ref, 10, cot * n2)
                add_row(sums_ref, 11, cot)
                gh2 = norm_back(cot, n2, r2_ref[at, 0:1], small[10:11, :])
                gy[at, :] = gh2
                low = gh2.astype(jnp.bfloat16)
                mixed[at, :] = low
                mixed_t[:, at] = low.T
                add_row(sums_ref, 9, low.astype(jnp.float32))
                return carry

            lax.fori_loop(0, mid // TILE, one, 0)

    def moves(b, count):
        slot = lax.rem(b, 2)
        return [
            send(
                grads.at[slot, :, lax.rem(t + dt, n_tp), 0:count],
                arrived.at[b, dt - 1, :, 0:count],
                (send_sem, recv_sem),
                b * others + dt - 1,
                beside(dt),
            )
            for dt in range(1, n_tp)
        ]

    def exchange(b, count):
        for copy in moves(b, count):
            copy.start()

    def keep(b, count):
        for copy in moves(b, count):
            copy.wait()
        slot = lax.rem(b, 2)
        for j in range(n_ctx):
            for i in range(count):
                value = grads[slot, c ^ j, t, i]
                for dt in range(others):
                    value = value + arrived[b, dt, c ^ j, i]
                sums[j, 2 * b + i] = value

    def near(b):
        pair = slice(2 * b, min(2 * b + 2, NEAR))
        return [
            send(
                sums.at[j, pair],
                near_ref.at[j - 1, pair],
                (n_s, n_r),
                b * (n_ctx - 1) + j - 1,
                (z, c ^ j, t),
            )
            for j in range(1, n_ctx)
        ]

    def outward(part, first, count):
        moved = [
            pltpu.make_async_copy(
                sums.at[0, first : first + count],
                own_ref.at[first : first + count],
                out_sem.at[part * n_ctx],
            )
        ]
        begin_at = max(first, NEAR)
        count -= begin_at - first
        for j, out in enumerate((x_ref, y_ref, xy_ref)):
            moved.append(
                pltpu.make_async_copy(
                    sums.at[j + 1, begin_at : begin_at + count],
                    out.at[begin_at - NEAR : begin_at - NEAR + count],
                    out_sem.at[part * n_ctx + j + 1],
                )
            )
        return moved

    def put(slot, i, value):
        low = value.astype(jnp.bfloat16)
        grads[slot, :, :, i] = low.reshape(n_ctx, n_tp, rows, width)

    @pl.when(step < 4)
    def ffn():
        up_block = matrix(up_w)
        down_block = matrix(down_w)
        slot = lax.rem(step, 2)

        def one(i, carry):
            at = pl.ds(pl.multiple_of(i * MID, MID), MID)
            grad = wide_dot(mixed[at, :], down_block, NN) * gel_ref[0, at, :].astype(jnp.float32)
            low = grad.astype(jnp.bfloat16)
            gu[at, :] = low
            gy[at, :] += wide_dot(low, up_block, NT)
            sums_ref[pl.ds(5 + step, 1), :] += jnp.sum(
                low.astype(jnp.float32), axis=0, keepdims=True
            )
            return carry

        lax.fori_loop(0, tokens // MID, one, 0)
        put(slot, 0, wide_dot(fit_ref[...], gu[...], NN))
        put(slot, 1, wide_dot(mixed_t[...], hid_ref[0], NN))
        exchange(step, 2)

    @pl.when(step > 0)
    def settle():
        keep(step - 1, 2)

    for b in range(CROSSINGS):

        @pl.when(step == b + 1)
        def cross(b=b):
            for copy in near(b):
                copy.start()

    @pl.when(step == 4)
    def first_norm():
        for copy in outward(0, 0, 8):
            copy.start()

        def one(i, carry):
            at = pl.ds(pl.multiple_of(i * TILE, TILE), TILE)
            grad = gy[at, :]
            n1 = n1_ref[at, :]
            gh1 = norm_back(grad, n1, r1_ref[at, 0:1], small[3:4, :])
            gh1_ref[at, :] = gh1
            low = gh1.astype(jnp.bfloat16)
            gu[at, :] = low
            add_row(sums_ref, 2, low.astype(jnp.float32))
            add_row(sums_ref, 3, grad * n1)
            add_row(sums_ref, 4, grad)
            return carry

        lax.fori_loop(0, tiles, one, 0)
        put(0, 0, wide_dot(ctx_ref[...].T, gu[...], NN))
        exchange(4, 1)
        out_w = matrix(wo)

        def two(i, carry):
            at = pl.ds(pl.multiple_of(i * TILE, TILE), TILE)
            dctx_ref[at, :] = wide_dot(gu[at, :], out_w, NT).astype(jnp.bfloat16)
            return carry

        lax.fori_loop(0, tiles, two, 0)
        keep(4, 1)
        for copy in outward(1, 8, 1):
            copy.start()
        crossed = [copy for b in range(CROSSINGS) for copy in near(b)]
        for copy in (*crossed, *outward(0, 0, 8), *outward(1, 8, 1)):
            copy.wait()

        @pl.when(stays)
        def done():
            keep_layer.wait()

        @pl.when(jnp.logical_not(stays))
        def gone():
            layer_moves[0].wait()

        layer_moves[1].wait()


def back(n2, r2, cots, hid, gel, fit, n1, r1, ctx, small, rest, layer, n_ctx, n_tp):
    tokens, width = n2.shape
    rows = rest.shape[2]
    dma = pltpu.SemaphoreType.DMA

    def whole(shape):
        return pl.BlockSpec(shape, lambda b: (0,) * len(shape), pipeline_mode=pl.Buffered(1))

    def block(b):
        return (jnp.minimum(b, 3), 0, 0)

    def held(first, single=False):
        return pl.BlockSpec(
            (n_ctx * n_tp, 1, rows, width),
            (lambda b: (0, first, 0, 0))
            if single
            else (lambda b: (0, first + jnp.minimum(b, 3), 0, 0)),
            pipeline_mode=pl.Buffered(1) if single else None,
        )

    def out(shape):
        return pl.BlockSpec(shape, lambda b: (0,) * len(shape))

    return pl.pallas_call(
        functools.partial(back_kernel, n_ctx, n_tp),
        name="back",
        grid=(5,),
        in_specs=[
            pl.BlockSpec(memory_space=pl.ANY),
            whole((tokens, 128)),
            whole((2, tokens // 2, width)),
            pl.BlockSpec((1, tokens, width), block),
            pl.BlockSpec((1, tokens, width), block),
            whole((width, tokens)),
            whole((tokens, width)),
            whole((tokens, 128)),
            whole((tokens, width)),
            whole(small.shape),
            held(1),
            held(5),
            held(0, True),
            pl.BlockSpec(memory_space=pl.ANY),
        ],
        out_specs=[
            *[pl.BlockSpec(memory_space=pl.ANY)] * 5,
            out((tokens, width)),
            out((tokens, width)),
            out((16, width)),
            pl.BlockSpec(memory_space=pl.ANY),
        ],
        out_shape=[
            bf16_of(9, rows, width),
            bf16_of(n_ctx - 1, NEAR, rows, width),
            *[bf16_of(9 - NEAR, rows, width)] * 3,
            f32_of(tokens, width),
            bf16_of(tokens, width),
            f32_of(16, width),
            bf16_of(*layer.shape),
        ],
        scratch_shapes=[
            pltpu.VMEM((tokens, width), jnp.float32),
            pltpu.VMEM((tokens, width), jnp.bfloat16),
            pltpu.VMEM((tokens, width), jnp.bfloat16),
            pltpu.VMEM((width, tokens), jnp.bfloat16),
            pltpu.VMEM((2, n_ctx, n_tp, 2, rows, width), jnp.bfloat16),
            pltpu.VMEM((5, n_tp - 1, n_ctx, 2, rows, width), jnp.bfloat16),
            pltpu.VMEM((n_ctx, 9 + 1, rows, width), jnp.bfloat16),
            dma((5 * (n_tp - 1),)),
            dma((5 * (n_tp - 1),)),
            dma((2,)),
            dma((2,)),
            dma((CROSSINGS * (n_ctx - 1),)),
            dma((CROSSINGS * (n_ctx - 1),)),
            dma((2,)),
            dma((2 * n_ctx,)),
        ],
        compiler_params=pltpu.CompilerParams(
            collective_id=3, has_side_effects=True, vmem_limit_bytes=62 << 20
        ),
        cost_estimate=pl.CostEstimate(
            flops=22_000_000_000, bytes_accessed=40 << 20, transcendentals=0
        ),
    )(n2, r2, cots, hid, gel, fit, n1, r1, ctx, small, rest, rest, rest, layer)


LATE = 3
EARLY = 9


def adam_update(weight, first, second, grad, decay, rate):
    count = float(STEP)
    first_new = beta_one * first + (1.0 - beta_one) * grad
    second_new = beta_two * second + (1.0 - beta_two) * grad * grad
    first_hat = first_new / (1.0 - beta_one**count)
    second_hat = second_new / (1.0 - beta_two**count)
    weight_new = weight - rate * (first_hat / (jnp.sqrt(second_hat) + adam_eps) + decay * weight)
    return (weight_new, first_new, second_new)


def finish_kernel(
    n_shard,
    n_ctx,
    n_tp,
    holder,
    late_at,
    x_hbm,
    dq_hbm,
    dk_hbm,
    dv_hbm,
    gh1_hbm,
    first_hbm,
    e0_hbm,
    near_hbm,
    e1_hbm,
    e2_hbm,
    e3_hbm,
    small_ref,
    home_ref,
    grad_out,
    small_out,
    x_s,
    dq_s,
    dk_s,
    dv_s,
    gh1_s,
    first_s,
    early,
    every,
    packed,
    right_met,
    left_met,
    flipped,
    grads,
    arrived,
    partial,
    met,
    over,
    more,
    back_s,
    small_s,
    small_t,
    small_m,
    small_p,
    flat_a,
    met_a,
    sum_a,
    mine_a,
    flat_b,
    met_b,
    sum_b,
    mine_b,
    pool,
    in_sem,
    c_s,
    c_r,
    p_s,
    p_r,
    o_s,
    o_r,
    h_s,
    h_r,
    sc_s,
    sc_r,
    sp_s,
    sp_r,
    e_s,
    e_r,
    l_s,
    l_r,
    a_s,
    a_r,
    b_s,
    b_r,
    d_s,
    d_r,
    f_s,
    f_r,
    keep_sem,
):
    z, c, t = place_of()
    side, core, bit = t // 2, lax.rem(t, 2), lax.rem(c, 2)
    _, mid, width = x_s.shape
    tokens = 2 * mid
    held, rows, _ = grad_out.shape
    per = n_ctx * n_tp // 2
    band = width // 2
    tile = mid

    loads = [
        pltpu.make_async_copy(src, dst, in_sem.at[i])
        for i, (src, dst) in enumerate(
            (
                (x_hbm, x_s),
                (dk_hbm, dk_s),
                (dv_hbm, dv_s),
                (dq_hbm, dq_s),
                (first_hbm, first_s),
                (gh1_hbm, gh1_s),
                (e0_hbm, early.at[0]),
                (near_hbm, early.at[1:4, 0:NEAR]),
                (e1_hbm, early.at[1, NEAR:EARLY]),
                (e2_hbm, early.at[2, NEAR:EARLY]),
                (e3_hbm, early.at[3, NEAR:EARLY]),
            )
        )
    ]
    for i in (6, 7, 8, 9, 10, 0, 1, 2, 3, 4, 5):
        loads[i].start()

    def far(dz):
        return (lax.rem(z + dz, n_shard), c, t)

    def across(mask):
        return (z, c ^ mask, t)

    def beside(dt):
        return (z, c, lax.rem(t + dt, n_tp))

    barrier = pltpu.get_barrier_semaphore()
    friends = [far(dz) for dz in range(1, n_shard)]
    friends += [(z, c ^ m, t) for m in range(1, n_ctx)]
    friends += [beside(dt) for dt in range(1, n_tp)]
    friends += [(z, c ^ m, t ^ 1) for m in range(1, n_ctx)]
    for friend in friends:
        pl.semaphore_signal(barrier, inc=1, device_id=friend, device_id_type=MESH)

    for i in range(6, 11):
        loads[i].wait()
    every[0:EARLY] = early[0] + early[1] + early[2] + early[3]
    every[EARLY] = jnp.zeros_like(every[EARLY])
    for s in range(n_shard * held):
        packed[s // held, s % held] = every[holder[s]]
    pl.semaphore_wait(barrier, len(friends))

    def run(owner_at, s, way):
        met, sems = (right_met, (e_s, e_r)) if way > 0 else (left_met, (l_s, l_r))
        target = (lax.rem(z + way + n_shard, n_shard), c, t)
        return send(packed.at[owner_at], met.at[s], sems, s, target)

    def each_run(hop):
        for s in range(hop + 1):
            for way in (1, -1):
                place = hop - s if way > 0 else n_shard - 1 - (hop - s)
                owner_at = n_shard - 1 - s if way > 0 else s
                yield s, way, place, owner_at

    def hop(h):
        for s, way, place, owner_at in each_run(h):

            @pl.when(z == place)
            def move(s=s, way=way, place=place, owner_at=owner_at):
                copy = run(owner_at, s, way)
                if h > s:
                    copy.wait_recv()
                    met = right_met if way > 0 else left_met
                    for j in range(held):
                        packed[owner_at, j] = packed[owner_at, j] + met[s, j]
                copy.start()

    def hops_end():
        for h in range(n_shard - 1):
            for s, way, place, owner_at in each_run(h):

                @pl.when(z == place)
                def sent(s=s, way=way, owner_at=owner_at):
                    run(owner_at, s, way).wait_send()

        for s in range(n_shard - 1):
            for way in (1, -1):
                owner_at = n_shard - 1 - s if way > 0 else s

                @pl.when(z == owner_at)
                def last(s=s, way=way, owner_at=owner_at):
                    run(owner_at, s, way).wait_recv()
                    met = right_met if way > 0 else left_met
                    for j in range(held):
                        packed[owner_at, j] = packed[owner_at, j] + met[s, j]

    hop(0)

    core_moves = []

    def exchange(m):
        for dt in range(1, n_tp):
            other = lax.rem(t + dt, n_tp)
            for k in range(n_ctx):
                copy = send(
                    grads.at[k * n_tp + other, m],
                    arrived.at[dt - 1, k, m],
                    (c_s, c_r),
                    ((dt - 1) * n_ctx + k) * LATE + m,
                    beside(dt),
                )
                copy.start()
                core_moves.append((m, copy))

    plane_moves = []

    def meet(m):
        for which, copy in core_moves:
            if which == m:
                copy.wait_recv()
        for k in range(n_ctx):
            value = grads[k * n_tp + t, m]
            for dt in range(1, n_tp):
                value = value + arrived[dt - 1, k, m]
            partial[k, m] = value
        for j in range(1, n_ctx):
            copy = send(
                partial.at[c ^ j, m], met.at[j - 1, m], (p_s, p_r), (j - 1) * LATE + m, across(j)
            )
            copy.start()
            plane_moves.append((m, copy))

    loads[0].wait()
    for a in range(4):
        chunk = 2 * (core if a < 2 else 1 - core) + ((a % 2) ^ bit)
        flipped[:, pl.ds(pl.multiple_of(chunk * mid, mid), mid)] = x_s[a].T

    def weight_grad(m, left_at, right):
        def one(i, carry):
            left = flipped[pl.ds(pl.multiple_of(i * band, band), band), left_at]
            value = wide_dot(left, right[...], NN).astype(jnp.bfloat16)
            grads[pl.ds(i * per, per), m] = value.reshape(per, rows, width)
            return carry

        lax.fori_loop(0, 2, one, 0)

    loads[1].wait()
    weight_grad(1, slice(None), dk_s)
    exchange(1)
    loads[2].wait()
    weight_grad(2, slice(None), dv_s)
    exchange(2)
    meet(1)
    for h in range(1, n_shard - 2):
        hop(h)
    loads[3].wait()
    weight_grad(0, pl.ds(pl.multiple_of(core * tokens, tokens), tokens), dq_s)
    exchange(0)
    meet(2)

    row = lax.broadcasted_iota(jnp.int32, small_ref.shape, 0)
    q_sum = jnp.sum(dq_s[...].astype(jnp.float32), axis=0, keepdims=True)
    v_sum = jnp.sum(dv_s[...].astype(jnp.float32), axis=0, keepdims=True)
    sums = jnp.where(row == 0, q_sum, jnp.where(row == 1, v_sum, small_ref[...]))
    small_s[...] = sums.astype(jnp.bfloat16)
    small_core = [
        send(small_s, small_t.at[dt - 1], (sc_s, sc_r), dt - 1, beside(dt)) for dt in range(1, n_tp)
    ]
    for copy in small_core:
        copy.start()

    loads[4].wait()

    def weight(m):
        return first_s[:, m * rows : (m + 1) * rows, :].reshape(width, width)

    wq, wk, wv = weight(0), weight(1), weight(2)
    over_moves = []
    for b in range(2):
        at = pl.ds(pl.multiple_of((1 - core) * tokens + b * mid, mid), mid)
        value = wide_dot(dk_s[at, :], wk, NT) + wide_dot(dv_s[at, :], wv, NT)
        over[b] = value.astype(jnp.bfloat16)
        copy = send(over.at[b], more.at[b], (o_s, o_r), b, (z, c, t ^ 1))
        copy.start()
        over_moves.append(copy)
        if b == 0:
            meet(0)
            if n_shard > 2:
                hop(n_shard - 2)

    value = small_s[...]
    for dt, copy in enumerate(small_core):
        copy.wait_recv()
        value = value + small_t[dt]
    small_m[...] = value
    small_plane = [
        send(small_m, small_p.at[j - 1], (sp_s, sp_r), j - 1, across(j)) for j in range(1, n_ctx)
    ]
    for copy in small_plane:
        copy.start()

    loads[5].wait()
    stays = c // 2 == core
    home_moves = []
    for copy in over_moves:
        copy.wait_recv()
    keep = pltpu.make_async_copy(back_s.at[0], home_ref.at[bit], keep_sem.at[0])
    for move in range(2):
        chunk = move ^ bit
        for i in range(mid // tile):
            at = pl.ds(pl.multiple_of(core * tokens + chunk * mid + i * tile, tile), tile)
            here = pl.ds(pl.multiple_of(chunk * mid + i * tile, tile), tile)
            value = gh1_s[here, :]
            value = value + more[chunk, i * tile : (i + 1) * tile, :].astype(jnp.float32)
            value = value + wide_dot(dq_s[here, :], wq, NT)
            value = value + wide_dot(dk_s[at, :], wk, NT)
            value = value + wide_dot(dv_s[at, :], wv, NT)
            back_s[move, i * tile : (i + 1) * tile, :] = value.astype(jnp.bfloat16)
        target = (z, 2 * core + chunk, 2 * side + c // 2)
        home_moves.append(send(back_s.at[move], home_ref.at[bit], (h_s, h_r), move, target))
        if move == 0:

            @pl.when(stays)
            def kept():
                keep.start()

            @pl.when(jnp.logical_not(stays))
            def left():
                home_moves[0].start()

        else:
            home_moves[1].start()

    def gathered_rows(m):
        for which, copy in plane_moves:
            if which == m:
                copy.wait_recv()
        value = partial[c, m]
        for j in range(n_ctx - 1):
            value = value + met[j, m]
        return value

    def piece_at(ref, k):
        piece = ref.shape[0] // n_shard
        return pl.ds(pl.multiple_of(k * piece, piece), piece)

    def scatter_lot(flat, lot_met, sems):
        moves = [
            send(flat.at[piece_at(flat, far(dz)[0])], lot_met.at[dz - 1], sems, dz - 1, far(dz))
            for dz in range(1, n_shard)
        ]
        for copy in moves:
            copy.start()
        return moves

    def spread_lot(moves, flat, lot_met, lot_sum, lot_mine, sems):
        total = flat[piece_at(flat, z), :].astype(jnp.float32)
        for dz, copy in enumerate(moves):
            copy.wait_recv()
            total = total + lot_met[dz].astype(jnp.float32)
        lot_mine[...] = total.astype(jnp.bfloat16)
        spreads = [
            send(lot_mine, lot_sum.at[piece_at(flat, z)], sems, dz - 1, far(dz))
            for dz in range(1, n_shard)
        ]
        for copy in spreads:
            copy.start()
        lot_sum[piece_at(flat, z), :] = lot_mine[...]
        return spreads

    small_rows = small_s.shape[0]
    flat_a[...] = jnp.zeros_like(flat_a)
    flat_b[...] = jnp.zeros_like(flat_b)
    flat_a[0:rows, :] = gathered_rows(1)
    flat_a[rows : 2 * rows, :] = gathered_rows(2)
    scatter_a = scatter_lot(flat_a, met_a, (a_s, a_r))
    flat_b[0:rows, :] = gathered_rows(0)
    value = small_m[...]
    for j, copy in enumerate(small_plane):
        copy.wait_recv()
        value = value + small_p[j]
    flat_b[rows : rows + small_rows, :] = value
    scatter_b = scatter_lot(flat_b, met_b, (b_s, b_r))
    spread_a = spread_lot(scatter_a, flat_a, met_a, sum_a, mine_a, (d_s, d_r))
    spread_b = spread_lot(scatter_b, flat_b, met_b, sum_b, mine_b, (f_s, f_r))
    hops_end()
    for copy in (*spread_a, *spread_b):
        copy.wait_recv()
    pool[0] = sum_b[0:rows, :]
    pool[1] = sum_a[0:rows, :]
    pool[2] = sum_a[rows : 2 * rows, :]
    pool[LATE] = jnp.zeros_like(pool[LATE])
    for j in range(held):
        grad = packed[z, j].astype(jnp.float32)
        grad = grad + pool[late_at[z * held + j]].astype(jnp.float32)
        grad_out[j] = grad
    small_out[...] = sum_b[rows : rows + small_rows, :].astype(jnp.float32)

    @pl.when(stays)
    def done():
        keep.wait()

    @pl.when(jnp.logical_not(stays))
    def gone():
        home_moves[0].wait()

    home_moves[1].wait()
    for _, copy in (*core_moves, *plane_moves):
        copy.wait_send()
    for copy in (
        *over_moves,
        *small_core,
        *small_plane,
        *scatter_a,
        *scatter_b,
        *spread_a,
        *spread_b,
    ):
        copy.wait_send()


def finish(
    holder,
    late_at,
    x_all,
    dq,
    dk,
    dv,
    gh1,
    first,
    early,
    small,
    held,
    n_shard,
    n_ctx,
    n_tp,
):
    _, mid, width = x_all.shape
    rows = width // (n_ctx * n_tp)
    groups = n_ctx * n_tp
    span = 16 * n_shard
    long_a = -(-2 * rows // span) * span
    long_b = -(-(rows + small.shape[0]) // span) * span
    smem = pl.BlockSpec(memory_space=pltpu.SMEM)
    anywhere = pl.BlockSpec(memory_space=pl.ANY)
    vmem = pl.BlockSpec(memory_space=pltpu.VMEM)
    dma = pltpu.SemaphoreType.DMA
    low = jnp.bfloat16
    pairs = [LATE * n_ctx * (n_tp - 1), LATE * (n_ctx - 1), 2, 2, n_tp - 1, n_ctx - 1]
    pairs += [n_shard - 1] * 6
    shapes = [
        x_all.shape,
        dq.shape,
        dk.shape,
        dv.shape,
        None,
        first.shape,
        (4, EARLY, rows, width),
        (EARLY + 1, rows, width),
        (n_shard, held, rows, width),
        (n_shard - 1, held, rows, width),
        (n_shard - 1, held, rows, width),
        (width, 4 * mid),
        (groups, LATE, rows, width),
        (n_tp - 1, n_ctx, LATE, rows, width),
        (n_ctx, LATE, rows, width),
        (n_ctx - 1, LATE, rows, width),
        (2, mid, width),
        (2, mid, width),
        (2, mid, width),
        small.shape,
        (n_tp - 1, *small.shape),
        small.shape,
        (n_ctx - 1, *small.shape),
        *[
            shape
            for long in (long_a, long_b)
            for shape in (
                (long, width),
                (n_shard - 1, long // n_shard, width),
                (long, width),
                (long // n_shard, width),
            )
        ],
        (LATE + 1, rows, width),
    ]
    return pl.pallas_call(
        functools.partial(finish_kernel, n_shard, n_ctx, n_tp),
        name="finish",
        in_specs=[smem] * 2 + [anywhere] * 11 + [vmem],
        out_specs=[vmem] * 3,
        out_shape=[bf16_of(2, mid, width), f32_of(held, rows, width), f32_of(*small.shape)],
        scratch_shapes=[
            pltpu.VMEM(s, low) if s else pltpu.VMEM(gh1.shape, jnp.float32) for s in shapes
        ]
        + [dma((11,))]
        + [dma((n,)) for n in pairs for _ in range(2)]
        + [dma((1,))],
        compiler_params=pltpu.CompilerParams(
            collective_id=1, has_side_effects=True, vmem_limit_bytes=63 << 20
        ),
        cost_estimate=pl.CostEstimate(
            flops=12_000_000_000, bytes_accessed=40 << 20, transcendentals=0
        ),
    )(holder, late_at, x_all, dq, dk, dv, gh1, first, *early, small)


def shards(
    inputs,
    cotangent,
    rand_blocks,
    slot_of,
    master,
    moment_one,
    moment_two,
    small_params,
    small_one,
    small_two,
):
    n_shard = lax.axis_size("shard")
    n_ctx = lax.axis_size("ctx")
    n_tp = lax.axis_size("tp")
    groups = n_ctx * n_tp
    held, rows, width = master.shape
    span = small_params.shape[0]
    my_ctx = lax.axis_index("ctx")
    my_tp = lax.axis_index("tp")
    half = lax.rem(my_tp, 2)
    plane = ("ctx", "tp")

    half_one = half.astype(jnp.int32).reshape(1)
    my_shard = lax.axis_index("shard")
    start = ((my_shard * n_ctx + my_ctx) * n_tp + my_tp) * span
    lone = lax.dynamic_update_slice(
        jnp.zeros((16 * width,), jnp.float32), small_params, (start,)
    ).reshape(16, width)
    local_at = slot_of[:LATE] - my_shard * held
    local_at = jnp.where((local_at >= 0) & (local_at < held), local_at, held)
    begun = begin(
        slot_of,
        local_at,
        rand_blocks,
        master,
        lone,
        inputs,
        cotangent,
        n_shard,
        n_ctx,
        n_tp,
    )
    x_all, first, rest, small, q, k, v, context, lse = begun[:9]
    cots, out_low, n1, r1, n2, r2, fit, hid, gel = begun[9:]
    *early, gh1, dctx, sums, layer_home = back(
        n2, r2, cots, hid, gel, fit, n1, r1, context, small, rest, out_low, n_ctx, n_tp
    )
    for j in range(1, n_ctx):
        crossing = [
            (a * n_tp + b, (a ^ j) * n_tp + b) for a in range(n_ctx) for b in range(n_tp)
        ]
        early[j + 1] = lax.ppermute(early[j + 1], plane, crossing)
    dq, dk, dv, layer_out = attend_back(
        half_one, rand_blocks, q, k, v, lse, dctx, layer_home, 15
    )
    stands = jnp.array([8, 0, 2, 4, 6, 1, 3, 5, 7], jnp.int32)
    slots_all = jnp.arange(n_shard * held, dtype=jnp.int32)
    hits = slot_of[None, :] == slots_all[:, None]
    holder = EARLY + jnp.sum(jnp.where(hits[:, LATE:], stands[None, :] - EARLY, 0), axis=1)
    ranks = jnp.arange(LATE, dtype=jnp.int32)[None, :]
    late_at = LATE + jnp.sum(jnp.where(hits[:, :LATE], ranks - LATE, 0), axis=1)
    came, slot_grads, small_sum = finish(
        holder.astype(jnp.int32),
        late_at.astype(jnp.int32),
        x_all,
        dq,
        dk,
        dv,
        gh1,
        first,
        early,
        sums,
        held,
        n_shard,
        n_ctx,
        n_tp,
    )
    input_grad = came.astype(jnp.float32)
    master_new, first_new, second_new = adam_update(
        master, moment_one, moment_two, slot_grads, 0.01, rate_value
    )
    small_owned = lax.dynamic_slice_in_dim(small_sum.reshape(-1), start, span)
    small_new, small_first, small_second = adam_update(
        small_params, small_one, small_two, small_owned, 0.0, small_rate
    )
    return (
        layer_out,
        input_grad,
        master_new,
        first_new,
        second_new,
        small_new,
        small_first,
        small_second,
    )


def solution(mesh):
    tokens = P(("shard", "tp"), "ctx", None)
    stored = P("shard", ("ctx", "tp"), None)
    spread = P(("shard", "ctx", "tp"))
    return jax.shard_map(
        shards,
        mesh=mesh,
        in_specs=(tokens, tokens, P(), P(), stored, stored, stored, spread, spread, spread),
        out_specs=(tokens, tokens, stored, stored, stored, spread, spread, spread),
        check_vma=False,
    )
```

```python
import functools

import jax
import jax.numpy as jnp
from jax import lax
from jax.experimental import pallas as pl
from jax.experimental.pallas import tpu as pltpu
from jax.sharding import PartitionSpec as P

STEP = 5
norm_eps = 1e-12
beta_one = 0.9
beta_two = 0.999
adam_eps = 1e-08
rate_value = 0.04
small_rate = 0.25
score_scale = 0.125
gelu_root = 0.7978845608
gelu_cube = 0.044715

BLOCK = 64
HEAD = 64
PACK = 4
masked_score = -1e30


def wide_dot(a, b, dims):
    return lax.dot_general(a, b, (dims, ((), ())), preferred_element_type=jnp.float32)


def head_masks(rows):
    lane = lax.broadcasted_iota(jnp.int32, (rows, PACK * HEAD), 1) // HEAD
    return [lane == h for h in range(PACK)]


def spread_heads(block, masks):
    zero = jnp.zeros_like(block)
    return jnp.concatenate([jnp.where(m, block, zero) for m in masks], axis=0)


def own_heads(full, masks):
    total = None
    for h, m in enumerate(masks):
        piece = jnp.where(m, full[h * BLOCK : (h + 1) * BLOCK], 0.0)
        total = piece if total is None else total + piece
    return total


def rows_of(ref, index, count=1):
    return ref[pl.ds(index, count)].reshape(count * BLOCK, ref.shape[2])


def flat_rows(ref, index):
    return ref[pl.ds(pl.multiple_of(index * BLOCK, BLOCK), BLOCK), :]


def picked_rows(ref, picks, low_half):
    halves = []
    for pair in range(PACK // 2):
        cols = slice(pair * 2 * HEAD, (pair + 1) * 2 * HEAD)
        first = ref[picks[2 * pair], :, cols]
        second = ref[picks[2 * pair + 1], :, cols]
        halves.append(jnp.where(low_half, first, second))
    return jnp.concatenate(halves, axis=1)


def gathered(ref, block, last, picks, low_half):
    pieces = [rows_of(ref, 0), rows_of(ref, last), rows_of(ref, block - 1, 3)]
    pieces += [picked_rows(ref, p, low_half) for p in picks]
    return jnp.concatenate(pieces, axis=0)


def middle_scores(keys, spread, block, last):
    scores = wide_dot(keys, spread, ((1,), (1,)))
    first_off = jnp.where(block == 1, masked_score, 0.0)
    last_off = jnp.where(block == last - 1, masked_score, 0.0)
    b = BLOCK
    return jnp.concatenate(
        [
            scores[: 2 * b],
            scores[2 * b : 3 * b] + first_off,
            scores[3 * b : 4 * b],
            scores[4 * b : 5 * b] + last_off,
            scores[5 * b :],
        ],
        axis=0,
    )


def attend_back_kernel(
    unroll,
    half_ref,
    table_ref,
    q_ref,
    k_ref,
    v_ref,
    lse_ref,
    do_ref,
    layer_ref,
    dq_ref,
    dk_ref,
    dv_ref,
    wide_ref,
    dk_acc,
    dv_acc,
    kept_p,
    kept_g,
):
    wide_ref[...] = layer_ref[...].astype(jnp.float32)
    half = half_ref[0]
    group = pl.program_id(0)
    q_ref, k_ref, v_ref = q_ref.at[0], k_ref.at[0], v_ref.at[0]
    nblocks, local = k_ref.shape[0], q_ref.shape[0]
    last = nblocks - 1
    picks_each = table_ref.shape[2]
    masks = head_masks(BLOCK)
    low_half = lax.broadcasted_iota(jnp.int32, (BLOCK, 2 * HEAD), 1) < HEAD
    span = 8 * BLOCK
    chunks = nblocks // 8

    edge = (local - 1) * half
    spread = spread_heads(rows_of(q_ref, edge), masks)
    spread_do = spread_heads(flat_rows(do_ref, edge), masks)
    lse = lse_ref[0, pl.ds(edge, 1), :]
    delta = None
    for c in range(chunks):
        rows = slice(c * span, (c + 1) * span)
        probs = jnp.exp(wide_dot(rows_of(k_ref, c * 8, 8), spread, ((1,), (1,))) - lse)
        gp = wide_dot(rows_of(v_ref, c * 8, 8), spread_do, ((1,), (1,)))
        kept_p[rows, :] = probs
        kept_g[rows, :] = gp
        part = jnp.sum(probs * gp, axis=0, keepdims=True)
        delta = part if delta is None else delta + part
    full = None
    for c in range(chunks):
        rows = slice(c * span, (c + 1) * span)
        probs = kept_p[rows, :]
        ds = (probs * (kept_g[rows, :] - delta)).astype(jnp.bfloat16)
        dv_acc[rows, :] = wide_dot(probs.astype(jnp.bfloat16), spread_do, ((1,), (0,)))
        dk_acc[rows, :] = wide_dot(ds, spread, ((1,), (0,)))
        part = wide_dot(ds, rows_of(k_ref, c * 8, 8), ((0,), (0,)))
        full = part if full is None else full + part
    dq_ref[pl.ds(pl.multiple_of(edge * BLOCK, BLOCK), BLOCK), :] = (
        own_heads(full, masks) * 0.125
    ).astype(jnp.bfloat16)

    def scatter(acc, piece, block, picks):
        b = BLOCK
        acc[0:b, :] += piece[:b]
        acc[last * b : (last + 1) * b, :] += piece[b : 2 * b]
        window = pl.ds(pl.multiple_of((block - 1) * b, b), 3 * b)
        acc[window, :] += piece[2 * b : 5 * b]
        for r, p in enumerate(picks):
            part = piece[(5 + r) * b : (6 + r) * b]
            for pair in range(PACK // 2):
                lanes = slice(pair * 2 * HEAD, (pair + 1) * 2 * HEAD)
                cols = pl.ds(pair * 2 * HEAD, 2 * HEAD)
                sub = part[:, lanes]
                acc[pl.ds(pl.multiple_of(p[2 * pair] * b, b), b), cols] += jnp.where(
                    low_half, sub, 0.0
                )
                acc[pl.ds(pl.multiple_of(p[2 * pair + 1] * b, b), b), cols] += jnp.where(
                    low_half, 0.0, sub
                )

    def middle(step, carry):
        mine = step + 1 - half
        block = mine + local * half
        picks = [
            [table_ref[group * PACK + h, block - 1, r] for h in range(PACK)]
            for r in range(picks_each)
        ]
        spread = spread_heads(rows_of(q_ref, mine), masks)
        spread_do = spread_heads(flat_rows(do_ref, mine), masks)
        keys = gathered(k_ref, block, last, picks, low_half)
        values = gathered(v_ref, block, last, picks, low_half)
        scores = middle_scores(keys, spread, block, last)
        probs = jnp.exp(scores - lse_ref[0, pl.ds(mine, 1), :])
        gp = wide_dot(values, spread_do, ((1,), (1,)))
        delta = jnp.sum(probs * gp, axis=0, keepdims=True)
        ds = (probs * (gp - delta)).astype(jnp.bfloat16)
        low = probs.astype(jnp.bfloat16)
        scatter(dv_acc, wide_dot(low, spread_do, ((1,), (0,))), block, picks)
        scatter(dk_acc, wide_dot(ds, spread, ((1,), (0,))), block, picks)
        full = wide_dot(ds, keys, ((0,), (0,)))
        dq_ref[pl.ds(pl.multiple_of(mine * BLOCK, BLOCK), BLOCK), :] = (
            own_heads(full, masks) * 0.125
        ).astype(jnp.bfloat16)
        return carry

    lax.fori_loop(0, local - 1, middle, 0, unroll=unroll)
    dk_ref[...] = dk_acc[...].astype(jnp.bfloat16)
    dv_ref[...] = dv_acc[...].astype(jnp.bfloat16)


def attend_back(half, table, q, k, v, lse, do, layer, unroll=3):
    tokens, width = do.shape
    groups, nblocks, _, lanes = k.shape
    seq = nblocks * BLOCK
    blocks = tokens // BLOCK
    mine = pl.BlockSpec((tokens, lanes), lambda g, *_: (0, g))
    whole = pl.BlockSpec((seq, lanes), lambda g, *_: (0, g))
    spec = pltpu.PrefetchScalarGridSpec(
        num_scalar_prefetch=2,
        grid=(groups,),
        in_specs=[
            pl.BlockSpec((1, blocks, BLOCK, lanes), lambda g, *_: (g, 0, 0, 0)),
            pl.BlockSpec((1, nblocks, BLOCK, lanes), lambda g, *_: (g, 0, 0, 0)),
            pl.BlockSpec((1, nblocks, BLOCK, lanes), lambda g, *_: (g, 0, 0, 0)),
            pl.BlockSpec((1, blocks, lanes), lambda g, *_: (g, 0, 0)),
            mine,
            pl.BlockSpec((*layer.shape[:2], lanes), lambda g, *_: (0, 0, g)),
        ],
        out_specs=[
            mine,
            whole,
            whole,
            pl.BlockSpec((*layer.shape[:2], lanes), lambda g, *_: (0, 0, g)),
        ],
        scratch_shapes=[pltpu.VMEM((seq, lanes), jnp.float32)] * 4,
    )
    return pl.pallas_call(
        functools.partial(attend_back_kernel, unroll),
        grid_spec=spec,
        out_shape=[
            jax.ShapeDtypeStruct((tokens, width), jnp.bfloat16),
            jax.ShapeDtypeStruct((seq, width), jnp.bfloat16),
            jax.ShapeDtypeStruct((seq, width), jnp.bfloat16),
            jax.ShapeDtypeStruct(layer.shape, jnp.float32),
        ],
        name="attend_back",
        compiler_params=pltpu.CompilerParams(vmem_limit_bytes=56 << 20),
        cost_estimate=pl.CostEstimate(
            flops=120_000_000_000, bytes_accessed=24 << 20, transcendentals=16_000_000
        ),
    )(half, table, q, k, v, lse, do, layer)


TILE = 256
MID = 512


def cols_mean(value):
    return jnp.mean(value, axis=-1, keepdims=True)


def normed(field):
    centred = field - cols_mean(field)
    rate = lax.rsqrt(cols_mean(centred * centred) + norm_eps)
    return centred * rate, rate


def norm_back(cot, normal, rate, gain):
    dn = cot * gain
    return rate * (dn - cols_mean(dn) - normal * cols_mean(dn * normal))


def matrix(ref):
    value = ref[...]
    return value.reshape(-1, value.shape[-1])


def add_row(ref, row, value):
    ref[row : row + 1, :] += jnp.sum(value, axis=0, keepdims=True)


def bf16_of(*shape):
    return jax.ShapeDtypeStruct(shape, jnp.bfloat16)


def f32_of(*shape):
    return jax.ShapeDtypeStruct(shape, jnp.float32)


NN = ((1,), (0,))
NT = ((1,), (1,))
TN = ((0,), (0,))


MESH = pl.DeviceIdType.MESH
KINDS = 3
CHUNKS = 3
PER = 3


def place_of():
    c, t = lax.axis_index("ctx"), lax.axis_index("tp")
    return lax.axis_index("shard"), c, t


def send(src, dst, sems, index, target):
    send_sems, recv_sems = sems
    return pltpu.make_async_remote_copy(
        src_ref=src,
        dst_ref=dst,
        send_sem=send_sems.at[index],
        recv_sem=recv_sems.at[index],
        device_id=target,
        device_id_type=MESH,
    )


def begin_kernel(
    n_shard,
    n_ctx,
    n_tp,
    slots,
    local_at,
    table,
    master_hbm,
    small_in,
    input_hbm,
    cot_hbm,
    x_ref,
    first_ref,
    rest_out,
    small_ref,
    q_ref,
    k_ref,
    v_ref,
    ctx_ref,
    lse_ref,
    cot_ref,
    layer_ref,
    n1_ref,
    r1_ref,
    n2_ref,
    r2_ref,
    fit_ref,
    hid_ref,
    gel_ref,
    raw,
    low,
    given,
    xs,
    x_all,
    part,
    got,
    mine,
    total,
    pool,
    sel,
    first,
    rest_ref,
    small,
    q_s,
    k_s,
    v_s,
    ctx_s,
    kept,
    n1_s,
    gel_s,
    hid_s,
    fit_s,
    layer_s,
    x_s,
    x_r,
    xt_s,
    xt_r,
    za_s,
    za_r,
    zb_s,
    zb_r,
    zc_s,
    zc_r,
    zd_s,
    zd_r,
    qm_s,
    qm_r,
    qt_s,
    qt_r,
    r_s,
    r_r,
    rt_s,
    rt_r,
    y_s,
    y_r,
    own_sem,
    out_sem,
    tile_sem,
    end_sem,
):
    z, c, t = place_of()
    side, core, bit = t // 2, lax.rem(t, 2), lax.rem(c, 2)
    held, rows, width = low.shape[0] - 1, low.shape[1], low.shape[2]
    piece = mine.shape[0]
    me = c * n_tp + t
    _, mid, _ = xs.shape
    nblocks = 4 * mid // BLOCK
    local = nblocks // 2
    lanes = PACK * HEAD
    groups = width // lanes
    others = n_tp - 1

    take_raw = pltpu.make_async_copy(master_hbm, raw, own_sem.at[0])
    take_given = pltpu.make_async_copy(input_hbm, given, own_sem.at[1])
    take_raw.start()
    take_given.start()

    def far(dz):
        return (lax.rem(z + dz, n_shard), c, t)

    def across(mask):
        return (z, c ^ mask, t)

    def beside(dt):
        return (z, c, lax.rem(t + dt, n_tp))

    barrier = pltpu.get_barrier_semaphore()
    friends = [far(dz) for dz in range(1, n_shard)]
    friends += [(z, c ^ m, t) for m in range(1, n_ctx)]
    friends += [beside(dt) for dt in range(1, n_tp)]
    friends += [(z, c ^ m, t ^ 1) for m in range(1, n_ctx)]
    for friend in friends:
        pl.semaphore_signal(barrier, inc=1, device_id=friend, device_id_type=MESH)

    take_raw.wait()
    for j in range(held):
        low[j] = raw[j].astype(jnp.bfloat16)
    low[held] = jnp.zeros_like(low[held])
    pool[pl.ds(z * held, held)] = low[0:held]
    part[...] = jnp.zeros_like(part)
    for m in range(KINDS):
        part[m * rows : (m + 1) * rows, :] = low[local_at[m]]
    part[KINDS * rows : KINDS * rows + 16, :] = small_in[...].astype(jnp.bfloat16)
    pl.semaphore_wait(barrier, len(friends))

    def piece_at(k):
        return pl.ds(pl.multiple_of(k * piece, piece), piece)

    def hop_copy(s, way):
        sems = (zc_s, zc_r) if way > 0 else (zd_s, zd_r)
        slot = pl.ds((z - way * (s - 1)) * held, held)
        return send(
            pool.at[slot], pool.at[slot], sems, s - 1, (lax.rem(z + way + n_shard, n_shard), c, t)
        )

    def hop_on(s, way):
        start = z - way * (s - 1)
        end = z + way
        return (start >= 0) & (start < n_shard) & (end >= 0) & (end < n_shard)

    def hop(s):
        for way in (1, -1):

            @pl.when(hop_on(s, way))
            def move(way=way):
                if s > 1:
                    hop_copy(s - 1, way).wait_recv()
                hop_copy(s, way).start()

    za = [
        send(part.at[piece_at(far(dz)[0])], got.at[dz - 1], (za_s, za_r), dz - 1, far(dz))
        for dz in range(1, n_shard)
    ]
    for copy in za:
        copy.start()

    stays = c // 2 == core
    goes = [(z, 2 * core + (p ^ bit), 2 * side + c // 2) for p in range(2)]
    x_moves = [send(xs.at[p], x_all.at[p], (x_s, x_r), p, goes[p]) for p in range(2)]
    x_keep = pltpu.make_async_copy(xs.at[0], x_all.at[0], own_sem.at[2])
    take_given.wait()
    xs[0] = given[bit].astype(jnp.bfloat16)

    @pl.when(stays)
    def keep():
        x_keep.start()

    @pl.when(jnp.logical_not(stays))
    def leave():
        x_moves[0].start()

    xs[1] = given[1 - bit].astype(jnp.bfloat16)
    x_moves[1].start()

    summed = part[piece_at(z), :]
    for dz, copy in enumerate(za):
        copy.wait_recv()
        summed = summed + got[dz]
    mine[...] = summed
    zb = [
        send(mine, total.at[piece_at(z)], (zb_s, zb_r), dz - 1, far(dz))
        for dz in range(1, n_shard)
    ]
    for copy in zb:
        copy.start()
    hop(1)
    total[piece_at(z), :] = summed
    def hops_end():
        for way, end in ((1, n_shard - 1), (-1, 0)):

            @pl.when(z == end)
            def gather(way=way):
                for s in range(1, n_shard):
                    hop_copy(s, way).wait_recv()

    def hops_sent():
        for s in range(1, n_shard):
            for way in (1, -1):

                @pl.when(hop_on(s, way))
                def sent(s=s, way=way):
                    hop_copy(s, way).wait_send()

    for copy in zb:
        copy.wait_recv()
    hop(2)

    q_moves = [
        send(total, first.at[me], (qm_s, qm_r), k, across(m)) for k, m in enumerate((1, 2, 3))
    ]
    for copy in q_moves:
        copy.start()
    qt_moves = [
        send(total, first.at[me], (qt_s, qt_r), dt - 1, beside(dt)) for dt in range(1, n_tp)
    ]
    for copy in qt_moves:
        copy.start()
    first[me] = total[...]

    x_over = [
        send(x_all.at[p], x_all.at[2 + p], (xt_s, xt_r), p, (z, c, t ^ 1)) for p in range(2)
    ]

    @pl.when(stays)
    def stayed():
        x_keep.wait()

    @pl.when(jnp.logical_not(stays))
    def came():
        x_moves[0].wait_recv()

    x_over[0].start()
    x_moves[1].wait_recv()
    x_over[1].start()
    for s in range(3, n_shard):
        hop(s)

    for k, m in enumerate((1, 2, 3)):
        q_moves[k].wait_recv()
        place = (c ^ m) * n_tp + t
        for dt in range(1, n_tp):
            copy = send(
                first.at[place],
                first.at[place],
                (qt_s, qt_r),
                (k + 1) * others + dt - 1,
                beside(dt),
            )
            copy.start()
            qt_moves.append(copy)
    for copy in qt_moves:
        copy.wait_recv()
    def span_of(k):
        return pl.ds(k * PER, PER)

    rest_own = pltpu.make_async_copy(sel, rest_ref.at[me], own_sem.at[3])
    direct = [
        [
            send(
                sel.at[span_of(k)], rest_ref.at[me, span_of(k)], (r_s, r_r), k * 3 + j, across(m)
            )
            for j, m in enumerate((1, 2))
        ]
        for k in range(CHUNKS)
    ]
    onward = []
    for k in range(CHUNKS):
        odd = lax.rem(core + k, 2)
        source = jnp.where(odd == 0, c ^ 1, c ^ 2) * n_tp + t
        target = (z, jnp.where(odd == 0, c ^ 2, c ^ 1), t)
        view = rest_ref.at[source, span_of(k)]
        onward.append(send(view, view, (r_s, r_r), k * 3 + 2, target))

    def passing(k, which):
        if which == 0:
            src = sel.at[span_of(k)]
        else:
            src = rest_ref.at[(c ^ which) * n_tp + t, span_of(k)]
        dst = rest_ref.at[(c ^ which) * n_tp + t, span_of(k)]
        return [
            send(src, dst, (rt_s, rt_r), (k * 4 + which) * others + dt - 1, beside(dt))
            for dt in range(1, n_tp)
        ]

    passed = [[passing(k, which) for which in range(4)] for k in range(CHUNKS)]

    def begin_rest():
        hops_end()
        for m in range(CHUNKS * PER):
            sel[m] = pool[slots[KINDS + m]]
        rest_own.start()
        launch(0)
        launch(1)
        launch(2)

    def launch(k):
        for copy in (*direct[k], *passed[k][0]):
            copy.start()

    def relay(k):
        for copy in direct[k]:
            copy.wait_recv()
        onward[k].start()
        for copy in passed[k][1] + passed[k][2]:
            copy.start()

    def last_relay(k):
        onward[k].wait_recv()
        for copy in passed[k][3]:
            copy.start()

    begin_rest()
    outs = [pltpu.make_async_copy(first, first_ref, out_sem.at[0])]
    outs[0].start()

    sums = None
    for g in range(n_ctx * n_tp):
        here = first[g, KINDS * rows : KINDS * rows + 16, :].astype(jnp.float32)
        sums = here if sums is None else sums + here
    small[...] = sums
    small_ref[...] = sums
    def weight(m):
        return first[:, m * rows : (m + 1) * rows, :].reshape(width, width)

    def split(dst, start, value):
        low_value = value.astype(jnp.bfloat16)
        per = TILE // BLOCK
        for g in range(groups):
            piece_value = low_value[:, g * lanes : (g + 1) * lanes]
            dst[g, pl.ds(start, per)] = piece_value.reshape(per, BLOCK, lanes)

    def project(a, chunk, own):
        def one(i, carry):
            x = x_all[a, pl.ds(pl.multiple_of(i * TILE, TILE), TILE), :]
            start = chunk * (mid // BLOCK) + i * (TILE // BLOCK)
            if own:
                q_start = (chunk - 2 * core) * (mid // BLOCK) + i * (TILE // BLOCK)
                q = wide_dot(x, weight(0), NN) + small[0:1, :]
                split(q_s, q_start, q.astype(jnp.bfloat16) * jnp.bfloat16(score_scale))
            split(k_s, start, wide_dot(x, weight(1), NN))
            split(v_s, start, wide_dot(x, weight(2), NN) + small[1:2, :])
            return carry

        lax.fori_loop(0, mid // TILE, one, 0)

    def own_project(a, carry):
        project(a, 2 * core + (a ^ bit), True)
        return carry

    def other_project(a, carry):
        project(2 + a, 2 * (1 - core) + (a ^ bit), False)
        return carry

    @pl.when(jnp.logical_not(stays))
    def left():
        x_moves[0].wait_send()

    x_moves[1].wait_send()
    take_cot = pltpu.make_async_copy(cot_hbm, given, own_sem.at[2])
    take_cot.start()
    lax.fori_loop(0, 2, own_project, 0)
    for copy in x_over:
        copy.wait_recv()
    outs.append(pltpu.make_async_copy(x_all, x_ref, out_sem.at[1]))
    outs[1].start()
    lax.fori_loop(0, 2, other_project, 0)
    take_cot.wait()
    xs[0] = given[bit].astype(jnp.bfloat16)
    xs[1] = given[1 - bit].astype(jnp.bfloat16)
    for i, (src, dst) in enumerate(((q_s, q_ref), (k_s, k_ref), (v_s, v_ref))):
        outs.append(pltpu.make_async_copy(src, dst, out_sem.at[2 + i]))
        outs[-1].start()

    last = nblocks - 1
    picks_each = table.shape[2]
    masks = head_masks(BLOCK)
    low_half = lax.broadcasted_iota(jnp.int32, (BLOCK, 2 * HEAD), 1) < HEAD
    each = 5
    subs = (local - 1) // each

    def attend_round(i, carry):
        g = i // subs
        sub = lax.rem(i, subs)
        qg, kg, vg = q_s.at[g], k_s.at[g], v_s.at[g]

        @pl.when(i == 4)
        def first_hook():
            relay(0)
            relay(1)

        @pl.when(i == 7)
        def second_hook():
            relay(2)

        @pl.when(sub == 0)
        def edge_block():
            edge = (local - 1) * core
            spread = spread_heads(rows_of(qg, edge), masks)
            span = 8 * BLOCK
            pieces = nblocks // 8
            top = None
            for n in range(pieces):
                scores = wide_dot(rows_of(kg, n * 8, 8), spread, NT)
                kept[n * span : (n + 1) * span, :] = scores
                high = jnp.max(scores, axis=0, keepdims=True)
                top = high if top is None else jnp.maximum(top, high)
            total_p = None
            for n in range(pieces):
                probs = jnp.exp(kept[n * span : (n + 1) * span, :] - top)
                kept[n * span : (n + 1) * span, :] = probs
                some = jnp.sum(probs, axis=0, keepdims=True)
                total_p = some if total_p is None else total_p + some
            scale = 1.0 / total_p
            full = None
            for n in range(pieces):
                probs = (kept[n * span : (n + 1) * span, :] * scale).astype(jnp.bfloat16)
                some = wide_dot(probs, rows_of(vg, n * 8, 8), TN)
                full = some if full is None else full + some
            at = pl.ds(pl.multiple_of(edge * BLOCK, BLOCK), BLOCK)
            ctx_s[g, at, :] = own_heads(full, masks).astype(jnp.bfloat16)
            lse_ref[g, pl.ds(edge, 1), :] = top + jnp.log(total_p)

        for u in range(each):
            spot = sub * each + u + 1 - core
            block = spot + local * core
            picks = [
                [table[g * PACK + h, block - 1, r] for h in range(PACK)]
                for r in range(picks_each)
            ]
            spread = spread_heads(rows_of(qg, spot), masks)
            keys = gathered(kg, block, last, picks, low_half)
            values = gathered(vg, block, last, picks, low_half)
            scores = middle_scores(keys, spread, block, last)
            top = jnp.max(scores, axis=0, keepdims=True)
            probs = jnp.exp(scores - top)
            total_p = jnp.sum(probs, axis=0, keepdims=True)
            probs = (probs * (1.0 / total_p)).astype(jnp.bfloat16)
            full = wide_dot(probs, values, TN)
            at = pl.ds(pl.multiple_of(spot * BLOCK, BLOCK), BLOCK)
            ctx_s[g, at, :] = own_heads(full, masks).astype(jnp.bfloat16)
            lse_ref[g, pl.ds(spot, 1), :] = top + jnp.log(total_p)
        return carry

    lax.fori_loop(0, groups * subs, attend_round, 0)
    for g in range(groups):
        outs.append(
            pltpu.make_async_copy(
                ctx_s.at[g], ctx_ref.at[:, g * lanes : (g + 1) * lanes], out_sem.at[5 + g]
            )
        )
        outs[-1].start()
    last_relay(0)
    last_relay(1)

    cot_moves = [send(xs.at[p], cot_ref.at[p], (y_s, y_r), p, goes[p]) for p in range(2)]
    cot_keep = pltpu.make_async_copy(xs.at[0], cot_ref.at[0], own_sem.at[1])

    for k in range(2):
        for group in passed[k]:
            for copy in group:
                copy.wait_recv()
    rest_own.wait()

    def keep_rest(part, first_m, last_m):
        span = slice(first_m, last_m)
        copy = pltpu.make_async_copy(
            rest_ref.at[:, span], rest_out.at[:, span], out_sem.at[5 + groups + part]
        )
        copy.start()
        outs.append(copy)

    keep_rest(0, 0, 2 * PER)
    tiles = 2 * mid // TILE
    per = mid // TILE

    def held_out(m):
        return rest_ref[:, m].reshape(width, width)

    def tile_out(i, slot):
        at = pl.ds(pl.multiple_of(i * TILE, TILE), TILE)
        return (
            pltpu.make_async_copy(n1_s.at[slot], n1_ref.at[at], tile_sem.at[slot]),
            pltpu.make_async_copy(gel_s.at[slot], gel_ref.at[:, at], tile_sem.at[2 + slot]),
        )

    def hid_out(i):
        at = pl.ds(pl.multiple_of(i * TILE, TILE), TILE)
        return pltpu.make_async_copy(hid_s.at[:, at], hid_ref.at[:, at], end_sem.at[2 * tiles + i])

    def rise_tile(i, carry):
        slot = lax.rem(i, 2)
        at = pl.ds(pl.multiple_of(i * TILE, TILE), TILE)
        inside = pl.ds(pl.multiple_of(lax.rem(i, per) * TILE, TILE), TILE)

        @pl.when(i == 1)
        def cross_cot():
            @pl.when(stays)
            def keep_cot():
                cot_keep.start()

            @pl.when(jnp.logical_not(stays))
            def leave_cot():
                cot_moves[0].start()

            cot_moves[1].start()

        @pl.when(i == 2)
        def late_relay():
            last_relay(2)

        @pl.when(i >= 2)
        def free():
            for copy in tile_out(i - 2, slot):
                copy.wait()

        context = jnp.concatenate([ctx_s[g, at, :] for g in range(groups)], axis=1)
        attn_out = wide_dot(context, held_out(0), NN) + small[2:3, :]
        x = x_all[(i // per) ^ bit, inside, :].astype(jnp.float32)
        n1, r1 = normed(x + attn_out)
        n1_s[slot] = n1
        r1_ref[at, :] = jnp.broadcast_to(r1, (TILE, r1_ref.shape[1]))
        after = n1 * small[3:4, :] + small[4:5, :]
        ffn_in = after.astype(jnp.bfloat16)
        fit_s[:, at] = ffn_in.T
        given[i // per, inside, :] = after + small[9:10, :]
        for b in range(4):
            up = wide_dot(ffn_in, held_out(1 + b), NN) + small[5 + b : 6 + b, :]
            square = up * up
            bent = jnp.tanh(gelu_root * up * (1.0 + gelu_cube * square))
            rise = 0.5 * (1.0 + bent)
            hid_s[b, at, :] = (up * rise).astype(jnp.bfloat16)
            slope = rise + (0.5 * gelu_root) * up * (1.0 - bent * bent) * (
                1.0 + (3.0 * gelu_cube) * square
            )
            gel_s[slot, b] = slope.astype(jnp.bfloat16)
        for copy in (*tile_out(i, slot), hid_out(i)):
            copy.start()
        return carry

    lax.fori_loop(0, tiles, rise_tile, 0)
    for i in range(tiles - 2, tiles):
        for copy in tile_out(i, i % 2):
            copy.wait()
    outs.append(pltpu.make_async_copy(fit_s, fit_ref, out_sem.at[7 + groups]))
    outs[-1].start()
    for group in passed[2]:
        for copy in group:
            copy.wait_recv()
    keep_rest(1, 2 * PER, 3 * PER)

    def end_out(i):
        at = pl.ds(pl.multiple_of(i * TILE, TILE), TILE)
        inside = pl.ds(pl.multiple_of(lax.rem(i, per) * TILE, TILE), TILE)
        chunk = i // per
        return (
            pltpu.make_async_copy(given.at[chunk, inside], n2_ref.at[at], end_sem.at[i]),
            pltpu.make_async_copy(
                layer_s.at[chunk ^ bit, inside],
                layer_ref.at[chunk ^ bit, inside],
                end_sem.at[tiles + i],
            ),
        )

    def fall_tile(i, carry):
        at = pl.ds(pl.multiple_of(i * TILE, TILE), TILE)
        inside = pl.ds(pl.multiple_of(lax.rem(i, per) * TILE, TILE), TILE)
        summed = given[i // per, inside, :]
        for b in range(4):
            summed = summed + wide_dot(hid_s[b, at, :], held_out(5 + b), NT)
        n2, r2 = normed(summed)
        layer_s[(i // per) ^ bit, inside, :] = (n2 * small[10:11, :] + small[11:12, :]).astype(
            jnp.bfloat16
        )
        given[i // per, inside, :] = n2
        r2_ref[at, :] = jnp.broadcast_to(r2, (TILE, r2_ref.shape[1]))
        for copy in end_out(i):
            copy.start()
        return carry

    lax.fori_loop(0, tiles, fall_tile, 0)
    for i in range(tiles):
        for copy in (*end_out(i), hid_out(i)):
            copy.wait()

    @pl.when(stays)
    def kept_cot():
        cot_keep.wait()

    @pl.when(jnp.logical_not(stays))
    def left_cot():
        cot_moves[0].wait()

    cot_moves[1].wait()
    for copy in (*x_over, *za, *zb, *q_moves, *qt_moves, *onward):
        copy.wait_send()
    for pair in direct:
        for copy in pair:
            copy.wait_send()
    for chunk in passed:
        for group in chunk:
            for copy in group:
                copy.wait_send()
    hops_sent()
    for copy in outs:
        copy.wait()


def begin(slots, local_at, table, master, small_in, inputs, cot, n_shard, n_ctx, n_tp):
    held, rows, width = master.shape
    _, mid, _ = inputs.shape
    groups = n_ctx * n_tp
    long = -(-(KINDS * rows + 16) // (16 * n_shard)) * 16 * n_shard
    lanes = PACK * HEAD
    packs = width // lanes
    tokens, seq = 2 * mid, 4 * mid
    anywhere = pl.BlockSpec(memory_space=pl.ANY)
    vmem = pl.BlockSpec(memory_space=pltpu.VMEM)
    smem = pl.BlockSpec(memory_space=pltpu.SMEM)
    dma = pltpu.SemaphoreType.DMA
    low = jnp.bfloat16
    f32 = jnp.float32
    pairs = [2, 2, n_shard - 1, n_shard - 1, n_shard - 1, n_shard - 1, 3]
    pairs += [4 * (n_tp - 1), 3 * CHUNKS, 4 * CHUNKS * (n_tp - 1), 2]
    return pl.pallas_call(
        functools.partial(begin_kernel, n_shard, n_ctx, n_tp),
        name="begin",
        in_specs=[smem, smem, smem, anywhere, vmem, anywhere, anywhere],
        out_specs=[anywhere] * 3
        + [vmem]
        + [anywhere] * 4
        + [vmem]
        + [anywhere] * 3
        + [vmem, anywhere, vmem]
        + [anywhere] * 3,
        out_shape=[
            bf16_of(4, mid, width),
            bf16_of(groups, long, width),
            bf16_of(groups, 9, rows, width),
            f32_of(16, width),
            bf16_of(packs, tokens // BLOCK, BLOCK, lanes),
            bf16_of(packs, seq // BLOCK, BLOCK, lanes),
            bf16_of(packs, seq // BLOCK, BLOCK, lanes),
            bf16_of(tokens, width),
            f32_of(packs, tokens // BLOCK, lanes),
            bf16_of(2, mid, width),
            bf16_of(2, mid, width),
            f32_of(tokens, width),
            f32_of(tokens, 128),
            f32_of(tokens, width),
            f32_of(tokens, 128),
            bf16_of(width, tokens),
            bf16_of(4, tokens, width),
            bf16_of(4, tokens, width),
        ],
        scratch_shapes=[
            pltpu.VMEM((held, rows, width), f32),
            pltpu.VMEM((held + 1, rows, width), low),
            pltpu.VMEM((2, mid, width), f32),
            pltpu.VMEM((2, mid, width), low),
            pltpu.VMEM((4, mid, width), low),
            pltpu.VMEM((long, width), low),
            pltpu.VMEM((n_shard - 1, long // n_shard, width), low),
            pltpu.VMEM((long // n_shard, width), low),
            pltpu.VMEM((long, width), low),
            pltpu.VMEM((n_shard * held, rows, width), low),
            pltpu.VMEM((9, rows, width), low),
            pltpu.VMEM((groups, long, width), low),
            pltpu.VMEM((groups, 9, rows, width), low),
            pltpu.VMEM((16, width), f32),
            pltpu.VMEM((packs, tokens // BLOCK, BLOCK, lanes), low),
            pltpu.VMEM((packs, seq // BLOCK, BLOCK, lanes), low),
            pltpu.VMEM((packs, seq // BLOCK, BLOCK, lanes), low),
            pltpu.VMEM((packs, tokens, lanes), low),
            pltpu.VMEM((seq, lanes), f32),
            pltpu.VMEM((2, TILE, width), f32),
            pltpu.VMEM((2, 4, TILE, width), low),
            pltpu.VMEM((4, tokens, width), low),
            pltpu.VMEM((width, tokens), low),
            pltpu.VMEM((2, mid, width), low),
            *[dma((n,)) for n in pairs for _ in range(2)],
            dma((4,)),
            dma((8 + packs,)),
            dma((4,)),
            dma((3 * (tokens // TILE),)),
        ],
        compiler_params=pltpu.CompilerParams(
            collective_id=0, has_side_effects=True, vmem_limit_bytes=64000 << 10
        ),
        cost_estimate=pl.CostEstimate(
            flops=60_000_000_000, bytes_accessed=60 << 20, transcendentals=16_000_000
        ),
    )(slots, local_at, table, master, small_in, inputs, cot)


NEAR = 3
CROSSINGS = -(-NEAR // 2)


def back_kernel(
    n_ctx,
    n_tp,
    n2_hbm,
    r2_ref,
    cots_ref,
    hid_ref,
    gel_ref,
    fit_ref,
    n1_ref,
    r1_ref,
    ctx_ref,
    small,
    up_w,
    down_w,
    wo,
    layer_ref,
    own_ref,
    near_ref,
    x_ref,
    y_ref,
    xy_ref,
    gh1_ref,
    dctx_ref,
    sums_ref,
    home_ref,
    gy,
    gu,
    mixed,
    mixed_t,
    grads,
    arrived,
    sums,
    send_sem,
    recv_sem,
    h_s,
    h_r,
    n_s,
    n_r,
    keep_sem,
    out_sem,
):
    z, c, t = place_of()
    step = pl.program_id(0)
    tokens, width = gy.shape
    tiles = tokens // TILE
    rows = grads.shape[4]
    others = n_tp - 1
    side, core, bit = t // 2, lax.rem(t, 2), lax.rem(c, 2)

    def beside(dt):
        return (z, c, lax.rem(t + dt, n_tp))

    stays = c // 2 == core
    keep_layer = pltpu.make_async_copy(layer_ref.at[0], home_ref.at[bit], keep_sem.at[0])
    layer_moves = [
        send(
            layer_ref.at[p],
            home_ref.at[bit],
            (h_s, h_r),
            p,
            (z, 2 * core + (p ^ bit), 2 * side + c // 2),
        )
        for p in range(2)
    ]

    @pl.when(step == 0)
    def start():
        take = pltpu.make_async_copy(n2_hbm, gy, keep_sem.at[1])
        take.start()
        barrier = pltpu.get_barrier_semaphore()
        friends = [beside(dt) for dt in range(1, n_tp)]
        friends += [(z, c ^ m, t) for m in range(1, n_ctx)]
        friends += [(z, c ^ m, t ^ 1) for m in range(1, n_ctx)]
        for friend in friends:
            pl.semaphore_signal(barrier, inc=1, device_id=friend, device_id_type=MESH)
        pl.semaphore_wait(barrier, len(friends))

        @pl.when(stays)
        def kept():
            keep_layer.start()

        @pl.when(jnp.logical_not(stays))
        def left():
            layer_moves[0].start()

        layer_moves[1].start()
        sums_ref[...] = jnp.zeros_like(sums_ref)
        take.wait()
        mid = tokens // 2
        for p in range(2):

            def one(i, carry, p=p):
                inside = pl.ds(pl.multiple_of(i * TILE, TILE), TILE)
                at = pl.ds(pl.multiple_of((p ^ bit) * mid + i * TILE, TILE), TILE)
                cot = cots_ref[p, inside, :].astype(jnp.float32)
                n2 = gy[at, :]
                add_row(sums_ref, 10, cot * n2)
                add_row(sums_ref, 11, cot)
                gh2 = norm_back(cot, n2, r2_ref[at, 0:1], small[10:11, :])
                gy[at, :] = gh2
                low = gh2.astype(jnp.bfloat16)
                mixed[at, :] = low
                mixed_t[:, at] = low.T
                add_row(sums_ref, 9, low.astype(jnp.float32))
                return carry

            lax.fori_loop(0, mid // TILE, one, 0)

    def moves(b, count):
        slot = lax.rem(b, 2)
        return [
            send(
                grads.at[slot, :, lax.rem(t + dt, n_tp), 0:count],
                arrived.at[b, dt - 1, :, 0:count],
                (send_sem, recv_sem),
                b * others + dt - 1,
                beside(dt),
            )
            for dt in range(1, n_tp)
        ]

    def exchange(b, count):
        for copy in moves(b, count):
            copy.start()

    def keep(b, count):
        for copy in moves(b, count):
            copy.wait()
        slot = lax.rem(b, 2)
        for j in range(n_ctx):
            for i in range(count):
                value = grads[slot, c ^ j, t, i]
                for dt in range(others):
                    value = value + arrived[b, dt, c ^ j, i]
                sums[j, 2 * b + i] = value

    def near(b):
        pair = slice(2 * b, min(2 * b + 2, NEAR))
        return [
            send(
                sums.at[j, pair],
                near_ref.at[j - 1, pair],
                (n_s, n_r),
                b * (n_ctx - 1) + j - 1,
                (z, c ^ j, t),
            )
            for j in range(1, n_ctx)
        ]

    def outward(part, first, count):
        moved = [
            pltpu.make_async_copy(
                sums.at[0, first : first + count],
                own_ref.at[first : first + count],
                out_sem.at[part * n_ctx],
            )
        ]
        begin_at = max(first, NEAR)
        count -= begin_at - first
        for j, out in enumerate((x_ref, y_ref, xy_ref)):
            moved.append(
                pltpu.make_async_copy(
                    sums.at[j + 1, begin_at : begin_at + count],
                    out.at[begin_at - NEAR : begin_at - NEAR + count],
                    out_sem.at[part * n_ctx + j + 1],
                )
            )
        return moved

    def put(slot, i, value):
        low = value.astype(jnp.bfloat16)
        grads[slot, :, :, i] = low.reshape(n_ctx, n_tp, rows, width)

    @pl.when(step < 4)
    def ffn():
        up_block = matrix(up_w)
        down_block = matrix(down_w)
        slot = lax.rem(step, 2)

        def one(i, carry):
            at = pl.ds(pl.multiple_of(i * MID, MID), MID)
            grad = wide_dot(mixed[at, :], down_block, NN) * gel_ref[0, at, :].astype(jnp.float32)
            low = grad.astype(jnp.bfloat16)
            gu[at, :] = low
            gy[at, :] += wide_dot(low, up_block, NT)
            sums_ref[pl.ds(5 + step, 1), :] += jnp.sum(
                low.astype(jnp.float32), axis=0, keepdims=True
            )
            return carry

        lax.fori_loop(0, tokens // MID, one, 0)
        put(slot, 0, wide_dot(fit_ref[...], gu[...], NN))
        put(slot, 1, wide_dot(mixed_t[...], hid_ref[0], NN))
        exchange(step, 2)

    @pl.when(step > 0)
    def settle():
        keep(step - 1, 2)

    for b in range(CROSSINGS):

        @pl.when(step == b + 1)
        def cross(b=b):
            for copy in near(b):
                copy.start()

    @pl.when(step == 4)
    def first_norm():
        for copy in outward(0, 0, 8):
            copy.start()

        def one(i, carry):
            at = pl.ds(pl.multiple_of(i * TILE, TILE), TILE)
            grad = gy[at, :]
            n1 = n1_ref[at, :]
            gh1 = norm_back(grad, n1, r1_ref[at, 0:1], small[3:4, :])
            gh1_ref[at, :] = gh1
            low = gh1.astype(jnp.bfloat16)
            gu[at, :] = low
            add_row(sums_ref, 2, low.astype(jnp.float32))
            add_row(sums_ref, 3, grad * n1)
            add_row(sums_ref, 4, grad)
            return carry

        lax.fori_loop(0, tiles, one, 0)
        put(0, 0, wide_dot(ctx_ref[...].T, gu[...], NN))
        exchange(4, 1)
        out_w = matrix(wo)

        def two(i, carry):
            at = pl.ds(pl.multiple_of(i * TILE, TILE), TILE)
            dctx_ref[at, :] = wide_dot(gu[at, :], out_w, NT).astype(jnp.bfloat16)
            return carry

        lax.fori_loop(0, tiles, two, 0)
        keep(4, 1)
        for copy in outward(1, 8, 1):
            copy.start()
        crossed = [copy for b in range(CROSSINGS) for copy in near(b)]
        for copy in (*crossed, *outward(0, 0, 8), *outward(1, 8, 1)):
            copy.wait()

        @pl.when(stays)
        def done():
            keep_layer.wait()

        @pl.when(jnp.logical_not(stays))
        def gone():
            layer_moves[0].wait()

        layer_moves[1].wait()


def back(n2, r2, cots, hid, gel, fit, n1, r1, ctx, small, rest, layer, n_ctx, n_tp):
    tokens, width = n2.shape
    rows = rest.shape[2]
    dma = pltpu.SemaphoreType.DMA

    def whole(shape):
        return pl.BlockSpec(shape, lambda b: (0,) * len(shape), pipeline_mode=pl.Buffered(1))

    def block(b):
        return (jnp.minimum(b, 3), 0, 0)

    def held(first, single=False):
        return pl.BlockSpec(
            (n_ctx * n_tp, 1, rows, width),
            (lambda b: (0, first, 0, 0))
            if single
            else (lambda b: (0, first + jnp.minimum(b, 3), 0, 0)),
            pipeline_mode=pl.Buffered(1) if single else None,
        )

    def out(shape):
        return pl.BlockSpec(shape, lambda b: (0,) * len(shape))

    return pl.pallas_call(
        functools.partial(back_kernel, n_ctx, n_tp),
        name="back",
        grid=(5,),
        in_specs=[
            pl.BlockSpec(memory_space=pl.ANY),
            whole((tokens, 128)),
            whole((2, tokens // 2, width)),
            pl.BlockSpec((1, tokens, width), block),
            pl.BlockSpec((1, tokens, width), block),
            whole((width, tokens)),
            whole((tokens, width)),
            whole((tokens, 128)),
            whole((tokens, width)),
            whole(small.shape),
            held(1),
            held(5),
            held(0, True),
            pl.BlockSpec(memory_space=pl.ANY),
        ],
        out_specs=[
            *[pl.BlockSpec(memory_space=pl.ANY)] * 5,
            out((tokens, width)),
            out((tokens, width)),
            out((16, width)),
            pl.BlockSpec(memory_space=pl.ANY),
        ],
        out_shape=[
            bf16_of(9, rows, width),
            bf16_of(n_ctx - 1, NEAR, rows, width),
            *[bf16_of(9 - NEAR, rows, width)] * 3,
            f32_of(tokens, width),
            bf16_of(tokens, width),
            f32_of(16, width),
            bf16_of(*layer.shape),
        ],
        scratch_shapes=[
            pltpu.VMEM((tokens, width), jnp.float32),
            pltpu.VMEM((tokens, width), jnp.bfloat16),
            pltpu.VMEM((tokens, width), jnp.bfloat16),
            pltpu.VMEM((width, tokens), jnp.bfloat16),
            pltpu.VMEM((2, n_ctx, n_tp, 2, rows, width), jnp.bfloat16),
            pltpu.VMEM((5, n_tp - 1, n_ctx, 2, rows, width), jnp.bfloat16),
            pltpu.VMEM((n_ctx, 9 + 1, rows, width), jnp.bfloat16),
            dma((5 * (n_tp - 1),)),
            dma((5 * (n_tp - 1),)),
            dma((2,)),
            dma((2,)),
            dma((CROSSINGS * (n_ctx - 1),)),
            dma((CROSSINGS * (n_ctx - 1),)),
            dma((2,)),
            dma((2 * n_ctx,)),
        ],
        compiler_params=pltpu.CompilerParams(
            collective_id=3, has_side_effects=True, vmem_limit_bytes=62 << 20
        ),
        cost_estimate=pl.CostEstimate(
            flops=22_000_000_000, bytes_accessed=40 << 20, transcendentals=0
        ),
    )(n2, r2, cots, hid, gel, fit, n1, r1, ctx, small, rest, rest, rest, layer)


LATE = 3
EARLY = 9


def adam_update(weight, first, second, grad, decay, rate):
    count = float(STEP)
    first_new = beta_one * first + (1.0 - beta_one) * grad
    second_new = beta_two * second + (1.0 - beta_two) * grad * grad
    first_hat = first_new / (1.0 - beta_one**count)
    second_hat = second_new / (1.0 - beta_two**count)
    weight_new = weight - rate * (first_hat / (jnp.sqrt(second_hat) + adam_eps) + decay * weight)
    return (weight_new, first_new, second_new)


def finish_kernel(
    n_shard,
    n_ctx,
    n_tp,
    holder,
    late_at,
    x_hbm,
    dq_hbm,
    dk_hbm,
    dv_hbm,
    gh1_hbm,
    first_hbm,
    e0_hbm,
    near_hbm,
    e1_hbm,
    e2_hbm,
    e3_hbm,
    small_ref,
    home_ref,
    grad_out,
    small_out,
    x_s,
    dq_s,
    dk_s,
    dv_s,
    gh1_s,
    first_s,
    early,
    every,
    packed,
    right_met,
    left_met,
    flipped,
    grads,
    arrived,
    partial,
    met,
    over,
    more,
    back_s,
    small_s,
    small_t,
    small_m,
    small_p,
    flat_a,
    met_a,
    sum_a,
    mine_a,
    flat_b,
    met_b,
    sum_b,
    mine_b,
    pool,
    in_sem,
    c_s,
    c_r,
    p_s,
    p_r,
    o_s,
    o_r,
    h_s,
    h_r,
    sc_s,
    sc_r,
    sp_s,
    sp_r,
    e_s,
    e_r,
    l_s,
    l_r,
    a_s,
    a_r,
    b_s,
    b_r,
    d_s,
    d_r,
    f_s,
    f_r,
    keep_sem,
):
    z, c, t = place_of()
    side, core, bit = t // 2, lax.rem(t, 2), lax.rem(c, 2)
    _, mid, width = x_s.shape
    tokens = 2 * mid
    held, rows, _ = grad_out.shape
    per = n_ctx * n_tp // 2
    band = width // 2
    tile = mid

    loads = [
        pltpu.make_async_copy(src, dst, in_sem.at[i])
        for i, (src, dst) in enumerate(
            (
                (x_hbm, x_s),
                (dk_hbm, dk_s),
                (dv_hbm, dv_s),
                (dq_hbm, dq_s),
                (first_hbm, first_s),
                (gh1_hbm, gh1_s),
                (e0_hbm, early.at[0]),
                (near_hbm, early.at[1:4, 0:NEAR]),
                (e1_hbm, early.at[1, NEAR:EARLY]),
                (e2_hbm, early.at[2, NEAR:EARLY]),
                (e3_hbm, early.at[3, NEAR:EARLY]),
            )
        )
    ]
    for i in (6, 7, 8, 9, 10, 0, 1, 2, 3, 4, 5):
        loads[i].start()

    def far(dz):
        return (lax.rem(z + dz, n_shard), c, t)

    def across(mask):
        return (z, c ^ mask, t)

    def beside(dt):
        return (z, c, lax.rem(t + dt, n_tp))

    barrier = pltpu.get_barrier_semaphore()
    friends = [far(dz) for dz in range(1, n_shard)]
    friends += [(z, c ^ m, t) for m in range(1, n_ctx)]
    friends += [beside(dt) for dt in range(1, n_tp)]
    friends += [(z, c ^ m, t ^ 1) for m in range(1, n_ctx)]
    for friend in friends:
        pl.semaphore_signal(barrier, inc=1, device_id=friend, device_id_type=MESH)

    for i in range(6, 11):
        loads[i].wait()
    every[0:EARLY] = early[0] + early[1] + early[2] + early[3]
    every[EARLY] = jnp.zeros_like(every[EARLY])
    for s in range(n_shard * held):
        packed[s // held, s % held] = every[holder[s]]
    pl.semaphore_wait(barrier, len(friends))

    def run(owner_at, s, way):
        met, sems = (right_met, (e_s, e_r)) if way > 0 else (left_met, (l_s, l_r))
        target = (lax.rem(z + way + n_shard, n_shard), c, t)
        return send(packed.at[owner_at], met.at[s], sems, s, target)

    def each_run(hop):
        for s in range(hop + 1):
            for way in (1, -1):
                place = hop - s if way > 0 else n_shard - 1 - (hop - s)
                owner_at = n_shard - 1 - s if way > 0 else s
                yield s, way, place, owner_at

    def hop(h):
        for s, way, place, owner_at in each_run(h):

            @pl.when(z == place)
            def move(s=s, way=way, place=place, owner_at=owner_at):
                copy = run(owner_at, s, way)
                if h > s:
                    copy.wait_recv()
                    met = right_met if way > 0 else left_met
                    for j in range(held):
                        packed[owner_at, j] = packed[owner_at, j] + met[s, j]
                copy.start()

    def hops_end():
        for h in range(n_shard - 1):
            for s, way, place, owner_at in each_run(h):

                @pl.when(z == place)
                def sent(s=s, way=way, owner_at=owner_at):
                    run(owner_at, s, way).wait_send()

        for s in range(n_shard - 1):
            for way in (1, -1):
                owner_at = n_shard - 1 - s if way > 0 else s

                @pl.when(z == owner_at)
                def last(s=s, way=way, owner_at=owner_at):
                    run(owner_at, s, way).wait_recv()
                    met = right_met if way > 0 else left_met
                    for j in range(held):
                        packed[owner_at, j] = packed[owner_at, j] + met[s, j]

    hop(0)

    core_moves = []

    def exchange(m):
        for dt in range(1, n_tp):
            other = lax.rem(t + dt, n_tp)
            for k in range(n_ctx):
                copy = send(
                    grads.at[k * n_tp + other, m],
                    arrived.at[dt - 1, k, m],
                    (c_s, c_r),
                    ((dt - 1) * n_ctx + k) * LATE + m,
                    beside(dt),
                )
                copy.start()
                core_moves.append((m, copy))

    plane_moves = []

    def meet(m):
        for which, copy in core_moves:
            if which == m:
                copy.wait_recv()
        for k in range(n_ctx):
            value = grads[k * n_tp + t, m]
            for dt in range(1, n_tp):
                value = value + arrived[dt - 1, k, m]
            partial[k, m] = value
        for j in range(1, n_ctx):
            copy = send(
                partial.at[c ^ j, m], met.at[j - 1, m], (p_s, p_r), (j - 1) * LATE + m, across(j)
            )
            copy.start()
            plane_moves.append((m, copy))

    loads[0].wait()
    for a in range(4):
        chunk = 2 * (core if a < 2 else 1 - core) + ((a % 2) ^ bit)
        flipped[:, pl.ds(pl.multiple_of(chunk * mid, mid), mid)] = x_s[a].T

    def weight_grad(m, left_at, right):
        def one(i, carry):
            left = flipped[pl.ds(pl.multiple_of(i * band, band), band), left_at]
            value = wide_dot(left, right[...], NN).astype(jnp.bfloat16)
            grads[pl.ds(i * per, per), m] = value.reshape(per, rows, width)
            return carry

        lax.fori_loop(0, 2, one, 0)

    loads[1].wait()
    weight_grad(1, slice(None), dk_s)
    exchange(1)
    loads[2].wait()
    weight_grad(2, slice(None), dv_s)
    exchange(2)
    meet(1)
    for h in range(1, n_shard - 2):
        hop(h)
    loads[3].wait()
    weight_grad(0, pl.ds(pl.multiple_of(core * tokens, tokens), tokens), dq_s)
    exchange(0)
    meet(2)

    row = lax.broadcasted_iota(jnp.int32, small_ref.shape, 0)
    q_sum = jnp.sum(dq_s[...].astype(jnp.float32), axis=0, keepdims=True)
    v_sum = jnp.sum(dv_s[...].astype(jnp.float32), axis=0, keepdims=True)
    sums = jnp.where(row == 0, q_sum, jnp.where(row == 1, v_sum, small_ref[...]))
    small_s[...] = sums.astype(jnp.bfloat16)
    small_core = [
        send(small_s, small_t.at[dt - 1], (sc_s, sc_r), dt - 1, beside(dt)) for dt in range(1, n_tp)
    ]
    for copy in small_core:
        copy.start()

    loads[4].wait()

    def weight(m):
        return first_s[:, m * rows : (m + 1) * rows, :].reshape(width, width)

    wq, wk, wv = weight(0), weight(1), weight(2)
    over_moves = []
    for b in range(2):
        at = pl.ds(pl.multiple_of((1 - core) * tokens + b * mid, mid), mid)
        value = wide_dot(dk_s[at, :], wk, NT) + wide_dot(dv_s[at, :], wv, NT)
        over[b] = value.astype(jnp.bfloat16)
        copy = send(over.at[b], more.at[b], (o_s, o_r), b, (z, c, t ^ 1))
        copy.start()
        over_moves.append(copy)
        if b == 0:
            meet(0)
            if n_shard > 2:
                hop(n_shard - 2)

    value = small_s[...]
    for dt, copy in enumerate(small_core):
        copy.wait_recv()
        value = value + small_t[dt]
    small_m[...] = value
    small_plane = [
        send(small_m, small_p.at[j - 1], (sp_s, sp_r), j - 1, across(j)) for j in range(1, n_ctx)
    ]
    for copy in small_plane:
        copy.start()

    loads[5].wait()
    stays = c // 2 == core
    home_moves = []
    for copy in over_moves:
        copy.wait_recv()
    keep = pltpu.make_async_copy(back_s.at[0], home_ref.at[bit], keep_sem.at[0])
    for move in range(2):
        chunk = move ^ bit
        for i in range(mid // tile):
            at = pl.ds(pl.multiple_of(core * tokens + chunk * mid + i * tile, tile), tile)
            here = pl.ds(pl.multiple_of(chunk * mid + i * tile, tile), tile)
            value = gh1_s[here, :]
            value = value + more[chunk, i * tile : (i + 1) * tile, :].astype(jnp.float32)
            value = value + wide_dot(dq_s[here, :], wq, NT)
            value = value + wide_dot(dk_s[at, :], wk, NT)
            value = value + wide_dot(dv_s[at, :], wv, NT)
            back_s[move, i * tile : (i + 1) * tile, :] = value.astype(jnp.bfloat16)
        target = (z, 2 * core + chunk, 2 * side + c // 2)
        home_moves.append(send(back_s.at[move], home_ref.at[bit], (h_s, h_r), move, target))
        if move == 0:

            @pl.when(stays)
            def kept():
                keep.start()

            @pl.when(jnp.logical_not(stays))
            def left():
                home_moves[0].start()

        else:
            home_moves[1].start()

    def gathered_rows(m):
        for which, copy in plane_moves:
            if which == m:
                copy.wait_recv()
        value = partial[c, m]
        for j in range(n_ctx - 1):
            value = value + met[j, m]
        return value

    def piece_at(ref, k):
        piece = ref.shape[0] // n_shard
        return pl.ds(pl.multiple_of(k * piece, piece), piece)

    def scatter_lot(flat, lot_met, sems):
        moves = [
            send(flat.at[piece_at(flat, far(dz)[0])], lot_met.at[dz - 1], sems, dz - 1, far(dz))
            for dz in range(1, n_shard)
        ]
        for copy in moves:
            copy.start()
        return moves

    def spread_lot(moves, flat, lot_met, lot_sum, lot_mine, sems):
        total = flat[piece_at(flat, z), :].astype(jnp.float32)
        for dz, copy in enumerate(moves):
            copy.wait_recv()
            total = total + lot_met[dz].astype(jnp.float32)
        lot_mine[...] = total.astype(jnp.bfloat16)
        spreads = [
            send(lot_mine, lot_sum.at[piece_at(flat, z)], sems, dz - 1, far(dz))
            for dz in range(1, n_shard)
        ]
        for copy in spreads:
            copy.start()
        lot_sum[piece_at(flat, z), :] = lot_mine[...]
        return spreads

    small_rows = small_s.shape[0]
    flat_a[...] = jnp.zeros_like(flat_a)
    flat_b[...] = jnp.zeros_like(flat_b)
    flat_a[0:rows, :] = gathered_rows(1)
    flat_a[rows : 2 * rows, :] = gathered_rows(2)
    scatter_a = scatter_lot(flat_a, met_a, (a_s, a_r))
    flat_b[0:rows, :] = gathered_rows(0)
    value = small_m[...]
    for j, copy in enumerate(small_plane):
        copy.wait_recv()
        value = value + small_p[j]
    flat_b[rows : rows + small_rows, :] = value
    scatter_b = scatter_lot(flat_b, met_b, (b_s, b_r))
    spread_a = spread_lot(scatter_a, flat_a, met_a, sum_a, mine_a, (d_s, d_r))
    spread_b = spread_lot(scatter_b, flat_b, met_b, sum_b, mine_b, (f_s, f_r))
    hops_end()
    for copy in (*spread_a, *spread_b):
        copy.wait_recv()
    pool[0] = sum_b[0:rows, :]
    pool[1] = sum_a[0:rows, :]
    pool[2] = sum_a[rows : 2 * rows, :]
    pool[LATE] = jnp.zeros_like(pool[LATE])
    for j in range(held):
        grad = packed[z, j].astype(jnp.float32)
        grad = grad + pool[late_at[z * held + j]].astype(jnp.float32)
        grad_out[j] = grad
    small_out[...] = sum_b[rows : rows + small_rows, :].astype(jnp.float32)

    @pl.when(stays)
    def done():
        keep.wait()

    @pl.when(jnp.logical_not(stays))
    def gone():
        home_moves[0].wait()

    home_moves[1].wait()
    for _, copy in (*core_moves, *plane_moves):
        copy.wait_send()
    for copy in (
        *over_moves,
        *small_core,
        *small_plane,
        *scatter_a,
        *scatter_b,
        *spread_a,
        *spread_b,
    ):
        copy.wait_send()


def finish(
    holder,
    late_at,
    x_all,
    dq,
    dk,
    dv,
    gh1,
    first,
    early,
    small,
    held,
    n_shard,
    n_ctx,
    n_tp,
):
    _, mid, width = x_all.shape
    rows = width // (n_ctx * n_tp)
    groups = n_ctx * n_tp
    span = 16 * n_shard
    long_a = -(-2 * rows // span) * span
    long_b = -(-(rows + small.shape[0]) // span) * span
    smem = pl.BlockSpec(memory_space=pltpu.SMEM)
    anywhere = pl.BlockSpec(memory_space=pl.ANY)
    vmem = pl.BlockSpec(memory_space=pltpu.VMEM)
    dma = pltpu.SemaphoreType.DMA
    low = jnp.bfloat16
    pairs = [LATE * n_ctx * (n_tp - 1), LATE * (n_ctx - 1), 2, 2, n_tp - 1, n_ctx - 1]
    pairs += [n_shard - 1] * 6
    shapes = [
        x_all.shape,
        dq.shape,
        dk.shape,
        dv.shape,
        None,
        first.shape,
        (4, EARLY, rows, width),
        (EARLY + 1, rows, width),
        (n_shard, held, rows, width),
        (n_shard - 1, held, rows, width),
        (n_shard - 1, held, rows, width),
        (width, 4 * mid),
        (groups, LATE, rows, width),
        (n_tp - 1, n_ctx, LATE, rows, width),
        (n_ctx, LATE, rows, width),
        (n_ctx - 1, LATE, rows, width),
        (2, mid, width),
        (2, mid, width),
        (2, mid, width),
        small.shape,
        (n_tp - 1, *small.shape),
        small.shape,
        (n_ctx - 1, *small.shape),
        *[
            shape
            for long in (long_a, long_b)
            for shape in (
                (long, width),
                (n_shard - 1, long // n_shard, width),
                (long, width),
                (long // n_shard, width),
            )
        ],
        (LATE + 1, rows, width),
    ]
    return pl.pallas_call(
        functools.partial(finish_kernel, n_shard, n_ctx, n_tp),
        name="finish",
        in_specs=[smem] * 2 + [anywhere] * 11 + [vmem],
        out_specs=[vmem] * 3,
        out_shape=[bf16_of(2, mid, width), f32_of(held, rows, width), f32_of(*small.shape)],
        scratch_shapes=[
            pltpu.VMEM(s, low) if s else pltpu.VMEM(gh1.shape, jnp.float32) for s in shapes
        ]
        + [dma((11,))]
        + [dma((n,)) for n in pairs for _ in range(2)]
        + [dma((1,))],
        compiler_params=pltpu.CompilerParams(
            collective_id=1, has_side_effects=True, vmem_limit_bytes=63 << 20
        ),
        cost_estimate=pl.CostEstimate(
            flops=12_000_000_000, bytes_accessed=40 << 20, transcendentals=0
        ),
    )(holder, late_at, x_all, dq, dk, dv, gh1, first, *early, small)


def shards(
    inputs,
    cotangent,
    rand_blocks,
    slot_of,
    master,
    moment_one,
    moment_two,
    small_params,
    small_one,
    small_two,
):
    n_shard = lax.axis_size("shard")
    n_ctx = lax.axis_size("ctx")
    n_tp = lax.axis_size("tp")
    groups = n_ctx * n_tp
    held, rows, width = master.shape
    span = small_params.shape[0]
    my_ctx = lax.axis_index("ctx")
    my_tp = lax.axis_index("tp")
    half = lax.rem(my_tp, 2)
    plane = ("ctx", "tp")

    half_one = half.astype(jnp.int32).reshape(1)
    my_shard = lax.axis_index("shard")
    start = ((my_shard * n_ctx + my_ctx) * n_tp + my_tp) * span
    lone = lax.dynamic_update_slice(
        jnp.zeros((16 * width,), jnp.float32), small_params, (start,)
    ).reshape(16, width)
    local_at = slot_of[:LATE] - my_shard * held
    local_at = jnp.where((local_at >= 0) & (local_at < held), local_at, held)
    begun = begin(
        slot_of,
        local_at,
        rand_blocks,
        master,
        lone,
        inputs,
        cotangent,
        n_shard,
        n_ctx,
        n_tp,
    )
    x_all, first, rest, small, q, k, v, context, lse = begun[:9]
    cots, out_low, n1, r1, n2, r2, fit, hid, gel = begun[9:]
    *early, gh1, dctx, sums, layer_home = back(
        n2, r2, cots, hid, gel, fit, n1, r1, context, small, rest, out_low, n_ctx, n_tp
    )
    for j in range(1, n_ctx):
        crossing = [
            (a * n_tp + b, (a ^ j) * n_tp + b) for a in range(n_ctx) for b in range(n_tp)
        ]
        early[j + 1] = lax.ppermute(early[j + 1], plane, crossing)
    dq, dk, dv, layer_out = attend_back(
        half_one, rand_blocks, q, k, v, lse, dctx, layer_home, 15
    )
    stands = jnp.array([8, 0, 2, 4, 6, 1, 3, 5, 7], jnp.int32)
    slots_all = jnp.arange(n_shard * held, dtype=jnp.int32)
    hits = slot_of[None, :] == slots_all[:, None]
    holder = EARLY + jnp.sum(jnp.where(hits[:, LATE:], stands[None, :] - EARLY, 0), axis=1)
    ranks = jnp.arange(LATE, dtype=jnp.int32)[None, :]
    late_at = LATE + jnp.sum(jnp.where(hits[:, :LATE], ranks - LATE, 0), axis=1)
    came, slot_grads, small_sum = finish(
        holder.astype(jnp.int32),
        late_at.astype(jnp.int32),
        x_all,
        dq,
        dk,
        dv,
        gh1,
        first,
        early,
        sums,
        held,
        n_shard,
        n_ctx,
        n_tp,
    )
    input_grad = came.astype(jnp.float32)
    master_new, first_new, second_new = adam_update(
        master, moment_one, moment_two, slot_grads, 0.01, rate_value
    )
    rows_held = -(-span // width) + 1
    first_row = jnp.minimum(start // width, small_sum.shape[0] - rows_held)
    near_rows = lax.dynamic_slice_in_dim(small_sum, first_row, rows_held).reshape(-1)
    small_owned = lax.dynamic_slice_in_dim(near_rows, start - first_row * width, span)
    small_new, small_first, small_second = adam_update(
        small_params, small_one, small_two, small_owned, 0.0, small_rate
    )
    return (
        layer_out,
        input_grad,
        master_new,
        first_new,
        second_new,
        small_new,
        small_first,
        small_second,
    )


def solution(mesh):
    tokens = P(("shard", "tp"), "ctx", None)
    stored = P("shard", ("ctx", "tp"), None)
    spread = P(("shard", "ctx", "tp"))
    return jax.shard_map(
        shards,
        mesh=mesh,
        in_specs=(tokens, tokens, P(), P(), stored, stored, stored, spread, spread, spread),
        out_specs=(tokens, tokens, stored, stored, stored, spread, spread, spread),
        check_vma=False,
    )
```

```python
import functools

import jax
import jax.numpy as jnp
from jax import lax
from jax.experimental import pallas as pl
from jax.experimental.pallas import tpu as pltpu
from jax.sharding import PartitionSpec as P

STEP = 5
norm_eps = 1e-12
beta_one = 0.9
beta_two = 0.999
adam_eps = 1e-08
rate_value = 0.04
small_rate = 0.25
score_scale = 0.125
gelu_root = 0.7978845608
gelu_cube = 0.044715

BLOCK = 64
HEAD = 64
PACK = 4
masked_score = -1e30
open_score = 3e38


def wide_dot(a, b, dims):
    return lax.dot_general(a, b, (dims, ((), ())), preferred_element_type=jnp.float32)


def head_masks(rows):
    lane = lax.broadcasted_iota(jnp.int32, (rows, PACK * HEAD), 1) // HEAD
    return [lane == h for h in range(PACK)]


def spread_heads(block, masks):
    zero = jnp.zeros_like(block)
    return jnp.concatenate([jnp.where(m, block, zero) for m in masks], axis=0)


def own_heads(full, masks):
    total = None
    for h, m in enumerate(masks):
        piece = jnp.where(m, full[h * BLOCK : (h + 1) * BLOCK], 0.0)
        total = piece if total is None else total + piece
    return total


def rows_of(ref, index, count=1):
    return ref[pl.ds(index, count)].reshape(count * BLOCK, ref.shape[2])


def flat_rows(ref, index):
    return ref[pl.ds(pl.multiple_of(index * BLOCK, BLOCK), BLOCK), :]


def picked_rows(ref, picks, low_half):
    halves = []
    for pair in range(PACK // 2):
        cols = slice(pair * 2 * HEAD, (pair + 1) * 2 * HEAD)
        first = ref[picks[2 * pair], :, cols]
        second = ref[picks[2 * pair + 1], :, cols]
        halves.append(jnp.where(low_half, first, second))
    return jnp.concatenate(halves, axis=1)


def gathered(ref, block, last, picks, low_half):
    pieces = [rows_of(ref, 0), rows_of(ref, last), rows_of(ref, block - 1, 3)]
    pieces += [picked_rows(ref, p, low_half) for p in picks]
    return jnp.concatenate(pieces, axis=0)


def middle_scores(keys, spread, block, last):
    scores = wide_dot(keys, spread, ((1,), (1,)))
    first_cap = jnp.where(block == 1, masked_score, open_score)
    last_cap = jnp.where(block == last - 1, masked_score, open_score)
    b = BLOCK
    return jnp.concatenate(
        [
            scores[: 2 * b],
            jnp.minimum(scores[2 * b : 3 * b], first_cap),
            scores[3 * b : 4 * b],
            jnp.minimum(scores[4 * b : 5 * b], last_cap),
            scores[5 * b :],
        ],
        axis=0,
    )


def attend_back_kernel(
    unroll,
    half_ref,
    table_ref,
    q_ref,
    k_ref,
    v_ref,
    lse_ref,
    do_ref,
    layer_ref,
    dq_ref,
    dk_ref,
    dv_ref,
    wide_ref,
    dk_acc,
    dv_acc,
    kept_p,
    kept_g,
):
    wide_ref[...] = layer_ref[...].astype(jnp.float32)
    half = half_ref[0]
    group = pl.program_id(0)
    q_ref, k_ref, v_ref = q_ref.at[0], k_ref.at[0], v_ref.at[0]
    nblocks, local = k_ref.shape[0], q_ref.shape[0]
    last = nblocks - 1
    picks_each = table_ref.shape[2]
    masks = head_masks(BLOCK)
    low_half = lax.broadcasted_iota(jnp.int32, (BLOCK, 2 * HEAD), 1) < HEAD
    span = 8 * BLOCK
    chunks = nblocks // 8

    edge = (local - 1) * half
    spread = spread_heads(rows_of(q_ref, edge), masks)
    spread_do = spread_heads(flat_rows(do_ref, edge), masks)
    lse = lse_ref[0, pl.ds(edge, 1), :]
    delta = None
    for c in range(chunks):
        rows = slice(c * span, (c + 1) * span)
        probs = jnp.exp(wide_dot(rows_of(k_ref, c * 8, 8), spread, ((1,), (1,))) - lse)
        gp = wide_dot(rows_of(v_ref, c * 8, 8), spread_do, ((1,), (1,)))
        kept_p[rows, :] = probs
        kept_g[rows, :] = gp
        part = jnp.sum(probs * gp, axis=0, keepdims=True)
        delta = part if delta is None else delta + part
    full = None
    for c in range(chunks):
        rows = slice(c * span, (c + 1) * span)
        probs = kept_p[rows, :]
        ds = (probs * (kept_g[rows, :] - delta)).astype(jnp.bfloat16)
        dv_acc[rows, :] = wide_dot(probs.astype(jnp.bfloat16), spread_do, ((1,), (0,)))
        dk_acc[rows, :] = wide_dot(ds, spread, ((1,), (0,)))
        part = wide_dot(ds, rows_of(k_ref, c * 8, 8), ((0,), (0,)))
        full = part if full is None else full + part
    dq_ref[pl.ds(pl.multiple_of(edge * BLOCK, BLOCK), BLOCK), :] = (
        own_heads(full, masks) * 0.125
    ).astype(jnp.bfloat16)

    def scatter(acc, piece, block, picks):
        b = BLOCK
        acc[0:b, :] += piece[:b]
        acc[last * b : (last + 1) * b, :] += piece[b : 2 * b]
        window = pl.ds(pl.multiple_of((block - 1) * b, b), 3 * b)
        acc[window, :] += piece[2 * b : 5 * b]
        for r, p in enumerate(picks):
            part = piece[(5 + r) * b : (6 + r) * b]
            for pair in range(PACK // 2):
                lanes = slice(pair * 2 * HEAD, (pair + 1) * 2 * HEAD)
                cols = pl.ds(pair * 2 * HEAD, 2 * HEAD)
                sub = part[:, lanes]
                acc[pl.ds(pl.multiple_of(p[2 * pair] * b, b), b), cols] += jnp.where(
                    low_half, sub, 0.0
                )
                acc[pl.ds(pl.multiple_of(p[2 * pair + 1] * b, b), b), cols] += jnp.where(
                    low_half, 0.0, sub
                )

    def middle(step, carry):
        mine = step + 1 - half
        block = mine + local * half
        picks = [
            [table_ref[group * PACK + h, block - 1, r] for h in range(PACK)]
            for r in range(picks_each)
        ]
        spread = spread_heads(rows_of(q_ref, mine), masks)
        spread_do = spread_heads(flat_rows(do_ref, mine), masks)
        keys = gathered(k_ref, block, last, picks, low_half)
        values = gathered(v_ref, block, last, picks, low_half)
        scores = middle_scores(keys, spread, block, last)
        probs = jnp.exp(scores - lse_ref[0, pl.ds(mine, 1), :])
        gp = wide_dot(values, spread_do, ((1,), (1,)))
        delta = jnp.sum(probs * gp, axis=0, keepdims=True)
        ds = (probs * (gp - delta)).astype(jnp.bfloat16)
        low = probs.astype(jnp.bfloat16)
        scatter(dv_acc, wide_dot(low, spread_do, ((1,), (0,))), block, picks)
        scatter(dk_acc, wide_dot(ds, spread, ((1,), (0,))), block, picks)
        full = wide_dot(ds, keys, ((0,), (0,)))
        dq_ref[pl.ds(pl.multiple_of(mine * BLOCK, BLOCK), BLOCK), :] = (
            own_heads(full, masks) * 0.125
        ).astype(jnp.bfloat16)
        return carry

    lax.fori_loop(0, local - 1, middle, 0, unroll=unroll)
    dk_ref[...] = dk_acc[...].astype(jnp.bfloat16)
    dv_ref[...] = dv_acc[...].astype(jnp.bfloat16)


def attend_back(half, table, q, k, v, lse, do, layer, unroll=3):
    tokens, width = do.shape
    groups, nblocks, _, lanes = k.shape
    seq = nblocks * BLOCK
    blocks = tokens // BLOCK
    mine = pl.BlockSpec((tokens, lanes), lambda g, *_: (0, g))
    whole = pl.BlockSpec((seq, lanes), lambda g, *_: (0, g))
    spec = pltpu.PrefetchScalarGridSpec(
        num_scalar_prefetch=2,
        grid=(groups,),
        in_specs=[
            pl.BlockSpec((1, blocks, BLOCK, lanes), lambda g, *_: (g, 0, 0, 0)),
            pl.BlockSpec((1, nblocks, BLOCK, lanes), lambda g, *_: (g, 0, 0, 0)),
            pl.BlockSpec((1, nblocks, BLOCK, lanes), lambda g, *_: (g, 0, 0, 0)),
            pl.BlockSpec((1, blocks, lanes), lambda g, *_: (g, 0, 0)),
            mine,
            pl.BlockSpec((*layer.shape[:2], lanes), lambda g, *_: (0, 0, g)),
        ],
        out_specs=[
            mine,
            whole,
            whole,
            pl.BlockSpec((*layer.shape[:2], lanes), lambda g, *_: (0, 0, g)),
        ],
        scratch_shapes=[pltpu.VMEM((seq, lanes), jnp.float32)] * 4,
    )
    return pl.pallas_call(
        functools.partial(attend_back_kernel, unroll),
        grid_spec=spec,
        out_shape=[
            jax.ShapeDtypeStruct((tokens, width), jnp.bfloat16),
            jax.ShapeDtypeStruct((seq, width), jnp.bfloat16),
            jax.ShapeDtypeStruct((seq, width), jnp.bfloat16),
            jax.ShapeDtypeStruct(layer.shape, jnp.float32),
        ],
        name="attend_back",
        compiler_params=pltpu.CompilerParams(vmem_limit_bytes=56 << 20),
        cost_estimate=pl.CostEstimate(
            flops=120_000_000_000, bytes_accessed=24 << 20, transcendentals=16_000_000
        ),
    )(half, table, q, k, v, lse, do, layer)


TILE = 256
MID = 512


def cols_mean(value):
    return jnp.mean(value, axis=-1, keepdims=True)


def normed(field):
    centred = field - cols_mean(field)
    rate = lax.rsqrt(cols_mean(centred * centred) + norm_eps)
    return centred * rate, rate


def norm_back(cot, normal, rate, gain):
    dn = cot * gain
    return rate * (dn - cols_mean(dn) - normal * cols_mean(dn * normal))


def matrix(ref):
    value = ref[...]
    return value.reshape(-1, value.shape[-1])


def add_row(ref, row, value):
    ref[row : row + 1, :] += jnp.sum(value, axis=0, keepdims=True)


def bf16_of(*shape):
    return jax.ShapeDtypeStruct(shape, jnp.bfloat16)


def f32_of(*shape):
    return jax.ShapeDtypeStruct(shape, jnp.float32)


NN = ((1,), (0,))
NT = ((1,), (1,))
TN = ((0,), (0,))


MESH = pl.DeviceIdType.MESH
KINDS = 3
CHUNKS = 3
PER = 3


def place_of():
    c, t = lax.axis_index("ctx"), lax.axis_index("tp")
    return lax.axis_index("shard"), c, t


def send(src, dst, sems, index, target):
    send_sems, recv_sems = sems
    return pltpu.make_async_remote_copy(
        src_ref=src,
        dst_ref=dst,
        send_sem=send_sems.at[index],
        recv_sem=recv_sems.at[index],
        device_id=target,
        device_id_type=MESH,
    )


def begin_kernel(
    n_shard,
    n_ctx,
    n_tp,
    slots,
    table,
    master_hbm,
    small_in,
    input_hbm,
    cot_hbm,
    x_ref,
    first_ref,
    rest_out,
    small_ref,
    q_ref,
    k_ref,
    v_ref,
    ctx_ref,
    lse_ref,
    cot_ref,
    layer_ref,
    n1_ref,
    r1_ref,
    n2_ref,
    r2_ref,
    fit_ref,
    hid_ref,
    gel_ref,
    raw,
    low,
    given,
    xs,
    x_all,
    part,
    got,
    mine,
    total,
    pool,
    sel,
    first,
    rest_ref,
    small,
    q_s,
    k_s,
    v_s,
    ctx_s,
    kept,
    n1_s,
    gel_s,
    hid_s,
    fit_s,
    layer_s,
    x_s,
    x_r,
    xt_s,
    xt_r,
    za_s,
    za_r,
    zb_s,
    zb_r,
    zc_s,
    zc_r,
    zd_s,
    zd_r,
    qm_s,
    qm_r,
    qt_s,
    qt_r,
    r_s,
    r_r,
    rt_s,
    rt_r,
    y_s,
    y_r,
    own_sem,
    out_sem,
    tile_sem,
    end_sem,
):
    z, c, t = place_of()
    side, core, bit = t // 2, lax.rem(t, 2), lax.rem(c, 2)
    held, rows, width = low.shape[0] - 1, low.shape[1], low.shape[2]
    piece = mine.shape[0]
    me = c * n_tp + t
    _, mid, _ = xs.shape
    nblocks = 4 * mid // BLOCK
    local = nblocks // 2
    lanes = PACK * HEAD
    groups = width // lanes
    others = n_tp - 1

    take_raw = pltpu.make_async_copy(master_hbm, raw, own_sem.at[0])
    take_given = pltpu.make_async_copy(input_hbm, given, own_sem.at[1])
    take_raw.start()
    take_given.start()

    def far(dz):
        return (lax.rem(z + dz, n_shard), c, t)

    def across(mask):
        return (z, c ^ mask, t)

    def beside(dt):
        return (z, c, lax.rem(t + dt, n_tp))

    barrier = pltpu.get_barrier_semaphore()
    friends = [far(dz) for dz in range(1, n_shard)]
    friends += [(z, c ^ m, t) for m in range(1, n_ctx)]
    friends += [beside(dt) for dt in range(1, n_tp)]
    friends += [(z, c ^ m, t ^ 1) for m in range(1, n_ctx)]
    for friend in friends:
        pl.semaphore_signal(barrier, inc=1, device_id=friend, device_id_type=MESH)

    take_raw.wait()
    for j in range(held):
        low[j] = raw[j].astype(jnp.bfloat16)
    low[held] = jnp.zeros_like(low[held])
    pool[pl.ds(z * held, held)] = low[0:held]
    part[...] = jnp.zeros_like(part)
    for m in range(KINDS):
        place = slots[m] - z * held
        mine_too = (place >= 0) & (place < held)
        part[m * rows : (m + 1) * rows, :] = low[jnp.where(mine_too, place, held)]
    part[KINDS * rows : KINDS * rows + 16, :] = small_in[...].astype(jnp.bfloat16)
    pl.semaphore_wait(barrier, len(friends))

    def piece_at(k):
        return pl.ds(pl.multiple_of(k * piece, piece), piece)

    def hop_copy(s, way):
        sems = (zc_s, zc_r) if way > 0 else (zd_s, zd_r)
        slot = pl.ds((z - way * (s - 1)) * held, held)
        return send(
            pool.at[slot], pool.at[slot], sems, s - 1, (lax.rem(z + way + n_shard, n_shard), c, t)
        )

    def hop_on(s, way):
        start = z - way * (s - 1)
        end = z + way
        return (start >= 0) & (start < n_shard) & (end >= 0) & (end < n_shard)

    def hop(s):
        for way in (1, -1):

            @pl.when(hop_on(s, way))
            def move(way=way):
                if s > 1:
                    hop_copy(s - 1, way).wait_recv()
                hop_copy(s, way).start()

    za = [
        send(part.at[piece_at(far(dz)[0])], got.at[dz - 1], (za_s, za_r), dz - 1, far(dz))
        for dz in range(1, n_shard)
    ]
    for copy in za:
        copy.start()

    stays = c // 2 == core
    goes = [(z, 2 * core + (p ^ bit), 2 * side + c // 2) for p in range(2)]
    x_moves = [send(xs.at[p], x_all.at[p], (x_s, x_r), p, goes[p]) for p in range(2)]
    x_keep = pltpu.make_async_copy(xs.at[0], x_all.at[0], own_sem.at[2])
    take_given.wait()
    xs[0] = given[bit].astype(jnp.bfloat16)

    @pl.when(stays)
    def keep():
        x_keep.start()

    @pl.when(jnp.logical_not(stays))
    def leave():
        x_moves[0].start()

    xs[1] = given[1 - bit].astype(jnp.bfloat16)
    x_moves[1].start()

    summed = part[piece_at(z), :]
    for dz, copy in enumerate(za):
        copy.wait_recv()
        summed = summed + got[dz]
    mine[...] = summed
    zb = [
        send(mine, total.at[piece_at(z)], (zb_s, zb_r), dz - 1, far(dz))
        for dz in range(1, n_shard)
    ]
    for copy in zb:
        copy.start()
    total[piece_at(z), :] = summed
    def hops_end():
        for way, end in ((1, n_shard - 1), (-1, 0)):

            @pl.when(z == end)
            def gather(way=way):
                for s in range(1, n_shard):
                    hop_copy(s, way).wait_recv()

    def hops_sent():
        for s in range(1, n_shard):
            for way in (1, -1):

                @pl.when(hop_on(s, way))
                def sent(s=s, way=way):
                    hop_copy(s, way).wait_send()

    for copy in zb:
        copy.wait_recv()
    hop(1)

    q_moves = [
        send(total, first.at[me], (qm_s, qm_r), k, across(m)) for k, m in enumerate((1, 2, 3))
    ]
    for copy in q_moves:
        copy.start()
    qt_moves = [
        send(total, first.at[me], (qt_s, qt_r), dt - 1, beside(dt)) for dt in range(1, n_tp)
    ]
    for copy in qt_moves:
        copy.start()
    first[me] = total[...]

    x_over = [
        send(x_all.at[p], x_all.at[2 + p], (xt_s, xt_r), p, (z, c, t ^ 1)) for p in range(2)
    ]

    @pl.when(stays)
    def stayed():
        x_keep.wait()

    @pl.when(jnp.logical_not(stays))
    def came():
        x_moves[0].wait_recv()

    x_over[0].start()
    x_moves[1].wait_recv()
    x_over[1].start()
    for s in range(2, n_shard):
        hop(s)

    for k, m in enumerate((1, 2, 3)):
        q_moves[k].wait_recv()
        place = (c ^ m) * n_tp + t
        for dt in range(1, n_tp):
            copy = send(
                first.at[place],
                first.at[place],
                (qt_s, qt_r),
                (k + 1) * others + dt - 1,
                beside(dt),
            )
            copy.start()
            qt_moves.append(copy)
    for copy in qt_moves:
        copy.wait_recv()
    def span_of(k):
        return pl.ds(k * PER, PER)

    rest_own = pltpu.make_async_copy(sel, rest_ref.at[me], own_sem.at[3])
    direct = [
        [
            send(
                sel.at[span_of(k)], rest_ref.at[me, span_of(k)], (r_s, r_r), k * 3 + j, across(m)
            )
            for j, m in enumerate((1, 2))
        ]
        for k in range(CHUNKS)
    ]
    onward = []
    for k in range(CHUNKS):
        odd = lax.rem(core + k, 2)
        source = jnp.where(odd == 0, c ^ 1, c ^ 2) * n_tp + t
        target = (z, jnp.where(odd == 0, c ^ 2, c ^ 1), t)
        view = rest_ref.at[source, span_of(k)]
        onward.append(send(view, view, (r_s, r_r), k * 3 + 2, target))

    def passing(k, which):
        if which == 0:
            src = sel.at[span_of(k)]
        else:
            src = rest_ref.at[(c ^ which) * n_tp + t, span_of(k)]
        dst = rest_ref.at[(c ^ which) * n_tp + t, span_of(k)]
        return [
            send(src, dst, (rt_s, rt_r), (k * 4 + which) * others + dt - 1, beside(dt))
            for dt in range(1, n_tp)
        ]

    passed = [[passing(k, which) for which in range(4)] for k in range(CHUNKS)]

    def begin_rest():
        hops_end()
        for m in range(CHUNKS * PER):
            sel[m] = pool[slots[KINDS + m]]
        rest_own.start()
        launch(0)
        launch(1)
        launch(2)

    def launch(k):
        for copy in (*direct[k], *passed[k][0]):
            copy.start()

    def relay(k):
        for copy in direct[k]:
            copy.wait_recv()
        onward[k].start()
        for copy in passed[k][1] + passed[k][2]:
            copy.start()

    def last_relay(k):
        onward[k].wait_recv()
        for copy in passed[k][3]:
            copy.start()

    begin_rest()
    outs = [pltpu.make_async_copy(first, first_ref, out_sem.at[0])]
    outs[0].start()

    sums = None
    for g in range(n_ctx * n_tp):
        here = first[g, KINDS * rows : KINDS * rows + 16, :].astype(jnp.float32)
        sums = here if sums is None else sums + here
    small[...] = sums
    small_ref[...] = sums
    def weight(m):
        return first[:, m * rows : (m + 1) * rows, :].reshape(width, width)

    def split(dst, start, value):
        low_value = value.astype(jnp.bfloat16)
        per = TILE // BLOCK
        for g in range(groups):
            piece_value = low_value[:, g * lanes : (g + 1) * lanes]
            dst[g, pl.ds(start, per)] = piece_value.reshape(per, BLOCK, lanes)

    def project(a, chunk, own):
        def one(i, carry):
            x = x_all[a, pl.ds(pl.multiple_of(i * TILE, TILE), TILE), :]
            start = chunk * (mid // BLOCK) + i * (TILE // BLOCK)
            if own:
                q_start = (chunk - 2 * core) * (mid // BLOCK) + i * (TILE // BLOCK)
                q = wide_dot(x, weight(0), NN) + small[0:1, :]
                split(q_s, q_start, q.astype(jnp.bfloat16) * jnp.bfloat16(score_scale))
            split(k_s, start, wide_dot(x, weight(1), NN))
            split(v_s, start, wide_dot(x, weight(2), NN) + small[1:2, :])
            return carry

        lax.fori_loop(0, mid // TILE, one, 0)

    def own_project(a, carry):
        project(a, 2 * core + (a ^ bit), True)
        return carry

    def other_project(a, carry):
        project(2 + a, 2 * (1 - core) + (a ^ bit), False)
        return carry

    @pl.when(jnp.logical_not(stays))
    def left():
        x_moves[0].wait_send()

    x_moves[1].wait_send()
    take_cot = pltpu.make_async_copy(cot_hbm, given, own_sem.at[2])
    take_cot.start()
    lax.fori_loop(0, 2, own_project, 0)
    for copy in x_over:
        copy.wait_recv()
    outs.append(pltpu.make_async_copy(x_all, x_ref, out_sem.at[1]))
    outs[1].start()
    lax.fori_loop(0, 2, other_project, 0)
    take_cot.wait()
    xs[0] = given[bit].astype(jnp.bfloat16)
    xs[1] = given[1 - bit].astype(jnp.bfloat16)
    for i, (src, dst) in enumerate(((q_s, q_ref), (k_s, k_ref), (v_s, v_ref))):
        outs.append(pltpu.make_async_copy(src, dst, out_sem.at[2 + i]))
        outs[-1].start()

    last = nblocks - 1
    picks_each = table.shape[2]
    masks = head_masks(BLOCK)
    low_half = lax.broadcasted_iota(jnp.int32, (BLOCK, 2 * HEAD), 1) < HEAD
    each = 5
    subs = (local - 1) // each

    def attend_round(i, carry):
        g = i // subs
        sub = lax.rem(i, subs)
        qg, kg, vg = q_s.at[g], k_s.at[g], v_s.at[g]

        @pl.when(i == 4)
        def first_hook():
            relay(0)
            relay(1)

        @pl.when(i == 7)
        def second_hook():
            relay(2)

        @pl.when(sub == 0)
        def edge_block():
            edge = (local - 1) * core
            spread = spread_heads(rows_of(qg, edge), masks)
            span = 8 * BLOCK
            pieces = nblocks // 8
            top = None
            for n in range(pieces):
                scores = wide_dot(rows_of(kg, n * 8, 8), spread, NT)
                kept[n * span : (n + 1) * span, :] = scores
                high = jnp.max(scores, axis=0, keepdims=True)
                top = high if top is None else jnp.maximum(top, high)
            total_p = None
            for n in range(pieces):
                probs = jnp.exp(kept[n * span : (n + 1) * span, :] - top)
                kept[n * span : (n + 1) * span, :] = probs
                some = jnp.sum(probs, axis=0, keepdims=True)
                total_p = some if total_p is None else total_p + some
            scale = 1.0 / total_p
            full = None
            for n in range(pieces):
                probs = (kept[n * span : (n + 1) * span, :] * scale).astype(jnp.bfloat16)
                some = wide_dot(probs, rows_of(vg, n * 8, 8), TN)
                full = some if full is None else full + some
            at = pl.ds(pl.multiple_of(edge * BLOCK, BLOCK), BLOCK)
            ctx_s[g, at, :] = own_heads(full, masks).astype(jnp.bfloat16)
            lse_ref[g, pl.ds(edge, 1), :] = top + jnp.log(total_p)

        for u in range(each):
            spot = sub * each + u + 1 - core
            block = spot + local * core
            picks = [
                [table[g * PACK + h, block - 1, r] for h in range(PACK)]
                for r in range(picks_each)
            ]
            spread = spread_heads(rows_of(qg, spot), masks)
            keys = gathered(kg, block, last, picks, low_half)
            values = gathered(vg, block, last, picks, low_half)
            scores = middle_scores(keys, spread, block, last)
            top = jnp.max(scores, axis=0, keepdims=True)
            probs = jnp.exp(scores - top)
            total_p = jnp.sum(probs, axis=0, keepdims=True)
            probs = (probs * (1.0 / total_p)).astype(jnp.bfloat16)
            full = wide_dot(probs, values, TN)
            at = pl.ds(pl.multiple_of(spot * BLOCK, BLOCK), BLOCK)
            ctx_s[g, at, :] = own_heads(full, masks).astype(jnp.bfloat16)
            lse_ref[g, pl.ds(spot, 1), :] = top + jnp.log(total_p)
        return carry

    lax.fori_loop(0, groups * subs, attend_round, 0)
    for g in range(groups):
        outs.append(
            pltpu.make_async_copy(
                ctx_s.at[g], ctx_ref.at[:, g * lanes : (g + 1) * lanes], out_sem.at[5 + g]
            )
        )
        outs[-1].start()
    last_relay(0)
    last_relay(1)

    cot_moves = [send(xs.at[p], cot_ref.at[p], (y_s, y_r), p, goes[p]) for p in range(2)]
    cot_keep = pltpu.make_async_copy(xs.at[0], cot_ref.at[0], own_sem.at[1])

    for k in range(2):
        for group in passed[k]:
            for copy in group:
                copy.wait_recv()
    rest_own.wait()

    def keep_rest(part, first_m, last_m):
        span = slice(first_m, last_m)
        copy = pltpu.make_async_copy(
            rest_ref.at[:, span], rest_out.at[:, span], out_sem.at[5 + groups + part]
        )
        copy.start()
        outs.append(copy)

    keep_rest(0, 0, 2 * PER)
    tiles = 2 * mid // TILE
    per = mid // TILE

    def held_out(m):
        return rest_ref[:, m].reshape(width, width)

    def tile_out(i, slot):
        at = pl.ds(pl.multiple_of(i * TILE, TILE), TILE)
        return (
            pltpu.make_async_copy(n1_s.at[slot], n1_ref.at[at], tile_sem.at[slot]),
            pltpu.make_async_copy(gel_s.at[slot], gel_ref.at[:, at], tile_sem.at[2 + slot]),
        )

    def hid_out(i):
        at = pl.ds(pl.multiple_of(i * TILE, TILE), TILE)
        return pltpu.make_async_copy(hid_s.at[:, at], hid_ref.at[:, at], end_sem.at[2 * tiles + i])

    def rise_tile(i, carry):
        slot = lax.rem(i, 2)
        at = pl.ds(pl.multiple_of(i * TILE, TILE), TILE)
        inside = pl.ds(pl.multiple_of(lax.rem(i, per) * TILE, TILE), TILE)

        @pl.when(i == 1)
        def cross_cot():
            @pl.when(stays)
            def keep_cot():
                cot_keep.start()

            @pl.when(jnp.logical_not(stays))
            def leave_cot():
                cot_moves[0].start()

            cot_moves[1].start()

        @pl.when(i == 2)
        def late_relay():
            last_relay(2)

        @pl.when(i >= 2)
        def free():
            for copy in tile_out(i - 2, slot):
                copy.wait()

        context = jnp.concatenate([ctx_s[g, at, :] for g in range(groups)], axis=1)
        attn_out = wide_dot(context, held_out(0), NN) + small[2:3, :]
        x = x_all[(i // per) ^ bit, inside, :].astype(jnp.float32)
        n1, r1 = normed(x + attn_out)
        n1_s[slot] = n1
        r1_ref[at, :] = jnp.broadcast_to(r1, (TILE, r1_ref.shape[1]))
        after = n1 * small[3:4, :] + small[4:5, :]
        ffn_in = after.astype(jnp.bfloat16)
        fit_s[:, at] = ffn_in.T
        given[i // per, inside, :] = after + small[9:10, :]
        for b in range(4):
            up = wide_dot(ffn_in, held_out(1 + b), NN) + small[5 + b : 6 + b, :]
            square = up * up
            bent = jnp.tanh(gelu_root * up * (1.0 + gelu_cube * square))
            rise = 0.5 * (1.0 + bent)
            hid_s[b, at, :] = (up * rise).astype(jnp.bfloat16)
            slope = rise + (0.5 * gelu_root) * up * (1.0 - bent * bent) * (
                1.0 + (3.0 * gelu_cube) * square
            )
            gel_s[slot, b] = slope.astype(jnp.bfloat16)
        for copy in (*tile_out(i, slot), hid_out(i)):
            copy.start()
        return carry

    lax.fori_loop(0, tiles, rise_tile, 0)
    for i in range(tiles - 2, tiles):
        for copy in tile_out(i, i % 2):
            copy.wait()
    outs.append(pltpu.make_async_copy(fit_s, fit_ref, out_sem.at[7 + groups]))
    outs[-1].start()
    for group in passed[2]:
        for copy in group:
            copy.wait_recv()
    keep_rest(1, 2 * PER, 3 * PER)

    def end_out(i):
        at = pl.ds(pl.multiple_of(i * TILE, TILE), TILE)
        inside = pl.ds(pl.multiple_of(lax.rem(i, per) * TILE, TILE), TILE)
        chunk = i // per
        return (
            pltpu.make_async_copy(given.at[chunk, inside], n2_ref.at[at], end_sem.at[i]),
            pltpu.make_async_copy(
                layer_s.at[chunk ^ bit, inside],
                layer_ref.at[chunk ^ bit, inside],
                end_sem.at[tiles + i],
            ),
        )

    def fall_tile(i, carry):
        at = pl.ds(pl.multiple_of(i * TILE, TILE), TILE)
        inside = pl.ds(pl.multiple_of(lax.rem(i, per) * TILE, TILE), TILE)
        summed = given[i // per, inside, :]
        for b in range(4):
            summed = summed + wide_dot(hid_s[b, at, :], held_out(5 + b), NT)
        n2, r2 = normed(summed)
        layer_s[(i // per) ^ bit, inside, :] = (n2 * small[10:11, :] + small[11:12, :]).astype(
            jnp.bfloat16
        )
        given[i // per, inside, :] = n2
        r2_ref[at, :] = jnp.broadcast_to(r2, (TILE, r2_ref.shape[1]))
        for copy in end_out(i):
            copy.start()
        return carry

    lax.fori_loop(0, tiles, fall_tile, 0)
    for i in range(tiles):
        for copy in (*end_out(i), hid_out(i)):
            copy.wait()

    @pl.when(stays)
    def kept_cot():
        cot_keep.wait()

    @pl.when(jnp.logical_not(stays))
    def left_cot():
        cot_moves[0].wait()

    cot_moves[1].wait()
    for copy in (*x_over, *za, *zb, *q_moves, *qt_moves, *onward):
        copy.wait_send()
    for pair in direct:
        for copy in pair:
            copy.wait_send()
    for chunk in passed:
        for group in chunk:
            for copy in group:
                copy.wait_send()
    hops_sent()
    for copy in outs:
        copy.wait()


def begin(slots, table, master, small_in, inputs, cot, n_shard, n_ctx, n_tp):
    held, rows, width = master.shape
    _, mid, _ = inputs.shape
    groups = n_ctx * n_tp
    long = -(-(KINDS * rows + 16) // (16 * n_shard)) * 16 * n_shard
    lanes = PACK * HEAD
    packs = width // lanes
    tokens, seq = 2 * mid, 4 * mid
    anywhere = pl.BlockSpec(memory_space=pl.ANY)
    vmem = pl.BlockSpec(memory_space=pltpu.VMEM)
    smem = pl.BlockSpec(memory_space=pltpu.SMEM)
    dma = pltpu.SemaphoreType.DMA
    low = jnp.bfloat16
    f32 = jnp.float32
    pairs = [2, 2, n_shard - 1, n_shard - 1, n_shard - 1, n_shard - 1, 3]
    pairs += [4 * (n_tp - 1), 3 * CHUNKS, 4 * CHUNKS * (n_tp - 1), 2]
    return pl.pallas_call(
        functools.partial(begin_kernel, n_shard, n_ctx, n_tp),
        name="begin",
        in_specs=[smem, smem, anywhere, vmem, anywhere, anywhere],
        out_specs=[anywhere] * 3
        + [vmem]
        + [anywhere] * 4
        + [vmem]
        + [anywhere] * 3
        + [vmem, anywhere, vmem]
        + [anywhere] * 3,
        out_shape=[
            bf16_of(4, mid, width),
            bf16_of(groups, long, width),
            bf16_of(groups, 9, rows, width),
            f32_of(16, width),
            bf16_of(packs, tokens // BLOCK, BLOCK, lanes),
            bf16_of(packs, seq // BLOCK, BLOCK, lanes),
            bf16_of(packs, seq // BLOCK, BLOCK, lanes),
            bf16_of(tokens, width),
            f32_of(packs, tokens // BLOCK, lanes),
            bf16_of(2, mid, width),
            bf16_of(2, mid, width),
            f32_of(tokens, width),
            f32_of(tokens, 128),
            f32_of(tokens, width),
            f32_of(tokens, 128),
            bf16_of(width, tokens),
            bf16_of(4, tokens, width),
            bf16_of(4, tokens, width),
        ],
        scratch_shapes=[
            pltpu.VMEM((held, rows, width), f32),
            pltpu.VMEM((held + 1, rows, width), low),
            pltpu.VMEM((2, mid, width), f32),
            pltpu.VMEM((2, mid, width), low),
            pltpu.VMEM((4, mid, width), low),
            pltpu.VMEM((long, width), low),
            pltpu.VMEM((n_shard - 1, long // n_shard, width), low),
            pltpu.VMEM((long // n_shard, width), low),
            pltpu.VMEM((long, width), low),
            pltpu.VMEM((n_shard * held, rows, width), low),
            pltpu.VMEM((9, rows, width), low),
            pltpu.VMEM((groups, long, width), low),
            pltpu.VMEM((groups, 9, rows, width), low),
            pltpu.VMEM((16, width), f32),
            pltpu.VMEM((packs, tokens // BLOCK, BLOCK, lanes), low),
            pltpu.VMEM((packs, seq // BLOCK, BLOCK, lanes), low),
            pltpu.VMEM((packs, seq // BLOCK, BLOCK, lanes), low),
            pltpu.VMEM((packs, tokens, lanes), low),
            pltpu.VMEM((seq, lanes), f32),
            pltpu.VMEM((2, TILE, width), f32),
            pltpu.VMEM((2, 4, TILE, width), low),
            pltpu.VMEM((4, tokens, width), low),
            pltpu.VMEM((width, tokens), low),
            pltpu.VMEM((2, mid, width), low),
            *[dma((n,)) for n in pairs for _ in range(2)],
            dma((4,)),
            dma((8 + packs,)),
            dma((4,)),
            dma((3 * (tokens // TILE),)),
        ],
        compiler_params=pltpu.CompilerParams(
            collective_id=0, has_side_effects=True, vmem_limit_bytes=64000 << 10
        ),
        cost_estimate=pl.CostEstimate(
            flops=60_000_000_000, bytes_accessed=60 << 20, transcendentals=16_000_000
        ),
    )(slots, table, master, small_in, inputs, cot)


NEAR = 3
CROSSINGS = -(-NEAR // 2)


def back_kernel(
    n_ctx,
    n_tp,
    n2_hbm,
    r2_ref,
    cots_ref,
    hid_ref,
    gel_ref,
    fit_ref,
    n1_ref,
    r1_ref,
    ctx_ref,
    small,
    up_w,
    down_w,
    wo,
    layer_ref,
    own_ref,
    near_ref,
    x_ref,
    y_ref,
    xy_ref,
    gh1_ref,
    dctx_ref,
    sums_ref,
    home_ref,
    gy,
    gu,
    mixed,
    mixed_t,
    grads,
    arrived,
    sums,
    send_sem,
    recv_sem,
    h_s,
    h_r,
    n_s,
    n_r,
    keep_sem,
    out_sem,
):
    z, c, t = place_of()
    step = pl.program_id(0)
    tokens, width = gy.shape
    tiles = tokens // TILE
    rows = grads.shape[4]
    others = n_tp - 1
    side, core, bit = t // 2, lax.rem(t, 2), lax.rem(c, 2)

    def beside(dt):
        return (z, c, lax.rem(t + dt, n_tp))

    stays = c // 2 == core
    keep_layer = pltpu.make_async_copy(layer_ref.at[0], home_ref.at[bit], keep_sem.at[0])
    layer_moves = [
        send(
            layer_ref.at[p],
            home_ref.at[bit],
            (h_s, h_r),
            p,
            (z, 2 * core + (p ^ bit), 2 * side + c // 2),
        )
        for p in range(2)
    ]

    @pl.when(step == 0)
    def start():
        take = pltpu.make_async_copy(n2_hbm, gy, keep_sem.at[1])
        take.start()
        barrier = pltpu.get_barrier_semaphore()
        friends = [beside(dt) for dt in range(1, n_tp)]
        friends += [(z, c ^ m, t) for m in range(1, n_ctx)]
        friends += [(z, c ^ m, t ^ 1) for m in range(1, n_ctx)]
        for friend in friends:
            pl.semaphore_signal(barrier, inc=1, device_id=friend, device_id_type=MESH)
        pl.semaphore_wait(barrier, len(friends))

        @pl.when(stays)
        def kept():
            keep_layer.start()

        @pl.when(jnp.logical_not(stays))
        def left():
            layer_moves[0].start()

        layer_moves[1].start()
        sums_ref[...] = jnp.zeros_like(sums_ref)
        take.wait()
        mid = tokens // 2
        for p in range(2):

            def one(i, carry, p=p):
                inside = pl.ds(pl.multiple_of(i * TILE, TILE), TILE)
                at = pl.ds(pl.multiple_of((p ^ bit) * mid + i * TILE, TILE), TILE)
                cot = cots_ref[p, inside, :].astype(jnp.float32)
                n2 = gy[at, :]
                add_row(sums_ref, 10, cot * n2)
                add_row(sums_ref, 11, cot)
                gh2 = norm_back(cot, n2, r2_ref[at, 0:1], small[10:11, :])
                gy[at, :] = gh2
                low = gh2.astype(jnp.bfloat16)
                mixed[at, :] = low
                mixed_t[:, at] = low.T
                add_row(sums_ref, 9, low.astype(jnp.float32))
                return carry

            lax.fori_loop(0, mid // TILE, one, 0)

    def moves(b, count):
        slot = lax.rem(b, 2)
        return [
            send(
                grads.at[slot, :, lax.rem(t + dt, n_tp), 0:count],
                arrived.at[b, dt - 1, :, 0:count],
                (send_sem, recv_sem),
                b * others + dt - 1,
                beside(dt),
            )
            for dt in range(1, n_tp)
        ]

    def exchange(b, count):
        for copy in moves(b, count):
            copy.start()

    def keep(b, count):
        for copy in moves(b, count):
            copy.wait()
        slot = lax.rem(b, 2)
        for j in range(n_ctx):
            for i in range(count):
                value = grads[slot, c ^ j, t, i]
                for dt in range(others):
                    value = value + arrived[b, dt, c ^ j, i]
                sums[j, 2 * b + i] = value

    def near(b):
        pair = slice(2 * b, min(2 * b + 2, NEAR))
        return [
            send(
                sums.at[j, pair],
                near_ref.at[j - 1, pair],
                (n_s, n_r),
                b * (n_ctx - 1) + j - 1,
                (z, c ^ j, t),
            )
            for j in range(1, n_ctx)
        ]

    def outward(part, first, count):
        moved = [
            pltpu.make_async_copy(
                sums.at[0, first : first + count],
                own_ref.at[first : first + count],
                out_sem.at[part * n_ctx],
            )
        ]
        begin_at = max(first, NEAR)
        count -= begin_at - first
        for j, out in enumerate((x_ref, y_ref, xy_ref)):
            moved.append(
                pltpu.make_async_copy(
                    sums.at[j + 1, begin_at : begin_at + count],
                    out.at[begin_at - NEAR : begin_at - NEAR + count],
                    out_sem.at[part * n_ctx + j + 1],
                )
            )
        return moved

    def put(slot, i, value):
        low = value.astype(jnp.bfloat16)
        grads[slot, :, :, i] = low.reshape(n_ctx, n_tp, rows, width)

    @pl.when(step < 4)
    def ffn():
        up_block = matrix(up_w)
        down_block = matrix(down_w)
        slot = lax.rem(step, 2)

        def one(i, carry):
            at = pl.ds(pl.multiple_of(i * MID, MID), MID)
            grad = wide_dot(mixed[at, :], down_block, NN) * gel_ref[0, at, :].astype(jnp.float32)
            low = grad.astype(jnp.bfloat16)
            gu[at, :] = low
            gy[at, :] += wide_dot(low, up_block, NT)
            sums_ref[pl.ds(5 + step, 1), :] += jnp.sum(
                low.astype(jnp.float32), axis=0, keepdims=True
            )
            return carry

        lax.fori_loop(0, tokens // MID, one, 0)
        put(slot, 0, wide_dot(fit_ref[...], gu[...], NN))
        put(slot, 1, wide_dot(mixed_t[...], hid_ref[0], NN))
        exchange(step, 2)

    @pl.when(step > 0)
    def settle():
        keep(step - 1, 2)

    for b in range(CROSSINGS):

        @pl.when(step == b + 1)
        def cross(b=b):
            for copy in near(b):
                copy.start()

    @pl.when(step == 4)
    def first_norm():
        for copy in outward(0, 0, 8):
            copy.start()

        def one(i, carry):
            at = pl.ds(pl.multiple_of(i * TILE, TILE), TILE)
            grad = gy[at, :]
            n1 = n1_ref[at, :]
            gh1 = norm_back(grad, n1, r1_ref[at, 0:1], small[3:4, :])
            gh1_ref[at, :] = gh1
            low = gh1.astype(jnp.bfloat16)
            gu[at, :] = low
            add_row(sums_ref, 2, low.astype(jnp.float32))
            add_row(sums_ref, 3, grad * n1)
            add_row(sums_ref, 4, grad)
            return carry

        lax.fori_loop(0, tiles, one, 0)
        put(0, 0, wide_dot(ctx_ref[...].T, gu[...], NN))
        exchange(4, 1)
        out_w = matrix(wo)

        def two(i, carry):
            at = pl.ds(pl.multiple_of(i * TILE, TILE), TILE)
            dctx_ref[at, :] = wide_dot(gu[at, :], out_w, NT).astype(jnp.bfloat16)
            return carry

        lax.fori_loop(0, tiles, two, 0)
        keep(4, 1)
        for copy in outward(1, 8, 1):
            copy.start()
        crossed = [copy for b in range(CROSSINGS) for copy in near(b)]
        for copy in (*crossed, *outward(0, 0, 8), *outward(1, 8, 1)):
            copy.wait()

        @pl.when(stays)
        def done():
            keep_layer.wait()

        @pl.when(jnp.logical_not(stays))
        def gone():
            layer_moves[0].wait()

        layer_moves[1].wait()


def back(n2, r2, cots, hid, gel, fit, n1, r1, ctx, small, rest, layer, n_ctx, n_tp):
    tokens, width = n2.shape
    rows = rest.shape[2]
    dma = pltpu.SemaphoreType.DMA

    def whole(shape):
        return pl.BlockSpec(shape, lambda b: (0,) * len(shape), pipeline_mode=pl.Buffered(1))

    def block(b):
        return (jnp.minimum(b, 3), 0, 0)

    def held(first, single=False):
        return pl.BlockSpec(
            (n_ctx * n_tp, 1, rows, width),
            (lambda b: (0, first, 0, 0))
            if single
            else (lambda b: (0, first + jnp.minimum(b, 3), 0, 0)),
            pipeline_mode=pl.Buffered(1) if single else None,
        )

    def out(shape):
        return pl.BlockSpec(shape, lambda b: (0,) * len(shape))

    return pl.pallas_call(
        functools.partial(back_kernel, n_ctx, n_tp),
        name="back",
        grid=(5,),
        in_specs=[
            pl.BlockSpec(memory_space=pl.ANY),
            whole((tokens, 128)),
            whole((2, tokens // 2, width)),
            pl.BlockSpec((1, tokens, width), block),
            pl.BlockSpec((1, tokens, width), block),
            whole((width, tokens)),
            whole((tokens, width)),
            whole((tokens, 128)),
            whole((tokens, width)),
            whole(small.shape),
            held(1),
            held(5),
            held(0, True),
            pl.BlockSpec(memory_space=pl.ANY),
        ],
        out_specs=[
            *[pl.BlockSpec(memory_space=pl.ANY)] * 5,
            out((tokens, width)),
            out((tokens, width)),
            out((16, width)),
            pl.BlockSpec(memory_space=pl.ANY),
        ],
        out_shape=[
            bf16_of(9, rows, width),
            bf16_of(n_ctx - 1, NEAR, rows, width),
            *[bf16_of(9 - NEAR, rows, width)] * 3,
            f32_of(tokens, width),
            bf16_of(tokens, width),
            f32_of(16, width),
            bf16_of(*layer.shape),
        ],
        scratch_shapes=[
            pltpu.VMEM((tokens, width), jnp.float32),
            pltpu.VMEM((tokens, width), jnp.bfloat16),
            pltpu.VMEM((tokens, width), jnp.bfloat16),
            pltpu.VMEM((width, tokens), jnp.bfloat16),
            pltpu.VMEM((2, n_ctx, n_tp, 2, rows, width), jnp.bfloat16),
            pltpu.VMEM((5, n_tp - 1, n_ctx, 2, rows, width), jnp.bfloat16),
            pltpu.VMEM((n_ctx, 9 + 1, rows, width), jnp.bfloat16),
            dma((5 * (n_tp - 1),)),
            dma((5 * (n_tp - 1),)),
            dma((2,)),
            dma((2,)),
            dma((CROSSINGS * (n_ctx - 1),)),
            dma((CROSSINGS * (n_ctx - 1),)),
            dma((2,)),
            dma((2 * n_ctx,)),
        ],
        compiler_params=pltpu.CompilerParams(
            collective_id=3, has_side_effects=True, vmem_limit_bytes=62 << 20
        ),
        cost_estimate=pl.CostEstimate(
            flops=22_000_000_000, bytes_accessed=40 << 20, transcendentals=0
        ),
    )(n2, r2, cots, hid, gel, fit, n1, r1, ctx, small, rest, rest, rest, layer)


LATE = 3
EARLY = 9


def adam_update(weight, first, second, grad, decay, rate):
    count = float(STEP)
    first_new = beta_one * first + (1.0 - beta_one) * grad
    second_new = beta_two * second + (1.0 - beta_two) * grad * grad
    first_hat = first_new / (1.0 - beta_one**count)
    second_hat = second_new / (1.0 - beta_two**count)
    weight_new = weight - rate * (first_hat / (jnp.sqrt(second_hat) + adam_eps) + decay * weight)
    return (weight_new, first_new, second_new)


def finish_kernel(
    n_shard,
    n_ctx,
    n_tp,
    holder,
    late_at,
    x_hbm,
    dq_hbm,
    dk_hbm,
    dv_hbm,
    gh1_hbm,
    first_hbm,
    e0_hbm,
    near_hbm,
    e1_hbm,
    e2_hbm,
    e3_hbm,
    small_ref,
    home_ref,
    grad_out,
    small_out,
    x_s,
    dq_s,
    dk_s,
    dv_s,
    gh1_s,
    first_s,
    early,
    every,
    packed,
    right_met,
    left_met,
    flipped,
    grads,
    arrived,
    partial,
    met,
    over,
    more,
    back_s,
    small_s,
    small_t,
    small_m,
    small_p,
    flat_a,
    met_a,
    sum_a,
    mine_a,
    flat_b,
    met_b,
    sum_b,
    mine_b,
    pool,
    in_sem,
    c_s,
    c_r,
    p_s,
    p_r,
    o_s,
    o_r,
    h_s,
    h_r,
    sc_s,
    sc_r,
    sp_s,
    sp_r,
    e_s,
    e_r,
    l_s,
    l_r,
    a_s,
    a_r,
    b_s,
    b_r,
    d_s,
    d_r,
    f_s,
    f_r,
    keep_sem,
):
    z, c, t = place_of()
    side, core, bit = t // 2, lax.rem(t, 2), lax.rem(c, 2)
    _, mid, width = x_s.shape
    tokens = 2 * mid
    held, rows, _ = grad_out.shape
    per = n_ctx * n_tp // 2
    band = width // 2
    tile = mid

    loads = [
        pltpu.make_async_copy(src, dst, in_sem.at[i])
        for i, (src, dst) in enumerate(
            (
                (x_hbm, x_s),
                (dk_hbm, dk_s),
                (dv_hbm, dv_s),
                (dq_hbm, dq_s),
                (first_hbm, first_s),
                (gh1_hbm, gh1_s),
                (e0_hbm, early.at[0]),
                (near_hbm, early.at[1:4, 0:NEAR]),
                (e1_hbm, early.at[1, NEAR:EARLY]),
                (e2_hbm, early.at[2, NEAR:EARLY]),
                (e3_hbm, early.at[3, NEAR:EARLY]),
            )
        )
    ]
    for i in (6, 7, 8, 9, 10, 0, 1, 2, 3, 4, 5):
        loads[i].start()

    def far(dz):
        return (lax.rem(z + dz, n_shard), c, t)

    def across(mask):
        return (z, c ^ mask, t)

    def beside(dt):
        return (z, c, lax.rem(t + dt, n_tp))

    barrier = pltpu.get_barrier_semaphore()
    friends = [far(dz) for dz in range(1, n_shard)]
    friends += [(z, c ^ m, t) for m in range(1, n_ctx)]
    friends += [beside(dt) for dt in range(1, n_tp)]
    friends += [(z, c ^ m, t ^ 1) for m in range(1, n_ctx)]
    for friend in friends:
        pl.semaphore_signal(barrier, inc=1, device_id=friend, device_id_type=MESH)

    for i in range(6, 11):
        loads[i].wait()
    every[0:EARLY] = early[0] + early[1] + early[2] + early[3]
    every[EARLY] = jnp.zeros_like(every[EARLY])
    for s in range(n_shard * held):
        packed[s // held, s % held] = every[holder[s]]
    pl.semaphore_wait(barrier, len(friends))

    def run(owner_at, s, way):
        met, sems = (right_met, (e_s, e_r)) if way > 0 else (left_met, (l_s, l_r))
        target = (lax.rem(z + way + n_shard, n_shard), c, t)
        return send(packed.at[owner_at], met.at[s], sems, s, target)

    def each_run(hop):
        for s in range(hop + 1):
            for way in (1, -1):
                place = hop - s if way > 0 else n_shard - 1 - (hop - s)
                owner_at = n_shard - 1 - s if way > 0 else s
                yield s, way, place, owner_at

    def hop(h):
        for s, way, place, owner_at in each_run(h):

            @pl.when(z == place)
            def move(s=s, way=way, place=place, owner_at=owner_at):
                copy = run(owner_at, s, way)
                if h > s:
                    copy.wait_recv()
                    met = right_met if way > 0 else left_met
                    for j in range(held):
                        packed[owner_at, j] = packed[owner_at, j] + met[s, j]
                copy.start()

    def hops_end():
        for h in range(n_shard - 1):
            for s, way, place, owner_at in each_run(h):

                @pl.when(z == place)
                def sent(s=s, way=way, owner_at=owner_at):
                    run(owner_at, s, way).wait_send()

        for s in range(n_shard - 1):
            for way in (1, -1):
                owner_at = n_shard - 1 - s if way > 0 else s

                @pl.when(z == owner_at)
                def last(s=s, way=way, owner_at=owner_at):
                    run(owner_at, s, way).wait_recv()
                    met = right_met if way > 0 else left_met
                    for j in range(held):
                        packed[owner_at, j] = packed[owner_at, j] + met[s, j]

    hop(0)

    core_moves = []

    def exchange(m):
        for dt in range(1, n_tp):
            other = lax.rem(t + dt, n_tp)
            for k in range(n_ctx):
                copy = send(
                    grads.at[k * n_tp + other, m],
                    arrived.at[dt - 1, k, m],
                    (c_s, c_r),
                    ((dt - 1) * n_ctx + k) * LATE + m,
                    beside(dt),
                )
                copy.start()
                core_moves.append((m, copy))

    plane_moves = []

    def meet(m):
        for which, copy in core_moves:
            if which == m:
                copy.wait_recv()
        for k in range(n_ctx):
            value = grads[k * n_tp + t, m]
            for dt in range(1, n_tp):
                value = value + arrived[dt - 1, k, m]
            partial[k, m] = value
        for j in range(1, n_ctx):
            copy = send(
                partial.at[c ^ j, m], met.at[j - 1, m], (p_s, p_r), (j - 1) * LATE + m, across(j)
            )
            copy.start()
            plane_moves.append((m, copy))

    loads[0].wait()
    for a in range(4):
        chunk = 2 * (core if a < 2 else 1 - core) + ((a % 2) ^ bit)
        flipped[:, pl.ds(pl.multiple_of(chunk * mid, mid), mid)] = x_s[a].T

    def weight_grad(m, left_at, right):
        def one(i, carry):
            left = flipped[pl.ds(pl.multiple_of(i * band, band), band), left_at]
            value = wide_dot(left, right[...], NN).astype(jnp.bfloat16)
            grads[pl.ds(i * per, per), m] = value.reshape(per, rows, width)
            return carry

        lax.fori_loop(0, 2, one, 0)

    loads[1].wait()
    weight_grad(1, slice(None), dk_s)
    exchange(1)
    loads[2].wait()
    weight_grad(2, slice(None), dv_s)
    exchange(2)
    meet(1)
    for h in range(1, n_shard - 2):
        hop(h)
    loads[3].wait()
    weight_grad(0, pl.ds(pl.multiple_of(core * tokens, tokens), tokens), dq_s)
    exchange(0)
    meet(2)

    row = lax.broadcasted_iota(jnp.int32, small_ref.shape, 0)
    q_sum = jnp.sum(dq_s[...].astype(jnp.float32), axis=0, keepdims=True)
    v_sum = jnp.sum(dv_s[...].astype(jnp.float32), axis=0, keepdims=True)
    sums = jnp.where(row == 0, q_sum, jnp.where(row == 1, v_sum, small_ref[...]))
    small_s[...] = sums.astype(jnp.bfloat16)
    small_core = [
        send(small_s, small_t.at[dt - 1], (sc_s, sc_r), dt - 1, beside(dt)) for dt in range(1, n_tp)
    ]
    for copy in small_core:
        copy.start()

    loads[4].wait()

    def weight(m):
        return first_s[:, m * rows : (m + 1) * rows, :].reshape(width, width)

    wq, wk, wv = weight(0), weight(1), weight(2)
    over_moves = []
    for b in range(2):
        at = pl.ds(pl.multiple_of((1 - core) * tokens + b * mid, mid), mid)
        value = wide_dot(dk_s[at, :], wk, NT) + wide_dot(dv_s[at, :], wv, NT)
        over[b] = value.astype(jnp.bfloat16)
        copy = send(over.at[b], more.at[b], (o_s, o_r), b, (z, c, t ^ 1))
        copy.start()
        over_moves.append(copy)
        if b == 0:
            meet(0)
            if n_shard > 2:
                hop(n_shard - 2)

    value = small_s[...]
    for dt, copy in enumerate(small_core):
        copy.wait_recv()
        value = value + small_t[dt]
    small_m[...] = value
    small_plane = [
        send(small_m, small_p.at[j - 1], (sp_s, sp_r), j - 1, across(j)) for j in range(1, n_ctx)
    ]
    for copy in small_plane:
        copy.start()

    loads[5].wait()
    stays = c // 2 == core
    home_moves = []
    for copy in over_moves:
        copy.wait_recv()
    keep = pltpu.make_async_copy(back_s.at[0], home_ref.at[bit], keep_sem.at[0])
    for move in range(2):
        chunk = move ^ bit
        for i in range(mid // tile):
            at = pl.ds(pl.multiple_of(core * tokens + chunk * mid + i * tile, tile), tile)
            here = pl.ds(pl.multiple_of(chunk * mid + i * tile, tile), tile)
            value = gh1_s[here, :]
            value = value + more[chunk, i * tile : (i + 1) * tile, :].astype(jnp.float32)
            value = value + wide_dot(dq_s[here, :], wq, NT)
            value = value + wide_dot(dk_s[at, :], wk, NT)
            value = value + wide_dot(dv_s[at, :], wv, NT)
            back_s[move, i * tile : (i + 1) * tile, :] = value.astype(jnp.bfloat16)
        target = (z, 2 * core + chunk, 2 * side + c // 2)
        home_moves.append(send(back_s.at[move], home_ref.at[bit], (h_s, h_r), move, target))
        if move == 0:

            @pl.when(stays)
            def kept():
                keep.start()

            @pl.when(jnp.logical_not(stays))
            def left():
                home_moves[0].start()

        else:
            home_moves[1].start()

    def gathered_rows(m):
        for which, copy in plane_moves:
            if which == m:
                copy.wait_recv()
        value = partial[c, m]
        for j in range(n_ctx - 1):
            value = value + met[j, m]
        return value

    def piece_at(ref, k):
        piece = ref.shape[0] // n_shard
        return pl.ds(pl.multiple_of(k * piece, piece), piece)

    def scatter_lot(flat, lot_met, sems):
        moves = [
            send(flat.at[piece_at(flat, far(dz)[0])], lot_met.at[dz - 1], sems, dz - 1, far(dz))
            for dz in range(1, n_shard)
        ]
        for copy in moves:
            copy.start()
        return moves

    def spread_lot(moves, flat, lot_met, lot_sum, lot_mine, sems):
        total = flat[piece_at(flat, z), :].astype(jnp.float32)
        for dz, copy in enumerate(moves):
            copy.wait_recv()
            total = total + lot_met[dz].astype(jnp.float32)
        lot_mine[...] = total.astype(jnp.bfloat16)
        spreads = [
            send(lot_mine, lot_sum.at[piece_at(flat, z)], sems, dz - 1, far(dz))
            for dz in range(1, n_shard)
        ]
        for copy in spreads:
            copy.start()
        lot_sum[piece_at(flat, z), :] = lot_mine[...]
        return spreads

    small_rows = small_s.shape[0]
    flat_a[...] = jnp.zeros_like(flat_a)
    flat_b[...] = jnp.zeros_like(flat_b)
    flat_a[0:rows, :] = gathered_rows(1)
    flat_a[rows : 2 * rows, :] = gathered_rows(2)
    scatter_a = scatter_lot(flat_a, met_a, (a_s, a_r))
    flat_b[0:rows, :] = gathered_rows(0)
    value = small_m[...]
    for j, copy in enumerate(small_plane):
        copy.wait_recv()
        value = value + small_p[j]
    flat_b[rows : rows + small_rows, :] = value
    scatter_b = scatter_lot(flat_b, met_b, (b_s, b_r))
    spread_a = spread_lot(scatter_a, flat_a, met_a, sum_a, mine_a, (d_s, d_r))
    spread_b = spread_lot(scatter_b, flat_b, met_b, sum_b, mine_b, (f_s, f_r))
    hops_end()
    for copy in (*spread_a, *spread_b):
        copy.wait_recv()
    pool[0] = sum_b[0:rows, :]
    pool[1] = sum_a[0:rows, :]
    pool[2] = sum_a[rows : 2 * rows, :]
    pool[LATE] = jnp.zeros_like(pool[LATE])
    for j in range(held):
        grad = packed[z, j].astype(jnp.float32)
        grad = grad + pool[late_at[z * held + j]].astype(jnp.float32)
        grad_out[j] = grad
    small_out[...] = sum_b[rows : rows + small_rows, :].astype(jnp.float32)

    @pl.when(stays)
    def done():
        keep.wait()

    @pl.when(jnp.logical_not(stays))
    def gone():
        home_moves[0].wait()

    home_moves[1].wait()
    for _, copy in (*core_moves, *plane_moves):
        copy.wait_send()
    for copy in (
        *over_moves,
        *small_core,
        *small_plane,
        *scatter_a,
        *scatter_b,
        *spread_a,
        *spread_b,
    ):
        copy.wait_send()


def finish(
    holder,
    late_at,
    x_all,
    dq,
    dk,
    dv,
    gh1,
    first,
    early,
    small,
    held,
    n_shard,
    n_ctx,
    n_tp,
):
    _, mid, width = x_all.shape
    rows = width // (n_ctx * n_tp)
    groups = n_ctx * n_tp
    span = 16 * n_shard
    long_a = -(-2 * rows // span) * span
    long_b = -(-(rows + small.shape[0]) // span) * span
    smem = pl.BlockSpec(memory_space=pltpu.SMEM)
    anywhere = pl.BlockSpec(memory_space=pl.ANY)
    vmem = pl.BlockSpec(memory_space=pltpu.VMEM)
    dma = pltpu.SemaphoreType.DMA
    low = jnp.bfloat16
    pairs = [LATE * n_ctx * (n_tp - 1), LATE * (n_ctx - 1), 2, 2, n_tp - 1, n_ctx - 1]
    pairs += [n_shard - 1] * 6
    shapes = [
        x_all.shape,
        dq.shape,
        dk.shape,
        dv.shape,
        None,
        first.shape,
        (4, EARLY, rows, width),
        (EARLY + 1, rows, width),
        (n_shard, held, rows, width),
        (n_shard - 1, held, rows, width),
        (n_shard - 1, held, rows, width),
        (width, 4 * mid),
        (groups, LATE, rows, width),
        (n_tp - 1, n_ctx, LATE, rows, width),
        (n_ctx, LATE, rows, width),
        (n_ctx - 1, LATE, rows, width),
        (2, mid, width),
        (2, mid, width),
        (2, mid, width),
        small.shape,
        (n_tp - 1, *small.shape),
        small.shape,
        (n_ctx - 1, *small.shape),
        *[
            shape
            for long in (long_a, long_b)
            for shape in (
                (long, width),
                (n_shard - 1, long // n_shard, width),
                (long, width),
                (long // n_shard, width),
            )
        ],
        (LATE + 1, rows, width),
    ]
    return pl.pallas_call(
        functools.partial(finish_kernel, n_shard, n_ctx, n_tp),
        name="finish",
        in_specs=[smem] * 2 + [anywhere] * 11 + [vmem],
        out_specs=[vmem] * 3,
        out_shape=[bf16_of(2, mid, width), f32_of(held, rows, width), f32_of(*small.shape)],
        scratch_shapes=[
            pltpu.VMEM(s, low) if s else pltpu.VMEM(gh1.shape, jnp.float32) for s in shapes
        ]
        + [dma((11,))]
        + [dma((n,)) for n in pairs for _ in range(2)]
        + [dma((1,))],
        compiler_params=pltpu.CompilerParams(
            collective_id=1, has_side_effects=True, vmem_limit_bytes=63 << 20
        ),
        cost_estimate=pl.CostEstimate(
            flops=12_000_000_000, bytes_accessed=40 << 20, transcendentals=0
        ),
    )(holder, late_at, x_all, dq, dk, dv, gh1, first, *early, small)


def shards(
    inputs,
    cotangent,
    rand_blocks,
    slot_of,
    master,
    moment_one,
    moment_two,
    small_params,
    small_one,
    small_two,
):
    n_shard = lax.axis_size("shard")
    n_ctx = lax.axis_size("ctx")
    n_tp = lax.axis_size("tp")
    groups = n_ctx * n_tp
    held, rows, width = master.shape
    span = small_params.shape[0]
    my_ctx = lax.axis_index("ctx")
    my_tp = lax.axis_index("tp")
    half = lax.rem(my_tp, 2)
    plane = ("ctx", "tp")

    half_one = half.astype(jnp.int32).reshape(1)
    my_shard = lax.axis_index("shard")
    start = ((my_shard * n_ctx + my_ctx) * n_tp + my_tp) * span
    lone = lax.dynamic_update_slice(
        jnp.zeros((16 * width,), jnp.float32), small_params, (start,)
    ).reshape(16, width)
    begun = begin(
        slot_of,
        rand_blocks,
        master,
        lone,
        inputs,
        cotangent,
        n_shard,
        n_ctx,
        n_tp,
    )
    x_all, first, rest, small, q, k, v, context, lse = begun[:9]
    cots, out_low, n1, r1, n2, r2, fit, hid, gel = begun[9:]
    *early, gh1, dctx, sums, layer_home = back(
        n2, r2, cots, hid, gel, fit, n1, r1, context, small, rest, out_low, n_ctx, n_tp
    )
    for j in range(1, n_ctx):
        crossing = [
            (a * n_tp + b, (a ^ j) * n_tp + b) for a in range(n_ctx) for b in range(n_tp)
        ]
        early[j + 1] = lax.ppermute(early[j + 1], plane, crossing)
    dq, dk, dv, layer_out = attend_back(
        half_one, rand_blocks, q, k, v, lse, dctx, layer_home, 15
    )
    stands = jnp.array([8, 0, 2, 4, 6, 1, 3, 5, 7], jnp.int32)
    slots_all = jnp.arange(n_shard * held, dtype=jnp.int32)
    hits = slot_of[None, :] == slots_all[:, None]
    holder = EARLY + jnp.sum(jnp.where(hits[:, LATE:], stands[None, :] - EARLY, 0), axis=1)
    ranks = jnp.arange(LATE, dtype=jnp.int32)[None, :]
    late_at = LATE + jnp.sum(jnp.where(hits[:, :LATE], ranks - LATE, 0), axis=1)
    came, slot_grads, small_sum = finish(
        holder.astype(jnp.int32),
        late_at.astype(jnp.int32),
        x_all,
        dq,
        dk,
        dv,
        gh1,
        first,
        early,
        sums,
        held,
        n_shard,
        n_ctx,
        n_tp,
    )
    input_grad = came.astype(jnp.float32)
    master_new, first_new, second_new = adam_update(
        master, moment_one, moment_two, slot_grads, 0.01, rate_value
    )
    rows_held = -(-span // width) + 1
    first_row = jnp.minimum(start // width, small_sum.shape[0] - rows_held)
    near_rows = lax.dynamic_slice_in_dim(small_sum, first_row, rows_held).reshape(-1)
    small_owned = lax.dynamic_slice_in_dim(near_rows, start - first_row * width, span)
    small_new, small_first, small_second = adam_update(
        small_params, small_one, small_two, small_owned, 0.0, small_rate
    )
    return (
        layer_out,
        input_grad,
        master_new,
        first_new,
        second_new,
        small_new,
        small_first,
        small_second,
    )


def solution(mesh):
    tokens = P(("shard", "tp"), "ctx", None)
    stored = P("shard", ("ctx", "tp"), None)
    spread = P(("shard", "ctx", "tp"))
    return jax.shard_map(
        shards,
        mesh=mesh,
        in_specs=(tokens, tokens, P(), P(), stored, stored, stored, spread, spread, spread),
        out_specs=(tokens, tokens, stored, stored, stored, spread, spread, spread),
        check_vma=False,
    )
```

```python
import functools

import jax
import jax.numpy as jnp
from jax import lax
from jax.experimental import pallas as pl
from jax.experimental.pallas import tpu as pltpu
from jax.sharding import PartitionSpec as P

STEP = 5
norm_eps = 1e-12
beta_one = 0.9
beta_two = 0.999
adam_eps = 1e-08
rate_value = 0.04
small_rate = 0.25
score_scale = 0.125
gelu_root = 0.7978845608
gelu_cube = 0.044715

BLOCK = 64
HEAD = 64
PACK = 4
masked_score = -1e30
open_score = 3e38


def wide_dot(a, b, dims):
    return lax.dot_general(a, b, (dims, ((), ())), preferred_element_type=jnp.float32)


def head_masks(rows):
    lane = lax.broadcasted_iota(jnp.int32, (rows, PACK * HEAD), 1) // HEAD
    return [lane == h for h in range(PACK)]


def spread_heads(block, masks):
    zero = jnp.zeros_like(block)
    return jnp.concatenate([jnp.where(m, block, zero) for m in masks], axis=0)


def own_heads(full, masks):
    total = None
    for h, m in enumerate(masks):
        piece = jnp.where(m, full[h * BLOCK : (h + 1) * BLOCK], 0.0)
        total = piece if total is None else total + piece
    return total


def rows_of(ref, index, count=1):
    return ref[pl.ds(index, count)].reshape(count * BLOCK, ref.shape[2])


def flat_rows(ref, index):
    return ref[pl.ds(pl.multiple_of(index * BLOCK, BLOCK), BLOCK), :]


def picked_rows(ref, picks, low_half):
    halves = []
    for pair in range(PACK // 2):
        cols = slice(pair * 2 * HEAD, (pair + 1) * 2 * HEAD)
        first = ref[picks[2 * pair], :, cols]
        second = ref[picks[2 * pair + 1], :, cols]
        halves.append(jnp.where(low_half, first, second))
    return jnp.concatenate(halves, axis=1)


def gathered(ref, block, last, picks, low_half):
    pieces = [rows_of(ref, 0), rows_of(ref, last), rows_of(ref, block - 1, 3)]
    pieces += [picked_rows(ref, p, low_half) for p in picks]
    return jnp.concatenate(pieces, axis=0)


def middle_scores(keys, spread, block, last):
    scores = wide_dot(keys, spread, ((1,), (1,)))
    first_cap = jnp.where(block == 1, masked_score, open_score)
    last_cap = jnp.where(block == last - 1, masked_score, open_score)
    b = BLOCK
    return jnp.concatenate(
        [
            scores[: 2 * b],
            jnp.minimum(scores[2 * b : 3 * b], first_cap),
            scores[3 * b : 4 * b],
            jnp.minimum(scores[4 * b : 5 * b], last_cap),
            scores[5 * b :],
        ],
        axis=0,
    )


def attend_back_kernel(
    unroll,
    half_ref,
    table_ref,
    q_ref,
    k_ref,
    v_ref,
    lse_ref,
    do_ref,
    layer_ref,
    dq_ref,
    dk_ref,
    dv_ref,
    wide_ref,
    dk_acc,
    dv_acc,
    kept_p,
    kept_g,
):
    wide_ref[...] = layer_ref[...].astype(jnp.float32)
    half = half_ref[0]
    group = pl.program_id(0)
    q_ref, k_ref, v_ref = q_ref.at[0], k_ref.at[0], v_ref.at[0]
    nblocks, local = k_ref.shape[0], q_ref.shape[0]
    last = nblocks - 1
    picks_each = table_ref.shape[2]
    masks = head_masks(BLOCK)
    low_half = lax.broadcasted_iota(jnp.int32, (BLOCK, 2 * HEAD), 1) < HEAD
    span = 8 * BLOCK
    chunks = nblocks // 8

    edge = (local - 1) * half
    spread = spread_heads(rows_of(q_ref, edge), masks)
    spread_do = spread_heads(flat_rows(do_ref, edge), masks)
    lse = lse_ref[0, pl.ds(edge, 1), :]
    delta = None
    for c in range(chunks):
        rows = slice(c * span, (c + 1) * span)
        probs = jnp.exp(wide_dot(rows_of(k_ref, c * 8, 8), spread, ((1,), (1,))) - lse)
        gp = wide_dot(rows_of(v_ref, c * 8, 8), spread_do, ((1,), (1,)))
        kept_p[rows, :] = probs
        kept_g[rows, :] = gp
        part = jnp.sum(probs * gp, axis=0, keepdims=True)
        delta = part if delta is None else delta + part
    full = None
    for c in range(chunks):
        rows = slice(c * span, (c + 1) * span)
        probs = kept_p[rows, :]
        ds = (probs * (kept_g[rows, :] - delta)).astype(jnp.bfloat16)
        dv_acc[rows, :] = wide_dot(probs.astype(jnp.bfloat16), spread_do, ((1,), (0,)))
        dk_acc[rows, :] = wide_dot(ds, spread, ((1,), (0,)))
        part = wide_dot(ds, rows_of(k_ref, c * 8, 8), ((0,), (0,)))
        full = part if full is None else full + part
    dq_ref[pl.ds(pl.multiple_of(edge * BLOCK, BLOCK), BLOCK), :] = (
        own_heads(full, masks) * 0.125
    ).astype(jnp.bfloat16)

    def scatter(acc, piece, block, picks):
        b = BLOCK
        acc[0:b, :] += piece[:b]
        acc[last * b : (last + 1) * b, :] += piece[b : 2 * b]
        window = pl.ds(pl.multiple_of((block - 1) * b, b), 3 * b)
        acc[window, :] += piece[2 * b : 5 * b]
        for r, p in enumerate(picks):
            part = piece[(5 + r) * b : (6 + r) * b]
            for pair in range(PACK // 2):
                lanes = slice(pair * 2 * HEAD, (pair + 1) * 2 * HEAD)
                cols = pl.ds(pair * 2 * HEAD, 2 * HEAD)
                sub = part[:, lanes]
                acc[pl.ds(pl.multiple_of(p[2 * pair] * b, b), b), cols] += jnp.where(
                    low_half, sub, 0.0
                )
                acc[pl.ds(pl.multiple_of(p[2 * pair + 1] * b, b), b), cols] += jnp.where(
                    low_half, 0.0, sub
                )

    def middle(step, carry):
        mine = step + 1 - half
        block = mine + local * half
        picks = [
            [table_ref[group * PACK + h, block - 1, r] for h in range(PACK)]
            for r in range(picks_each)
        ]
        spread = spread_heads(rows_of(q_ref, mine), masks)
        spread_do = spread_heads(flat_rows(do_ref, mine), masks)
        keys = gathered(k_ref, block, last, picks, low_half)
        values = gathered(v_ref, block, last, picks, low_half)
        scores = middle_scores(keys, spread, block, last)
        probs = jnp.exp(scores - lse_ref[0, pl.ds(mine, 1), :])
        gp = wide_dot(values, spread_do, ((1,), (1,)))
        delta = jnp.sum(probs * gp, axis=0, keepdims=True)
        ds = (probs * (gp - delta)).astype(jnp.bfloat16)
        low = probs.astype(jnp.bfloat16)
        scatter(dv_acc, wide_dot(low, spread_do, ((1,), (0,))), block, picks)
        scatter(dk_acc, wide_dot(ds, spread, ((1,), (0,))), block, picks)
        full = wide_dot(ds, keys, ((0,), (0,)))
        dq_ref[pl.ds(pl.multiple_of(mine * BLOCK, BLOCK), BLOCK), :] = (
            own_heads(full, masks) * 0.125
        ).astype(jnp.bfloat16)
        return carry

    lax.fori_loop(0, local - 1, middle, 0, unroll=unroll)
    dk_ref[...] = dk_acc[...].astype(jnp.bfloat16)
    dv_ref[...] = dv_acc[...].astype(jnp.bfloat16)


def attend_back(half, table, q, k, v, lse, do, layer, unroll=3):
    tokens, width = do.shape
    groups, nblocks, _, lanes = k.shape
    seq = nblocks * BLOCK
    blocks = tokens // BLOCK
    mine = pl.BlockSpec((tokens, lanes), lambda g, *_: (0, g))
    whole = pl.BlockSpec((seq, lanes), lambda g, *_: (0, g))
    spec = pltpu.PrefetchScalarGridSpec(
        num_scalar_prefetch=2,
        grid=(groups,),
        in_specs=[
            pl.BlockSpec((1, blocks, BLOCK, lanes), lambda g, *_: (g, 0, 0, 0)),
            pl.BlockSpec((1, nblocks, BLOCK, lanes), lambda g, *_: (g, 0, 0, 0)),
            pl.BlockSpec((1, nblocks, BLOCK, lanes), lambda g, *_: (g, 0, 0, 0)),
            pl.BlockSpec((1, blocks, lanes), lambda g, *_: (g, 0, 0)),
            mine,
            pl.BlockSpec((*layer.shape[:2], lanes), lambda g, *_: (0, 0, g)),
        ],
        out_specs=[
            mine,
            whole,
            whole,
            pl.BlockSpec((*layer.shape[:2], lanes), lambda g, *_: (0, 0, g)),
        ],
        scratch_shapes=[pltpu.VMEM((seq, lanes), jnp.float32)] * 4,
    )
    return pl.pallas_call(
        functools.partial(attend_back_kernel, unroll),
        grid_spec=spec,
        out_shape=[
            jax.ShapeDtypeStruct((tokens, width), jnp.bfloat16),
            jax.ShapeDtypeStruct((seq, width), jnp.bfloat16),
            jax.ShapeDtypeStruct((seq, width), jnp.bfloat16),
            jax.ShapeDtypeStruct(layer.shape, jnp.float32),
        ],
        name="attend_back",
        compiler_params=pltpu.CompilerParams(vmem_limit_bytes=56 << 20),
        cost_estimate=pl.CostEstimate(
            flops=120_000_000_000, bytes_accessed=24 << 20, transcendentals=16_000_000
        ),
    )(half, table, q, k, v, lse, do, layer)


TILE = 256
MID = 512


def cols_mean(value):
    return jnp.mean(value, axis=-1, keepdims=True)


def normed(field):
    centred = field - cols_mean(field)
    rate = lax.rsqrt(cols_mean(centred * centred) + norm_eps)
    return centred * rate, rate


def norm_back(cot, normal, rate, gain):
    dn = cot * gain
    return rate * (dn - cols_mean(dn) - normal * cols_mean(dn * normal))


def matrix(ref):
    value = ref[...]
    return value.reshape(-1, value.shape[-1])


def add_row(ref, row, value):
    ref[row : row + 1, :] += jnp.sum(value, axis=0, keepdims=True)


def bf16_of(*shape):
    return jax.ShapeDtypeStruct(shape, jnp.bfloat16)


def f32_of(*shape):
    return jax.ShapeDtypeStruct(shape, jnp.float32)


NN = ((1,), (0,))
NT = ((1,), (1,))
TN = ((0,), (0,))


MESH = pl.DeviceIdType.MESH
KINDS = 3
CHUNKS = 3
PER = 3


def place_of():
    c, t = lax.axis_index("ctx"), lax.axis_index("tp")
    return lax.axis_index("shard"), c, t


def send(src, dst, sems, index, target):
    send_sems, recv_sems = sems
    return pltpu.make_async_remote_copy(
        src_ref=src,
        dst_ref=dst,
        send_sem=send_sems.at[index],
        recv_sem=recv_sems.at[index],
        device_id=target,
        device_id_type=MESH,
    )


def begin_kernel(
    n_shard,
    n_ctx,
    n_tp,
    slots,
    table,
    master_hbm,
    small_in,
    input_hbm,
    cot_hbm,
    x_ref,
    first_ref,
    rest_out,
    small_ref,
    q_ref,
    k_ref,
    v_ref,
    ctx_ref,
    lse_ref,
    cot_ref,
    layer_ref,
    n1_ref,
    r1_ref,
    n2_ref,
    r2_ref,
    fit_ref,
    hid_ref,
    gel_ref,
    raw,
    low,
    given,
    xs,
    x_all,
    part,
    got,
    mine,
    total,
    pool,
    sel,
    first,
    rest_ref,
    small,
    q_s,
    k_s,
    v_s,
    ctx_s,
    kept,
    n1_s,
    gel_s,
    hid_s,
    fit_s,
    layer_s,
    x_s,
    x_r,
    xt_s,
    xt_r,
    za_s,
    za_r,
    zb_s,
    zb_r,
    zc_s,
    zc_r,
    zd_s,
    zd_r,
    qm_s,
    qm_r,
    qt_s,
    qt_r,
    r_s,
    r_r,
    rt_s,
    rt_r,
    y_s,
    y_r,
    own_sem,
    out_sem,
    tile_sem,
    end_sem,
):
    z, c, t = place_of()
    side, core, bit = t // 2, lax.rem(t, 2), lax.rem(c, 2)
    held, rows, width = low.shape[0] - 1, low.shape[1], low.shape[2]
    piece = mine.shape[0]
    me = c * n_tp + t
    _, mid, _ = xs.shape
    nblocks = 4 * mid // BLOCK
    local = nblocks // 2
    lanes = PACK * HEAD
    groups = width // lanes
    others = n_tp - 1

    take_raw = pltpu.make_async_copy(master_hbm, raw, own_sem.at[0])
    take_given = pltpu.make_async_copy(input_hbm, given, own_sem.at[1])
    take_raw.start()
    take_given.start()

    def far(dz):
        return (lax.rem(z + dz, n_shard), c, t)

    def across(mask):
        return (z, c ^ mask, t)

    def beside(dt):
        return (z, c, lax.rem(t + dt, n_tp))

    barrier = pltpu.get_barrier_semaphore()
    friends = [far(dz) for dz in range(1, n_shard)]
    friends += [(z, c ^ m, t) for m in range(1, n_ctx)]
    friends += [beside(dt) for dt in range(1, n_tp)]
    friends += [(z, c ^ m, t ^ 1) for m in range(1, n_ctx)]
    for friend in friends:
        pl.semaphore_signal(barrier, inc=1, device_id=friend, device_id_type=MESH)

    take_raw.wait()
    for j in range(held):
        low[j] = raw[j].astype(jnp.bfloat16)
    low[held] = jnp.zeros_like(low[held])
    pool[pl.ds(z * held, held)] = low[0:held]
    part[...] = jnp.zeros_like(part)
    for m in range(KINDS):
        place = slots[m] - z * held
        mine_too = (place >= 0) & (place < held)
        part[m * rows : (m + 1) * rows, :] = low[jnp.where(mine_too, place, held)]
    part[KINDS * rows : KINDS * rows + 16, :] = small_in[...].astype(jnp.bfloat16)
    pl.semaphore_wait(barrier, len(friends))

    def piece_at(k):
        return pl.ds(pl.multiple_of(k * piece, piece), piece)

    def hop_copy(s, way):
        sems = (zc_s, zc_r) if way > 0 else (zd_s, zd_r)
        slot = pl.ds((z - way * (s - 1)) * held, held)
        return send(
            pool.at[slot], pool.at[slot], sems, s - 1, (lax.rem(z + way + n_shard, n_shard), c, t)
        )

    def hop_on(s, way):
        start = z - way * (s - 1)
        end = z + way
        return (start >= 0) & (start < n_shard) & (end >= 0) & (end < n_shard)

    def hop(s):
        for way in (1, -1):

            @pl.when(hop_on(s, way))
            def move(way=way):
                if s > 1:
                    hop_copy(s - 1, way).wait_recv()
                hop_copy(s, way).start()

    za = [
        send(part.at[piece_at(far(dz)[0])], got.at[dz - 1], (za_s, za_r), dz - 1, far(dz))
        for dz in range(1, n_shard)
    ]
    for copy in za:
        copy.start()

    stays = c // 2 == core
    goes = [(z, 2 * core + (p ^ bit), 2 * side + c // 2) for p in range(2)]
    x_moves = [send(xs.at[p], x_all.at[p], (x_s, x_r), p, goes[p]) for p in range(2)]
    x_keep = pltpu.make_async_copy(xs.at[0], x_all.at[0], own_sem.at[2])
    take_given.wait()
    xs[0] = given[bit].astype(jnp.bfloat16)

    @pl.when(stays)
    def keep():
        x_keep.start()

    @pl.when(jnp.logical_not(stays))
    def leave():
        x_moves[0].start()

    xs[1] = given[1 - bit].astype(jnp.bfloat16)
    x_moves[1].start()

    summed = part[piece_at(z), :]
    for dz, copy in enumerate(za):
        copy.wait_recv()
        summed = summed + got[dz]
    mine[...] = summed
    zb = [
        send(mine, total.at[piece_at(z)], (zb_s, zb_r), dz - 1, far(dz))
        for dz in range(1, n_shard)
    ]
    for copy in zb:
        copy.start()
    total[piece_at(z), :] = summed
    def hops_end():
        for way, end in ((1, n_shard - 1), (-1, 0)):

            @pl.when(z == end)
            def gather(way=way):
                for s in range(1, n_shard):
                    hop_copy(s, way).wait_recv()

    def hops_sent():
        for s in range(1, n_shard):
            for way in (1, -1):

                @pl.when(hop_on(s, way))
                def sent(s=s, way=way):
                    hop_copy(s, way).wait_send()

    for copy in zb:
        copy.wait_recv()
    hop(1)

    q_moves = [
        send(total, first.at[me], (qm_s, qm_r), k, across(m)) for k, m in enumerate((1, 2, 3))
    ]
    for copy in q_moves:
        copy.start()
    qt_moves = [
        send(total, first.at[me], (qt_s, qt_r), dt - 1, beside(dt)) for dt in range(1, n_tp)
    ]
    for copy in qt_moves:
        copy.start()
    first[me] = total[...]

    x_over = [
        send(x_all.at[p], x_all.at[2 + p], (xt_s, xt_r), p, (z, c, t ^ 1)) for p in range(2)
    ]

    @pl.when(stays)
    def stayed():
        x_keep.wait()

    @pl.when(jnp.logical_not(stays))
    def came():
        x_moves[0].wait_recv()

    x_over[0].start()
    x_moves[1].wait_recv()
    x_over[1].start()
    for s in range(2, n_shard):
        hop(s)

    for k, m in enumerate((1, 2, 3)):
        q_moves[k].wait_recv()
        place = (c ^ m) * n_tp + t
        for dt in range(1, n_tp):
            copy = send(
                first.at[place],
                first.at[place],
                (qt_s, qt_r),
                (k + 1) * others + dt - 1,
                beside(dt),
            )
            copy.start()
            qt_moves.append(copy)
    for copy in qt_moves:
        copy.wait_recv()
    def span_of(k):
        return pl.ds(k * PER, PER)

    rest_own = pltpu.make_async_copy(sel, rest_ref.at[me], own_sem.at[3])
    direct = [
        [
            send(
                sel.at[span_of(k)], rest_ref.at[me, span_of(k)], (r_s, r_r), k * 3 + j, across(m)
            )
            for j, m in enumerate((1, 2))
        ]
        for k in range(CHUNKS)
    ]
    onward = []
    for k in range(CHUNKS):
        odd = lax.rem(core + k, 2)
        source = jnp.where(odd == 0, c ^ 1, c ^ 2) * n_tp + t
        target = (z, jnp.where(odd == 0, c ^ 2, c ^ 1), t)
        view = rest_ref.at[source, span_of(k)]
        onward.append(send(view, view, (r_s, r_r), k * 3 + 2, target))

    def passing(k, which):
        if which == 0:
            src = sel.at[span_of(k)]
        else:
            src = rest_ref.at[(c ^ which) * n_tp + t, span_of(k)]
        dst = rest_ref.at[(c ^ which) * n_tp + t, span_of(k)]
        return [
            send(src, dst, (rt_s, rt_r), (k * 4 + which) * others + dt - 1, beside(dt))
            for dt in range(1, n_tp)
        ]

    passed = [[passing(k, which) for which in range(4)] for k in range(CHUNKS)]

    def begin_rest():
        hops_end()
        for m in range(CHUNKS * PER):
            sel[m] = pool[slots[KINDS + m]]
        rest_own.start()
        launch(0)
        launch(1)
        launch(2)

    def launch(k):
        for copy in (*direct[k], *passed[k][0]):
            copy.start()

    def relay(k):
        for copy in direct[k]:
            copy.wait_recv()
        onward[k].start()
        for copy in passed[k][1] + passed[k][2]:
            copy.start()

    def last_relay(k):
        onward[k].wait_recv()
        for copy in passed[k][3]:
            copy.start()

    begin_rest()
    outs = [pltpu.make_async_copy(first, first_ref, out_sem.at[0])]
    outs[0].start()

    sums = None
    for g in range(n_ctx * n_tp):
        here = first[g, KINDS * rows : KINDS * rows + 16, :].astype(jnp.float32)
        sums = here if sums is None else sums + here
    small[...] = sums
    small_ref[...] = sums
    def weight(m):
        return first[:, m * rows : (m + 1) * rows, :].reshape(width, width)

    def split(dst, start, value):
        low_value = value.astype(jnp.bfloat16)
        per = TILE // BLOCK
        for g in range(groups):
            piece_value = low_value[:, g * lanes : (g + 1) * lanes]
            dst[g, pl.ds(start, per)] = piece_value.reshape(per, BLOCK, lanes)

    def project(a, chunk, own):
        def one(i, carry):
            x = x_all[a, pl.ds(pl.multiple_of(i * TILE, TILE), TILE), :]
            start = chunk * (mid // BLOCK) + i * (TILE // BLOCK)
            if own:
                q_start = (chunk - 2 * core) * (mid // BLOCK) + i * (TILE // BLOCK)
                q = wide_dot(x, weight(0), NN) + small[0:1, :]
                split(q_s, q_start, q.astype(jnp.bfloat16) * jnp.bfloat16(score_scale))
            split(k_s, start, wide_dot(x, weight(1), NN))
            split(v_s, start, wide_dot(x, weight(2), NN) + small[1:2, :])
            return carry

        lax.fori_loop(0, mid // TILE, one, 0)

    def own_project(a, carry):
        project(a, 2 * core + (a ^ bit), True)
        return carry

    def other_project(a, carry):
        project(2 + a, 2 * (1 - core) + (a ^ bit), False)
        return carry

    @pl.when(jnp.logical_not(stays))
    def left():
        x_moves[0].wait_send()

    x_moves[1].wait_send()
    take_cot = pltpu.make_async_copy(cot_hbm, given, own_sem.at[2])
    take_cot.start()
    lax.fori_loop(0, 2, own_project, 0)
    for copy in x_over:
        copy.wait_recv()
    outs.append(pltpu.make_async_copy(x_all, x_ref, out_sem.at[1]))
    outs[1].start()
    lax.fori_loop(0, 2, other_project, 0)
    take_cot.wait()
    xs[0] = given[bit].astype(jnp.bfloat16)
    xs[1] = given[1 - bit].astype(jnp.bfloat16)
    for i, (src, dst) in enumerate(((q_s, q_ref), (k_s, k_ref), (v_s, v_ref))):
        outs.append(pltpu.make_async_copy(src, dst, out_sem.at[2 + i]))
        outs[-1].start()

    last = nblocks - 1
    picks_each = table.shape[2]
    masks = head_masks(BLOCK)
    low_half = lax.broadcasted_iota(jnp.int32, (BLOCK, 2 * HEAD), 1) < HEAD
    each = 5
    subs = (local - 1) // each

    def attend_round(i, carry):
        g = i // subs
        sub = lax.rem(i, subs)
        qg, kg, vg = q_s.at[g], k_s.at[g], v_s.at[g]

        @pl.when(i == 3)
        def first_hook():
            relay(0)
            relay(1)

        @pl.when(i == 6)
        def second_hook():
            relay(2)

        @pl.when(sub == 0)
        def edge_block():
            edge = (local - 1) * core
            spread = spread_heads(rows_of(qg, edge), masks)
            span = 8 * BLOCK
            pieces = nblocks // 8
            top = None
            for n in range(pieces):
                scores = wide_dot(rows_of(kg, n * 8, 8), spread, NT)
                kept[n * span : (n + 1) * span, :] = scores
                high = jnp.max(scores, axis=0, keepdims=True)
                top = high if top is None else jnp.maximum(top, high)
            total_p = None
            for n in range(pieces):
                probs = jnp.exp(kept[n * span : (n + 1) * span, :] - top)
                kept[n * span : (n + 1) * span, :] = probs
                some = jnp.sum(probs, axis=0, keepdims=True)
                total_p = some if total_p is None else total_p + some
            scale = 1.0 / total_p
            full = None
            for n in range(pieces):
                probs = (kept[n * span : (n + 1) * span, :] * scale).astype(jnp.bfloat16)
                some = wide_dot(probs, rows_of(vg, n * 8, 8), TN)
                full = some if full is None else full + some
            at = pl.ds(pl.multiple_of(edge * BLOCK, BLOCK), BLOCK)
            ctx_s[g, at, :] = own_heads(full, masks).astype(jnp.bfloat16)
            lse_ref[g, pl.ds(edge, 1), :] = top + jnp.log(total_p)

        for u in range(each):
            spot = sub * each + u + 1 - core
            block = spot + local * core
            picks = [
                [table[g * PACK + h, block - 1, r] for h in range(PACK)]
                for r in range(picks_each)
            ]
            spread = spread_heads(rows_of(qg, spot), masks)
            keys = gathered(kg, block, last, picks, low_half)
            values = gathered(vg, block, last, picks, low_half)
            scores = middle_scores(keys, spread, block, last)
            top = jnp.max(scores, axis=0, keepdims=True)
            probs = jnp.exp(scores - top)
            total_p = jnp.sum(probs, axis=0, keepdims=True)
            probs = (probs * (1.0 / total_p)).astype(jnp.bfloat16)
            full = wide_dot(probs, values, TN)
            at = pl.ds(pl.multiple_of(spot * BLOCK, BLOCK), BLOCK)
            ctx_s[g, at, :] = own_heads(full, masks).astype(jnp.bfloat16)
            lse_ref[g, pl.ds(spot, 1), :] = top + jnp.log(total_p)
        return carry

    lax.fori_loop(0, groups * subs, attend_round, 0)
    for g in range(groups):
        outs.append(
            pltpu.make_async_copy(
                ctx_s.at[g], ctx_ref.at[:, g * lanes : (g + 1) * lanes], out_sem.at[5 + g]
            )
        )
        outs[-1].start()
    last_relay(0)
    last_relay(1)

    cot_moves = [send(xs.at[p], cot_ref.at[p], (y_s, y_r), p, goes[p]) for p in range(2)]
    cot_keep = pltpu.make_async_copy(xs.at[0], cot_ref.at[0], own_sem.at[1])

    for k in range(2):
        for group in passed[k]:
            for copy in group:
                copy.wait_recv()
    rest_own.wait()

    def keep_rest(part, first_m, last_m):
        span = slice(first_m, last_m)
        copy = pltpu.make_async_copy(
            rest_ref.at[:, span], rest_out.at[:, span], out_sem.at[5 + groups + part]
        )
        copy.start()
        outs.append(copy)

    keep_rest(0, 0, 2 * PER)
    tiles = 2 * mid // TILE
    per = mid // TILE

    def held_out(m):
        return rest_ref[:, m].reshape(width, width)

    def tile_out(i, slot):
        at = pl.ds(pl.multiple_of(i * TILE, TILE), TILE)
        return (
            pltpu.make_async_copy(n1_s.at[slot], n1_ref.at[at], tile_sem.at[slot]),
            pltpu.make_async_copy(gel_s.at[slot], gel_ref.at[:, at], tile_sem.at[2 + slot]),
        )

    def hid_out(i):
        at = pl.ds(pl.multiple_of(i * TILE, TILE), TILE)
        return pltpu.make_async_copy(hid_s.at[:, at], hid_ref.at[:, at], end_sem.at[2 * tiles + i])

    def rise_tile(i, carry):
        slot = lax.rem(i, 2)
        at = pl.ds(pl.multiple_of(i * TILE, TILE), TILE)
        inside = pl.ds(pl.multiple_of(lax.rem(i, per) * TILE, TILE), TILE)

        @pl.when(i == 1)
        def cross_cot():
            @pl.when(stays)
            def keep_cot():
                cot_keep.start()

            @pl.when(jnp.logical_not(stays))
            def leave_cot():
                cot_moves[0].start()

            cot_moves[1].start()

        @pl.when(i == 2)
        def late_relay():
            last_relay(2)

        @pl.when(i >= 2)
        def free():
            for copy in tile_out(i - 2, slot):
                copy.wait()

        context = jnp.concatenate([ctx_s[g, at, :] for g in range(groups)], axis=1)
        attn_out = wide_dot(context, held_out(0), NN) + small[2:3, :]
        x = x_all[(i // per) ^ bit, inside, :].astype(jnp.float32)
        n1, r1 = normed(x + attn_out)
        n1_s[slot] = n1
        r1_ref[at, :] = jnp.broadcast_to(r1, (TILE, r1_ref.shape[1]))
        after = n1 * small[3:4, :] + small[4:5, :]
        ffn_in = after.astype(jnp.bfloat16)
        fit_s[:, at] = ffn_in.T
        given[i // per, inside, :] = after + small[9:10, :]
        for b in range(4):
            up = wide_dot(ffn_in, held_out(1 + b), NN) + small[5 + b : 6 + b, :]
            square = up * up
            bent = jnp.tanh(gelu_root * up * (1.0 + gelu_cube * square))
            rise = 0.5 * (1.0 + bent)
            hid_s[b, at, :] = (up * rise).astype(jnp.bfloat16)
            slope = rise + (0.5 * gelu_root) * up * (1.0 - bent * bent) * (
                1.0 + (3.0 * gelu_cube) * square
            )
            gel_s[slot, b] = slope.astype(jnp.bfloat16)
        for copy in (*tile_out(i, slot), hid_out(i)):
            copy.start()
        return carry

    lax.fori_loop(0, tiles, rise_tile, 0)
    for i in range(tiles - 2, tiles):
        for copy in tile_out(i, i % 2):
            copy.wait()
    outs.append(pltpu.make_async_copy(fit_s, fit_ref, out_sem.at[7 + groups]))
    outs[-1].start()
    for group in passed[2]:
        for copy in group:
            copy.wait_recv()
    keep_rest(1, 2 * PER, 3 * PER)

    def end_out(i):
        at = pl.ds(pl.multiple_of(i * TILE, TILE), TILE)
        inside = pl.ds(pl.multiple_of(lax.rem(i, per) * TILE, TILE), TILE)
        chunk = i // per
        return (
            pltpu.make_async_copy(given.at[chunk, inside], n2_ref.at[at], end_sem.at[i]),
            pltpu.make_async_copy(
                layer_s.at[chunk ^ bit, inside],
                layer_ref.at[chunk ^ bit, inside],
                end_sem.at[tiles + i],
            ),
        )

    def fall_tile(i, carry):
        at = pl.ds(pl.multiple_of(i * TILE, TILE), TILE)
        inside = pl.ds(pl.multiple_of(lax.rem(i, per) * TILE, TILE), TILE)
        summed = given[i // per, inside, :]
        for b in range(4):
            summed = summed + wide_dot(hid_s[b, at, :], held_out(5 + b), NT)
        n2, r2 = normed(summed)
        layer_s[(i // per) ^ bit, inside, :] = (n2 * small[10:11, :] + small[11:12, :]).astype(
            jnp.bfloat16
        )
        given[i // per, inside, :] = n2
        r2_ref[at, :] = jnp.broadcast_to(r2, (TILE, r2_ref.shape[1]))
        for copy in end_out(i):
            copy.start()
        return carry

    lax.fori_loop(0, tiles, fall_tile, 0)
    for i in range(tiles):
        for copy in (*end_out(i), hid_out(i)):
            copy.wait()

    @pl.when(stays)
    def kept_cot():
        cot_keep.wait()

    @pl.when(jnp.logical_not(stays))
    def left_cot():
        cot_moves[0].wait()

    cot_moves[1].wait()
    for copy in (*x_over, *za, *zb, *q_moves, *qt_moves, *onward):
        copy.wait_send()
    for pair in direct:
        for copy in pair:
            copy.wait_send()
    for chunk in passed:
        for group in chunk:
            for copy in group:
                copy.wait_send()
    hops_sent()
    for copy in outs:
        copy.wait()


def begin(slots, table, master, small_in, inputs, cot, n_shard, n_ctx, n_tp):
    held, rows, width = master.shape
    _, mid, _ = inputs.shape
    groups = n_ctx * n_tp
    long = -(-(KINDS * rows + 16) // (16 * n_shard)) * 16 * n_shard
    lanes = PACK * HEAD
    packs = width // lanes
    tokens, seq = 2 * mid, 4 * mid
    anywhere = pl.BlockSpec(memory_space=pl.ANY)
    vmem = pl.BlockSpec(memory_space=pltpu.VMEM)
    smem = pl.BlockSpec(memory_space=pltpu.SMEM)
    dma = pltpu.SemaphoreType.DMA
    low = jnp.bfloat16
    f32 = jnp.float32
    pairs = [2, 2, n_shard - 1, n_shard - 1, n_shard - 1, n_shard - 1, 3]
    pairs += [4 * (n_tp - 1), 3 * CHUNKS, 4 * CHUNKS * (n_tp - 1), 2]
    return pl.pallas_call(
        functools.partial(begin_kernel, n_shard, n_ctx, n_tp),
        name="begin",
        in_specs=[smem, smem, anywhere, vmem, anywhere, anywhere],
        out_specs=[anywhere] * 3
        + [vmem]
        + [anywhere] * 4
        + [vmem]
        + [anywhere] * 3
        + [vmem, anywhere, vmem]
        + [anywhere] * 3,
        out_shape=[
            bf16_of(4, mid, width),
            bf16_of(groups, long, width),
            bf16_of(groups, 9, rows, width),
            f32_of(16, width),
            bf16_of(packs, tokens // BLOCK, BLOCK, lanes),
            bf16_of(packs, seq // BLOCK, BLOCK, lanes),
            bf16_of(packs, seq // BLOCK, BLOCK, lanes),
            bf16_of(tokens, width),
            f32_of(packs, tokens // BLOCK, lanes),
            bf16_of(2, mid, width),
            bf16_of(2, mid, width),
            f32_of(tokens, width),
            f32_of(tokens, 128),
            f32_of(tokens, width),
            f32_of(tokens, 128),
            bf16_of(width, tokens),
            bf16_of(4, tokens, width),
            bf16_of(4, tokens, width),
        ],
        scratch_shapes=[
            pltpu.VMEM((held, rows, width), f32),
            pltpu.VMEM((held + 1, rows, width), low),
            pltpu.VMEM((2, mid, width), f32),
            pltpu.VMEM((2, mid, width), low),
            pltpu.VMEM((4, mid, width), low),
            pltpu.VMEM((long, width), low),
            pltpu.VMEM((n_shard - 1, long // n_shard, width), low),
            pltpu.VMEM((long // n_shard, width), low),
            pltpu.VMEM((long, width), low),
            pltpu.VMEM((n_shard * held, rows, width), low),
            pltpu.VMEM((9, rows, width), low),
            pltpu.VMEM((groups, long, width), low),
            pltpu.VMEM((groups, 9, rows, width), low),
            pltpu.VMEM((16, width), f32),
            pltpu.VMEM((packs, tokens // BLOCK, BLOCK, lanes), low),
            pltpu.VMEM((packs, seq // BLOCK, BLOCK, lanes), low),
            pltpu.VMEM((packs, seq // BLOCK, BLOCK, lanes), low),
            pltpu.VMEM((packs, tokens, lanes), low),
            pltpu.VMEM((seq, lanes), f32),
            pltpu.VMEM((2, TILE, width), f32),
            pltpu.VMEM((2, 4, TILE, width), low),
            pltpu.VMEM((4, tokens, width), low),
            pltpu.VMEM((width, tokens), low),
            pltpu.VMEM((2, mid, width), low),
            *[dma((n,)) for n in pairs for _ in range(2)],
            dma((4,)),
            dma((8 + packs,)),
            dma((4,)),
            dma((3 * (tokens // TILE),)),
        ],
        compiler_params=pltpu.CompilerParams(
            collective_id=0, has_side_effects=True, vmem_limit_bytes=64000 << 10
        ),
        cost_estimate=pl.CostEstimate(
            flops=60_000_000_000, bytes_accessed=60 << 20, transcendentals=16_000_000
        ),
    )(slots, table, master, small_in, inputs, cot)


NEAR = 3
CROSSINGS = -(-NEAR // 2)


def back_kernel(
    n_ctx,
    n_tp,
    n2_hbm,
    r2_ref,
    cots_ref,
    hid_ref,
    gel_ref,
    fit_ref,
    n1_ref,
    r1_ref,
    ctx_ref,
    small,
    up_w,
    down_w,
    wo,
    layer_ref,
    own_ref,
    near_ref,
    x_ref,
    y_ref,
    xy_ref,
    gh1_ref,
    dctx_ref,
    sums_ref,
    home_ref,
    gy,
    gu,
    mixed,
    mixed_t,
    grads,
    arrived,
    sums,
    send_sem,
    recv_sem,
    h_s,
    h_r,
    n_s,
    n_r,
    keep_sem,
    out_sem,
):
    z, c, t = place_of()
    step = pl.program_id(0)
    tokens, width = gy.shape
    tiles = tokens // TILE
    rows = grads.shape[4]
    others = n_tp - 1
    side, core, bit = t // 2, lax.rem(t, 2), lax.rem(c, 2)

    def beside(dt):
        return (z, c, lax.rem(t + dt, n_tp))

    stays = c // 2 == core
    keep_layer = pltpu.make_async_copy(layer_ref.at[0], home_ref.at[bit], keep_sem.at[0])
    layer_moves = [
        send(
            layer_ref.at[p],
            home_ref.at[bit],
            (h_s, h_r),
            p,
            (z, 2 * core + (p ^ bit), 2 * side + c // 2),
        )
        for p in range(2)
    ]

    @pl.when(step == 0)
    def start():
        take = pltpu.make_async_copy(n2_hbm, gy, keep_sem.at[1])
        take.start()
        barrier = pltpu.get_barrier_semaphore()
        friends = [beside(dt) for dt in range(1, n_tp)]
        friends += [(z, c ^ m, t) for m in range(1, n_ctx)]
        friends += [(z, c ^ m, t ^ 1) for m in range(1, n_ctx)]
        for friend in friends:
            pl.semaphore_signal(barrier, inc=1, device_id=friend, device_id_type=MESH)
        pl.semaphore_wait(barrier, len(friends))

        @pl.when(stays)
        def kept():
            keep_layer.start()

        @pl.when(jnp.logical_not(stays))
        def left():
            layer_moves[0].start()

        layer_moves[1].start()
        sums_ref[...] = jnp.zeros_like(sums_ref)
        take.wait()
        mid = tokens // 2
        for p in range(2):

            def one(i, carry, p=p):
                inside = pl.ds(pl.multiple_of(i * TILE, TILE), TILE)
                at = pl.ds(pl.multiple_of((p ^ bit) * mid + i * TILE, TILE), TILE)
                cot = cots_ref[p, inside, :].astype(jnp.float32)
                n2 = gy[at, :]
                add_row(sums_ref, 10, cot * n2)
                add_row(sums_ref, 11, cot)
                gh2 = norm_back(cot, n2, r2_ref[at, 0:1], small[10:11, :])
                gy[at, :] = gh2
                low = gh2.astype(jnp.bfloat16)
                mixed[at, :] = low
                mixed_t[:, at] = low.T
                add_row(sums_ref, 9, low.astype(jnp.float32))
                return carry

            lax.fori_loop(0, mid // TILE, one, 0)

    def moves(b, count):
        slot = lax.rem(b, 2)
        return [
            send(
                grads.at[slot, :, lax.rem(t + dt, n_tp), 0:count],
                arrived.at[b, dt - 1, :, 0:count],
                (send_sem, recv_sem),
                b * others + dt - 1,
                beside(dt),
            )
            for dt in range(1, n_tp)
        ]

    def exchange(b, count):
        for copy in moves(b, count):
            copy.start()

    def keep(b, count):
        for copy in moves(b, count):
            copy.wait()
        slot = lax.rem(b, 2)
        for j in range(n_ctx):
            for i in range(count):
                value = grads[slot, c ^ j, t, i]
                for dt in range(others):
                    value = value + arrived[b, dt, c ^ j, i]
                sums[j, 2 * b + i] = value

    def near(b):
        pair = slice(2 * b, min(2 * b + 2, NEAR))
        return [
            send(
                sums.at[j, pair],
                near_ref.at[j - 1, pair],
                (n_s, n_r),
                b * (n_ctx - 1) + j - 1,
                (z, c ^ j, t),
            )
            for j in range(1, n_ctx)
        ]

    def outward(part, first, count):
        moved = [
            pltpu.make_async_copy(
                sums.at[0, first : first + count],
                own_ref.at[first : first + count],
                out_sem.at[part * n_ctx],
            )
        ]
        begin_at = max(first, NEAR)
        count -= begin_at - first
        for j, out in enumerate((x_ref, y_ref, xy_ref)):
            moved.append(
                pltpu.make_async_copy(
                    sums.at[j + 1, begin_at : begin_at + count],
                    out.at[begin_at - NEAR : begin_at - NEAR + count],
                    out_sem.at[part * n_ctx + j + 1],
                )
            )
        return moved

    def put(slot, i, value):
        low = value.astype(jnp.bfloat16)
        grads[slot, :, :, i] = low.reshape(n_ctx, n_tp, rows, width)

    @pl.when(step < 4)
    def ffn():
        up_block = matrix(up_w)
        down_block = matrix(down_w)
        slot = lax.rem(step, 2)

        def one(i, carry):
            at = pl.ds(pl.multiple_of(i * MID, MID), MID)
            grad = wide_dot(mixed[at, :], down_block, NN) * gel_ref[0, at, :].astype(jnp.float32)
            low = grad.astype(jnp.bfloat16)
            gu[at, :] = low
            gy[at, :] += wide_dot(low, up_block, NT)
            sums_ref[pl.ds(5 + step, 1), :] += jnp.sum(
                low.astype(jnp.float32), axis=0, keepdims=True
            )
            return carry

        lax.fori_loop(0, tokens // MID, one, 0)
        put(slot, 0, wide_dot(fit_ref[...], gu[...], NN))
        put(slot, 1, wide_dot(mixed_t[...], hid_ref[0], NN))
        exchange(step, 2)

    @pl.when(step > 0)
    def settle():
        keep(step - 1, 2)

    for b in range(CROSSINGS):

        @pl.when(step == b + 1)
        def cross(b=b):
            for copy in near(b):
                copy.start()

    @pl.when(step == 4)
    def first_norm():
        for copy in outward(0, 0, 8):
            copy.start()

        def one(i, carry):
            at = pl.ds(pl.multiple_of(i * TILE, TILE), TILE)
            grad = gy[at, :]
            n1 = n1_ref[at, :]
            gh1 = norm_back(grad, n1, r1_ref[at, 0:1], small[3:4, :])
            gh1_ref[at, :] = gh1
            low = gh1.astype(jnp.bfloat16)
            gu[at, :] = low
            add_row(sums_ref, 2, low.astype(jnp.float32))
            add_row(sums_ref, 3, grad * n1)
            add_row(sums_ref, 4, grad)
            return carry

        lax.fori_loop(0, tiles, one, 0)
        put(0, 0, wide_dot(ctx_ref[...].T, gu[...], NN))
        exchange(4, 1)
        out_w = matrix(wo)

        def two(i, carry):
            at = pl.ds(pl.multiple_of(i * TILE, TILE), TILE)
            dctx_ref[at, :] = wide_dot(gu[at, :], out_w, NT).astype(jnp.bfloat16)
            return carry

        lax.fori_loop(0, tiles, two, 0)
        keep(4, 1)
        for copy in outward(1, 8, 1):
            copy.start()
        crossed = [copy for b in range(CROSSINGS) for copy in near(b)]
        for copy in (*crossed, *outward(0, 0, 8), *outward(1, 8, 1)):
            copy.wait()

        @pl.when(stays)
        def done():
            keep_layer.wait()

        @pl.when(jnp.logical_not(stays))
        def gone():
            layer_moves[0].wait()

        layer_moves[1].wait()


def back(n2, r2, cots, hid, gel, fit, n1, r1, ctx, small, rest, layer, n_ctx, n_tp):
    tokens, width = n2.shape
    rows = rest.shape[2]
    dma = pltpu.SemaphoreType.DMA

    def whole(shape):
        return pl.BlockSpec(shape, lambda b: (0,) * len(shape), pipeline_mode=pl.Buffered(1))

    def block(b):
        return (jnp.minimum(b, 3), 0, 0)

    def held(first, single=False):
        return pl.BlockSpec(
            (n_ctx * n_tp, 1, rows, width),
            (lambda b: (0, first, 0, 0))
            if single
            else (lambda b: (0, first + jnp.minimum(b, 3), 0, 0)),
            pipeline_mode=pl.Buffered(1) if single else None,
        )

    def out(shape):
        return pl.BlockSpec(shape, lambda b: (0,) * len(shape))

    return pl.pallas_call(
        functools.partial(back_kernel, n_ctx, n_tp),
        name="back",
        grid=(5,),
        in_specs=[
            pl.BlockSpec(memory_space=pl.ANY),
            whole((tokens, 128)),
            whole((2, tokens // 2, width)),
            pl.BlockSpec((1, tokens, width), block),
            pl.BlockSpec((1, tokens, width), block),
            whole((width, tokens)),
            whole((tokens, width)),
            whole((tokens, 128)),
            whole((tokens, width)),
            whole(small.shape),
            held(1),
            held(5),
            held(0, True),
            pl.BlockSpec(memory_space=pl.ANY),
        ],
        out_specs=[
            *[pl.BlockSpec(memory_space=pl.ANY)] * 5,
            out((tokens, width)),
            out((tokens, width)),
            out((16, width)),
            pl.BlockSpec(memory_space=pl.ANY),
        ],
        out_shape=[
            bf16_of(9, rows, width),
            bf16_of(n_ctx - 1, NEAR, rows, width),
            *[bf16_of(9 - NEAR, rows, width)] * 3,
            f32_of(tokens, width),
            bf16_of(tokens, width),
            f32_of(16, width),
            bf16_of(*layer.shape),
        ],
        scratch_shapes=[
            pltpu.VMEM((tokens, width), jnp.float32),
            pltpu.VMEM((tokens, width), jnp.bfloat16),
            pltpu.VMEM((tokens, width), jnp.bfloat16),
            pltpu.VMEM((width, tokens), jnp.bfloat16),
            pltpu.VMEM((2, n_ctx, n_tp, 2, rows, width), jnp.bfloat16),
            pltpu.VMEM((5, n_tp - 1, n_ctx, 2, rows, width), jnp.bfloat16),
            pltpu.VMEM((n_ctx, 9 + 1, rows, width), jnp.bfloat16),
            dma((5 * (n_tp - 1),)),
            dma((5 * (n_tp - 1),)),
            dma((2,)),
            dma((2,)),
            dma((CROSSINGS * (n_ctx - 1),)),
            dma((CROSSINGS * (n_ctx - 1),)),
            dma((2,)),
            dma((2 * n_ctx,)),
        ],
        compiler_params=pltpu.CompilerParams(
            collective_id=3, has_side_effects=True, vmem_limit_bytes=62 << 20
        ),
        cost_estimate=pl.CostEstimate(
            flops=22_000_000_000, bytes_accessed=40 << 20, transcendentals=0
        ),
    )(n2, r2, cots, hid, gel, fit, n1, r1, ctx, small, rest, rest, rest, layer)


LATE = 3
EARLY = 9


def adam_update(weight, first, second, grad, decay, rate):
    count = float(STEP)
    first_new = beta_one * first + (1.0 - beta_one) * grad
    second_new = beta_two * second + (1.0 - beta_two) * grad * grad
    first_hat = first_new / (1.0 - beta_one**count)
    second_hat = second_new / (1.0 - beta_two**count)
    weight_new = weight - rate * (first_hat / (jnp.sqrt(second_hat) + adam_eps) + decay * weight)
    return (weight_new, first_new, second_new)


def finish_kernel(
    n_shard,
    n_ctx,
    n_tp,
    holder,
    late_at,
    x_hbm,
    dq_hbm,
    dk_hbm,
    dv_hbm,
    gh1_hbm,
    first_hbm,
    e0_hbm,
    near_hbm,
    e1_hbm,
    e2_hbm,
    e3_hbm,
    small_ref,
    home_ref,
    grad_out,
    small_out,
    x_s,
    dq_s,
    dk_s,
    dv_s,
    gh1_s,
    first_s,
    early,
    every,
    packed,
    right_met,
    left_met,
    flipped,
    grads,
    arrived,
    partial,
    met,
    over,
    more,
    back_s,
    small_s,
    small_t,
    small_m,
    small_p,
    flat_a,
    met_a,
    sum_a,
    mine_a,
    flat_b,
    met_b,
    sum_b,
    mine_b,
    pool,
    in_sem,
    c_s,
    c_r,
    p_s,
    p_r,
    o_s,
    o_r,
    h_s,
    h_r,
    sc_s,
    sc_r,
    sp_s,
    sp_r,
    e_s,
    e_r,
    l_s,
    l_r,
    a_s,
    a_r,
    b_s,
    b_r,
    d_s,
    d_r,
    f_s,
    f_r,
    keep_sem,
):
    z, c, t = place_of()
    side, core, bit = t // 2, lax.rem(t, 2), lax.rem(c, 2)
    _, mid, width = x_s.shape
    tokens = 2 * mid
    held, rows, _ = grad_out.shape
    per = n_ctx * n_tp // 2
    band = width // 2
    tile = mid

    loads = [
        pltpu.make_async_copy(src, dst, in_sem.at[i])
        for i, (src, dst) in enumerate(
            (
                (x_hbm, x_s),
                (dk_hbm, dk_s),
                (dv_hbm, dv_s),
                (dq_hbm, dq_s),
                (first_hbm, first_s),
                (gh1_hbm, gh1_s),
                (e0_hbm, early.at[0]),
                (near_hbm, early.at[1:4, 0:NEAR]),
                (e1_hbm, early.at[1, NEAR:EARLY]),
                (e2_hbm, early.at[2, NEAR:EARLY]),
                (e3_hbm, early.at[3, NEAR:EARLY]),
            )
        )
    ]
    for i in (6, 7, 8, 9, 10, 0, 1, 2, 3, 4, 5):
        loads[i].start()

    def far(dz):
        return (lax.rem(z + dz, n_shard), c, t)

    def across(mask):
        return (z, c ^ mask, t)

    def beside(dt):
        return (z, c, lax.rem(t + dt, n_tp))

    barrier = pltpu.get_barrier_semaphore()
    friends = [far(dz) for dz in range(1, n_shard)]
    friends += [(z, c ^ m, t) for m in range(1, n_ctx)]
    friends += [beside(dt) for dt in range(1, n_tp)]
    friends += [(z, c ^ m, t ^ 1) for m in range(1, n_ctx)]
    for friend in friends:
        pl.semaphore_signal(barrier, inc=1, device_id=friend, device_id_type=MESH)

    for i in range(6, 11):
        loads[i].wait()
    every[0:EARLY] = early[0] + early[1] + early[2] + early[3]
    every[EARLY] = jnp.zeros_like(every[EARLY])
    for s in range(n_shard * held):
        packed[s // held, s % held] = every[holder[s]]
    pl.semaphore_wait(barrier, len(friends))

    def run(owner_at, s, way):
        met, sems = (right_met, (e_s, e_r)) if way > 0 else (left_met, (l_s, l_r))
        target = (lax.rem(z + way + n_shard, n_shard), c, t)
        return send(packed.at[owner_at], met.at[s], sems, s, target)

    def each_run(hop):
        for s in range(hop + 1):
            for way in (1, -1):
                place = hop - s if way > 0 else n_shard - 1 - (hop - s)
                owner_at = n_shard - 1 - s if way > 0 else s
                yield s, way, place, owner_at

    def hop(h):
        for s, way, place, owner_at in each_run(h):

            @pl.when(z == place)
            def move(s=s, way=way, place=place, owner_at=owner_at):
                copy = run(owner_at, s, way)
                if h > s:
                    copy.wait_recv()
                    met = right_met if way > 0 else left_met
                    for j in range(held):
                        packed[owner_at, j] = packed[owner_at, j] + met[s, j]
                copy.start()

    def hops_end():
        for h in range(n_shard - 1):
            for s, way, place, owner_at in each_run(h):

                @pl.when(z == place)
                def sent(s=s, way=way, owner_at=owner_at):
                    run(owner_at, s, way).wait_send()

        for s in range(n_shard - 1):
            for way in (1, -1):
                owner_at = n_shard - 1 - s if way > 0 else s

                @pl.when(z == owner_at)
                def last(s=s, way=way, owner_at=owner_at):
                    run(owner_at, s, way).wait_recv()
                    met = right_met if way > 0 else left_met
                    for j in range(held):
                        packed[owner_at, j] = packed[owner_at, j] + met[s, j]

    hop(0)

    core_moves = []

    def exchange(m):
        for dt in range(1, n_tp):
            other = lax.rem(t + dt, n_tp)
            for k in range(n_ctx):
                copy = send(
                    grads.at[k * n_tp + other, m],
                    arrived.at[dt - 1, k, m],
                    (c_s, c_r),
                    ((dt - 1) * n_ctx + k) * LATE + m,
                    beside(dt),
                )
                copy.start()
                core_moves.append((m, copy))

    plane_moves = []

    def meet(m):
        for which, copy in core_moves:
            if which == m:
                copy.wait_recv()
        for k in range(n_ctx):
            value = grads[k * n_tp + t, m]
            for dt in range(1, n_tp):
                value = value + arrived[dt - 1, k, m]
            partial[k, m] = value
        for j in range(1, n_ctx):
            copy = send(
                partial.at[c ^ j, m], met.at[j - 1, m], (p_s, p_r), (j - 1) * LATE + m, across(j)
            )
            copy.start()
            plane_moves.append((m, copy))

    loads[0].wait()
    for a in range(4):
        chunk = 2 * (core if a < 2 else 1 - core) + ((a % 2) ^ bit)
        flipped[:, pl.ds(pl.multiple_of(chunk * mid, mid), mid)] = x_s[a].T

    def weight_grad(m, left_at, right):
        def one(i, carry):
            left = flipped[pl.ds(pl.multiple_of(i * band, band), band), left_at]
            value = wide_dot(left, right[...], NN).astype(jnp.bfloat16)
            grads[pl.ds(i * per, per), m] = value.reshape(per, rows, width)
            return carry

        lax.fori_loop(0, 2, one, 0)

    loads[1].wait()
    weight_grad(1, slice(None), dk_s)
    exchange(1)
    loads[2].wait()
    weight_grad(2, slice(None), dv_s)
    exchange(2)
    meet(1)
    for h in range(1, n_shard - 2):
        hop(h)
    loads[3].wait()
    weight_grad(0, pl.ds(pl.multiple_of(core * tokens, tokens), tokens), dq_s)
    exchange(0)
    meet(2)

    row = lax.broadcasted_iota(jnp.int32, small_ref.shape, 0)
    q_sum = jnp.sum(dq_s[...].astype(jnp.float32), axis=0, keepdims=True)
    v_sum = jnp.sum(dv_s[...].astype(jnp.float32), axis=0, keepdims=True)
    sums = jnp.where(row == 0, q_sum, jnp.where(row == 1, v_sum, small_ref[...]))
    small_s[...] = sums.astype(jnp.bfloat16)
    small_core = [
        send(small_s, small_t.at[dt - 1], (sc_s, sc_r), dt - 1, beside(dt)) for dt in range(1, n_tp)
    ]
    for copy in small_core:
        copy.start()

    loads[4].wait()

    def weight(m):
        return first_s[:, m * rows : (m + 1) * rows, :].reshape(width, width)

    wq, wk, wv = weight(0), weight(1), weight(2)
    over_moves = []
    for b in range(2):
        at = pl.ds(pl.multiple_of((1 - core) * tokens + b * mid, mid), mid)
        value = wide_dot(dk_s[at, :], wk, NT) + wide_dot(dv_s[at, :], wv, NT)
        over[b] = value.astype(jnp.bfloat16)
        copy = send(over.at[b], more.at[b], (o_s, o_r), b, (z, c, t ^ 1))
        copy.start()
        over_moves.append(copy)
        if b == 0:
            meet(0)
            if n_shard > 2:
                hop(n_shard - 2)

    value = small_s[...]
    for dt, copy in enumerate(small_core):
        copy.wait_recv()
        value = value + small_t[dt]
    small_m[...] = value
    small_plane = [
        send(small_m, small_p.at[j - 1], (sp_s, sp_r), j - 1, across(j)) for j in range(1, n_ctx)
    ]
    for copy in small_plane:
        copy.start()

    loads[5].wait()
    stays = c // 2 == core
    home_moves = []
    for copy in over_moves:
        copy.wait_recv()
    keep = pltpu.make_async_copy(back_s.at[0], home_ref.at[bit], keep_sem.at[0])
    for move in range(2):
        chunk = move ^ bit
        for i in range(mid // tile):
            at = pl.ds(pl.multiple_of(core * tokens + chunk * mid + i * tile, tile), tile)
            here = pl.ds(pl.multiple_of(chunk * mid + i * tile, tile), tile)
            value = gh1_s[here, :]
            value = value + more[chunk, i * tile : (i + 1) * tile, :].astype(jnp.float32)
            value = value + wide_dot(dq_s[here, :], wq, NT)
            value = value + wide_dot(dk_s[at, :], wk, NT)
            value = value + wide_dot(dv_s[at, :], wv, NT)
            back_s[move, i * tile : (i + 1) * tile, :] = value.astype(jnp.bfloat16)
        target = (z, 2 * core + chunk, 2 * side + c // 2)
        home_moves.append(send(back_s.at[move], home_ref.at[bit], (h_s, h_r), move, target))
        if move == 0:

            @pl.when(stays)
            def kept():
                keep.start()

            @pl.when(jnp.logical_not(stays))
            def left():
                home_moves[0].start()

        else:
            home_moves[1].start()

    def gathered_rows(m):
        for which, copy in plane_moves:
            if which == m:
                copy.wait_recv()
        value = partial[c, m]
        for j in range(n_ctx - 1):
            value = value + met[j, m]
        return value

    def piece_at(ref, k):
        piece = ref.shape[0] // n_shard
        return pl.ds(pl.multiple_of(k * piece, piece), piece)

    def scatter_lot(flat, lot_met, sems):
        moves = [
            send(flat.at[piece_at(flat, far(dz)[0])], lot_met.at[dz - 1], sems, dz - 1, far(dz))
            for dz in range(1, n_shard)
        ]
        for copy in moves:
            copy.start()
        return moves

    def spread_lot(moves, flat, lot_met, lot_sum, lot_mine, sems):
        total = flat[piece_at(flat, z), :].astype(jnp.float32)
        for dz, copy in enumerate(moves):
            copy.wait_recv()
            total = total + lot_met[dz].astype(jnp.float32)
        lot_mine[...] = total.astype(jnp.bfloat16)
        spreads = [
            send(lot_mine, lot_sum.at[piece_at(flat, z)], sems, dz - 1, far(dz))
            for dz in range(1, n_shard)
        ]
        for copy in spreads:
            copy.start()
        lot_sum[piece_at(flat, z), :] = lot_mine[...]
        return spreads

    small_rows = small_s.shape[0]
    flat_a[...] = jnp.zeros_like(flat_a)
    flat_b[...] = jnp.zeros_like(flat_b)
    flat_a[0:rows, :] = gathered_rows(1)
    flat_a[rows : 2 * rows, :] = gathered_rows(2)
    scatter_a = scatter_lot(flat_a, met_a, (a_s, a_r))
    flat_b[0:rows, :] = gathered_rows(0)
    value = small_m[...]
    for j, copy in enumerate(small_plane):
        copy.wait_recv()
        value = value + small_p[j]
    flat_b[rows : rows + small_rows, :] = value
    scatter_b = scatter_lot(flat_b, met_b, (b_s, b_r))
    spread_a = spread_lot(scatter_a, flat_a, met_a, sum_a, mine_a, (d_s, d_r))
    spread_b = spread_lot(scatter_b, flat_b, met_b, sum_b, mine_b, (f_s, f_r))
    hops_end()
    for copy in (*spread_a, *spread_b):
        copy.wait_recv()
    pool[0] = sum_b[0:rows, :]
    pool[1] = sum_a[0:rows, :]
    pool[2] = sum_a[rows : 2 * rows, :]
    pool[LATE] = jnp.zeros_like(pool[LATE])
    for j in range(held):
        grad = packed[z, j].astype(jnp.float32)
        grad = grad + pool[late_at[z * held + j]].astype(jnp.float32)
        grad_out[j] = grad
    small_out[...] = sum_b[rows : rows + small_rows, :].astype(jnp.float32)

    @pl.when(stays)
    def done():
        keep.wait()

    @pl.when(jnp.logical_not(stays))
    def gone():
        home_moves[0].wait()

    home_moves[1].wait()
    for _, copy in (*core_moves, *plane_moves):
        copy.wait_send()
    for copy in (
        *over_moves,
        *small_core,
        *small_plane,
        *scatter_a,
        *scatter_b,
        *spread_a,
        *spread_b,
    ):
        copy.wait_send()


def finish(
    holder,
    late_at,
    x_all,
    dq,
    dk,
    dv,
    gh1,
    first,
    early,
    small,
    held,
    n_shard,
    n_ctx,
    n_tp,
):
    _, mid, width = x_all.shape
    rows = width // (n_ctx * n_tp)
    groups = n_ctx * n_tp
    span = 16 * n_shard
    long_a = -(-2 * rows // span) * span
    long_b = -(-(rows + small.shape[0]) // span) * span
    smem = pl.BlockSpec(memory_space=pltpu.SMEM)
    anywhere = pl.BlockSpec(memory_space=pl.ANY)
    vmem = pl.BlockSpec(memory_space=pltpu.VMEM)
    dma = pltpu.SemaphoreType.DMA
    low = jnp.bfloat16
    pairs = [LATE * n_ctx * (n_tp - 1), LATE * (n_ctx - 1), 2, 2, n_tp - 1, n_ctx - 1]
    pairs += [n_shard - 1] * 6
    shapes = [
        x_all.shape,
        dq.shape,
        dk.shape,
        dv.shape,
        None,
        first.shape,
        (4, EARLY, rows, width),
        (EARLY + 1, rows, width),
        (n_shard, held, rows, width),
        (n_shard - 1, held, rows, width),
        (n_shard - 1, held, rows, width),
        (width, 4 * mid),
        (groups, LATE, rows, width),
        (n_tp - 1, n_ctx, LATE, rows, width),
        (n_ctx, LATE, rows, width),
        (n_ctx - 1, LATE, rows, width),
        (2, mid, width),
        (2, mid, width),
        (2, mid, width),
        small.shape,
        (n_tp - 1, *small.shape),
        small.shape,
        (n_ctx - 1, *small.shape),
        *[
            shape
            for long in (long_a, long_b)
            for shape in (
                (long, width),
                (n_shard - 1, long // n_shard, width),
                (long, width),
                (long // n_shard, width),
            )
        ],
        (LATE + 1, rows, width),
    ]
    return pl.pallas_call(
        functools.partial(finish_kernel, n_shard, n_ctx, n_tp),
        name="finish",
        in_specs=[smem] * 2 + [anywhere] * 11 + [vmem],
        out_specs=[vmem] * 3,
        out_shape=[bf16_of(2, mid, width), f32_of(held, rows, width), f32_of(*small.shape)],
        scratch_shapes=[
            pltpu.VMEM(s, low) if s else pltpu.VMEM(gh1.shape, jnp.float32) for s in shapes
        ]
        + [dma((11,))]
        + [dma((n,)) for n in pairs for _ in range(2)]
        + [dma((1,))],
        compiler_params=pltpu.CompilerParams(
            collective_id=1, has_side_effects=True, vmem_limit_bytes=63 << 20
        ),
        cost_estimate=pl.CostEstimate(
            flops=12_000_000_000, bytes_accessed=40 << 20, transcendentals=0
        ),
    )(holder, late_at, x_all, dq, dk, dv, gh1, first, *early, small)


def shards(
    inputs,
    cotangent,
    rand_blocks,
    slot_of,
    master,
    moment_one,
    moment_two,
    small_params,
    small_one,
    small_two,
):
    n_shard = lax.axis_size("shard")
    n_ctx = lax.axis_size("ctx")
    n_tp = lax.axis_size("tp")
    groups = n_ctx * n_tp
    held, rows, width = master.shape
    span = small_params.shape[0]
    my_ctx = lax.axis_index("ctx")
    my_tp = lax.axis_index("tp")
    half = lax.rem(my_tp, 2)
    plane = ("ctx", "tp")

    half_one = half.astype(jnp.int32).reshape(1)
    my_shard = lax.axis_index("shard")
    start = ((my_shard * n_ctx + my_ctx) * n_tp + my_tp) * span
    lone = lax.dynamic_update_slice(
        jnp.zeros((16 * width,), jnp.float32), small_params, (start,)
    ).reshape(16, width)
    begun = begin(
        slot_of,
        rand_blocks,
        master,
        lone,
        inputs,
        cotangent,
        n_shard,
        n_ctx,
        n_tp,
    )
    x_all, first, rest, small, q, k, v, context, lse = begun[:9]
    cots, out_low, n1, r1, n2, r2, fit, hid, gel = begun[9:]
    *early, gh1, dctx, sums, layer_home = back(
        n2, r2, cots, hid, gel, fit, n1, r1, context, small, rest, out_low, n_ctx, n_tp
    )
    for j in range(1, n_ctx):
        crossing = [
            (a * n_tp + b, (a ^ j) * n_tp + b) for a in range(n_ctx) for b in range(n_tp)
        ]
        early[j + 1] = lax.ppermute(early[j + 1], plane, crossing)
    dq, dk, dv, layer_out = attend_back(
        half_one, rand_blocks, q, k, v, lse, dctx, layer_home, 15
    )
    stands = jnp.array([8, 0, 2, 4, 6, 1, 3, 5, 7], jnp.int32)
    slots_all = jnp.arange(n_shard * held, dtype=jnp.int32)
    hits = slot_of[None, :] == slots_all[:, None]
    holder = EARLY + jnp.sum(jnp.where(hits[:, LATE:], stands[None, :] - EARLY, 0), axis=1)
    ranks = jnp.arange(LATE, dtype=jnp.int32)[None, :]
    late_at = LATE + jnp.sum(jnp.where(hits[:, :LATE], ranks - LATE, 0), axis=1)
    came, slot_grads, small_sum = finish(
        holder.astype(jnp.int32),
        late_at.astype(jnp.int32),
        x_all,
        dq,
        dk,
        dv,
        gh1,
        first,
        early,
        sums,
        held,
        n_shard,
        n_ctx,
        n_tp,
    )
    input_grad = came.astype(jnp.float32)
    master_new, first_new, second_new = adam_update(
        master, moment_one, moment_two, slot_grads, 0.01, rate_value
    )
    rows_held = -(-span // width) + 1
    first_row = jnp.minimum(start // width, small_sum.shape[0] - rows_held)
    near_rows = lax.dynamic_slice_in_dim(small_sum, first_row, rows_held).reshape(-1)
    small_owned = lax.dynamic_slice_in_dim(near_rows, start - first_row * width, span)
    small_new, small_first, small_second = adam_update(
        small_params, small_one, small_two, small_owned, 0.0, small_rate
    )
    return (
        layer_out,
        input_grad,
        master_new,
        first_new,
        second_new,
        small_new,
        small_first,
        small_second,
    )


def solution(mesh):
    tokens = P(("shard", "tp"), "ctx", None)
    stored = P("shard", ("ctx", "tp"), None)
    spread = P(("shard", "ctx", "tp"))
    return jax.shard_map(
        shards,
        mesh=mesh,
        in_specs=(tokens, tokens, P(), P(), stored, stored, stored, spread, spread, spread),
        out_specs=(tokens, tokens, stored, stored, stored, spread, spread, spread),
        check_vma=False,
    )
```
